32 devices in a mesh: dp: 8 (over z, x), tensor: 4 (over y, core).
Axes of the slice: x: 2, y: 2, z: 4, core: 2. Of those that a mesh axis runs over, the one named last changes fastest.
Arguments:
- tokens: bfloat16 [16384, 1024], P(('dp', 'tensor')), may hold values from -6 to 6
- memory: bfloat16 [16384, 1024], P(('dp', 'tensor')), may hold values from -6 to 6
- dec_lengths: int32 [8, 4], P('dp'), may hold values from 1 to 512, 1536 in all within a row
- mem_lengths: int32 [8, 4], P('dp'), may hold values from 1 to 512, 1536 in all within a row
- self_qkv: bfloat16 [3, 1024, 1024], P(None, None, 'tensor'), may hold values from -0.1875 to 0.1875
- self_out: bfloat16 [1024, 1024], P('tensor'), may hold values from -3 to 3
- cross_q: bfloat16 [1024, 1024], P(None, 'tensor'), may hold values from -0.1875 to 0.1875
- cross_kv: bfloat16 [2, 1024, 1024], P(None, None, 'tensor'), may hold values from -0.1875 to 0.1875
- cross_out: bfloat16 [1024, 1024], P('tensor'), may hold values from -3 to 3
- ffn_in: bfloat16 [1024, 4096], P(None, 'tensor'), may hold values from -0.1875 to 0.1875
- ffn_out: bfloat16 [4096, 1024], P('tensor'), may hold values from -0.375 to 0.375
- norm_gains: float32 [3, 1024], replicated, may hold values from 0.25 to 1.75
- norm_biases: float32 [3, 1024], replicated, may hold values from -3 to 3
- cotangent: bfloat16 [16384, 1024], P(('dp', 'tensor')), may hold values from -6 to 6
Outputs:
- out: bfloat16 [16384, 1024], P(('dp', 'tensor'))
- grad_tokens: float32 [16384, 1024], P(('dp', 'tensor'))
- grad_memory: float32 [16384, 1024], P(('dp', 'tensor'))
- grad_self_qkv: float32 [3, 1024, 1024], P(None, 'dp', 'tensor')
- grad_self_out: float32 [1024, 1024], P('tensor', 'dp')
- grad_cross_q: float32 [1024, 1024], P('dp', 'tensor')
- grad_cross_kv: float32 [2, 1024, 1024], P(None, 'dp', 'tensor')
- grad_cross_out: float32 [1024, 1024], P('tensor', 'dp')
- grad_ffn_in: float32 [1024, 4096], P('dp', 'tensor')
- grad_ffn_out: float32 [4096, 1024], P('tensor', 'dp')
- grad_gains: float32 [3, 1024], replicated
- grad_biases: float32 [3, 1024], replicated
The draws below stay inside these ranges and needn't reach their ends.
Inputs may be any that keep to these rules, and one draw needn't show every extreme that they name: `dec_lengths`: each index of dp holds 4 decoder lengths summing to 1536, the longest exactly 512. `mem_lengths`: each index of dp holds 4 memory lengths summing to 1536, the longest exactly 512.
All inputs are finite; a program needn't handle non-finite values.
Results may differ from the reference program's by a relative error of at most 0.039.
Values may be sent and summed in bfloat16 or wider, within the bound.
No kernel may reach another device: no remote copies, remote signals or barrier semaphores. Data moves between devices by JAX's collectives and lax.ppermute only.
A program may use at most 256 MiB of HBM per device.

```python
import math
import jax
import jax.numpy as jnp
import numpy as np
from jax import lax

D = 1024
HEADS = 16
HEAD_DIM = 64
FF = 4096
SEQS = 4
LEN = 512
MLEN = 512
TOKENS = 16384
MTOKENS = 16384
N_DP = 8


def level_of(stream_key, extent, cuts, smallest, largest):
    level, own = 1.0, jax.random.fold_in(stream_key, 6)
    for dim, shards_of in cuts:
        steps = jnp.exp(jax.random.uniform(jax.random.fold_in(own, dim), (shards_of,), jnp.float32, smallest / len(cuts), largest / len(cuts)))
        level = level * jnp.repeat(steps, extent[dim] // shards_of).reshape([-1 if axis == dim else 1 for axis in range(len(extent))])
    return level


def length_profile(amount, total, limit, lean):
    portions = [(1 << 20) // math.isqrt(rank ** lean) + 1 for rank in range(2, amount + 1)]
    rest, counts = total - limit - (amount - 1), [1] * (amount - 1)
    while rest > 0:
        movable = [i for i in range(amount - 1) if counts[i] < limit]
        mass, left = sum([portions[i] for i in movable]), rest
        for i in movable:
            extra = min(limit - counts[i], max(1, left * portions[i] // mass), rest)
            counts[i] = counts[i] + extra
            rest = rest - extra
    return np.array([limit] + counts)


def ragged(rng, count, total, limit, lean):
    if count == 2:
        one = jax.random.randint(rng, (), max(1, total - limit), min(limit, total - 1) + 1)
        return jnp.stack([one, total - one])
    sizes = jnp.asarray(length_profile(count, total, limit, lean), jnp.int32)
    twos = (count - 1) // 2
    source_of, sink = sizes[1:1 + 2 * twos:2], sizes[2:2 + 2 * twos:2]
    room = jnp.minimum(source_of - 1, limit - sink)
    shifted = jax.random.randint(jax.random.fold_in(rng, 1), (twos,), 0, 1 << 20) % (room + 1)
    sizes = sizes.at[1:1 + 2 * twos:2].set(source_of - shifted).at[2:2 + 2 * twos:2].set(sink + shifted)
    return sizes[jax.random.permutation(jax.random.fold_in(rng, 2), count)]


def centred(stream_key, shape, scale, most, cuts=(), kind=jnp.bfloat16):
    values = scale * jax.random.normal(stream_key, shape, jnp.float32)
    if cuts:
        values = values * level_of(stream_key, shape, cuts, -0.22, 0.18)
    return jnp.clip(values, -most, most).astype(kind)


def setup_inputs(seed: int = 0) -> dict:
    key_list = jax.random.split(jax.random.key(seed), 15)
    return {
        "tokens": centred(key_list[0], (TOKENS, D), 1.0, 6.0, ((0, 32),)),
        "memory": centred(key_list[1], (MTOKENS, D), 1.0, 6.0, ((0, 32),)),
        "dec_lengths": jax.vmap(lambda own: ragged(own, SEQS, 3 * SEQS * LEN // 4, LEN, 1))(jax.random.split(key_list[2], N_DP)).reshape((N_DP, SEQS)).astype(jnp.int32),
        "mem_lengths": jax.vmap(lambda own: ragged(own, SEQS, 3 * SEQS * MLEN // 4, MLEN, 1))(jax.random.split(key_list[3], N_DP)).reshape((N_DP, SEQS)).astype(jnp.int32),
        "self_qkv": centred(key_list[4], (3, D, D), D ** -0.5, 0.1875, ((2, 4),)),
        "self_out": centred(key_list[5], (D, D), (2 * D // LEN) ** -0.5, 3.0, ((0, 4),)),
        "cross_q": centred(key_list[6], (D, D), D ** -0.5, 0.1875, ((1, 4),)),
        "cross_kv": centred(key_list[7], (2, D, D), D ** -0.5, 0.1875, ((2, 4),)),
        "cross_out": centred(key_list[8], (D, D), (2 * D // MLEN) ** -0.5, 3.0, ((0, 4),)),
        "ffn_in": centred(key_list[9], (D, FF), D ** -0.5, 0.1875, ((1, 4),)),
        "ffn_out": centred(key_list[10], (FF, D), (FF // 16) ** -0.5, 0.375, ((0, 4),)),
        "norm_gains": jnp.clip(1.0 + 0.15 * jax.random.normal(key_list[11], (3, D), jnp.float32), 0.25, 1.75),
        "norm_biases": centred(key_list[12], (3, D), 0.5, 3.0, (), jnp.float32),
        "cotangent": centred(key_list[13], (TOKENS, D), 1.0, 6.0, ((0, 32),)),
    }


RESIDUAL_ALPHA = 4.16
NORM_EPSILON = 1e-05
MASKED_SCORE = -1000000000.0
FULL_PRECISION = lax.Precision.HIGHEST
GROUP_TOKENS = 4096

@jax.custom_vjp
def low(v):
    return lax.optimization_barrier(v.astype(jnp.bfloat16)).astype(jnp.float32)

@jax.custom_vjp
def low_back(v):
    return v

def low_keep(v):
    return (low(v), None)

def low_pass(kept, grad):
    return (grad,)

def back_keep(v):
    return (v, None)

def back_low(kept, grad):
    return (low(grad),)
low.defvjp(low_keep, low_pass)
low_back.defvjp(back_keep, back_low)

def round_both(values):
    return low_back(low(values))

def matmul(left, right):
    return jnp.dot(left, right, precision=FULL_PRECISION)

def layer_norm(hidden, norm_gain, norm_bias):
    center = hidden - lax.optimization_barrier(jnp.mean(hidden, axis=-1, keepdims=True))
    inverse = lax.rsqrt(lax.optimization_barrier(jnp.mean(center * center, axis=-1, keepdims=True)) + NORM_EPSILON)
    return center * inverse * norm_gain + norm_bias

def attend(queries, key_rows, value_rows, key_mask):
    query_heads = queries.reshape(queries.shape[0], HEADS, HEAD_DIM)
    key_heads = key_rows.reshape(key_rows.shape[0], HEADS, HEAD_DIM)
    value_heads = value_rows.reshape(value_rows.shape[0], HEADS, HEAD_DIM)
    scores = jnp.einsum('qhe,khe->hqk', query_heads, key_heads, precision=FULL_PRECISION)
    scores = low_back(scores * HEAD_DIM ** (-0.5))
    scores = jnp.where(key_mask[None], scores, MASKED_SCORE)
    softmax_probs = jax.nn.softmax(scores, axis=-1)
    attended = jnp.einsum('hqk,khe->qhe', low(softmax_probs), value_heads, precision=FULL_PRECISION)
    return round_both(attended.reshape(queries.shape[0], D))

def forward(tokens, memory, self_qkv, self_out, cross_q, cross_kv, cross_out, ffn_in, ffn_out, norm_gains, norm_biases, dec_lengths, mem_lengths):
    sentences = dec_lengths.shape[0]
    positions = jnp.arange(LEN, dtype=jnp.int32)
    mem_positions = jnp.arange(MLEN, dtype=jnp.int32)
    self_query = round_both(matmul(tokens, self_qkv[0])).reshape(sentences, LEN, D)
    self_keys = round_both(matmul(tokens, self_qkv[1])).reshape(sentences, LEN, D)
    self_values = round_both(matmul(tokens, self_qkv[2])).reshape(sentences, LEN, D)

    def self_sentence(inputs):
        queries, key_rows, value_rows, length_now = inputs
        key_mask = (positions[None, :] <= positions[:, None]) & (positions[None, :] < length_now)
        return attend(queries, key_rows, value_rows, key_mask)
    self_att = lax.map(jax.checkpoint(self_sentence), (self_query, self_keys, self_values, dec_lengths)).reshape(-1, D)
    first = layer_norm(RESIDUAL_ALPHA * tokens + low_back(matmul(self_att, self_out)), norm_gains[0], norm_biases[0])
    first_low = low(first)
    cross_query = round_both(matmul(first_low, cross_q)).reshape(sentences, LEN, D)
    cross_keys = round_both(matmul(memory, cross_kv[0])).reshape(sentences, MLEN, D)
    cross_values = round_both(matmul(memory, cross_kv[1])).reshape(sentences, MLEN, D)

    def cross_sentence(inputs):
        queries, key_rows, value_rows, length_now = inputs
        key_mask = jnp.broadcast_to(mem_positions[None, :] < length_now, (LEN, MLEN))
        return attend(queries, key_rows, value_rows, key_mask)
    cross_att = lax.map(jax.checkpoint(cross_sentence), (cross_query, cross_keys, cross_values, mem_lengths)).reshape(-1, D)
    second = layer_norm(RESIDUAL_ALPHA * first + low_back(matmul(cross_att, cross_out)), norm_gains[1], norm_biases[1])
    activated = low(jax.nn.gelu(low_back(matmul(low(second), ffn_in)), approximate=True))
    third = RESIDUAL_ALPHA * second + low_back(matmul(activated, ffn_out))
    return layer_norm(third, norm_gains[2], norm_biases[2])

def group_count(total_sentences):
    most = max(1, GROUP_TOKENS // LEN)
    width = 1
    for candidate in range(1, total_sentences + 1):
        if candidate <= most and total_sentences % candidate == 0:
            width = candidate
    return width

def reference(tokens, memory, dec_lengths, mem_lengths, self_qkv, self_out, cross_q, cross_kv, cross_out, ffn_in, ffn_out, norm_gains, norm_biases, cotangent):
    flat_dec = dec_lengths.reshape(-1).astype(jnp.int32)
    flat_mem = mem_lengths.reshape(-1).astype(jnp.int32)
    total_sentences = flat_dec.shape[0]
    width = group_count(total_sentences)
    groups = total_sentences // width
    dec_groups = flat_dec.reshape(groups, width)
    mem_groups = flat_mem.reshape(groups, width)

    def closed(tok_f, mem_f, sqkv_f, sout_f, cq_f, ckv_f, cout_f, fin_f, fout_f, gain_f, bias_f):

        def one_group(inputs):
            tok_part, mem_part, dec_part, memlen_part = inputs
            return forward(tok_part, mem_part, sqkv_f, sout_f, cq_f, ckv_f, cout_f, fin_f, fout_f, gain_f, bias_f, dec_part, memlen_part)
        tok_blocks = tok_f.reshape(groups, width * LEN, D)
        mem_blocks = mem_f.reshape(groups, width * MLEN, D)
        results = lax.map(jax.checkpoint(one_group), (tok_blocks, mem_blocks, dec_groups, mem_groups))
        return results.reshape(-1, D)
    result, pullback = jax.vjp(closed, tokens.astype(jnp.float32), memory.astype(jnp.float32), self_qkv.astype(jnp.float32), self_out.astype(jnp.float32), cross_q.astype(jnp.float32), cross_kv.astype(jnp.float32), cross_out.astype(jnp.float32), ffn_in.astype(jnp.float32), ffn_out.astype(jnp.float32), norm_gains.astype(jnp.float32), norm_biases.astype(jnp.float32))
    grads = pullback(cotangent.astype(jnp.float32))
    return (result.astype(jnp.bfloat16), grads[0], grads[1], grads[2], grads[3], grads[4], grads[5], grads[6], grads[7], grads[8], grads[9], grads[10])
```

```python
import functools
import jax
import jax.numpy as jnp
from jax import lax
from jax.experimental import pallas as pl
from jax.experimental.pallas import tpu as pltpu
from jax.sharding import PartitionSpec as P

HEAD_DIM = 64
RESIDUAL_ALPHA = 4.16
NORM_EPSILON = 1e-05
MASKED_SCORE = -1000000000.0
SCORE_SCALE = HEAD_DIM ** (-0.5)
UNIT = 128
QUERY_BLOCK = 256
FFN_UNIT = 256
ROW_CHUNK = 64
BF16 = jnp.bfloat16
F32 = jnp.float32


def dot(left, right):
    return lax.dot_general(left, right, (((1,), (0,)), ((), ())), preferred_element_type=F32)


def dot_nt(left, right):
    return lax.dot_general(left, right, (((1,), (1,)), ((), ())), preferred_element_type=F32)


def shard_of(position):
    return ((position >> 2) & 1) | (position & 2) | ((position & 1) << 2)


def copy_of(source, target, sem):
    return pltpu.make_async_copy(source, target, sem)


def augment(rows, head, extra):
    lanes = lax.broadcasted_iota(jnp.int32, rows.shape, 1)
    inside = (lanes >= HEAD_DIM) if head else (lanes < HEAD_DIM)
    spare = lanes == (0 if head else HEAD_DIM)
    return jnp.where(inside, rows, jnp.where(spare, extra, 0.0)).astype(BF16)


def key_bias(keys, length):
    return jnp.where(lax.broadcasted_iota(jnp.int32, (keys, 1), 0) < length, 0.0, MASKED_SCORE)


def fill_diagonal(diagonal):
    keys = lax.broadcasted_iota(jnp.int32, diagonal.shape, 0)
    queries = lax.broadcasted_iota(jnp.int32, diagonal.shape, 1)
    diagonal[...] = jnp.where(keys <= queries, 0.0, MASKED_SCORE)


def scores_of(keys_aug, query_aug, block, causal, diagonal):
    if not causal:
        return dot_nt(keys_aug, query_aug)
    low = block * QUERY_BLOCK
    here = dot_nt(keys_aug[low : low + QUERY_BLOCK], query_aug) + diagonal[...]
    if not block:
        return here
    return jnp.concatenate([dot_nt(keys_aug[:low], query_aug), here], axis=0)


def attend_unit(query, keys, values, length, causal, diagonal, lse_ref):
    rows = query.shape[0]
    bias = key_bias(keys.shape[0], length)
    values_t = jnp.transpose(values.astype(F32)).astype(BF16)
    keys_f, query_f = keys.astype(F32), query.astype(F32)
    keys_aug = [augment(keys_f, head, bias) for head in (0, 1)]
    query_aug = [augment(query_f, head, 1.0) for head in (0, 1)]
    out = []
    for block in range(rows // QUERY_BLOCK):
        low = block * QUERY_BLOCK
        live = low + QUERY_BLOCK if causal else keys.shape[0]
        parts = []
        for head in (0, 1):
            scores = scores_of(
                keys_aug[head], query_aug[head][low : low + QUERY_BLOCK], block, causal, diagonal
            )
            peak = jnp.max(scores, axis=0, keepdims=True)
            terms = jnp.exp(scores - peak)
            total = jnp.sum(terms, axis=0, keepdims=True)
            mixed = dot(
                values_t[head * HEAD_DIM : (head + 1) * HEAD_DIM, :live], terms.astype(BF16)
            )
            parts.append(mixed / total)
            lse_ref[head : head + 1, low : low + QUERY_BLOCK] = peak + jnp.log(total)
        out.append(jnp.transpose(jnp.concatenate(parts, axis=0)))
    return jnp.concatenate(out, axis=0).astype(BF16)


def attend_back_unit(query, keys, values, attended, grad, length, causal, diagonal, lse_ref):
    rows = query.shape[0]
    bias = key_bias(keys.shape[0], length)
    query_f, keys_f, values_f, grad_f = (a.astype(F32) for a in (query, keys, values, grad))
    delta = jnp.transpose(grad_f * attended.astype(F32))
    deltas = [
        jnp.sum(delta[head * HEAD_DIM : (head + 1) * HEAD_DIM], axis=0, keepdims=True)
        for head in (0, 1)
    ]
    keys_t = jnp.transpose(keys_f).astype(BF16)
    keys_aug = [augment(keys_f, head, bias) for head in (0, 1)]
    query_aug = [augment(query_f, head, 1.0) for head in (0, 1)]
    query_own = [augment(query_f, head, 0.0) for head in (0, 1)]
    grad_own = [augment(grad_f, head, 0.0) for head in (0, 1)]
    grad_query = []
    grad_keys = grad_values = None
    for block in reversed(range(rows // QUERY_BLOCK)):
        low = block * QUERY_BLOCK
        live = low + QUERY_BLOCK if causal else keys.shape[0]
        parts, add_keys, add_values = [], None, None
        for head in (0, 1):
            scores = scores_of(
                keys_aug[head], query_aug[head][low : low + QUERY_BLOCK], block, causal, diagonal
            )
            probs = jnp.exp(scores - lse_ref[head : head + 1, low : low + QUERY_BLOCK])
            grad_head = grad_own[head][low : low + QUERY_BLOCK]
            grad_probs = dot_nt(values[:live], grad_head)
            grad_scores = (
                probs * (grad_probs - deltas[head][:, low : low + QUERY_BLOCK])
            ).astype(BF16)
            part_values = dot(probs.astype(BF16), grad_head)
            part_keys = dot(grad_scores, query_own[head][low : low + QUERY_BLOCK])
            add_values = part_values if add_values is None else add_values + part_values
            add_keys = part_keys if add_keys is None else add_keys + part_keys
            parts.append(
                dot(keys_t[head * HEAD_DIM : (head + 1) * HEAD_DIM, :live], grad_scores)
            )
        grad_query.append(jnp.transpose(jnp.concatenate(parts, axis=0)) * SCORE_SCALE)
        if grad_keys is None:
            grad_keys, grad_values = add_keys, add_values
        elif live == grad_keys.shape[0]:
            grad_keys, grad_values = grad_keys + add_keys, grad_values + add_values
        else:
            grad_keys = jnp.concatenate([grad_keys[:live] + add_keys, grad_keys[live:]], axis=0)
            grad_values = jnp.concatenate(
                [grad_values[:live] + add_values, grad_values[live:]], axis=0
            )
    return (
        jnp.concatenate(grad_query[::-1], axis=0).astype(BF16),
        grad_keys.astype(BF16),
        grad_values.astype(BF16),
    )


def norm_chunk(hidden, gain, bias):
    center = hidden - jnp.mean(hidden, axis=-1, keepdims=True)
    inverse = lax.rsqrt(jnp.mean(center * center, axis=-1, keepdims=True) + NORM_EPSILON)
    normed = center * inverse
    return normed * gain + bias, normed, inverse


def norm_back_chunk(gradient, normed, inverse, gain):
    scaled = gradient * gain
    return inverse * (
        scaled
        - jnp.mean(scaled, axis=-1, keepdims=True)
        - normed * jnp.mean(scaled * normed, axis=-1, keepdims=True)
    )


def fold_rows(values):
    return jnp.sum(values.reshape(values.shape[0] // 8, 8, values.shape[1]), axis=0)


def each_chunk(rows, body):
    def step(index, carry):
        body(pl.ds(pl.multiple_of(index * ROW_CHUNK, ROW_CHUNK), ROW_CHUNK))
        return carry

    lax.fori_loop(0, rows // ROW_CHUNK, step, 0)


def natural_index(u, per_piece, split, swap):
    per_part = per_piece // split
    inner = lax.rem(u, per_piece)
    return (u - inner) + ((inner // per_part) ^ swap) * per_part + lax.rem(inner, per_part)


def select_start(index, groups):
    for number, group in enumerate(groups):
        @pl.when(index == number)
        def _(group=group):
            for copy in group:
                copy.start()


def transpose_shards(source, target, dp):
    for position in range(8):
        block = dp ^ shard_of(position)
        columns = source[:, pl.ds(pl.multiple_of(block * UNIT, UNIT), UNIT)]
        target[position * UNIT : (position + 1) * UNIT, :] = jnp.transpose(
            columns.astype(F32)
        ).astype(BF16)


SMEM = pl.BlockSpec(memory_space=pltpu.SMEM)
VMEM = pl.BlockSpec(memory_space=pltpu.VMEM)
ANY = pl.BlockSpec(memory_space=pl.ANY)


def params(limit=56):
    return pltpu.CompilerParams(vmem_limit_bytes=limit * 1024 * 1024)


def cost_of(microseconds):
    return pl.CostEstimate(flops=int(microseconds * 1.1e9), bytes_accessed=4 << 20, transcendentals=0)


def sds(shape, dtype):
    return jax.ShapeDtypeStruct(shape, dtype)


def attention_fwd_call(scalars, residual, others, weights, outs, plan, halved, partial, gain, bias):
    rows, depth = others[0].shape
    causal = len(others) == 1
    number = len(plan)
    last = gain is not None
    n_in, n_w, n_o = len(others), len(weights), len(outs)
    flat_w = [a for a in weights]
    has_partial = partial is not None

    def kernel(*refs):
        it = iter(refs)
        sc = next(it)
        in_refs = [next(it) for _ in range(n_in)]
        res_refs = [next(it) for _ in residual] if last else []
        w_refs = [[next(it) for _ in group] for group in flat_w]
        o_refs = [next(it) for _ in range(n_o)]
        part_ref = next(it) if has_partial else None
        gain_ref, bias_ref = (next(it), next(it)) if last else (None, None)
        q_ref, k_ref, v_ref, att_ref, lse_ref = (next(it) for _ in range(5))
        if last:
            low_ref, hat_ref, inv_ref = next(it), next(it), next(it)
        else:
            sum_ref = next(it)
        wbuf, obuf, att_all, diagonal, acc, wsem, osem = (next(it) for _ in range(7))
        length, swap = sc[0], sc[1]

        def offset(unit):
            array, half = unit
            if not halved[array]:
                return 0
            return pl.multiple_of((half ^ swap) * UNIT, UNIT)

        def w_copies(unit, slot):
            copies, column = [], 0
            for group in w_refs:
                ref = group[unit[0]]
                at = pl.ds(offset(unit), UNIT)
                if len(ref.shape) == 2:
                    copies.append(copy_of(ref.at[:, at], wbuf.at[slot, :, column * UNIT : (column + 1) * UNIT], wsem.at[slot, column]))
                    column += 1
                else:
                    for c in range(ref.shape[0]):
                        copies.append(copy_of(ref.at[c, :, at], wbuf.at[slot, :, column * UNIT : (column + 1) * UNIT], wsem.at[slot, column]))
                        column += 1
            return copies

        def o_copy(index):
            unit = plan[index]
            return copy_of(o_refs[unit[0]].at[pl.ds(offset(unit), UNIT), :], obuf.at[index * UNIT : (index + 1) * UNIT, :], osem.at[index])

        select_start(0, [w_copies(plan[0], 0)])
        for index in range(number):
            o_copy(index).start()
        if causal:
            fill_diagonal(diagonal)

        def step(u, carry):
            slot = lax.rem(u, 2)

            @pl.when(u + 1 < number)
            def _():
                select_start(u + 1, [w_copies(unit, 1 - slot) for unit in plan])

            for copy in w_copies(plan[0], slot):
                copy.wait()
            if causal:
                proj = dot(in_refs[0][...], wbuf[slot])
            else:
                proj = jnp.concatenate(
                    [
                        dot(in_refs[0][...], wbuf[slot, :, :UNIT]),
                        dot(in_refs[1][...], wbuf[slot, :, UNIT:]),
                    ],
                    axis=1,
                )
            query = (proj[:, :UNIT].astype(BF16).astype(F32) * SCORE_SCALE).astype(BF16)
            keys, values = proj[:, UNIT : 2 * UNIT].astype(BF16), proj[:, 2 * UNIT :].astype(BF16)
            q_ref[u], k_ref[u], v_ref[u] = query, keys, values
            attended = attend_unit(query, keys, values, length, causal, diagonal, lse_ref.at[u])
            att_ref[u] = attended
            att_all[:, pl.ds(pl.multiple_of(u * UNIT, UNIT), UNIT)] = attended
            return carry

        lax.fori_loop(0, number, step, 0)
        for index in range(number):
            o_copy(index).wait()
        target = acc if last else sum_ref
        if has_partial:
            target[...] = part_ref[...] + dot(att_all[...], obuf[...])
        else:
            target[...] = dot(att_all[...], obuf[...])
        if last:
            def chunk(at):
                if len(res_refs) == 1:
                    old = res_refs[0][at, :].astype(F32)
                else:
                    old = res_refs[0][at, :] * res_refs[1][...] + res_refs[2][...]
                normed, hat, inverse = norm_chunk(RESIDUAL_ALPHA * old + acc[at, :], gain_ref[...], bias_ref[...])
                low_ref[at, :] = normed.astype(BF16)
                hat_ref[at, :] = hat
                inv_ref[at, :] = jnp.broadcast_to(inverse, (ROW_CHUNK, 128))

            each_chunk(rows, chunk)

    unit_rows = sds((number, rows, UNIT), BF16)
    shapes = [unit_rows] * 4 + [sds((number, 2, rows), F32)]
    if last:
        shapes += [sds((rows, depth), BF16), sds((rows, depth), F32), sds((rows, 128), F32)]
    else:
        shapes += [sds((rows, depth), F32)]
    args = [scalars, *others] + (list(residual) if last else [])
    specs = [SMEM] + [VMEM] * (len(args) - 1)
    for group in flat_w:
        args += group
        specs += [ANY] * len(group)
    args += outs
    specs += [ANY] * n_o
    if has_partial:
        args.append(partial)
        specs.append(VMEM)
    if last:
        args += [gain, bias]
        specs += [VMEM, VMEM]
    return pl.pallas_call(
        kernel,
        out_shape=shapes,
        in_specs=specs,
        out_specs=[VMEM] * len(shapes),
        scratch_shapes=[
            pltpu.VMEM((2, depth, 3 * UNIT), BF16),
            pltpu.VMEM((number * UNIT, depth), BF16),
            pltpu.VMEM((rows, number * UNIT), BF16),
            pltpu.VMEM((QUERY_BLOCK, QUERY_BLOCK), F32),
            pltpu.VMEM((rows, depth) if last else (8, 128), F32),
            pltpu.SemaphoreType.DMA((2, 3)),
            pltpu.SemaphoreType.DMA((number,)),
        ],
        compiler_params=params(),
        cost_estimate=cost_of(number * 3.8),
        name="self_fwd" if causal else "cross_fwd",
    )(*args)


def attention_bwd_call(scalars, grad_low, others, weights, outs, saved, plan, halved, carried, norm):
    rows, depth = grad_low.shape
    causal = len(others) == 1
    number, n_in = len(plan), len(others)
    last = norm is not None

    def kernel(*refs):
        it = iter(refs)
        sc = next(it)
        h_ref = next(it)
        in_refs = [next(it) for _ in range(n_in)]
        acc_in = [next(it) for _ in range(n_in)]
        gain_ref = next(it) if last else None
        late_in = [next(it), next(it)] if last else []
        w_refs = [[next(it) for _ in group] for group in weights]
        o_refs = [next(it) for _ in outs]
        s_refs = [[next(it) for _ in call] for call in saved]
        sums = [next(it) for _ in range(n_in)] if not last else [None] + [next(it) for _ in range(n_in - 1)]
        if last:
            low_ref, scaled_ref, gsum_ref, bsum_ref = (next(it) for _ in range(4))
        g_ref = next(it)
        wbuf, obuf, sbuf, lbuf, h_t = (next(it) for _ in range(5))
        in_t = [next(it) for _ in range(n_in)]
        dall, stage, diagonal = next(it), next(it), next(it)
        if last:
            acc, hat, inv = next(it), next(it), next(it)
            lsem = next(it)
        wsem, ssem, gsem = next(it), next(it), next(it)
        length, swap, dp = sc[0], sc[1], sc[2]
        if last:
            sums[0] = acc

        def offset(unit):
            if not halved[unit[0]]:
                return 0
            return pl.multiple_of((unit[1] ^ swap) * UNIT, UNIT)

        def copies(unit, slot):
            out, column = [], 0
            at = pl.ds(offset(unit), UNIT)
            for group in w_refs:
                ref = group[unit[0]]
                sources = [ref.at[:, at]] if len(ref.shape) == 2 else [ref.at[c, :, at] for c in range(ref.shape[0])]
                for source in sources:
                    out.append(copy_of(source, wbuf.at[slot, :, column * UNIT : (column + 1) * UNIT], wsem.at[slot, column]))
                    column += 1
            out.append(copy_of(o_refs[unit[0]].at[at, :], obuf.at[slot], wsem.at[slot, 3]))
            for c in range(4):
                out.append(copy_of(s_refs[unit[2]][c].at[unit[3]], sbuf.at[slot, c], ssem.at[slot, c]))
            out.append(copy_of(s_refs[unit[2]][4].at[unit[3]], lbuf.at[slot], ssem.at[slot, 4]))
            return out

        select_start(0, [copies(plan[0], 0)])
        if last:
            late = [copy_of(late_in[0], hat, lsem.at[0]), copy_of(late_in[1], inv, lsem.at[1])]
            for copy in late:
                copy.start()
        if causal:
            fill_diagonal(diagonal)
        transpose_shards(h_ref, h_t, dp)
        for ref, target in zip(in_refs, in_t):
            transpose_shards(ref, target, dp)
        for source, target in zip(acc_in, sums):
            target[...] = source[...]

        def step(u, carry):
            slot = lax.rem(u, 2)

            @pl.when(u + 1 < number)
            def _():
                select_start(u + 1, [copies(unit, 1 - slot) for unit in plan])

            for copy in copies(plan[0], slot):
                copy.wait()

            @pl.when(u >= 2)
            def _():
                copy_of(stage.at[slot], g_ref.at[0], gsem.at[slot]).wait()

            grad_att = dot_nt(h_ref[...], obuf[slot]).astype(BF16)
            attended = sbuf[slot, 3]
            parts = attend_back_unit(
                sbuf[slot, 0], sbuf[slot, 1], sbuf[slot, 2], attended, grad_att, length, causal, diagonal, lbuf.at[slot]
            )
            for c in range(3):
                dall[:, c * UNIT : (c + 1) * UNIT] = parts[c]
            if causal:
                sums[0][...] += dot_nt(dall[...], wbuf[slot])
                weight = dot(in_t[0][...], dall[...]).astype(BF16)
                stage[slot, :, :, : 3 * UNIT] = weight.reshape(8, UNIT, 3 * UNIT)
            else:
                sums[0][...] += dot_nt(dall[:, :UNIT], wbuf[slot, :, :UNIT])
                sums[1][...] += dot_nt(dall[:, UNIT:], wbuf[slot, :, UNIT:])
                stage[slot, :, :, :UNIT] = dot(in_t[0][...], dall[:, :UNIT]).astype(BF16).reshape(8, UNIT, UNIT)
                stage[slot, :, :, UNIT : 3 * UNIT] = dot(in_t[1][...], dall[:, UNIT:]).astype(BF16).reshape(8, UNIT, 2 * UNIT)
            stage[slot, :, :, 3 * UNIT :] = dot(h_t[...], attended).astype(BF16).reshape(8, UNIT, UNIT)
            copy_of(stage.at[slot], g_ref.at[natural_index(u, 2, 2, swap)], gsem.at[slot]).start()
            return carry

        lax.fori_loop(0, number, step, 0)
        if last:
            for copy in late:
                copy.wait()
            norm_back_rows(acc, hat, inv, gain_ref, low_ref, scaled_ref, gsum_ref, bsum_ref, rows)
        for index in range(max(0, number - 2), number):
            copy_of(stage.at[index % 2], g_ref.at[0], gsem.at[index % 2]).wait()

    big = sds((rows, depth), F32)
    sum_shapes = [big] * (n_in - 1 if last else n_in)
    shapes = list(sum_shapes)
    if last:
        shapes += [sds((rows, depth), BF16), big, sds((8, depth), F32), sds((8, depth), F32)]
    specs_out = [VMEM] * len(shapes) + [ANY]
    shapes.append(sds((number, 8, UNIT, 4 * UNIT), BF16))
    args = [scalars, grad_low, *others, *carried]
    if last:
        args.append(norm[2])
    specs = [SMEM] + [VMEM] * (len(args) - 1)
    tail = []
    if last:
        tail += [norm[0], norm[1]]
    for group in weights:
        tail += group
    tail += outs
    for call in saved:
        tail += call
    scratch = [
        pltpu.VMEM((2, depth, 3 * UNIT), BF16),
        pltpu.VMEM((2, UNIT, depth), BF16),
        pltpu.VMEM((2, 4, rows, UNIT), BF16),
        pltpu.VMEM((2, 2, rows), F32),
        pltpu.VMEM((depth, rows), BF16),
    ]
    scratch += [pltpu.VMEM((depth, rows), BF16)] * n_in
    scratch += [
        pltpu.VMEM((rows, 3 * UNIT), BF16),
        pltpu.VMEM((2, 8, UNIT, 4 * UNIT), BF16),
        pltpu.VMEM((QUERY_BLOCK, QUERY_BLOCK), F32),
    ]
    if last:
        scratch += [
            pltpu.VMEM((rows, depth), F32),
            pltpu.VMEM((rows, depth), F32),
            pltpu.VMEM((rows, 128), F32),
            pltpu.SemaphoreType.DMA((2,)),
        ]
    scratch += [
        pltpu.SemaphoreType.DMA((2, 4)),
        pltpu.SemaphoreType.DMA((2, 5)),
        pltpu.SemaphoreType.DMA((2,)),
    ]
    return pl.pallas_call(
        kernel,
        out_shape=shapes,
        in_specs=specs + [ANY] * len(tail),
        out_specs=specs_out,
        scratch_shapes=scratch,
        compiler_params=params(),
        cost_estimate=cost_of(number * 5.6),
        name="self_bwd" if causal else "cross_bwd",
    )(*args, *tail)


def norm_back_rows(acc, hat, inv, gain_ref, low_ref, scaled_ref, gsum_ref, bsum_ref, rows):
    gsum_ref[...] = jnp.zeros_like(gsum_ref)
    bsum_ref[...] = jnp.zeros_like(bsum_ref)

    def chunk(at):
        gradient, normed = acc[at, :], hat[at, :]
        grad_in = norm_back_chunk(gradient, normed, inv[at, :1], gain_ref[...])
        low_ref[at, :] = grad_in.astype(BF16)
        scaled_ref[at, :] = RESIDUAL_ALPHA * grad_in
        gsum_ref[...] += fold_rows(gradient * normed)
        bsum_ref[...] += fold_rows(gradient)

    each_chunk(rows, chunk)


GELU_SCALE = 0.7978845608028654
GELU_CUBE = 0.044715


def gelu_and_slope(pre):
    square = pre * pre
    inner = pre * (GELU_SCALE + (GELU_SCALE * GELU_CUBE) * square)
    curve = jnp.tanh(inner)
    half = 0.5 + 0.5 * curve
    slope = half * (1.0 + pre * (1.0 - curve) * (GELU_SCALE + (3.0 * GELU_SCALE * GELU_CUBE) * square))
    return pre * half, slope


def ffn_offset(unit, split, swap, total):
    per_part = total // FFN_UNIT // split
    part, inner = unit[1] // per_part, unit[1] % per_part
    if split == 1:
        return inner * FFN_UNIT
    return pl.multiple_of((part ^ swap) * (total // split) + inner * FFN_UNIT, FFN_UNIT)


def ffn_fwd_call(scalars, inputs, ups, downs, plan, splits, partial, final):
    rows, depth = inputs.shape
    number = len(plan)
    last, has_partial = final is not None, partial is not None

    def kernel(*refs):
        it = iter(refs)
        sc, x_ref = next(it), next(it)
        part_ref = next(it) if has_partial else None
        if last:
            gain_old, bias_old, gain_ref, bias_ref = (next(it) for _ in range(4))
            late_in = [next(it), next(it)]
        up_refs = [next(it) for _ in ups]
        down_refs = [next(it) for _ in downs]
        if last:
            out_ref, low_ref, scaled_ref, gsum_ref, bsum_ref = (next(it) for _ in range(5))
        else:
            sum_ref = next(it)
        act_ref, slope_ref = next(it), next(it)
        ubuf, dbuf, abuf, sbuf = (next(it) for _ in range(4))
        if last:
            acc, hat, cot, lsem = (next(it) for _ in range(4))
        wsem, gsem = next(it), next(it)
        swap = sc[1]
        target = acc if last else sum_ref

        def copies(unit, slot):
            up, down = up_refs[unit[0]], down_refs[unit[0]]
            at = pl.ds(ffn_offset(unit, splits[unit[0]], swap, up.shape[1]), FFN_UNIT)
            return [
                copy_of(up.at[:, at], ubuf.at[slot], wsem.at[slot, 0]),
                copy_of(down.at[at, :], dbuf.at[slot], wsem.at[slot, 1]),
            ]

        def saves(u, slot):
            return [
                copy_of(abuf.at[slot], act_ref.at[u], gsem.at[slot, 0]),
                copy_of(sbuf.at[slot], slope_ref.at[u], gsem.at[slot, 1]),
            ]

        select_start(0, [copies(plan[0], 0)])
        if last:
            late = [copy_of(late_in[0], hat, lsem.at[0]), copy_of(late_in[1], cot, lsem.at[1])]
            for copy in late:
                copy.start()
        if has_partial:
            target[...] = part_ref[...]
        else:
            target[...] = jnp.zeros_like(target)

        def step(u, carry):
            slot = lax.rem(u, 2)

            @pl.when(u + 1 < number)
            def _():
                select_start(u + 1, [copies(unit, 1 - slot) for unit in plan])

            for copy in copies(plan[0], slot):
                copy.wait()

            @pl.when(u >= 2)
            def _():
                for copy in saves(u - 2, slot):
                    copy.wait()

            activated, slope = gelu_and_slope(dot(x_ref[...], ubuf[slot]))
            abuf[slot] = activated.astype(BF16)
            sbuf[slot] = slope.astype(BF16)
            target[...] += dot(abuf[slot], dbuf[slot])
            for copy in saves(u, slot):
                copy.start()
            return carry

        lax.fori_loop(0, number, step, 0)
        if last:
            for copy in late:
                copy.wait()
            gsum_ref[...] = jnp.zeros_like(gsum_ref)
            bsum_ref[...] = jnp.zeros_like(bsum_ref)

            def chunk(at):
                old = hat[at, :] * gain_old[...] + bias_old[...]
                normed, xhat, inverse = norm_chunk(RESIDUAL_ALPHA * old + acc[at, :], gain_ref[...], bias_ref[...])
                out_ref[at, :] = normed.astype(BF16)
                gradient = cot[at, :].astype(F32)
                grad_in = norm_back_chunk(gradient, xhat, inverse, gain_ref[...])
                low_ref[at, :] = grad_in.astype(BF16)
                scaled_ref[at, :] = RESIDUAL_ALPHA * grad_in
                gsum_ref[...] += fold_rows(gradient * xhat)
                bsum_ref[...] += fold_rows(gradient)

            each_chunk(rows, chunk)
        for index in range(max(0, number - 2), number):
            for copy in saves(index, index % 2):
                copy.wait()

    big, low = sds((rows, depth), F32), sds((rows, depth), BF16)
    if last:
        shapes = [low, low, big, sds((8, depth), F32), sds((8, depth), F32)]
    else:
        shapes = [big]
    specs_out = [VMEM] * len(shapes) + [ANY, ANY]
    shapes += [sds((number, rows, FFN_UNIT), BF16)] * 2
    args = [scalars, inputs] + ([partial] if has_partial else [])
    if last:
        args += [final[1], final[2], final[4], final[5]]
    specs = [SMEM] + [VMEM] * (len(args) - 1)
    tail = ([final[0], final[3]] if last else []) + list(ups) + list(downs)
    scratch = [
        pltpu.VMEM((2, depth, FFN_UNIT), BF16),
        pltpu.VMEM((2, FFN_UNIT, depth), BF16),
        pltpu.VMEM((2, rows, FFN_UNIT), BF16),
        pltpu.VMEM((2, rows, FFN_UNIT), BF16),
    ]
    if last:
        scratch += [
            pltpu.VMEM((rows, depth), F32),
            pltpu.VMEM((rows, depth), F32),
            pltpu.VMEM((rows, depth), BF16),
            pltpu.SemaphoreType.DMA((2,)),
        ]
    scratch += [pltpu.SemaphoreType.DMA((2, 2)), pltpu.SemaphoreType.DMA((2, 2))]
    return pl.pallas_call(
        kernel,
        out_shape=shapes,
        in_specs=specs + [ANY] * len(tail),
        out_specs=specs_out,
        scratch_shapes=scratch,
        compiler_params=params(),
        cost_estimate=cost_of(number * 2.1),
        name="ffn_fwd",
    )(*args, *tail)


def ffn_bwd_call(scalars, grad_low, inputs, ups, downs, saved, plan, splits, carried, norm, per_piece, parts):
    rows, depth = inputs.shape
    number = len(plan)
    last = norm is not None

    def kernel(*refs):
        it = iter(refs)
        sc, g_in, x_ref, acc_in = (next(it) for _ in range(4))
        gain_ref = next(it) if last else None
        late_in = [next(it), next(it)] if last else []
        up_refs = [next(it) for _ in ups]
        down_refs = [next(it) for _ in downs]
        s_refs = [[next(it) for _ in call] for call in saved]
        if last:
            low_ref, scaled_ref, gsum_ref, bsum_ref = (next(it) for _ in range(4))
        else:
            sum_ref = next(it)
        g_ref = next(it)
        ubuf, dbuf, sbuf, x_t, g_t, stage = (next(it) for _ in range(6))
        if last:
            acc, hat, inv, lsem = (next(it) for _ in range(4))
        wsem, gsem = next(it), next(it)
        swap, dp = sc[1], sc[2]
        target = acc if last else sum_ref

        def copies(unit, slot):
            up, down = up_refs[unit[0]], down_refs[unit[0]]
            at = pl.ds(ffn_offset(unit, splits[unit[0]], swap, up.shape[1]), FFN_UNIT)
            return [
                copy_of(up.at[:, at], ubuf.at[slot], wsem.at[slot, 0]),
                copy_of(down.at[at, :], dbuf.at[slot], wsem.at[slot, 1]),
                copy_of(s_refs[unit[2]][0].at[unit[3]], sbuf.at[slot, 0], wsem.at[slot, 2]),
                copy_of(s_refs[unit[2]][1].at[unit[3]], sbuf.at[slot, 1], wsem.at[slot, 3]),
            ]

        select_start(0, [copies(plan[0], 0)])
        if last:
            late = [copy_of(late_in[0], hat, lsem.at[0]), copy_of(late_in[1], inv, lsem.at[1])]
            for copy in late:
                copy.start()
        transpose_shards(g_in, g_t, dp)
        transpose_shards(x_ref, x_t, dp)
        target[...] = acc_in[...]

        def step(u, carry):
            slot = lax.rem(u, 2)

            @pl.when(u + 1 < number)
            def _():
                select_start(u + 1, [copies(unit, 1 - slot) for unit in plan])

            for copy in copies(plan[0], slot):
                copy.wait()

            @pl.when(u >= 2)
            def _():
                copy_of(stage.at[slot], g_ref.at[0], gsem.at[slot]).wait()

            grad_act = (dot_nt(g_in[...], dbuf[slot]) * sbuf[slot, 1].astype(F32)).astype(BF16)
            stage[slot, :, :, FFN_UNIT:] = dot(g_t[...], sbuf[slot, 0]).astype(BF16).reshape(8, UNIT, FFN_UNIT)
            stage[slot, :, :, :FFN_UNIT] = dot(x_t[...], grad_act).astype(BF16).reshape(8, UNIT, FFN_UNIT)
            target[...] += dot_nt(grad_act, ubuf[slot])
            copy_of(stage.at[slot], g_ref.at[natural_index(u, per_piece, parts, swap)], gsem.at[slot]).start()
            return carry

        lax.fori_loop(0, number, step, 0)
        if last:
            for copy in late:
                copy.wait()
            norm_back_rows(acc, hat, inv, gain_ref, low_ref, scaled_ref, gsum_ref, bsum_ref, rows)
        for index in range(max(0, number - 2), number):
            copy_of(stage.at[index % 2], g_ref.at[0], gsem.at[index % 2]).wait()

    big, low = sds((rows, depth), F32), sds((rows, depth), BF16)
    shapes = [low, big, sds((8, depth), F32), sds((8, depth), F32)] if last else [big]
    specs_out = [VMEM] * len(shapes) + [ANY]
    shapes.append(sds((number, 8, UNIT, 2 * FFN_UNIT), BF16))
    args = [scalars, grad_low, inputs, carried] + ([norm[2]] if last else [])
    specs = [SMEM] + [VMEM] * (len(args) - 1)
    tail = ([norm[0], norm[1]] if last else []) + list(ups) + list(downs)
    for call in saved:
        tail += call
    scratch = [
        pltpu.VMEM((2, depth, FFN_UNIT), BF16),
        pltpu.VMEM((2, FFN_UNIT, depth), BF16),
        pltpu.VMEM((2, 2, rows, FFN_UNIT), BF16),
        pltpu.VMEM((depth, rows), BF16),
        pltpu.VMEM((depth, rows), BF16),
        pltpu.VMEM((2, 8, UNIT, 2 * FFN_UNIT), BF16),
    ]
    if last:
        scratch += [
            pltpu.VMEM((rows, depth), F32),
            pltpu.VMEM((rows, depth), F32),
            pltpu.VMEM((rows, 128), F32),
            pltpu.SemaphoreType.DMA((2,)),
        ]
    scratch += [pltpu.SemaphoreType.DMA((2, 4)), pltpu.SemaphoreType.DMA((2,))]
    return pl.pallas_call(
        kernel,
        out_shape=shapes,
        in_specs=specs + [ANY] * len(tail),
        out_specs=specs_out,
        scratch_shapes=scratch,
        compiler_params=params(),
        cost_estimate=cost_of(number * 2.4),
        name="ffn_bwd",
    )(*args, *tail)


def swap_pairs(count, mask):
    return [(i, i ^ mask) for i in range(count)]


def to_sibling(values):
    return lax.ppermute(values, "tensor", swap_pairs(4, 1))


def over_y(values):
    return lax.ppermute(values, "tensor", swap_pairs(4, 2))


def over_dp(values, mask):
    return lax.ppermute(values, "dp", swap_pairs(8, mask))


def over_x(values):
    return over_dp(values, 1)


def over_z_near(values):
    return over_dp(values, 2)


def over_z_far(values):
    return over_dp(values, 4)


def after(values, *earlier):
    return lax.optimization_barrier((values, *earlier))[0]


def add(*terms):
    total = terms[0].astype(F32)
    for term in terms[1:]:
        total = total + term.astype(F32)
    return total.astype(BF16)


class Reduction:
    def __init__(self, sent):
        self.sent = sent

    def first(self, kept):
        other = to_sibling(self.sent)
        units = kept.shape[0] // 2
        half = units // 2
        pair_kept = kept.reshape(2, units, *kept.shape[1:])[:, half:]
        pair_other = other.reshape(2, units, *other.shape[1:])[:, half:]
        self.left = (kept[:half], other[:half])
        self.right = (pair_kept[:, :, :4], pair_other[:, :, :4])
        self.sends = (
            add(kept[units : units + half], other[units : units + half]),
            add(pair_kept[:, :, 4:], pair_other[:, :, 4:]),
        )
        return self.sends

    def second(self):
        over = over_y(self.sends[0])
        cross = over_x(self.sends[1])
        left, right = self.left, self.right
        self.sends = (
            add(left[0][:, 4:], left[1][:, 4:], over[:, 4:]),
            add(right[0][1], right[1][1], cross[1]),
        )
        self.left = (left[0][:, :4], left[1][:, :4], over[:, :4])
        self.right = (right[0][0], right[1][0], cross[0])
        return self.sends

    def third(self):
        left, right = over_x(self.sends[0]), over_y(self.sends[1])
        self.low = jnp.concatenate([add(*self.left, left), add(*self.right, right)], axis=0)
        self.sends = self.low[:, 2:]
        return self.sends

    def fourth(self):
        low = add(self.low[:, :2], over_z_near(self.sends))
        self.low, self.sends = low[:, 0], low[:, 1]
        return self.sends

    def last(self):
        return add(self.low, over_z_far(self.sends)).astype(F32)


def sentence_body(
    tokens,
    memory,
    dec_lengths,
    mem_lengths,
    self_qkv,
    self_out,
    cross_q,
    cross_kv,
    cross_out,
    ffn_in,
    ffn_out,
    norm_gains,
    norm_biases,
    cotangent,
):
    dp = lax.axis_index("dp")
    mine = lax.axis_index("tensor")
    swap = dp & 1
    self_scalars = jnp.stack([dec_lengths[0, mine], swap, dp, mine]).astype(jnp.int32)
    cross_scalars = jnp.stack([mem_lengths[0, mine], swap, dp, mine]).astype(jnp.int32)
    gains = [norm_gains[i : i + 1] for i in range(3)]
    biases = [norm_biases[i : i + 1] for i in range(3)]

    def own_half(values, axis):
        half = values.shape[axis] // 2
        return lax.dynamic_slice_in_dim(values, swap * half, half, axis)

    def fetch(values, axis, *earlier):
        send = own_half(values, axis)
        if earlier:
            send = after(send, *earlier)
        near = over_y(send)
        far = over_dp(near, 1)
        return [values, to_sibling(values), near, far, to_sibling(near), to_sibling(far)]

    halves = [True, True]
    early = [(0, 0), (0, 1), (1, 0), (1, 1)]
    pair = [(0, 0), (1, 0)]

    qkv_sib, out_sib = to_sibling(self_qkv), to_sibling(self_out)
    qkv_near = over_y(own_half(self_qkv, 2))
    out_near = over_y(own_half(self_out, 0))
    self_a = attention_fwd_call(
        self_scalars, [], [tokens], [[self_qkv, qkv_sib]], [self_out, out_sib], early, halves, None, None, None
    )
    cq_near = over_y(after(own_half(cross_q, 1), out_near))
    ckv_near = over_y(after(own_half(cross_kv, 2), out_near))
    cout_near = over_y(after(own_half(cross_out, 0), out_near))
    qkv_gone, out_gone = after(qkv_near, self_a[5]), after(out_near, self_a[5])
    qkv_far, qkv_near3 = over_x(qkv_gone), to_sibling(qkv_gone)
    out_far, out_near3 = over_x(out_gone), to_sibling(out_gone)
    self_b = attention_fwd_call(
        self_scalars, [], [tokens], [[qkv_near, qkv_near3]], [out_near, out_near3], pair, [False] * 2,
        self_a[5], None, None,
    )
    qkv_far3, out_far3 = to_sibling(qkv_far), to_sibling(out_far)
    self_c = attention_fwd_call(
        self_scalars, [tokens], [tokens], [[qkv_far, qkv_far3]], [out_far, out_far3], pair, [False] * 2,
        self_b[5], gains[0], biases[0],
    )
    first_low, first_hat, first_inv = self_c[5:]
    w_qkv = [self_qkv, qkv_sib, qkv_near, qkv_far, qkv_near3, qkv_far3]
    w_self = [self_out, out_sib, out_near, out_far, out_near3, out_far3]

    cq_sib, ckv_sib, cout_sib = (
        to_sibling(after(w, out_near)) for w in (cross_q, cross_kv, cross_out)
    )
    cq_far, ckv_far, cout_far = (over_x(w) for w in (cq_near, ckv_near, cout_near))
    cq_near3, ckv_near3, cout_near3 = (to_sibling(w) for w in (cq_near, ckv_near, cout_near))
    cross_in = [first_low, memory]
    cross_a = attention_fwd_call(
        cross_scalars, [], cross_in, [[cross_q, cq_sib], [cross_kv, ckv_sib]], [cross_out, cout_sib], early,
        halves, None, None, None,
    )
    in_near = over_y(after(own_half(ffn_in, 1), cout_near))
    down_near = over_y(after(own_half(ffn_out, 0), cout_near))
    cross_b = attention_fwd_call(
        cross_scalars, [], cross_in, [[cq_near, cq_near3], [ckv_near, ckv_near3]], [cout_near, cout_near3],
        pair, [False] * 2, cross_a[5], None, None,
    )
    cq_far3, ckv_far3, cout_far3 = (to_sibling(w) for w in (cq_far, ckv_far, cout_far))
    cross_c = attention_fwd_call(
        cross_scalars, [first_hat, gains[0], biases[0]], cross_in, [[cq_far, cq_far3], [ckv_far, ckv_far3]],
        [cout_far, cout_far3], pair, [False] * 2, cross_b[5], gains[1], biases[1],
    )
    second_low, second_hat, second_inv = cross_c[5:]
    w_cq = [cross_q, cq_sib, cq_near, cq_far, cq_near3, cq_far3]
    w_ckv = [cross_kv, ckv_sib, ckv_near, ckv_far, ckv_near3, ckv_far3]
    w_cross = [cross_out, cout_sib, cout_near, cout_far, cout_near3, cout_far3]

    in_sib, down_sib = to_sibling(after(ffn_in, cout_near)), to_sibling(after(ffn_out, cout_near))
    in_far, down_far = over_x(in_near), over_x(down_near)
    in_near3, down_near3 = to_sibling(in_near), to_sibling(down_near)
    in_far3, down_far3 = to_sibling(in_far), to_sibling(down_far)
    w_in = [ffn_in, in_sib, in_near, in_far, in_near3, in_far3]
    w_down = [ffn_out, down_sib, down_near, down_far, down_near3, down_far3]
    per_piece = ffn_in.shape[1] // FFN_UNIT
    ffn_early = [(p, u) for p in (0, 1) for u in range(per_piece)]
    ffn_pair = [(p, u) for p in (0, 1) for u in range(per_piece // 2)]
    ffn_a = ffn_fwd_call(
        cross_scalars, second_low, w_in[:2], w_down[:2], ffn_early, [2, 2], None, None
    )
    ffn_b = ffn_fwd_call(
        cross_scalars, second_low, w_in[2::2], w_down[2::2], ffn_pair, [1] * 2, ffn_a[0], None
    )
    ffn_c = ffn_fwd_call(
        cross_scalars, second_low, w_in[3::2], w_down[3::2], ffn_pair, [1] * 2, ffn_b[0],
        (second_hat, gains[1], biases[1], cotangent, gains[2], biases[2]),
    )
    out_rows, third_low, third_scaled, third_gain, third_bias = ffn_c[:5]

    def ffn_plan(pieces):
        units = []
        for piece in pieces:
            for u in range(per_piece):
                inner = u % (per_piece // 2)
                if piece < 2:
                    units.append((piece, u, 0, piece * per_piece + u))
                elif u < per_piece // 2:
                    units.append((2 * piece - 2, inner, 1, (piece - 2) * (per_piece // 2) + inner))
                else:
                    units.append((2 * piece - 1, inner, 2, (piece - 2) * (per_piece // 2) + inner))
        return units

    def plan_of(pieces):
        units = []
        for piece in pieces:
            for half in (0, 1):
                if piece < 2:
                    units.append((piece, half, 0, 2 * piece + half))
                else:
                    units.append((2 * piece - 2 + half, 0, 1 + half, piece - 2))
        return units

    splits = [2, 2, 1, 1, 1, 1]
    halved = [True, True, False, False, False, False]
    ffn_saved = [ffn_a[1:3], ffn_b[1:3], ffn_c[5:7]]
    ffn_d = ffn_bwd_call(
        cross_scalars, third_low, second_low, w_in, w_down, ffn_saved, ffn_plan((1, 3)), splits,
        third_scaled, None, per_piece, 2,
    )
    ffn_sum = Reduction(ffn_d[1])
    ffn_e = ffn_bwd_call(
        cross_scalars, third_low, second_low, w_in, w_down, ffn_saved, ffn_plan((0, 2)), splits,
        ffn_d[0], (second_hat, second_inv, gains[1]), per_piece, 2,
    )
    second_back, second_scaled, second_gain, second_bias = ffn_e[:4]
    second_back = after(second_back, *ffn_sum.first(ffn_e[4]))

    cross_saved = [cross_a[:5], cross_b[:5], cross_c[:5]]
    cross_d = attention_bwd_call(
        cross_scalars, second_back, cross_in, [w_cq, w_ckv], w_cross, cross_saved, plan_of((1, 3)), halved,
        [second_scaled, jnp.zeros(second_scaled.shape, F32)], None,
    )
    cross_sum = Reduction(cross_d[2])
    cross_e = attention_bwd_call(
        cross_scalars, second_back, cross_in, [w_cq, w_ckv], w_cross, cross_saved, plan_of((0, 2)), halved,
        cross_d[:2], (first_hat, first_inv, gains[0]),
    )
    grad_memory, first_back, first_scaled, first_gain, first_bias = cross_e[:5]
    norm_sums = jnp.stack([first_gain, second_gain, third_gain, first_bias, second_bias, third_bias])
    norm_total = jnp.sum(norm_sums, axis=1)
    first_back = after(first_back, *ffn_sum.second(), *cross_sum.first(cross_e[5]), norm_total)

    self_saved = [self_a[:5], self_b[:5], self_c[:5]]
    self_d = attention_bwd_call(
        self_scalars, first_back, [tokens], [w_qkv], w_self, self_saved, plan_of((1, 3)), halved,
        [first_scaled], None,
    )
    self_sum = Reduction(self_d[1])
    norm_total = norm_total + to_sibling(norm_total)
    gate = after(self_d[0], ffn_sum.third(), norm_total)
    self_e = attention_bwd_call(
        self_scalars, first_back, [tokens], [w_qkv], w_self, self_saved, plan_of((0, 2)), halved,
        [gate], None,
    )
    grad_tokens = self_e[0]
    own_sends = self_sum.first(self_e[1])
    cross_sum.second()
    ffn_sum.fourth()
    norm_total = norm_total + over_y(norm_total)
    self_sum.second()
    cross_sum.third()
    ffn_sum = ffn_sum.last()
    norm_total = norm_total + over_x(norm_total)
    self_sum.third()
    cross_sum.fourth()
    norm_total = norm_total + over_z_near(norm_total)
    self_sum.fourth()
    cross_sum = cross_sum.last()
    norm_total = norm_total + over_z_far(norm_total)
    self_sum = self_sum.last()

    def matrices(total):
        return total.reshape(2, UNIT, 4, UNIT).transpose(2, 1, 0, 3).reshape(4, UNIT, 2 * UNIT)

    self_grads, cross_grads = matrices(self_sum), matrices(cross_sum)
    ffn_grads = ffn_sum.transpose(1, 0, 2)
    return (
        out_rows,
        grad_tokens,
        grad_memory,
        self_grads[:3],
        self_grads[3].T,
        cross_grads[0],
        cross_grads[1:3],
        cross_grads[3].T,
        ffn_grads[:, :, :FFN_UNIT].reshape(UNIT, -1),
        ffn_grads[:, :, FFN_UNIT:].reshape(UNIT, -1).T,
        norm_total[:3],
        norm_total[3:],
    )


def sentence_fits(mesh, tokens, memory, dec_lengths):
    shape = dict(mesh.shape)
    rows = tokens.shape[0] // mesh.size
    sentences = dec_lengths.shape[1]
    return (
        shape["tensor"] == 4
        and shape["dp"] == 8
        and sentences == 4
        and rows == 512
        and memory.shape[0] // mesh.size == rows
        and tokens.shape[1] == 1024
    )


def smooth_gate(values):
    return jax.nn.gelu(values, approximate=True)


def norm_rows(hidden, norm_gain, norm_bias):
    center = hidden - jnp.mean(hidden, axis=-1, keepdims=True)
    inverse = lax.rsqrt(jnp.mean(center * center, axis=-1, keepdims=True) + NORM_EPSILON)
    normed = center * inverse
    return (normed * norm_gain + norm_bias, normed, inverse)


def norm_back(gradient, normed, inverse, norm_gain):
    scaled = gradient * norm_gain
    grad_in = inverse * (
        scaled
        - jnp.mean(scaled, axis=-1, keepdims=True)
        - normed * jnp.mean(scaled * normed, axis=-1, keepdims=True)
    )
    return (grad_in, jnp.sum(gradient * normed, axis=0), jnp.sum(gradient, axis=0))


def head_view(values, sentences):
    return values.reshape(sentences, -1, values.shape[1] // HEAD_DIM, HEAD_DIM)


def masked_scores(query_heads, key_heads, key_mask):
    scores = jnp.einsum(
        "sqhe,skhe->shqk", query_heads, key_heads, preferred_element_type=jnp.float32
    ) * HEAD_DIM ** (-0.5)
    return jnp.where(key_mask, scores, MASKED_SCORE)


def attention_forward(query_rows, key_rows, value_rows, key_mask, sentences):
    scores = masked_scores(
        head_view(query_rows, sentences), head_view(key_rows, sentences), key_mask
    )
    row_peak = jnp.max(scores, axis=-1, keepdims=True)
    exponent_terms = jnp.exp(scores - row_peak)
    row_sum = jnp.sum(exponent_terms, axis=-1, keepdims=True)
    softmax_probs = exponent_terms / row_sum
    attended = jnp.einsum(
        "shqk,skhe->sqhe",
        softmax_probs.astype(jnp.bfloat16),
        head_view(value_rows, sentences),
        preferred_element_type=jnp.float32,
    ).astype(jnp.bfloat16)
    return (attended.reshape(query_rows.shape), row_peak + jnp.log(row_sum))


def attention_backward(query_rows, key_rows, value_rows, key_mask, log_total, grad_rows, sentences):
    query_heads = head_view(query_rows, sentences)
    key_heads = head_view(key_rows, sentences)
    value_heads = head_view(value_rows, sentences)
    grad_heads = head_view(grad_rows, sentences)
    softmax_probs = jnp.exp(masked_scores(query_heads, key_heads, key_mask) - log_total)
    grad_probs = jnp.einsum(
        "sqhe,skhe->shqk", grad_heads, value_heads, preferred_element_type=jnp.float32
    )
    row_delta = jnp.sum(softmax_probs * grad_probs, axis=-1, keepdims=True)
    grad_scores = (softmax_probs * (grad_probs - row_delta)).astype(jnp.bfloat16)
    score_scale = HEAD_DIM ** (-0.5)
    grad_query = (
        jnp.einsum("shqk,skhe->sqhe", grad_scores, key_heads, preferred_element_type=jnp.float32)
        * score_scale
    ).astype(jnp.bfloat16)
    grad_key = (
        jnp.einsum("shqk,sqhe->skhe", grad_scores, query_heads, preferred_element_type=jnp.float32)
        * score_scale
    ).astype(jnp.bfloat16)
    grad_value = jnp.einsum(
        "shqk,sqhe->skhe",
        softmax_probs.astype(jnp.bfloat16),
        grad_heads,
        preferred_element_type=jnp.float32,
    ).astype(jnp.bfloat16)
    return (
        grad_query.reshape(query_rows.shape),
        grad_key.reshape(key_rows.shape),
        grad_value.reshape(value_rows.shape),
    )


def body(
    tokens,
    memory,
    dec_lengths,
    mem_lengths,
    self_qkv,
    self_out,
    cross_q,
    cross_kv,
    cross_out,
    ffn_in,
    ffn_out,
    norm_gains,
    norm_biases,
    cotangent,
):
    row_share = tokens.shape[0]
    sentences = dec_lengths.shape[1]
    all_tokens, all_memory = (
        lax.all_gather(tokens, "tensor", axis=0, tiled=True),
        lax.all_gather(memory, "tensor", axis=0, tiled=True),
    )
    sentence_len = all_tokens.shape[0] // sentences
    memory_len = all_memory.shape[0] // sentences
    positions = jnp.arange(sentence_len, dtype=jnp.int32)
    self_mask = (
        (positions[None, :] <= positions[:, None])[None]
        & (positions[None, None, :] < dec_lengths[0][:, None, None])
    )[:, None]
    memory_positions = jnp.arange(memory_len, dtype=jnp.int32)
    cross_mask = (memory_positions[None, :] < mem_lengths[0][:, None])[:, None, None, :]

    def branch_rows(attended, weight):
        return lax.psum_scatter(
            jnp.dot(attended, weight, preferred_element_type=jnp.float32).astype(jnp.bfloat16),
            "tensor",
            scatter_dimension=0,
            tiled=True,
        ).astype(jnp.float32)

    def branch_grad(grad_rows, attended, weight):
        grad_low = grad_rows.astype(jnp.bfloat16)
        grad_all = lax.all_gather(grad_low, "tensor", axis=0, tiled=True)
        grad_attended = jnp.dot(grad_all, weight.T, preferred_element_type=jnp.float32).astype(
            jnp.bfloat16
        )
        weight_part = jnp.dot(attended.T, grad_all, preferred_element_type=jnp.float32)
        return (grad_attended, weight_part)

    def gather_normed(values):
        return lax.all_gather(values, "tensor", axis=0, tiled=True)

    def head_input_sum(term):
        return lax.psum_scatter(
            term(jnp.int32(0), row_share * lax.axis_size("tensor")).astype(jnp.bfloat16),
            "tensor",
            scatter_dimension=0,
            tiled=True,
        ).astype(jnp.float32)

    self_proj = jnp.einsum(
        "td,cde->cte", all_tokens, self_qkv, preferred_element_type=jnp.float32
    ).astype(jnp.bfloat16)
    self_att, self_lse = attention_forward(
        self_proj[0], self_proj[1], self_proj[2], self_mask, sentences
    )
    self_branch = branch_rows(self_att, self_out)
    first_norm, first_hat, first_inv = norm_rows(
        RESIDUAL_ALPHA * tokens.astype(jnp.float32) + self_branch, norm_gains[0], norm_biases[0]
    )
    first_all = gather_normed(first_norm.astype(jnp.bfloat16))
    cross_query = jnp.dot(first_all, cross_q, preferred_element_type=jnp.float32).astype(
        jnp.bfloat16
    )
    cross_proj = jnp.einsum(
        "td,cde->cte", all_memory, cross_kv, preferred_element_type=jnp.float32
    ).astype(jnp.bfloat16)
    cross_att, cross_lse = attention_forward(
        cross_query, cross_proj[0], cross_proj[1], cross_mask, sentences
    )
    cross_branch = branch_rows(cross_att, cross_out)
    second_norm, second_hat, second_inv = norm_rows(
        RESIDUAL_ALPHA * first_norm + cross_branch, norm_gains[1], norm_biases[1]
    )
    second_all = gather_normed(second_norm.astype(jnp.bfloat16))
    pre_gate = jnp.dot(second_all, ffn_in, preferred_element_type=jnp.float32)
    activated = smooth_gate(pre_gate).astype(jnp.bfloat16)
    ffn_branch = lax.psum_scatter(
        jnp.dot(activated, ffn_out, preferred_element_type=jnp.float32).astype(jnp.bfloat16),
        "tensor",
        scatter_dimension=0,
        tiled=True,
    ).astype(jnp.float32)
    out_rows, third_hat, third_inv = norm_rows(
        RESIDUAL_ALPHA * second_norm + ffn_branch, norm_gains[2], norm_biases[2]
    )
    grad_third, third_gain, third_bias = norm_back(
        cotangent.astype(jnp.float32), third_hat, third_inv, norm_gains[2]
    )
    grad_ffn_all = lax.all_gather(grad_third.astype(jnp.bfloat16), "tensor", axis=0, tiled=True)
    unused_gate, gate_pull = jax.vjp(smooth_gate, pre_gate)
    grad_act = gate_pull(jnp.dot(grad_ffn_all, ffn_out.T, preferred_element_type=jnp.float32))[
        0
    ].astype(jnp.bfloat16)
    grad_ffn_out = jnp.dot(activated.T, grad_ffn_all, preferred_element_type=jnp.float32)
    grad_ffn_in = jnp.dot(second_all.T, grad_act, preferred_element_type=jnp.float32)
    grad_second = RESIDUAL_ALPHA * grad_third + lax.psum_scatter(
        jnp.dot(grad_act, ffn_in.T, preferred_element_type=jnp.float32).astype(jnp.bfloat16),
        "tensor",
        scatter_dimension=0,
        tiled=True,
    ).astype(jnp.float32)
    grad_second_in, second_gain, second_bias = norm_back(
        grad_second, second_hat, second_inv, norm_gains[1]
    )
    grad_cross_att, cross_out_part = branch_grad(grad_second_in, cross_att, cross_out)
    grad_cq, grad_ck, grad_cv = attention_backward(
        cross_query, cross_proj[0], cross_proj[1], cross_mask, cross_lse, grad_cross_att, sentences
    )
    grad_cross_q = jnp.dot(first_all.T, grad_cq, preferred_element_type=jnp.float32)
    cross_grads = jnp.stack([grad_ck, grad_cv])
    grad_cross_kv = jnp.einsum(
        "td,cte->cde", all_memory, cross_grads, preferred_element_type=jnp.float32
    )
    grad_memory = lax.psum_scatter(
        jnp.einsum("cte,cde->td", cross_grads, cross_kv, preferred_element_type=jnp.float32).astype(
            jnp.bfloat16
        ),
        "tensor",
        scatter_dimension=0,
        tiled=True,
    ).astype(jnp.float32)

    def cross_input_term(first_row, row_total):
        return jnp.dot(grad_cq, cross_q.T, preferred_element_type=jnp.float32)

    cross_input = head_input_sum(cross_input_term)
    grad_first = RESIDUAL_ALPHA * grad_second_in + cross_input
    grad_first_in, first_gain, first_bias = norm_back(
        grad_first, first_hat, first_inv, norm_gains[0]
    )
    grad_self_att, self_out_part = branch_grad(grad_first_in, self_att, self_out)
    grad_sq, grad_sk, grad_sv = attention_backward(
        self_proj[0], self_proj[1], self_proj[2], self_mask, self_lse, grad_self_att, sentences
    )
    self_grads = jnp.stack([grad_sq, grad_sk, grad_sv])
    grad_self_qkv = jnp.einsum(
        "td,cte->cde", all_tokens, self_grads, preferred_element_type=jnp.float32
    )

    def self_input_term(first_row, row_total):
        return jnp.einsum("cte,cde->td", self_grads, self_qkv, preferred_element_type=jnp.float32)

    self_input = head_input_sum(self_input_term)
    grad_tokens = RESIDUAL_ALPHA * grad_first_in + self_input
    summed = (
        lax.psum_scatter(
            grad_self_qkv.astype(jnp.bfloat16), "dp", scatter_dimension=1, tiled=True
        ).astype(jnp.float32),
        lax.psum_scatter(
            self_out_part.astype(jnp.bfloat16), "dp", scatter_dimension=1, tiled=True
        ).astype(jnp.float32),
        lax.psum_scatter(
            grad_cross_q.astype(jnp.bfloat16), "dp", scatter_dimension=0, tiled=True
        ).astype(jnp.float32),
        lax.psum_scatter(
            grad_cross_kv.astype(jnp.bfloat16), "dp", scatter_dimension=1, tiled=True
        ).astype(jnp.float32),
        lax.psum_scatter(
            cross_out_part.astype(jnp.bfloat16), "dp", scatter_dimension=1, tiled=True
        ).astype(jnp.float32),
        lax.psum_scatter(
            grad_ffn_in.astype(jnp.bfloat16), "dp", scatter_dimension=0, tiled=True
        ).astype(jnp.float32),
        lax.psum_scatter(
            grad_ffn_out.astype(jnp.bfloat16), "dp", scatter_dimension=1, tiled=True
        ).astype(jnp.float32),
    )
    gain_total, bias_total = lax.psum(
        (
            jnp.stack([first_gain, second_gain, third_gain]),
            jnp.stack([first_bias, second_bias, third_bias]),
        ),
        ("dp", "tensor"),
    )
    return (
        out_rows.astype(jnp.bfloat16),
        grad_tokens,
        grad_memory,
        summed[0],
        summed[1],
        summed[2],
        summed[3],
        summed[4],
        summed[5],
        summed[6],
        gain_total,
        bias_total,
    )


def solution(mesh):
    in_specs = (
        P(("dp", "tensor"), None),
        P(("dp", "tensor"), None),
        P("dp", None),
        P("dp", None),
        P(None, None, "tensor"),
        P("tensor", None),
        P(None, "tensor"),
        P(None, None, "tensor"),
        P("tensor", None),
        P(None, "tensor"),
        P("tensor", None),
        P(),
        P(),
        P(("dp", "tensor"), None),
    )
    out_specs = (
        P(("dp", "tensor"), None),
        P(("dp", "tensor"), None),
        P(("dp", "tensor"), None),
        P(None, "dp", "tensor"),
        P("tensor", "dp"),
        P("dp", "tensor"),
        P(None, "dp", "tensor"),
        P("tensor", "dp"),
        P("dp", "tensor"),
        P("tensor", "dp"),
        P(),
        P(),
    )

    def step(*args):
        chosen = sentence_body if sentence_fits(mesh, args[0], args[1], args[2]) else body
        return jax.shard_map(
            chosen, mesh=mesh, in_specs=in_specs, out_specs=out_specs, check_vma=False
        )(*args)

    return step
```

```python
import functools
import jax
import jax.numpy as jnp
from jax import lax
from jax.experimental import pallas as pl
from jax.experimental.pallas import tpu as pltpu
from jax.sharding import PartitionSpec as P

HEAD_DIM = 64
RESIDUAL_ALPHA = 4.16
NORM_EPSILON = 1e-05
MASKED_SCORE = -1000000000.0
SCORE_SCALE = HEAD_DIM ** (-0.5)
UNIT = 128
QUERY_BLOCK = 256
FFN_UNIT = 512
ROW_CHUNK = 64
BF16 = jnp.bfloat16
F32 = jnp.float32


def dot(left, right):
    return lax.dot_general(left, right, (((1,), (0,)), ((), ())), preferred_element_type=F32)


def dot_nt(left, right):
    return lax.dot_general(left, right, (((1,), (1,)), ((), ())), preferred_element_type=F32)


def shard_of(position):
    return ((position >> 2) & 1) | (position & 2) | ((position & 1) << 2)


def copy_of(source, target, sem):
    return pltpu.make_async_copy(source, target, sem)


def own_lanes(rows, head):
    lanes = lax.broadcasted_iota(jnp.int32, rows.shape, 1)
    return jnp.where((lanes >= HEAD_DIM) if head else (lanes < HEAD_DIM), rows, 0.0)


def extended_keys(keys, length):
    lanes = lax.broadcasted_iota(jnp.int32, keys.shape, 1)
    rows = lax.broadcasted_iota(jnp.int32, keys.shape, 0)
    mask = jnp.where((lanes == 0) & (rows >= length), MASKED_SCORE, 0.0).astype(BF16)
    keys = keys.astype(F32)
    return [jnp.concatenate([own_lanes(keys, head).astype(BF16), mask], axis=1) for head in (0, 1)]


def extended_query(query):
    lanes = lax.broadcasted_iota(jnp.int32, query.shape, 1)
    return jnp.concatenate([query, jnp.where(lanes == 0, 1.0, 0.0).astype(BF16)], axis=1)


def fill_diagonal(diagonal):
    keys = lax.broadcasted_iota(jnp.int32, diagonal.shape, 0)
    queries = lax.broadcasted_iota(jnp.int32, diagonal.shape, 1)
    diagonal[...] = jnp.where(keys <= queries, 0.0, MASKED_SCORE)


def key_ranges(block, keys, causal):
    if not causal:
        return [(0, keys)]
    return [(low, low + QUERY_BLOCK) for low in range(0, (block + 1) * QUERY_BLOCK, QUERY_BLOCK)]


def attend_unit(query, keys, values, length, causal, diagonal, lse_ref):
    rows, count = query.shape[0], keys.shape[0]
    values_t = jnp.transpose(values.astype(F32)).astype(BF16)
    wide_keys, wide_query = extended_keys(keys, length), extended_query(query)
    items = [(head, block) for block in range(rows // QUERY_BLOCK) for head in (0, 1)]
    scores, probs, totals, mixed = {}, {}, {}, {}
    for head, block in items:
        part = wide_query[block * QUERY_BLOCK : (block + 1) * QUERY_BLOCK]
        ranges = key_ranges(block, count, causal)
        scores[head, block] = [dot_nt(wide_keys[head][a:b], part) for a, b in ranges]
        if causal:
            scores[head, block][-1] = scores[head, block][-1] + diagonal[...]
    for head, block in items:
        pieces = scores[head, block]
        peak = functools.reduce(jnp.maximum, [jnp.max(p, axis=0, keepdims=True) for p in pieces])
        terms = [jnp.exp(p - peak) for p in pieces]
        total = sum(jnp.sum(t, axis=0, keepdims=True) for t in terms)
        at = slice(block * QUERY_BLOCK, (block + 1) * QUERY_BLOCK)
        lse_ref[head : head + 1, at] = peak + jnp.log(total)
        totals[head, block] = total
        probs[head, block] = jnp.concatenate([t.astype(BF16) for t in terms], axis=0)
    for head, block in items:
        own = values_t[head * HEAD_DIM : (head + 1) * HEAD_DIM, : probs[head, block].shape[0]]
        mixed[head, block] = dot(own, probs[head, block]) / totals[head, block]
    out = [
        jnp.transpose(jnp.concatenate([mixed[0, block], mixed[1, block]], axis=0))
        for block in range(rows // QUERY_BLOCK)
    ]
    return jnp.concatenate(out, axis=0).astype(BF16)


def attend_back_unit(query, keys, values, attended, grad, length, causal, diagonal, lse_ref):
    rows, count = query.shape[0], keys.shape[0]
    blocks = range(rows // QUERY_BLOCK)
    query_f, keys_f, grad_f = (a.astype(F32) for a in (query, keys, grad))
    wide_keys, wide_query = extended_keys(keys, length), extended_query(query)
    delta = jnp.transpose(grad_f * attended.astype(F32))
    deltas = [
        jnp.sum(delta[head * HEAD_DIM : (head + 1) * HEAD_DIM], axis=0, keepdims=True)
        for head in (0, 1)
    ]
    keys_t = jnp.transpose(keys_f).astype(BF16)
    query_own = [own_lanes(query_f, head).astype(BF16) for head in (0, 1)]
    grad_own = [own_lanes(grad_f, head).astype(BF16) for head in (0, 1)]
    items = [(head, block) for block in blocks for head in (0, 1)]
    scores, slopes, probs, back, grad_query = {}, {}, {}, {}, {}
    for head, block in items:
        at = slice(block * QUERY_BLOCK, (block + 1) * QUERY_BLOCK)
        for a, b in key_ranges(block, count, causal):
            scores[head, block, a] = dot_nt(wide_keys[head][a:b], wide_query[at])
            slopes[head, block, a] = dot_nt(values[a:b], grad_own[head][at])
    for head, block in items:
        at = slice(block * QUERY_BLOCK, (block + 1) * QUERY_BLOCK)
        ranges = key_ranges(block, count, causal)
        for a, b in ranges:
            score = scores[head, block, a]
            if causal and (a, b) == ranges[-1]:
                score = score + diagonal[...]
            prob = jnp.exp(score - lse_ref[head : head + 1, at])
            probs[head, block, a] = prob.astype(BF16)
            back[head, block, a] = (prob * (slopes[head, block, a] - deltas[head][:, at])).astype(BF16)
    for head, block in items:
        own = keys_t[head * HEAD_DIM : (head + 1) * HEAD_DIM]
        grad_query[head, block] = sum(
            dot(own[:, a:b], back[head, block, a]) for a, b in key_ranges(block, count, causal)
        )
    grad_keys, grad_values = [], []
    for low in sorted({key[2] for key in back}):
        live = [key for key in back if key[2] == low]
        at = [slice(block * QUERY_BLOCK, (block + 1) * QUERY_BLOCK) for _, block, _ in live]
        grad_values.append(
            dot(
                jnp.concatenate([probs[key] for key in live], axis=1),
                jnp.concatenate([grad_own[key[0]][a] for key, a in zip(live, at)], axis=0),
            )
        )
        grad_keys.append(
            dot(
                jnp.concatenate([back[key] for key in live], axis=1),
                jnp.concatenate([query_own[key[0]][a] for key, a in zip(live, at)], axis=0),
            )
        )
    grad_query = [
        jnp.transpose(jnp.concatenate([grad_query[0, block], grad_query[1, block]], axis=0)) * SCORE_SCALE
        for block in blocks
    ]
    return tuple(
        jnp.concatenate(parts, axis=0).astype(BF16) for parts in (grad_query, grad_keys, grad_values)
    )


def norm_chunk(hidden, gain, bias):
    center = hidden - jnp.mean(hidden, axis=-1, keepdims=True)
    inverse = lax.rsqrt(jnp.mean(center * center, axis=-1, keepdims=True) + NORM_EPSILON)
    normed = center * inverse
    return normed * gain + bias, normed, inverse


def norm_back_chunk(gradient, normed, inverse, gain):
    scaled = gradient * gain
    return inverse * (
        scaled
        - jnp.mean(scaled, axis=-1, keepdims=True)
        - normed * jnp.mean(scaled * normed, axis=-1, keepdims=True)
    )


def fold_rows(values):
    return jnp.sum(values.reshape(values.shape[0] // 8, 8, values.shape[1]), axis=0)


def each_chunk(rows, body):
    def step(index, carry):
        body(pl.ds(pl.multiple_of(index * ROW_CHUNK, ROW_CHUNK), ROW_CHUNK))
        return carry

    lax.fori_loop(0, rows // ROW_CHUNK, step, 0)


def natural_index(u, per_piece, split, swap):
    per_part = per_piece // split
    inner = lax.rem(u, per_piece)
    return (u - inner) + ((inner // per_part) ^ swap) * per_part + lax.rem(inner, per_part)


def transpose_shards(source, target, dp):
    for position in range(8):
        block = dp ^ shard_of(position)
        columns = source[:, pl.ds(pl.multiple_of(block * UNIT, UNIT), UNIT)]
        target[position * UNIT : (position + 1) * UNIT, :] = jnp.transpose(
            columns.astype(F32)
        ).astype(BF16)


SMEM = pl.BlockSpec(memory_space=pltpu.SMEM)
VMEM = pl.BlockSpec(memory_space=pltpu.VMEM)
ANY = pl.BlockSpec(memory_space=pl.ANY)


def params(limit=56):
    return pltpu.CompilerParams(vmem_limit_bytes=limit * 1024 * 1024)


def cost_of(microseconds):
    return pl.CostEstimate(flops=int(microseconds * 1.1e9), bytes_accessed=4 << 20, transcendentals=0)


def sds(shape, dtype):
    return jax.ShapeDtypeStruct(shape, dtype)


def attention_fwd_call(scalars, residual, others, weights, outs, plan, halved, partial, gain, bias):
    rows, depth = others[0].shape
    causal = len(others) == 1
    number = len(plan)
    last = gain is not None
    n_in, n_w, n_o = len(others), len(weights), len(outs)
    flat_w = [a for a in weights]
    has_partial = partial is not None

    def kernel(*refs):
        it = iter(refs)
        sc = next(it)
        in_refs = [next(it) for _ in range(n_in)]
        res_refs = [next(it) for _ in residual] if last else []
        w_refs = [[next(it) for _ in group] for group in flat_w]
        o_refs = [next(it) for _ in range(n_o)]
        part_ref = next(it) if has_partial else None
        gain_ref, bias_ref = (next(it), next(it)) if last else (None, None)
        q_ref, k_ref, v_ref, att_ref, lse_ref = (next(it) for _ in range(5))
        if last:
            low_ref, hat_ref, inv_ref = next(it), next(it), next(it)
        else:
            sum_ref = next(it)
        wbuf, obuf, att_all, diagonal, acc, wsem, osem = (next(it) for _ in range(7))
        length, swap = sc[0], sc[1]

        def offset(unit):
            array, half = unit
            if not halved[array]:
                return 0
            return pl.multiple_of((half ^ swap) * UNIT, UNIT)

        def w_copies():
            groups, column = [], 0
            for group in w_refs:
                stacked = len(group[0].shape) == 3
                for c in range(group[0].shape[0] if stacked else 1):
                    copies = []
                    for index, unit in enumerate(plan):
                        at = pl.ds(offset(unit), UNIT)
                        ref = group[unit[0]]
                        lanes = slice((column * number + index) * UNIT, (column * number + index + 1) * UNIT)
                        copies.append(copy_of(ref.at[c, :, at] if stacked else ref.at[:, at], wbuf.at[:, lanes], wsem.at[column, index]))
                    groups.append(copies)
                    column += 1
            return groups

        groups = w_copies()
        o_copies = [
            copy_of(o_refs[unit[0]].at[pl.ds(offset(unit), UNIT), :], obuf.at[index * UNIT : (index + 1) * UNIT, :], osem.at[index])
            for index, unit in enumerate(plan)
        ]
        for copies in groups:
            for copy in copies:
                copy.start()
        for copy in o_copies:
            copy.start()
        if causal:
            fill_diagonal(diagonal)
        for c, target in enumerate((q_ref, k_ref, v_ref)):
            for copy in groups[c]:
                copy.wait()
            rows_in = in_refs[0] if causal or c == 0 else in_refs[1]
            proj = dot(rows_in[...], wbuf[:, c * number * UNIT : (c + 1) * number * UNIT]).astype(BF16)
            if c == 0:
                proj = (proj.astype(F32) * SCORE_SCALE).astype(BF16)
            for index in range(number):
                target[index] = proj[:, index * UNIT : (index + 1) * UNIT]

        def step(u, carry):
            attended = attend_unit(q_ref[u], k_ref[u], v_ref[u], length, causal, diagonal, lse_ref.at[u])
            att_ref[u] = attended
            att_all[:, pl.ds(pl.multiple_of(u * UNIT, UNIT), UNIT)] = attended
            return carry

        lax.fori_loop(0, number, step, 0)
        for copy in o_copies:
            copy.wait()
        target = acc if last else sum_ref
        if has_partial:
            target[...] = part_ref[...] + dot(att_all[...], obuf[...])
        else:
            target[...] = dot(att_all[...], obuf[...])
        if last:
            def chunk(at):
                if len(res_refs) == 1:
                    old = res_refs[0][at, :].astype(F32)
                else:
                    old = res_refs[0][at, :] * res_refs[1][...] + res_refs[2][...]
                normed, hat, inverse = norm_chunk(RESIDUAL_ALPHA * old + acc[at, :], gain_ref[...], bias_ref[...])
                low_ref[at, :] = normed.astype(BF16)
                hat_ref[at, :] = hat
                inv_ref[at, :] = jnp.broadcast_to(inverse, (ROW_CHUNK, 128))

            each_chunk(rows, chunk)

    unit_rows = sds((number, rows, UNIT), BF16)
    shapes = [unit_rows] * 4 + [sds((number, 2, rows), F32)]
    if last:
        shapes += [sds((rows, depth), BF16), sds((rows, depth), F32), sds((rows, 128), F32)]
    else:
        shapes += [sds((rows, depth), F32)]
    args = [scalars, *others] + (list(residual) if last else [])
    specs = [SMEM] + [VMEM] * (len(args) - 1)
    for group in flat_w:
        args += group
        specs += [ANY] * len(group)
    args += outs
    specs += [ANY] * n_o
    if has_partial:
        args.append(partial)
        specs.append(VMEM)
    if last:
        args += [gain, bias]
        specs += [VMEM, VMEM]
    return pl.pallas_call(
        kernel,
        out_shape=shapes,
        in_specs=specs,
        out_specs=[VMEM] * len(shapes),
        scratch_shapes=[
            pltpu.VMEM((depth, 3 * number * UNIT), BF16),
            pltpu.VMEM((number * UNIT, depth), BF16),
            pltpu.VMEM((rows, number * UNIT), BF16),
            pltpu.VMEM((QUERY_BLOCK, QUERY_BLOCK), F32),
            pltpu.VMEM((rows, depth) if last else (8, 128), F32),
            pltpu.SemaphoreType.DMA((3, number)),
            pltpu.SemaphoreType.DMA((number,)),
        ],
        compiler_params=params(),
        cost_estimate=cost_of(number * 2.2),
        name="self_fwd" if causal else "cross_fwd",
    )(*args)


def attention_bwd_call(scalars, grad_low, others, weights, outs, saved, plan, halved, carried, norm):
    rows, depth = grad_low.shape
    causal = len(others) == 1
    number, n_in = len(plan), len(others)
    last = norm is not None

    def kernel(*refs):
        it = iter(refs)
        sc = next(it)
        h_ref = next(it)
        in_refs = [next(it) for _ in range(n_in)]
        acc_in = [next(it) for _ in carried]
        gain_ref = next(it) if last else None
        late_in = [next(it), next(it)] if last else []
        w_refs = [[next(it) for _ in group] for group in weights]
        o_refs = [next(it) for _ in outs]
        s_refs = [[next(it) for _ in call] for call in saved]
        sums = [next(it) for _ in range(n_in)] if not last else [None] + [next(it) for _ in range(n_in - 1)]
        if last:
            low_ref, scaled_ref, gsum_ref, bsum_ref = (next(it) for _ in range(4))
        g_ref = next(it)
        wbuf, obuf, sbuf, lbuf, att_all, grad_all, h_t = (next(it) for _ in range(7))
        in_t = [next(it) for _ in range(n_in)]
        dall, stage, diagonal = next(it), next(it), next(it)
        if last:
            acc, hat, inv = next(it), next(it), next(it)
            lsem = next(it)
        wsem, ssem, gsem = next(it), next(it), next(it)
        length, swap, dp = sc[0], sc[1], sc[2]
        if last:
            sums[0] = acc
        wide = number * UNIT

        def offset(unit):
            if not halved[unit[0]]:
                return 0
            return pl.multiple_of((unit[1] ^ swap) * UNIT, UNIT)

        o_copies, s_copies, w_copies = [], [], []
        for index, unit in enumerate(plan):
            at = pl.ds(offset(unit), UNIT)
            lanes = slice(index * UNIT, (index + 1) * UNIT)
            o_copies.append(copy_of(o_refs[unit[0]].at[at, :], obuf.at[lanes, :], wsem.at[3, index]))
            call = s_refs[unit[2]]
            for c in range(3):
                s_copies.append(copy_of(call[c].at[unit[3]], sbuf.at[index, c], ssem.at[c, index]))
            s_copies.append(copy_of(call[3].at[unit[3]], att_all.at[:, lanes], ssem.at[3, index]))
            s_copies.append(copy_of(call[4].at[unit[3]], lbuf.at[index], ssem.at[4, index]))
            column = 0
            for group in w_refs:
                ref = group[unit[0]]
                for source in [ref.at[:, at]] if len(ref.shape) == 2 else [ref.at[c, :, at] for c in range(ref.shape[0])]:
                    low = (column * number + index) * UNIT
                    w_copies.append(copy_of(source, wbuf.at[:, low : low + UNIT], wsem.at[column, index]))
                    column += 1
        for copy in o_copies + s_copies + w_copies:
            copy.start()
        if last:
            late = [copy_of(late_in[0], hat, lsem.at[0]), copy_of(late_in[1], inv, lsem.at[1])]
            for copy in late:
                copy.start()
        if causal:
            fill_diagonal(diagonal)
        transpose_shards(h_ref, h_t, dp)
        for ref, target in zip(in_refs, in_t):
            transpose_shards(ref, target, dp)
        for copy in o_copies:
            copy.wait()
        grad_att = dot_nt(h_ref[...], obuf[...]).astype(BF16)
        for index in range(number):
            grad_all[index] = grad_att[:, index * UNIT : (index + 1) * UNIT]
        for copy in s_copies:
            copy.wait()

        def step(u, carry):
            at = pl.ds(pl.multiple_of(u * UNIT, UNIT), UNIT)
            parts = attend_back_unit(
                sbuf[u, 0], sbuf[u, 1], sbuf[u, 2], att_all[:, at], grad_all[u], length, causal, diagonal, lbuf.at[u]
            )
            for c in range(3):
                dall[:, pl.ds(pl.multiple_of(c * wide + u * UNIT, UNIT), UNIT)] = parts[c]
            return carry

        lax.fori_loop(0, number, step, 0)

        def keep(weight, column):
            for index in range(number):
                part = weight[:, index * UNIT : (index + 1) * UNIT].astype(BF16)
                stage[index, :, :, column * UNIT : (column + 1) * UNIT] = part.reshape(8, UNIT, UNIT)

        for c in range(3):
            rows_t = in_t[0] if causal or c == 0 else in_t[1]
            keep(dot(rows_t[...], dall[:, c * wide : (c + 1) * wide]), c)
        keep(dot(h_t[...], att_all[...]), 3)
        g_copies = [
            copy_of(stage.at[index], g_ref.at[natural_index(index, 2, 2, swap)], gsem.at[index]) for index in range(number)
        ]
        for copy in g_copies:
            copy.start()
        for copy in w_copies:
            copy.wait()
        if causal:
            sums[0][...] = acc_in[0][...] + dot_nt(dall[...], wbuf[...])
        else:
            sums[0][...] = acc_in[0][...] + dot_nt(dall[:, :wide], wbuf[:, :wide])
            memory_sum = dot_nt(dall[:, wide:], wbuf[:, wide:])
            sums[1][...] = memory_sum + acc_in[1][...] if n_in == len(acc_in) else memory_sum
        if last:
            for copy in late:
                copy.wait()
            norm_back_rows(acc, hat, inv, gain_ref, low_ref, scaled_ref, gsum_ref, bsum_ref, rows)
        for copy in g_copies:
            copy.wait()

    big = sds((rows, depth), F32)
    sum_shapes = [big] * (n_in - 1 if last else n_in)
    shapes = list(sum_shapes)
    if last:
        shapes += [sds((rows, depth), BF16), big, sds((8, depth), F32), sds((8, depth), F32)]
    specs_out = [VMEM] * len(shapes) + [ANY]
    shapes.append(sds((number, 8, UNIT, 4 * UNIT), BF16))
    args = [scalars, grad_low, *others, *carried]
    if last:
        args.append(norm[2])
    specs = [SMEM] + [VMEM] * (len(args) - 1)
    tail = []
    if last:
        tail += [norm[0], norm[1]]
    for group in weights:
        tail += group
    tail += outs
    for call in saved:
        tail += call
    scratch = [
        pltpu.VMEM((depth, 3 * number * UNIT), BF16),
        pltpu.VMEM((number * UNIT, depth), BF16),
        pltpu.VMEM((number, 3, rows, UNIT), BF16),
        pltpu.VMEM((number, 2, rows), F32),
        pltpu.VMEM((rows, number * UNIT), BF16),
        pltpu.VMEM((number, rows, UNIT), BF16),
        pltpu.VMEM((depth, rows), BF16),
    ]
    scratch += [pltpu.VMEM((depth, rows), BF16)] * n_in
    scratch += [
        pltpu.VMEM((rows, 3 * number * UNIT), BF16),
        pltpu.VMEM((number, 8, UNIT, 4 * UNIT), BF16),
        pltpu.VMEM((QUERY_BLOCK, QUERY_BLOCK), F32),
    ]
    if last:
        scratch += [
            pltpu.VMEM((rows, depth), F32),
            pltpu.VMEM((rows, depth), F32),
            pltpu.VMEM((rows, 128), F32),
            pltpu.SemaphoreType.DMA((2,)),
        ]
    scratch += [
        pltpu.SemaphoreType.DMA((4, number)),
        pltpu.SemaphoreType.DMA((5, number)),
        pltpu.SemaphoreType.DMA((number,)),
    ]
    return pl.pallas_call(
        kernel,
        out_shape=shapes,
        in_specs=specs + [ANY] * len(tail),
        out_specs=specs_out,
        scratch_shapes=scratch,
        compiler_params=params(),
        cost_estimate=cost_of(number * 3.5),
        name="self_bwd" if causal else "cross_bwd",
    )(*args, *tail)


def norm_back_rows(acc, hat, inv, gain_ref, low_ref, scaled_ref, gsum_ref, bsum_ref, rows):
    gsum_ref[...] = jnp.zeros_like(gsum_ref)
    bsum_ref[...] = jnp.zeros_like(bsum_ref)

    def chunk(at):
        gradient, normed = acc[at, :], hat[at, :]
        grad_in = norm_back_chunk(gradient, normed, inv[at, :1], gain_ref[...])
        low_ref[at, :] = grad_in.astype(BF16)
        scaled_ref[at, :] = RESIDUAL_ALPHA * grad_in
        gsum_ref[...] += fold_rows(gradient * normed)
        bsum_ref[...] += fold_rows(gradient)

    each_chunk(rows, chunk)


GELU_SCALE = 0.7978845608028654
GELU_CUBE = 0.044715


def gelu_and_slope(pre):
    square = pre * pre
    inner = pre * (GELU_SCALE + (GELU_SCALE * GELU_CUBE) * square)
    curve = jnp.tanh(inner)
    half = 0.5 + 0.5 * curve
    slope = half * (1.0 + pre * (1.0 - curve) * (GELU_SCALE + (3.0 * GELU_SCALE * GELU_CUBE) * square))
    return pre * half, slope


def ffn_fwd_call(scalars, inputs, ups, downs, plan, halved, partial, final):
    rows, depth = inputs.shape
    number = len(plan)
    last, has_partial = final is not None, partial is not None

    def kernel(*refs):
        it = iter(refs)
        sc, x_ref = next(it), next(it)
        if last:
            gain_old, bias_old, gain_ref, bias_ref = (next(it) for _ in range(4))
            late_in = [next(it), next(it)]
        part_in = next(it) if has_partial else None
        up_refs = [next(it) for _ in ups]
        down_refs = [next(it) for _ in downs]
        if last:
            out_ref, low_ref, scaled_ref, gsum_ref, bsum_ref = (next(it) for _ in range(5))
        else:
            sum_ref = next(it)
        act_ref, slope_ref = next(it), next(it)
        ubuf, dbuf, abuf, sbuf, pbuf, psem = (next(it) for _ in range(6))
        if last:
            acc, hat, cot, lsem = (next(it) for _ in range(4))
        wsem, gsem = next(it), next(it)
        swap = sc[1]
        target = acc if last else sum_ref

        up_copies, down_copies = [], []
        for index, unit in enumerate(plan):
            low = pl.multiple_of((unit[1] ^ swap) * FFN_UNIT, FFN_UNIT) if halved[unit[0]] else 0
            at = pl.ds(low, FFN_UNIT)
            up_copies.append(copy_of(up_refs[unit[0]].at[:, at], ubuf.at[index], wsem.at[0, index]))
            down_copies.append(
                copy_of(down_refs[unit[0]].at[at, :], dbuf.at[index * FFN_UNIT : (index + 1) * FFN_UNIT, :], wsem.at[1, index])
            )
        for copy in up_copies + down_copies:
            copy.start()
        if has_partial:
            part_copy = copy_of(part_in, target, psem)
            part_copy.start()
        if last:
            late = [copy_of(late_in[0], hat, lsem.at[0]), copy_of(late_in[1], cot, lsem.at[1])]
            for copy in late:
                copy.start()
        saves = []

        def gate(pre, index):
            activated, slope = gelu_and_slope(pre)
            abuf[:, index * FFN_UNIT : (index + 1) * FFN_UNIT] = activated.astype(BF16)
            sbuf[:, index * FFN_UNIT : (index + 1) * FFN_UNIT] = slope.astype(BF16)

        for index in range(number):
            up_copies[index].wait()
            if index:
                gate(pbuf[(index - 1) % 2], index - 1)
            pbuf[index % 2] = dot(x_ref[...], ubuf[index])
        gate(pbuf[(number - 1) % 2], number - 1)
        for index in range(number):
            at = slice(index * FFN_UNIT, (index + 1) * FFN_UNIT)
            saves += [
                copy_of(abuf.at[:, at], act_ref.at[index], gsem.at[0, index]),
                copy_of(sbuf.at[:, at], slope_ref.at[index], gsem.at[1, index]),
            ]
        for copy in saves:
            copy.start()
        for copy in down_copies:
            copy.wait()
        if has_partial:
            part_copy.wait()
            target[...] += dot(abuf[...], dbuf[...])
        else:
            target[...] = dot(abuf[...], dbuf[...])
        if last:
            for copy in late:
                copy.wait()
            gsum_ref[...] = jnp.zeros_like(gsum_ref)
            bsum_ref[...] = jnp.zeros_like(bsum_ref)

            def chunk(at):
                old = hat[at, :] * gain_old[...] + bias_old[...]
                normed, xhat, inverse = norm_chunk(RESIDUAL_ALPHA * old + acc[at, :], gain_ref[...], bias_ref[...])
                out_ref[at, :] = normed.astype(BF16)
                gradient = cot[at, :].astype(F32)
                grad_in = norm_back_chunk(gradient, xhat, inverse, gain_ref[...])
                low_ref[at, :] = grad_in.astype(BF16)
                scaled_ref[at, :] = RESIDUAL_ALPHA * grad_in
                gsum_ref[...] += fold_rows(gradient * xhat)
                bsum_ref[...] += fold_rows(gradient)

            each_chunk(rows, chunk)
        for copy in saves:
            copy.wait()

    big, low = sds((rows, depth), F32), sds((rows, depth), BF16)
    if last:
        shapes = [low, low, big, sds((8, depth), F32), sds((8, depth), F32)]
    else:
        shapes = [big]
    specs_out = [VMEM] * len(shapes) + [ANY, ANY]
    shapes += [sds((number, rows, FFN_UNIT), BF16)] * 2
    args = [scalars, inputs]
    if last:
        args += [final[1], final[2], final[4], final[5]]
    specs = [SMEM] + [VMEM] * (len(args) - 1)
    tail = ([final[0], final[3]] if last else []) + ([partial] if has_partial else []) + list(ups) + list(downs)
    scratch = [
        pltpu.VMEM((number, depth, FFN_UNIT), BF16),
        pltpu.VMEM((number * FFN_UNIT, depth), BF16),
        pltpu.VMEM((rows, number * FFN_UNIT), BF16),
        pltpu.VMEM((rows, number * FFN_UNIT), BF16),
        pltpu.VMEM((2, rows, FFN_UNIT), F32),
        pltpu.SemaphoreType.DMA,
    ]
    if last:
        scratch += [
            pltpu.VMEM((rows, depth), F32),
            pltpu.VMEM((rows, depth), F32),
            pltpu.VMEM((rows, depth), BF16),
            pltpu.SemaphoreType.DMA((2,)),
        ]
    scratch += [pltpu.SemaphoreType.DMA((2, number)), pltpu.SemaphoreType.DMA((2, number))]
    return pl.pallas_call(
        kernel,
        out_shape=shapes,
        in_specs=specs + [ANY] * len(tail),
        out_specs=specs_out,
        scratch_shapes=scratch,
        compiler_params=params(),
        cost_estimate=cost_of(number * 2.2),
        name="ffn_fwd",
    )(*args, *tail)


def ffn_bwd_call(scalars, grad_low, inputs, ups, downs, saved, plan, halved, carried, norm):
    rows, depth = inputs.shape
    number = len(plan)
    last = norm is not None

    def kernel(*refs):
        it = iter(refs)
        sc, g_in, x_ref = (next(it) for _ in range(3))
        gain_ref = next(it) if last else None
        late_in = [next(it), next(it)] if last else []
        acc_in = next(it)
        up_refs = [next(it) for _ in ups]
        down_refs = [next(it) for _ in downs]
        s_refs = [[next(it) for _ in call] for call in saved]
        if last:
            low_ref, scaled_ref, gsum_ref, bsum_ref = (next(it) for _ in range(4))
        else:
            sum_ref = next(it)
        g_ref = next(it)
        ubuf, dbuf, abuf, sbuf, gbuf, x_t, g_t, stage, psem = (next(it) for _ in range(9))
        if last:
            acc, hat, inv, lsem = (next(it) for _ in range(4))
        wsem, gsem = next(it), next(it)
        swap, dp = sc[1], sc[2]
        target = acc if last else sum_ref

        copies = [[], [], [], []]
        for index, unit in enumerate(plan):
            low = pl.multiple_of((unit[1] ^ swap) * FFN_UNIT, FFN_UNIT) if halved[unit[0]] else 0
            at, lanes = pl.ds(low, FFN_UNIT), slice(index * FFN_UNIT, (index + 1) * FFN_UNIT)
            call = s_refs[unit[2]]
            copies[0].append(copy_of(down_refs[unit[0]].at[at, :], dbuf.at[lanes, :], wsem.at[0, index]))
            copies[1].append(copy_of(call[1].at[unit[3]], sbuf.at[index], wsem.at[1, index]))
            copies[2].append(copy_of(call[0].at[unit[3]], abuf.at[:, lanes], wsem.at[2, index]))
            copies[3].append(copy_of(up_refs[unit[0]].at[:, at], ubuf.at[:, lanes], wsem.at[3, index]))
        for group in copies:
            for copy in group:
                copy.start()
        part_copy = copy_of(acc_in, target, psem)
        part_copy.start()
        if last:
            late = [copy_of(late_in[0], hat, lsem.at[0]), copy_of(late_in[1], inv, lsem.at[1])]
            for copy in late:
                copy.start()
        transpose_shards(g_in, g_t, dp)
        transpose_shards(x_ref, x_t, dp)
        for index in range(number):
            copies[0][index].wait()
            copies[1][index].wait()
            grad_act = dot_nt(g_in[...], dbuf[index * FFN_UNIT : (index + 1) * FFN_UNIT, :]) * sbuf[index].astype(F32)
            gbuf[:, index * FFN_UNIT : (index + 1) * FFN_UNIT] = grad_act.astype(BF16)
        for copy in copies[2]:
            copy.wait()

        def keep(rows_t, source, column):
            for half in range(number // 2):
                wide = 2 * FFN_UNIT
                weight = dot(rows_t[...], source[:, half * wide : (half + 1) * wide]).astype(BF16)
                for inner in (0, 1):
                    part = weight[:, inner * FFN_UNIT : (inner + 1) * FFN_UNIT]
                    stage[2 * half + inner, :, :, column * FFN_UNIT : (column + 1) * FFN_UNIT] = part.reshape(8, UNIT, FFN_UNIT)

        keep(x_t, gbuf, 0)
        keep(g_t, abuf, 1)
        g_copies = [
            copy_of(stage.at[index], g_ref.at[natural_index(index, 2, 2, swap)], gsem.at[index]) for index in range(number)
        ]
        for copy in g_copies:
            copy.start()
        for copy in copies[3]:
            copy.wait()
        part_copy.wait()
        target[...] += dot_nt(gbuf[...], ubuf[...])
        if last:
            for copy in late:
                copy.wait()
            norm_back_rows(acc, hat, inv, gain_ref, low_ref, scaled_ref, gsum_ref, bsum_ref, rows)
        for copy in g_copies:
            copy.wait()

    big, low = sds((rows, depth), F32), sds((rows, depth), BF16)
    shapes = [low, big, sds((8, depth), F32), sds((8, depth), F32)] if last else [big]
    specs_out = [VMEM] * len(shapes) + [ANY]
    shapes.append(sds((number, 8, UNIT, 2 * FFN_UNIT), BF16))
    args = [scalars, grad_low, inputs] + ([norm[2]] if last else [])
    specs = [SMEM] + [VMEM] * (len(args) - 1)
    tail = ([norm[0], norm[1]] if last else []) + [carried] + list(ups) + list(downs)
    for call in saved:
        tail += call
    scratch = [
        pltpu.VMEM((depth, number * FFN_UNIT), BF16),
        pltpu.VMEM((number * FFN_UNIT, depth), BF16),
        pltpu.VMEM((rows, number * FFN_UNIT), BF16),
        pltpu.VMEM((number, rows, FFN_UNIT), BF16),
        pltpu.VMEM((rows, number * FFN_UNIT), BF16),
        pltpu.VMEM((depth, rows), BF16),
        pltpu.VMEM((depth, rows), BF16),
        pltpu.VMEM((number, 8, UNIT, 2 * FFN_UNIT), BF16),
        pltpu.SemaphoreType.DMA,
    ]
    if last:
        scratch += [
            pltpu.VMEM((rows, depth), F32),
            pltpu.VMEM((rows, depth), F32),
            pltpu.VMEM((rows, 128), F32),
            pltpu.SemaphoreType.DMA((2,)),
        ]
    scratch += [pltpu.SemaphoreType.DMA((4, number)), pltpu.SemaphoreType.DMA((number,))]
    return pl.pallas_call(
        kernel,
        out_shape=shapes,
        in_specs=specs + [ANY] * len(tail),
        out_specs=specs_out,
        scratch_shapes=scratch,
        compiler_params=params(),
        cost_estimate=cost_of(number * 3.6),
        name="ffn_bwd",
    )(*args, *tail)


def swap_pairs(count, mask):
    return [(i, i ^ mask) for i in range(count)]


def to_sibling(values):
    return lax.ppermute(values, "tensor", swap_pairs(4, 1))


def over_y(values):
    return lax.ppermute(values, "tensor", swap_pairs(4, 2))


def over_dp(values, mask):
    return lax.ppermute(values, "dp", swap_pairs(8, mask))


def over_x(values):
    return over_dp(values, 1)


def over_z_near(values):
    return over_dp(values, 2)


def over_z_far(values):
    return over_dp(values, 4)


def after(values, *earlier):
    return lax.optimization_barrier((values, *earlier))[0]


def add(*terms):
    total = terms[0].astype(F32)
    for term in terms[1:]:
        total = total + term.astype(F32)
    return total.astype(BF16)


class Reduction:
    def __init__(self, sent):
        self.sent = sent

    def first(self, kept):
        other = to_sibling(self.sent)
        units = kept.shape[0] // 2
        half = units // 2
        pair_kept = kept.reshape(2, units, *kept.shape[1:])[:, half:]
        pair_other = other.reshape(2, units, *other.shape[1:])[:, half:]
        self.left = (kept[:half], other[:half])
        self.right = (pair_kept[:, :, :4], pair_other[:, :, :4])
        self.sends = (
            add(kept[units : units + half], other[units : units + half]),
            add(pair_kept[:, :, 4:], pair_other[:, :, 4:]),
        )
        return self.sends

    def second(self):
        over = over_y(self.sends[0])
        cross = over_x(self.sends[1])
        left, right = self.left, self.right
        self.sends = (
            add(left[0][:, 4:], left[1][:, 4:], over[:, 4:]),
            add(right[0][1], right[1][1], cross[1]),
        )
        self.left = (left[0][:, :4], left[1][:, :4], over[:, :4])
        self.right = (right[0][0], right[1][0], cross[0])
        return self.sends

    def third(self):
        left, right = over_x(self.sends[0]), over_y(self.sends[1])
        self.low = jnp.concatenate([add(*self.left, left), add(*self.right, right)], axis=0)
        self.sends = self.low[:, 2:]
        return self.sends

    def fourth(self):
        low = add(self.low[:, :2], over_z_near(self.sends))
        self.low, self.sends = low[:, 0], low[:, 1]
        return self.sends

    def last(self):
        return add(self.low, over_z_far(self.sends)).astype(F32)


def sentence_body(
    tokens,
    memory,
    dec_lengths,
    mem_lengths,
    self_qkv,
    self_out,
    cross_q,
    cross_kv,
    cross_out,
    ffn_in,
    ffn_out,
    norm_gains,
    norm_biases,
    cotangent,
):
    dp = lax.axis_index("dp")
    mine = lax.axis_index("tensor")
    swap = dp & 1
    self_scalars = jnp.stack([dec_lengths[0, mine], swap, dp, mine]).astype(jnp.int32)
    cross_scalars = jnp.stack([mem_lengths[0, mine], swap, dp, mine]).astype(jnp.int32)
    gains = [norm_gains[i : i + 1] for i in range(3)]
    biases = [norm_biases[i : i + 1] for i in range(3)]

    def own_half(values, axis):
        half = values.shape[axis] // 2
        return lax.dynamic_slice_in_dim(values, swap * half, half, axis)

    def fetch(values, axis, *earlier):
        send = own_half(values, axis)
        if earlier:
            send = after(send, *earlier)
        near = over_y(send)
        far = over_dp(near, 1)
        return [values, to_sibling(values), near, far, to_sibling(near), to_sibling(far)]

    halves = [True, True]
    early = [(0, 0), (0, 1), (1, 0), (1, 1)]
    pair = [(0, 0), (1, 0)]

    qkv_sib, out_sib = to_sibling(self_qkv), to_sibling(self_out)
    qkv_near = over_y(own_half(self_qkv, 2))
    out_near = over_y(own_half(self_out, 0))
    self_a = attention_fwd_call(
        self_scalars, [], [tokens], [[self_qkv, qkv_sib]], [self_out, out_sib], early, halves, None, None, None
    )
    cq_near = over_y(after(own_half(cross_q, 1), out_near))
    ckv_near = over_y(after(own_half(cross_kv, 2), out_near))
    cout_near = over_y(after(own_half(cross_out, 0), out_near))
    qkv_gone, out_gone = after(qkv_near, self_a[5]), after(out_near, self_a[5])
    qkv_far, qkv_near3 = over_x(qkv_gone), to_sibling(qkv_gone)
    out_far, out_near3 = over_x(out_gone), to_sibling(out_gone)
    self_b = attention_fwd_call(
        self_scalars, [], [tokens], [[qkv_near, qkv_near3]], [out_near, out_near3], pair, [False] * 2,
        self_a[5], None, None,
    )
    qkv_far3, out_far3 = to_sibling(qkv_far), to_sibling(out_far)
    self_c = attention_fwd_call(
        self_scalars, [tokens], [tokens], [[qkv_far, qkv_far3]], [out_far, out_far3], pair, [False] * 2,
        self_b[5], gains[0], biases[0],
    )
    first_low, first_hat, first_inv = self_c[5:]
    w_qkv = [self_qkv, qkv_sib, qkv_near, qkv_far, qkv_near3, qkv_far3]
    w_self = [self_out, out_sib, out_near, out_far, out_near3, out_far3]

    cq_sib, ckv_sib, cout_sib = (
        to_sibling(after(w, out_near)) for w in (cross_q, cross_kv, cross_out)
    )
    cq_far, ckv_far, cout_far = (over_x(w) for w in (cq_near, ckv_near, cout_near))
    cq_near3, ckv_near3, cout_near3 = (to_sibling(w) for w in (cq_near, ckv_near, cout_near))
    cross_in = [first_low, memory]
    cross_a = attention_fwd_call(
        cross_scalars, [], cross_in, [[cross_q, cq_sib], [cross_kv, ckv_sib]], [cross_out, cout_sib], early,
        halves, None, None, None,
    )
    in_near = over_y(after(own_half(ffn_in, 1), cout_near))
    down_near = over_y(after(own_half(ffn_out, 0), cout_near))
    cross_b = attention_fwd_call(
        cross_scalars, [], cross_in, [[cq_near, cq_near3], [ckv_near, ckv_near3]], [cout_near, cout_near3],
        pair, [False] * 2, cross_a[5], None, None,
    )
    cq_far3, ckv_far3, cout_far3 = (to_sibling(w) for w in (cq_far, ckv_far, cout_far))
    cross_c = attention_fwd_call(
        cross_scalars, [first_hat, gains[0], biases[0]], cross_in, [[cq_far, cq_far3], [ckv_far, ckv_far3]],
        [cout_far, cout_far3], pair, [False] * 2, cross_b[5], gains[1], biases[1],
    )
    second_low, second_hat, second_inv = cross_c[5:]
    w_cq = [cross_q, cq_sib, cq_near, cq_far, cq_near3, cq_far3]
    w_ckv = [cross_kv, ckv_sib, ckv_near, ckv_far, ckv_near3, ckv_far3]
    w_cross = [cross_out, cout_sib, cout_near, cout_far, cout_near3, cout_far3]

    in_sib, down_sib = to_sibling(after(ffn_in, cout_near)), to_sibling(after(ffn_out, cout_near))
    in_far, down_far = over_x(in_near), over_x(down_near)
    in_near3, down_near3 = to_sibling(in_near), to_sibling(down_near)
    in_far3, down_far3 = to_sibling(in_far), to_sibling(down_far)
    w_in = [ffn_in, in_sib, in_near, in_far, in_near3, in_far3]
    w_down = [ffn_out, down_sib, down_near, down_far, down_near3, down_far3]
    ffn_a = ffn_fwd_call(
        cross_scalars, second_low, w_in[:2], w_down[:2], early, halves, None, None
    )
    ffn_b = ffn_fwd_call(
        cross_scalars, second_low, w_in[2::2], w_down[2::2], pair, [False] * 2, ffn_a[0], None
    )
    ffn_c = ffn_fwd_call(
        cross_scalars, second_low, w_in[3::2], w_down[3::2], pair, [False] * 2, ffn_b[0],
        (second_hat, gains[1], biases[1], cotangent, gains[2], biases[2]),
    )
    out_rows, third_low, third_scaled, third_gain, third_bias = ffn_c[:5]

    def plan_of(pieces):
        units = []
        for piece in pieces:
            for half in (0, 1):
                if piece < 2:
                    units.append((piece, half, 0, 2 * piece + half))
                else:
                    units.append((2 * piece - 2 + half, 0, 1 + half, piece - 2))
        return units

    halved = [True, True, False, False, False, False]
    ffn_saved = [ffn_a[1:3], ffn_b[1:3], ffn_c[5:7]]
    ffn_d = ffn_bwd_call(
        cross_scalars, third_low, second_low, w_in, w_down, ffn_saved, plan_of((1, 3)), halved,
        third_scaled, None,
    )
    ffn_sum = Reduction(ffn_d[1])
    ffn_e = ffn_bwd_call(
        cross_scalars, third_low, second_low, w_in, w_down, ffn_saved, plan_of((0, 2)), halved,
        ffn_d[0], (second_hat, second_inv, gains[1]),
    )
    second_back, second_scaled, second_gain, second_bias = ffn_e[:4]
    second_back = after(second_back, *ffn_sum.first(ffn_e[4]))

    cross_saved = [cross_a[:5], cross_b[:5], cross_c[:5]]
    cross_d = attention_bwd_call(
        cross_scalars, second_back, cross_in, [w_cq, w_ckv], w_cross, cross_saved, plan_of((1, 3)), halved,
        [second_scaled], None,
    )
    cross_sum = Reduction(cross_d[2])
    cross_e = attention_bwd_call(
        cross_scalars, second_back, cross_in, [w_cq, w_ckv], w_cross, cross_saved, plan_of((0, 2)), halved,
        cross_d[:2], (first_hat, first_inv, gains[0]),
    )
    grad_memory, first_back, first_scaled, first_gain, first_bias = cross_e[:5]
    norm_sums = jnp.stack([first_gain, second_gain, third_gain, first_bias, second_bias, third_bias])
    norm_total = jnp.sum(norm_sums, axis=1)
    first_back = after(first_back, *ffn_sum.second(), *cross_sum.first(cross_e[5]), norm_total)

    self_saved = [self_a[:5], self_b[:5], self_c[:5]]
    self_d = attention_bwd_call(
        self_scalars, first_back, [tokens], [w_qkv], w_self, self_saved, plan_of((1, 3)), halved,
        [first_scaled], None,
    )
    self_sum = Reduction(self_d[1])
    norm_total = norm_total + to_sibling(norm_total)
    gate = after(self_d[0], ffn_sum.third(), norm_total)
    self_e = attention_bwd_call(
        self_scalars, first_back, [tokens], [w_qkv], w_self, self_saved, plan_of((0, 2)), halved,
        [gate], None,
    )
    grad_tokens = self_e[0]
    own_sends = self_sum.first(self_e[1])
    cross_sum.second()
    ffn_sum.fourth()
    norm_total = norm_total + over_y(norm_total)
    self_sum.second()
    cross_sum.third()
    ffn_sum = ffn_sum.last()
    norm_total = norm_total + over_x(norm_total)
    self_sum.third()
    cross_sum.fourth()
    norm_total = norm_total + over_z_near(norm_total)
    self_sum.fourth()
    cross_sum = cross_sum.last()
    norm_total = norm_total + over_z_far(norm_total)
    self_sum = self_sum.last()

    def matrices(total):
        return total.reshape(2, UNIT, 4, UNIT).transpose(2, 1, 0, 3).reshape(4, UNIT, 2 * UNIT)

    self_grads, cross_grads = matrices(self_sum), matrices(cross_sum)
    ffn_grads = ffn_sum.transpose(1, 0, 2)
    return (
        out_rows,
        grad_tokens,
        grad_memory,
        self_grads[:3],
        self_grads[3].T,
        cross_grads[0],
        cross_grads[1:3],
        cross_grads[3].T,
        ffn_grads[:, :, :FFN_UNIT].reshape(UNIT, -1),
        ffn_grads[:, :, FFN_UNIT:].reshape(UNIT, -1).T,
        norm_total[:3],
        norm_total[3:],
    )


def sentence_fits(mesh, tokens, memory, dec_lengths):
    shape = dict(mesh.shape)
    rows = tokens.shape[0] // mesh.size
    sentences = dec_lengths.shape[1]
    return (
        shape["tensor"] == 4
        and shape["dp"] == 8
        and sentences == 4
        and rows == 512
        and memory.shape[0] // mesh.size == rows
        and tokens.shape[1] == 1024
    )


def smooth_gate(values):
    return jax.nn.gelu(values, approximate=True)


def norm_rows(hidden, norm_gain, norm_bias):
    center = hidden - jnp.mean(hidden, axis=-1, keepdims=True)
    inverse = lax.rsqrt(jnp.mean(center * center, axis=-1, keepdims=True) + NORM_EPSILON)
    normed = center * inverse
    return (normed * norm_gain + norm_bias, normed, inverse)


def norm_back(gradient, normed, inverse, norm_gain):
    scaled = gradient * norm_gain
    grad_in = inverse * (
        scaled
        - jnp.mean(scaled, axis=-1, keepdims=True)
        - normed * jnp.mean(scaled * normed, axis=-1, keepdims=True)
    )
    return (grad_in, jnp.sum(gradient * normed, axis=0), jnp.sum(gradient, axis=0))


def head_view(values, sentences):
    return values.reshape(sentences, -1, values.shape[1] // HEAD_DIM, HEAD_DIM)


def masked_scores(query_heads, key_heads, key_mask):
    scores = jnp.einsum(
        "sqhe,skhe->shqk", query_heads, key_heads, preferred_element_type=jnp.float32
    ) * HEAD_DIM ** (-0.5)
    return jnp.where(key_mask, scores, MASKED_SCORE)


def attention_forward(query_rows, key_rows, value_rows, key_mask, sentences):
    scores = masked_scores(
        head_view(query_rows, sentences), head_view(key_rows, sentences), key_mask
    )
    row_peak = jnp.max(scores, axis=-1, keepdims=True)
    exponent_terms = jnp.exp(scores - row_peak)
    row_sum = jnp.sum(exponent_terms, axis=-1, keepdims=True)
    softmax_probs = exponent_terms / row_sum
    attended = jnp.einsum(
        "shqk,skhe->sqhe",
        softmax_probs.astype(jnp.bfloat16),
        head_view(value_rows, sentences),
        preferred_element_type=jnp.float32,
    ).astype(jnp.bfloat16)
    return (attended.reshape(query_rows.shape), row_peak + jnp.log(row_sum))


def attention_backward(query_rows, key_rows, value_rows, key_mask, log_total, grad_rows, sentences):
    query_heads = head_view(query_rows, sentences)
    key_heads = head_view(key_rows, sentences)
    value_heads = head_view(value_rows, sentences)
    grad_heads = head_view(grad_rows, sentences)
    softmax_probs = jnp.exp(masked_scores(query_heads, key_heads, key_mask) - log_total)
    grad_probs = jnp.einsum(
        "sqhe,skhe->shqk", grad_heads, value_heads, preferred_element_type=jnp.float32
    )
    row_delta = jnp.sum(softmax_probs * grad_probs, axis=-1, keepdims=True)
    grad_scores = (softmax_probs * (grad_probs - row_delta)).astype(jnp.bfloat16)
    score_scale = HEAD_DIM ** (-0.5)
    grad_query = (
        jnp.einsum("shqk,skhe->sqhe", grad_scores, key_heads, preferred_element_type=jnp.float32)
        * score_scale
    ).astype(jnp.bfloat16)
    grad_key = (
        jnp.einsum("shqk,sqhe->skhe", grad_scores, query_heads, preferred_element_type=jnp.float32)
        * score_scale
    ).astype(jnp.bfloat16)
    grad_value = jnp.einsum(
        "shqk,sqhe->skhe",
        softmax_probs.astype(jnp.bfloat16),
        grad_heads,
        preferred_element_type=jnp.float32,
    ).astype(jnp.bfloat16)
    return (
        grad_query.reshape(query_rows.shape),
        grad_key.reshape(key_rows.shape),
        grad_value.reshape(value_rows.shape),
    )


def body(
    tokens,
    memory,
    dec_lengths,
    mem_lengths,
    self_qkv,
    self_out,
    cross_q,
    cross_kv,
    cross_out,
    ffn_in,
    ffn_out,
    norm_gains,
    norm_biases,
    cotangent,
):
    row_share = tokens.shape[0]
    sentences = dec_lengths.shape[1]
    all_tokens, all_memory = (
        lax.all_gather(tokens, "tensor", axis=0, tiled=True),
        lax.all_gather(memory, "tensor", axis=0, tiled=True),
    )
    sentence_len = all_tokens.shape[0] // sentences
    memory_len = all_memory.shape[0] // sentences
    positions = jnp.arange(sentence_len, dtype=jnp.int32)
    self_mask = (
        (positions[None, :] <= positions[:, None])[None]
        & (positions[None, None, :] < dec_lengths[0][:, None, None])
    )[:, None]
    memory_positions = jnp.arange(memory_len, dtype=jnp.int32)
    cross_mask = (memory_positions[None, :] < mem_lengths[0][:, None])[:, None, None, :]

    def branch_rows(attended, weight):
        return lax.psum_scatter(
            jnp.dot(attended, weight, preferred_element_type=jnp.float32).astype(jnp.bfloat16),
            "tensor",
            scatter_dimension=0,
            tiled=True,
        ).astype(jnp.float32)

    def branch_grad(grad_rows, attended, weight):
        grad_low = grad_rows.astype(jnp.bfloat16)
        grad_all = lax.all_gather(grad_low, "tensor", axis=0, tiled=True)
        grad_attended = jnp.dot(grad_all, weight.T, preferred_element_type=jnp.float32).astype(
            jnp.bfloat16
        )
        weight_part = jnp.dot(attended.T, grad_all, preferred_element_type=jnp.float32)
        return (grad_attended, weight_part)

    def gather_normed(values):
        return lax.all_gather(values, "tensor", axis=0, tiled=True)

    def head_input_sum(term):
        return lax.psum_scatter(
            term(jnp.int32(0), row_share * lax.axis_size("tensor")).astype(jnp.bfloat16),
            "tensor",
            scatter_dimension=0,
            tiled=True,
        ).astype(jnp.float32)

    self_proj = jnp.einsum(
        "td,cde->cte", all_tokens, self_qkv, preferred_element_type=jnp.float32
    ).astype(jnp.bfloat16)
    self_att, self_lse = attention_forward(
        self_proj[0], self_proj[1], self_proj[2], self_mask, sentences
    )
    self_branch = branch_rows(self_att, self_out)
    first_norm, first_hat, first_inv = norm_rows(
        RESIDUAL_ALPHA * tokens.astype(jnp.float32) + self_branch, norm_gains[0], norm_biases[0]
    )
    first_all = gather_normed(first_norm.astype(jnp.bfloat16))
    cross_query = jnp.dot(first_all, cross_q, preferred_element_type=jnp.float32).astype(
        jnp.bfloat16
    )
    cross_proj = jnp.einsum(
        "td,cde->cte", all_memory, cross_kv, preferred_element_type=jnp.float32
    ).astype(jnp.bfloat16)
    cross_att, cross_lse = attention_forward(
        cross_query, cross_proj[0], cross_proj[1], cross_mask, sentences
    )
    cross_branch = branch_rows(cross_att, cross_out)
    second_norm, second_hat, second_inv = norm_rows(
        RESIDUAL_ALPHA * first_norm + cross_branch, norm_gains[1], norm_biases[1]
    )
    second_all = gather_normed(second_norm.astype(jnp.bfloat16))
    pre_gate = jnp.dot(second_all, ffn_in, preferred_element_type=jnp.float32)
    activated = smooth_gate(pre_gate).astype(jnp.bfloat16)
    ffn_branch = lax.psum_scatter(
        jnp.dot(activated, ffn_out, preferred_element_type=jnp.float32).astype(jnp.bfloat16),
        "tensor",
        scatter_dimension=0,
        tiled=True,
    ).astype(jnp.float32)
    out_rows, third_hat, third_inv = norm_rows(
        RESIDUAL_ALPHA * second_norm + ffn_branch, norm_gains[2], norm_biases[2]
    )
    grad_third, third_gain, third_bias = norm_back(
        cotangent.astype(jnp.float32), third_hat, third_inv, norm_gains[2]
    )
    grad_ffn_all = lax.all_gather(grad_third.astype(jnp.bfloat16), "tensor", axis=0, tiled=True)
    unused_gate, gate_pull = jax.vjp(smooth_gate, pre_gate)
    grad_act = gate_pull(jnp.dot(grad_ffn_all, ffn_out.T, preferred_element_type=jnp.float32))[
        0
    ].astype(jnp.bfloat16)
    grad_ffn_out = jnp.dot(activated.T, grad_ffn_all, preferred_element_type=jnp.float32)
    grad_ffn_in = jnp.dot(second_all.T, grad_act, preferred_element_type=jnp.float32)
    grad_second = RESIDUAL_ALPHA * grad_third + lax.psum_scatter(
        jnp.dot(grad_act, ffn_in.T, preferred_element_type=jnp.float32).astype(jnp.bfloat16),
        "tensor",
        scatter_dimension=0,
        tiled=True,
    ).astype(jnp.float32)
    grad_second_in, second_gain, second_bias = norm_back(
        grad_second, second_hat, second_inv, norm_gains[1]
    )
    grad_cross_att, cross_out_part = branch_grad(grad_second_in, cross_att, cross_out)
    grad_cq, grad_ck, grad_cv = attention_backward(
        cross_query, cross_proj[0], cross_proj[1], cross_mask, cross_lse, grad_cross_att, sentences
    )
    grad_cross_q = jnp.dot(first_all.T, grad_cq, preferred_element_type=jnp.float32)
    cross_grads = jnp.stack([grad_ck, grad_cv])
    grad_cross_kv = jnp.einsum(
        "td,cte->cde", all_memory, cross_grads, preferred_element_type=jnp.float32
    )
    grad_memory = lax.psum_scatter(
        jnp.einsum("cte,cde->td", cross_grads, cross_kv, preferred_element_type=jnp.float32).astype(
            jnp.bfloat16
        ),
        "tensor",
        scatter_dimension=0,
        tiled=True,
    ).astype(jnp.float32)

    def cross_input_term(first_row, row_total):
        return jnp.dot(grad_cq, cross_q.T, preferred_element_type=jnp.float32)

    cross_input = head_input_sum(cross_input_term)
    grad_first = RESIDUAL_ALPHA * grad_second_in + cross_input
    grad_first_in, first_gain, first_bias = norm_back(
        grad_first, first_hat, first_inv, norm_gains[0]
    )
    grad_self_att, self_out_part = branch_grad(grad_first_in, self_att, self_out)
    grad_sq, grad_sk, grad_sv = attention_backward(
        self_proj[0], self_proj[1], self_proj[2], self_mask, self_lse, grad_self_att, sentences
    )
    self_grads = jnp.stack([grad_sq, grad_sk, grad_sv])
    grad_self_qkv = jnp.einsum(
        "td,cte->cde", all_tokens, self_grads, preferred_element_type=jnp.float32
    )

    def self_input_term(first_row, row_total):
        return jnp.einsum("cte,cde->td", self_grads, self_qkv, preferred_element_type=jnp.float32)

    self_input = head_input_sum(self_input_term)
    grad_tokens = RESIDUAL_ALPHA * grad_first_in + self_input
    summed = (
        lax.psum_scatter(
            grad_self_qkv.astype(jnp.bfloat16), "dp", scatter_dimension=1, tiled=True
        ).astype(jnp.float32),
        lax.psum_scatter(
            self_out_part.astype(jnp.bfloat16), "dp", scatter_dimension=1, tiled=True
        ).astype(jnp.float32),
        lax.psum_scatter(
            grad_cross_q.astype(jnp.bfloat16), "dp", scatter_dimension=0, tiled=True
        ).astype(jnp.float32),
        lax.psum_scatter(
            grad_cross_kv.astype(jnp.bfloat16), "dp", scatter_dimension=1, tiled=True
        ).astype(jnp.float32),
        lax.psum_scatter(
            cross_out_part.astype(jnp.bfloat16), "dp", scatter_dimension=1, tiled=True
        ).astype(jnp.float32),
        lax.psum_scatter(
            grad_ffn_in.astype(jnp.bfloat16), "dp", scatter_dimension=0, tiled=True
        ).astype(jnp.float32),
        lax.psum_scatter(
            grad_ffn_out.astype(jnp.bfloat16), "dp", scatter_dimension=1, tiled=True
        ).astype(jnp.float32),
    )
    gain_total, bias_total = lax.psum(
        (
            jnp.stack([first_gain, second_gain, third_gain]),
            jnp.stack([first_bias, second_bias, third_bias]),
        ),
        ("dp", "tensor"),
    )
    return (
        out_rows.astype(jnp.bfloat16),
        grad_tokens,
        grad_memory,
        summed[0],
        summed[1],
        summed[2],
        summed[3],
        summed[4],
        summed[5],
        summed[6],
        gain_total,
        bias_total,
    )


def solution(mesh):
    in_specs = (
        P(("dp", "tensor"), None),
        P(("dp", "tensor"), None),
        P("dp", None),
        P("dp", None),
        P(None, None, "tensor"),
        P("tensor", None),
        P(None, "tensor"),
        P(None, None, "tensor"),
        P("tensor", None),
        P(None, "tensor"),
        P("tensor", None),
        P(),
        P(),
        P(("dp", "tensor"), None),
    )
    out_specs = (
        P(("dp", "tensor"), None),
        P(("dp", "tensor"), None),
        P(("dp", "tensor"), None),
        P(None, "dp", "tensor"),
        P("tensor", "dp"),
        P("dp", "tensor"),
        P(None, "dp", "tensor"),
        P("tensor", "dp"),
        P("dp", "tensor"),
        P("tensor", "dp"),
        P(),
        P(),
    )

    def step(*args):
        chosen = sentence_body if sentence_fits(mesh, args[0], args[1], args[2]) else body
        return jax.shard_map(
            chosen, mesh=mesh, in_specs=in_specs, out_specs=out_specs, check_vma=False
        )(*args)

    return step
```

```python
import functools
import jax
import jax.numpy as jnp
from jax import lax
from jax.experimental import pallas as pl
from jax.experimental.pallas import tpu as pltpu
from jax.sharding import PartitionSpec as P

HEAD_DIM = 64
RESIDUAL_ALPHA = 4.16
NORM_EPSILON = 1e-05
MASKED_SCORE = -1000000000.0
SCORE_SCALE = HEAD_DIM ** (-0.5)
UNIT = 128
QUERY_BLOCK = 256
FFN_UNIT = 512
ROW_CHUNK = 64
BF16 = jnp.bfloat16
F32 = jnp.float32


def dot(left, right):
    return lax.dot_general(left, right, (((1,), (0,)), ((), ())), preferred_element_type=F32)


def dot_nt(left, right):
    return lax.dot_general(left, right, (((1,), (1,)), ((), ())), preferred_element_type=F32)


def shard_of(position):
    return ((position >> 2) & 1) | (position & 2) | ((position & 1) << 2)


def copy_of(source, target, sem):
    return pltpu.make_async_copy(source, target, sem)


def own_lanes(rows, head):
    lanes = lax.broadcasted_iota(jnp.int32, rows.shape, 1)
    return jnp.where((lanes >= HEAD_DIM) if head else (lanes < HEAD_DIM), rows, 0.0)


def extended_keys(keys, length):
    lanes = lax.broadcasted_iota(jnp.int32, keys.shape, 1)
    rows = lax.broadcasted_iota(jnp.int32, keys.shape, 0)
    mask = jnp.where((lanes == 0) & (rows >= length), MASKED_SCORE, 0.0).astype(BF16)
    keys = keys.astype(F32)
    return [jnp.concatenate([own_lanes(keys, head).astype(BF16), mask], axis=1) for head in (0, 1)]


def extended_query(query):
    lanes = lax.broadcasted_iota(jnp.int32, query.shape, 1)
    return jnp.concatenate([query, jnp.where(lanes == 0, 1.0, 0.0).astype(BF16)], axis=1)


def fill_diagonal(diagonal):
    keys = lax.broadcasted_iota(jnp.int32, diagonal.shape, 0)
    queries = lax.broadcasted_iota(jnp.int32, diagonal.shape, 1)
    diagonal[...] = jnp.where(keys <= queries, 0.0, MASKED_SCORE)


def key_ranges(block, keys, causal):
    if not causal:
        return [(0, keys)]
    return [(low, low + QUERY_BLOCK) for low in range(0, (block + 1) * QUERY_BLOCK, QUERY_BLOCK)]


def attend_unit(query, keys, values, length, causal, diagonal, lse_ref):
    rows, count = query.shape[0], keys.shape[0]
    values_t = jnp.transpose(values.astype(F32)).astype(BF16)
    wide_keys, wide_query = extended_keys(keys, length), extended_query(query)
    items = [(head, block) for block in range(rows // QUERY_BLOCK) for head in (0, 1)]
    scores, probs, totals, mixed = {}, {}, {}, {}
    for head, block in items:
        part = wide_query[block * QUERY_BLOCK : (block + 1) * QUERY_BLOCK]
        ranges = key_ranges(block, count, causal)
        scores[head, block] = [dot_nt(wide_keys[head][a:b], part) for a, b in ranges]
        if causal:
            scores[head, block][-1] = scores[head, block][-1] + diagonal[...]
    for head, block in items:
        pieces = scores[head, block]
        peak = functools.reduce(jnp.maximum, [jnp.max(p, axis=0, keepdims=True) for p in pieces])
        terms = [jnp.exp(p - peak) for p in pieces]
        total = sum(jnp.sum(t, axis=0, keepdims=True) for t in terms)
        at = slice(block * QUERY_BLOCK, (block + 1) * QUERY_BLOCK)
        lse_ref[head : head + 1, at] = peak + jnp.log(total)
        totals[head, block] = total
        probs[head, block] = jnp.concatenate([t.astype(BF16) for t in terms], axis=0)
    for head, block in items:
        own = values_t[head * HEAD_DIM : (head + 1) * HEAD_DIM, : probs[head, block].shape[0]]
        mixed[head, block] = dot(own, probs[head, block]) / totals[head, block]
    out = [
        jnp.transpose(jnp.concatenate([mixed[0, block], mixed[1, block]], axis=0))
        for block in range(rows // QUERY_BLOCK)
    ]
    return jnp.concatenate(out, axis=0).astype(BF16)


def attend_back_unit(query, keys, values, attended, grad, length, causal, diagonal, lse_ref):
    rows, count = query.shape[0], keys.shape[0]
    blocks = range(rows // QUERY_BLOCK)
    query_f, keys_f, grad_f = (a.astype(F32) for a in (query, keys, grad))
    wide_keys, wide_query = extended_keys(keys, length), extended_query(query)
    delta = jnp.transpose(grad_f * attended.astype(F32))
    deltas = [
        jnp.sum(delta[head * HEAD_DIM : (head + 1) * HEAD_DIM], axis=0, keepdims=True)
        for head in (0, 1)
    ]
    keys_t = jnp.transpose(keys_f).astype(BF16)
    query_own = [own_lanes(query_f, head).astype(BF16) for head in (0, 1)]
    grad_own = [own_lanes(grad_f, head).astype(BF16) for head in (0, 1)]
    items = [(head, block) for block in blocks for head in (0, 1)]
    scores, slopes, probs, back, grad_query = {}, {}, {}, {}, {}
    for head, block in items:
        at = slice(block * QUERY_BLOCK, (block + 1) * QUERY_BLOCK)
        for a, b in key_ranges(block, count, causal):
            scores[head, block, a] = dot_nt(wide_keys[head][a:b], wide_query[at])
            slopes[head, block, a] = dot_nt(values[a:b], grad_own[head][at])
    for head, block in items:
        at = slice(block * QUERY_BLOCK, (block + 1) * QUERY_BLOCK)
        ranges = key_ranges(block, count, causal)
        for a, b in ranges:
            score = scores[head, block, a]
            if causal and (a, b) == ranges[-1]:
                score = score + diagonal[...]
            prob = jnp.exp(score - lse_ref[head : head + 1, at])
            probs[head, block, a] = prob.astype(BF16)
            back[head, block, a] = (prob * (slopes[head, block, a] - deltas[head][:, at])).astype(BF16)
    for head, block in items:
        own = keys_t[head * HEAD_DIM : (head + 1) * HEAD_DIM]
        grad_query[head, block] = sum(
            dot(own[:, a:b], back[head, block, a]) for a, b in key_ranges(block, count, causal)
        )
    grad_keys, grad_values = [], []
    for low in sorted({key[2] for key in back}):
        live = [key for key in back if key[2] == low]
        at = [slice(block * QUERY_BLOCK, (block + 1) * QUERY_BLOCK) for _, block, _ in live]
        grad_values.append(
            dot(
                jnp.concatenate([probs[key] for key in live], axis=1),
                jnp.concatenate([grad_own[key[0]][a] for key, a in zip(live, at)], axis=0),
            )
        )
        grad_keys.append(
            dot(
                jnp.concatenate([back[key] for key in live], axis=1),
                jnp.concatenate([query_own[key[0]][a] for key, a in zip(live, at)], axis=0),
            )
        )
    grad_query = [
        jnp.transpose(jnp.concatenate([grad_query[0, block], grad_query[1, block]], axis=0)) * SCORE_SCALE
        for block in blocks
    ]
    return tuple(
        jnp.concatenate(parts, axis=0).astype(BF16) for parts in (grad_query, grad_keys, grad_values)
    )


def norm_chunk(hidden, gain, bias):
    center = hidden - jnp.mean(hidden, axis=-1, keepdims=True)
    inverse = lax.rsqrt(jnp.mean(center * center, axis=-1, keepdims=True) + NORM_EPSILON)
    normed = center * inverse
    return normed * gain + bias, normed, inverse


def norm_back_chunk(gradient, normed, inverse, gain):
    scaled = gradient * gain
    return inverse * (
        scaled
        - jnp.mean(scaled, axis=-1, keepdims=True)
        - normed * jnp.mean(scaled * normed, axis=-1, keepdims=True)
    )


def fold_rows(values):
    return jnp.sum(values.reshape(values.shape[0] // 8, 8, values.shape[1]), axis=0)


def each_chunk(rows, body):
    def step(index, carry):
        body(pl.ds(pl.multiple_of(index * ROW_CHUNK, ROW_CHUNK), ROW_CHUNK))
        return carry

    lax.fori_loop(0, rows // ROW_CHUNK, step, 0)


def transpose_shards(source, target, dp):
    for position in range(8):
        block = dp ^ shard_of(position)
        columns = source[:, pl.ds(pl.multiple_of(block * UNIT, UNIT), UNIT)]
        target[position * UNIT : (position + 1) * UNIT, :] = jnp.transpose(
            columns.astype(F32)
        ).astype(BF16)


SMEM = pl.BlockSpec(memory_space=pltpu.SMEM)
VMEM = pl.BlockSpec(memory_space=pltpu.VMEM)
ANY = pl.BlockSpec(memory_space=pl.ANY)


def params(limit=56):
    return pltpu.CompilerParams(vmem_limit_bytes=limit * 1024 * 1024)


def cost_of(microseconds):
    return pl.CostEstimate(flops=int(microseconds * 1.1e9), bytes_accessed=4 << 20, transcendentals=0)


def sds(shape, dtype):
    return jax.ShapeDtypeStruct(shape, dtype)


def pack_copies(packs, plan, number, order, buffer, sems):
    groups = []
    for matrix in range(4):
        copies = []
        for index, (array, half, relative) in enumerate(plan):
            quarter = half + 2 * (matrix // 2)
            if relative:
                quarter = quarter ^ order
            low = (matrix * number + index) * UNIT
            copies.append(
                copy_of(packs[array].at[quarter, matrix % 2], buffer.at[:, low : low + UNIT], sems.at[matrix, index])
            )
        groups.append(copies)
    return groups


def attention_fwd_call(scalars, residual, others, packs, plan, partial, norm):
    rows, depth = others[0].shape
    causal = len(others) == 1
    number, wide = len(plan), len(plan) * UNIT
    last, has_partial = norm is not None, partial is not None

    def kernel(*refs):
        it = iter(refs)
        sc = next(it)
        in_refs = [next(it) for _ in others]
        gain_ref, bias_ref = (next(it), next(it)) if last else (None, None)
        old_rows = [next(it) for _ in residual[1:]] if last else []
        res_in = next(it) if last else None
        part_in = next(it) if has_partial else None
        w_refs = [next(it) for _ in packs]
        q_ref, k_ref, v_ref, att_ref, lse_ref = (next(it) for _ in range(5))
        if last:
            low_ref, hat_ref, inv_ref = next(it), next(it), next(it)
        else:
            sum_ref = next(it)
        wbuf, att_all, diagonal, wsem, lsem = (next(it) for _ in range(5))
        if last:
            acc, old = next(it), next(it)
        length, order = sc[0], sc[1]
        groups = pack_copies(w_refs, plan, number, order, wbuf, wsem)
        for copies in groups:
            for copy in copies:
                copy.start()
        target = acc if last else sum_ref
        late = []
        if has_partial:
            late.append(copy_of(part_in, target, lsem.at[0]))
        if last:
            late.append(copy_of(res_in, old, lsem.at[1]))
        for copy in late:
            copy.start()
        if causal:
            fill_diagonal(diagonal)
        for c, result in enumerate((q_ref, k_ref, v_ref)):
            for copy in groups[c]:
                copy.wait()
            rows_in = in_refs[0] if causal or c == 0 else in_refs[1]
            proj = dot(rows_in[...], wbuf[:, c * wide : (c + 1) * wide]).astype(BF16)
            if c == 0:
                proj = (proj.astype(F32) * SCORE_SCALE).astype(BF16)
            for index in range(number):
                result[index] = proj[:, index * UNIT : (index + 1) * UNIT]

        def step(u, carry):
            attended = attend_unit(q_ref[u], k_ref[u], v_ref[u], length, causal, diagonal, lse_ref.at[u])
            att_ref[u] = attended
            att_all[:, pl.ds(pl.multiple_of(u * UNIT, UNIT), UNIT)] = attended
            return carry

        lax.fori_loop(0, number, step, 0)
        for copy in groups[3] + late:
            copy.wait()
        if has_partial:
            target[...] += dot_nt(att_all[...], wbuf[:, 3 * wide :])
        else:
            target[...] = dot_nt(att_all[...], wbuf[:, 3 * wide :])
        if last:
            def chunk(at):
                before = old[at, :].astype(F32)
                if old_rows:
                    before = before * old_rows[0][...] + old_rows[1][...]
                normed, hat, inverse = norm_chunk(RESIDUAL_ALPHA * before + acc[at, :], gain_ref[...], bias_ref[...])
                low_ref[at, :] = normed.astype(BF16)
                hat_ref[at, :] = hat
                inv_ref[at, :] = jnp.broadcast_to(inverse, (ROW_CHUNK, 128))

            each_chunk(rows, chunk)

    unit_rows = sds((number, rows, UNIT), BF16)
    shapes = [unit_rows] * 4 + [sds((number, 2, rows), F32)]
    if last:
        shapes += [sds((rows, depth), BF16), sds((rows, depth), F32), sds((rows, 128), F32)]
    else:
        shapes += [sds((rows, depth), F32)]
    args = [scalars, *others]
    if last:
        args += [*norm, *residual[1:]]
    tail = ([residual[0]] if last else []) + ([partial] if has_partial else []) + list(packs)
    scratch = [
        pltpu.VMEM((depth, 4 * wide), BF16),
        pltpu.VMEM((rows, wide), BF16),
        pltpu.VMEM((QUERY_BLOCK, QUERY_BLOCK), F32),
        pltpu.SemaphoreType.DMA((4, number)),
        pltpu.SemaphoreType.DMA((2,)),
    ]
    if last:
        scratch += [pltpu.VMEM((rows, depth), F32), pltpu.VMEM((rows, depth), residual[0].dtype)]
    return pl.pallas_call(
        kernel,
        out_shape=shapes,
        in_specs=[SMEM] + [VMEM] * (len(args) - 1) + [ANY] * len(tail),
        out_specs=[VMEM] * len(shapes),
        scratch_shapes=scratch,
        compiler_params=params(),
        cost_estimate=cost_of(2.7 * number),
        name="self_fwd" if causal else "cross_fwd",
    )(*args, *tail)


def attention_bwd_call(scalars, grad_low, others, packs, saved, plan, carried, norm, results=1):
    rows, depth = grad_low.shape
    causal = len(others) == 1
    number, n_in, wide = len(plan), len(others), len(plan) * UNIT
    last = norm is not None

    def kernel(*refs):
        it = iter(refs)
        sc = next(it)
        h_ref = next(it)
        in_refs = [next(it) for _ in range(n_in)]
        gain_ref = next(it) if last else None
        late_in = [next(it), next(it)] if last else []
        acc_in = [next(it) for _ in carried]
        w_refs = [next(it) for _ in packs]
        s_refs = [[next(it) for _ in call] for call in saved]
        sums = [None if last and not index else next(it) for index in range(n_in)]
        if last:
            low_ref, scaled_ref, gsum_ref, bsum_ref = (next(it) for _ in range(4))
        g_refs = [next(it) for _ in range(results)]
        wbuf, sbuf, lbuf, att_all, grad_all, h_t = (next(it) for _ in range(6))
        in_t = [next(it) for _ in range(n_in)]
        dall, stage, diagonal = next(it), next(it), next(it)
        if last:
            acc, hat, inv = next(it), next(it), next(it)
            sums[0] = acc
        wsem, ssem, gsem, lsem = (next(it) for _ in range(4))
        length, order, dp = sc[0], sc[1], sc[2]

        groups = pack_copies(w_refs, [unit[:3] for unit in plan], number, order, wbuf, wsem)
        for copy in groups[3]:
            copy.start()
        s_copies = []
        for index, unit in enumerate(plan):
            lanes = slice(index * UNIT, (index + 1) * UNIT)
            call = s_refs[unit[3]]
            for c in range(3):
                s_copies.append(copy_of(call[c].at[unit[4]], sbuf.at[index, c], ssem.at[c, index]))
            s_copies.append(copy_of(call[3].at[unit[4]], att_all.at[:, lanes], ssem.at[3, index]))
            s_copies.append(copy_of(call[4].at[unit[4]], lbuf.at[index], ssem.at[4, index]))
        w_copies = groups[0] + groups[1] + groups[2]
        late = [copy_of(source, sums[index], lsem.at[index]) for index, source in enumerate(acc_in)]
        if last:
            late += [copy_of(late_in[0], hat, lsem.at[2]), copy_of(late_in[1], inv, lsem.at[3])]
        for copy in s_copies + w_copies + late:
            copy.start()
        if causal:
            fill_diagonal(diagonal)
        transpose_shards(h_ref, h_t, dp)
        for ref, target in zip(in_refs, in_t):
            transpose_shards(ref, target, dp)
        for copy in groups[3]:
            copy.wait()
        grad_att = dot(h_ref[...], wbuf[:, 3 * wide :]).astype(BF16)
        for index in range(number):
            grad_all[index] = grad_att[:, index * UNIT : (index + 1) * UNIT]
        for copy in s_copies:
            copy.wait()

        def step(u, carry):
            at = pl.ds(pl.multiple_of(u * UNIT, UNIT), UNIT)
            parts = attend_back_unit(
                sbuf[u, 0], sbuf[u, 1], sbuf[u, 2], att_all[:, at], grad_all[u], length, causal, diagonal, lbuf.at[u]
            )
            for c in range(3):
                dall[:, pl.ds(pl.multiple_of(c * wide + u * UNIT, UNIT), UNIT)] = parts[c]
            return carry

        lax.fori_loop(0, number, step, 0)

        def keep(weight, column):
            for index in range(number):
                part = weight[:, index * UNIT : (index + 1) * UNIT].astype(BF16)
                low = ((index % 2) * 4 + column) * UNIT
                stage[index // 2, :, :, low : low + UNIT] = part.reshape(8, UNIT, UNIT)

        for c in range(3):
            rows_t = in_t[0] if causal or c == 0 else in_t[1]
            keep(dot(rows_t[...], dall[:, c * wide : (c + 1) * wide]), c)
        keep(dot(h_t[...], att_all[...]), 3)
        share = number // 2 // results
        g_copies = [
            copy_of(stage.at[index * share : (index + 1) * share], ref, gsem.at[index]) for index, ref in enumerate(g_refs)
        ]
        for copy in g_copies:
            copy.start()
        for copy in w_copies + late[: len(acc_in)]:
            copy.wait()
        if causal:
            sums[0][...] += dot_nt(dall[...], wbuf[:, : 3 * wide])
        else:
            sums[0][...] += dot_nt(dall[:, :wide], wbuf[:, :wide])
            memory_sum = dot_nt(dall[:, wide:], wbuf[:, wide : 3 * wide])
            sums[1][...] = memory_sum + sums[1][...] if len(acc_in) == n_in else memory_sum
        if last:
            for copy in late[len(acc_in) :]:
                copy.wait()
            norm_back_rows(acc, hat, inv, gain_ref, low_ref, scaled_ref, gsum_ref, bsum_ref, rows)
        for copy in g_copies:
            copy.wait()

    big = sds((rows, depth), F32)
    shapes = [big] * (n_in - 1 if last else n_in)
    if last:
        shapes += [sds((rows, depth), BF16), big, sds((8, depth), F32), sds((8, depth), F32)]
    specs_out = [VMEM] * len(shapes) + [ANY] * results
    shapes += [sds((number // 2 // results, 8, UNIT, 8 * UNIT), BF16)] * results
    args = [scalars, grad_low, *others] + ([norm[2]] if last else [])
    tail = ([norm[0], norm[1]] if last else []) + list(carried) + list(packs)
    for call in saved:
        tail += call
    scratch = [
        pltpu.VMEM((depth, 4 * wide), BF16),
        pltpu.VMEM((number, 3, rows, UNIT), BF16),
        pltpu.VMEM((number, 2, rows), F32),
        pltpu.VMEM((rows, wide), BF16),
        pltpu.VMEM((number, rows, UNIT), BF16),
        pltpu.VMEM((depth, rows), BF16),
    ]
    scratch += [pltpu.VMEM((depth, rows), BF16)] * n_in
    scratch += [
        pltpu.VMEM((rows, 3 * wide), BF16),
        pltpu.VMEM((number // 2, 8, UNIT, 8 * UNIT), BF16),
        pltpu.VMEM((QUERY_BLOCK, QUERY_BLOCK), F32),
    ]
    if last:
        scratch += [pltpu.VMEM((rows, depth), F32), pltpu.VMEM((rows, depth), F32), pltpu.VMEM((rows, 128), F32)]
    scratch += [
        pltpu.SemaphoreType.DMA((4, number)),
        pltpu.SemaphoreType.DMA((5, number)),
        pltpu.SemaphoreType.DMA((results,)),
        pltpu.SemaphoreType.DMA((4,)),
    ]
    return pl.pallas_call(
        kernel,
        out_shape=shapes,
        in_specs=[SMEM] + [VMEM] * (len(args) - 1) + [ANY] * len(tail),
        out_specs=specs_out,
        scratch_shapes=scratch,
        compiler_params=params(),
        cost_estimate=cost_of(4.5 * number),
        name="self_bwd" if causal else "cross_bwd",
    )(*args, *tail)


def norm_back_rows(acc, hat, inv, gain_ref, low_ref, scaled_ref, gsum_ref, bsum_ref, rows):
    gsum_ref[...] = jnp.zeros_like(gsum_ref)
    bsum_ref[...] = jnp.zeros_like(bsum_ref)

    def chunk(at):
        gradient, normed = acc[at, :], hat[at, :]
        grad_in = norm_back_chunk(gradient, normed, inv[at, :1], gain_ref[...])
        low_ref[at, :] = grad_in.astype(BF16)
        scaled_ref[at, :] = RESIDUAL_ALPHA * grad_in
        gsum_ref[...] += fold_rows(gradient * normed)
        bsum_ref[...] += fold_rows(gradient)

    each_chunk(rows, chunk)


GELU_SCALE = 0.7978845608028654
GELU_CUBE = 0.044715


def gelu_and_slope(pre):
    square = pre * pre
    inner = pre * (GELU_SCALE + (GELU_SCALE * GELU_CUBE) * square)
    curve = jnp.tanh(inner)
    half = 0.5 + 0.5 * curve
    slope = half * (1.0 + pre * (1.0 - curve) * (GELU_SCALE + (3.0 * GELU_SCALE * GELU_CUBE) * square))
    return pre * half, slope


FFN_PART = FFN_UNIT // 2


def ffn_fwd_call(scalars, inputs, arrays, plan, partial, final):
    rows, depth = inputs.shape
    number = len(plan)
    last, has_partial = final is not None, partial is not None

    def kernel(*refs):
        it = iter(refs)
        sc, x_ref = next(it), next(it)
        if last:
            gain_old, bias_old, gain_ref, bias_ref = (next(it) for _ in range(4))
            late_in = [next(it), next(it)]
        part_in = next(it) if has_partial else None
        w_refs = [next(it) for _ in arrays]
        if last:
            out_ref, low_ref, scaled_ref, gsum_ref, bsum_ref = (next(it) for _ in range(5))
        else:
            sum_ref = next(it)
        act_ref, slope_ref = next(it), next(it)
        ubuf, dbuf, abuf, sbuf, pbuf, psem = (next(it) for _ in range(6))
        if last:
            acc, hat, cot, lsem = (next(it) for _ in range(4))
        wsem, gsem = next(it), next(it)
        target = acc if last else sum_ref

        up_copies, down_copies = [], []
        for index, unit in enumerate(plan):
            for inner, (up, down) in enumerate(unit):
                at = slice(inner * FFN_PART, (inner + 1) * FFN_PART)
                low = index * FFN_UNIT + inner * FFN_PART
                up_copies.append(copy_of(w_refs[up[0]].at[up[1]], ubuf.at[index, :, at], wsem.at[0, 2 * index + inner]))
                down_copies.append(
                    copy_of(w_refs[down[0]].at[down[1]], dbuf.at[:, low : low + FFN_PART], wsem.at[1, 2 * index + inner])
                )
        for copy in up_copies + down_copies:
            copy.start()
        if has_partial:
            part_copy = copy_of(part_in, target, psem)
            part_copy.start()
        if last:
            late = [copy_of(late_in[0], hat, lsem.at[0]), copy_of(late_in[1], cot, lsem.at[1])]
            for copy in late:
                copy.start()
        saves = []

        def gate(pre, index):
            activated, slope = gelu_and_slope(pre)
            abuf[:, index * FFN_UNIT : (index + 1) * FFN_UNIT] = activated.astype(BF16)
            sbuf[:, index * FFN_UNIT : (index + 1) * FFN_UNIT] = slope.astype(BF16)

        for index in range(number):
            up_copies[2 * index].wait()
            up_copies[2 * index + 1].wait()
            if index:
                gate(pbuf[(index - 1) % 2], index - 1)
            pbuf[index % 2] = dot(x_ref[...], ubuf[index])
        gate(pbuf[(number - 1) % 2], number - 1)
        for index in range(number):
            at = slice(index * FFN_UNIT, (index + 1) * FFN_UNIT)
            saves += [
                copy_of(abuf.at[:, at], act_ref.at[index], gsem.at[0, index]),
                copy_of(sbuf.at[:, at], slope_ref.at[index], gsem.at[1, index]),
            ]
        for copy in saves:
            copy.start()
        for copy in down_copies:
            copy.wait()
        if has_partial:
            part_copy.wait()
            target[...] += dot_nt(abuf[...], dbuf[...])
        else:
            target[...] = dot_nt(abuf[...], dbuf[...])
        if last:
            for copy in late:
                copy.wait()
            gsum_ref[...] = jnp.zeros_like(gsum_ref)
            bsum_ref[...] = jnp.zeros_like(bsum_ref)

            def chunk(at):
                old = hat[at, :] * gain_old[...] + bias_old[...]
                normed, xhat, inverse = norm_chunk(RESIDUAL_ALPHA * old + acc[at, :], gain_ref[...], bias_ref[...])
                out_ref[at, :] = normed.astype(BF16)
                gradient = cot[at, :].astype(F32)
                grad_in = norm_back_chunk(gradient, xhat, inverse, gain_ref[...])
                low_ref[at, :] = grad_in.astype(BF16)
                scaled_ref[at, :] = RESIDUAL_ALPHA * grad_in
                gsum_ref[...] += fold_rows(gradient * xhat)
                bsum_ref[...] += fold_rows(gradient)

            each_chunk(rows, chunk)
        for copy in saves:
            copy.wait()

    big, low = sds((rows, depth), F32), sds((rows, depth), BF16)
    if last:
        shapes = [low, low, big, sds((8, depth), F32), sds((8, depth), F32)]
    else:
        shapes = [big]
    specs_out = [VMEM] * len(shapes) + [ANY, ANY]
    shapes += [sds((number, rows, FFN_UNIT), BF16)] * 2
    args = [scalars, inputs]
    if last:
        args += [final[1], final[2], final[4], final[5]]
    specs = [SMEM] + [VMEM] * (len(args) - 1)
    tail = ([final[0], final[3]] if last else []) + ([partial] if has_partial else []) + list(arrays)
    scratch = [
        pltpu.VMEM((number, depth, FFN_UNIT), BF16),
        pltpu.VMEM((depth, number * FFN_UNIT), BF16),
        pltpu.VMEM((rows, number * FFN_UNIT), BF16),
        pltpu.VMEM((rows, number * FFN_UNIT), BF16),
        pltpu.VMEM((2, rows, FFN_UNIT), F32),
        pltpu.SemaphoreType.DMA,
    ]
    if last:
        scratch += [
            pltpu.VMEM((rows, depth), F32),
            pltpu.VMEM((rows, depth), F32),
            pltpu.VMEM((rows, depth), BF16),
            pltpu.SemaphoreType.DMA((2,)),
        ]
    scratch += [pltpu.SemaphoreType.DMA((2, 2 * number)), pltpu.SemaphoreType.DMA((2, number))]
    return pl.pallas_call(
        kernel,
        out_shape=shapes,
        in_specs=specs + [ANY] * len(tail),
        out_specs=specs_out,
        scratch_shapes=scratch,
        compiler_params=params(),
        cost_estimate=cost_of(12),
        name="ffn_fwd",
    )(*args, *tail)


def ffn_bwd_call(scalars, grad_low, inputs, arrays, saved, plan, carried, norm):
    rows, depth = inputs.shape
    number = len(plan)
    last = norm is not None

    def kernel(*refs):
        it = iter(refs)
        sc, g_in, x_ref = (next(it) for _ in range(3))
        gain_ref = next(it) if last else None
        late_in = [next(it), next(it)] if last else []
        acc_in = next(it)
        w_refs = [next(it) for _ in arrays]
        s_refs = [[next(it) for _ in call] for call in saved]
        if last:
            low_ref, scaled_ref, gsum_ref, bsum_ref = (next(it) for _ in range(4))
        else:
            sum_ref = next(it)
        g_ref = next(it)
        ubuf, dbuf, abuf, sbuf, gbuf, x_t, g_t, stage, psem = (next(it) for _ in range(9))
        if last:
            acc, hat, inv, lsem = (next(it) for _ in range(4))
        wsem, gsem = next(it), next(it)
        order, dp = sc[1], sc[2]
        target = acc if last else sum_ref

        copies = [[], [], [], []]
        for index, (quarters, _, _, call, at) in enumerate(plan):
            for inner, (up, down) in enumerate(quarters):
                low, number_of = index * FFN_UNIT + inner * FFN_PART, 2 * index + inner
                copies[0].append(copy_of(w_refs[down[0]].at[down[1]], dbuf.at[:, low : low + FFN_PART], wsem.at[0, number_of]))
                copies[3].append(copy_of(w_refs[up[0]].at[up[1]], ubuf.at[:, low : low + FFN_PART], wsem.at[3, number_of]))
            lanes = slice(index * FFN_UNIT, (index + 1) * FFN_UNIT)
            copies[1].append(copy_of(s_refs[call][1].at[at], sbuf.at[index], wsem.at[1, index]))
            copies[2].append(copy_of(s_refs[call][0].at[at], abuf.at[:, lanes], wsem.at[2, index]))
        for group in copies:
            for copy in group:
                copy.start()
        part_copy = copy_of(acc_in, target, psem)
        part_copy.start()
        if last:
            late = [copy_of(late_in[0], hat, lsem.at[0]), copy_of(late_in[1], inv, lsem.at[1])]
            for copy in late:
                copy.start()
        transpose_shards(g_in, g_t, dp)
        transpose_shards(x_ref, x_t, dp)
        for index in range(number):
            copies[0][2 * index].wait()
            copies[0][2 * index + 1].wait()
            copies[1][index].wait()
            grad_act = dot(g_in[...], dbuf[:, index * FFN_UNIT : (index + 1) * FFN_UNIT]) * sbuf[index].astype(F32)
            gbuf[:, index * FFN_UNIT : (index + 1) * FFN_UNIT] = grad_act.astype(BF16)
        for copy in copies[2]:
            copy.wait()

        def keep(rows_t, source, column):
            for half in range(number // 2):
                wide = 2 * FFN_UNIT
                weight = dot(rows_t[...], source[:, half * wide : (half + 1) * wide]).astype(BF16)
                for inner in range(4):
                    part = weight[:, inner * FFN_PART : (inner + 1) * FFN_PART]
                    stage[4 * half + inner, :, :, column * FFN_PART : (column + 1) * FFN_PART] = part.reshape(8, UNIT, FFN_PART)

        keep(x_t, gbuf, 0)
        keep(g_t, abuf, 1)
        g_copies = []
        for index, (_, places, relative, _, _) in enumerate(plan):
            for inner, place in enumerate(places):
                place = place ^ order if relative else place
                at = pl.ds(pl.multiple_of(place * FFN_UNIT, FFN_UNIT), FFN_UNIT)
                g_copies.append(
                    copy_of(stage.at[2 * index + inner], g_ref.at[index // 2, :, :, at], gsem.at[2 * index + inner])
                )
        for copy in g_copies:
            copy.start()
        for copy in copies[3]:
            copy.wait()
        part_copy.wait()
        target[...] += dot_nt(gbuf[...], ubuf[...])
        if last:
            for copy in late:
                copy.wait()
            norm_back_rows(acc, hat, inv, gain_ref, low_ref, scaled_ref, gsum_ref, bsum_ref, rows)
        for copy in g_copies:
            copy.wait()

    big, low = sds((rows, depth), F32), sds((rows, depth), BF16)
    shapes = [low, big, sds((8, depth), F32), sds((8, depth), F32)] if last else [big]
    specs_out = [VMEM] * len(shapes) + [ANY]
    shapes.append(sds((number // 2, 8, UNIT, 4 * FFN_UNIT), BF16))
    args = [scalars, grad_low, inputs] + ([norm[2]] if last else [])
    specs = [SMEM] + [VMEM] * (len(args) - 1)
    tail = ([norm[0], norm[1]] if last else []) + [carried] + list(arrays)
    for call in saved:
        tail += call
    scratch = [
        pltpu.VMEM((depth, number * FFN_UNIT), BF16),
        pltpu.VMEM((depth, number * FFN_UNIT), BF16),
        pltpu.VMEM((rows, number * FFN_UNIT), BF16),
        pltpu.VMEM((number, rows, FFN_UNIT), BF16),
        pltpu.VMEM((rows, number * FFN_UNIT), BF16),
        pltpu.VMEM((depth, rows), BF16),
        pltpu.VMEM((depth, rows), BF16),
        pltpu.VMEM((2 * number, 8, UNIT, 2 * FFN_PART), BF16),
        pltpu.SemaphoreType.DMA,
    ]
    if last:
        scratch += [
            pltpu.VMEM((rows, depth), F32),
            pltpu.VMEM((rows, depth), F32),
            pltpu.VMEM((rows, 128), F32),
            pltpu.SemaphoreType.DMA((2,)),
        ]
    scratch += [pltpu.SemaphoreType.DMA((4, 2 * number)), pltpu.SemaphoreType.DMA((2 * number,))]
    return pl.pallas_call(
        kernel,
        out_shape=shapes,
        in_specs=specs + [ANY] * len(tail),
        out_specs=specs_out,
        scratch_shapes=scratch,
        compiler_params=params(),
        cost_estimate=cost_of(17),
        name="ffn_bwd",
    )(*args, *tail)


def swap_pairs(count, mask):
    return [(i, i ^ mask) for i in range(count)]


def to_sibling(values):
    return lax.ppermute(values, "tensor", swap_pairs(4, 1))


def over_y(values):
    return lax.ppermute(values, "tensor", swap_pairs(4, 2))


def over_dp(values, mask):
    return lax.ppermute(values, "dp", swap_pairs(8, mask))


def over_x(values):
    return over_dp(values, 1)


def over_z_near(values):
    return over_dp(values, 2)


def over_z_far(values):
    return over_dp(values, 4)


def after(values, *earlier):
    return lax.optimization_barrier((values, *earlier))[0]


def add(*terms):
    total = terms[0].astype(F32)
    for term in terms[1:]:
        total = total + term.astype(F32)
    return total.astype(BF16)


MOVES = {"y": over_y, "x": over_x, "z": over_z_near}


class Reduction:
    def __init__(self, sent, portions):
        self.other = to_sibling(sent)
        self.portions = portions

    def start(self, kept, *earlier):
        other = after(self.other, *earlier) if earlier else self.other
        split = (2, 2, 2, 2, *kept.shape[2:])
        kept, other = kept.reshape(split), other.reshape(split)
        self.states = []
        for low, high, orders in self.portions:
            self.states.append(([kept[..., low:high], other[..., low:high]], ["y", "x", "z", "w"], list(orders)))
        return self.send()

    def send(self):
        self.sends = []
        for terms, axes, orders in self.states:
            axis = axes.index(orders[0])
            self.sends.append(add(*[lax.index_in_dim(t, 1, axis, False) for t in terms]))
            terms[:] = [lax.index_in_dim(t, 0, axis, False) for t in terms]
            axes.remove(orders[0])
        return self.sends

    def step(self, *earlier):
        for send, (terms, _, orders) in zip(self.sends, self.states):
            moved = MOVES[orders.pop(0)](send)
            terms.append(after(moved, *earlier) if earlier else moved)
        if self.states[0][2]:
            return self.send()
        whole = [jnp.concatenate([add(*[t[i] for t in terms]) for terms, _, _ in self.states], axis=-1) for i in (0, 1)]
        self.states, self.sends = whole[0], [whole[1]]
        return self.sends

    def last(self):
        return add(self.states, over_z_far(self.sends[0])).astype(F32)


def sentence_body(
    tokens,
    memory,
    dec_lengths,
    mem_lengths,
    self_qkv,
    self_out,
    cross_q,
    cross_kv,
    cross_out,
    ffn_in,
    ffn_out,
    norm_gains,
    norm_biases,
    cotangent,
):
    dp = lax.axis_index("dp")
    mine = lax.axis_index("tensor")
    order = dp & 3
    self_scalars = jnp.stack([dec_lengths[0, mine], order, dp, mine]).astype(jnp.int32)
    cross_scalars = jnp.stack([mem_lengths[0, mine], order, dp, mine]).astype(jnp.int32)
    gains = [norm_gains[i : i + 1] for i in range(3)]
    biases = [norm_biases[i : i + 1] for i in range(3)]

    def quarters(matrices):
        halves = matrices.reshape(2, 2, matrices.shape[1], 2, UNIT).transpose(0, 3, 1, 2, 4)
        return halves.reshape(4, 2, matrices.shape[1], UNIT)

    def own_quarter(pack):
        return lax.dynamic_index_in_dim(pack, order, 0, False)

    def joined(near, side, up, corner):
        return jnp.stack([near, side, up, corner])

    self_pack = quarters(jnp.concatenate([self_qkv, self_out.T[None]], axis=0))
    self_near = over_y(own_quarter(self_pack))
    self_sib = to_sibling(self_pack)
    cross_pack = quarters(jnp.concatenate([cross_q[None], cross_kv, cross_out.T[None]], axis=0))
    ffn_pack = jnp.stack([ffn_in, ffn_out.T]).reshape(2, ffn_in.shape[0], 4, FFN_PART).transpose(2, 0, 1, 3)
    cross_quarter, ffn_quarter = own_quarter(cross_pack), own_quarter(ffn_pack)

    cross_near = over_y(after(cross_quarter, self_near))
    self_side, self_up = over_x(self_near), over_z_near(self_near)
    early = [(0, 0, False), (0, 1, False), (1, 0, False), (1, 1, False)]
    late = [(0, 0, True), (0, 1, True), (1, 0, True), (1, 1, True)]
    self_a = attention_fwd_call(
        after(self_scalars, self_near, cross_quarter, ffn_quarter), [], [tokens], [self_pack, self_sib], early, None, None
    )
    self_side, self_up, cross_near = after(self_side, self_a[4]), after(self_up, self_a[4]), after(cross_near, self_a[4])
    self_corner = over_x(self_up)
    ffn_near = over_y(after(ffn_quarter, cross_near))
    cross_side, cross_up = over_x(cross_near), over_z_near(cross_near)
    self_rest = joined(self_near, self_side, self_up, self_corner)
    self_far = to_sibling(self_rest)
    cross_sib = to_sibling(after(cross_pack, self_near))
    ffn_sib = to_sibling(after(ffn_pack, self_side))
    self_packs = [self_pack, self_sib, self_rest, self_far]
    cross_corner = over_x(cross_up)
    self_b = attention_fwd_call(
        after(self_scalars, cross_up), [tokens], [tokens], self_packs[2:], late, self_a[5], (gains[0], biases[0])
    )
    first_low, first_hat, first_inv = self_b[5:]
    cross_in = [first_low, memory]
    cross_rest = joined(cross_near, cross_side, cross_up, after(cross_corner, self_b[4]))
    ffn_near = after(ffn_near, self_b[4])
    ffn_side, ffn_up = over_x(ffn_near), over_z_near(ffn_near)
    cross_far = to_sibling(cross_rest)
    ffn_near_far = to_sibling(ffn_near)
    cross_packs = [cross_pack, cross_sib, cross_rest, cross_far]
    cross_b = attention_fwd_call(
        cross_scalars, [first_hat, gains[0], biases[0]], cross_in, cross_packs,
        early + [(a + 2, h, r) for a, h, r in late], None, (gains[1], biases[1]),
    )
    second_low, second_hat, second_inv = cross_b[5:]
    ffn_side, ffn_up = after(ffn_side, cross_b[4]), after(ffn_up, cross_b[4])
    up_corner, down_corner = over_x(ffn_up[:1]), over_z_near(ffn_side[1:])
    ffn_side_far, ffn_up_far = to_sibling(ffn_side), to_sibling(ffn_up)
    ffn_a = ffn_fwd_call(
        cross_scalars, second_low, [ffn_pack, ffn_sib],
        [[((p, (q, 0)), (p, (q, 1))) for q in (2 * h, 2 * h + 1)] for p in (0, 1) for h in (0, 1)], None, None,
    )
    up_corner, down_corner = after(up_corner, ffn_a[0]), after(down_corner, ffn_a[0])
    up_corner_far, down_corner_far = to_sibling(up_corner), to_sibling(down_corner)
    ffn_arrays = [ffn_pack, ffn_sib, ffn_near, ffn_side, ffn_up, up_corner, down_corner]
    ffn_arrays += [ffn_near_far, ffn_side_far, ffn_up_far, up_corner_far, down_corner_far]

    def parts(piece, base):
        if piece < 2:
            return [((piece, (q, 0)), (piece, (q, 1))) for q in range(4)]
        low = base + 5 * (piece - 2)
        return [((low + q, (0,)), (low + q, (1,))) for q in range(3)] + [((low + 3, (0,)), (low + 4, (0,)))]

    def units_of(piece, base):
        quarter = parts(piece, base)
        return [quarter[:2], quarter[2:]]

    ffn_b = ffn_fwd_call(
        cross_scalars, second_low, ffn_arrays[2:], units_of(2, 0) + units_of(3, 0), ffn_a[0],
        (second_hat, gains[1], biases[1], cotangent, gains[2], biases[2]),
    )
    out_rows, third_low, third_scaled, third_gain, third_bias = ffn_b[:5]

    def ffn_plan(pieces):
        return [
            (unit, (2 * u, 2 * u + 1), piece > 1, piece // 2, 2 * (piece % 2) + u)
            for piece in pieces
            for u, unit in enumerate(units_of(piece, 2))
        ]

    def plan_of(pieces):
        return [
            (piece, half, piece > 1, piece // 2, 2 * (piece % 2) + half) for piece in pieces for half in (0, 1)
        ]

    ffn_saved = [ffn_a[1:3], ffn_b[5:7]]
    ffn_d = ffn_bwd_call(
        cross_scalars, third_low, second_low, ffn_arrays, ffn_saved, ffn_plan((1, 3)), third_scaled, None
    )
    ffn_sum = Reduction(ffn_d[1], [(0, 768, "yxz"), (768, 1408, "xzy"), (1408, 2048, "zyx")])
    ffn_e = ffn_bwd_call(
        cross_scalars, third_low, second_low, ffn_arrays, ffn_saved, ffn_plan((0, 2)), ffn_d[0],
        (second_hat, second_inv, gains[1]),
    )
    second_back, second_scaled, second_gain, second_bias = ffn_e[:4]
    second_back = after(second_back, *ffn_sum.start(ffn_e[4], second_gain))

    cross_e = attention_bwd_call(
        cross_scalars, second_back, cross_in, cross_packs, [cross_b[:5]],
        [(p, h, p > 1, 0, 2 * p + h) for p in (1, 3, 0, 2) for h in (0, 1)], [second_scaled],
        (first_hat, first_inv, gains[0]), 2,
    )
    grad_memory, first_back, first_scaled, first_gain, first_bias = cross_e[:5]
    norm_sums = jnp.stack([first_gain, second_gain, third_gain, first_bias, second_bias, third_bias])
    norm_total = jnp.sum(norm_sums, axis=1)
    sends = ffn_sum.step(first_gain)
    cross_sum = Reduction(after(cross_e[5], *sends), [(0, 512, "xzy"), (512, 1024, "yxz")])
    first_back = after(first_back, *sends, norm_total)

    self_saved = [self_a[:5], self_b[:5]]
    self_d = attention_bwd_call(
        self_scalars, first_back, [tokens], self_packs, self_saved, plan_of((1, 3)), [first_scaled], None
    )
    sends = ffn_sum.step(self_d[0]) + cross_sum.start(cross_e[6], self_d[0])
    self_sum = Reduction(after(self_d[1], *sends), [(0, 512, "xzy"), (512, 1024, "yxz")])
    gate = after(self_d[0], *sends)
    self_e = attention_bwd_call(
        self_scalars, first_back, [tokens], self_packs, self_saved, plan_of((0, 2)), [gate], None
    )
    grad_tokens = self_e[0]
    sends = self_sum.start(self_e[1], grad_tokens)
    sends = cross_sum.step(*sends)
    sends = ffn_sum.step(*sends)
    norm_total = norm_total + after(to_sibling(norm_total), *sends)
    norm_total = norm_total + over_y(norm_total)
    sends = self_sum.step(*sends, norm_total)
    sends = cross_sum.step(*sends)
    norm_total = norm_total + after(over_x(norm_total), *sends)
    sends = self_sum.step(*sends, norm_total)
    cross_sum.step(*sends)
    norm_total = norm_total + after(over_z_near(norm_total), *sends)
    sends = self_sum.step(*sends, norm_total)
    norm_total = norm_total + after(over_z_far(norm_total), *sends)
    ffn_sum = ffn_sum.last()
    cross_sum = cross_sum.last()
    self_sum = self_sum.last()

    def matrices(total):
        return total.reshape(UNIT, 2, 4, UNIT).transpose(2, 0, 1, 3).reshape(4, UNIT, 2 * UNIT)

    self_grads, cross_grads = matrices(self_sum), matrices(cross_sum)
    ffn_grads = ffn_sum.reshape(UNIT, 4, 2, FFN_PART).transpose(2, 0, 1, 3).reshape(2, UNIT, -1)
    return (
        out_rows,
        grad_tokens,
        grad_memory,
        self_grads[:3],
        self_grads[3].T,
        cross_grads[0],
        cross_grads[1:3],
        cross_grads[3].T,
        ffn_grads[0],
        ffn_grads[1].T,
        norm_total[:3],
        norm_total[3:],
    )


def sentence_fits(mesh, tokens, memory, dec_lengths):
    shape = dict(mesh.shape)
    rows = tokens.shape[0] // mesh.size
    sentences = dec_lengths.shape[1]
    return (
        shape["tensor"] == 4
        and shape["dp"] == 8
        and sentences == 4
        and rows == 512
        and memory.shape[0] // mesh.size == rows
        and tokens.shape[1] == 1024
    )


def smooth_gate(values):
    return jax.nn.gelu(values, approximate=True)


def norm_rows(hidden, norm_gain, norm_bias):
    center = hidden - jnp.mean(hidden, axis=-1, keepdims=True)
    inverse = lax.rsqrt(jnp.mean(center * center, axis=-1, keepdims=True) + NORM_EPSILON)
    normed = center * inverse
    return (normed * norm_gain + norm_bias, normed, inverse)


def norm_back(gradient, normed, inverse, norm_gain):
    scaled = gradient * norm_gain
    grad_in = inverse * (
        scaled
        - jnp.mean(scaled, axis=-1, keepdims=True)
        - normed * jnp.mean(scaled * normed, axis=-1, keepdims=True)
    )
    return (grad_in, jnp.sum(gradient * normed, axis=0), jnp.sum(gradient, axis=0))


def head_view(values, sentences):
    return values.reshape(sentences, -1, values.shape[1] // HEAD_DIM, HEAD_DIM)


def masked_scores(query_heads, key_heads, key_mask):
    scores = jnp.einsum(
        "sqhe,skhe->shqk", query_heads, key_heads, preferred_element_type=jnp.float32
    ) * HEAD_DIM ** (-0.5)
    return jnp.where(key_mask, scores, MASKED_SCORE)


def attention_forward(query_rows, key_rows, value_rows, key_mask, sentences):
    scores = masked_scores(
        head_view(query_rows, sentences), head_view(key_rows, sentences), key_mask
    )
    row_peak = jnp.max(scores, axis=-1, keepdims=True)
    exponent_terms = jnp.exp(scores - row_peak)
    row_sum = jnp.sum(exponent_terms, axis=-1, keepdims=True)
    softmax_probs = exponent_terms / row_sum
    attended = jnp.einsum(
        "shqk,skhe->sqhe",
        softmax_probs.astype(jnp.bfloat16),
        head_view(value_rows, sentences),
        preferred_element_type=jnp.float32,
    ).astype(jnp.bfloat16)
    return (attended.reshape(query_rows.shape), row_peak + jnp.log(row_sum))


def attention_backward(query_rows, key_rows, value_rows, key_mask, log_total, grad_rows, sentences):
    query_heads = head_view(query_rows, sentences)
    key_heads = head_view(key_rows, sentences)
    value_heads = head_view(value_rows, sentences)
    grad_heads = head_view(grad_rows, sentences)
    softmax_probs = jnp.exp(masked_scores(query_heads, key_heads, key_mask) - log_total)
    grad_probs = jnp.einsum(
        "sqhe,skhe->shqk", grad_heads, value_heads, preferred_element_type=jnp.float32
    )
    row_delta = jnp.sum(softmax_probs * grad_probs, axis=-1, keepdims=True)
    grad_scores = (softmax_probs * (grad_probs - row_delta)).astype(jnp.bfloat16)
    score_scale = HEAD_DIM ** (-0.5)
    grad_query = (
        jnp.einsum("shqk,skhe->sqhe", grad_scores, key_heads, preferred_element_type=jnp.float32)
        * score_scale
    ).astype(jnp.bfloat16)
    grad_key = (
        jnp.einsum("shqk,sqhe->skhe", grad_scores, query_heads, preferred_element_type=jnp.float32)
        * score_scale
    ).astype(jnp.bfloat16)
    grad_value = jnp.einsum(
        "shqk,sqhe->skhe",
        softmax_probs.astype(jnp.bfloat16),
        grad_heads,
        preferred_element_type=jnp.float32,
    ).astype(jnp.bfloat16)
    return (
        grad_query.reshape(query_rows.shape),
        grad_key.reshape(key_rows.shape),
        grad_value.reshape(value_rows.shape),
    )


def body(
    tokens,
    memory,
    dec_lengths,
    mem_lengths,
    self_qkv,
    self_out,
    cross_q,
    cross_kv,
    cross_out,
    ffn_in,
    ffn_out,
    norm_gains,
    norm_biases,
    cotangent,
):
    row_share = tokens.shape[0]
    sentences = dec_lengths.shape[1]
    all_tokens, all_memory = (
        lax.all_gather(tokens, "tensor", axis=0, tiled=True),
        lax.all_gather(memory, "tensor", axis=0, tiled=True),
    )
    sentence_len = all_tokens.shape[0] // sentences
    memory_len = all_memory.shape[0] // sentences
    positions = jnp.arange(sentence_len, dtype=jnp.int32)
    self_mask = (
        (positions[None, :] <= positions[:, None])[None]
        & (positions[None, None, :] < dec_lengths[0][:, None, None])
    )[:, None]
    memory_positions = jnp.arange(memory_len, dtype=jnp.int32)
    cross_mask = (memory_positions[None, :] < mem_lengths[0][:, None])[:, None, None, :]

    def branch_rows(attended, weight):
        return lax.psum_scatter(
            jnp.dot(attended, weight, preferred_element_type=jnp.float32).astype(jnp.bfloat16),
            "tensor",
            scatter_dimension=0,
            tiled=True,
        ).astype(jnp.float32)

    def branch_grad(grad_rows, attended, weight):
        grad_low = grad_rows.astype(jnp.bfloat16)
        grad_all = lax.all_gather(grad_low, "tensor", axis=0, tiled=True)
        grad_attended = jnp.dot(grad_all, weight.T, preferred_element_type=jnp.float32).astype(
            jnp.bfloat16
        )
        weight_part = jnp.dot(attended.T, grad_all, preferred_element_type=jnp.float32)
        return (grad_attended, weight_part)

    def gather_normed(values):
        return lax.all_gather(values, "tensor", axis=0, tiled=True)

    def head_input_sum(term):
        return lax.psum_scatter(
            term(jnp.int32(0), row_share * lax.axis_size("tensor")).astype(jnp.bfloat16),
            "tensor",
            scatter_dimension=0,
            tiled=True,
        ).astype(jnp.float32)

    self_proj = jnp.einsum(
        "td,cde->cte", all_tokens, self_qkv, preferred_element_type=jnp.float32
    ).astype(jnp.bfloat16)
    self_att, self_lse = attention_forward(
        self_proj[0], self_proj[1], self_proj[2], self_mask, sentences
    )
    self_branch = branch_rows(self_att, self_out)
    first_norm, first_hat, first_inv = norm_rows(
        RESIDUAL_ALPHA * tokens.astype(jnp.float32) + self_branch, norm_gains[0], norm_biases[0]
    )
    first_all = gather_normed(first_norm.astype(jnp.bfloat16))
    cross_query = jnp.dot(first_all, cross_q, preferred_element_type=jnp.float32).astype(
        jnp.bfloat16
    )
    cross_proj = jnp.einsum(
        "td,cde->cte", all_memory, cross_kv, preferred_element_type=jnp.float32
    ).astype(jnp.bfloat16)
    cross_att, cross_lse = attention_forward(
        cross_query, cross_proj[0], cross_proj[1], cross_mask, sentences
    )
    cross_branch = branch_rows(cross_att, cross_out)
    second_norm, second_hat, second_inv = norm_rows(
        RESIDUAL_ALPHA * first_norm + cross_branch, norm_gains[1], norm_biases[1]
    )
    second_all = gather_normed(second_norm.astype(jnp.bfloat16))
    pre_gate = jnp.dot(second_all, ffn_in, preferred_element_type=jnp.float32)
    activated = smooth_gate(pre_gate).astype(jnp.bfloat16)
    ffn_branch = lax.psum_scatter(
        jnp.dot(activated, ffn_out, preferred_element_type=jnp.float32).astype(jnp.bfloat16),
        "tensor",
        scatter_dimension=0,
        tiled=True,
    ).astype(jnp.float32)
    out_rows, third_hat, third_inv = norm_rows(
        RESIDUAL_ALPHA * second_norm + ffn_branch, norm_gains[2], norm_biases[2]
    )
    grad_third, third_gain, third_bias = norm_back(
        cotangent.astype(jnp.float32), third_hat, third_inv, norm_gains[2]
    )
    grad_ffn_all = lax.all_gather(grad_third.astype(jnp.bfloat16), "tensor", axis=0, tiled=True)
    unused_gate, gate_pull = jax.vjp(smooth_gate, pre_gate)
    grad_act = gate_pull(jnp.dot(grad_ffn_all, ffn_out.T, preferred_element_type=jnp.float32))[
        0
    ].astype(jnp.bfloat16)
    grad_ffn_out = jnp.dot(activated.T, grad_ffn_all, preferred_element_type=jnp.float32)
    grad_ffn_in = jnp.dot(second_all.T, grad_act, preferred_element_type=jnp.float32)
    grad_second = RESIDUAL_ALPHA * grad_third + lax.psum_scatter(
        jnp.dot(grad_act, ffn_in.T, preferred_element_type=jnp.float32).astype(jnp.bfloat16),
        "tensor",
        scatter_dimension=0,
        tiled=True,
    ).astype(jnp.float32)
    grad_second_in, second_gain, second_bias = norm_back(
        grad_second, second_hat, second_inv, norm_gains[1]
    )
    grad_cross_att, cross_out_part = branch_grad(grad_second_in, cross_att, cross_out)
    grad_cq, grad_ck, grad_cv = attention_backward(
        cross_query, cross_proj[0], cross_proj[1], cross_mask, cross_lse, grad_cross_att, sentences
    )
    grad_cross_q = jnp.dot(first_all.T, grad_cq, preferred_element_type=jnp.float32)
    cross_grads = jnp.stack([grad_ck, grad_cv])
    grad_cross_kv = jnp.einsum(
        "td,cte->cde", all_memory, cross_grads, preferred_element_type=jnp.float32
    )
    grad_memory = lax.psum_scatter(
        jnp.einsum("cte,cde->td", cross_grads, cross_kv, preferred_element_type=jnp.float32).astype(
            jnp.bfloat16
        ),
        "tensor",
        scatter_dimension=0,
        tiled=True,
    ).astype(jnp.float32)

    def cross_input_term(first_row, row_total):
        return jnp.dot(grad_cq, cross_q.T, preferred_element_type=jnp.float32)

    cross_input = head_input_sum(cross_input_term)
    grad_first = RESIDUAL_ALPHA * grad_second_in + cross_input
    grad_first_in, first_gain, first_bias = norm_back(
        grad_first, first_hat, first_inv, norm_gains[0]
    )
    grad_self_att, self_out_part = branch_grad(grad_first_in, self_att, self_out)
    grad_sq, grad_sk, grad_sv = attention_backward(
        self_proj[0], self_proj[1], self_proj[2], self_mask, self_lse, grad_self_att, sentences
    )
    self_grads = jnp.stack([grad_sq, grad_sk, grad_sv])
    grad_self_qkv = jnp.einsum(
        "td,cte->cde", all_tokens, self_grads, preferred_element_type=jnp.float32
    )

    def self_input_term(first_row, row_total):
        return jnp.einsum("cte,cde->td", self_grads, self_qkv, preferred_element_type=jnp.float32)

    self_input = head_input_sum(self_input_term)
    grad_tokens = RESIDUAL_ALPHA * grad_first_in + self_input
    summed = (
        lax.psum_scatter(
            grad_self_qkv.astype(jnp.bfloat16), "dp", scatter_dimension=1, tiled=True
        ).astype(jnp.float32),
        lax.psum_scatter(
            self_out_part.astype(jnp.bfloat16), "dp", scatter_dimension=1, tiled=True
        ).astype(jnp.float32),
        lax.psum_scatter(
            grad_cross_q.astype(jnp.bfloat16), "dp", scatter_dimension=0, tiled=True
        ).astype(jnp.float32),
        lax.psum_scatter(
            grad_cross_kv.astype(jnp.bfloat16), "dp", scatter_dimension=1, tiled=True
        ).astype(jnp.float32),
        lax.psum_scatter(
            cross_out_part.astype(jnp.bfloat16), "dp", scatter_dimension=1, tiled=True
        ).astype(jnp.float32),
        lax.psum_scatter(
            grad_ffn_in.astype(jnp.bfloat16), "dp", scatter_dimension=0, tiled=True
        ).astype(jnp.float32),
        lax.psum_scatter(
            grad_ffn_out.astype(jnp.bfloat16), "dp", scatter_dimension=1, tiled=True
        ).astype(jnp.float32),
    )
    gain_total, bias_total = lax.psum(
        (
            jnp.stack([first_gain, second_gain, third_gain]),
            jnp.stack([first_bias, second_bias, third_bias]),
        ),
        ("dp", "tensor"),
    )
    return (
        out_rows.astype(jnp.bfloat16),
        grad_tokens,
        grad_memory,
        summed[0],
        summed[1],
        summed[2],
        summed[3],
        summed[4],
        summed[5],
        summed[6],
        gain_total,
        bias_total,
    )


def solution(mesh):
    in_specs = (
        P(("dp", "tensor"), None),
        P(("dp", "tensor"), None),
        P("dp", None),
        P("dp", None),
        P(None, None, "tensor"),
        P("tensor", None),
        P(None, "tensor"),
        P(None, None, "tensor"),
        P("tensor", None),
        P(None, "tensor"),
        P("tensor", None),
        P(),
        P(),
        P(("dp", "tensor"), None),
    )
    out_specs = (
        P(("dp", "tensor"), None),
        P(("dp", "tensor"), None),
        P(("dp", "tensor"), None),
        P(None, "dp", "tensor"),
        P("tensor", "dp"),
        P("dp", "tensor"),
        P(None, "dp", "tensor"),
        P("tensor", "dp"),
        P("dp", "tensor"),
        P("tensor", "dp"),
        P(),
        P(),
    )

    def step(*args):
        chosen = sentence_body if sentence_fits(mesh, args[0], args[1], args[2]) else body
        return jax.shard_map(
            chosen, mesh=mesh, in_specs=in_specs, out_specs=out_specs, check_vma=False
        )(*args)

    return step
```

```python
import functools
import jax
import jax.numpy as jnp
from jax import lax
from jax.experimental import pallas as pl
from jax.experimental.pallas import tpu as pltpu
from jax.sharding import PartitionSpec as P

HEAD_DIM = 64
RESIDUAL_ALPHA = 4.16
NORM_EPSILON = 1e-05
MASKED_SCORE = -1000000000.0
SCORE_SCALE = HEAD_DIM ** (-0.5)
UNIT = 128
QUERY_BLOCK = 256
FFN_UNIT = 512
ROW_CHUNK = 64
BF16 = jnp.bfloat16
F32 = jnp.float32


def dot(left, right):
    return lax.dot_general(left, right, (((1,), (0,)), ((), ())), preferred_element_type=F32)


def dot_nt(left, right):
    return lax.dot_general(left, right, (((1,), (1,)), ((), ())), preferred_element_type=F32)


def shard_of(position):
    return ((position >> 2) & 1) | (position & 2) | ((position & 1) << 2)


def copy_of(source, target, sem):
    return pltpu.make_async_copy(source, target, sem)


def own_lanes(rows, head):
    lanes = lax.broadcasted_iota(jnp.int32, rows.shape, 1)
    return jnp.where((lanes >= HEAD_DIM) if head else (lanes < HEAD_DIM), rows, 0.0)


def extended_keys(keys, length):
    lanes = lax.broadcasted_iota(jnp.int32, keys.shape, 1)
    rows = lax.broadcasted_iota(jnp.int32, keys.shape, 0)
    mask = jnp.where((lanes == 0) & (rows >= length), MASKED_SCORE, 0.0).astype(BF16)
    keys = keys.astype(F32)
    return [jnp.concatenate([own_lanes(keys, head).astype(BF16), mask], axis=1) for head in (0, 1)]


def extended_query(query):
    lanes = lax.broadcasted_iota(jnp.int32, query.shape, 1)
    return jnp.concatenate([query, jnp.where(lanes == 0, 1.0, 0.0).astype(BF16)], axis=1)


def fill_diagonal(diagonal):
    keys = lax.broadcasted_iota(jnp.int32, diagonal.shape, 0)
    queries = lax.broadcasted_iota(jnp.int32, diagonal.shape, 1)
    diagonal[...] = jnp.where(keys <= queries, 0.0, MASKED_SCORE)


def key_ranges(block, keys, causal):
    if not causal:
        return [(0, keys)]
    return [(low, low + QUERY_BLOCK) for low in range(0, (block + 1) * QUERY_BLOCK, QUERY_BLOCK)]


def attend_unit(query, keys, values, length, causal, diagonal, lse_ref):
    rows, count = query.shape[0], keys.shape[0]
    values_t = jnp.transpose(values.astype(F32)).astype(BF16)
    wide_keys, wide_query = extended_keys(keys, length), extended_query(query)
    items = [(head, block) for block in range(rows // QUERY_BLOCK) for head in (0, 1)]
    scores, probs, totals, mixed = {}, {}, {}, {}
    for head, block in items:
        part = wide_query[block * QUERY_BLOCK : (block + 1) * QUERY_BLOCK]
        ranges = key_ranges(block, count, causal)
        scores[head, block] = [dot_nt(wide_keys[head][a:b], part) for a, b in ranges]
        if causal:
            scores[head, block][-1] = scores[head, block][-1] + diagonal[...]
    for head, block in items:
        pieces = scores[head, block]
        peak = functools.reduce(jnp.maximum, [jnp.max(p, axis=0, keepdims=True) for p in pieces])
        terms = [jnp.exp(p - peak) for p in pieces]
        total = sum(jnp.sum(t, axis=0, keepdims=True) for t in terms)
        at = slice(block * QUERY_BLOCK, (block + 1) * QUERY_BLOCK)
        lse_ref[head : head + 1, at] = peak + jnp.log(total)
        totals[head, block] = total
        probs[head, block] = jnp.concatenate([t.astype(BF16) for t in terms], axis=0)
    for head, block in items:
        own = values_t[head * HEAD_DIM : (head + 1) * HEAD_DIM, : probs[head, block].shape[0]]
        mixed[head, block] = dot(own, probs[head, block]) / totals[head, block]
    out = [
        jnp.transpose(jnp.concatenate([mixed[0, block], mixed[1, block]], axis=0))
        for block in range(rows // QUERY_BLOCK)
    ]
    return jnp.concatenate(out, axis=0).astype(BF16)


def attend_back_unit(query, keys, values, attended, grad, length, causal, diagonal, lse_ref):
    rows, count = query.shape[0], keys.shape[0]
    blocks = range(rows // QUERY_BLOCK)
    query_f, keys_f, grad_f = (a.astype(F32) for a in (query, keys, grad))
    wide_keys, wide_query = extended_keys(keys, length), extended_query(query)
    delta = jnp.transpose(grad_f * attended.astype(F32))
    deltas = [
        jnp.sum(delta[head * HEAD_DIM : (head + 1) * HEAD_DIM], axis=0, keepdims=True)
        for head in (0, 1)
    ]
    keys_t = jnp.transpose(keys_f).astype(BF16)
    query_own = [own_lanes(query_f, head).astype(BF16) for head in (0, 1)]
    grad_own = [own_lanes(grad_f, head).astype(BF16) for head in (0, 1)]
    items = [(head, block) for block in blocks for head in (0, 1)]
    scores, slopes, probs, back, grad_query = {}, {}, {}, {}, {}
    for head, block in items:
        at = slice(block * QUERY_BLOCK, (block + 1) * QUERY_BLOCK)
        for a, b in key_ranges(block, count, causal):
            scores[head, block, a] = dot_nt(wide_keys[head][a:b], wide_query[at])
            slopes[head, block, a] = dot_nt(values[a:b], grad_own[head][at])
    for head, block in items:
        at = slice(block * QUERY_BLOCK, (block + 1) * QUERY_BLOCK)
        ranges = key_ranges(block, count, causal)
        for a, b in ranges:
            score = scores[head, block, a]
            if causal and (a, b) == ranges[-1]:
                score = score + diagonal[...]
            prob = jnp.exp(score - lse_ref[head : head + 1, at])
            probs[head, block, a] = prob.astype(BF16)
            back[head, block, a] = (prob * (slopes[head, block, a] - deltas[head][:, at])).astype(BF16)
    for head, block in items:
        own = keys_t[head * HEAD_DIM : (head + 1) * HEAD_DIM]
        grad_query[head, block] = sum(
            dot(own[:, a:b], back[head, block, a]) for a, b in key_ranges(block, count, causal)
        )
    grad_keys, grad_values = [], []
    for low in sorted({key[2] for key in back}):
        live = [key for key in back if key[2] == low]
        at = [slice(block * QUERY_BLOCK, (block + 1) * QUERY_BLOCK) for _, block, _ in live]
        grad_values.append(
            dot(
                jnp.concatenate([probs[key] for key in live], axis=1),
                jnp.concatenate([grad_own[key[0]][a] for key, a in zip(live, at)], axis=0),
            )
        )
        grad_keys.append(
            dot(
                jnp.concatenate([back[key] for key in live], axis=1),
                jnp.concatenate([query_own[key[0]][a] for key, a in zip(live, at)], axis=0),
            )
        )
    grad_query = [
        jnp.transpose(jnp.concatenate([grad_query[0, block], grad_query[1, block]], axis=0)) * SCORE_SCALE
        for block in blocks
    ]
    return tuple(
        jnp.concatenate(parts, axis=0).astype(BF16) for parts in (grad_query, grad_keys, grad_values)
    )


def norm_chunk(hidden, gain, bias):
    center = hidden - jnp.mean(hidden, axis=-1, keepdims=True)
    inverse = lax.rsqrt(jnp.mean(center * center, axis=-1, keepdims=True) + NORM_EPSILON)
    normed = center * inverse
    return normed * gain + bias, normed, inverse


def norm_back_chunk(gradient, normed, inverse, gain):
    scaled = gradient * gain
    return inverse * (
        scaled
        - jnp.mean(scaled, axis=-1, keepdims=True)
        - normed * jnp.mean(scaled * normed, axis=-1, keepdims=True)
    )


def fold_rows(values):
    return jnp.sum(values.reshape(values.shape[0] // 8, 8, values.shape[1]), axis=0)


def each_chunk(rows, body):
    def step(index, carry):
        body(pl.ds(pl.multiple_of(index * ROW_CHUNK, ROW_CHUNK), ROW_CHUNK))
        return carry

    lax.fori_loop(0, rows // ROW_CHUNK, step, 0)


def transpose_shards(source, target, dp):
    for position in range(8):
        block = dp ^ shard_of(position)
        columns = source[:, pl.ds(pl.multiple_of(block * UNIT, UNIT), UNIT)]
        target[position * UNIT : (position + 1) * UNIT, :] = jnp.transpose(
            columns.astype(F32)
        ).astype(BF16)


SMEM = pl.BlockSpec(memory_space=pltpu.SMEM)
VMEM = pl.BlockSpec(memory_space=pltpu.VMEM)
ANY = pl.BlockSpec(memory_space=pl.ANY)


def params(limit=56):
    return pltpu.CompilerParams(vmem_limit_bytes=limit * 1024 * 1024)


def cost_of(microseconds):
    return pl.CostEstimate(flops=int(microseconds * 1.1e9), bytes_accessed=4 << 20, transcendentals=0)


def sds(shape, dtype):
    return jax.ShapeDtypeStruct(shape, dtype)


def weight_copies(pieces, order, wbuf, obuf, wsem, osem):
    groups, outs = [[], [], []], []
    wide = 2 * UNIT
    for index, refs in enumerate(pieces):
        at = slice(index * wide, (index + 1) * wide)
        if len(refs) > 1:
            column = 0
            for ref in refs[:-1]:
                for source in [ref] if len(ref.shape) == 2 else [ref.at[c] for c in range(ref.shape[0])]:
                    low = (column * len(pieces) + index) * wide
                    groups[column].append(copy_of(source, wbuf.at[:, low : low + wide], wsem.at[column, index, 0]))
                    column += 1
            outs.append(copy_of(refs[-1], obuf.at[at, :], osem.at[index, 0]))
            continue
        rest, = refs
        rows = rest.shape[2]
        part = wide // 4
        for quarter in range(4):
            place = quarter ^ order
            for column in range(3):
                low = (column * len(pieces) + index) * wide
                groups[column].append(
                    copy_of(
                        rest.at[quarter, column],
                        wbuf.at[pl.ds(pl.multiple_of(place * rows, rows), rows), low : low + wide],
                        wsem.at[column, index, quarter],
                    )
                )
            for block in range(4):
                outs.append(
                    copy_of(
                        rest.at[quarter, 3, block * part : (block + 1) * part, :],
                        obuf.at[pl.ds(pl.multiple_of(index * wide + place * part, part), part), block * wide : (block + 1) * wide],
                        osem.at[index, 4 * quarter + block],
                    )
                )
    return groups, outs


def attention_fwd_call(scalars, residual, others, pieces, partial, norm):
    rows, depth = others[0].shape
    causal = len(others) == 1
    number, wide = 2 * len(pieces), 2 * len(pieces) * UNIT
    last, has_partial = norm is not None, partial is not None

    def kernel(*refs):
        it = iter(refs)
        sc = next(it)
        in_refs = [next(it) for _ in others]
        gain_ref, bias_ref = (next(it), next(it)) if last else (None, None)
        old_rows = [next(it) for _ in residual[1:]] if last else []
        res_in = next(it) if last else None
        part_in = next(it) if has_partial else None
        w_refs = [[next(it) for _ in piece] for piece in pieces]
        q_ref, k_ref, v_ref, att_ref, lse_ref = (next(it) for _ in range(5))
        if last:
            low_ref, hat_ref, inv_ref = next(it), next(it), next(it)
        else:
            sum_ref = next(it)
        wbuf, obuf, att_all, diagonal, wsem, osem, lsem = (next(it) for _ in range(7))
        if last:
            acc, old = next(it), next(it)
        length, order = sc[0], sc[1]
        groups, outs = weight_copies(w_refs, order, wbuf, obuf, wsem, osem)
        for copies in groups + [outs]:
            for copy in copies:
                copy.start()
        target = acc if last else sum_ref
        late = []
        if has_partial:
            late.append(copy_of(part_in, target, lsem.at[0]))
        if last:
            late.append(copy_of(res_in, old, lsem.at[1]))
        for copy in late:
            copy.start()
        if causal:
            fill_diagonal(diagonal)
        for c, result in enumerate((q_ref, k_ref, v_ref)):
            for copy in groups[c]:
                copy.wait()
            rows_in = in_refs[0] if causal or c == 0 else in_refs[1]
            proj = dot(rows_in[...], wbuf[:, c * wide : (c + 1) * wide]).astype(BF16)
            if c == 0:
                proj = (proj.astype(F32) * SCORE_SCALE).astype(BF16)
            for index in range(number):
                result[index] = proj[:, index * UNIT : (index + 1) * UNIT]

        def step(u, carry):
            attended = attend_unit(q_ref[u], k_ref[u], v_ref[u], length, causal, diagonal, lse_ref.at[u])
            att_ref[u] = attended
            att_all[:, pl.ds(pl.multiple_of(u * UNIT, UNIT), UNIT)] = attended
            return carry

        lax.fori_loop(0, number, step, 0)
        for copy in outs + late:
            copy.wait()
        if has_partial:
            target[...] += dot(att_all[...], obuf[...])
        else:
            target[...] = dot(att_all[...], obuf[...])
        if last:
            def chunk(at):
                before = old[at, :].astype(F32)
                if old_rows:
                    before = before * old_rows[0][...] + old_rows[1][...]
                normed, hat, inverse = norm_chunk(RESIDUAL_ALPHA * before + acc[at, :], gain_ref[...], bias_ref[...])
                low_ref[at, :] = normed.astype(BF16)
                hat_ref[at, :] = hat
                inv_ref[at, :] = jnp.broadcast_to(inverse, (ROW_CHUNK, 128))

            each_chunk(rows, chunk)

    unit_rows = sds((number, rows, UNIT), BF16)
    shapes = [unit_rows] * 4 + [sds((number, 2, rows), F32)]
    if last:
        shapes += [sds((rows, depth), BF16), sds((rows, depth), F32), sds((rows, 128), F32)]
    else:
        shapes += [sds((rows, depth), F32)]
    args = [scalars, *others]
    if last:
        args += [*norm, *residual[1:]]
    tail = ([residual[0]] if last else []) + ([partial] if has_partial else [])
    tail += [array for piece in pieces for array in piece]
    scratch = [
        pltpu.VMEM((depth, 3 * wide), BF16),
        pltpu.VMEM((wide, depth), BF16),
        pltpu.VMEM((rows, wide), BF16),
        pltpu.VMEM((QUERY_BLOCK, QUERY_BLOCK), F32),
        pltpu.SemaphoreType.DMA((3, len(pieces), 4)),
        pltpu.SemaphoreType.DMA((len(pieces), 16)),
        pltpu.SemaphoreType.DMA((2,)),
    ]
    if last:
        scratch += [pltpu.VMEM((rows, depth), F32), pltpu.VMEM((rows, depth), residual[0].dtype)]
    return pl.pallas_call(
        kernel,
        out_shape=shapes,
        in_specs=[SMEM] + [VMEM] * (len(args) - 1) + [ANY] * len(tail),
        out_specs=[VMEM] * len(shapes),
        scratch_shapes=scratch,
        compiler_params=params(),
        cost_estimate=cost_of(2.7 * number),
        name="self_fwd" if causal else "cross_fwd",
    )(*args, *tail)


def attention_bwd_call(scalars, grad_low, others, pieces, saved, plan, carried, norm, results=1):
    rows, depth = grad_low.shape
    causal = len(others) == 1
    number, n_in, wide = len(plan), len(others), len(plan) * UNIT
    last = norm is not None

    def kernel(*refs):
        it = iter(refs)
        sc = next(it)
        h_ref = next(it)
        in_refs = [next(it) for _ in range(n_in)]
        gain_ref = next(it) if last else None
        late_in = [next(it), next(it)] if last else []
        acc_in = [next(it) for _ in carried]
        w_refs = [[next(it) for _ in piece] for piece in pieces]
        s_refs = [[next(it) for _ in call] for call in saved]
        sums = [None if last and not index else next(it) for index in range(n_in)]
        if last:
            low_ref, scaled_ref, gsum_ref, bsum_ref = (next(it) for _ in range(4))
        g_refs = [next(it) for _ in range(results)]
        wbuf, obuf, sbuf, lbuf, att_all, grad_all, h_t = (next(it) for _ in range(7))
        in_t = [next(it) for _ in range(n_in)]
        dall, stage, diagonal = next(it), next(it), next(it)
        if last:
            acc, hat, inv = next(it), next(it), next(it)
            sums[0] = acc
        wsem, osem, ssem, gsem, lsem = (next(it) for _ in range(5))
        length, order, dp = sc[0], sc[1], sc[2]

        groups, o_copies = weight_copies(w_refs, order, wbuf, obuf, wsem, osem)
        for copy in o_copies:
            copy.start()
        s_copies = []
        for index, unit in enumerate(plan):
            lanes = slice(index * UNIT, (index + 1) * UNIT)
            call = s_refs[unit[0]]
            for c in range(3):
                s_copies.append(copy_of(call[c].at[unit[1]], sbuf.at[index, c], ssem.at[c, index]))
            s_copies.append(copy_of(call[3].at[unit[1]], att_all.at[:, lanes], ssem.at[3, index]))
            s_copies.append(copy_of(call[4].at[unit[1]], lbuf.at[index], ssem.at[4, index]))
        w_copies = groups[0] + groups[1] + groups[2]
        late = [copy_of(source, sums[index], lsem.at[index]) for index, source in enumerate(acc_in)]
        if last:
            late += [copy_of(late_in[0], hat, lsem.at[2]), copy_of(late_in[1], inv, lsem.at[3])]
        for copy in s_copies + w_copies + late:
            copy.start()
        if causal:
            fill_diagonal(diagonal)
        transpose_shards(h_ref, h_t, dp)
        for ref, target in zip(in_refs, in_t):
            transpose_shards(ref, target, dp)
        for copy in o_copies:
            copy.wait()
        grad_att = dot_nt(h_ref[...], obuf[...]).astype(BF16)
        for index in range(number):
            grad_all[index] = grad_att[:, index * UNIT : (index + 1) * UNIT]
        for copy in s_copies:
            copy.wait()

        def step(u, carry):
            at = pl.ds(pl.multiple_of(u * UNIT, UNIT), UNIT)
            parts = attend_back_unit(
                sbuf[u, 0], sbuf[u, 1], sbuf[u, 2], att_all[:, at], grad_all[u], length, causal, diagonal, lbuf.at[u]
            )
            for c in range(3):
                dall[:, pl.ds(pl.multiple_of(c * wide + u * UNIT, UNIT), UNIT)] = parts[c]
            return carry

        lax.fori_loop(0, number, step, 0)

        share = number // 2 // results

        def keep(weight, column):
            for index in range(number):
                part = weight[:, index * UNIT : (index + 1) * UNIT].astype(BF16)
                piece = index // 2
                stage[piece // share, (index % 2) * 4 + column, piece % share] = part.reshape(8, UNIT, UNIT)

        for c in range(3):
            rows_t = in_t[0] if causal or c == 0 else in_t[1]
            keep(dot(rows_t[...], dall[:, c * wide : (c + 1) * wide]), c)
        keep(dot(h_t[...], att_all[...]), 3)
        g_copies = [copy_of(stage.at[index], ref, gsem.at[index]) for index, ref in enumerate(g_refs)]
        for copy in g_copies:
            copy.start()
        for copy in w_copies + late[: len(acc_in)]:
            copy.wait()
        if causal:
            sums[0][...] += dot_nt(dall[...], wbuf[...])
        else:
            sums[0][...] += dot_nt(dall[:, :wide], wbuf[:, :wide])
            memory_sum = dot_nt(dall[:, wide:], wbuf[:, wide:])
            sums[1][...] = memory_sum + sums[1][...] if len(acc_in) == n_in else memory_sum
        if last:
            for copy in late[len(acc_in) :]:
                copy.wait()
            norm_back_rows(acc, hat, inv, gain_ref, low_ref, scaled_ref, gsum_ref, bsum_ref, rows)
        for copy in g_copies:
            copy.wait()

    big = sds((rows, depth), F32)
    shapes = [big] * (n_in - 1 if last else n_in)
    if last:
        shapes += [sds((rows, depth), BF16), big, sds((8, depth), F32), sds((8, depth), F32)]
    specs_out = [VMEM] * len(shapes) + [ANY] * results
    shapes += [sds((8, number // 2 // results, 8, UNIT, UNIT), BF16)] * results
    args = [scalars, grad_low, *others] + ([norm[2]] if last else [])
    tail = ([norm[0], norm[1]] if last else []) + list(carried)
    tail += [array for piece in pieces for array in piece]
    for call in saved:
        tail += call
    scratch = [
        pltpu.VMEM((depth, 3 * wide), BF16),
        pltpu.VMEM((wide, depth), BF16),
        pltpu.VMEM((number, 3, rows, UNIT), BF16),
        pltpu.VMEM((number, 2, rows), F32),
        pltpu.VMEM((rows, wide), BF16),
        pltpu.VMEM((number, rows, UNIT), BF16),
        pltpu.VMEM((depth, rows), BF16),
    ]
    scratch += [pltpu.VMEM((depth, rows), BF16)] * n_in
    scratch += [
        pltpu.VMEM((rows, 3 * wide), BF16),
        pltpu.VMEM((results, 8, number // 2 // results, 8, UNIT, UNIT), BF16),
        pltpu.VMEM((QUERY_BLOCK, QUERY_BLOCK), F32),
    ]
    if last:
        scratch += [pltpu.VMEM((rows, depth), F32), pltpu.VMEM((rows, depth), F32), pltpu.VMEM((rows, 128), F32)]
    scratch += [
        pltpu.SemaphoreType.DMA((3, len(pieces), 4)),
        pltpu.SemaphoreType.DMA((len(pieces), 16)),
        pltpu.SemaphoreType.DMA((5, number)),
        pltpu.SemaphoreType.DMA((results,)),
        pltpu.SemaphoreType.DMA((4,)),
    ]
    return pl.pallas_call(
        kernel,
        out_shape=shapes,
        in_specs=[SMEM] + [VMEM] * (len(args) - 1) + [ANY] * len(tail),
        out_specs=specs_out,
        scratch_shapes=scratch,
        compiler_params=params(),
        cost_estimate=cost_of(4.5 * number),
        name="self_bwd" if causal else "cross_bwd",
    )(*args, *tail)


def norm_back_rows(acc, hat, inv, gain_ref, low_ref, scaled_ref, gsum_ref, bsum_ref, rows):
    gsum_ref[...] = jnp.zeros_like(gsum_ref)
    bsum_ref[...] = jnp.zeros_like(bsum_ref)

    def chunk(at):
        gradient, normed = acc[at, :], hat[at, :]
        grad_in = norm_back_chunk(gradient, normed, inv[at, :1], gain_ref[...])
        low_ref[at, :] = grad_in.astype(BF16)
        scaled_ref[at, :] = RESIDUAL_ALPHA * grad_in
        gsum_ref[...] += fold_rows(gradient * normed)
        bsum_ref[...] += fold_rows(gradient)

    each_chunk(rows, chunk)


GELU_SCALE = 0.7978845608028654
GELU_CUBE = 0.044715


def gelu_and_slope(pre):
    square = pre * pre
    inner = pre * (GELU_SCALE + (GELU_SCALE * GELU_CUBE) * square)
    curve = jnp.tanh(inner)
    half = 0.5 + 0.5 * curve
    slope = half * (1.0 + pre * (1.0 - curve) * (GELU_SCALE + (3.0 * GELU_SCALE * GELU_CUBE) * square))
    return pre * half, slope


FFN_PART = FFN_UNIT // 2


def ffn_copies(pieces, order, ubuf, dbuf, usem, dsem):
    ups, downs = [], []
    for index, refs in enumerate(pieces):
        wide = 2 * FFN_UNIT
        at = slice(index * wide, (index + 1) * wide)
        if len(refs) == 2:
            ups.append([copy_of(refs[0], ubuf.at[:, at], usem.at[index, 0])])
            downs.append([copy_of(refs[1], dbuf.at[at, :], dsem.at[index, 0])])
            continue
        ups.append([])
        downs.append([])
        rows = refs[0].shape[1]
        for quarter in range(4):
            up = refs[quarter].at[0]
            down = refs[quarter].at[1] if quarter < 3 else refs[4].at[0]
            place = (quarter ^ order) * rows
            ups[-1].append(copy_of(up, ubuf.at[pl.ds(pl.multiple_of(place, rows), rows), at], usem.at[index, quarter]))
            downs[-1].append(
                copy_of(down, dbuf.at[pl.ds(pl.multiple_of(index * wide + place, rows), rows), :], dsem.at[index, quarter])
            )
    return ups, downs


def ffn_fwd_call(scalars, inputs, pieces, partial, final):
    rows, depth = inputs.shape
    number = 2 * len(pieces)
    last, has_partial = final is not None, partial is not None

    def kernel(*refs):
        it = iter(refs)
        sc, x_ref = next(it), next(it)
        if last:
            gain_old, bias_old, gain_ref, bias_ref = (next(it) for _ in range(4))
            late_in = [next(it), next(it)]
        part_in = next(it) if has_partial else None
        w_refs = [[next(it) for _ in piece] for piece in pieces]
        if last:
            out_ref, low_ref, scaled_ref, gsum_ref, bsum_ref = (next(it) for _ in range(5))
        else:
            sum_ref = next(it)
        act_ref, slope_ref = next(it), next(it)
        ubuf, dbuf, abuf, sbuf, pbuf, psem = (next(it) for _ in range(6))
        if last:
            acc, hat, cot, lsem = (next(it) for _ in range(4))
        wsem, gsem = next(it), next(it)
        target = acc if last else sum_ref

        up_copies, down_copies = ffn_copies(w_refs, sc[1], ubuf, dbuf, wsem.at[0], wsem.at[1])
        for copies in up_copies + down_copies:
            for copy in copies:
                copy.start()
        if has_partial:
            part_copy = copy_of(part_in, target, psem)
            part_copy.start()
        if last:
            late = [copy_of(late_in[0], hat, lsem.at[0]), copy_of(late_in[1], cot, lsem.at[1])]
            for copy in late:
                copy.start()
        saves = []

        def gate(pre, index):
            activated, slope = gelu_and_slope(pre)
            abuf[:, index * FFN_UNIT : (index + 1) * FFN_UNIT] = activated.astype(BF16)
            sbuf[:, index * FFN_UNIT : (index + 1) * FFN_UNIT] = slope.astype(BF16)

        for index in range(number):
            if index % 2 == 0:
                for copy in up_copies[index // 2]:
                    copy.wait()
            if index:
                gate(pbuf[(index - 1) % 2], index - 1)
            pbuf[index % 2] = dot(x_ref[...], ubuf[:, index * FFN_UNIT : (index + 1) * FFN_UNIT])
        gate(pbuf[(number - 1) % 2], number - 1)
        for index in range(number):
            at = slice(index * FFN_UNIT, (index + 1) * FFN_UNIT)
            saves += [
                copy_of(abuf.at[:, at], act_ref.at[index], gsem.at[0, index]),
                copy_of(sbuf.at[:, at], slope_ref.at[index], gsem.at[1, index]),
            ]
        for copy in saves:
            copy.start()
        for copies in down_copies:
            for copy in copies:
                copy.wait()
        if has_partial:
            part_copy.wait()
            target[...] += dot(abuf[...], dbuf[...])
        else:
            target[...] = dot(abuf[...], dbuf[...])
        if last:
            for copy in late:
                copy.wait()
            gsum_ref[...] = jnp.zeros_like(gsum_ref)
            bsum_ref[...] = jnp.zeros_like(bsum_ref)

            def chunk(at):
                old = hat[at, :] * gain_old[...] + bias_old[...]
                normed, xhat, inverse = norm_chunk(RESIDUAL_ALPHA * old + acc[at, :], gain_ref[...], bias_ref[...])
                out_ref[at, :] = normed.astype(BF16)
                gradient = cot[at, :].astype(F32)
                grad_in = norm_back_chunk(gradient, xhat, inverse, gain_ref[...])
                low_ref[at, :] = grad_in.astype(BF16)
                scaled_ref[at, :] = RESIDUAL_ALPHA * grad_in
                gsum_ref[...] += fold_rows(gradient * xhat)
                bsum_ref[...] += fold_rows(gradient)

            each_chunk(rows, chunk)
        for copy in saves:
            copy.wait()

    big, low = sds((rows, depth), F32), sds((rows, depth), BF16)
    if last:
        shapes = [low, low, big, sds((8, depth), F32), sds((8, depth), F32)]
    else:
        shapes = [big]
    specs_out = [VMEM] * len(shapes) + [ANY, ANY]
    shapes += [sds((number, rows, FFN_UNIT), BF16)] * 2
    args = [scalars, inputs]
    if last:
        args += [final[1], final[2], final[4], final[5]]
    specs = [SMEM] + [VMEM] * (len(args) - 1)
    tail = ([final[0], final[3]] if last else []) + ([partial] if has_partial else []) + [array for piece in pieces for array in piece]
    scratch = [
        pltpu.VMEM((depth, number * FFN_UNIT), BF16),
        pltpu.VMEM((number * FFN_UNIT, depth), BF16),
        pltpu.VMEM((rows, number * FFN_UNIT), BF16),
        pltpu.VMEM((rows, number * FFN_UNIT), BF16),
        pltpu.VMEM((2, rows, FFN_UNIT), F32),
        pltpu.SemaphoreType.DMA,
    ]
    if last:
        scratch += [
            pltpu.VMEM((rows, depth), F32),
            pltpu.VMEM((rows, depth), F32),
            pltpu.VMEM((rows, depth), BF16),
            pltpu.SemaphoreType.DMA((2,)),
        ]
    scratch += [pltpu.SemaphoreType.DMA((2, len(pieces), 4)), pltpu.SemaphoreType.DMA((2, number))]
    return pl.pallas_call(
        kernel,
        out_shape=shapes,
        in_specs=specs + [ANY] * len(tail),
        out_specs=specs_out,
        scratch_shapes=scratch,
        compiler_params=params(),
        cost_estimate=cost_of(12),
        name="ffn_fwd",
    )(*args, *tail)


def ffn_bwd_call(scalars, grad_low, inputs, pieces, saved, plan, carried, norm):
    rows, depth = inputs.shape
    number = len(plan)
    last = norm is not None

    def kernel(*refs):
        it = iter(refs)
        sc, g_in, x_ref = (next(it) for _ in range(3))
        gain_ref = next(it) if last else None
        late_in = [next(it), next(it)] if last else []
        acc_in = next(it)
        w_refs = [[next(it) for _ in piece] for piece in pieces]
        s_refs = [[next(it) for _ in call] for call in saved]
        if last:
            low_ref, scaled_ref, gsum_ref, bsum_ref = (next(it) for _ in range(4))
        else:
            sum_ref = next(it)
        g_ref = next(it)
        ubuf, dbuf, abuf, sbuf, gbuf, x_t, g_t, stage, psem = (next(it) for _ in range(9))
        if last:
            acc, hat, inv, lsem = (next(it) for _ in range(4))
        wsem, ssem, gsem = next(it), next(it), next(it)
        order, dp = sc[1], sc[2]
        target = acc if last else sum_ref

        ups, downs = ffn_copies(w_refs, order, ubuf, dbuf, wsem.at[0], wsem.at[1])
        slopes, acts = [], []
        for index, (call, at) in enumerate(plan):
            lanes = slice(index * FFN_UNIT, (index + 1) * FFN_UNIT)
            slopes.append(copy_of(s_refs[call][1].at[at], sbuf.at[index], ssem.at[0, index]))
            acts.append(copy_of(s_refs[call][0].at[at], abuf.at[:, lanes], ssem.at[1, index]))
        for copies in downs + [slopes, acts] + ups:
            for copy in copies:
                copy.start()
        part_copy = copy_of(acc_in, target, psem)
        part_copy.start()
        if last:
            late = [copy_of(late_in[0], hat, lsem.at[0]), copy_of(late_in[1], inv, lsem.at[1])]
            for copy in late:
                copy.start()
        transpose_shards(g_in, g_t, dp)
        transpose_shards(x_ref, x_t, dp)
        for index in range(number):
            if index % 2 == 0:
                for copy in downs[index // 2]:
                    copy.wait()
            slopes[index].wait()
            grad_act = dot_nt(g_in[...], dbuf[index * FFN_UNIT : (index + 1) * FFN_UNIT, :]) * sbuf[index].astype(F32)
            gbuf[:, index * FFN_UNIT : (index + 1) * FFN_UNIT] = grad_act.astype(BF16)
        for copy in acts:
            copy.wait()

        def keep(rows_t, source, column):
            for half in range(number // 2):
                wide = 2 * FFN_UNIT
                weight = dot(rows_t[...], source[:, half * wide : (half + 1) * wide]).astype(BF16)
                for inner in range(4):
                    part = weight[:, inner * FFN_PART : (inner + 1) * FFN_PART]
                    stage[2 * inner + column, half] = part.reshape(8, UNIT, FFN_PART)

        keep(x_t, gbuf, 0)
        keep(g_t, abuf, 1)
        g_copies = [copy_of(stage, g_ref, gsem)]
        for copy in g_copies:
            copy.start()
        for copies in ups:
            for copy in copies:
                copy.wait()
        part_copy.wait()
        target[...] += dot_nt(gbuf[...], ubuf[...])
        if last:
            for copy in late:
                copy.wait()
            norm_back_rows(acc, hat, inv, gain_ref, low_ref, scaled_ref, gsum_ref, bsum_ref, rows)
        for copy in g_copies:
            copy.wait()

    big, low = sds((rows, depth), F32), sds((rows, depth), BF16)
    shapes = [low, big, sds((8, depth), F32), sds((8, depth), F32)] if last else [big]
    specs_out = [VMEM] * len(shapes) + [ANY]
    shapes.append(sds((8, number // 2, 8, UNIT, FFN_PART), BF16))
    args = [scalars, grad_low, inputs] + ([norm[2]] if last else [])
    specs = [SMEM] + [VMEM] * (len(args) - 1)
    tail = ([norm[0], norm[1]] if last else []) + [carried] + [array for piece in pieces for array in piece]
    for call in saved:
        tail += call
    scratch = [
        pltpu.VMEM((depth, number * FFN_UNIT), BF16),
        pltpu.VMEM((number * FFN_UNIT, depth), BF16),
        pltpu.VMEM((rows, number * FFN_UNIT), BF16),
        pltpu.VMEM((number, rows, FFN_UNIT), BF16),
        pltpu.VMEM((rows, number * FFN_UNIT), BF16),
        pltpu.VMEM((depth, rows), BF16),
        pltpu.VMEM((depth, rows), BF16),
        pltpu.VMEM((8, number // 2, 8, UNIT, FFN_PART), BF16),
        pltpu.SemaphoreType.DMA,
    ]
    if last:
        scratch += [
            pltpu.VMEM((rows, depth), F32),
            pltpu.VMEM((rows, depth), F32),
            pltpu.VMEM((rows, 128), F32),
            pltpu.SemaphoreType.DMA((2,)),
        ]
    scratch += [pltpu.SemaphoreType.DMA((2, len(pieces), 4)), pltpu.SemaphoreType.DMA((2, number)), pltpu.SemaphoreType.DMA]
    return pl.pallas_call(
        kernel,
        out_shape=shapes,
        in_specs=specs + [ANY] * len(tail),
        out_specs=specs_out,
        scratch_shapes=scratch,
        compiler_params=params(),
        cost_estimate=cost_of(17),
        name="ffn_bwd",
    )(*args, *tail)


def combine(jobs, shapes):
    arrays = []
    for terms, _, _ in jobs:
        for array, _ in terms:
            if not any(array is known for known in arrays):
                arrays.append(array)
    position = {id(array): index for index, array in enumerate(arrays)}

    def part_shape(array, index):
        kept = []
        for extent, at in zip(array.shape, index + (slice(None),) * (array.ndim - len(index))):
            if isinstance(at, slice):
                kept.append(len(range(*at.indices(extent))))
        return tuple(kept)

    part_shapes = [part_shape(*terms[0]) for terms, _, _ in jobs]
    count = sum(len(terms) for terms, _, _ in jobs)

    def kernel(*refs):
        ins, outs = refs[: len(arrays)], refs[len(arrays) : len(arrays) + len(shapes)]
        rest = refs[len(arrays) + len(shapes) :]
        term_bufs, sum_bufs, isem, osem = rest[:count], rest[count : count + len(jobs)], rest[-2], rest[-1]
        loads, number = [], 0
        for terms, _, _ in jobs:
            loads.append([])
            for array, index in terms:
                loads[-1].append(copy_of(ins[position[id(array)]].at[index], term_bufs[number], isem.at[number]))
                number += 1
        for group in loads:
            for copy in group:
                copy.start()
        stores, number = [], 0
        for job, (terms, out, place) in enumerate(jobs):
            for copy in loads[job]:
                copy.wait()
            bufs = term_bufs[number : number + len(terms)]
            number += len(terms)
            lead = part_shapes[job][:-2]
            size = 1
            for extent in lead:
                size *= extent

            def one(flat, carry, bufs=bufs, lead=lead, target=sum_bufs[job]):
                index, left = [], flat
                for extent in reversed(lead):
                    index.append(lax.rem(left, extent))
                    left = lax.div(left, extent)
                index = tuple(reversed(index))
                total = bufs[0][index].astype(F32)
                for buf in bufs[1:]:
                    total = total + buf[index].astype(F32)
                target[index] = total.astype(target.dtype)
                return carry

            lax.fori_loop(0, size, one, 0)
            stores.append(copy_of(sum_bufs[job], outs[out].at[place], osem.at[job]))
            stores[-1].start()
        for copy in stores:
            copy.wait()

    scratch = [pltpu.VMEM(part_shapes[job], array.dtype) for job, (terms, _, _) in enumerate(jobs) for array, _ in terms]
    scratch += [pltpu.VMEM(part_shapes[job], shapes[out].dtype) for job, (_, out, _) in enumerate(jobs)]
    scratch += [pltpu.SemaphoreType.DMA((count,)), pltpu.SemaphoreType.DMA((len(jobs),))]
    return pl.pallas_call(
        kernel,
        out_shape=list(shapes),
        in_specs=[ANY] * len(arrays),
        out_specs=[ANY] * len(shapes),
        scratch_shapes=scratch,
        compiler_params=params(),
        cost_estimate=cost_of(3),
        name="combine",
    )(*arrays)


def swap_pairs(count, mask):
    return [(i, i ^ mask) for i in range(count)]


def to_sibling(values):
    return lax.ppermute(values, "tensor", swap_pairs(4, 1))


def over_y(values):
    return lax.ppermute(values, "tensor", swap_pairs(4, 2))


def over_dp(values, mask):
    return lax.ppermute(values, "dp", swap_pairs(8, mask))


def over_x(values):
    return over_dp(values, 1)


def over_z_near(values):
    return over_dp(values, 2)


def over_z_far(values):
    return over_dp(values, 4)


def after(values, *earlier):
    return lax.optimization_barrier((values, *earlier))[0]


MOVES = {"y": over_y, "x": over_x, "z": over_z_near}


class Reduction:
    def __init__(self, sent, portions):
        self.other = to_sibling(sent)
        self.portions, self.stage, self.sends, self.total = portions, 0, None, None

    def begin(self, kept, *earlier):
        other = after(self.other, *earlier)
        split = (kept.shape[0], 2, 2, 2, 2, *kept.shape[3:])
        arrays = (kept.reshape(split), other.reshape(split))
        self.blocks, self.tail = kept.shape[0], kept.shape[3:]
        self.terms = [[(array, ("b", "y", "x", "z", "w"), low, {}) for array in arrays] for low, _, _ in self.portions]

    def receive(self, *earlier):
        if self.stage == 4:
            moved = after(over_z_far(self.sends[0]), *earlier)
            for (low, _, _), terms in zip(self.portions, self.terms):
                terms.append((moved, ("b",), low, {}))
        elif self.stage:
            for send, (_, _, orders), terms in zip(self.sends, self.portions, self.terms):
                left = tuple(a for a in ("b", "y", "x", "z", "w") if a not in orders[: self.stage])
                terms.append((after(MOVES[orders[self.stage - 1]](send), *earlier), left, 0, {}))

    def jobs(self, first_out):
        jobs, shapes = [], []
        stage = self.stage
        for number, ((low, high, orders), terms) in enumerate(zip(self.portions, self.terms)):
            axis = (*orders, "w", None)[stage]
            picked = []
            for array, axes, start, fixed in terms:
                index = [slice(start, start + high - low)]
                for name in axes[1:]:
                    index.append(1 if name == axis else fixed.get(name, 0 if name in orders[:stage] or (stage > 3 and name == "w") else slice(None)))
                picked.append((array, tuple(index)))
            if stage < 3:
                left = 3 - stage + 1 - 1
                shapes.append(sds((high - low, *(2,) * left, *self.tail), BF16))
                jobs.append((picked, first_out + number, slice(0, high - low)))
            else:
                if not number:
                    shapes.append(sds((self.blocks, *self.tail), BF16 if stage == 3 else F32))
                jobs.append((picked, first_out, slice(low, high)))
        self.stage += 1
        return jobs, shapes


def advance(reductions, *earlier):
    jobs, shapes, bounds = [], [], []
    for reduction in reductions:
        reduction.receive(*earlier)
        more, made = reduction.jobs(len(shapes))
        bounds.append((len(shapes), len(shapes) + len(made)))
        jobs, shapes = jobs + more, shapes + made
    results = combine(jobs, shapes)
    for reduction, (low, high) in zip(reductions, bounds):
        reduction.sends = list(results[low:high])
        if reduction.stage == 5:
            reduction.total = results[low]
    return list(results)


def sentence_body(
    tokens,
    memory,
    dec_lengths,
    mem_lengths,
    self_qkv,
    self_out,
    cross_q,
    cross_kv,
    cross_out,
    ffn_in,
    ffn_out,
    norm_gains,
    norm_biases,
    cotangent,
):
    dp = lax.axis_index("dp")
    mine = lax.axis_index("tensor")
    order = dp & 3
    self_scalars = jnp.stack([dec_lengths[0, mine], order, dp, mine]).astype(jnp.int32)
    cross_scalars = jnp.stack([mem_lengths[0, mine], order, dp, mine]).astype(jnp.int32)
    gains = [norm_gains[i : i + 1] for i in range(3)]
    biases = [norm_biases[i : i + 1] for i in range(3)]

    def quarter_rows(values):
        rows = values.shape[-2] // 4
        return lax.dynamic_slice_in_dim(values, order * rows, rows, values.ndim - 2)

    def folded(values):
        blocks = values.reshape(values.shape[0], 4, 2 * UNIT)
        return blocks.transpose(1, 0, 2).reshape(1, 4 * values.shape[0], 2 * UNIT)

    self_near = over_y(jnp.concatenate([quarter_rows(self_qkv), folded(quarter_rows(self_out))]))
    cross_near = over_y(
        jnp.concatenate([quarter_rows(cross_q)[None], quarter_rows(cross_kv), folded(quarter_rows(cross_out))])
    )
    ffn_near = over_y(jnp.stack([quarter_rows(ffn_in), quarter_rows(ffn_out)]))
    self_own = (self_qkv, self_out)
    self_sib = tuple(to_sibling(w) for w in self_own)
    self_side, self_up = over_x(self_near), over_z_near(self_near)
    self_a = attention_fwd_call(after(self_scalars, self_near), [], [tokens], [self_own, self_sib], None, None)
    self_side, self_up, cross_near = (after(w, self_a[4]) for w in (self_side, self_up, cross_near))
    self_corner = over_x(self_up)
    cross_side, cross_up = over_x(cross_near), over_z_near(cross_near)
    self_rest = jnp.stack([self_near, self_side, self_up, self_corner])
    self_far = to_sibling(self_rest)
    self_pieces = [self_own, self_sib, (self_rest,), (self_far,)]
    self_b = attention_fwd_call(
        after(self_scalars, cross_near, ffn_near), [tokens], [tokens], self_pieces[2:], self_a[5], (gains[0], biases[0])
    )
    first_low, first_hat, first_inv = self_b[5:]
    cross_own = (cross_q, cross_kv, cross_out)
    cross_sib = tuple(to_sibling(after(w, self_near)) for w in cross_own)
    ffn_own = (ffn_in, ffn_out)
    ffn_sib = tuple(to_sibling(after(w, self_near)) for w in ffn_own)
    cross_in = [first_low, memory]
    cross_corner = over_x(cross_up)
    cross_rest = jnp.stack([cross_near, cross_side, cross_up, cross_corner])
    cross_far = to_sibling(cross_rest)
    ffn_side, ffn_up = over_x(ffn_near), over_z_near(ffn_near)
    cross_pieces = [cross_own, cross_sib, (cross_rest,), (cross_far,)]
    cross_b = attention_fwd_call(
        cross_scalars, [first_hat, gains[0], biases[0]], cross_in, cross_pieces, None, (gains[1], biases[1])
    )
    second_low, second_hat, second_inv = cross_b[5:]
    ffn_side, ffn_up = after(ffn_side, cross_b[4]), after(ffn_up, cross_b[4])
    up_corner, down_corner = over_x(ffn_up[:1]), over_z_near(ffn_side[1:])
    ffn_pieces = [ffn_own, ffn_sib]
    ffn_a = ffn_fwd_call(cross_scalars, second_low, ffn_pieces, None, None)
    up_corner, down_corner = after(up_corner, ffn_a[0]), after(down_corner, ffn_a[0])
    ffn_rest = (ffn_near, ffn_side, ffn_up, up_corner, down_corner)
    ffn_pieces += [ffn_rest, tuple(to_sibling(w) for w in ffn_rest)]
    ffn_b = ffn_fwd_call(
        cross_scalars, second_low, ffn_pieces[2:], ffn_a[0],
        (second_hat, gains[1], biases[1], cotangent, gains[2], biases[2]),
    )
    out_rows, third_low, third_scaled, third_gain, third_bias = ffn_b[:5]

    def plan_of(pieces):
        return [(piece // 2, 2 * (piece % 2) + half) for piece in pieces for half in (0, 1)]

    ffn_saved = [ffn_a[1:3], ffn_b[5:7]]
    ffn_d = ffn_bwd_call(
        cross_scalars, third_low, second_low, ffn_pieces[1::2], ffn_saved, plan_of((1, 3)), third_scaled, None
    )
    ffn_sum = Reduction(ffn_d[1], [(0, 3, "yxz"), (3, 6, "xzy"), (6, 8, "zyx")])
    ffn_e = ffn_bwd_call(
        cross_scalars, third_low, second_low, ffn_pieces[::2], ffn_saved, plan_of((0, 2)), ffn_d[0],
        (second_hat, second_inv, gains[1]),
    )
    second_back, second_scaled, second_gain, second_bias = ffn_e[:4]
    ffn_sum.begin(ffn_e[4], second_gain)
    second_back = after(second_back, *advance([ffn_sum]))

    cross_e = attention_bwd_call(
        cross_scalars, second_back, cross_in, cross_pieces[1::2] + cross_pieces[::2], [cross_b[:5]],
        [(0, 2 * p + h) for p in (1, 3, 0, 2) for h in (0, 1)], [second_scaled],
        (first_hat, first_inv, gains[0]), 2,
    )
    grad_memory, first_back, first_scaled, first_gain, first_bias = cross_e[:5]
    norm_sums = jnp.stack([first_gain, second_gain, third_gain, first_bias, second_bias, third_bias])
    norm_sums = jnp.concatenate([jnp.sum(norm_sums, axis=1), jnp.zeros((2, norm_sums.shape[2]), F32)])
    norm_total = jnp.sum(lax.all_gather(norm_sums, ("dp", "tensor"), axis=0), axis=0)
    sends = advance([ffn_sum], first_gain)
    cross_sum = Reduction(after(cross_e[5], *sends), [(0, 4, "xzy"), (4, 8, "yxz")])
    first_back = after(first_back, *sends, norm_sums)

    self_saved = [self_a[:5], self_b[:5]]
    self_d = attention_bwd_call(
        self_scalars, first_back, [tokens], self_pieces[1::2], self_saved, plan_of((1, 3)), [first_scaled], None
    )
    cross_sum.begin(cross_e[6], self_d[0])
    sends = advance([cross_sum, ffn_sum], self_d[0])
    self_sum = Reduction(after(self_d[1], *sends), [(0, 4, "xzy"), (4, 8, "yxz")])
    gate = after(self_d[0], *sends)
    self_e = attention_bwd_call(
        self_scalars, first_back, [tokens], self_pieces[::2], self_saved, plan_of((0, 2)), [gate], None
    )
    grad_tokens = self_e[0]
    self_sum.begin(self_e[1], grad_tokens)
    sends = advance([self_sum])
    sends = advance([cross_sum, ffn_sum], *sends)
    sends = advance([self_sum], *sends)
    sends = advance([cross_sum, ffn_sum], *sends)
    sends = advance([self_sum], *sends)
    sends = advance([cross_sum], *sends)
    sends = advance([self_sum], *sends)
    sends = advance([cross_sum], *sends)
    advance([self_sum], *sends)
    self_sum, cross_sum, ffn_sum = self_sum.total, cross_sum.total, ffn_sum.total

    def matrices(total):
        return total.reshape(2, 4, UNIT, UNIT).transpose(1, 2, 0, 3).reshape(4, UNIT, 2 * UNIT)

    self_grads, cross_grads = matrices(self_sum), matrices(cross_sum)
    ffn_grads = ffn_sum.reshape(4, 2, UNIT, FFN_PART).transpose(1, 2, 0, 3).reshape(2, UNIT, -1)
    return (
        out_rows,
        grad_tokens,
        grad_memory,
        self_grads[:3],
        self_grads[3].T,
        cross_grads[0],
        cross_grads[1:3],
        cross_grads[3].T,
        ffn_grads[0],
        ffn_grads[1].T,
        norm_total[:3],
        norm_total[3:6],
    )


def sentence_fits(mesh, tokens, memory, dec_lengths):
    shape = dict(mesh.shape)
    rows = tokens.shape[0] // mesh.size
    sentences = dec_lengths.shape[1]
    return (
        shape["tensor"] == 4
        and shape["dp"] == 8
        and sentences == 4
        and rows == 512
        and memory.shape[0] // mesh.size == rows
        and tokens.shape[1] == 1024
    )


def smooth_gate(values):
    return jax.nn.gelu(values, approximate=True)


def norm_rows(hidden, norm_gain, norm_bias):
    center = hidden - jnp.mean(hidden, axis=-1, keepdims=True)
    inverse = lax.rsqrt(jnp.mean(center * center, axis=-1, keepdims=True) + NORM_EPSILON)
    normed = center * inverse
    return (normed * norm_gain + norm_bias, normed, inverse)


def norm_back(gradient, normed, inverse, norm_gain):
    scaled = gradient * norm_gain
    grad_in = inverse * (
        scaled
        - jnp.mean(scaled, axis=-1, keepdims=True)
        - normed * jnp.mean(scaled * normed, axis=-1, keepdims=True)
    )
    return (grad_in, jnp.sum(gradient * normed, axis=0), jnp.sum(gradient, axis=0))


def head_view(values, sentences):
    return values.reshape(sentences, -1, values.shape[1] // HEAD_DIM, HEAD_DIM)


def masked_scores(query_heads, key_heads, key_mask):
    scores = jnp.einsum(
        "sqhe,skhe->shqk", query_heads, key_heads, preferred_element_type=jnp.float32
    ) * HEAD_DIM ** (-0.5)
    return jnp.where(key_mask, scores, MASKED_SCORE)


def attention_forward(query_rows, key_rows, value_rows, key_mask, sentences):
    scores = masked_scores(
        head_view(query_rows, sentences), head_view(key_rows, sentences), key_mask
    )
    row_peak = jnp.max(scores, axis=-1, keepdims=True)
    exponent_terms = jnp.exp(scores - row_peak)
    row_sum = jnp.sum(exponent_terms, axis=-1, keepdims=True)
    softmax_probs = exponent_terms / row_sum
    attended = jnp.einsum(
        "shqk,skhe->sqhe",
        softmax_probs.astype(jnp.bfloat16),
        head_view(value_rows, sentences),
        preferred_element_type=jnp.float32,
    ).astype(jnp.bfloat16)
    return (attended.reshape(query_rows.shape), row_peak + jnp.log(row_sum))


def attention_backward(query_rows, key_rows, value_rows, key_mask, log_total, grad_rows, sentences):
    query_heads = head_view(query_rows, sentences)
    key_heads = head_view(key_rows, sentences)
    value_heads = head_view(value_rows, sentences)
    grad_heads = head_view(grad_rows, sentences)
    softmax_probs = jnp.exp(masked_scores(query_heads, key_heads, key_mask) - log_total)
    grad_probs = jnp.einsum(
        "sqhe,skhe->shqk", grad_heads, value_heads, preferred_element_type=jnp.float32
    )
    row_delta = jnp.sum(softmax_probs * grad_probs, axis=-1, keepdims=True)
    grad_scores = (softmax_probs * (grad_probs - row_delta)).astype(jnp.bfloat16)
    score_scale = HEAD_DIM ** (-0.5)
    grad_query = (
        jnp.einsum("shqk,skhe->sqhe", grad_scores, key_heads, preferred_element_type=jnp.float32)
        * score_scale
    ).astype(jnp.bfloat16)
    grad_key = (
        jnp.einsum("shqk,sqhe->skhe", grad_scores, query_heads, preferred_element_type=jnp.float32)
        * score_scale
    ).astype(jnp.bfloat16)
    grad_value = jnp.einsum(
        "shqk,sqhe->skhe",
        softmax_probs.astype(jnp.bfloat16),
        grad_heads,
        preferred_element_type=jnp.float32,
    ).astype(jnp.bfloat16)
    return (
        grad_query.reshape(query_rows.shape),
        grad_key.reshape(key_rows.shape),
        grad_value.reshape(value_rows.shape),
    )


def body(
    tokens,
    memory,
    dec_lengths,
    mem_lengths,
    self_qkv,
    self_out,
    cross_q,
    cross_kv,
    cross_out,
    ffn_in,
    ffn_out,
    norm_gains,
    norm_biases,
    cotangent,
):
    row_share = tokens.shape[0]
    sentences = dec_lengths.shape[1]
    all_tokens, all_memory = (
        lax.all_gather(tokens, "tensor", axis=0, tiled=True),
        lax.all_gather(memory, "tensor", axis=0, tiled=True),
    )
    sentence_len = all_tokens.shape[0] // sentences
    memory_len = all_memory.shape[0] // sentences
    positions = jnp.arange(sentence_len, dtype=jnp.int32)
    self_mask = (
        (positions[None, :] <= positions[:, None])[None]
        & (positions[None, None, :] < dec_lengths[0][:, None, None])
    )[:, None]
    memory_positions = jnp.arange(memory_len, dtype=jnp.int32)
    cross_mask = (memory_positions[None, :] < mem_lengths[0][:, None])[:, None, None, :]

    def branch_rows(attended, weight):
        return lax.psum_scatter(
            jnp.dot(attended, weight, preferred_element_type=jnp.float32).astype(jnp.bfloat16),
            "tensor",
            scatter_dimension=0,
            tiled=True,
        ).astype(jnp.float32)

    def branch_grad(grad_rows, attended, weight):
        grad_low = grad_rows.astype(jnp.bfloat16)
        grad_all = lax.all_gather(grad_low, "tensor", axis=0, tiled=True)
        grad_attended = jnp.dot(grad_all, weight.T, preferred_element_type=jnp.float32).astype(
            jnp.bfloat16
        )
        weight_part = jnp.dot(attended.T, grad_all, preferred_element_type=jnp.float32)
        return (grad_attended, weight_part)

    def gather_normed(values):
        return lax.all_gather(values, "tensor", axis=0, tiled=True)

    def head_input_sum(term):
        return lax.psum_scatter(
            term(jnp.int32(0), row_share * lax.axis_size("tensor")).astype(jnp.bfloat16),
            "tensor",
            scatter_dimension=0,
            tiled=True,
        ).astype(jnp.float32)

    self_proj = jnp.einsum(
        "td,cde->cte", all_tokens, self_qkv, preferred_element_type=jnp.float32
    ).astype(jnp.bfloat16)
    self_att, self_lse = attention_forward(
        self_proj[0], self_proj[1], self_proj[2], self_mask, sentences
    )
    self_branch = branch_rows(self_att, self_out)
    first_norm, first_hat, first_inv = norm_rows(
        RESIDUAL_ALPHA * tokens.astype(jnp.float32) + self_branch, norm_gains[0], norm_biases[0]
    )
    first_all = gather_normed(first_norm.astype(jnp.bfloat16))
    cross_query = jnp.dot(first_all, cross_q, preferred_element_type=jnp.float32).astype(
        jnp.bfloat16
    )
    cross_proj = jnp.einsum(
        "td,cde->cte", all_memory, cross_kv, preferred_element_type=jnp.float32
    ).astype(jnp.bfloat16)
    cross_att, cross_lse = attention_forward(
        cross_query, cross_proj[0], cross_proj[1], cross_mask, sentences
    )
    cross_branch = branch_rows(cross_att, cross_out)
    second_norm, second_hat, second_inv = norm_rows(
        RESIDUAL_ALPHA * first_norm + cross_branch, norm_gains[1], norm_biases[1]
    )
    second_all = gather_normed(second_norm.astype(jnp.bfloat16))
    pre_gate = jnp.dot(second_all, ffn_in, preferred_element_type=jnp.float32)
    activated = smooth_gate(pre_gate).astype(jnp.bfloat16)
    ffn_branch = lax.psum_scatter(
        jnp.dot(activated, ffn_out, preferred_element_type=jnp.float32).astype(jnp.bfloat16),
        "tensor",
        scatter_dimension=0,
        tiled=True,
    ).astype(jnp.float32)
    out_rows, third_hat, third_inv = norm_rows(
        RESIDUAL_ALPHA * second_norm + ffn_branch, norm_gains[2], norm_biases[2]
    )
    grad_third, third_gain, third_bias = norm_back(
        cotangent.astype(jnp.float32), third_hat, third_inv, norm_gains[2]
    )
    grad_ffn_all = lax.all_gather(grad_third.astype(jnp.bfloat16), "tensor", axis=0, tiled=True)
    unused_gate, gate_pull = jax.vjp(smooth_gate, pre_gate)
    grad_act = gate_pull(jnp.dot(grad_ffn_all, ffn_out.T, preferred_element_type=jnp.float32))[
        0
    ].astype(jnp.bfloat16)
    grad_ffn_out = jnp.dot(activated.T, grad_ffn_all, preferred_element_type=jnp.float32)
    grad_ffn_in = jnp.dot(second_all.T, grad_act, preferred_element_type=jnp.float32)
    grad_second = RESIDUAL_ALPHA * grad_third + lax.psum_scatter(
        jnp.dot(grad_act, ffn_in.T, preferred_element_type=jnp.float32).astype(jnp.bfloat16),
        "tensor",
        scatter_dimension=0,
        tiled=True,
    ).astype(jnp.float32)
    grad_second_in, second_gain, second_bias = norm_back(
        grad_second, second_hat, second_inv, norm_gains[1]
    )
    grad_cross_att, cross_out_part = branch_grad(grad_second_in, cross_att, cross_out)
    grad_cq, grad_ck, grad_cv = attention_backward(
        cross_query, cross_proj[0], cross_proj[1], cross_mask, cross_lse, grad_cross_att, sentences
    )
    grad_cross_q = jnp.dot(first_all.T, grad_cq, preferred_element_type=jnp.float32)
    cross_grads = jnp.stack([grad_ck, grad_cv])
    grad_cross_kv = jnp.einsum(
        "td,cte->cde", all_memory, cross_grads, preferred_element_type=jnp.float32
    )
    grad_memory = lax.psum_scatter(
        jnp.einsum("cte,cde->td", cross_grads, cross_kv, preferred_element_type=jnp.float32).astype(
            jnp.bfloat16
        ),
        "tensor",
        scatter_dimension=0,
        tiled=True,
    ).astype(jnp.float32)

    def cross_input_term(first_row, row_total):
        return jnp.dot(grad_cq, cross_q.T, preferred_element_type=jnp.float32)

    cross_input = head_input_sum(cross_input_term)
    grad_first = RESIDUAL_ALPHA * grad_second_in + cross_input
    grad_first_in, first_gain, first_bias = norm_back(
        grad_first, first_hat, first_inv, norm_gains[0]
    )
    grad_self_att, self_out_part = branch_grad(grad_first_in, self_att, self_out)
    grad_sq, grad_sk, grad_sv = attention_backward(
        self_proj[0], self_proj[1], self_proj[2], self_mask, self_lse, grad_self_att, sentences
    )
    self_grads = jnp.stack([grad_sq, grad_sk, grad_sv])
    grad_self_qkv = jnp.einsum(
        "td,cte->cde", all_tokens, self_grads, preferred_element_type=jnp.float32
    )

    def self_input_term(first_row, row_total):
        return jnp.einsum("cte,cde->td", self_grads, self_qkv, preferred_element_type=jnp.float32)

    self_input = head_input_sum(self_input_term)
    grad_tokens = RESIDUAL_ALPHA * grad_first_in + self_input
    summed = (
        lax.psum_scatter(
            grad_self_qkv.astype(jnp.bfloat16), "dp", scatter_dimension=1, tiled=True
        ).astype(jnp.float32),
        lax.psum_scatter(
            self_out_part.astype(jnp.bfloat16), "dp", scatter_dimension=1, tiled=True
        ).astype(jnp.float32),
        lax.psum_scatter(
            grad_cross_q.astype(jnp.bfloat16), "dp", scatter_dimension=0, tiled=True
        ).astype(jnp.float32),
        lax.psum_scatter(
            grad_cross_kv.astype(jnp.bfloat16), "dp", scatter_dimension=1, tiled=True
        ).astype(jnp.float32),
        lax.psum_scatter(
            cross_out_part.astype(jnp.bfloat16), "dp", scatter_dimension=1, tiled=True
        ).astype(jnp.float32),
        lax.psum_scatter(
            grad_ffn_in.astype(jnp.bfloat16), "dp", scatter_dimension=0, tiled=True
        ).astype(jnp.float32),
        lax.psum_scatter(
            grad_ffn_out.astype(jnp.bfloat16), "dp", scatter_dimension=1, tiled=True
        ).astype(jnp.float32),
    )
    gain_total, bias_total = lax.psum(
        (
            jnp.stack([first_gain, second_gain, third_gain]),
            jnp.stack([first_bias, second_bias, third_bias]),
        ),
        ("dp", "tensor"),
    )
    return (
        out_rows.astype(jnp.bfloat16),
        grad_tokens,
        grad_memory,
        summed[0],
        summed[1],
        summed[2],
        summed[3],
        summed[4],
        summed[5],
        summed[6],
        gain_total,
        bias_total,
    )


def solution(mesh):
    in_specs = (
        P(("dp", "tensor"), None),
        P(("dp", "tensor"), None),
        P("dp", None),
        P("dp", None),
        P(None, None, "tensor"),
        P("tensor", None),
        P(None, "tensor"),
        P(None, None, "tensor"),
        P("tensor", None),
        P(None, "tensor"),
        P("tensor", None),
        P(),
        P(),
        P(("dp", "tensor"), None),
    )
    out_specs = (
        P(("dp", "tensor"), None),
        P(("dp", "tensor"), None),
        P(("dp", "tensor"), None),
        P(None, "dp", "tensor"),
        P("tensor", "dp"),
        P("dp", "tensor"),
        P(None, "dp", "tensor"),
        P("tensor", "dp"),
        P("dp", "tensor"),
        P("tensor", "dp"),
        P(),
        P(),
    )

    def step(*args):
        chosen = sentence_body if sentence_fits(mesh, args[0], args[1], args[2]) else body
        return jax.shard_map(
            chosen, mesh=mesh, in_specs=in_specs, out_specs=out_specs, check_vma=False
        )(*args)

    return step
```

```python
import functools
import jax
import jax.numpy as jnp
from jax import lax
from jax.experimental import pallas as pl
from jax.experimental.pallas import tpu as pltpu
from jax.sharding import PartitionSpec as P

HEAD_DIM = 64
RESIDUAL_ALPHA = 4.16
NORM_EPSILON = 1e-05
MASKED_SCORE = -1000000000.0
SCORE_SCALE = HEAD_DIM ** (-0.5)
UNIT = 128
QUERY_BLOCK = 256
FFN_UNIT = 512
ROW_CHUNK = 64
BF16 = jnp.bfloat16
F32 = jnp.float32


def dot(left, right):
    return lax.dot_general(left, right, (((1,), (0,)), ((), ())), preferred_element_type=F32)


def dot_tn(left, right):
    return lax.dot_general(left, right, (((0,), (0,)), ((), ())), preferred_element_type=F32)


def dot_nt(left, right):
    return lax.dot_general(left, right, (((1,), (1,)), ((), ())), preferred_element_type=F32)


def shard_of(position):
    return ((position >> 2) & 1) | (position & 2) | ((position & 1) << 2)


def copy_of(source, target, sem):
    return pltpu.make_async_copy(source, target, sem)


def own_lanes(rows, head):
    lanes = lax.broadcasted_iota(jnp.int32, rows.shape, 1)
    return jnp.where((lanes >= HEAD_DIM) if head else (lanes < HEAD_DIM), rows, 0.0)


def extended_keys(keys, length):
    lanes = lax.broadcasted_iota(jnp.int32, keys.shape, 1)
    rows = lax.broadcasted_iota(jnp.int32, keys.shape, 0)
    mask = jnp.where((lanes == 0) & (rows >= length), MASKED_SCORE, 0.0).astype(BF16)
    keys = keys.astype(F32)
    return [jnp.concatenate([own_lanes(keys, head).astype(BF16), mask], axis=1) for head in (0, 1)]


def extended_query(query):
    lanes = lax.broadcasted_iota(jnp.int32, query.shape, 1)
    return jnp.concatenate([query, jnp.where(lanes == 0, 1.0, 0.0).astype(BF16)], axis=1)


def fill_diagonal(diagonal):
    keys = lax.broadcasted_iota(jnp.int32, diagonal.shape, 0)
    queries = lax.broadcasted_iota(jnp.int32, diagonal.shape, 1)
    diagonal[...] = jnp.where(keys <= queries, 0.0, MASKED_SCORE)


def key_ranges(block, keys, causal):
    if not causal:
        return [(0, keys)]
    return [(low, low + QUERY_BLOCK) for low in range(0, (block + 1) * QUERY_BLOCK, QUERY_BLOCK)]


def attend_unit(query, keys, values, length, causal, diagonal, lse_ref):
    rows, count = query.shape[0], keys.shape[0]
    values_t = jnp.transpose(values.astype(F32)).astype(BF16)
    wide_keys, wide_query = extended_keys(keys, length), extended_query(query)
    items = [(head, block) for block in range(rows // QUERY_BLOCK) for head in (0, 1)]
    scores, probs, totals, mixed = {}, {}, {}, {}
    for head, block in items:
        part = wide_query[block * QUERY_BLOCK : (block + 1) * QUERY_BLOCK]
        ranges = key_ranges(block, count, causal)
        scores[head, block] = [dot_nt(wide_keys[head][a:b], part) for a, b in ranges]
        if causal:
            scores[head, block][-1] = scores[head, block][-1] + diagonal[...]
    for head, block in items:
        pieces = scores[head, block]
        peak = functools.reduce(jnp.maximum, [jnp.max(p, axis=0, keepdims=True) for p in pieces])
        terms = [jnp.exp(p - peak) for p in pieces]
        total = sum(jnp.sum(t, axis=0, keepdims=True) for t in terms)
        at = slice(block * QUERY_BLOCK, (block + 1) * QUERY_BLOCK)
        lse_ref[head : head + 1, at] = peak + jnp.log(total)
        totals[head, block] = total
        probs[head, block] = jnp.concatenate([t.astype(BF16) for t in terms], axis=0)
    for head, block in items:
        own = values_t[head * HEAD_DIM : (head + 1) * HEAD_DIM, : probs[head, block].shape[0]]
        mixed[head, block] = dot(own, probs[head, block]) / totals[head, block]
    out = [
        jnp.transpose(jnp.concatenate([mixed[0, block], mixed[1, block]], axis=0))
        for block in range(rows // QUERY_BLOCK)
    ]
    return jnp.concatenate(out, axis=0).astype(BF16)


def attend_back_unit(query, keys, values, attended, grad, length, causal, diagonal, lse_ref):
    rows, count = query.shape[0], keys.shape[0]
    blocks = range(rows // QUERY_BLOCK)
    query_f, keys_f, grad_f = (a.astype(F32) for a in (query, keys, grad))
    wide_keys, wide_query = extended_keys(keys, length), extended_query(query)
    delta = jnp.transpose(grad_f * attended.astype(F32))
    deltas = [
        jnp.sum(delta[head * HEAD_DIM : (head + 1) * HEAD_DIM], axis=0, keepdims=True)
        for head in (0, 1)
    ]
    keys_t = jnp.transpose(keys_f).astype(BF16)
    query_own = [own_lanes(query_f, head).astype(BF16) for head in (0, 1)]
    grad_own = [own_lanes(grad_f, head).astype(BF16) for head in (0, 1)]
    items = [(head, block) for block in blocks for head in (0, 1)]
    scores, slopes, probs, back, grad_query = {}, {}, {}, {}, {}
    for head, block in items:
        at = slice(block * QUERY_BLOCK, (block + 1) * QUERY_BLOCK)
        for a, b in key_ranges(block, count, causal):
            scores[head, block, a] = dot_nt(wide_keys[head][a:b], wide_query[at])
            slopes[head, block, a] = dot_nt(values[a:b], grad_own[head][at])
    for head, block in items:
        at = slice(block * QUERY_BLOCK, (block + 1) * QUERY_BLOCK)
        ranges = key_ranges(block, count, causal)
        for a, b in ranges:
            score = scores[head, block, a]
            if causal and (a, b) == ranges[-1]:
                score = score + diagonal[...]
            prob = jnp.exp(score - lse_ref[head : head + 1, at])
            probs[head, block, a] = prob.astype(BF16)
            back[head, block, a] = (prob * (slopes[head, block, a] - deltas[head][:, at])).astype(BF16)
    for head, block in items:
        own = keys_t[head * HEAD_DIM : (head + 1) * HEAD_DIM]
        grad_query[head, block] = sum(
            dot(own[:, a:b], back[head, block, a]) for a, b in key_ranges(block, count, causal)
        )
    grad_keys, grad_values = [], []
    for low in sorted({key[2] for key in back}):
        live = [key for key in back if key[2] == low]
        at = [slice(block * QUERY_BLOCK, (block + 1) * QUERY_BLOCK) for _, block, _ in live]
        grad_values.append(
            dot(
                jnp.concatenate([probs[key] for key in live], axis=1),
                jnp.concatenate([grad_own[key[0]][a] for key, a in zip(live, at)], axis=0),
            )
        )
        grad_keys.append(
            dot(
                jnp.concatenate([back[key] for key in live], axis=1),
                jnp.concatenate([query_own[key[0]][a] for key, a in zip(live, at)], axis=0),
            )
        )
    grad_query = [
        jnp.transpose(jnp.concatenate([grad_query[0, block], grad_query[1, block]], axis=0)) * SCORE_SCALE
        for block in blocks
    ]
    return tuple(
        jnp.concatenate(parts, axis=0).astype(BF16) for parts in (grad_query, grad_keys, grad_values)
    )


def norm_chunk(hidden, gain, bias):
    center = hidden - jnp.mean(hidden, axis=-1, keepdims=True)
    inverse = lax.rsqrt(jnp.mean(center * center, axis=-1, keepdims=True) + NORM_EPSILON)
    normed = center * inverse
    return normed * gain + bias, normed, inverse


def norm_back_chunk(gradient, normed, inverse, gain):
    scaled = gradient * gain
    return inverse * (
        scaled
        - jnp.mean(scaled, axis=-1, keepdims=True)
        - normed * jnp.mean(scaled * normed, axis=-1, keepdims=True)
    )


def fold_rows(values):
    return jnp.sum(values.reshape(values.shape[0] // 8, 8, values.shape[1]), axis=0)


def each_chunk(rows, body):
    def step(index, carry):
        body(pl.ds(pl.multiple_of(index * ROW_CHUNK, ROW_CHUNK), ROW_CHUNK))
        return carry

    lax.fori_loop(0, rows // ROW_CHUNK, step, 0)


def store_shards(target, weight, dp):
    for block in range(8):
        target[shard_of(block ^ dp)] = weight[block * UNIT : (block + 1) * UNIT]


SMEM = pl.BlockSpec(memory_space=pltpu.SMEM)
VMEM = pl.BlockSpec(memory_space=pltpu.VMEM)
ANY = pl.BlockSpec(memory_space=pl.ANY)


def params(limit=62):
    return pltpu.CompilerParams(vmem_limit_bytes=limit * 1024 * 1024)


def cost_of(microseconds):
    return pl.CostEstimate(flops=int(microseconds * 1.1e9), bytes_accessed=4 << 20, transcendentals=0)


def sds(shape, dtype):
    return jax.ShapeDtypeStruct(shape, dtype)


def weight_copies(pieces, order, wbuf, obuf, wsem, osem, columns=(0, 1, 2)):
    groups, outs = [[], [], []], []
    wide = 2 * UNIT
    for index, refs in enumerate(pieces):
        at = slice(index * wide, (index + 1) * wide)
        if len(refs) > 1:
            column = 0
            for ref in refs[:-1]:
                for source in [ref] if len(ref.shape) == 2 else [ref.at[c] for c in range(ref.shape[0])]:
                    if column in columns:
                        low = (columns.index(column) * len(pieces) + index) * wide
                        groups[column].append(copy_of(source, wbuf.at[:, low : low + wide], wsem.at[column, index, 0]))
                    column += 1
            if obuf is not None:
                outs.append(copy_of(refs[-1], obuf.at[at, :], osem.at[index, 0]))
            continue
        rest, = refs
        rows = rest.shape[2]
        part = wide // 4
        for quarter in range(4):
            place = quarter ^ order
            for column in columns:
                low = (columns.index(column) * len(pieces) + index) * wide
                groups[column].append(
                    copy_of(
                        rest.at[quarter, column],
                        wbuf.at[pl.ds(pl.multiple_of(place * rows, rows), rows), low : low + wide],
                        wsem.at[column, index, quarter],
                    )
                )
            for block in range(4 if obuf is not None else 0):
                outs.append(
                    copy_of(
                        rest.at[quarter, 3, block * part : (block + 1) * part, :],
                        obuf.at[pl.ds(pl.multiple_of(index * wide + place * part, part), part), block * wide : (block + 1) * wide],
                        osem.at[index, 4 * quarter + block],
                    )
                )
    return groups, outs


def attention_fwd_call(scalars, residual, others, pieces, partial, norm):
    rows, depth = others[0].shape
    causal = len(others) == 1
    number, wide = 2 * len(pieces), 2 * len(pieces) * UNIT
    last, has_partial = norm is not None, partial is not None

    def kernel(*refs):
        it = iter(refs)
        sc = next(it)
        in_refs = [next(it) for _ in others]
        gain_ref, bias_ref = (next(it), next(it)) if last else (None, None)
        old_rows = [next(it) for _ in residual[1:]] if last else []
        res_in = next(it) if last else None
        part_in = next(it) if has_partial else None
        w_refs = [[next(it) for _ in piece] for piece in pieces]
        q_ref, k_ref, v_ref, att_ref, lse_ref = (next(it) for _ in range(5))
        if last:
            low_ref, hat_ref, inv_ref = next(it), next(it), next(it)
        else:
            sum_ref = next(it)
        wbuf, obuf, att_all, diagonal, wsem, osem, lsem = (next(it) for _ in range(7))
        if last:
            acc, old = next(it), next(it)
        length, order = sc[0], sc[1]
        groups, outs = weight_copies(w_refs, order, wbuf, obuf, wsem, osem)
        for copies in groups + [outs]:
            for copy in copies:
                copy.start()
        target = acc if last else sum_ref
        late = []
        if has_partial:
            late.append(copy_of(part_in, target, lsem.at[0]))
        if last:
            late.append(copy_of(res_in, old, lsem.at[1]))
        for copy in late:
            copy.start()
        if causal:
            fill_diagonal(diagonal)
        for c, result in enumerate((q_ref, k_ref, v_ref)):
            for copy in groups[c]:
                copy.wait()
            rows_in = in_refs[0] if causal or c == 0 else in_refs[1]
            proj = dot(rows_in[...], wbuf[:, c * wide : (c + 1) * wide]).astype(BF16)
            if c == 0:
                proj = (proj.astype(F32) * SCORE_SCALE).astype(BF16)
            for index in range(number):
                result[index] = proj[:, index * UNIT : (index + 1) * UNIT]

        def step(u, carry):
            attended = attend_unit(q_ref[u], k_ref[u], v_ref[u], length, causal, diagonal, lse_ref.at[u])
            att_ref[u] = attended
            att_all[:, pl.ds(pl.multiple_of(u * UNIT, UNIT), UNIT)] = attended
            return carry

        lax.fori_loop(0, number, step, 0)
        for copy in outs + late:
            copy.wait()
        if has_partial:
            target[...] += dot(att_all[...], obuf[...])
        else:
            target[...] = dot(att_all[...], obuf[...])
        if last:
            def chunk(at):
                before = old[at, :].astype(F32)
                if old_rows:
                    before = before * old_rows[0][...] + old_rows[1][...]
                normed, hat, inverse = norm_chunk(RESIDUAL_ALPHA * before + acc[at, :], gain_ref[...], bias_ref[...])
                low_ref[at, :] = normed.astype(BF16)
                hat_ref[at, :] = hat
                inv_ref[at, :] = jnp.broadcast_to(inverse, (ROW_CHUNK, 128))

            each_chunk(rows, chunk)

    unit_rows = sds((number, rows, UNIT), BF16)
    shapes = [unit_rows] * 4 + [sds((number, 2, rows), F32)]
    if last:
        shapes += [sds((rows, depth), BF16), sds((rows, depth), F32), sds((rows, 128), F32)]
    else:
        shapes += [sds((rows, depth), F32)]
    args = [scalars, *others]
    if last:
        args += [*norm, *residual[1:]]
    tail = ([residual[0]] if last else []) + ([partial] if has_partial else [])
    tail += [array for piece in pieces for array in piece]
    scratch = [
        pltpu.VMEM((depth, 3 * wide), BF16),
        pltpu.VMEM((wide, depth), BF16),
        pltpu.VMEM((rows, wide), BF16),
        pltpu.VMEM((QUERY_BLOCK, QUERY_BLOCK), F32),
        pltpu.SemaphoreType.DMA((3, len(pieces), 4)),
        pltpu.SemaphoreType.DMA((len(pieces), 16)),
        pltpu.SemaphoreType.DMA((2,)),
    ]
    if last:
        scratch += [pltpu.VMEM((rows, depth), F32), pltpu.VMEM((rows, depth), residual[0].dtype)]
    return pl.pallas_call(
        kernel,
        out_shape=shapes,
        in_specs=[SMEM] + [VMEM] * (len(args) - 1) + [ANY] * len(tail),
        out_specs=[VMEM] * len(shapes),
        scratch_shapes=scratch,
        compiler_params=params(),
        cost_estimate=cost_of(0.6 * number),
        name="self_fwd" if causal else "cross_fwd",
    )(*args, *tail)


def attention_bwd_call(scalars, grad_low, others, pieces, saved, plan, carried, norm, results=1):
    rows, depth = grad_low.shape
    causal = len(others) == 1
    number, n_in, wide = len(plan), len(others), len(plan) * UNIT
    last = norm is not None
    skip = 1 if last else 0

    def kernel(*refs):
        it = iter(refs)
        sc = next(it)
        h_ref = next(it)
        in_refs = [next(it) for _ in range(n_in)]
        gain_ref = next(it) if last else None
        late_in = [next(it), next(it)] if last else []
        acc_in = next(it) if last else None
        w_refs = [[next(it) for _ in piece] for piece in pieces]
        s_refs = [[next(it) for _ in call] for call in saved]
        if last:
            low_ref, scaled_ref, gsum_ref, bsum_ref = (next(it) for _ in range(4))
        dall_ref = next(it)
        g_refs = [next(it) for _ in range(results)]
        wbuf, obuf, sbuf, lbuf, att_all, grad_all = (next(it) for _ in range(6))
        stage, diagonal = next(it), next(it)
        if last:
            dquery, acc, hat, inv = (next(it) for _ in range(4))
        wsem, osem, ssem, gsem, lsem = (next(it) for _ in range(5))
        length, order, dp = sc[0], sc[1], sc[2]

        groups, o_copies = weight_copies(w_refs, order, wbuf, obuf, wsem, osem, (0,) if last else ())
        for copy in o_copies:
            copy.start()
        s_copies = []
        for index, unit in enumerate(plan):
            lanes = slice(index * UNIT, (index + 1) * UNIT)
            call = s_refs[unit[0]]
            for c in range(3):
                s_copies.append(copy_of(call[c].at[unit[1]], sbuf.at[index, c], ssem.at[c, index]))
            s_copies.append(copy_of(call[3].at[unit[1]], att_all.at[:, lanes], ssem.at[3, index]))
            s_copies.append(copy_of(call[4].at[unit[1]], lbuf.at[index], ssem.at[4, index]))
        late = []
        if last:
            late = groups[0] + [
                copy_of(source, target, lsem.at[index])
                for index, (source, target) in enumerate(((acc_in, acc), (late_in[0], hat), (late_in[1], inv)))
            ]
        for copy in s_copies + late:
            copy.start()
        if causal:
            fill_diagonal(diagonal)
        for copy in o_copies:
            copy.wait()
        grad_att = dot_nt(h_ref[...], obuf[...]).astype(BF16)
        for index in range(number):
            grad_all[index] = grad_att[:, index * UNIT : (index + 1) * UNIT]
        for copy in s_copies:
            copy.wait()

        def step(u, carry):
            at = pl.ds(pl.multiple_of(u * UNIT, UNIT), UNIT)
            parts = attend_back_unit(
                sbuf[u, 0], sbuf[u, 1], sbuf[u, 2], att_all[:, at], grad_all[u], length, causal, diagonal, lbuf.at[u]
            )
            if last:
                dquery[:, at] = parts[0]
            for c in range(skip, 3):
                dall_ref[:, pl.ds(pl.multiple_of((c - skip) * wide + u * UNIT, UNIT), UNIT)] = parts[c]
            return carry

        lax.fori_loop(0, number, step, 0)

        share = number // 2 // results

        def keep(rows_in, source, column):
            weight = dot_tn(rows_in[...], source).astype(BF16)
            for index in range(number):
                piece = index // 2
                target = stage.at[piece // share, (index % 2) * 4 + column, piece % share]
                store_shards(target, weight[:, index * UNIT : (index + 1) * UNIT], dp)

        if last:
            keep(in_refs[0], dquery[...], 0)
        for c in range(skip, 3):
            keep(in_refs[-1], dall_ref[:, (c - skip) * wide : (c - skip + 1) * wide], c)
        keep(h_ref, att_all[...], 3)
        g_copies = [copy_of(stage.at[index], ref, gsem.at[index]) for index, ref in enumerate(g_refs)]
        for copy in g_copies:
            copy.start()
        for copy in late:
            copy.wait()
        if last:
            acc[...] += dot_nt(dquery[...], wbuf[...])
            norm_back_rows(acc, hat, inv, gain_ref, low_ref, scaled_ref, gsum_ref, bsum_ref, rows)
        for copy in g_copies:
            copy.wait()

    big = sds((rows, depth), F32)
    shapes = []
    if last:
        shapes += [sds((rows, depth), BF16), big, sds((8, depth), F32), sds((8, depth), F32)]
    shapes.append(sds((rows, (3 - skip) * wide), BF16))
    specs_out = [VMEM] * len(shapes) + [ANY] * results
    shapes += [sds((8, number // 2 // results, 8, UNIT, UNIT), BF16)] * results
    args = [scalars, grad_low, *others] + ([norm[2]] if last else [])
    tail = [norm[0], norm[1], carried] if last else []
    tail += [array for piece in pieces for array in piece]
    for call in saved:
        tail += call
    scratch = [
        pltpu.VMEM((depth, wide) if last else (16, 128), BF16),
        pltpu.VMEM((wide, depth), BF16),
        pltpu.VMEM((number, 3, rows, UNIT), BF16),
        pltpu.VMEM((number, 2, rows), F32),
        pltpu.VMEM((rows, wide), BF16),
        pltpu.VMEM((number, rows, UNIT), BF16),
        pltpu.VMEM((results, 8, number // 2 // results, 8, UNIT, UNIT), BF16),
        pltpu.VMEM((QUERY_BLOCK, QUERY_BLOCK), F32),
    ]
    if last:
        scratch += [pltpu.VMEM((rows, wide), BF16), pltpu.VMEM((rows, depth), F32), pltpu.VMEM((rows, depth), F32), pltpu.VMEM((rows, 128), F32)]
    scratch += [
        pltpu.SemaphoreType.DMA((3, len(pieces), 4)),
        pltpu.SemaphoreType.DMA((len(pieces), 16)),
        pltpu.SemaphoreType.DMA((5, number)),
        pltpu.SemaphoreType.DMA((results,)),
        pltpu.SemaphoreType.DMA((4,)),
    ]
    return pl.pallas_call(
        kernel,
        out_shape=shapes,
        in_specs=[SMEM] + [VMEM] * (len(args) - 1) + [ANY] * len(tail),
        out_specs=specs_out,
        scratch_shapes=scratch,
        compiler_params=params(),
        cost_estimate=cost_of(4.2 * number),
        name="self_bwd" if causal else "cross_bwd",
    )(*args, *tail)


def inputs_back_call(scalars, base, parts, memory_part):
    rows, depth = base.shape
    jobs = [(0, grad, pieces, (0, 1, 2)) for grad, pieces in parts] + [(1, *memory_part, (1, 2))]

    def kernel(*refs):
        it = iter(refs)
        sc, base_ref = next(it), next(it)
        grads = [next(it) for _ in jobs]
        w_refs = [[[next(it) for _ in piece] for piece in pieces] for _, _, pieces, _ in jobs]
        outs = [next(it), next(it)]
        bufs, sems = [next(it) for _ in jobs], [next(it) for _ in jobs]
        copies = []
        for index, (_, _, _, columns) in enumerate(jobs):
            groups, _ = weight_copies(w_refs[index], sc[1], bufs[index], None, sems[index], None, columns)
            copies.append([copy for group in groups for copy in group])
            for copy in copies[-1]:
                copy.start()
        outs[0][...] = base_ref[...]
        for index, (out, _, _, _) in enumerate(jobs):
            for copy in copies[index]:
                copy.wait()
            if out:
                outs[1][...] = dot_nt(grads[index][...], bufs[index][...])
            else:
                outs[0][...] += dot_nt(grads[index][...], bufs[index][...])

    args = [scalars, base] + [grad for _, grad, _, _ in jobs]
    tail = [array for _, _, pieces, _ in jobs for piece in pieces for array in piece]
    return pl.pallas_call(
        kernel,
        out_shape=[sds((rows, depth), F32)] * 2,
        in_specs=[SMEM] + [VMEM] * (len(args) - 1) + [ANY] * len(tail),
        out_specs=[VMEM] * 2,
        scratch_shapes=[pltpu.VMEM((depth, grad.shape[1]), BF16) for _, grad, _, _ in jobs]
        + [pltpu.SemaphoreType.DMA((3, len(pieces), 4)) for _, _, pieces, _ in jobs],
        compiler_params=params(),
        cost_estimate=cost_of(12),
        name="inputs_back",
    )(*args, *tail)


def norm_back_rows(acc, hat, inv, gain_ref, low_ref, scaled_ref, gsum_ref, bsum_ref, rows):
    gsum_ref[...] = jnp.zeros_like(gsum_ref)
    bsum_ref[...] = jnp.zeros_like(bsum_ref)

    def chunk(at):
        gradient, normed = acc[at, :], hat[at, :]
        grad_in = norm_back_chunk(gradient, normed, inv[at, :1], gain_ref[...])
        low_ref[at, :] = grad_in.astype(BF16)
        scaled_ref[at, :] = RESIDUAL_ALPHA * grad_in
        gsum_ref[...] += fold_rows(gradient * normed)
        bsum_ref[...] += fold_rows(gradient)

    each_chunk(rows, chunk)


GELU_SCALE = 0.7978845608028654
GELU_CUBE = 0.044715


def gelu_and_slope(pre):
    square = pre * pre
    inner = pre * (GELU_SCALE + (GELU_SCALE * GELU_CUBE) * square)
    curve = jnp.tanh(inner)
    half = 0.5 + 0.5 * curve
    slope = half * (1.0 + pre * (1.0 - curve) * (GELU_SCALE + (3.0 * GELU_SCALE * GELU_CUBE) * square))
    return pre * half, slope


FFN_PART = FFN_UNIT // 2


def ffn_copies(pieces, order, ubuf, dbuf, usem, dsem):
    ups, downs = [], []
    for index, refs in enumerate(pieces):
        wide = 2 * FFN_UNIT
        at = slice(index * wide, (index + 1) * wide)
        if len(refs) == 2:
            ups.append([copy_of(refs[0], ubuf.at[:, at], usem.at[index, 0])])
            downs.append([copy_of(refs[1], dbuf.at[at, :], dsem.at[index, 0])])
            continue
        ups.append([])
        downs.append([])
        rows = refs[0].shape[1]
        for quarter in range(4):
            up = refs[quarter].at[0]
            down = refs[quarter].at[1] if quarter < 3 else refs[4].at[0]
            place = (quarter ^ order) * rows
            ups[-1].append(copy_of(up, ubuf.at[pl.ds(pl.multiple_of(place, rows), rows), at], usem.at[index, quarter]))
            downs[-1].append(
                copy_of(down, dbuf.at[pl.ds(pl.multiple_of(index * wide + place, rows), rows), :], dsem.at[index, quarter])
            )
    return ups, downs


def ffn_fwd_call(scalars, inputs, pieces, partial, final):
    rows, depth = inputs.shape
    number = 2 * len(pieces)
    last, has_partial = final is not None, partial is not None

    def kernel(*refs):
        it = iter(refs)
        sc, x_ref = next(it), next(it)
        if last:
            gain_old, bias_old, gain_ref, bias_ref = (next(it) for _ in range(4))
            late_in = [next(it), next(it)]
        part_in = next(it) if has_partial else None
        w_refs = [[next(it) for _ in piece] for piece in pieces]
        if last:
            out_ref, low_ref, scaled_ref, gsum_ref, bsum_ref = (next(it) for _ in range(5))
        else:
            sum_ref = next(it)
        act_ref, slope_ref = next(it), next(it)
        ubuf, dbuf, abuf, sbuf, pbuf, psem = (next(it) for _ in range(6))
        if last:
            acc, hat, cot, lsem = (next(it) for _ in range(4))
        wsem, gsem = next(it), next(it)
        target = acc if last else sum_ref

        up_copies, down_copies = ffn_copies(w_refs, sc[1], ubuf, dbuf, wsem.at[0], wsem.at[1])
        for copies in up_copies + down_copies:
            for copy in copies:
                copy.start()
        if has_partial:
            part_copy = copy_of(part_in, target, psem)
            part_copy.start()
        if last:
            late = [copy_of(late_in[0], hat, lsem.at[0]), copy_of(late_in[1], cot, lsem.at[1])]
            for copy in late:
                copy.start()
        saves = []

        def gate(pre, index):
            activated, slope = gelu_and_slope(pre)
            abuf[:, index * FFN_UNIT : (index + 1) * FFN_UNIT] = activated.astype(BF16)
            sbuf[:, index * FFN_UNIT : (index + 1) * FFN_UNIT] = slope.astype(BF16)

        for index in range(number):
            if index % 2 == 0:
                for copy in up_copies[index // 2]:
                    copy.wait()
            if index:
                gate(pbuf[(index - 1) % 2], index - 1)
            pbuf[index % 2] = dot(x_ref[...], ubuf[:, index * FFN_UNIT : (index + 1) * FFN_UNIT])
        gate(pbuf[(number - 1) % 2], number - 1)
        for index in range(number):
            at = slice(index * FFN_UNIT, (index + 1) * FFN_UNIT)
            saves += [
                copy_of(abuf.at[:, at], act_ref.at[index], gsem.at[0, index]),
                copy_of(sbuf.at[:, at], slope_ref.at[index], gsem.at[1, index]),
            ]
        for copy in saves:
            copy.start()
        for copies in down_copies:
            for copy in copies:
                copy.wait()
        if has_partial:
            part_copy.wait()
            target[...] += dot(abuf[...], dbuf[...])
        else:
            target[...] = dot(abuf[...], dbuf[...])
        if last:
            for copy in late:
                copy.wait()
            gsum_ref[...] = jnp.zeros_like(gsum_ref)
            bsum_ref[...] = jnp.zeros_like(bsum_ref)

            def chunk(at):
                old = hat[at, :] * gain_old[...] + bias_old[...]
                normed, xhat, inverse = norm_chunk(RESIDUAL_ALPHA * old + acc[at, :], gain_ref[...], bias_ref[...])
                out_ref[at, :] = normed.astype(BF16)
                gradient = cot[at, :].astype(F32)
                grad_in = norm_back_chunk(gradient, xhat, inverse, gain_ref[...])
                low_ref[at, :] = grad_in.astype(BF16)
                scaled_ref[at, :] = RESIDUAL_ALPHA * grad_in
                gsum_ref[...] += fold_rows(gradient * xhat)
                bsum_ref[...] += fold_rows(gradient)

            each_chunk(rows, chunk)
        for copy in saves:
            copy.wait()

    big, low = sds((rows, depth), F32), sds((rows, depth), BF16)
    if last:
        shapes = [low, low, big, sds((8, depth), F32), sds((8, depth), F32)]
    else:
        shapes = [big]
    specs_out = [VMEM] * len(shapes) + [ANY, ANY]
    shapes += [sds((number, rows, FFN_UNIT), BF16)] * 2
    args = [scalars, inputs]
    if last:
        args += [final[1], final[2], final[4], final[5]]
    specs = [SMEM] + [VMEM] * (len(args) - 1)
    tail = ([final[0], final[3]] if last else []) + ([partial] if has_partial else []) + [array for piece in pieces for array in piece]
    scratch = [
        pltpu.VMEM((depth, number * FFN_UNIT), BF16),
        pltpu.VMEM((number * FFN_UNIT, depth), BF16),
        pltpu.VMEM((rows, number * FFN_UNIT), BF16),
        pltpu.VMEM((rows, number * FFN_UNIT), BF16),
        pltpu.VMEM((2, rows, FFN_UNIT), F32),
        pltpu.SemaphoreType.DMA,
    ]
    if last:
        scratch += [
            pltpu.VMEM((rows, depth), F32),
            pltpu.VMEM((rows, depth), F32),
            pltpu.VMEM((rows, depth), BF16),
            pltpu.SemaphoreType.DMA((2,)),
        ]
    scratch += [pltpu.SemaphoreType.DMA((2, len(pieces), 4)), pltpu.SemaphoreType.DMA((2, number))]
    return pl.pallas_call(
        kernel,
        out_shape=shapes,
        in_specs=specs + [ANY] * len(tail),
        out_specs=specs_out,
        scratch_shapes=scratch,
        compiler_params=params(),
        cost_estimate=cost_of(12),
        name="ffn_fwd",
    )(*args, *tail)


def ffn_bwd_call(scalars, grad_low, inputs, pieces, saved, plan, carried, norm):
    rows, depth = inputs.shape
    number = len(plan)
    last = norm is not None

    def kernel(*refs):
        it = iter(refs)
        sc, g_in, x_ref = (next(it) for _ in range(3))
        gain_ref = next(it) if last else None
        late_in = [next(it), next(it)] if last else []
        acc_in = next(it)
        w_refs = [[next(it) for _ in piece] for piece in pieces]
        s_refs = [[next(it) for _ in call] for call in saved]
        if last:
            low_ref, scaled_ref, gsum_ref, bsum_ref = (next(it) for _ in range(4))
        else:
            sum_ref = next(it)
        g_ref = next(it)
        ubuf, dbuf, abuf, sbuf, gbuf, stage, psem = (next(it) for _ in range(7))
        if last:
            acc, hat, inv, lsem = (next(it) for _ in range(4))
        wsem, ssem, gsem = next(it), next(it), next(it)
        order, dp = sc[1], sc[2]
        target = acc if last else sum_ref

        ups, downs = ffn_copies(w_refs, order, ubuf, dbuf, wsem.at[0], wsem.at[1])
        slopes, acts = [], []
        for index, (call, at) in enumerate(plan):
            lanes = slice(index * FFN_UNIT, (index + 1) * FFN_UNIT)
            slopes.append(copy_of(s_refs[call][1].at[at], sbuf.at[index], ssem.at[0, index]))
            acts.append(copy_of(s_refs[call][0].at[at], abuf.at[:, lanes], ssem.at[1, index]))
        for copies in downs + [slopes, acts] + ups:
            for copy in copies:
                copy.start()
        part_copy = copy_of(acc_in, target, psem)
        part_copy.start()
        if last:
            late = [copy_of(late_in[0], hat, lsem.at[0]), copy_of(late_in[1], inv, lsem.at[1])]
            for copy in late:
                copy.start()
        for index in range(number):
            if index % 2 == 0:
                for copy in downs[index // 2]:
                    copy.wait()
            slopes[index].wait()
            grad_act = dot_nt(g_in[...], dbuf[index * FFN_UNIT : (index + 1) * FFN_UNIT, :]) * sbuf[index].astype(F32)
            gbuf[:, index * FFN_UNIT : (index + 1) * FFN_UNIT] = grad_act.astype(BF16)
        for copy in acts:
            copy.wait()

        def keep(rows_in, source, column):
            for half in range(number // 2):
                wide = 2 * FFN_UNIT
                weight = dot_tn(rows_in[...], source[:, half * wide : (half + 1) * wide]).astype(BF16)
                for inner in range(4):
                    part = weight[:, inner * FFN_PART : (inner + 1) * FFN_PART]
                    store_shards(stage.at[2 * inner + column, half], part, dp)

        keep(x_ref, gbuf, 0)
        keep(g_in, abuf, 1)
        g_copies = [copy_of(stage, g_ref, gsem)]
        for copy in g_copies:
            copy.start()
        for copies in ups:
            for copy in copies:
                copy.wait()
        part_copy.wait()
        target[...] += dot_nt(gbuf[...], ubuf[...])
        if last:
            for copy in late:
                copy.wait()
            norm_back_rows(acc, hat, inv, gain_ref, low_ref, scaled_ref, gsum_ref, bsum_ref, rows)
        for copy in g_copies:
            copy.wait()

    big, low = sds((rows, depth), F32), sds((rows, depth), BF16)
    shapes = [low, big, sds((8, depth), F32), sds((8, depth), F32)] if last else [big]
    specs_out = [VMEM] * len(shapes) + [ANY]
    shapes.append(sds((8, number // 2, 8, UNIT, FFN_PART), BF16))
    args = [scalars, grad_low, inputs] + ([norm[2]] if last else [])
    specs = [SMEM] + [VMEM] * (len(args) - 1)
    tail = ([norm[0], norm[1]] if last else []) + [carried] + [array for piece in pieces for array in piece]
    for call in saved:
        tail += call
    scratch = [
        pltpu.VMEM((depth, number * FFN_UNIT), BF16),
        pltpu.VMEM((number * FFN_UNIT, depth), BF16),
        pltpu.VMEM((rows, number * FFN_UNIT), BF16),
        pltpu.VMEM((number, rows, FFN_UNIT), BF16),
        pltpu.VMEM((rows, number * FFN_UNIT), BF16),
        pltpu.VMEM((8, number // 2, 8, UNIT, FFN_PART), BF16),
        pltpu.SemaphoreType.DMA,
    ]
    if last:
        scratch += [
            pltpu.VMEM((rows, depth), F32),
            pltpu.VMEM((rows, depth), F32),
            pltpu.VMEM((rows, 128), F32),
            pltpu.SemaphoreType.DMA((2,)),
        ]
    scratch += [pltpu.SemaphoreType.DMA((2, len(pieces), 4)), pltpu.SemaphoreType.DMA((2, number)), pltpu.SemaphoreType.DMA]
    return pl.pallas_call(
        kernel,
        out_shape=shapes,
        in_specs=specs + [ANY] * len(tail),
        out_specs=specs_out,
        scratch_shapes=scratch,
        compiler_params=params(),
        cost_estimate=cost_of(17),
        name="ffn_bwd",
    )(*args, *tail)


def combine(jobs, shapes):
    arrays = []
    for terms, _, _ in jobs:
        for array, _ in terms:
            if not any(array is known for known in arrays):
                arrays.append(array)
    position = {id(array): index for index, array in enumerate(arrays)}

    def part_shape(array, index):
        kept = []
        for extent, at in zip(array.shape, index + (slice(None),) * (array.ndim - len(index))):
            if isinstance(at, slice):
                kept.append(len(range(*at.indices(extent))))
        return tuple(kept)

    part_shapes = [part_shape(*terms[0]) for terms, _, _ in jobs]
    count = sum(len(terms) for terms, _, _ in jobs)

    def kernel(*refs):
        ins, outs = refs[: len(arrays)], refs[len(arrays) : len(arrays) + len(shapes)]
        rest = refs[len(arrays) + len(shapes) :]
        term_bufs, sum_bufs, isem, osem = rest[:count], rest[count : count + len(jobs)], rest[-2], rest[-1]
        loads, number = [], 0
        for terms, _, _ in jobs:
            loads.append([])
            for array, index in terms:
                loads[-1].append(copy_of(ins[position[id(array)]].at[index], term_bufs[number], isem.at[number]))
                number += 1
        for group in loads:
            for copy in group:
                copy.start()
        stores, number = [], 0
        for job, (terms, out, place) in enumerate(jobs):
            for copy in loads[job]:
                copy.wait()
            bufs = term_bufs[number : number + len(terms)]
            number += len(terms)
            lead = part_shapes[job][:-2]
            size = 1
            for extent in lead:
                size *= extent

            def one(flat, carry, bufs=bufs, lead=lead, target=sum_bufs[job]):
                index, left = [], flat
                for extent in reversed(lead):
                    index.append(lax.rem(left, extent))
                    left = lax.div(left, extent)
                index = tuple(reversed(index))
                total = bufs[0][index].astype(F32)
                for buf in bufs[1:]:
                    total = total + buf[index].astype(F32)
                target[index] = total.astype(target.dtype)
                return carry

            lax.fori_loop(0, size, one, 0)
            stores.append(copy_of(sum_bufs[job], outs[out].at[place], osem.at[job]))
            stores[-1].start()
        for copy in stores:
            copy.wait()

    scratch = [pltpu.VMEM(part_shapes[job], array.dtype) for job, (terms, _, _) in enumerate(jobs) for array, _ in terms]
    scratch += [pltpu.VMEM(part_shapes[job], shapes[out].dtype) for job, (_, out, _) in enumerate(jobs)]
    scratch += [pltpu.SemaphoreType.DMA((count,)), pltpu.SemaphoreType.DMA((len(jobs),))]
    return pl.pallas_call(
        kernel,
        out_shape=list(shapes),
        in_specs=[ANY] * len(arrays),
        out_specs=[ANY] * len(shapes),
        scratch_shapes=scratch,
        compiler_params=params(),
        cost_estimate=cost_of(3),
        name="combine",
    )(*arrays)


def swap_pairs(count, mask):
    return [(i, i ^ mask) for i in range(count)]


def to_sibling(values):
    return lax.ppermute(values, "tensor", swap_pairs(4, 1))


def over_y(values):
    return lax.ppermute(values, "tensor", swap_pairs(4, 2))


def over_dp(values, mask):
    return lax.ppermute(values, "dp", swap_pairs(8, mask))


def over_x(values):
    return over_dp(values, 1)


def over_z_near(values):
    return over_dp(values, 2)


def over_z_far(values):
    return over_dp(values, 4)


def after(values, *earlier):
    return lax.optimization_barrier((values, *earlier))[0]


MOVES = {"y": over_y, "x": over_x, "z": over_z_near}


class Reduction:
    def __init__(self, sent, portions):
        self.other = to_sibling(sent)
        self.portions, self.stage, self.sends, self.total = portions, 0, None, None

    def begin(self, kept, *earlier):
        other = after(self.other, *earlier)
        split = (kept.shape[0], 2, 2, 2, 2, *kept.shape[3:])
        arrays = (kept.reshape(split), other.reshape(split))
        self.blocks, self.tail = kept.shape[0], kept.shape[3:]
        self.terms = [[(array, ("b", "y", "x", "z", "w"), low, {}) for array in arrays] for low, _, _ in self.portions]

    def receive(self, *earlier):
        if self.stage == 4:
            moved = after(over_z_far(self.sends[0]), *earlier)
            for (low, _, _), terms in zip(self.portions, self.terms):
                terms.append((moved, ("b",), low, {}))
        elif self.stage:
            for send, (_, _, orders), terms in zip(self.sends, self.portions, self.terms):
                left = tuple(a for a in ("b", "y", "x", "z", "w") if a not in orders[: self.stage])
                terms.append((after(MOVES[orders[self.stage - 1]](send), *earlier), left, 0, {}))

    def jobs(self, first_out):
        jobs, shapes = [], []
        stage = self.stage
        for number, ((low, high, orders), terms) in enumerate(zip(self.portions, self.terms)):
            axis = (*orders, "w", None)[stage]
            picked = []
            for array, axes, start, fixed in terms:
                index = [slice(start, start + high - low)]
                for name in axes[1:]:
                    index.append(1 if name == axis else fixed.get(name, 0 if name in orders[:stage] or (stage > 3 and name == "w") else slice(None)))
                picked.append((array, tuple(index)))
            if stage < 3:
                left = 3 - stage + 1 - 1
                shapes.append(sds((high - low, *(2,) * left, *self.tail), BF16))
                jobs.append((picked, first_out + number, slice(0, high - low)))
            else:
                if not number:
                    shapes.append(sds((self.blocks, *self.tail), BF16 if stage == 3 else F32))
                jobs.append((picked, first_out, slice(low, high)))
        self.stage += 1
        return jobs, shapes


def advance(reductions, *earlier):
    jobs, shapes, bounds = [], [], []
    for reduction in reductions:
        reduction.receive(*earlier)
        more, made = reduction.jobs(len(shapes))
        bounds.append((len(shapes), len(shapes) + len(made)))
        jobs, shapes = jobs + more, shapes + made
    results = combine(jobs, shapes)
    for reduction, (low, high) in zip(reductions, bounds):
        reduction.sends = list(results[low:high])
        if reduction.stage == 5:
            reduction.total = results[low]
    return list(results)


def sentence_body(
    tokens,
    memory,
    dec_lengths,
    mem_lengths,
    self_qkv,
    self_out,
    cross_q,
    cross_kv,
    cross_out,
    ffn_in,
    ffn_out,
    norm_gains,
    norm_biases,
    cotangent,
):
    dp = lax.axis_index("dp")
    mine = lax.axis_index("tensor")
    order = dp & 3
    self_scalars = jnp.stack([dec_lengths[0, mine], order, dp, mine]).astype(jnp.int32)
    cross_scalars = jnp.stack([mem_lengths[0, mine], order, dp, mine]).astype(jnp.int32)
    gains = [norm_gains[i : i + 1] for i in range(3)]
    biases = [norm_biases[i : i + 1] for i in range(3)]

    def quarter_rows(values):
        rows = values.shape[-2] // 4
        return lax.dynamic_slice_in_dim(values, order * rows, rows, values.ndim - 2)

    def folded(values):
        blocks = values.reshape(values.shape[0], 4, 2 * UNIT)
        return blocks.transpose(1, 0, 2).reshape(1, 4 * values.shape[0], 2 * UNIT)

    self_near = over_y(jnp.concatenate([quarter_rows(self_qkv), folded(quarter_rows(self_out))]))
    cross_near = over_y(
        jnp.concatenate([quarter_rows(cross_q)[None], quarter_rows(cross_kv), folded(quarter_rows(cross_out))])
    )
    ffn_near = over_y(jnp.stack([quarter_rows(ffn_in), quarter_rows(ffn_out)]))
    self_own = (self_qkv, self_out)
    self_sib = tuple(to_sibling(w) for w in self_own)
    self_side, self_up = over_x(self_near), over_z_near(self_near)
    self_a = attention_fwd_call(after(self_scalars, self_near), [], [tokens], [self_own, self_sib], None, None)
    self_side, self_up, cross_near = (after(w, self_a[4]) for w in (self_side, self_up, cross_near))
    self_corner = over_x(self_up)
    cross_side, cross_up = over_x(cross_near), over_z_near(cross_near)
    self_rest = jnp.stack([after(self_near, cross_near), self_side, self_up, self_corner])
    self_far = to_sibling(self_rest)
    self_pieces = [self_own, self_sib, (self_rest,), (self_far,)]
    self_b = attention_fwd_call(
        after(self_scalars, cross_near), [tokens], [tokens], self_pieces[2:], self_a[5], (gains[0], biases[0])
    )
    first_low, first_hat, first_inv = self_b[5:]
    cross_own = (cross_q, cross_kv, cross_out)
    cross_sib = tuple(to_sibling(after(w, self_near)) for w in cross_own)
    ffn_own = (ffn_in, ffn_out)
    ffn_sib = tuple(to_sibling(after(w, self_near)) for w in ffn_own)
    cross_in = [first_low, memory]
    cross_corner = over_x(cross_up)
    cross_rest = jnp.stack([cross_near, cross_side, cross_up, after(cross_corner, self_b[4], ffn_near)])
    cross_far = to_sibling(cross_rest)
    ffn_side, ffn_up = over_x(ffn_near), over_z_near(ffn_near)
    cross_pieces = [cross_own, cross_sib, (cross_rest,), (cross_far,)]
    cross_b = attention_fwd_call(
        cross_scalars, [first_hat, gains[0], biases[0]], cross_in, cross_pieces, None, (gains[1], biases[1])
    )
    second_low, second_hat, second_inv = cross_b[5:]
    ffn_side, ffn_up = after(ffn_side, cross_b[4]), after(ffn_up, cross_b[4])
    up_corner, down_corner = over_x(ffn_up[:1]), over_z_near(ffn_side[1:])
    ffn_pieces = [ffn_own, ffn_sib]
    ffn_a = ffn_fwd_call(cross_scalars, second_low, ffn_pieces, None, None)
    up_corner, down_corner = after(up_corner, ffn_a[0]), after(down_corner, ffn_a[0])
    ffn_rest = (ffn_near, ffn_side, ffn_up, up_corner, down_corner)
    ffn_pieces += [ffn_rest, tuple(to_sibling(w) for w in ffn_rest)]
    ffn_b = ffn_fwd_call(
        cross_scalars, second_low, ffn_pieces[2:], ffn_a[0],
        (second_hat, gains[1], biases[1], cotangent, gains[2], biases[2]),
    )
    out_rows, third_low, third_scaled, third_gain, third_bias = ffn_b[:5]

    def plan_of(pieces):
        return [(piece // 2, 2 * (piece % 2) + half) for piece in pieces for half in (0, 1)]

    ffn_saved = [ffn_a[1:3], ffn_b[5:7]]
    ffn_d = ffn_bwd_call(
        cross_scalars, third_low, second_low, ffn_pieces[1::2], ffn_saved, plan_of((1, 3)), third_scaled, None
    )
    ffn_sum = Reduction(ffn_d[1], [(0, 3, "yxz"), (3, 6, "xzy"), (6, 8, "zyx")])
    ffn_e = ffn_bwd_call(
        cross_scalars, third_low, second_low, ffn_pieces[::2], ffn_saved, plan_of((0, 2)), ffn_d[0],
        (second_hat, second_inv, gains[1]),
    )
    second_back, second_scaled, second_gain, second_bias = ffn_e[:4]
    ffn_sum.begin(ffn_e[4], second_gain)
    second_back = after(second_back, *advance([ffn_sum]))

    cross_e = attention_bwd_call(
        cross_scalars, second_back, cross_in, cross_pieces[1::2] + cross_pieces[::2], [cross_b[:5]],
        [(0, 2 * p + h) for p in (1, 3, 0, 2) for h in (0, 1)], second_scaled,
        (first_hat, first_inv, gains[0]), 2,
    )
    first_back, first_scaled, first_gain, first_bias, memory_part = cross_e[:5]
    norm_sums = jnp.stack([first_gain, second_gain, third_gain, first_bias, second_bias, third_bias])
    norm_sums = jnp.concatenate([jnp.sum(norm_sums, axis=1), jnp.zeros((2, norm_sums.shape[2]), F32)])
    norm_sums = lax.all_gather(norm_sums, ("dp", "tensor"), axis=0)
    sends = advance([ffn_sum], first_gain)
    cross_sum = Reduction(after(cross_e[5], *sends), [(0, 4, "xzy"), (4, 8, "yxz")])
    first_back = after(first_back, *sends)

    self_saved = [self_a[:5], self_b[:5]]
    self_d = attention_bwd_call(
        self_scalars, first_back, [tokens], self_pieces[1::2], self_saved, plan_of((1, 3)), None, None
    )
    cross_sum.begin(cross_e[6], self_d[0])
    sends = advance([cross_sum, ffn_sum], self_d[0])
    self_sum = Reduction(after(self_d[1], *sends), [(0, 4, "xzy"), (4, 8, "yxz")])
    first_back = after(first_back, *sends)
    self_e = attention_bwd_call(
        self_scalars, first_back, [tokens], self_pieces[::2], self_saved, plan_of((0, 2)), None, None
    )
    self_sum.begin(self_e[1], self_e[0])
    sends = advance([self_sum])
    grad_tokens, grad_memory = inputs_back_call(
        self_scalars, after(first_scaled, *sends),
        [(self_d[0], self_pieces[1::2]), (self_e[0], self_pieces[::2])],
        (memory_part, cross_pieces[1::2] + cross_pieces[::2]),
    )
    sends = advance([cross_sum, ffn_sum], *sends)
    sends = advance([self_sum, cross_sum], *sends, grad_tokens)
    sends = advance([self_sum, cross_sum, ffn_sum], *sends)
    sends = advance([self_sum, cross_sum], *sends)
    sends = advance([self_sum], *sends)
    norm_total = jnp.sum(after(norm_sums, *sends), axis=0)
    self_sum, cross_sum, ffn_sum = self_sum.total, cross_sum.total, ffn_sum.total

    def matrices(total):
        return total.reshape(2, 4, UNIT, UNIT).transpose(1, 2, 0, 3).reshape(4, UNIT, 2 * UNIT)

    self_grads, cross_grads = matrices(self_sum), matrices(cross_sum)
    ffn_grads = ffn_sum.reshape(4, 2, UNIT, FFN_PART).transpose(1, 2, 0, 3).reshape(2, UNIT, -1)
    return (
        out_rows,
        grad_tokens,
        grad_memory,
        self_grads[:3],
        self_grads[3].T,
        cross_grads[0],
        cross_grads[1:3],
        cross_grads[3].T,
        ffn_grads[0],
        ffn_grads[1].T,
        norm_total[:3],
        norm_total[3:6],
    )


def sentence_fits(mesh, tokens, memory, dec_lengths):
    shape = dict(mesh.shape)
    rows = tokens.shape[0] // mesh.size
    sentences = dec_lengths.shape[1]
    return (
        shape["tensor"] == 4
        and shape["dp"] == 8
        and sentences == 4
        and rows == 512
        and memory.shape[0] // mesh.size == rows
        and tokens.shape[1] == 1024
    )


def smooth_gate(values):
    return jax.nn.gelu(values, approximate=True)


def norm_rows(hidden, norm_gain, norm_bias):
    center = hidden - jnp.mean(hidden, axis=-1, keepdims=True)
    inverse = lax.rsqrt(jnp.mean(center * center, axis=-1, keepdims=True) + NORM_EPSILON)
    normed = center * inverse
    return (normed * norm_gain + norm_bias, normed, inverse)


def norm_back(gradient, normed, inverse, norm_gain):
    scaled = gradient * norm_gain
    grad_in = inverse * (
        scaled
        - jnp.mean(scaled, axis=-1, keepdims=True)
        - normed * jnp.mean(scaled * normed, axis=-1, keepdims=True)
    )
    return (grad_in, jnp.sum(gradient * normed, axis=0), jnp.sum(gradient, axis=0))


def head_view(values, sentences):
    return values.reshape(sentences, -1, values.shape[1] // HEAD_DIM, HEAD_DIM)


def masked_scores(query_heads, key_heads, key_mask):
    scores = jnp.einsum(
        "sqhe,skhe->shqk", query_heads, key_heads, preferred_element_type=jnp.float32
    ) * HEAD_DIM ** (-0.5)
    return jnp.where(key_mask, scores, MASKED_SCORE)


def attention_forward(query_rows, key_rows, value_rows, key_mask, sentences):
    scores = masked_scores(
        head_view(query_rows, sentences), head_view(key_rows, sentences), key_mask
    )
    row_peak = jnp.max(scores, axis=-1, keepdims=True)
    exponent_terms = jnp.exp(scores - row_peak)
    row_sum = jnp.sum(exponent_terms, axis=-1, keepdims=True)
    softmax_probs = exponent_terms / row_sum
    attended = jnp.einsum(
        "shqk,skhe->sqhe",
        softmax_probs.astype(jnp.bfloat16),
        head_view(value_rows, sentences),
        preferred_element_type=jnp.float32,
    ).astype(jnp.bfloat16)
    return (attended.reshape(query_rows.shape), row_peak + jnp.log(row_sum))


def attention_backward(query_rows, key_rows, value_rows, key_mask, log_total, grad_rows, sentences):
    query_heads = head_view(query_rows, sentences)
    key_heads = head_view(key_rows, sentences)
    value_heads = head_view(value_rows, sentences)
    grad_heads = head_view(grad_rows, sentences)
    softmax_probs = jnp.exp(masked_scores(query_heads, key_heads, key_mask) - log_total)
    grad_probs = jnp.einsum(
        "sqhe,skhe->shqk", grad_heads, value_heads, preferred_element_type=jnp.float32
    )
    row_delta = jnp.sum(softmax_probs * grad_probs, axis=-1, keepdims=True)
    grad_scores = (softmax_probs * (grad_probs - row_delta)).astype(jnp.bfloat16)
    score_scale = HEAD_DIM ** (-0.5)
    grad_query = (
        jnp.einsum("shqk,skhe->sqhe", grad_scores, key_heads, preferred_element_type=jnp.float32)
        * score_scale
    ).astype(jnp.bfloat16)
    grad_key = (
        jnp.einsum("shqk,sqhe->skhe", grad_scores, query_heads, preferred_element_type=jnp.float32)
        * score_scale
    ).astype(jnp.bfloat16)
    grad_value = jnp.einsum(
        "shqk,sqhe->skhe",
        softmax_probs.astype(jnp.bfloat16),
        grad_heads,
        preferred_element_type=jnp.float32,
    ).astype(jnp.bfloat16)
    return (
        grad_query.reshape(query_rows.shape),
        grad_key.reshape(key_rows.shape),
        grad_value.reshape(value_rows.shape),
    )


def body(
    tokens,
    memory,
    dec_lengths,
    mem_lengths,
    self_qkv,
    self_out,
    cross_q,
    cross_kv,
    cross_out,
    ffn_in,
    ffn_out,
    norm_gains,
    norm_biases,
    cotangent,
):
    row_share = tokens.shape[0]
    sentences = dec_lengths.shape[1]
    all_tokens, all_memory = (
        lax.all_gather(tokens, "tensor", axis=0, tiled=True),
        lax.all_gather(memory, "tensor", axis=0, tiled=True),
    )
    sentence_len = all_tokens.shape[0] // sentences
    memory_len = all_memory.shape[0] // sentences
    positions = jnp.arange(sentence_len, dtype=jnp.int32)
    self_mask = (
        (positions[None, :] <= positions[:, None])[None]
        & (positions[None, None, :] < dec_lengths[0][:, None, None])
    )[:, None]
    memory_positions = jnp.arange(memory_len, dtype=jnp.int32)
    cross_mask = (memory_positions[None, :] < mem_lengths[0][:, None])[:, None, None, :]

    def branch_rows(attended, weight):
        return lax.psum_scatter(
            jnp.dot(attended, weight, preferred_element_type=jnp.float32).astype(jnp.bfloat16),
            "tensor",
            scatter_dimension=0,
            tiled=True,
        ).astype(jnp.float32)

    def branch_grad(grad_rows, attended, weight):
        grad_low = grad_rows.astype(jnp.bfloat16)
        grad_all = lax.all_gather(grad_low, "tensor", axis=0, tiled=True)
        grad_attended = jnp.dot(grad_all, weight.T, preferred_element_type=jnp.float32).astype(
            jnp.bfloat16
        )
        weight_part = jnp.dot(attended.T, grad_all, preferred_element_type=jnp.float32)
        return (grad_attended, weight_part)

    def gather_normed(values):
        return lax.all_gather(values, "tensor", axis=0, tiled=True)

    def head_input_sum(term):
        return lax.psum_scatter(
            term(jnp.int32(0), row_share * lax.axis_size("tensor")).astype(jnp.bfloat16),
            "tensor",
            scatter_dimension=0,
            tiled=True,
        ).astype(jnp.float32)

    self_proj = jnp.einsum(
        "td,cde->cte", all_tokens, self_qkv, preferred_element_type=jnp.float32
    ).astype(jnp.bfloat16)
    self_att, self_lse = attention_forward(
        self_proj[0], self_proj[1], self_proj[2], self_mask, sentences
    )
    self_branch = branch_rows(self_att, self_out)
    first_norm, first_hat, first_inv = norm_rows(
        RESIDUAL_ALPHA * tokens.astype(jnp.float32) + self_branch, norm_gains[0], norm_biases[0]
    )
    first_all = gather_normed(first_norm.astype(jnp.bfloat16))
    cross_query = jnp.dot(first_all, cross_q, preferred_element_type=jnp.float32).astype(
        jnp.bfloat16
    )
    cross_proj = jnp.einsum(
        "td,cde->cte", all_memory, cross_kv, preferred_element_type=jnp.float32
    ).astype(jnp.bfloat16)
    cross_att, cross_lse = attention_forward(
        cross_query, cross_proj[0], cross_proj[1], cross_mask, sentences
    )
    cross_branch = branch_rows(cross_att, cross_out)
    second_norm, second_hat, second_inv = norm_rows(
        RESIDUAL_ALPHA * first_norm + cross_branch, norm_gains[1], norm_biases[1]
    )
    second_all = gather_normed(second_norm.astype(jnp.bfloat16))
    pre_gate = jnp.dot(second_all, ffn_in, preferred_element_type=jnp.float32)
    activated = smooth_gate(pre_gate).astype(jnp.bfloat16)
    ffn_branch = lax.psum_scatter(
        jnp.dot(activated, ffn_out, preferred_element_type=jnp.float32).astype(jnp.bfloat16),
        "tensor",
        scatter_dimension=0,
        tiled=True,
    ).astype(jnp.float32)
    out_rows, third_hat, third_inv = norm_rows(
        RESIDUAL_ALPHA * second_norm + ffn_branch, norm_gains[2], norm_biases[2]
    )
    grad_third, third_gain, third_bias = norm_back(
        cotangent.astype(jnp.float32), third_hat, third_inv, norm_gains[2]
    )
    grad_ffn_all = lax.all_gather(grad_third.astype(jnp.bfloat16), "tensor", axis=0, tiled=True)
    unused_gate, gate_pull = jax.vjp(smooth_gate, pre_gate)
    grad_act = gate_pull(jnp.dot(grad_ffn_all, ffn_out.T, preferred_element_type=jnp.float32))[
        0
    ].astype(jnp.bfloat16)
    grad_ffn_out = jnp.dot(activated.T, grad_ffn_all, preferred_element_type=jnp.float32)
    grad_ffn_in = jnp.dot(second_all.T, grad_act, preferred_element_type=jnp.float32)
    grad_second = RESIDUAL_ALPHA * grad_third + lax.psum_scatter(
        jnp.dot(grad_act, ffn_in.T, preferred_element_type=jnp.float32).astype(jnp.bfloat16),
        "tensor",
        scatter_dimension=0,
        tiled=True,
    ).astype(jnp.float32)
    grad_second_in, second_gain, second_bias = norm_back(
        grad_second, second_hat, second_inv, norm_gains[1]
    )
    grad_cross_att, cross_out_part = branch_grad(grad_second_in, cross_att, cross_out)
    grad_cq, grad_ck, grad_cv = attention_backward(
        cross_query, cross_proj[0], cross_proj[1], cross_mask, cross_lse, grad_cross_att, sentences
    )
    grad_cross_q = jnp.dot(first_all.T, grad_cq, preferred_element_type=jnp.float32)
    cross_grads = jnp.stack([grad_ck, grad_cv])
    grad_cross_kv = jnp.einsum(
        "td,cte->cde", all_memory, cross_grads, preferred_element_type=jnp.float32
    )
    grad_memory = lax.psum_scatter(
        jnp.einsum("cte,cde->td", cross_grads, cross_kv, preferred_element_type=jnp.float32).astype(
            jnp.bfloat16
        ),
        "tensor",
        scatter_dimension=0,
        tiled=True,
    ).astype(jnp.float32)

    def cross_input_term(first_row, row_total):
        return jnp.dot(grad_cq, cross_q.T, preferred_element_type=jnp.float32)

    cross_input = head_input_sum(cross_input_term)
    grad_first = RESIDUAL_ALPHA * grad_second_in + cross_input
    grad_first_in, first_gain, first_bias = norm_back(
        grad_first, first_hat, first_inv, norm_gains[0]
    )
    grad_self_att, self_out_part = branch_grad(grad_first_in, self_att, self_out)
    grad_sq, grad_sk, grad_sv = attention_backward(
        self_proj[0], self_proj[1], self_proj[2], self_mask, self_lse, grad_self_att, sentences
    )
    self_grads = jnp.stack([grad_sq, grad_sk, grad_sv])
    grad_self_qkv = jnp.einsum(
        "td,cte->cde", all_tokens, self_grads, preferred_element_type=jnp.float32
    )

    def self_input_term(first_row, row_total):
        return jnp.einsum("cte,cde->td", self_grads, self_qkv, preferred_element_type=jnp.float32)

    self_input = head_input_sum(self_input_term)
    grad_tokens = RESIDUAL_ALPHA * grad_first_in + self_input
    summed = (
        lax.psum_scatter(
            grad_self_qkv.astype(jnp.bfloat16), "dp", scatter_dimension=1, tiled=True
        ).astype(jnp.float32),
        lax.psum_scatter(
            self_out_part.astype(jnp.bfloat16), "dp", scatter_dimension=1, tiled=True
        ).astype(jnp.float32),
        lax.psum_scatter(
            grad_cross_q.astype(jnp.bfloat16), "dp", scatter_dimension=0, tiled=True
        ).astype(jnp.float32),
        lax.psum_scatter(
            grad_cross_kv.astype(jnp.bfloat16), "dp", scatter_dimension=1, tiled=True
        ).astype(jnp.float32),
        lax.psum_scatter(
            cross_out_part.astype(jnp.bfloat16), "dp", scatter_dimension=1, tiled=True
        ).astype(jnp.float32),
        lax.psum_scatter(
            grad_ffn_in.astype(jnp.bfloat16), "dp", scatter_dimension=0, tiled=True
        ).astype(jnp.float32),
        lax.psum_scatter(
            grad_ffn_out.astype(jnp.bfloat16), "dp", scatter_dimension=1, tiled=True
        ).astype(jnp.float32),
    )
    gain_total, bias_total = lax.psum(
        (
            jnp.stack([first_gain, second_gain, third_gain]),
            jnp.stack([first_bias, second_bias, third_bias]),
        ),
        ("dp", "tensor"),
    )
    return (
        out_rows.astype(jnp.bfloat16),
        grad_tokens,
        grad_memory,
        summed[0],
        summed[1],
        summed[2],
        summed[3],
        summed[4],
        summed[5],
        summed[6],
        gain_total,
        bias_total,
    )


def solution(mesh):
    in_specs = (
        P(("dp", "tensor"), None),
        P(("dp", "tensor"), None),
        P("dp", None),
        P("dp", None),
        P(None, None, "tensor"),
        P("tensor", None),
        P(None, "tensor"),
        P(None, None, "tensor"),
        P("tensor", None),
        P(None, "tensor"),
        P("tensor", None),
        P(),
        P(),
        P(("dp", "tensor"), None),
    )
    out_specs = (
        P(("dp", "tensor"), None),
        P(("dp", "tensor"), None),
        P(("dp", "tensor"), None),
        P(None, "dp", "tensor"),
        P("tensor", "dp"),
        P("dp", "tensor"),
        P(None, "dp", "tensor"),
        P("tensor", "dp"),
        P("dp", "tensor"),
        P("tensor", "dp"),
        P(),
        P(),
    )

    def step(*args):
        chosen = sentence_body if sentence_fits(mesh, args[0], args[1], args[2]) else body
        return jax.shard_map(
            chosen, mesh=mesh, in_specs=in_specs, out_specs=out_specs, check_vma=False
        )(*args)

    return step
```

```python
import functools
import jax
import jax.numpy as jnp
from jax import lax
from jax.experimental import pallas as pl
from jax.experimental.pallas import tpu as pltpu
from jax.sharding import PartitionSpec as P

HEAD_DIM = 64
RESIDUAL_ALPHA = 4.16
NORM_EPSILON = 1e-05
MASKED_SCORE = -1000000000.0
SCORE_SCALE = HEAD_DIM ** (-0.5)
UNIT = 128
QUERY_BLOCK = 256
FFN_UNIT = 512
ROW_CHUNK = 64
BF16 = jnp.bfloat16
F32 = jnp.float32


def dot(left, right):
    return lax.dot_general(left, right, (((1,), (0,)), ((), ())), preferred_element_type=F32)


def dot_tn(left, right):
    return lax.dot_general(left, right, (((0,), (0,)), ((), ())), preferred_element_type=F32)


def dot_nt(left, right):
    return lax.dot_general(left, right, (((1,), (1,)), ((), ())), preferred_element_type=F32)


def shard_of(position):
    return ((position >> 2) & 1) | (position & 2) | ((position & 1) << 2)


def copy_of(source, target, sem):
    return pltpu.make_async_copy(source, target, sem)


def own_lanes(rows, head):
    lanes = lax.broadcasted_iota(jnp.int32, rows.shape, 1)
    return jnp.where((lanes >= HEAD_DIM) if head else (lanes < HEAD_DIM), rows, 0.0)


def extended_keys(keys, length):
    lanes = lax.broadcasted_iota(jnp.int32, keys.shape, 1)
    rows = lax.broadcasted_iota(jnp.int32, keys.shape, 0)
    mask = jnp.where((lanes == 0) & (rows >= length), MASKED_SCORE, 0.0).astype(BF16)
    keys = keys.astype(F32)
    return [jnp.concatenate([own_lanes(keys, head).astype(BF16), mask], axis=1) for head in (0, 1)]


def extended_query(query):
    lanes = lax.broadcasted_iota(jnp.int32, query.shape, 1)
    return jnp.concatenate([query, jnp.where(lanes == 0, 1.0, 0.0).astype(BF16)], axis=1)


def fill_diagonal(diagonal):
    keys = lax.broadcasted_iota(jnp.int32, diagonal.shape, 0)
    queries = lax.broadcasted_iota(jnp.int32, diagonal.shape, 1)
    diagonal[...] = jnp.where(keys <= queries, 0.0, MASKED_SCORE)


def key_ranges(block, keys, causal):
    if not causal:
        return [(0, keys)]
    return [(low, low + QUERY_BLOCK) for low in range(0, (block + 1) * QUERY_BLOCK, QUERY_BLOCK)]


def attend_unit(query, keys, values, length, causal, diagonal, lse_ref):
    rows, count = query.shape[0], keys.shape[0]
    values_t = jnp.transpose(values.astype(F32)).astype(BF16)
    wide_keys, wide_query = extended_keys(keys, length), extended_query(query)
    items = [(head, block) for block in range(rows // QUERY_BLOCK) for head in (0, 1)]
    scores, probs, totals, mixed = {}, {}, {}, {}
    for head, block in items:
        part = wide_query[block * QUERY_BLOCK : (block + 1) * QUERY_BLOCK]
        ranges = key_ranges(block, count, causal)
        scores[head, block] = [dot_nt(wide_keys[head][a:b], part) for a, b in ranges]
        if causal:
            scores[head, block][-1] = scores[head, block][-1] + diagonal[...]
    for head, block in items:
        pieces = scores[head, block]
        peak = functools.reduce(jnp.maximum, [jnp.max(p, axis=0, keepdims=True) for p in pieces])
        terms = [jnp.exp(p - peak) for p in pieces]
        total = sum(jnp.sum(t, axis=0, keepdims=True) for t in terms)
        at = slice(block * QUERY_BLOCK, (block + 1) * QUERY_BLOCK)
        lse_ref[head : head + 1, at] = peak + jnp.log(total)
        totals[head, block] = total
        probs[head, block] = jnp.concatenate([t.astype(BF16) for t in terms], axis=0)
    for head, block in items:
        own = values_t[head * HEAD_DIM : (head + 1) * HEAD_DIM, : probs[head, block].shape[0]]
        mixed[head, block] = dot(own, probs[head, block]) / totals[head, block]
    out = [
        jnp.transpose(jnp.concatenate([mixed[0, block], mixed[1, block]], axis=0))
        for block in range(rows // QUERY_BLOCK)
    ]
    return jnp.concatenate(out, axis=0).astype(BF16)


def attend_back_unit(query, keys, values, attended, grad, length, causal, diagonal, lse_ref):
    rows, count = query.shape[0], keys.shape[0]
    blocks = range(rows // QUERY_BLOCK)
    query_f, keys_f, grad_f = (a.astype(F32) for a in (query, keys, grad))
    wide_keys, wide_query = extended_keys(keys, length), extended_query(query)
    delta = jnp.transpose(grad_f * attended.astype(F32))
    deltas = [
        jnp.sum(delta[head * HEAD_DIM : (head + 1) * HEAD_DIM], axis=0, keepdims=True)
        for head in (0, 1)
    ]
    keys_t = jnp.transpose(keys_f).astype(BF16)
    query_own = [own_lanes(query_f, head).astype(BF16) for head in (0, 1)]
    grad_own = [own_lanes(grad_f, head).astype(BF16) for head in (0, 1)]
    items = [(head, block) for block in blocks for head in (0, 1)]
    scores, slopes, probs, back, grad_query = {}, {}, {}, {}, {}
    for head, block in items:
        at = slice(block * QUERY_BLOCK, (block + 1) * QUERY_BLOCK)
        for a, b in key_ranges(block, count, causal):
            scores[head, block, a] = dot_nt(wide_keys[head][a:b], wide_query[at])
            slopes[head, block, a] = dot_nt(values[a:b], grad_own[head][at])
    for head, block in items:
        at = slice(block * QUERY_BLOCK, (block + 1) * QUERY_BLOCK)
        ranges = key_ranges(block, count, causal)
        for a, b in ranges:
            score = scores[head, block, a]
            if causal and (a, b) == ranges[-1]:
                score = score + diagonal[...]
            prob = jnp.exp(score - lse_ref[head : head + 1, at])
            probs[head, block, a] = prob.astype(BF16)
            back[head, block, a] = (prob * (slopes[head, block, a] - deltas[head][:, at])).astype(BF16)
    for head, block in items:
        own = keys_t[head * HEAD_DIM : (head + 1) * HEAD_DIM]
        grad_query[head, block] = sum(
            dot(own[:, a:b], back[head, block, a]) for a, b in key_ranges(block, count, causal)
        )
    grad_keys, grad_values = [], []
    for low in sorted({key[2] for key in back}):
        live = [key for key in back if key[2] == low]
        at = [slice(block * QUERY_BLOCK, (block + 1) * QUERY_BLOCK) for _, block, _ in live]
        grad_values.append(
            dot(
                jnp.concatenate([probs[key] for key in live], axis=1),
                jnp.concatenate([grad_own[key[0]][a] for key, a in zip(live, at)], axis=0),
            )
        )
        grad_keys.append(
            dot(
                jnp.concatenate([back[key] for key in live], axis=1),
                jnp.concatenate([query_own[key[0]][a] for key, a in zip(live, at)], axis=0),
            )
        )
    grad_query = [
        jnp.transpose(jnp.concatenate([grad_query[0, block], grad_query[1, block]], axis=0)) * SCORE_SCALE
        for block in blocks
    ]
    return tuple(
        jnp.concatenate(parts, axis=0).astype(BF16) for parts in (grad_query, grad_keys, grad_values)
    )


def norm_chunk(hidden, gain, bias):
    center = hidden - jnp.mean(hidden, axis=-1, keepdims=True)
    inverse = lax.rsqrt(jnp.mean(center * center, axis=-1, keepdims=True) + NORM_EPSILON)
    normed = center * inverse
    return normed * gain + bias, normed, inverse


def norm_back_chunk(gradient, normed, inverse, gain):
    scaled = gradient * gain
    return inverse * (
        scaled
        - jnp.mean(scaled, axis=-1, keepdims=True)
        - normed * jnp.mean(scaled * normed, axis=-1, keepdims=True)
    )


def fold_rows(values):
    return jnp.sum(values.reshape(values.shape[0] // 8, 8, values.shape[1]), axis=0)


def each_chunk(rows, body):
    def step(index, carry):
        body(pl.ds(pl.multiple_of(index * ROW_CHUNK, ROW_CHUNK), ROW_CHUNK))
        return carry

    lax.fori_loop(0, rows // ROW_CHUNK, step, 0)


def store_shards(target, weight, dp):
    for block in range(8):
        target[shard_of(block ^ dp)] = weight[block * UNIT : (block + 1) * UNIT]


SMEM = pl.BlockSpec(memory_space=pltpu.SMEM)
VMEM = pl.BlockSpec(memory_space=pltpu.VMEM)
ANY = pl.BlockSpec(memory_space=pl.ANY)


def params(limit=62):
    return pltpu.CompilerParams(vmem_limit_bytes=limit * 1024 * 1024)


def cost_of(microseconds):
    return pl.CostEstimate(flops=int(microseconds * 1.1e9), bytes_accessed=4 << 20, transcendentals=0)


def sds(shape, dtype):
    return jax.ShapeDtypeStruct(shape, dtype)


def weight_copies(pieces, sc, wbuf, obuf, wsem, osem, columns=(0, 1, 2)):
    groups, outs = [[], [], []], []
    wide = 2 * UNIT
    for index, refs in enumerate(pieces):
        at = slice(index * wide, (index + 1) * wide)
        if len(refs) > 1:
            column = 0
            for ref in refs[:-1]:
                for source in [ref] if len(ref.shape) == 2 else [ref.at[c] for c in range(ref.shape[0])]:
                    if column in columns:
                        low = (columns.index(column) * len(pieces) + index) * wide
                        groups[column].append(copy_of(source, wbuf.at[:, low : low + wide], wsem.at[column, index, 0]))
                    column += 1
            if obuf is not None:
                outs.append(copy_of(refs[-1], obuf.at[at, :], osem.at[index, 0]))
            continue
        rest, = refs
        rows = rest.shape[2]
        part = wide // rest.shape[0]
        for quarter in range(rest.shape[0]):
            place = quarter ^ (sc[1] if rest.shape[0] == 4 else sc[3])
            for column in columns:
                low = (columns.index(column) * len(pieces) + index) * wide
                groups[column].append(
                    copy_of(
                        rest.at[quarter, column],
                        wbuf.at[pl.ds(pl.multiple_of(place * rows, rows), rows), low : low + wide],
                        wsem.at[column, index, quarter],
                    )
                )
            for block in range(4 if obuf is not None else 0):
                outs.append(
                    copy_of(
                        rest.at[quarter, 3, block * part : (block + 1) * part, :],
                        obuf.at[pl.ds(pl.multiple_of(index * wide + place * part, part), part), block * wide : (block + 1) * wide],
                        osem.at[index, 4 * quarter + block],
                    )
                )
    return groups, outs


def attention_fwd_call(scalars, residual, others, pieces, partial, norm):
    rows, depth = others[0].shape
    causal = len(others) == 1
    number, wide = 2 * len(pieces), 2 * len(pieces) * UNIT
    last, has_partial = norm is not None, partial is not None

    def kernel(*refs):
        it = iter(refs)
        sc = next(it)
        in_refs = [next(it) for _ in others]
        gain_ref, bias_ref = (next(it), next(it)) if last else (None, None)
        old_rows = [next(it) for _ in residual[1:]] if last else []
        res_in = next(it) if last else None
        part_in = next(it) if has_partial else None
        w_refs = [[next(it) for _ in piece] for piece in pieces]
        q_ref, k_ref, v_ref, att_ref, lse_ref = (next(it) for _ in range(5))
        if last:
            low_ref, hat_ref, inv_ref = next(it), next(it), next(it)
        else:
            sum_ref = next(it)
        wbuf, obuf, att_all, diagonal, wsem, osem, lsem = (next(it) for _ in range(7))
        if last:
            acc, old = next(it), next(it)
        length = sc[0]
        groups, outs = weight_copies(w_refs, sc, wbuf, obuf, wsem, osem)
        for copies in groups + [outs]:
            for copy in copies:
                copy.start()
        target = acc if last else sum_ref
        late = []
        if has_partial:
            late.append(copy_of(part_in, target, lsem.at[0]))
        if last:
            late.append(copy_of(res_in, old, lsem.at[1]))
        for copy in late:
            copy.start()
        if causal:
            fill_diagonal(diagonal)
        for c, result in enumerate((q_ref, k_ref, v_ref)):
            for copy in groups[c]:
                copy.wait()
            rows_in = in_refs[0] if causal or c == 0 else in_refs[1]
            proj = dot(rows_in[...], wbuf[:, c * wide : (c + 1) * wide]).astype(BF16)
            if c == 0:
                proj = (proj.astype(F32) * SCORE_SCALE).astype(BF16)
            for index in range(number):
                result[index] = proj[:, index * UNIT : (index + 1) * UNIT]

        def step(u, carry):
            attended = attend_unit(q_ref[u], k_ref[u], v_ref[u], length, causal, diagonal, lse_ref.at[u])
            att_ref[u] = attended
            att_all[:, pl.ds(pl.multiple_of(u * UNIT, UNIT), UNIT)] = attended
            return carry

        lax.fori_loop(0, number, step, 0)
        for copy in outs + late:
            copy.wait()
        if has_partial:
            target[...] += dot(att_all[...], obuf[...])
        else:
            target[...] = dot(att_all[...], obuf[...])
        if last:
            def chunk(at):
                before = old[at, :].astype(F32)
                if old_rows:
                    before = before * old_rows[0][...] + old_rows[1][...]
                normed, hat, inverse = norm_chunk(RESIDUAL_ALPHA * before + acc[at, :], gain_ref[...], bias_ref[...])
                low_ref[at, :] = normed.astype(BF16)
                hat_ref[at, :] = hat
                inv_ref[at, :] = jnp.broadcast_to(inverse, (ROW_CHUNK, 128))

            each_chunk(rows, chunk)

    unit_rows = sds((number, rows, UNIT), BF16)
    shapes = [unit_rows] * 4 + [sds((number, 2, rows), F32)]
    if last:
        shapes += [sds((rows, depth), BF16), sds((rows, depth), F32), sds((rows, 128), F32)]
    else:
        shapes += [sds((rows, depth), F32)]
    args = [scalars, *others]
    if last:
        args += [*norm, *residual[1:]]
    tail = ([residual[0]] if last else []) + ([partial] if has_partial else [])
    tail += [array for piece in pieces for array in piece]
    scratch = [
        pltpu.VMEM((depth, 3 * wide), BF16),
        pltpu.VMEM((wide, depth), BF16),
        pltpu.VMEM((rows, wide), BF16),
        pltpu.VMEM((QUERY_BLOCK, QUERY_BLOCK), F32),
        pltpu.SemaphoreType.DMA((3, len(pieces), 4)),
        pltpu.SemaphoreType.DMA((len(pieces), 16)),
        pltpu.SemaphoreType.DMA((2,)),
    ]
    if last:
        scratch += [pltpu.VMEM((rows, depth), F32), pltpu.VMEM((rows, depth), residual[0].dtype)]
    return pl.pallas_call(
        kernel,
        out_shape=shapes,
        in_specs=[SMEM] + [VMEM] * (len(args) - 1) + [ANY] * len(tail),
        out_specs=[VMEM] * len(shapes),
        scratch_shapes=scratch,
        compiler_params=params(),
        cost_estimate=cost_of(0.6 * number),
        name="self_fwd" if causal else "cross_fwd",
    )(*args, *tail)


def attention_bwd_call(scalars, grad_low, others, pieces, saved, plan, carried, norm, results=1):
    rows, depth = grad_low.shape
    causal = len(others) == 1
    number, n_in, wide = len(plan), len(others), len(plan) * UNIT
    last = norm is not None
    skip = 1 if last else 0

    def kernel(*refs):
        it = iter(refs)
        sc = next(it)
        h_ref = next(it)
        in_refs = [next(it) for _ in range(n_in)]
        gain_ref = next(it) if last else None
        late_in = [next(it), next(it)] if last else []
        acc_in = next(it) if last else None
        w_refs = [[next(it) for _ in piece] for piece in pieces]
        s_refs = [[next(it) for _ in call] for call in saved]
        if last:
            low_ref, scaled_ref, gsum_ref, bsum_ref = (next(it) for _ in range(4))
        dall_ref = next(it)
        g_refs = [next(it) for _ in range(results)]
        wbuf, obuf, sbuf, lbuf, att_all, grad_all = (next(it) for _ in range(6))
        stage, diagonal = next(it), next(it)
        if last:
            dquery, acc, hat, inv = (next(it) for _ in range(4))
        wsem, osem, ssem, gsem, lsem = (next(it) for _ in range(5))
        length, dp = sc[0], sc[2]

        groups, o_copies = weight_copies(w_refs, sc, wbuf, obuf, wsem, osem, (0,) if last else ())
        for copy in o_copies:
            copy.start()
        s_copies = []
        for index, unit in enumerate(plan):
            lanes = slice(index * UNIT, (index + 1) * UNIT)
            call = s_refs[unit[0]]
            for c in range(3):
                s_copies.append(copy_of(call[c].at[unit[1]], sbuf.at[index, c], ssem.at[c, index]))
            s_copies.append(copy_of(call[3].at[unit[1]], att_all.at[:, lanes], ssem.at[3, index]))
            s_copies.append(copy_of(call[4].at[unit[1]], lbuf.at[index], ssem.at[4, index]))
        late = []
        if last:
            late = groups[0] + [
                copy_of(source, target, lsem.at[index])
                for index, (source, target) in enumerate(((acc_in, acc), (late_in[0], hat), (late_in[1], inv)))
            ]
        for copy in s_copies + late:
            copy.start()
        if causal:
            fill_diagonal(diagonal)
        for copy in o_copies:
            copy.wait()
        grad_att = dot_nt(h_ref[...], obuf[...]).astype(BF16)
        for index in range(number):
            grad_all[index] = grad_att[:, index * UNIT : (index + 1) * UNIT]
        for copy in s_copies:
            copy.wait()

        def step(u, carry):
            at = pl.ds(pl.multiple_of(u * UNIT, UNIT), UNIT)
            parts = attend_back_unit(
                sbuf[u, 0], sbuf[u, 1], sbuf[u, 2], att_all[:, at], grad_all[u], length, causal, diagonal, lbuf.at[u]
            )
            if last:
                dquery[:, at] = parts[0]
            for c in range(skip, 3):
                dall_ref[:, pl.ds(pl.multiple_of((c - skip) * wide + u * UNIT, UNIT), UNIT)] = parts[c]
            return carry

        lax.fori_loop(0, number, step, 0)

        share = number // 2 // results

        def keep(rows_in, source, column):
            weight = dot_tn(rows_in[...], source).astype(BF16)
            for index in range(number):
                piece = index // 2
                target = stage.at[piece // share, (index % 2) * 4 + column, piece % share]
                store_shards(target, weight[:, index * UNIT : (index + 1) * UNIT], dp)

        if last:
            keep(in_refs[0], dquery[...], 0)
        for c in range(skip, 3):
            keep(in_refs[-1], dall_ref[:, (c - skip) * wide : (c - skip + 1) * wide], c)
        keep(h_ref, att_all[...], 3)
        g_copies = [copy_of(stage.at[index], ref, gsem.at[index]) for index, ref in enumerate(g_refs)]
        for copy in g_copies:
            copy.start()
        for copy in late:
            copy.wait()
        if last:
            acc[...] += dot_nt(dquery[...], wbuf[...])
            norm_back_rows(acc, hat, inv, gain_ref, low_ref, scaled_ref, gsum_ref, bsum_ref, rows)
        for copy in g_copies:
            copy.wait()

    big = sds((rows, depth), F32)
    shapes = []
    if last:
        shapes += [sds((rows, depth), BF16), big, sds((8, depth), F32), sds((8, depth), F32)]
    shapes.append(sds((rows, (3 - skip) * wide), BF16))
    specs_out = [VMEM] * len(shapes) + [ANY] * results
    shapes += [sds((8, number // 2 // results, 8, UNIT, UNIT), BF16)] * results
    args = [scalars, grad_low, *others] + ([norm[2]] if last else [])
    tail = [norm[0], norm[1], carried] if last else []
    tail += [array for piece in pieces for array in piece]
    for call in saved:
        tail += call
    scratch = [
        pltpu.VMEM((depth, wide) if last else (16, 128), BF16),
        pltpu.VMEM((wide, depth), BF16),
        pltpu.VMEM((number, 3, rows, UNIT), BF16),
        pltpu.VMEM((number, 2, rows), F32),
        pltpu.VMEM((rows, wide), BF16),
        pltpu.VMEM((number, rows, UNIT), BF16),
        pltpu.VMEM((results, 8, number // 2 // results, 8, UNIT, UNIT), BF16),
        pltpu.VMEM((QUERY_BLOCK, QUERY_BLOCK), F32),
    ]
    if last:
        scratch += [pltpu.VMEM((rows, wide), BF16), pltpu.VMEM((rows, depth), F32), pltpu.VMEM((rows, depth), F32), pltpu.VMEM((rows, 128), F32)]
    scratch += [
        pltpu.SemaphoreType.DMA((3, len(pieces), 4)),
        pltpu.SemaphoreType.DMA((len(pieces), 16)),
        pltpu.SemaphoreType.DMA((5, number)),
        pltpu.SemaphoreType.DMA((results,)),
        pltpu.SemaphoreType.DMA((4,)),
    ]
    return pl.pallas_call(
        kernel,
        out_shape=shapes,
        in_specs=[SMEM] + [VMEM] * (len(args) - 1) + [ANY] * len(tail),
        out_specs=specs_out,
        scratch_shapes=scratch,
        compiler_params=params(),
        cost_estimate=cost_of(4.2 * number),
        name="self_bwd" if causal else "cross_bwd",
    )(*args, *tail)


def inputs_back_call(scalars, base, parts, memory_part):
    rows, depth = base.shape
    jobs = [(0, grad, pieces, (0, 1, 2)) for grad, pieces in parts] + [(1, *memory_part, (1, 2))]

    def kernel(*refs):
        it = iter(refs)
        sc, base_ref = next(it), next(it)
        grads = [next(it) for _ in jobs]
        w_refs = [[[next(it) for _ in piece] for piece in pieces] for _, _, pieces, _ in jobs]
        outs = [next(it), next(it)]
        bufs, sems = [next(it) for _ in jobs], [next(it) for _ in jobs]
        copies = []
        for index, (_, _, _, columns) in enumerate(jobs):
            groups, _ = weight_copies(w_refs[index], sc, bufs[index], None, sems[index], None, columns)
            copies.append([copy for group in groups for copy in group])
            for copy in copies[-1]:
                copy.start()
        outs[0][...] = base_ref[...]
        for index, (out, _, _, _) in enumerate(jobs):
            for copy in copies[index]:
                copy.wait()
            if out:
                outs[1][...] = dot_nt(grads[index][...], bufs[index][...])
            else:
                outs[0][...] += dot_nt(grads[index][...], bufs[index][...])

    args = [scalars, base] + [grad for _, grad, _, _ in jobs]
    tail = [array for _, _, pieces, _ in jobs for piece in pieces for array in piece]
    return pl.pallas_call(
        kernel,
        out_shape=[sds((rows, depth), F32)] * 2,
        in_specs=[SMEM] + [VMEM] * (len(args) - 1) + [ANY] * len(tail),
        out_specs=[VMEM] * 2,
        scratch_shapes=[pltpu.VMEM((depth, grad.shape[1]), BF16) for _, grad, _, _ in jobs]
        + [pltpu.SemaphoreType.DMA((3, len(pieces), 4)) for _, _, pieces, _ in jobs],
        compiler_params=params(),
        cost_estimate=cost_of(12),
        name="inputs_back",
    )(*args, *tail)


def norm_back_rows(acc, hat, inv, gain_ref, low_ref, scaled_ref, gsum_ref, bsum_ref, rows):
    gsum_ref[...] = jnp.zeros_like(gsum_ref)
    bsum_ref[...] = jnp.zeros_like(bsum_ref)

    def chunk(at):
        gradient, normed = acc[at, :], hat[at, :]
        grad_in = norm_back_chunk(gradient, normed, inv[at, :1], gain_ref[...])
        low_ref[at, :] = grad_in.astype(BF16)
        scaled_ref[at, :] = RESIDUAL_ALPHA * grad_in
        gsum_ref[...] += fold_rows(gradient * normed)
        bsum_ref[...] += fold_rows(gradient)

    each_chunk(rows, chunk)


GELU_SCALE = 0.7978845608028654
GELU_CUBE = 0.044715


def gelu_and_slope(pre):
    square = pre * pre
    inner = pre * (GELU_SCALE + (GELU_SCALE * GELU_CUBE) * square)
    curve = jnp.tanh(inner)
    half = 0.5 + 0.5 * curve
    slope = half * (1.0 + pre * (1.0 - curve) * (GELU_SCALE + (3.0 * GELU_SCALE * GELU_CUBE) * square))
    return pre * half, slope


FFN_PART = FFN_UNIT // 2


def ffn_copies(pieces, order, ubuf, dbuf, usem, dsem):
    ups, downs = [], []
    for index, refs in enumerate(pieces):
        wide = 2 * FFN_UNIT
        at = slice(index * wide, (index + 1) * wide)
        if len(refs) == 2:
            ups.append([copy_of(refs[0], ubuf.at[:, at], usem.at[index, 0])])
            downs.append([copy_of(refs[1], dbuf.at[at, :], dsem.at[index, 0])])
            continue
        ups.append([])
        downs.append([])
        rows = refs[0].shape[1]
        for quarter in range(4):
            up = refs[quarter].at[0]
            down = refs[quarter].at[1] if quarter < 3 else refs[4].at[0]
            place = (quarter ^ order) * rows
            ups[-1].append(copy_of(up, ubuf.at[pl.ds(pl.multiple_of(place, rows), rows), at], usem.at[index, quarter]))
            downs[-1].append(
                copy_of(down, dbuf.at[pl.ds(pl.multiple_of(index * wide + place, rows), rows), :], dsem.at[index, quarter])
            )
    return ups, downs


def ffn_fwd_call(scalars, inputs, pieces, partial, final):
    rows, depth = inputs.shape
    number = 2 * len(pieces)
    last, has_partial = final is not None, partial is not None

    def kernel(*refs):
        it = iter(refs)
        sc, x_ref = next(it), next(it)
        if last:
            gain_old, bias_old, gain_ref, bias_ref = (next(it) for _ in range(4))
            late_in = [next(it), next(it)]
        part_in = next(it) if has_partial else None
        w_refs = [[next(it) for _ in piece] for piece in pieces]
        if last:
            out_ref, low_ref, scaled_ref, gsum_ref, bsum_ref = (next(it) for _ in range(5))
        else:
            sum_ref = next(it)
        act_ref, slope_ref = next(it), next(it)
        ubuf, dbuf, abuf, sbuf, pbuf, psem = (next(it) for _ in range(6))
        if last:
            acc, hat, cot, lsem = (next(it) for _ in range(4))
        wsem, gsem = next(it), next(it)
        target = acc if last else sum_ref

        up_copies, down_copies = ffn_copies(w_refs, sc[1], ubuf, dbuf, wsem.at[0], wsem.at[1])
        for copies in up_copies + down_copies:
            for copy in copies:
                copy.start()
        if has_partial:
            part_copy = copy_of(part_in, target, psem)
            part_copy.start()
        if last:
            late = [copy_of(late_in[0], hat, lsem.at[0]), copy_of(late_in[1], cot, lsem.at[1])]
            for copy in late:
                copy.start()
        saves = []

        def gate(pre, index):
            activated, slope = gelu_and_slope(pre)
            abuf[:, index * FFN_UNIT : (index + 1) * FFN_UNIT] = activated.astype(BF16)
            sbuf[:, index * FFN_UNIT : (index + 1) * FFN_UNIT] = slope.astype(BF16)

        for index in range(number):
            if index % 2 == 0:
                for copy in up_copies[index // 2]:
                    copy.wait()
            if index:
                gate(pbuf[(index - 1) % 2], index - 1)
            pbuf[index % 2] = dot(x_ref[...], ubuf[:, index * FFN_UNIT : (index + 1) * FFN_UNIT])
        gate(pbuf[(number - 1) % 2], number - 1)
        for index in range(number):
            at = slice(index * FFN_UNIT, (index + 1) * FFN_UNIT)
            saves += [
                copy_of(abuf.at[:, at], act_ref.at[index], gsem.at[0, index]),
                copy_of(sbuf.at[:, at], slope_ref.at[index], gsem.at[1, index]),
            ]
        for copy in saves:
            copy.start()
        for copies in down_copies:
            for copy in copies:
                copy.wait()
        if has_partial:
            part_copy.wait()
            target[...] += dot(abuf[...], dbuf[...])
        else:
            target[...] = dot(abuf[...], dbuf[...])
        if last:
            for copy in late:
                copy.wait()
            gsum_ref[...] = jnp.zeros_like(gsum_ref)
            bsum_ref[...] = jnp.zeros_like(bsum_ref)

            def chunk(at):
                old = hat[at, :] * gain_old[...] + bias_old[...]
                normed, xhat, inverse = norm_chunk(RESIDUAL_ALPHA * old + acc[at, :], gain_ref[...], bias_ref[...])
                out_ref[at, :] = normed.astype(BF16)
                gradient = cot[at, :].astype(F32)
                grad_in = norm_back_chunk(gradient, xhat, inverse, gain_ref[...])
                low_ref[at, :] = grad_in.astype(BF16)
                scaled_ref[at, :] = RESIDUAL_ALPHA * grad_in
                gsum_ref[...] += fold_rows(gradient * xhat)
                bsum_ref[...] += fold_rows(gradient)

            each_chunk(rows, chunk)
        for copy in saves:
            copy.wait()

    big, low = sds((rows, depth), F32), sds((rows, depth), BF16)
    if last:
        shapes = [low, low, big, sds((8, depth), F32), sds((8, depth), F32)]
    else:
        shapes = [big]
    specs_out = [VMEM] * len(shapes) + [ANY, ANY]
    shapes += [sds((number, rows, FFN_UNIT), BF16)] * 2
    args = [scalars, inputs]
    if last:
        args += [final[1], final[2], final[4], final[5]]
    specs = [SMEM] + [VMEM] * (len(args) - 1)
    tail = ([final[0], final[3]] if last else []) + ([partial] if has_partial else []) + [array for piece in pieces for array in piece]
    scratch = [
        pltpu.VMEM((depth, number * FFN_UNIT), BF16),
        pltpu.VMEM((number * FFN_UNIT, depth), BF16),
        pltpu.VMEM((rows, number * FFN_UNIT), BF16),
        pltpu.VMEM((rows, number * FFN_UNIT), BF16),
        pltpu.VMEM((2, rows, FFN_UNIT), F32),
        pltpu.SemaphoreType.DMA,
    ]
    if last:
        scratch += [
            pltpu.VMEM((rows, depth), F32),
            pltpu.VMEM((rows, depth), F32),
            pltpu.VMEM((rows, depth), BF16),
            pltpu.SemaphoreType.DMA((2,)),
        ]
    scratch += [pltpu.SemaphoreType.DMA((2, len(pieces), 4)), pltpu.SemaphoreType.DMA((2, number))]
    return pl.pallas_call(
        kernel,
        out_shape=shapes,
        in_specs=specs + [ANY] * len(tail),
        out_specs=specs_out,
        scratch_shapes=scratch,
        compiler_params=params(),
        cost_estimate=cost_of(12),
        name="ffn_fwd",
    )(*args, *tail)


def ffn_bwd_call(scalars, grad_low, inputs, pieces, saved, plan, carried, norm):
    rows, depth = inputs.shape
    number = len(plan)
    last = norm is not None

    def kernel(*refs):
        it = iter(refs)
        sc, g_in, x_ref = (next(it) for _ in range(3))
        gain_ref = next(it) if last else None
        late_in = [next(it), next(it)] if last else []
        acc_in = next(it)
        w_refs = [[next(it) for _ in piece] for piece in pieces]
        s_refs = [[next(it) for _ in call] for call in saved]
        if last:
            low_ref, scaled_ref, gsum_ref, bsum_ref = (next(it) for _ in range(4))
        else:
            sum_ref = next(it)
        g_ref = next(it)
        ubuf, dbuf, abuf, sbuf, gbuf, stage, psem = (next(it) for _ in range(7))
        if last:
            acc, hat, inv, lsem = (next(it) for _ in range(4))
        wsem, ssem, gsem = next(it), next(it), next(it)
        order, dp = sc[1], sc[2]
        target = acc if last else sum_ref

        ups, downs = ffn_copies(w_refs, order, ubuf, dbuf, wsem.at[0], wsem.at[1])
        slopes, acts = [], []
        for index, (call, at) in enumerate(plan):
            lanes = slice(index * FFN_UNIT, (index + 1) * FFN_UNIT)
            slopes.append(copy_of(s_refs[call][1].at[at], sbuf.at[index], ssem.at[0, index]))
            acts.append(copy_of(s_refs[call][0].at[at], abuf.at[:, lanes], ssem.at[1, index]))
        for copies in downs + [slopes, acts] + ups:
            for copy in copies:
                copy.start()
        part_copy = copy_of(acc_in, target, psem)
        part_copy.start()
        if last:
            late = [copy_of(late_in[0], hat, lsem.at[0]), copy_of(late_in[1], inv, lsem.at[1])]
            for copy in late:
                copy.start()
        for index in range(number):
            if index % 2 == 0:
                for copy in downs[index // 2]:
                    copy.wait()
            slopes[index].wait()
            grad_act = dot_nt(g_in[...], dbuf[index * FFN_UNIT : (index + 1) * FFN_UNIT, :]) * sbuf[index].astype(F32)
            gbuf[:, index * FFN_UNIT : (index + 1) * FFN_UNIT] = grad_act.astype(BF16)
        for copy in acts:
            copy.wait()

        def keep(rows_in, source, column):
            for half in range(number // 2):
                wide = 2 * FFN_UNIT
                weight = dot_tn(rows_in[...], source[:, half * wide : (half + 1) * wide]).astype(BF16)
                for inner in range(4):
                    part = weight[:, inner * FFN_PART : (inner + 1) * FFN_PART]
                    store_shards(stage.at[2 * inner + column, half], part, dp)

        keep(x_ref, gbuf, 0)
        keep(g_in, abuf, 1)
        g_copies = [copy_of(stage, g_ref, gsem)]
        for copy in g_copies:
            copy.start()
        for copies in ups:
            for copy in copies:
                copy.wait()
        part_copy.wait()
        target[...] += dot_nt(gbuf[...], ubuf[...])
        if last:
            for copy in late:
                copy.wait()
            norm_back_rows(acc, hat, inv, gain_ref, low_ref, scaled_ref, gsum_ref, bsum_ref, rows)
        for copy in g_copies:
            copy.wait()

    big, low = sds((rows, depth), F32), sds((rows, depth), BF16)
    shapes = [low, big, sds((8, depth), F32), sds((8, depth), F32)] if last else [big]
    specs_out = [VMEM] * len(shapes) + [ANY]
    shapes.append(sds((8, number // 2, 8, UNIT, FFN_PART), BF16))
    args = [scalars, grad_low, inputs] + ([norm[2]] if last else [])
    specs = [SMEM] + [VMEM] * (len(args) - 1)
    tail = ([norm[0], norm[1]] if last else []) + [carried] + [array for piece in pieces for array in piece]
    for call in saved:
        tail += call
    scratch = [
        pltpu.VMEM((depth, number * FFN_UNIT), BF16),
        pltpu.VMEM((number * FFN_UNIT, depth), BF16),
        pltpu.VMEM((rows, number * FFN_UNIT), BF16),
        pltpu.VMEM((number, rows, FFN_UNIT), BF16),
        pltpu.VMEM((rows, number * FFN_UNIT), BF16),
        pltpu.VMEM((8, number // 2, 8, UNIT, FFN_PART), BF16),
        pltpu.SemaphoreType.DMA,
    ]
    if last:
        scratch += [
            pltpu.VMEM((rows, depth), F32),
            pltpu.VMEM((rows, depth), F32),
            pltpu.VMEM((rows, 128), F32),
            pltpu.SemaphoreType.DMA((2,)),
        ]
    scratch += [pltpu.SemaphoreType.DMA((2, len(pieces), 4)), pltpu.SemaphoreType.DMA((2, number)), pltpu.SemaphoreType.DMA]
    return pl.pallas_call(
        kernel,
        out_shape=shapes,
        in_specs=specs + [ANY] * len(tail),
        out_specs=specs_out,
        scratch_shapes=scratch,
        compiler_params=params(),
        cost_estimate=cost_of(17),
        name="ffn_bwd",
    )(*args, *tail)


def combine(jobs, shapes):
    arrays = []
    for terms, _, _, _ in jobs:
        for array, _ in terms:
            if not any(array is known for known in arrays):
                arrays.append(array)
    position = {id(array): index for index, array in enumerate(arrays)}

    def part_shape(array, index):
        kept = []
        for extent, at in zip(array.shape, index + (slice(None),) * (array.ndim - len(index))):
            if isinstance(at, slice):
                kept.append(len(range(*at.indices(extent))))
        return tuple(kept)

    part_shapes = [part_shape(*terms[0]) for terms, _, _, _ in jobs]
    count = sum(len(terms) for terms, _, _, _ in jobs)

    def kernel(*refs):
        ins, outs = refs[: len(arrays)], refs[len(arrays) : len(arrays) + len(shapes)]
        rest = refs[len(arrays) + len(shapes) :]
        term_bufs, sum_bufs, isem, osem = rest[:count], rest[count : count + len(jobs)], rest[-2], rest[-1]
        loads, number = [], 0
        for terms, _, _, _ in jobs:
            loads.append([])
            for array, index in terms:
                loads[-1].append(copy_of(ins[position[id(array)]].at[index], term_bufs[number], isem.at[number]))
                number += 1
        for group in loads:
            for copy in group:
                copy.start()
        stores, number = [], 0
        for job, (terms, out, place, kind) in enumerate(jobs):
            for copy in loads[job]:
                copy.wait()
            bufs = term_bufs[number : number + len(terms)]
            number += len(terms)
            lead = part_shapes[job][:-2]
            size = 1
            for extent in lead:
                size *= extent

            def one(flat, carry, bufs=bufs, lead=lead, target=sum_bufs[job]):
                index, left = [], flat
                for extent in reversed(lead):
                    index.append(lax.rem(left, extent))
                    left = lax.div(left, extent)
                index = tuple(reversed(index))
                total = bufs[0][index].astype(F32)
                for buf in bufs[1:]:
                    total = total + buf[index].astype(F32)
                target[index] = total.astype(target.dtype)
                return carry

            if kind == "range":
                lax.fori_loop(0, size, one, 0)
            else:
                total = bufs[0][0].astype(F32)
                for buf in bufs[1:]:
                    total = total + buf[0].astype(F32)
                sum_bufs[job][...] = jnp.transpose(total) if kind == "turned" else total
            stores.append(copy_of(sum_bufs[job], outs[out].at[place], osem.at[job]))
            stores[-1].start()
        for copy in stores:
            copy.wait()

    scratch = [pltpu.VMEM(part_shapes[job], array.dtype) for job, (terms, _, _, _) in enumerate(jobs) for array, _ in terms]
    for job, (_, out, _, kind) in enumerate(jobs):
        shape = part_shapes[job]
        shape = {"range": shape, "plain": shape[1:], "turned": shape[:0:-1]}[kind]
        scratch.append(pltpu.VMEM(shape, shapes[out].dtype))
    scratch += [pltpu.SemaphoreType.DMA((count,)), pltpu.SemaphoreType.DMA((len(jobs),))]
    return pl.pallas_call(
        kernel,
        out_shape=list(shapes),
        in_specs=[ANY] * len(arrays),
        out_specs=[ANY] * len(shapes),
        scratch_shapes=scratch,
        compiler_params=params(),
        cost_estimate=cost_of(3),
        name="combine",
    )(*arrays)


def swap_pairs(count, mask):
    return [(i, i ^ mask) for i in range(count)]


def to_sibling(values):
    return lax.ppermute(values, "tensor", swap_pairs(4, 1))


def over_y(values):
    return lax.ppermute(values, "tensor", swap_pairs(4, 2))


def over_dp(values, mask):
    return lax.ppermute(values, "dp", swap_pairs(8, mask))


def over_x(values):
    return over_dp(values, 1)


def over_z_near(values):
    return over_dp(values, 2)


def over_z_far(values):
    return over_dp(values, 4)


def after(values, *earlier):
    return lax.optimization_barrier((values, *earlier))[0]


MOVES = {"y": over_y, "x": over_x, "z": over_z_near}


class Reduction:
    def __init__(self, sent, portions, finish):
        self.other, self.finish = to_sibling(sent), finish
        self.portions, self.stage, self.sends, self.total = portions, 0, None, None

    def begin(self, kept, *earlier):
        other = after(self.other, *earlier)
        split = (kept.shape[0], 2, 2, 2, 2, *kept.shape[3:])
        arrays = (kept.reshape(split), other.reshape(split))
        self.blocks, self.tail = kept.shape[0], kept.shape[3:]
        self.terms = [[(array, ("b", "y", "x", "z", "w"), low, {}) for array in arrays] for low, _, _ in self.portions]

    def receive(self, *earlier):
        if self.stage == 4:
            moved = after(over_z_far(self.sends[0]), *earlier)
            for (low, _, _), terms in zip(self.portions, self.terms):
                terms.append((moved, ("b",), low, {}))
        elif self.stage:
            for send, (_, _, orders), terms in zip(self.sends, self.portions, self.terms):
                left = tuple(a for a in ("b", "y", "x", "z", "w") if a not in orders[: self.stage])
                terms.append((after(MOVES[orders[self.stage - 1]](send), *earlier), left, 0, {}))

    def jobs(self, first_out):
        jobs, shapes = [], []
        stage = self.stage
        for number, ((low, high, orders), terms) in enumerate(zip(self.portions, self.terms)):
            axis = (*orders, "w", None)[stage]
            picked = []
            for array, axes, start, fixed in terms:
                index = [slice(start, start + high - low)]
                for name in axes[1:]:
                    index.append(1 if name == axis else fixed.get(name, 0 if name in orders[:stage] or (stage > 3 and name == "w") else slice(None)))
                picked.append((array, tuple(index)))
            if stage < 3:
                shapes.append(sds((high - low, *(2,) * (3 - stage), *self.tail), BF16))
                jobs.append((picked, first_out + number, slice(0, high - low), "range"))
            elif stage == 3:
                if not number:
                    shapes.append(sds((self.blocks, *self.tail), BF16))
                jobs.append((picked, first_out, slice(low, high), "range"))
            else:
                if not number:
                    shapes += self.finish[0]
                for block in range(low, high):
                    shift = block - low
                    one = [(a, (slice(index[0].start + shift, index[0].start + shift + 1), *index[1:])) for a, index in picked]
                    out, place, kind = self.finish[1](block)
                    jobs.append((one, first_out + out, place, kind))
        self.stage += 1
        return jobs, shapes


def attention_finish(counts):
    stacks = [sds((count, UNIT, 2 * UNIT) if count > 1 else (UNIT, 2 * UNIT), F32) for count in counts]

    def place_of(block):
        half, matrix = block // 4, block % 4
        lanes = slice(half * UNIT, (half + 1) * UNIT)
        if matrix == 3:
            return len(counts), (lanes, slice(None)), "turned"
        stack = 0 if matrix < counts[0] else 1
        if counts[stack] == 1:
            return stack, (slice(None), lanes), "plain"
        return stack, (matrix - sum(counts[:stack]), slice(None), lanes), "plain"

    return [*stacks, sds((2 * UNIT, UNIT), F32)], place_of


def ffn_finish():
    def place_of(block):
        lanes = slice(block // 2 * FFN_PART, (block // 2 + 1) * FFN_PART)
        if block % 2:
            return 1, (lanes, slice(None)), "turned"
        return 0, (slice(None), lanes), "plain"

    return [sds((UNIT, 4 * FFN_PART), F32), sds((4 * FFN_PART, UNIT), F32)], place_of


def advance(reductions, *earlier):
    jobs, shapes, bounds = [], [], []
    for reduction in reductions:
        reduction.receive(*earlier)
        more, made = reduction.jobs(len(shapes))
        bounds.append((len(shapes), len(shapes) + len(made)))
        jobs, shapes = jobs + more, shapes + made
    results = combine(jobs, shapes)
    for reduction, (low, high) in zip(reductions, bounds):
        reduction.sends = list(results[low:high])
        if reduction.stage == 5:
            reduction.total = results[low:high]
    return list(results)


def sentence_body(
    tokens,
    memory,
    dec_lengths,
    mem_lengths,
    self_qkv,
    self_out,
    cross_q,
    cross_kv,
    cross_out,
    ffn_in,
    ffn_out,
    norm_gains,
    norm_biases,
    cotangent,
):
    dp = lax.axis_index("dp")
    mine = lax.axis_index("tensor")
    order = dp & 3
    inner = (dp >> 1) & 1
    self_scalars = jnp.stack([dec_lengths[0, mine], order, dp, inner]).astype(jnp.int32)
    cross_scalars = jnp.stack([mem_lengths[0, mine], order, dp, inner]).astype(jnp.int32)
    gains = [norm_gains[i : i + 1] for i in range(3)]
    biases = [norm_biases[i : i + 1] for i in range(3)]

    def part_rows(values, parts):
        rows = values.shape[-2] // parts
        place = order if parts == 4 else inner
        return lax.dynamic_slice_in_dim(values, place * rows, rows, values.ndim - 2)

    def folded(values):
        blocks = values.reshape(values.shape[0], 4, 2 * UNIT)
        return blocks.transpose(1, 0, 2).reshape(1, 4 * values.shape[0], 2 * UNIT)

    self_near = over_y(jnp.concatenate([part_rows(self_qkv, 4), folded(part_rows(self_out, 4))]))
    cross_near = over_y(
        jnp.concatenate([part_rows(cross_q, 2)[None], part_rows(cross_kv, 2), folded(part_rows(cross_out, 2))])
    )
    ffn_near = over_y(jnp.stack([part_rows(ffn_in, 4), part_rows(ffn_out, 4)]))
    self_own = (self_qkv, self_out)
    self_sib = tuple(to_sibling(w) for w in self_own)
    self_a = attention_fwd_call(self_scalars, [], [tokens], [self_own, self_sib], None, None)
    self_near = after(self_near, self_a[4])
    self_side, self_up = over_x(self_near), over_z_near(self_near)
    self_corner = over_x(self_up)
    self_rest = jnp.stack([after(self_near, cross_near), self_side, self_up, self_corner])
    cross_up = over_z_near(cross_near)
    self_far = to_sibling(self_rest)
    self_pieces = [self_own, self_sib, (self_rest,), (self_far,)]
    self_b = attention_fwd_call(
        self_scalars, [tokens], [tokens], self_pieces[2:], self_a[5], (gains[0], biases[0])
    )
    first_low, first_hat, first_inv = self_b[5:]
    cross_own = (cross_q, cross_kv, cross_out)
    cross_sib = tuple(to_sibling(after(w, self_near)) for w in cross_own)
    ffn_own = (ffn_in, ffn_out)
    ffn_sib = tuple(to_sibling(after(w, first_inv)) for w in ffn_own)
    cross_in = [first_low, memory]
    cross_rest = jnp.stack([cross_near, after(cross_up, self_b[4])])
    cross_far = to_sibling(cross_rest)
    cross_a = attention_fwd_call(after(cross_scalars, ffn_near), [], cross_in, [cross_own, cross_sib], None, None)
    ffn_side, ffn_up = over_x(ffn_near), over_z_near(ffn_near)
    cross_pieces = [cross_own, cross_sib, (cross_rest,), (after(cross_far, cross_a[4]),)]
    cross_b = attention_fwd_call(
        cross_scalars, [first_hat, gains[0], biases[0]], cross_in, cross_pieces[2:], cross_a[5], (gains[1], biases[1])
    )
    second_low, second_hat, second_inv = cross_b[5:]
    ffn_side, ffn_up = after(ffn_side, cross_b[4]), after(ffn_up, cross_b[4])
    up_corner, down_corner = over_x(ffn_up[:1]), over_z_near(ffn_side[1:])
    ffn_pieces = [ffn_own, ffn_sib]
    ffn_a = ffn_fwd_call(cross_scalars, second_low, ffn_pieces, None, None)
    up_corner, down_corner = after(up_corner, ffn_a[0]), after(down_corner, ffn_a[0])
    ffn_rest = (ffn_near, ffn_side, ffn_up, up_corner, down_corner)
    ffn_pieces += [ffn_rest, tuple(to_sibling(w) for w in ffn_rest)]
    ffn_b = ffn_fwd_call(
        cross_scalars, second_low, ffn_pieces[2:], ffn_a[0],
        (second_hat, gains[1], biases[1], cotangent, gains[2], biases[2]),
    )
    out_rows, third_low, third_scaled, third_gain, third_bias = ffn_b[:5]

    def plan_of(pieces):
        return [(piece // 2, 2 * (piece % 2) + half) for piece in pieces for half in (0, 1)]

    ffn_saved = [ffn_a[1:3], ffn_b[5:7]]
    ffn_d = ffn_bwd_call(
        cross_scalars, third_low, second_low, ffn_pieces[1::2], ffn_saved, plan_of((1, 3)), third_scaled, None
    )
    ffn_sum = Reduction(ffn_d[1], [(0, 3, "yxz"), (3, 6, "xzy"), (6, 8, "zyx")], ffn_finish())
    ffn_e = ffn_bwd_call(
        cross_scalars, third_low, second_low, ffn_pieces[::2], ffn_saved, plan_of((0, 2)), ffn_d[0],
        (second_hat, second_inv, gains[1]),
    )
    second_back, second_scaled, second_gain, second_bias = ffn_e[:4]
    ffn_sum.begin(ffn_e[4], second_gain)
    second_back = after(second_back, *advance([ffn_sum]))

    cross_e = attention_bwd_call(
        cross_scalars, second_back, cross_in, cross_pieces[1::2] + cross_pieces[::2],
        [cross_a[:5], cross_b[:5]], plan_of((1, 3, 0, 2)), second_scaled,
        (first_hat, first_inv, gains[0]), 2,
    )
    first_back, first_scaled, first_gain, first_bias, memory_part = cross_e[:5]
    norm_sums = jnp.stack([first_gain, second_gain, third_gain, first_bias, second_bias, third_bias])
    norm_sums = jnp.concatenate([jnp.sum(norm_sums, axis=1), jnp.zeros((2, norm_sums.shape[2]), F32)])
    norm_sums = lax.all_gather(norm_sums, ("dp", "tensor"), axis=0)
    sends = advance([ffn_sum], first_gain)
    cross_sum = Reduction(after(cross_e[5], *sends), [(0, 4, "xzy"), (4, 8, "zxy")], attention_finish((1, 2)))
    first_back = after(first_back, *sends)

    self_saved = [self_a[:5], self_b[:5]]
    self_d = attention_bwd_call(
        self_scalars, first_back, [tokens], self_pieces[1::2], self_saved, plan_of((1, 3)), None, None
    )
    cross_sum.begin(cross_e[6], self_d[0])
    sends = advance([cross_sum, ffn_sum], self_d[0])
    self_sum = Reduction(after(self_d[1], *sends), [(0, 4, "yzx"), (4, 8, "xyz")], attention_finish((3,)))
    first_back = after(first_back, *sends)
    self_e = attention_bwd_call(
        self_scalars, first_back, [tokens], self_pieces[::2], self_saved, plan_of((0, 2)), None, None
    )
    self_sum.begin(self_e[1], self_e[0])
    sends = advance([self_sum])
    grad_tokens, grad_memory = inputs_back_call(
        self_scalars, after(first_scaled, *sends),
        [(self_d[0], self_pieces[1::2]), (self_e[0], self_pieces[::2])],
        (memory_part, cross_pieces[1::2] + cross_pieces[::2]),
    )
    sends = advance([cross_sum, ffn_sum], *sends)
    sends = advance([self_sum, cross_sum], *sends, grad_tokens)
    sends = advance([self_sum, cross_sum, ffn_sum], *sends)
    sends = advance([self_sum, cross_sum], *sends)
    sends = advance([self_sum], *sends)
    norm_total = jnp.sum(after(norm_sums, *sends), axis=0)
    self_sum, cross_sum, ffn_sum = self_sum.total, cross_sum.total, ffn_sum.total

    return (
        out_rows,
        grad_tokens,
        grad_memory,
        *self_sum,
        *cross_sum,
        *ffn_sum,
        norm_total[:3],
        norm_total[3:6],
    )


def sentence_fits(mesh, tokens, memory, dec_lengths):
    shape = dict(mesh.shape)
    rows = tokens.shape[0] // mesh.size
    sentences = dec_lengths.shape[1]
    return (
        shape["tensor"] == 4
        and shape["dp"] == 8
        and sentences == 4
        and rows == 512
        and memory.shape[0] // mesh.size == rows
        and tokens.shape[1] == 1024
    )


def smooth_gate(values):
    return jax.nn.gelu(values, approximate=True)


def norm_rows(hidden, norm_gain, norm_bias):
    center = hidden - jnp.mean(hidden, axis=-1, keepdims=True)
    inverse = lax.rsqrt(jnp.mean(center * center, axis=-1, keepdims=True) + NORM_EPSILON)
    normed = center * inverse
    return (normed * norm_gain + norm_bias, normed, inverse)


def norm_back(gradient, normed, inverse, norm_gain):
    scaled = gradient * norm_gain
    grad_in = inverse * (
        scaled
        - jnp.mean(scaled, axis=-1, keepdims=True)
        - normed * jnp.mean(scaled * normed, axis=-1, keepdims=True)
    )
    return (grad_in, jnp.sum(gradient * normed, axis=0), jnp.sum(gradient, axis=0))


def head_view(values, sentences):
    return values.reshape(sentences, -1, values.shape[1] // HEAD_DIM, HEAD_DIM)


def masked_scores(query_heads, key_heads, key_mask):
    scores = jnp.einsum(
        "sqhe,skhe->shqk", query_heads, key_heads, preferred_element_type=jnp.float32
    ) * HEAD_DIM ** (-0.5)
    return jnp.where(key_mask, scores, MASKED_SCORE)


def attention_forward(query_rows, key_rows, value_rows, key_mask, sentences):
    scores = masked_scores(
        head_view(query_rows, sentences), head_view(key_rows, sentences), key_mask
    )
    row_peak = jnp.max(scores, axis=-1, keepdims=True)
    exponent_terms = jnp.exp(scores - row_peak)
    row_sum = jnp.sum(exponent_terms, axis=-1, keepdims=True)
    softmax_probs = exponent_terms / row_sum
    attended = jnp.einsum(
        "shqk,skhe->sqhe",
        softmax_probs.astype(jnp.bfloat16),
        head_view(value_rows, sentences),
        preferred_element_type=jnp.float32,
    ).astype(jnp.bfloat16)
    return (attended.reshape(query_rows.shape), row_peak + jnp.log(row_sum))


def attention_backward(query_rows, key_rows, value_rows, key_mask, log_total, grad_rows, sentences):
    query_heads = head_view(query_rows, sentences)
    key_heads = head_view(key_rows, sentences)
    value_heads = head_view(value_rows, sentences)
    grad_heads = head_view(grad_rows, sentences)
    softmax_probs = jnp.exp(masked_scores(query_heads, key_heads, key_mask) - log_total)
    grad_probs = jnp.einsum(
        "sqhe,skhe->shqk", grad_heads, value_heads, preferred_element_type=jnp.float32
    )
    row_delta = jnp.sum(softmax_probs * grad_probs, axis=-1, keepdims=True)
    grad_scores = (softmax_probs * (grad_probs - row_delta)).astype(jnp.bfloat16)
    score_scale = HEAD_DIM ** (-0.5)
    grad_query = (
        jnp.einsum("shqk,skhe->sqhe", grad_scores, key_heads, preferred_element_type=jnp.float32)
        * score_scale
    ).astype(jnp.bfloat16)
    grad_key = (
        jnp.einsum("shqk,sqhe->skhe", grad_scores, query_heads, preferred_element_type=jnp.float32)
        * score_scale
    ).astype(jnp.bfloat16)
    grad_value = jnp.einsum(
        "shqk,sqhe->skhe",
        softmax_probs.astype(jnp.bfloat16),
        grad_heads,
        preferred_element_type=jnp.float32,
    ).astype(jnp.bfloat16)
    return (
        grad_query.reshape(query_rows.shape),
        grad_key.reshape(key_rows.shape),
        grad_value.reshape(value_rows.shape),
    )


def body(
    tokens,
    memory,
    dec_lengths,
    mem_lengths,
    self_qkv,
    self_out,
    cross_q,
    cross_kv,
    cross_out,
    ffn_in,
    ffn_out,
    norm_gains,
    norm_biases,
    cotangent,
):
    row_share = tokens.shape[0]
    sentences = dec_lengths.shape[1]
    all_tokens, all_memory = (
        lax.all_gather(tokens, "tensor", axis=0, tiled=True),
        lax.all_gather(memory, "tensor", axis=0, tiled=True),
    )
    sentence_len = all_tokens.shape[0] // sentences
    memory_len = all_memory.shape[0] // sentences
    positions = jnp.arange(sentence_len, dtype=jnp.int32)
    self_mask = (
        (positions[None, :] <= positions[:, None])[None]
        & (positions[None, None, :] < dec_lengths[0][:, None, None])
    )[:, None]
    memory_positions = jnp.arange(memory_len, dtype=jnp.int32)
    cross_mask = (memory_positions[None, :] < mem_lengths[0][:, None])[:, None, None, :]

    def branch_rows(attended, weight):
        return lax.psum_scatter(
            jnp.dot(attended, weight, preferred_element_type=jnp.float32).astype(jnp.bfloat16),
            "tensor",
            scatter_dimension=0,
            tiled=True,
        ).astype(jnp.float32)

    def branch_grad(grad_rows, attended, weight):
        grad_low = grad_rows.astype(jnp.bfloat16)
        grad_all = lax.all_gather(grad_low, "tensor", axis=0, tiled=True)
        grad_attended = jnp.dot(grad_all, weight.T, preferred_element_type=jnp.float32).astype(
            jnp.bfloat16
        )
        weight_part = jnp.dot(attended.T, grad_all, preferred_element_type=jnp.float32)
        return (grad_attended, weight_part)

    def gather_normed(values):
        return lax.all_gather(values, "tensor", axis=0, tiled=True)

    def head_input_sum(term):
        return lax.psum_scatter(
            term(jnp.int32(0), row_share * lax.axis_size("tensor")).astype(jnp.bfloat16),
            "tensor",
            scatter_dimension=0,
            tiled=True,
        ).astype(jnp.float32)

    self_proj = jnp.einsum(
        "td,cde->cte", all_tokens, self_qkv, preferred_element_type=jnp.float32
    ).astype(jnp.bfloat16)
    self_att, self_lse = attention_forward(
        self_proj[0], self_proj[1], self_proj[2], self_mask, sentences
    )
    self_branch = branch_rows(self_att, self_out)
    first_norm, first_hat, first_inv = norm_rows(
        RESIDUAL_ALPHA * tokens.astype(jnp.float32) + self_branch, norm_gains[0], norm_biases[0]
    )
    first_all = gather_normed(first_norm.astype(jnp.bfloat16))
    cross_query = jnp.dot(first_all, cross_q, preferred_element_type=jnp.float32).astype(
        jnp.bfloat16
    )
    cross_proj = jnp.einsum(
        "td,cde->cte", all_memory, cross_kv, preferred_element_type=jnp.float32
    ).astype(jnp.bfloat16)
    cross_att, cross_lse = attention_forward(
        cross_query, cross_proj[0], cross_proj[1], cross_mask, sentences
    )
    cross_branch = branch_rows(cross_att, cross_out)
    second_norm, second_hat, second_inv = norm_rows(
        RESIDUAL_ALPHA * first_norm + cross_branch, norm_gains[1], norm_biases[1]
    )
    second_all = gather_normed(second_norm.astype(jnp.bfloat16))
    pre_gate = jnp.dot(second_all, ffn_in, preferred_element_type=jnp.float32)
    activated = smooth_gate(pre_gate).astype(jnp.bfloat16)
    ffn_branch = lax.psum_scatter(
        jnp.dot(activated, ffn_out, preferred_element_type=jnp.float32).astype(jnp.bfloat16),
        "tensor",
        scatter_dimension=0,
        tiled=True,
    ).astype(jnp.float32)
    out_rows, third_hat, third_inv = norm_rows(
        RESIDUAL_ALPHA * second_norm + ffn_branch, norm_gains[2], norm_biases[2]
    )
    grad_third, third_gain, third_bias = norm_back(
        cotangent.astype(jnp.float32), third_hat, third_inv, norm_gains[2]
    )
    grad_ffn_all = lax.all_gather(grad_third.astype(jnp.bfloat16), "tensor", axis=0, tiled=True)
    unused_gate, gate_pull = jax.vjp(smooth_gate, pre_gate)
    grad_act = gate_pull(jnp.dot(grad_ffn_all, ffn_out.T, preferred_element_type=jnp.float32))[
        0
    ].astype(jnp.bfloat16)
    grad_ffn_out = jnp.dot(activated.T, grad_ffn_all, preferred_element_type=jnp.float32)
    grad_ffn_in = jnp.dot(second_all.T, grad_act, preferred_element_type=jnp.float32)
    grad_second = RESIDUAL_ALPHA * grad_third + lax.psum_scatter(
        jnp.dot(grad_act, ffn_in.T, preferred_element_type=jnp.float32).astype(jnp.bfloat16),
        "tensor",
        scatter_dimension=0,
        tiled=True,
    ).astype(jnp.float32)
    grad_second_in, second_gain, second_bias = norm_back(
        grad_second, second_hat, second_inv, norm_gains[1]
    )
    grad_cross_att, cross_out_part = branch_grad(grad_second_in, cross_att, cross_out)
    grad_cq, grad_ck, grad_cv = attention_backward(
        cross_query, cross_proj[0], cross_proj[1], cross_mask, cross_lse, grad_cross_att, sentences
    )
    grad_cross_q = jnp.dot(first_all.T, grad_cq, preferred_element_type=jnp.float32)
    cross_grads = jnp.stack([grad_ck, grad_cv])
    grad_cross_kv = jnp.einsum(
        "td,cte->cde", all_memory, cross_grads, preferred_element_type=jnp.float32
    )
    grad_memory = lax.psum_scatter(
        jnp.einsum("cte,cde->td", cross_grads, cross_kv, preferred_element_type=jnp.float32).astype(
            jnp.bfloat16
        ),
        "tensor",
        scatter_dimension=0,
        tiled=True,
    ).astype(jnp.float32)

    def cross_input_term(first_row, row_total):
        return jnp.dot(grad_cq, cross_q.T, preferred_element_type=jnp.float32)

    cross_input = head_input_sum(cross_input_term)
    grad_first = RESIDUAL_ALPHA * grad_second_in + cross_input
    grad_first_in, first_gain, first_bias = norm_back(
        grad_first, first_hat, first_inv, norm_gains[0]
    )
    grad_self_att, self_out_part = branch_grad(grad_first_in, self_att, self_out)
    grad_sq, grad_sk, grad_sv = attention_backward(
        self_proj[0], self_proj[1], self_proj[2], self_mask, self_lse, grad_self_att, sentences
    )
    self_grads = jnp.stack([grad_sq, grad_sk, grad_sv])
    grad_self_qkv = jnp.einsum(
        "td,cte->cde", all_tokens, self_grads, preferred_element_type=jnp.float32
    )

    def self_input_term(first_row, row_total):
        return jnp.einsum("cte,cde->td", self_grads, self_qkv, preferred_element_type=jnp.float32)

    self_input = head_input_sum(self_input_term)
    grad_tokens = RESIDUAL_ALPHA * grad_first_in + self_input
    summed = (
        lax.psum_scatter(
            grad_self_qkv.astype(jnp.bfloat16), "dp", scatter_dimension=1, tiled=True
        ).astype(jnp.float32),
        lax.psum_scatter(
            self_out_part.astype(jnp.bfloat16), "dp", scatter_dimension=1, tiled=True
        ).astype(jnp.float32),
        lax.psum_scatter(
            grad_cross_q.astype(jnp.bfloat16), "dp", scatter_dimension=0, tiled=True
        ).astype(jnp.float32),
        lax.psum_scatter(
            grad_cross_kv.astype(jnp.bfloat16), "dp", scatter_dimension=1, tiled=True
        ).astype(jnp.float32),
        lax.psum_scatter(
            cross_out_part.astype(jnp.bfloat16), "dp", scatter_dimension=1, tiled=True
        ).astype(jnp.float32),
        lax.psum_scatter(
            grad_ffn_in.astype(jnp.bfloat16), "dp", scatter_dimension=0, tiled=True
        ).astype(jnp.float32),
        lax.psum_scatter(
            grad_ffn_out.astype(jnp.bfloat16), "dp", scatter_dimension=1, tiled=True
        ).astype(jnp.float32),
    )
    gain_total, bias_total = lax.psum(
        (
            jnp.stack([first_gain, second_gain, third_gain]),
            jnp.stack([first_bias, second_bias, third_bias]),
        ),
        ("dp", "tensor"),
    )
    return (
        out_rows.astype(jnp.bfloat16),
        grad_tokens,
        grad_memory,
        summed[0],
        summed[1],
        summed[2],
        summed[3],
        summed[4],
        summed[5],
        summed[6],
        gain_total,
        bias_total,
    )


def solution(mesh):
    in_specs = (
        P(("dp", "tensor"), None),
        P(("dp", "tensor"), None),
        P("dp", None),
        P("dp", None),
        P(None, None, "tensor"),
        P("tensor", None),
        P(None, "tensor"),
        P(None, None, "tensor"),
        P("tensor", None),
        P(None, "tensor"),
        P("tensor", None),
        P(),
        P(),
        P(("dp", "tensor"), None),
    )
    out_specs = (
        P(("dp", "tensor"), None),
        P(("dp", "tensor"), None),
        P(("dp", "tensor"), None),
        P(None, "dp", "tensor"),
        P("tensor", "dp"),
        P("dp", "tensor"),
        P(None, "dp", "tensor"),
        P("tensor", "dp"),
        P("dp", "tensor"),
        P("tensor", "dp"),
        P(),
        P(),
    )

    def step(*args):
        chosen = sentence_body if sentence_fits(mesh, args[0], args[1], args[2]) else body
        return jax.shard_map(
            chosen, mesh=mesh, in_specs=in_specs, out_specs=out_specs, check_vma=False
        )(*args)

    return step
```

```python
import functools
import jax
import jax.numpy as jnp
from jax import lax
from jax.experimental import pallas as pl
from jax.experimental.pallas import tpu as pltpu
from jax.sharding import PartitionSpec as P

HEAD_DIM = 64
RESIDUAL_ALPHA = 4.16
NORM_EPSILON = 1e-05
MASKED_SCORE = -1000000000.0
SCORE_SCALE = HEAD_DIM ** (-0.5)
UNIT = 128
QUERY_BLOCK = 256
FFN_UNIT = 512
ROW_CHUNK = 64
BF16 = jnp.bfloat16
F32 = jnp.float32


def dot(left, right):
    return lax.dot_general(left, right, (((1,), (0,)), ((), ())), preferred_element_type=F32)


def dot_tn(left, right):
    return lax.dot_general(left, right, (((0,), (0,)), ((), ())), preferred_element_type=F32)


def dot_nt(left, right):
    return lax.dot_general(left, right, (((1,), (1,)), ((), ())), preferred_element_type=F32)


def shard_of(position):
    return ((position >> 2) & 1) | (position & 2) | ((position & 1) << 2)


def copy_of(source, target, sem):
    return pltpu.make_async_copy(source, target, sem)


def own_lanes(rows, head):
    lanes = lax.broadcasted_iota(jnp.int32, rows.shape, 1)
    return jnp.where((lanes >= HEAD_DIM) if head else (lanes < HEAD_DIM), rows, 0.0)


def extended_keys(keys, length):
    lanes = lax.broadcasted_iota(jnp.int32, keys.shape, 1)
    rows = lax.broadcasted_iota(jnp.int32, keys.shape, 0)
    mask = jnp.where((lanes == 0) & (rows >= length), MASKED_SCORE, 0.0).astype(BF16)
    keys = keys.astype(F32)
    return [jnp.concatenate([own_lanes(keys, head).astype(BF16), mask], axis=1) for head in (0, 1)]


def extended_query(query):
    lanes = lax.broadcasted_iota(jnp.int32, query.shape, 1)
    return jnp.concatenate([query, jnp.where(lanes == 0, 1.0, 0.0).astype(BF16)], axis=1)


def fill_diagonal(diagonal):
    keys = lax.broadcasted_iota(jnp.int32, diagonal.shape, 0)
    queries = lax.broadcasted_iota(jnp.int32, diagonal.shape, 1)
    diagonal[...] = jnp.where(keys <= queries, 0.0, MASKED_SCORE)


def key_ranges(block, keys, causal):
    if not causal:
        return [(0, keys)]
    return [(low, low + QUERY_BLOCK) for low in range(0, (block + 1) * QUERY_BLOCK, QUERY_BLOCK)]


def attend_unit(query, keys, values, length, causal, diagonal, lse_ref):
    rows, count = query.shape[0], keys.shape[0]
    values_t = jnp.transpose(values.astype(F32)).astype(BF16)
    wide_keys, wide_query = extended_keys(keys, length), extended_query(query)
    items = [(head, block) for block in range(rows // QUERY_BLOCK) for head in (0, 1)]
    scores, probs, totals, mixed = {}, {}, {}, {}
    for head, block in items:
        part = wide_query[block * QUERY_BLOCK : (block + 1) * QUERY_BLOCK]
        ranges = key_ranges(block, count, causal)
        scores[head, block] = [dot_nt(wide_keys[head][a:b], part) for a, b in ranges]
        if causal:
            scores[head, block][-1] = scores[head, block][-1] + diagonal[...]
    for head, block in items:
        pieces = scores[head, block]
        peak = functools.reduce(jnp.maximum, [jnp.max(p, axis=0, keepdims=True) for p in pieces])
        terms = [jnp.exp(p - peak) for p in pieces]
        total = sum(jnp.sum(t, axis=0, keepdims=True) for t in terms)
        at = slice(block * QUERY_BLOCK, (block + 1) * QUERY_BLOCK)
        lse_ref[head : head + 1, at] = peak + jnp.log(total)
        totals[head, block] = total
        probs[head, block] = jnp.concatenate([t.astype(BF16) for t in terms], axis=0)
    for head, block in items:
        own = values_t[head * HEAD_DIM : (head + 1) * HEAD_DIM, : probs[head, block].shape[0]]
        mixed[head, block] = dot(own, probs[head, block]) / totals[head, block]
    out = [
        jnp.transpose(jnp.concatenate([mixed[0, block], mixed[1, block]], axis=0))
        for block in range(rows // QUERY_BLOCK)
    ]
    return jnp.concatenate(out, axis=0).astype(BF16)


def attend_back_unit(query, keys, values, attended, grad, length, causal, diagonal, lse_ref):
    rows, count = query.shape[0], keys.shape[0]
    blocks = range(rows // QUERY_BLOCK)
    query_f, keys_f, grad_f = (a.astype(F32) for a in (query, keys, grad))
    wide_keys, wide_query = extended_keys(keys, length), extended_query(query)
    delta = jnp.transpose(grad_f * attended.astype(F32))
    deltas = [
        jnp.sum(delta[head * HEAD_DIM : (head + 1) * HEAD_DIM], axis=0, keepdims=True)
        for head in (0, 1)
    ]
    keys_t = jnp.transpose(keys_f).astype(BF16)
    query_own = [own_lanes(query_f, head).astype(BF16) for head in (0, 1)]
    grad_own = [own_lanes(grad_f, head).astype(BF16) for head in (0, 1)]
    items = [(head, block) for block in blocks for head in (0, 1)]
    scores, slopes, probs, back, grad_query = {}, {}, {}, {}, {}
    for head, block in items:
        at = slice(block * QUERY_BLOCK, (block + 1) * QUERY_BLOCK)
        for a, b in key_ranges(block, count, causal):
            scores[head, block, a] = dot_nt(wide_keys[head][a:b], wide_query[at])
            slopes[head, block, a] = dot_nt(values[a:b], grad_own[head][at])
    for head, block in items:
        at = slice(block * QUERY_BLOCK, (block + 1) * QUERY_BLOCK)
        ranges = key_ranges(block, count, causal)
        for a, b in ranges:
            score = scores[head, block, a]
            if causal and (a, b) == ranges[-1]:
                score = score + diagonal[...]
            prob = jnp.exp(score - lse_ref[head : head + 1, at])
            probs[head, block, a] = prob.astype(BF16)
            back[head, block, a] = (prob * (slopes[head, block, a] - deltas[head][:, at])).astype(BF16)
    for head, block in items:
        own = keys_t[head * HEAD_DIM : (head + 1) * HEAD_DIM]
        grad_query[head, block] = sum(
            dot(own[:, a:b], back[head, block, a]) for a, b in key_ranges(block, count, causal)
        )
    grad_keys, grad_values = [], []
    for low in sorted({key[2] for key in back}):
        live = [key for key in back if key[2] == low]
        at = [slice(block * QUERY_BLOCK, (block + 1) * QUERY_BLOCK) for _, block, _ in live]
        grad_values.append(
            dot(
                jnp.concatenate([probs[key] for key in live], axis=1),
                jnp.concatenate([grad_own[key[0]][a] for key, a in zip(live, at)], axis=0),
            )
        )
        grad_keys.append(
            dot(
                jnp.concatenate([back[key] for key in live], axis=1),
                jnp.concatenate([query_own[key[0]][a] for key, a in zip(live, at)], axis=0),
            )
        )
    grad_query = [
        jnp.transpose(jnp.concatenate([grad_query[0, block], grad_query[1, block]], axis=0)) * SCORE_SCALE
        for block in blocks
    ]
    return tuple(
        jnp.concatenate(parts, axis=0).astype(BF16) for parts in (grad_query, grad_keys, grad_values)
    )


def norm_chunk(hidden, gain, bias):
    center = hidden - jnp.mean(hidden, axis=-1, keepdims=True)
    inverse = lax.rsqrt(jnp.mean(center * center, axis=-1, keepdims=True) + NORM_EPSILON)
    normed = center * inverse
    return normed * gain + bias, normed, inverse


def norm_back_chunk(gradient, normed, inverse, gain):
    scaled = gradient * gain
    return inverse * (
        scaled
        - jnp.mean(scaled, axis=-1, keepdims=True)
        - normed * jnp.mean(scaled * normed, axis=-1, keepdims=True)
    )


def fold_rows(values):
    return jnp.sum(values.reshape(values.shape[0] // 8, 8, values.shape[1]), axis=0)


def each_chunk(rows, body):
    def step(index, carry):
        body(pl.ds(pl.multiple_of(index * ROW_CHUNK, ROW_CHUNK), ROW_CHUNK))
        return carry

    lax.fori_loop(0, rows // ROW_CHUNK, step, 0)


def store_shards(target, weight, dp):
    for block in range(8):
        target[shard_of(block ^ dp)] = weight[block * UNIT : (block + 1) * UNIT]


SMEM = pl.BlockSpec(memory_space=pltpu.SMEM)
VMEM = pl.BlockSpec(memory_space=pltpu.VMEM)
ANY = pl.BlockSpec(memory_space=pl.ANY)


def params(limit=62):
    return pltpu.CompilerParams(vmem_limit_bytes=limit * 1024 * 1024)


def cost_of(microseconds):
    return pl.CostEstimate(flops=int(microseconds * 1.1e9), bytes_accessed=4 << 20, transcendentals=0)


def sds(shape, dtype):
    return jax.ShapeDtypeStruct(shape, dtype)


def weight_copies(pieces, sc, wbuf, obuf, wsem, osem, columns=(0, 1, 2)):
    groups, outs = [[], [], []], []
    wide = 2 * UNIT
    for index, refs in enumerate(pieces):
        at = slice(index * wide, (index + 1) * wide)
        if len(refs) > 1:
            column = 0
            for ref in refs[:-1]:
                for source in [ref] if len(ref.shape) == 2 else [ref.at[c] for c in range(ref.shape[0])]:
                    if column in columns:
                        low = (columns.index(column) * len(pieces) + index) * wide
                        groups[column].append(copy_of(source, wbuf.at[:, low : low + wide], wsem.at[column, index, 0]))
                    column += 1
            if obuf is not None:
                outs.append(copy_of(refs[-1], obuf.at[at, :], osem.at[index, 0]))
            continue
        rest, = refs
        rows = rest.shape[2]
        part = wide // rest.shape[0]
        for quarter in range(rest.shape[0]):
            place = quarter ^ (sc[1] if rest.shape[0] == 4 else sc[3])
            for column in columns:
                low = (columns.index(column) * len(pieces) + index) * wide
                groups[column].append(
                    copy_of(
                        rest.at[quarter, column],
                        wbuf.at[pl.ds(pl.multiple_of(place * rows, rows), rows), low : low + wide],
                        wsem.at[column, index, quarter],
                    )
                )
            for block in range(4 if obuf is not None else 0):
                outs.append(
                    copy_of(
                        rest.at[quarter, 3, block * part : (block + 1) * part, :],
                        obuf.at[pl.ds(pl.multiple_of(index * wide + place * part, part), part), block * wide : (block + 1) * wide],
                        osem.at[index, 4 * quarter + block],
                    )
                )
    return groups, outs


def attention_fwd_call(scalars, residual, others, pieces, partial, norm):
    rows, depth = others[0].shape
    causal = len(others) == 1
    number, wide = 2 * len(pieces), 2 * len(pieces) * UNIT
    last, has_partial = norm is not None, partial is not None

    def kernel(*refs):
        it = iter(refs)
        sc = next(it)
        in_refs = [next(it) for _ in others]
        gain_ref, bias_ref = (next(it), next(it)) if last else (None, None)
        old_rows = [next(it) for _ in residual[1:]] if last else []
        res_in = next(it) if last else None
        part_in = next(it) if has_partial else None
        w_refs = [[next(it) for _ in piece] for piece in pieces]
        q_ref, k_ref, v_ref, att_ref, lse_ref = (next(it) for _ in range(5))
        if last:
            low_ref, hat_ref, inv_ref = next(it), next(it), next(it)
        else:
            sum_ref = next(it)
        wbuf, obuf, att_all, diagonal, wsem, osem, lsem = (next(it) for _ in range(7))
        if last:
            acc, old = next(it), next(it)
        length = sc[0]
        groups, outs = weight_copies(w_refs, sc, wbuf, obuf, wsem, osem)
        for copies in groups + [outs]:
            for copy in copies:
                copy.start()
        target = acc if last else sum_ref
        late = []
        if has_partial:
            late.append(copy_of(part_in, target, lsem.at[0]))
        if last:
            late.append(copy_of(res_in, old, lsem.at[1]))
        for copy in late:
            copy.start()
        if causal:
            fill_diagonal(diagonal)
        for c, result in enumerate((q_ref, k_ref, v_ref)):
            for copy in groups[c]:
                copy.wait()
            rows_in = in_refs[0] if causal or c == 0 else in_refs[1]
            proj = dot(rows_in[...], wbuf[:, c * wide : (c + 1) * wide]).astype(BF16)
            if c == 0:
                proj = (proj.astype(F32) * SCORE_SCALE).astype(BF16)
            for index in range(number):
                result[index] = proj[:, index * UNIT : (index + 1) * UNIT]

        def step(u, carry):
            attended = attend_unit(q_ref[u], k_ref[u], v_ref[u], length, causal, diagonal, lse_ref.at[u])
            att_ref[u] = attended
            att_all[:, pl.ds(pl.multiple_of(u * UNIT, UNIT), UNIT)] = attended
            return carry

        lax.fori_loop(0, number, step, 0)
        for copy in outs + late:
            copy.wait()
        if has_partial:
            target[...] += dot(att_all[...], obuf[...])
        else:
            target[...] = dot(att_all[...], obuf[...])
        if last:
            def chunk(at):
                before = old[at, :].astype(F32)
                if old_rows:
                    before = before * old_rows[0][...] + old_rows[1][...]
                normed, hat, inverse = norm_chunk(RESIDUAL_ALPHA * before + acc[at, :], gain_ref[...], bias_ref[...])
                low_ref[at, :] = normed.astype(BF16)
                hat_ref[at, :] = hat
                inv_ref[at, :] = jnp.broadcast_to(inverse, (ROW_CHUNK, 128))

            each_chunk(rows, chunk)

    unit_rows = sds((number, rows, UNIT), BF16)
    shapes = [unit_rows] * 4 + [sds((number, 2, rows), F32)]
    if last:
        shapes += [sds((rows, depth), BF16), sds((rows, depth), F32), sds((rows, 128), F32)]
    else:
        shapes += [sds((rows, depth), F32)]
    args = [scalars, *others]
    if last:
        args += [*norm, *residual[1:]]
    tail = ([residual[0]] if last else []) + ([partial] if has_partial else [])
    tail += [array for piece in pieces for array in piece]
    scratch = [
        pltpu.VMEM((depth, 3 * wide), BF16),
        pltpu.VMEM((wide, depth), BF16),
        pltpu.VMEM((rows, wide), BF16),
        pltpu.VMEM((QUERY_BLOCK, QUERY_BLOCK), F32),
        pltpu.SemaphoreType.DMA((3, len(pieces), 4)),
        pltpu.SemaphoreType.DMA((len(pieces), 16)),
        pltpu.SemaphoreType.DMA((2,)),
    ]
    if last:
        scratch += [pltpu.VMEM((rows, depth), F32), pltpu.VMEM((rows, depth), residual[0].dtype)]
    return pl.pallas_call(
        kernel,
        out_shape=shapes,
        in_specs=[SMEM] + [VMEM] * (len(args) - 1) + [ANY] * len(tail),
        out_specs=[VMEM] * len(shapes),
        scratch_shapes=scratch,
        compiler_params=params(),
        cost_estimate=cost_of(0.6 * number),
        name="self_fwd" if causal else "cross_fwd",
    )(*args, *tail)


def attention_bwd_call(scalars, grad_low, others, pieces, saved, plan, carried, norm, results=1):
    rows, depth = grad_low.shape
    causal = len(others) == 1
    number, n_in, wide = len(plan), len(others), len(plan) * UNIT
    last = norm is not None
    skip = 1 if last else 0

    def kernel(*refs):
        it = iter(refs)
        sc = next(it)
        h_ref = next(it)
        in_refs = [next(it) for _ in range(n_in)]
        gain_ref = next(it) if last else None
        late_in = [next(it), next(it)] if last else []
        acc_in = next(it) if last else None
        w_refs = [[next(it) for _ in piece] for piece in pieces]
        s_refs = [[next(it) for _ in call] for call in saved]
        if last:
            low_ref, scaled_ref, gsum_ref, bsum_ref = (next(it) for _ in range(4))
        dall_ref = next(it)
        g_refs = [next(it) for _ in range(results)]
        wbuf, obuf, sbuf, lbuf, att_all, grad_all = (next(it) for _ in range(6))
        stage, diagonal = next(it), next(it)
        if last:
            dquery, acc, hat, inv = (next(it) for _ in range(4))
        wsem, osem, ssem, gsem, lsem = (next(it) for _ in range(5))
        length, dp = sc[0], sc[2]

        groups, o_copies = weight_copies(w_refs, sc, wbuf, obuf, wsem, osem, (0,) if last else ())
        for copy in o_copies:
            copy.start()
        s_copies = []
        for index, unit in enumerate(plan):
            lanes = slice(index * UNIT, (index + 1) * UNIT)
            call = s_refs[unit[0]]
            for c in range(3):
                s_copies.append(copy_of(call[c].at[unit[1]], sbuf.at[index, c], ssem.at[c, index]))
            s_copies.append(copy_of(call[3].at[unit[1]], att_all.at[:, lanes], ssem.at[3, index]))
            s_copies.append(copy_of(call[4].at[unit[1]], lbuf.at[index], ssem.at[4, index]))
        late = []
        if last:
            late = groups[0] + [
                copy_of(source, target, lsem.at[index])
                for index, (source, target) in enumerate(((acc_in, acc), (late_in[0], hat), (late_in[1], inv)))
            ]
        for copy in s_copies + late:
            copy.start()
        if causal:
            fill_diagonal(diagonal)
        for copy in o_copies:
            copy.wait()
        grad_att = dot_nt(h_ref[...], obuf[...]).astype(BF16)
        for index in range(number):
            grad_all[index] = grad_att[:, index * UNIT : (index + 1) * UNIT]
        for copy in s_copies:
            copy.wait()

        def step(u, carry):
            at = pl.ds(pl.multiple_of(u * UNIT, UNIT), UNIT)
            parts = attend_back_unit(
                sbuf[u, 0], sbuf[u, 1], sbuf[u, 2], att_all[:, at], grad_all[u], length, causal, diagonal, lbuf.at[u]
            )
            if last:
                dquery[:, at] = parts[0]
            for c in range(skip, 3):
                dall_ref[:, pl.ds(pl.multiple_of((c - skip) * wide + u * UNIT, UNIT), UNIT)] = parts[c]
            return carry

        lax.fori_loop(0, number, step, 0)

        share = number // 2 // results

        def keep(rows_in, source, column):
            weight = dot_tn(rows_in[...], source).astype(BF16)
            for index in range(number):
                piece = index // 2
                target = stage.at[piece // share, (index % 2) * 4 + column, piece % share]
                store_shards(target, weight[:, index * UNIT : (index + 1) * UNIT], dp)

        if last:
            keep(in_refs[0], dquery[...], 0)
        for c in range(skip, 3):
            keep(in_refs[-1], dall_ref[:, (c - skip) * wide : (c - skip + 1) * wide], c)
        keep(h_ref, att_all[...], 3)
        g_copies = [copy_of(stage.at[index], ref, gsem.at[index]) for index, ref in enumerate(g_refs)]
        for copy in g_copies:
            copy.start()
        for copy in late:
            copy.wait()
        if last:
            acc[...] += dot_nt(dquery[...], wbuf[...])
            norm_back_rows(acc, hat, inv, gain_ref, low_ref, scaled_ref, gsum_ref, bsum_ref, rows)
        for copy in g_copies:
            copy.wait()

    big = sds((rows, depth), F32)
    shapes = []
    if last:
        shapes += [sds((rows, depth), BF16), big, sds((8, depth), F32), sds((8, depth), F32)]
    shapes.append(sds((rows, (3 - skip) * wide), BF16))
    specs_out = [VMEM] * len(shapes) + [ANY] * results
    shapes += [sds((8, number // 2 // results, 8, UNIT, UNIT), BF16)] * results
    args = [scalars, grad_low, *others] + ([norm[2]] if last else [])
    tail = [norm[0], norm[1], carried] if last else []
    tail += [array for piece in pieces for array in piece]
    for call in saved:
        tail += call
    scratch = [
        pltpu.VMEM((depth, wide) if last else (16, 128), BF16),
        pltpu.VMEM((wide, depth), BF16),
        pltpu.VMEM((number, 3, rows, UNIT), BF16),
        pltpu.VMEM((number, 2, rows), F32),
        pltpu.VMEM((rows, wide), BF16),
        pltpu.VMEM((number, rows, UNIT), BF16),
        pltpu.VMEM((results, 8, number // 2 // results, 8, UNIT, UNIT), BF16),
        pltpu.VMEM((QUERY_BLOCK, QUERY_BLOCK), F32),
    ]
    if last:
        scratch += [pltpu.VMEM((rows, wide), BF16), pltpu.VMEM((rows, depth), F32), pltpu.VMEM((rows, depth), F32), pltpu.VMEM((rows, 128), F32)]
    scratch += [
        pltpu.SemaphoreType.DMA((3, len(pieces), 4)),
        pltpu.SemaphoreType.DMA((len(pieces), 16)),
        pltpu.SemaphoreType.DMA((5, number)),
        pltpu.SemaphoreType.DMA((results,)),
        pltpu.SemaphoreType.DMA((4,)),
    ]
    return pl.pallas_call(
        kernel,
        out_shape=shapes,
        in_specs=[SMEM] + [VMEM] * (len(args) - 1) + [ANY] * len(tail),
        out_specs=specs_out,
        scratch_shapes=scratch,
        compiler_params=params(),
        cost_estimate=cost_of(4.2 * number),
        name="self_bwd" if causal else "cross_bwd",
    )(*args, *tail)


def inputs_back_call(scalars, base, parts, memory_part):
    rows, depth = base.shape
    jobs = [(0, grad, pieces, (0, 1, 2)) for grad, pieces in parts] + [(1, *memory_part, (1, 2))]

    def kernel(*refs):
        it = iter(refs)
        sc, base_ref = next(it), next(it)
        grads = [next(it) for _ in jobs]
        w_refs = [[[next(it) for _ in piece] for piece in pieces] for _, _, pieces, _ in jobs]
        outs = [next(it), next(it)]
        bufs, sems = [next(it) for _ in jobs], [next(it) for _ in jobs]
        copies = []
        for index, (_, _, _, columns) in enumerate(jobs):
            groups, _ = weight_copies(w_refs[index], sc, bufs[index], None, sems[index], None, columns)
            copies.append([copy for group in groups for copy in group])
            for copy in copies[-1]:
                copy.start()
        outs[0][...] = base_ref[...]
        for index, (out, _, _, _) in enumerate(jobs):
            for copy in copies[index]:
                copy.wait()
            if out:
                outs[1][...] = dot_nt(grads[index][...], bufs[index][...])
            else:
                outs[0][...] += dot_nt(grads[index][...], bufs[index][...])

    args = [scalars, base] + [grad for _, grad, _, _ in jobs]
    tail = [array for _, _, pieces, _ in jobs for piece in pieces for array in piece]
    return pl.pallas_call(
        kernel,
        out_shape=[sds((rows, depth), F32)] * 2,
        in_specs=[SMEM] + [VMEM] * (len(args) - 1) + [ANY] * len(tail),
        out_specs=[VMEM] * 2,
        scratch_shapes=[pltpu.VMEM((depth, grad.shape[1]), BF16) for _, grad, _, _ in jobs]
        + [pltpu.SemaphoreType.DMA((3, len(pieces), 4)) for _, _, pieces, _ in jobs],
        compiler_params=params(),
        cost_estimate=cost_of(12),
        name="inputs_back",
    )(*args, *tail)


def norm_back_rows(acc, hat, inv, gain_ref, low_ref, scaled_ref, gsum_ref, bsum_ref, rows):
    gsum_ref[...] = jnp.zeros_like(gsum_ref)
    bsum_ref[...] = jnp.zeros_like(bsum_ref)

    def chunk(at):
        gradient, normed = acc[at, :], hat[at, :]
        grad_in = norm_back_chunk(gradient, normed, inv[at, :1], gain_ref[...])
        low_ref[at, :] = grad_in.astype(BF16)
        scaled_ref[at, :] = RESIDUAL_ALPHA * grad_in
        gsum_ref[...] += fold_rows(gradient * normed)
        bsum_ref[...] += fold_rows(gradient)

    each_chunk(rows, chunk)


GELU_SCALE = 0.7978845608028654
GELU_CUBE = 0.044715


def gelu_and_slope(pre):
    square = pre * pre
    inner = pre * (GELU_SCALE + (GELU_SCALE * GELU_CUBE) * square)
    curve = jnp.tanh(inner)
    half = 0.5 + 0.5 * curve
    slope = half * (1.0 + pre * (1.0 - curve) * (GELU_SCALE + (3.0 * GELU_SCALE * GELU_CUBE) * square))
    return pre * half, slope


FFN_PART = FFN_UNIT // 2


def ffn_copies(pieces, order, ubuf, dbuf, usem, dsem):
    ups, downs = [], []
    for index, refs in enumerate(pieces):
        wide = 2 * FFN_UNIT
        at = slice(index * wide, (index + 1) * wide)
        if len(refs) == 2:
            ups.append([copy_of(refs[0], ubuf.at[:, at], usem.at[index, 0])])
            downs.append([copy_of(refs[1], dbuf.at[at, :], dsem.at[index, 0])])
            continue
        ups.append([])
        downs.append([])
        rows = refs[0].shape[1]
        for quarter in range(4):
            up = refs[quarter].at[0]
            down = refs[quarter].at[1] if quarter < 3 else refs[4].at[0]
            place = (quarter ^ order) * rows
            ups[-1].append(copy_of(up, ubuf.at[pl.ds(pl.multiple_of(place, rows), rows), at], usem.at[index, quarter]))
            downs[-1].append(
                copy_of(down, dbuf.at[pl.ds(pl.multiple_of(index * wide + place, rows), rows), :], dsem.at[index, quarter])
            )
    return ups, downs


def ffn_fwd_call(scalars, inputs, pieces, partial, final):
    rows, depth = inputs.shape
    number = 2 * len(pieces)
    last, has_partial = final is not None, partial is not None

    def kernel(*refs):
        it = iter(refs)
        sc, x_ref = next(it), next(it)
        if last:
            gain_old, bias_old, gain_ref, bias_ref = (next(it) for _ in range(4))
            late_in = [next(it), next(it)]
        part_in = next(it) if has_partial else None
        w_refs = [[next(it) for _ in piece] for piece in pieces]
        if last:
            out_ref, low_ref, scaled_ref, gsum_ref, bsum_ref = (next(it) for _ in range(5))
        else:
            sum_ref = next(it)
        act_ref, slope_ref = next(it), next(it)
        ubuf, dbuf, abuf, sbuf, pbuf, psem = (next(it) for _ in range(6))
        if last:
            acc, hat, cot, lsem = (next(it) for _ in range(4))
        wsem, gsem = next(it), next(it)
        target = acc if last else sum_ref

        up_copies, down_copies = ffn_copies(w_refs, sc[1], ubuf, dbuf, wsem.at[0], wsem.at[1])
        for copies in up_copies + down_copies:
            for copy in copies:
                copy.start()
        if has_partial:
            part_copy = copy_of(part_in, target, psem)
            part_copy.start()
        if last:
            late = [copy_of(late_in[0], hat, lsem.at[0]), copy_of(late_in[1], cot, lsem.at[1])]
            for copy in late:
                copy.start()
        saves = []

        def gate(pre, index):
            activated, slope = gelu_and_slope(pre)
            abuf[:, index * FFN_UNIT : (index + 1) * FFN_UNIT] = activated.astype(BF16)
            sbuf[:, index * FFN_UNIT : (index + 1) * FFN_UNIT] = slope.astype(BF16)

        for index in range(number):
            if index % 2 == 0:
                for copy in up_copies[index // 2]:
                    copy.wait()
            if index:
                gate(pbuf[(index - 1) % 2], index - 1)
            pbuf[index % 2] = dot(x_ref[...], ubuf[:, index * FFN_UNIT : (index + 1) * FFN_UNIT])
        gate(pbuf[(number - 1) % 2], number - 1)
        for index in range(number):
            at = slice(index * FFN_UNIT, (index + 1) * FFN_UNIT)
            saves += [
                copy_of(abuf.at[:, at], act_ref.at[index], gsem.at[0, index]),
                copy_of(sbuf.at[:, at], slope_ref.at[index], gsem.at[1, index]),
            ]
        for copy in saves:
            copy.start()
        for copies in down_copies:
            for copy in copies:
                copy.wait()
        if has_partial:
            part_copy.wait()
            target[...] += dot(abuf[...], dbuf[...])
        else:
            target[...] = dot(abuf[...], dbuf[...])
        if last:
            for copy in late:
                copy.wait()
            gsum_ref[...] = jnp.zeros_like(gsum_ref)
            bsum_ref[...] = jnp.zeros_like(bsum_ref)

            def chunk(at):
                old = hat[at, :] * gain_old[...] + bias_old[...]
                normed, xhat, inverse = norm_chunk(RESIDUAL_ALPHA * old + acc[at, :], gain_ref[...], bias_ref[...])
                out_ref[at, :] = normed.astype(BF16)
                gradient = cot[at, :].astype(F32)
                grad_in = norm_back_chunk(gradient, xhat, inverse, gain_ref[...])
                low_ref[at, :] = grad_in.astype(BF16)
                scaled_ref[at, :] = RESIDUAL_ALPHA * grad_in
                gsum_ref[...] += fold_rows(gradient * xhat)
                bsum_ref[...] += fold_rows(gradient)

            each_chunk(rows, chunk)
        for copy in saves:
            copy.wait()

    big, low = sds((rows, depth), F32), sds((rows, depth), BF16)
    if last:
        shapes = [low, low, big, sds((8, depth), F32), sds((8, depth), F32)]
    else:
        shapes = [big]
    specs_out = [VMEM] * len(shapes) + [ANY, ANY]
    shapes += [sds((number, rows, FFN_UNIT), BF16)] * 2
    args = [scalars, inputs]
    if last:
        args += [final[1], final[2], final[4], final[5]]
    specs = [SMEM] + [VMEM] * (len(args) - 1)
    tail = ([final[0], final[3]] if last else []) + ([partial] if has_partial else []) + [array for piece in pieces for array in piece]
    scratch = [
        pltpu.VMEM((depth, number * FFN_UNIT), BF16),
        pltpu.VMEM((number * FFN_UNIT, depth), BF16),
        pltpu.VMEM((rows, number * FFN_UNIT), BF16),
        pltpu.VMEM((rows, number * FFN_UNIT), BF16),
        pltpu.VMEM((2, rows, FFN_UNIT), F32),
        pltpu.SemaphoreType.DMA,
    ]
    if last:
        scratch += [
            pltpu.VMEM((rows, depth), F32),
            pltpu.VMEM((rows, depth), F32),
            pltpu.VMEM((rows, depth), BF16),
            pltpu.SemaphoreType.DMA((2,)),
        ]
    scratch += [pltpu.SemaphoreType.DMA((2, len(pieces), 4)), pltpu.SemaphoreType.DMA((2, number))]
    return pl.pallas_call(
        kernel,
        out_shape=shapes,
        in_specs=specs + [ANY] * len(tail),
        out_specs=specs_out,
        scratch_shapes=scratch,
        compiler_params=params(),
        cost_estimate=cost_of(12),
        name="ffn_fwd",
    )(*args, *tail)


def ffn_bwd_call(scalars, grad_low, inputs, pieces, saved, plan, carried, norm):
    rows, depth = inputs.shape
    number = len(plan)
    last = norm is not None

    def kernel(*refs):
        it = iter(refs)
        sc, g_in, x_ref = (next(it) for _ in range(3))
        gain_ref = next(it) if last else None
        late_in = [next(it), next(it)] if last else []
        acc_in = next(it)
        w_refs = [[next(it) for _ in piece] for piece in pieces]
        s_refs = [[next(it) for _ in call] for call in saved]
        if last:
            low_ref, scaled_ref, gsum_ref, bsum_ref = (next(it) for _ in range(4))
        else:
            sum_ref = next(it)
        g_ref = next(it)
        ubuf, dbuf, abuf, sbuf, gbuf, stage, psem = (next(it) for _ in range(7))
        if last:
            acc, hat, inv, lsem = (next(it) for _ in range(4))
        wsem, ssem, gsem = next(it), next(it), next(it)
        order, dp = sc[1], sc[2]
        target = acc if last else sum_ref

        ups, downs = ffn_copies(w_refs, order, ubuf, dbuf, wsem.at[0], wsem.at[1])
        slopes, acts = [], []
        for index, (call, at) in enumerate(plan):
            lanes = slice(index * FFN_UNIT, (index + 1) * FFN_UNIT)
            slopes.append(copy_of(s_refs[call][1].at[at], sbuf.at[index], ssem.at[0, index]))
            acts.append(copy_of(s_refs[call][0].at[at], abuf.at[:, lanes], ssem.at[1, index]))
        for copies in downs + [slopes, acts] + ups:
            for copy in copies:
                copy.start()
        part_copy = copy_of(acc_in, target, psem)
        part_copy.start()
        if last:
            late = [copy_of(late_in[0], hat, lsem.at[0]), copy_of(late_in[1], inv, lsem.at[1])]
            for copy in late:
                copy.start()
        for index in range(number):
            if index % 2 == 0:
                for copy in downs[index // 2]:
                    copy.wait()
            slopes[index].wait()
            grad_act = dot_nt(g_in[...], dbuf[index * FFN_UNIT : (index + 1) * FFN_UNIT, :]) * sbuf[index].astype(F32)
            gbuf[:, index * FFN_UNIT : (index + 1) * FFN_UNIT] = grad_act.astype(BF16)
        for copy in acts:
            copy.wait()

        def keep(rows_in, source, column):
            for half in range(number // 2):
                wide = 2 * FFN_UNIT
                weight = dot_tn(rows_in[...], source[:, half * wide : (half + 1) * wide]).astype(BF16)
                for inner in range(4):
                    part = weight[:, inner * FFN_PART : (inner + 1) * FFN_PART]
                    store_shards(stage.at[2 * inner + column, half], part, dp)

        keep(x_ref, gbuf, 0)
        keep(g_in, abuf, 1)
        g_copies = [copy_of(stage, g_ref, gsem)]
        for copy in g_copies:
            copy.start()
        for copies in ups:
            for copy in copies:
                copy.wait()
        part_copy.wait()
        target[...] += dot_nt(gbuf[...], ubuf[...])
        if last:
            for copy in late:
                copy.wait()
            norm_back_rows(acc, hat, inv, gain_ref, low_ref, scaled_ref, gsum_ref, bsum_ref, rows)
        for copy in g_copies:
            copy.wait()

    big, low = sds((rows, depth), F32), sds((rows, depth), BF16)
    shapes = [low, big, sds((8, depth), F32), sds((8, depth), F32)] if last else [big]
    specs_out = [VMEM] * len(shapes) + [ANY]
    shapes.append(sds((8, number // 2, 8, UNIT, FFN_PART), BF16))
    args = [scalars, grad_low, inputs] + ([norm[2]] if last else [])
    specs = [SMEM] + [VMEM] * (len(args) - 1)
    tail = ([norm[0], norm[1]] if last else []) + [carried] + [array for piece in pieces for array in piece]
    for call in saved:
        tail += call
    scratch = [
        pltpu.VMEM((depth, number * FFN_UNIT), BF16),
        pltpu.VMEM((number * FFN_UNIT, depth), BF16),
        pltpu.VMEM((rows, number * FFN_UNIT), BF16),
        pltpu.VMEM((number, rows, FFN_UNIT), BF16),
        pltpu.VMEM((rows, number * FFN_UNIT), BF16),
        pltpu.VMEM((8, number // 2, 8, UNIT, FFN_PART), BF16),
        pltpu.SemaphoreType.DMA,
    ]
    if last:
        scratch += [
            pltpu.VMEM((rows, depth), F32),
            pltpu.VMEM((rows, depth), F32),
            pltpu.VMEM((rows, 128), F32),
            pltpu.SemaphoreType.DMA((2,)),
        ]
    scratch += [pltpu.SemaphoreType.DMA((2, len(pieces), 4)), pltpu.SemaphoreType.DMA((2, number)), pltpu.SemaphoreType.DMA]
    return pl.pallas_call(
        kernel,
        out_shape=shapes,
        in_specs=specs + [ANY] * len(tail),
        out_specs=specs_out,
        scratch_shapes=scratch,
        compiler_params=params(),
        cost_estimate=cost_of(17),
        name="ffn_bwd",
    )(*args, *tail)


def combine(jobs, shapes):
    arrays = []
    for terms, _, _, _ in jobs:
        for array, _ in terms:
            if not any(array is known for known in arrays):
                arrays.append(array)
    position = {id(array): index for index, array in enumerate(arrays)}

    def part_shape(array, index):
        kept = []
        for extent, at in zip(array.shape, index + (slice(None),) * (array.ndim - len(index))):
            if isinstance(at, slice):
                kept.append(len(range(*at.indices(extent))))
        return tuple(kept)

    part_shapes = [part_shape(*terms[0]) for terms, _, _, _ in jobs]
    count = sum(len(terms) for terms, _, _, _ in jobs)

    def kernel(*refs):
        ins, outs = refs[: len(arrays)], refs[len(arrays) : len(arrays) + len(shapes)]
        rest = refs[len(arrays) + len(shapes) :]
        term_bufs, sum_bufs, isem, osem = rest[:count], rest[count : count + len(jobs)], rest[-2], rest[-1]
        loads, number = [], 0
        for terms, _, _, _ in jobs:
            loads.append([])
            for array, index in terms:
                loads[-1].append(copy_of(ins[position[id(array)]].at[index], term_bufs[number], isem.at[number]))
                number += 1
        for group in loads:
            for copy in group:
                copy.start()
        stores, number = [], 0
        for job, (terms, out, place, kind) in enumerate(jobs):
            for copy in loads[job]:
                copy.wait()
            bufs = term_bufs[number : number + len(terms)]
            number += len(terms)
            lead = part_shapes[job][:-2]
            size = 1
            for extent in lead:
                size *= extent

            def one(flat, carry, bufs=bufs, lead=lead, target=sum_bufs[job]):
                index, left = [], flat
                for extent in reversed(lead):
                    index.append(lax.rem(left, extent))
                    left = lax.div(left, extent)
                index = tuple(reversed(index))
                total = bufs[0][index].astype(F32)
                for buf in bufs[1:]:
                    total = total + buf[index].astype(F32)
                target[index] = total.astype(target.dtype)
                return carry

            if kind == "range":
                lax.fori_loop(0, size, one, 0)
            else:
                total = bufs[0][0].astype(F32)
                for buf in bufs[1:]:
                    total = total + buf[0].astype(F32)
                sum_bufs[job][...] = jnp.transpose(total) if kind == "turned" else total
            stores.append(copy_of(sum_bufs[job], outs[out].at[place], osem.at[job]))
            stores[-1].start()
        for copy in stores:
            copy.wait()

    scratch = [pltpu.VMEM(part_shapes[job], array.dtype) for job, (terms, _, _, _) in enumerate(jobs) for array, _ in terms]
    for job, (_, out, _, kind) in enumerate(jobs):
        shape = part_shapes[job]
        shape = {"range": shape, "plain": shape[1:], "turned": shape[:0:-1]}[kind]
        scratch.append(pltpu.VMEM(shape, shapes[out].dtype))
    scratch += [pltpu.SemaphoreType.DMA((count,)), pltpu.SemaphoreType.DMA((len(jobs),))]
    return pl.pallas_call(
        kernel,
        out_shape=list(shapes),
        in_specs=[ANY] * len(arrays),
        out_specs=[ANY] * len(shapes),
        scratch_shapes=scratch,
        compiler_params=params(),
        cost_estimate=cost_of(3),
        name="combine",
    )(*arrays)


def swap_pairs(count, mask):
    return [(i, i ^ mask) for i in range(count)]


def to_sibling(values):
    return lax.ppermute(values, "tensor", swap_pairs(4, 1))


def over_y(values):
    return lax.ppermute(values, "tensor", swap_pairs(4, 2))


def over_dp(values, mask):
    return lax.ppermute(values, "dp", swap_pairs(8, mask))


def over_x(values):
    return over_dp(values, 1)


def over_z_near(values):
    return over_dp(values, 2)


def over_z_far(values):
    return over_dp(values, 4)


def after(values, *earlier):
    return lax.optimization_barrier((values, *earlier))[0]


MOVES = {"y": over_y, "x": over_x, "z": over_z_near}


class Reduction:
    def __init__(self, sent, portions, finish):
        self.other, self.finish = to_sibling(sent), finish
        self.portions, self.stage, self.sends, self.total = portions, 0, None, None

    def begin(self, kept, *earlier):
        other = after(self.other, *earlier)
        split = (kept.shape[0], 2, 2, 2, 2, *kept.shape[3:])
        arrays = (kept.reshape(split), other.reshape(split))
        self.blocks, self.tail = kept.shape[0], kept.shape[3:]
        self.terms = [[(array, ("b", "y", "x", "z", "w"), low, {}) for array in arrays] for low, _, _ in self.portions]

    def receive(self, *earlier):
        if self.stage == 4:
            moved = after(over_z_far(self.sends[0]), *earlier)
            for (low, _, _), terms in zip(self.portions, self.terms):
                terms.append((moved, ("b",), low, {}))
        elif self.stage:
            for send, (_, _, orders), terms in zip(self.sends, self.portions, self.terms):
                left = tuple(a for a in ("b", "y", "x", "z", "w") if a not in orders[: self.stage])
                terms.append((after(MOVES[orders[self.stage - 1]](send), *earlier), left, 0, {}))

    def jobs(self, first_out):
        jobs, shapes = [], []
        stage = self.stage
        for number, ((low, high, orders), terms) in enumerate(zip(self.portions, self.terms)):
            axis = (*orders, "w", None)[stage]
            picked = []
            for array, axes, start, fixed in terms:
                index = [slice(start, start + high - low)]
                for name in axes[1:]:
                    index.append(1 if name == axis else fixed.get(name, 0 if name in orders[:stage] or (stage > 3 and name == "w") else slice(None)))
                picked.append((array, tuple(index)))
            if stage < 3:
                shapes.append(sds((high - low, *(2,) * (3 - stage), *self.tail), BF16))
                jobs.append((picked, first_out + number, slice(0, high - low), "range"))
            elif stage == 3:
                if not number:
                    shapes.append(sds((self.blocks, *self.tail), BF16))
                jobs.append((picked, first_out, slice(low, high), "range"))
            else:
                if not number:
                    shapes += self.finish[0]
                for block in range(low, high):
                    shift = block - low
                    one = [(a, (slice(index[0].start + shift, index[0].start + shift + 1), *index[1:])) for a, index in picked]
                    out, place, kind = self.finish[1](block)
                    jobs.append((one, first_out + out, place, kind))
        self.stage += 1
        return jobs, shapes


def attention_finish(counts):
    stacks = [sds((count, UNIT, 2 * UNIT) if count > 1 else (UNIT, 2 * UNIT), F32) for count in counts]

    def place_of(block):
        half, matrix = block // 4, block % 4
        lanes = slice(half * UNIT, (half + 1) * UNIT)
        if matrix == 3:
            return len(counts), (lanes, slice(None)), "turned"
        stack = 0 if matrix < counts[0] else 1
        if counts[stack] == 1:
            return stack, (slice(None), lanes), "plain"
        return stack, (matrix - sum(counts[:stack]), slice(None), lanes), "plain"

    return [*stacks, sds((2 * UNIT, UNIT), F32)], place_of


def ffn_finish():
    def place_of(block):
        lanes = slice(block // 2 * FFN_PART, (block // 2 + 1) * FFN_PART)
        if block % 2:
            return 1, (lanes, slice(None)), "turned"
        return 0, (slice(None), lanes), "plain"

    return [sds((UNIT, 4 * FFN_PART), F32), sds((4 * FFN_PART, UNIT), F32)], place_of


def advance(reductions, *earlier):
    jobs, shapes, bounds = [], [], []
    for reduction in reductions:
        reduction.receive(*earlier)
        more, made = reduction.jobs(len(shapes))
        bounds.append((len(shapes), len(shapes) + len(made)))
        jobs, shapes = jobs + more, shapes + made
    results = combine(jobs, shapes)
    for reduction, (low, high) in zip(reductions, bounds):
        reduction.sends = list(results[low:high])
        if reduction.stage == 5:
            reduction.total = results[low:high]
    return list(results)


def sentence_body(
    tokens,
    memory,
    dec_lengths,
    mem_lengths,
    self_qkv,
    self_out,
    cross_q,
    cross_kv,
    cross_out,
    ffn_in,
    ffn_out,
    norm_gains,
    norm_biases,
    cotangent,
):
    dp = lax.axis_index("dp")
    mine = lax.axis_index("tensor")
    order = dp & 3
    inner = (dp >> 1) & 1
    self_scalars = jnp.stack([dec_lengths[0, mine], order, dp, inner]).astype(jnp.int32)
    cross_scalars = jnp.stack([mem_lengths[0, mine], order, dp, inner]).astype(jnp.int32)
    gains = [norm_gains[i : i + 1] for i in range(3)]
    biases = [norm_biases[i : i + 1] for i in range(3)]

    def part_rows(values, parts):
        rows = values.shape[-2] // parts
        place = order if parts == 4 else inner
        return lax.dynamic_slice_in_dim(values, place * rows, rows, values.ndim - 2)

    def folded(values):
        blocks = values.reshape(values.shape[0], 4, 2 * UNIT)
        return blocks.transpose(1, 0, 2).reshape(1, 4 * values.shape[0], 2 * UNIT)

    self_near = over_y(jnp.concatenate([part_rows(self_qkv, 4), folded(part_rows(self_out, 4))]))
    cross_near = over_y(
        jnp.concatenate([part_rows(cross_q, 2)[None], part_rows(cross_kv, 2), folded(part_rows(cross_out, 2))])
    )
    ffn_near = over_y(jnp.stack([part_rows(ffn_in, 4), part_rows(ffn_out, 4)]))
    self_own = (self_qkv, self_out)
    self_sib = tuple(to_sibling(w) for w in self_own)
    self_a = attention_fwd_call(self_scalars, [], [tokens], [self_own, self_sib], None, None)
    self_near = after(self_near, self_a[4])
    self_side, self_up = over_x(self_near), over_z_near(self_near)
    self_corner = over_x(self_up)
    self_rest = jnp.stack([after(self_near, cross_near), self_side, self_up, self_corner])
    cross_up = over_z_near(cross_near)
    self_far = to_sibling(self_rest)
    self_pieces = [self_own, self_sib, (self_rest,), (self_far,)]
    cross_own, ffn_own = (cross_q, cross_kv, cross_out), (ffn_in, ffn_out)
    cross_sib = tuple(to_sibling(after(w, self_near)) for w in cross_own)
    self_b = attention_fwd_call(
        after(self_scalars, *cross_sib), [tokens], [tokens], self_pieces[2:], self_a[5], (gains[0], biases[0])
    )
    first_low, first_hat, first_inv = self_b[5:]
    cross_in = [first_low, memory]
    cross_rest = jnp.stack([cross_near, after(cross_up, self_b[4])])
    cross_far = to_sibling(cross_rest)
    cross_a = attention_fwd_call(after(cross_scalars, ffn_near), [], cross_in, [cross_own, cross_sib], None, None)
    ffn_sib = tuple(to_sibling(after(w, ffn_near)) for w in ffn_own)
    ffn_side, ffn_up = over_x(ffn_near), over_z_near(ffn_near)
    cross_pieces = [cross_own, cross_sib, (cross_rest,), (after(cross_far, cross_a[4]),)]
    cross_b = attention_fwd_call(
        cross_scalars, [first_hat, gains[0], biases[0]], cross_in, cross_pieces[2:], cross_a[5], (gains[1], biases[1])
    )
    second_low, second_hat, second_inv = cross_b[5:]
    ffn_side, ffn_up = after(ffn_side, cross_b[4]), after(ffn_up, cross_b[4])
    up_corner, down_corner = over_x(ffn_up[:1]), over_z_near(ffn_side[1:])
    ffn_pieces = [ffn_own, ffn_sib]
    ffn_a = ffn_fwd_call(cross_scalars, second_low, ffn_pieces, None, None)
    up_corner, down_corner = after(up_corner, ffn_a[0]), after(down_corner, ffn_a[0])
    ffn_rest = (ffn_near, ffn_side, ffn_up, up_corner, down_corner)
    ffn_pieces += [ffn_rest, tuple(to_sibling(w) for w in ffn_rest)]
    ffn_b = ffn_fwd_call(
        cross_scalars, second_low, ffn_pieces[2:], ffn_a[0],
        (second_hat, gains[1], biases[1], cotangent, gains[2], biases[2]),
    )
    out_rows, third_low, third_scaled, third_gain, third_bias = ffn_b[:5]

    def plan_of(pieces):
        return [(piece // 2, 2 * (piece % 2) + half) for piece in pieces for half in (0, 1)]

    ffn_saved = [ffn_a[1:3], ffn_b[5:7]]
    ffn_d = ffn_bwd_call(
        cross_scalars, third_low, second_low, ffn_pieces[1::2], ffn_saved, plan_of((1, 3)), third_scaled, None
    )
    ffn_sum = Reduction(ffn_d[1], [(0, 3, "yxz"), (3, 6, "xzy"), (6, 8, "zyx")], ffn_finish())
    ffn_e = ffn_bwd_call(
        cross_scalars, third_low, second_low, ffn_pieces[::2], ffn_saved, plan_of((0, 2)), ffn_d[0],
        (second_hat, second_inv, gains[1]),
    )
    second_back, second_scaled, second_gain, second_bias = ffn_e[:4]
    ffn_sum.begin(ffn_e[4], second_gain)
    second_back = after(second_back, *advance([ffn_sum]))

    cross_e = attention_bwd_call(
        cross_scalars, second_back, cross_in, cross_pieces[1::2] + cross_pieces[::2],
        [cross_a[:5], cross_b[:5]], plan_of((1, 3, 0, 2)), second_scaled,
        (first_hat, first_inv, gains[0]), 2,
    )
    first_back, first_scaled, first_gain, first_bias, memory_part = cross_e[:5]
    norm_sums = jnp.stack([first_gain, second_gain, third_gain, first_bias, second_bias, third_bias])
    norm_sums = jnp.concatenate([jnp.sum(norm_sums, axis=1), jnp.zeros((2, norm_sums.shape[2]), F32)])
    norm_sums = lax.all_gather(norm_sums, ("dp", "tensor"), axis=0)
    sends = advance([ffn_sum], first_gain)
    cross_sum = Reduction(after(cross_e[5], *sends), [(0, 4, "xyz"), (4, 8, "yzx")], attention_finish((1, 2)))
    first_back = after(first_back, *sends)

    self_saved = [self_a[:5], self_b[:5]]
    self_d = attention_bwd_call(
        self_scalars, first_back, [tokens], self_pieces[1::2], self_saved, plan_of((1, 3)), None, None
    )
    cross_sum.begin(cross_e[6], self_d[0])
    sends = advance([cross_sum, ffn_sum], self_d[0])
    self_sum = Reduction(after(self_d[1], *sends), [(0, 4, "zxy"), (4, 8, "xyz")], attention_finish((3,)))
    first_back = after(first_back, *sends)
    self_e = attention_bwd_call(
        self_scalars, first_back, [tokens], self_pieces[::2], self_saved, plan_of((0, 2)), None, None
    )
    self_sum.begin(self_e[1], self_e[0])
    sends = advance([self_sum])
    grad_tokens, grad_memory = inputs_back_call(
        self_scalars, after(first_scaled, *sends),
        [(self_d[0], self_pieces[1::2]), (self_e[0], self_pieces[::2])],
        (memory_part, cross_pieces[1::2] + cross_pieces[::2]),
    )
    sends = advance([cross_sum, ffn_sum], *sends)
    sends = advance([self_sum, cross_sum], *sends, grad_tokens)
    sends = advance([self_sum, cross_sum, ffn_sum], *sends)
    norm_total = jnp.sum(after(norm_sums, *sends), axis=0)
    sends = advance([self_sum, cross_sum], *sends, norm_total)
    advance([self_sum], *sends)
    self_sum, cross_sum, ffn_sum = self_sum.total, cross_sum.total, ffn_sum.total

    return (
        out_rows,
        grad_tokens,
        grad_memory,
        *self_sum,
        *cross_sum,
        *ffn_sum,
        norm_total[:3],
        norm_total[3:6],
    )


def sentence_fits(mesh, tokens, memory, dec_lengths):
    shape = dict(mesh.shape)
    rows = tokens.shape[0] // mesh.size
    sentences = dec_lengths.shape[1]
    return (
        shape["tensor"] == 4
        and shape["dp"] == 8
        and sentences == 4
        and rows == 512
        and memory.shape[0] // mesh.size == rows
        and tokens.shape[1] == 1024
    )


def smooth_gate(values):
    return jax.nn.gelu(values, approximate=True)


def norm_rows(hidden, norm_gain, norm_bias):
    center = hidden - jnp.mean(hidden, axis=-1, keepdims=True)
    inverse = lax.rsqrt(jnp.mean(center * center, axis=-1, keepdims=True) + NORM_EPSILON)
    normed = center * inverse
    return (normed * norm_gain + norm_bias, normed, inverse)


def norm_back(gradient, normed, inverse, norm_gain):
    scaled = gradient * norm_gain
    grad_in = inverse * (
        scaled
        - jnp.mean(scaled, axis=-1, keepdims=True)
        - normed * jnp.mean(scaled * normed, axis=-1, keepdims=True)
    )
    return (grad_in, jnp.sum(gradient * normed, axis=0), jnp.sum(gradient, axis=0))


def head_view(values, sentences):
    return values.reshape(sentences, -1, values.shape[1] // HEAD_DIM, HEAD_DIM)


def masked_scores(query_heads, key_heads, key_mask):
    scores = jnp.einsum(
        "sqhe,skhe->shqk", query_heads, key_heads, preferred_element_type=jnp.float32
    ) * HEAD_DIM ** (-0.5)
    return jnp.where(key_mask, scores, MASKED_SCORE)


def attention_forward(query_rows, key_rows, value_rows, key_mask, sentences):
    scores = masked_scores(
        head_view(query_rows, sentences), head_view(key_rows, sentences), key_mask
    )
    row_peak = jnp.max(scores, axis=-1, keepdims=True)
    exponent_terms = jnp.exp(scores - row_peak)
    row_sum = jnp.sum(exponent_terms, axis=-1, keepdims=True)
    softmax_probs = exponent_terms / row_sum
    attended = jnp.einsum(
        "shqk,skhe->sqhe",
        softmax_probs.astype(jnp.bfloat16),
        head_view(value_rows, sentences),
        preferred_element_type=jnp.float32,
    ).astype(jnp.bfloat16)
    return (attended.reshape(query_rows.shape), row_peak + jnp.log(row_sum))


def attention_backward(query_rows, key_rows, value_rows, key_mask, log_total, grad_rows, sentences):
    query_heads = head_view(query_rows, sentences)
    key_heads = head_view(key_rows, sentences)
    value_heads = head_view(value_rows, sentences)
    grad_heads = head_view(grad_rows, sentences)
    softmax_probs = jnp.exp(masked_scores(query_heads, key_heads, key_mask) - log_total)
    grad_probs = jnp.einsum(
        "sqhe,skhe->shqk", grad_heads, value_heads, preferred_element_type=jnp.float32
    )
    row_delta = jnp.sum(softmax_probs * grad_probs, axis=-1, keepdims=True)
    grad_scores = (softmax_probs * (grad_probs - row_delta)).astype(jnp.bfloat16)
    score_scale = HEAD_DIM ** (-0.5)
    grad_query = (
        jnp.einsum("shqk,skhe->sqhe", grad_scores, key_heads, preferred_element_type=jnp.float32)
        * score_scale
    ).astype(jnp.bfloat16)
    grad_key = (
        jnp.einsum("shqk,sqhe->skhe", grad_scores, query_heads, preferred_element_type=jnp.float32)
        * score_scale
    ).astype(jnp.bfloat16)
    grad_value = jnp.einsum(
        "shqk,sqhe->skhe",
        softmax_probs.astype(jnp.bfloat16),
        grad_heads,
        preferred_element_type=jnp.float32,
    ).astype(jnp.bfloat16)
    return (
        grad_query.reshape(query_rows.shape),
        grad_key.reshape(key_rows.shape),
        grad_value.reshape(value_rows.shape),
    )


def body(
    tokens,
    memory,
    dec_lengths,
    mem_lengths,
    self_qkv,
    self_out,
    cross_q,
    cross_kv,
    cross_out,
    ffn_in,
    ffn_out,
    norm_gains,
    norm_biases,
    cotangent,
):
    row_share = tokens.shape[0]
    sentences = dec_lengths.shape[1]
    all_tokens, all_memory = (
        lax.all_gather(tokens, "tensor", axis=0, tiled=True),
        lax.all_gather(memory, "tensor", axis=0, tiled=True),
    )
    sentence_len = all_tokens.shape[0] // sentences
    memory_len = all_memory.shape[0] // sentences
    positions = jnp.arange(sentence_len, dtype=jnp.int32)
    self_mask = (
        (positions[None, :] <= positions[:, None])[None]
        & (positions[None, None, :] < dec_lengths[0][:, None, None])
    )[:, None]
    memory_positions = jnp.arange(memory_len, dtype=jnp.int32)
    cross_mask = (memory_positions[None, :] < mem_lengths[0][:, None])[:, None, None, :]

    def branch_rows(attended, weight):
        return lax.psum_scatter(
            jnp.dot(attended, weight, preferred_element_type=jnp.float32).astype(jnp.bfloat16),
            "tensor",
            scatter_dimension=0,
            tiled=True,
        ).astype(jnp.float32)

    def branch_grad(grad_rows, attended, weight):
        grad_low = grad_rows.astype(jnp.bfloat16)
        grad_all = lax.all_gather(grad_low, "tensor", axis=0, tiled=True)
        grad_attended = jnp.dot(grad_all, weight.T, preferred_element_type=jnp.float32).astype(
            jnp.bfloat16
        )
        weight_part = jnp.dot(attended.T, grad_all, preferred_element_type=jnp.float32)
        return (grad_attended, weight_part)

    def gather_normed(values):
        return lax.all_gather(values, "tensor", axis=0, tiled=True)

    def head_input_sum(term):
        return lax.psum_scatter(
            term(jnp.int32(0), row_share * lax.axis_size("tensor")).astype(jnp.bfloat16),
            "tensor",
            scatter_dimension=0,
            tiled=True,
        ).astype(jnp.float32)

    self_proj = jnp.einsum(
        "td,cde->cte", all_tokens, self_qkv, preferred_element_type=jnp.float32
    ).astype(jnp.bfloat16)
    self_att, self_lse = attention_forward(
        self_proj[0], self_proj[1], self_proj[2], self_mask, sentences
    )
    self_branch = branch_rows(self_att, self_out)
    first_norm, first_hat, first_inv = norm_rows(
        RESIDUAL_ALPHA * tokens.astype(jnp.float32) + self_branch, norm_gains[0], norm_biases[0]
    )
    first_all = gather_normed(first_norm.astype(jnp.bfloat16))
    cross_query = jnp.dot(first_all, cross_q, preferred_element_type=jnp.float32).astype(
        jnp.bfloat16
    )
    cross_proj = jnp.einsum(
        "td,cde->cte", all_memory, cross_kv, preferred_element_type=jnp.float32
    ).astype(jnp.bfloat16)
    cross_att, cross_lse = attention_forward(
        cross_query, cross_proj[0], cross_proj[1], cross_mask, sentences
    )
    cross_branch = branch_rows(cross_att, cross_out)
    second_norm, second_hat, second_inv = norm_rows(
        RESIDUAL_ALPHA * first_norm + cross_branch, norm_gains[1], norm_biases[1]
    )
    second_all = gather_normed(second_norm.astype(jnp.bfloat16))
    pre_gate = jnp.dot(second_all, ffn_in, preferred_element_type=jnp.float32)
    activated = smooth_gate(pre_gate).astype(jnp.bfloat16)
    ffn_branch = lax.psum_scatter(
        jnp.dot(activated, ffn_out, preferred_element_type=jnp.float32).astype(jnp.bfloat16),
        "tensor",
        scatter_dimension=0,
        tiled=True,
    ).astype(jnp.float32)
    out_rows, third_hat, third_inv = norm_rows(
        RESIDUAL_ALPHA * second_norm + ffn_branch, norm_gains[2], norm_biases[2]
    )
    grad_third, third_gain, third_bias = norm_back(
        cotangent.astype(jnp.float32), third_hat, third_inv, norm_gains[2]
    )
    grad_ffn_all = lax.all_gather(grad_third.astype(jnp.bfloat16), "tensor", axis=0, tiled=True)
    unused_gate, gate_pull = jax.vjp(smooth_gate, pre_gate)
    grad_act = gate_pull(jnp.dot(grad_ffn_all, ffn_out.T, preferred_element_type=jnp.float32))[
        0
    ].astype(jnp.bfloat16)
    grad_ffn_out = jnp.dot(activated.T, grad_ffn_all, preferred_element_type=jnp.float32)
    grad_ffn_in = jnp.dot(second_all.T, grad_act, preferred_element_type=jnp.float32)
    grad_second = RESIDUAL_ALPHA * grad_third + lax.psum_scatter(
        jnp.dot(grad_act, ffn_in.T, preferred_element_type=jnp.float32).astype(jnp.bfloat16),
        "tensor",
        scatter_dimension=0,
        tiled=True,
    ).astype(jnp.float32)
    grad_second_in, second_gain, second_bias = norm_back(
        grad_second, second_hat, second_inv, norm_gains[1]
    )
    grad_cross_att, cross_out_part = branch_grad(grad_second_in, cross_att, cross_out)
    grad_cq, grad_ck, grad_cv = attention_backward(
        cross_query, cross_proj[0], cross_proj[1], cross_mask, cross_lse, grad_cross_att, sentences
    )
    grad_cross_q = jnp.dot(first_all.T, grad_cq, preferred_element_type=jnp.float32)
    cross_grads = jnp.stack([grad_ck, grad_cv])
    grad_cross_kv = jnp.einsum(
        "td,cte->cde", all_memory, cross_grads, preferred_element_type=jnp.float32
    )
    grad_memory = lax.psum_scatter(
        jnp.einsum("cte,cde->td", cross_grads, cross_kv, preferred_element_type=jnp.float32).astype(
            jnp.bfloat16
        ),
        "tensor",
        scatter_dimension=0,
        tiled=True,
    ).astype(jnp.float32)

    def cross_input_term(first_row, row_total):
        return jnp.dot(grad_cq, cross_q.T, preferred_element_type=jnp.float32)

    cross_input = head_input_sum(cross_input_term)
    grad_first = RESIDUAL_ALPHA * grad_second_in + cross_input
    grad_first_in, first_gain, first_bias = norm_back(
        grad_first, first_hat, first_inv, norm_gains[0]
    )
    grad_self_att, self_out_part = branch_grad(grad_first_in, self_att, self_out)
    grad_sq, grad_sk, grad_sv = attention_backward(
        self_proj[0], self_proj[1], self_proj[2], self_mask, self_lse, grad_self_att, sentences
    )
    self_grads = jnp.stack([grad_sq, grad_sk, grad_sv])
    grad_self_qkv = jnp.einsum(
        "td,cte->cde", all_tokens, self_grads, preferred_element_type=jnp.float32
    )

    def self_input_term(first_row, row_total):
        return jnp.einsum("cte,cde->td", self_grads, self_qkv, preferred_element_type=jnp.float32)

    self_input = head_input_sum(self_input_term)
    grad_tokens = RESIDUAL_ALPHA * grad_first_in + self_input
    summed = (
        lax.psum_scatter(
            grad_self_qkv.astype(jnp.bfloat16), "dp", scatter_dimension=1, tiled=True
        ).astype(jnp.float32),
        lax.psum_scatter(
            self_out_part.astype(jnp.bfloat16), "dp", scatter_dimension=1, tiled=True
        ).astype(jnp.float32),
        lax.psum_scatter(
            grad_cross_q.astype(jnp.bfloat16), "dp", scatter_dimension=0, tiled=True
        ).astype(jnp.float32),
        lax.psum_scatter(
            grad_cross_kv.astype(jnp.bfloat16), "dp", scatter_dimension=1, tiled=True
        ).astype(jnp.float32),
        lax.psum_scatter(
            cross_out_part.astype(jnp.bfloat16), "dp", scatter_dimension=1, tiled=True
        ).astype(jnp.float32),
        lax.psum_scatter(
            grad_ffn_in.astype(jnp.bfloat16), "dp", scatter_dimension=0, tiled=True
        ).astype(jnp.float32),
        lax.psum_scatter(
            grad_ffn_out.astype(jnp.bfloat16), "dp", scatter_dimension=1, tiled=True
        ).astype(jnp.float32),
    )
    gain_total, bias_total = lax.psum(
        (
            jnp.stack([first_gain, second_gain, third_gain]),
            jnp.stack([first_bias, second_bias, third_bias]),
        ),
        ("dp", "tensor"),
    )
    return (
        out_rows.astype(jnp.bfloat16),
        grad_tokens,
        grad_memory,
        summed[0],
        summed[1],
        summed[2],
        summed[3],
        summed[4],
        summed[5],
        summed[6],
        gain_total,
        bias_total,
    )


def solution(mesh):
    in_specs = (
        P(("dp", "tensor"), None),
        P(("dp", "tensor"), None),
        P("dp", None),
        P("dp", None),
        P(None, None, "tensor"),
        P("tensor", None),
        P(None, "tensor"),
        P(None, None, "tensor"),
        P("tensor", None),
        P(None, "tensor"),
        P("tensor", None),
        P(),
        P(),
        P(("dp", "tensor"), None),
    )
    out_specs = (
        P(("dp", "tensor"), None),
        P(("dp", "tensor"), None),
        P(("dp", "tensor"), None),
        P(None, "dp", "tensor"),
        P("tensor", "dp"),
        P("dp", "tensor"),
        P(None, "dp", "tensor"),
        P("tensor", "dp"),
        P("dp", "tensor"),
        P("tensor", "dp"),
        P(),
        P(),
    )

    def step(*args):
        chosen = sentence_body if sentence_fits(mesh, args[0], args[1], args[2]) else body
        return jax.shard_map(
            chosen, mesh=mesh, in_specs=in_specs, out_specs=out_specs, check_vma=False
        )(*args)

    return step
```

```python
import functools
import jax
import jax.numpy as jnp
from jax import lax
from jax.experimental import pallas as pl
from jax.experimental.pallas import tpu as pltpu
from jax.sharding import PartitionSpec as P

HEAD_DIM = 64
RESIDUAL_ALPHA = 4.16
NORM_EPSILON = 1e-05
MASKED_SCORE = -1000000000.0
SCORE_SCALE = HEAD_DIM ** (-0.5)
UNIT = 128
QUERY_BLOCK = 256
FFN_UNIT = 512
ROW_CHUNK = 64
BF16 = jnp.bfloat16
F32 = jnp.float32


def dot(left, right):
    return lax.dot_general(left, right, (((1,), (0,)), ((), ())), preferred_element_type=F32)


def dot_tn(left, right):
    return lax.dot_general(left, right, (((0,), (0,)), ((), ())), preferred_element_type=F32)


def dot_nt(left, right):
    return lax.dot_general(left, right, (((1,), (1,)), ((), ())), preferred_element_type=F32)


def shard_of(position):
    return ((position >> 2) & 1) | (position & 2) | ((position & 1) << 2)


def copy_of(source, target, sem):
    return pltpu.make_async_copy(source, target, sem)


def own_lanes(rows, head):
    lanes = lax.broadcasted_iota(jnp.int32, rows.shape, 1)
    return jnp.where((lanes >= HEAD_DIM) if head else (lanes < HEAD_DIM), rows, 0.0)


def extended_keys(keys, length):
    lanes = lax.broadcasted_iota(jnp.int32, keys.shape, 1)
    rows = lax.broadcasted_iota(jnp.int32, keys.shape, 0)
    mask = jnp.where((lanes == 0) & (rows >= length), MASKED_SCORE, 0.0).astype(BF16)
    keys = keys.astype(F32)
    return [jnp.concatenate([own_lanes(keys, head).astype(BF16), mask], axis=1) for head in (0, 1)]


def extended_query(query):
    lanes = lax.broadcasted_iota(jnp.int32, query.shape, 1)
    return jnp.concatenate([query, jnp.where(lanes == 0, 1.0, 0.0).astype(BF16)], axis=1)


def fill_diagonal(diagonal):
    keys = lax.broadcasted_iota(jnp.int32, diagonal.shape, 0)
    queries = lax.broadcasted_iota(jnp.int32, diagonal.shape, 1)
    diagonal[...] = jnp.where(keys <= queries, 0.0, MASKED_SCORE)


def key_ranges(block, keys, causal):
    if not causal:
        return [(0, keys)]
    return [(low, low + QUERY_BLOCK) for low in range(0, (block + 1) * QUERY_BLOCK, QUERY_BLOCK)]


def attend_unit(query, keys, values, length, causal, diagonal, lse_ref):
    rows, count = query.shape[0], keys.shape[0]
    values_t = jnp.transpose(values.astype(F32)).astype(BF16)
    wide_keys, wide_query = extended_keys(keys, length), extended_query(query)
    items = [(head, block) for block in range(rows // QUERY_BLOCK) for head in (0, 1)]
    scores, probs, totals, mixed = {}, {}, {}, {}
    for head, block in items:
        part = wide_query[block * QUERY_BLOCK : (block + 1) * QUERY_BLOCK]
        ranges = key_ranges(block, count, causal)
        scores[head, block] = [dot_nt(wide_keys[head][a:b], part) for a, b in ranges]
        if causal:
            scores[head, block][-1] = scores[head, block][-1] + diagonal[...]
    for head, block in items:
        pieces = scores[head, block]
        peak = functools.reduce(jnp.maximum, [jnp.max(p, axis=0, keepdims=True) for p in pieces])
        terms = [jnp.exp(p - peak) for p in pieces]
        total = sum(jnp.sum(t, axis=0, keepdims=True) for t in terms)
        at = slice(block * QUERY_BLOCK, (block + 1) * QUERY_BLOCK)
        lse_ref[head : head + 1, at] = peak + jnp.log(total)
        totals[head, block] = total
        probs[head, block] = jnp.concatenate([t.astype(BF16) for t in terms], axis=0)
    for head, block in items:
        own = values_t[head * HEAD_DIM : (head + 1) * HEAD_DIM, : probs[head, block].shape[0]]
        mixed[head, block] = dot(own, probs[head, block]) / totals[head, block]
    out = [
        jnp.transpose(jnp.concatenate([mixed[0, block], mixed[1, block]], axis=0))
        for block in range(rows // QUERY_BLOCK)
    ]
    return jnp.concatenate(out, axis=0).astype(BF16)


def attend_back_unit(query, keys, values, attended, grad, length, causal, diagonal, lse_ref):
    rows, count = query.shape[0], keys.shape[0]
    blocks = range(rows // QUERY_BLOCK)
    query_f, keys_f, grad_f = (a.astype(F32) for a in (query, keys, grad))
    wide_keys, wide_query = extended_keys(keys, length), extended_query(query)
    delta = jnp.transpose(grad_f * attended.astype(F32))
    deltas = [
        jnp.sum(delta[head * HEAD_DIM : (head + 1) * HEAD_DIM], axis=0, keepdims=True)
        for head in (0, 1)
    ]
    keys_t = jnp.transpose(keys_f).astype(BF16)
    query_own = [own_lanes(query_f, head).astype(BF16) for head in (0, 1)]
    grad_own = [own_lanes(grad_f, head).astype(BF16) for head in (0, 1)]
    items = [(head, block) for block in blocks for head in (0, 1)]
    scores, slopes, probs, back, grad_query = {}, {}, {}, {}, {}
    for head, block in items:
        at = slice(block * QUERY_BLOCK, (block + 1) * QUERY_BLOCK)
        for a, b in key_ranges(block, count, causal):
            scores[head, block, a] = dot_nt(wide_keys[head][a:b], wide_query[at])
            slopes[head, block, a] = dot_nt(values[a:b], grad_own[head][at])
    for head, block in items:
        at = slice(block * QUERY_BLOCK, (block + 1) * QUERY_BLOCK)
        ranges = key_ranges(block, count, causal)
        for a, b in ranges:
            score = scores[head, block, a]
            if causal and (a, b) == ranges[-1]:
                score = score + diagonal[...]
            prob = jnp.exp(score - lse_ref[head : head + 1, at])
            probs[head, block, a] = prob.astype(BF16)
            back[head, block, a] = (prob * (slopes[head, block, a] - deltas[head][:, at])).astype(BF16)
    for head, block in items:
        own = keys_t[head * HEAD_DIM : (head + 1) * HEAD_DIM]
        grad_query[head, block] = sum(
            dot(own[:, a:b], back[head, block, a]) for a, b in key_ranges(block, count, causal)
        )
    grad_keys, grad_values = [], []
    for low in sorted({key[2] for key in back}):
        live = [key for key in back if key[2] == low]
        at = [slice(block * QUERY_BLOCK, (block + 1) * QUERY_BLOCK) for _, block, _ in live]
        grad_values.append(
            dot(
                jnp.concatenate([probs[key] for key in live], axis=1),
                jnp.concatenate([grad_own[key[0]][a] for key, a in zip(live, at)], axis=0),
            )
        )
        grad_keys.append(
            dot(
                jnp.concatenate([back[key] for key in live], axis=1),
                jnp.concatenate([query_own[key[0]][a] for key, a in zip(live, at)], axis=0),
            )
        )
    grad_query = [
        jnp.transpose(jnp.concatenate([grad_query[0, block], grad_query[1, block]], axis=0)) * SCORE_SCALE
        for block in blocks
    ]
    return tuple(
        jnp.concatenate(parts, axis=0).astype(BF16) for parts in (grad_query, grad_keys, grad_values)
    )


def norm_chunk(hidden, gain, bias):
    center = hidden - jnp.mean(hidden, axis=-1, keepdims=True)
    inverse = lax.rsqrt(jnp.mean(center * center, axis=-1, keepdims=True) + NORM_EPSILON)
    normed = center * inverse
    return normed * gain + bias, normed, inverse


def norm_back_chunk(gradient, normed, inverse, gain):
    scaled = gradient * gain
    return inverse * (
        scaled
        - jnp.mean(scaled, axis=-1, keepdims=True)
        - normed * jnp.mean(scaled * normed, axis=-1, keepdims=True)
    )


def fold_rows(values):
    return jnp.sum(values.reshape(values.shape[0] // 8, 8, values.shape[1]), axis=0)


def each_chunk(rows, body):
    def step(index, carry):
        body(pl.ds(pl.multiple_of(index * ROW_CHUNK, ROW_CHUNK), ROW_CHUNK))
        return carry

    lax.fori_loop(0, rows // ROW_CHUNK, step, 0)


def store_shards(target, weight, dp):
    for block in range(8):
        target[shard_of(block ^ dp)] = weight[block * UNIT : (block + 1) * UNIT]


SMEM = pl.BlockSpec(memory_space=pltpu.SMEM)
VMEM = pl.BlockSpec(memory_space=pltpu.VMEM)
ANY = pl.BlockSpec(memory_space=pl.ANY)


def params(limit=62):
    return pltpu.CompilerParams(vmem_limit_bytes=limit * 1024 * 1024)


def cost_of(microseconds):
    return pl.CostEstimate(flops=int(microseconds * 1.1e9), bytes_accessed=4 << 20, transcendentals=0)


def sds(shape, dtype):
    return jax.ShapeDtypeStruct(shape, dtype)


def weight_copies(pieces, sc, wbuf, obuf, wsem, osem, columns=(0, 1, 2)):
    groups, outs = [[], [], []], []
    wide = 2 * UNIT
    for index, refs in enumerate(pieces):
        at = slice(index * wide, (index + 1) * wide)
        if len(refs) > 1:
            column = 0
            for ref in refs[:-1]:
                for source in [ref] if len(ref.shape) == 2 else [ref.at[c] for c in range(ref.shape[0])]:
                    if column in columns:
                        low = (columns.index(column) * len(pieces) + index) * wide
                        groups[column].append(copy_of(source, wbuf.at[:, low : low + wide], wsem.at[column, index, 0]))
                    column += 1
            if obuf is not None:
                outs.append(copy_of(refs[-1], obuf.at[at, :], osem.at[index, 0]))
            continue
        rest, = refs
        rows = rest.shape[2]
        part = wide // rest.shape[0]
        for quarter in range(rest.shape[0]):
            place = quarter ^ (sc[1] if rest.shape[0] == 4 else sc[3])
            for column in columns:
                low = (columns.index(column) * len(pieces) + index) * wide
                groups[column].append(
                    copy_of(
                        rest.at[quarter, column],
                        wbuf.at[pl.ds(pl.multiple_of(place * rows, rows), rows), low : low + wide],
                        wsem.at[column, index, quarter],
                    )
                )
            for block in range(4 if obuf is not None else 0):
                outs.append(
                    copy_of(
                        rest.at[quarter, 3, block * part : (block + 1) * part, :],
                        obuf.at[pl.ds(pl.multiple_of(index * wide + place * part, part), part), block * wide : (block + 1) * wide],
                        osem.at[index, 4 * quarter + block],
                    )
                )
    return groups, outs


def attention_fwd_call(scalars, residual, others, pieces, partial, norm):
    rows, depth = others[0].shape
    causal = len(others) == 1
    number, wide = 2 * len(pieces), 2 * len(pieces) * UNIT
    last, has_partial = norm is not None, partial is not None

    def kernel(*refs):
        it = iter(refs)
        sc = next(it)
        in_refs = [next(it) for _ in others]
        gain_ref, bias_ref = (next(it), next(it)) if last else (None, None)
        old_rows = [next(it) for _ in residual[1:]] if last else []
        res_in = next(it) if last else None
        part_in = next(it) if has_partial else None
        w_refs = [[next(it) for _ in piece] for piece in pieces]
        q_ref, k_ref, v_ref, att_ref, lse_ref = (next(it) for _ in range(5))
        if last:
            low_ref, hat_ref, inv_ref = next(it), next(it), next(it)
        else:
            sum_ref = next(it)
        wbuf, obuf, att_all, diagonal, wsem, osem, lsem = (next(it) for _ in range(7))
        if last:
            acc, old = next(it), next(it)
        length = sc[0]
        groups, outs = weight_copies(w_refs, sc, wbuf, obuf, wsem, osem)
        for copies in groups + [outs]:
            for copy in copies:
                copy.start()
        target = acc if last else sum_ref
        late = []
        if has_partial:
            late.append(copy_of(part_in, target, lsem.at[0]))
        if last:
            late.append(copy_of(res_in, old, lsem.at[1]))
        for copy in late:
            copy.start()
        if causal:
            fill_diagonal(diagonal)
        for c, result in enumerate((q_ref, k_ref, v_ref)):
            for copy in groups[c]:
                copy.wait()
            rows_in = in_refs[0] if causal or c == 0 else in_refs[1]
            proj = dot(rows_in[...], wbuf[:, c * wide : (c + 1) * wide]).astype(BF16)
            if c == 0:
                proj = (proj.astype(F32) * SCORE_SCALE).astype(BF16)
            for index in range(number):
                result[index] = proj[:, index * UNIT : (index + 1) * UNIT]

        def step(u, carry):
            attended = attend_unit(q_ref[u], k_ref[u], v_ref[u], length, causal, diagonal, lse_ref.at[u])
            att_ref[u] = attended
            att_all[:, pl.ds(pl.multiple_of(u * UNIT, UNIT), UNIT)] = attended
            return carry

        lax.fori_loop(0, number, step, 0)
        for copy in outs + late:
            copy.wait()
        if has_partial:
            target[...] += dot(att_all[...], obuf[...])
        else:
            target[...] = dot(att_all[...], obuf[...])
        if last:
            def chunk(at):
                before = old[at, :].astype(F32)
                if old_rows:
                    before = before * old_rows[0][...] + old_rows[1][...]
                normed, hat, inverse = norm_chunk(RESIDUAL_ALPHA * before + acc[at, :], gain_ref[...], bias_ref[...])
                low_ref[at, :] = normed.astype(BF16)
                hat_ref[at, :] = hat
                inv_ref[at, :] = jnp.broadcast_to(inverse, (ROW_CHUNK, 128))

            each_chunk(rows, chunk)

    unit_rows = sds((number, rows, UNIT), BF16)
    shapes = [unit_rows] * 4 + [sds((number, 2, rows), F32)]
    if last:
        shapes += [sds((rows, depth), BF16), sds((rows, depth), F32), sds((rows, 128), F32)]
    else:
        shapes += [sds((rows, depth), F32)]
    args = [scalars, *others]
    if last:
        args += [*norm, *residual[1:]]
    tail = ([residual[0]] if last else []) + ([partial] if has_partial else [])
    tail += [array for piece in pieces for array in piece]
    scratch = [
        pltpu.VMEM((depth, 3 * wide), BF16),
        pltpu.VMEM((wide, depth), BF16),
        pltpu.VMEM((rows, wide), BF16),
        pltpu.VMEM((QUERY_BLOCK, QUERY_BLOCK), F32),
        pltpu.SemaphoreType.DMA((3, len(pieces), 4)),
        pltpu.SemaphoreType.DMA((len(pieces), 16)),
        pltpu.SemaphoreType.DMA((2,)),
    ]
    if last:
        scratch += [pltpu.VMEM((rows, depth), F32), pltpu.VMEM((rows, depth), residual[0].dtype)]
    return pl.pallas_call(
        kernel,
        out_shape=shapes,
        in_specs=[SMEM] + [VMEM] * (len(args) - 1) + [ANY] * len(tail),
        out_specs=[VMEM] * len(shapes),
        scratch_shapes=scratch,
        compiler_params=params(),
        cost_estimate=cost_of(0.6 * number),
        name="self_fwd" if causal else "cross_fwd",
    )(*args, *tail)


def attention_bwd_call(scalars, grad_low, others, pieces, saved, plan, carried, norm, results=1):
    rows, depth = grad_low.shape
    causal = len(others) == 1
    number, n_in, wide = len(plan), len(others), len(plan) * UNIT
    last = norm is not None
    skip = 1 if last else 0

    def kernel(*refs):
        it = iter(refs)
        sc = next(it)
        h_ref = next(it)
        in_refs = [next(it) for _ in range(n_in)]
        gain_ref = next(it) if last else None
        late_in = [next(it), next(it)] if last else []
        acc_in = next(it) if last else None
        w_refs = [[next(it) for _ in piece] for piece in pieces]
        s_refs = [[next(it) for _ in call] for call in saved]
        if last:
            low_ref, scaled_ref, gsum_ref, bsum_ref = (next(it) for _ in range(4))
        dall_ref = next(it)
        g_refs = [next(it) for _ in range(results)]
        wbuf, obuf, sbuf, lbuf, att_all, grad_all = (next(it) for _ in range(6))
        stage, diagonal = next(it), next(it)
        if last:
            dquery, acc, hat, inv = (next(it) for _ in range(4))
        wsem, osem, ssem, gsem, lsem = (next(it) for _ in range(5))
        length, dp = sc[0], sc[2]

        groups, o_copies = weight_copies(w_refs, sc, wbuf, obuf, wsem, osem, (0,) if last else ())
        for copy in o_copies:
            copy.start()
        s_copies = []
        for index, unit in enumerate(plan):
            lanes = slice(index * UNIT, (index + 1) * UNIT)
            call = s_refs[unit[0]]
            for c in range(3):
                s_copies.append(copy_of(call[c].at[unit[1]], sbuf.at[index, c], ssem.at[c, index]))
            s_copies.append(copy_of(call[3].at[unit[1]], att_all.at[:, lanes], ssem.at[3, index]))
            s_copies.append(copy_of(call[4].at[unit[1]], lbuf.at[index], ssem.at[4, index]))
        late = []
        if last:
            late = groups[0] + [
                copy_of(source, target, lsem.at[index])
                for index, (source, target) in enumerate(((acc_in, acc), (late_in[0], hat), (late_in[1], inv)))
            ]
        for copy in s_copies + late:
            copy.start()
        if causal:
            fill_diagonal(diagonal)
        for copy in o_copies:
            copy.wait()
        grad_att = dot_nt(h_ref[...], obuf[...]).astype(BF16)
        for index in range(number):
            grad_all[index] = grad_att[:, index * UNIT : (index + 1) * UNIT]
        for copy in s_copies:
            copy.wait()

        def step(u, carry):
            at = pl.ds(pl.multiple_of(u * UNIT, UNIT), UNIT)
            parts = attend_back_unit(
                sbuf[u, 0], sbuf[u, 1], sbuf[u, 2], att_all[:, at], grad_all[u], length, causal, diagonal, lbuf.at[u]
            )
            if last:
                dquery[:, at] = parts[0]
            for c in range(skip, 3):
                dall_ref[:, pl.ds(pl.multiple_of((c - skip) * wide + u * UNIT, UNIT), UNIT)] = parts[c]
            return carry

        lax.fori_loop(0, number, step, 0)

        share = number // 2 // results

        def keep(rows_in, source, column):
            weight = dot_tn(rows_in[...], source).astype(BF16)
            for index in range(number):
                piece = index // 2
                target = stage.at[piece // share, (index % 2) * 4 + column, piece % share]
                store_shards(target, weight[:, index * UNIT : (index + 1) * UNIT], dp)

        if last:
            keep(in_refs[0], dquery[...], 0)
        for c in range(skip, 3):
            keep(in_refs[-1], dall_ref[:, (c - skip) * wide : (c - skip + 1) * wide], c)
        keep(h_ref, att_all[...], 3)
        g_copies = [copy_of(stage.at[index], ref, gsem.at[index]) for index, ref in enumerate(g_refs)]
        for copy in g_copies:
            copy.start()
        for copy in late:
            copy.wait()
        if last:
            acc[...] += dot_nt(dquery[...], wbuf[...])
            norm_back_rows(acc, hat, inv, gain_ref, low_ref, scaled_ref, gsum_ref, bsum_ref, rows)
        for copy in g_copies:
            copy.wait()

    big = sds((rows, depth), F32)
    shapes = []
    if last:
        shapes += [sds((rows, depth), BF16), big, sds((8, depth), F32), sds((8, depth), F32)]
    shapes.append(sds((rows, (3 - skip) * wide), BF16))
    specs_out = [VMEM] * len(shapes) + [ANY] * results
    shapes += [sds((8, number // 2 // results, 8, UNIT, UNIT), BF16)] * results
    args = [scalars, grad_low, *others] + ([norm[2]] if last else [])
    tail = [norm[0], norm[1], carried] if last else []
    tail += [array for piece in pieces for array in piece]
    for call in saved:
        tail += call
    scratch = [
        pltpu.VMEM((depth, wide) if last else (16, 128), BF16),
        pltpu.VMEM((wide, depth), BF16),
        pltpu.VMEM((number, 3, rows, UNIT), BF16),
        pltpu.VMEM((number, 2, rows), F32),
        pltpu.VMEM((rows, wide), BF16),
        pltpu.VMEM((number, rows, UNIT), BF16),
        pltpu.VMEM((results, 8, number // 2 // results, 8, UNIT, UNIT), BF16),
        pltpu.VMEM((QUERY_BLOCK, QUERY_BLOCK), F32),
    ]
    if last:
        scratch += [pltpu.VMEM((rows, wide), BF16), pltpu.VMEM((rows, depth), F32), pltpu.VMEM((rows, depth), F32), pltpu.VMEM((rows, 128), F32)]
    scratch += [
        pltpu.SemaphoreType.DMA((3, len(pieces), 4)),
        pltpu.SemaphoreType.DMA((len(pieces), 16)),
        pltpu.SemaphoreType.DMA((5, number)),
        pltpu.SemaphoreType.DMA((results,)),
        pltpu.SemaphoreType.DMA((4,)),
    ]
    return pl.pallas_call(
        kernel,
        out_shape=shapes,
        in_specs=[SMEM] + [VMEM] * (len(args) - 1) + [ANY] * len(tail),
        out_specs=specs_out,
        scratch_shapes=scratch,
        compiler_params=params(),
        cost_estimate=cost_of(4.2 * number),
        name="self_bwd" if causal else "cross_bwd",
    )(*args, *tail)


def inputs_back_call(scalars, base, parts, memory_part):
    rows, depth = base.shape
    jobs = [(0, grad, pieces, (0, 1, 2)) for grad, pieces in parts] + [(1, *memory_part, (1, 2))]

    def kernel(*refs):
        it = iter(refs)
        sc, base_ref = next(it), next(it)
        grads = [next(it) for _ in jobs]
        w_refs = [[[next(it) for _ in piece] for piece in pieces] for _, _, pieces, _ in jobs]
        outs = [next(it), next(it)]
        bufs, sems = [next(it) for _ in jobs], [next(it) for _ in jobs]
        copies = []
        for index, (_, _, _, columns) in enumerate(jobs):
            groups, _ = weight_copies(w_refs[index], sc, bufs[index], None, sems[index], None, columns)
            copies.append([copy for group in groups for copy in group])
            for copy in copies[-1]:
                copy.start()
        outs[0][...] = base_ref[...]
        for index, (out, _, _, _) in enumerate(jobs):
            for copy in copies[index]:
                copy.wait()
            if out:
                outs[1][...] = dot_nt(grads[index][...], bufs[index][...])
            else:
                outs[0][...] += dot_nt(grads[index][...], bufs[index][...])

    args = [scalars, base] + [grad for _, grad, _, _ in jobs]
    tail = [array for _, _, pieces, _ in jobs for piece in pieces for array in piece]
    return pl.pallas_call(
        kernel,
        out_shape=[sds((rows, depth), F32)] * 2,
        in_specs=[SMEM] + [VMEM] * (len(args) - 1) + [ANY] * len(tail),
        out_specs=[VMEM] * 2,
        scratch_shapes=[pltpu.VMEM((depth, grad.shape[1]), BF16) for _, grad, _, _ in jobs]
        + [pltpu.SemaphoreType.DMA((3, len(pieces), 4)) for _, _, pieces, _ in jobs],
        compiler_params=params(),
        cost_estimate=cost_of(12),
        name="inputs_back",
    )(*args, *tail)


def norm_back_rows(acc, hat, inv, gain_ref, low_ref, scaled_ref, gsum_ref, bsum_ref, rows):
    gsum_ref[...] = jnp.zeros_like(gsum_ref)
    bsum_ref[...] = jnp.zeros_like(bsum_ref)

    def chunk(at):
        gradient, normed = acc[at, :], hat[at, :]
        grad_in = norm_back_chunk(gradient, normed, inv[at, :1], gain_ref[...])
        low_ref[at, :] = grad_in.astype(BF16)
        scaled_ref[at, :] = RESIDUAL_ALPHA * grad_in
        gsum_ref[...] += fold_rows(gradient * normed)
        bsum_ref[...] += fold_rows(gradient)

    each_chunk(rows, chunk)


GELU_SCALE = 0.7978845608028654
GELU_CUBE = 0.044715


def gelu_and_slope(pre):
    square = pre * pre
    inner = pre * (GELU_SCALE + (GELU_SCALE * GELU_CUBE) * square)
    curve = jnp.tanh(inner)
    half = 0.5 + 0.5 * curve
    slope = half * (1.0 + pre * (1.0 - curve) * (GELU_SCALE + (3.0 * GELU_SCALE * GELU_CUBE) * square))
    return pre * half, slope


FFN_PART = FFN_UNIT // 2


def ffn_copies(pieces, order, ubuf, dbuf, usem, dsem):
    ups, downs = [], []
    for index, refs in enumerate(pieces):
        wide = 2 * FFN_UNIT
        at = slice(index * wide, (index + 1) * wide)
        if len(refs) == 2:
            ups.append([copy_of(refs[0], ubuf.at[:, at], usem.at[index, 0])])
            downs.append([copy_of(refs[1], dbuf.at[at, :], dsem.at[index, 0])])
            continue
        ups.append([])
        downs.append([])
        rows = refs[0].shape[1]
        for quarter in range(4):
            up = refs[quarter].at[0]
            down = refs[quarter].at[1] if quarter < 3 else refs[4].at[0]
            place = (quarter ^ order) * rows
            ups[-1].append(copy_of(up, ubuf.at[pl.ds(pl.multiple_of(place, rows), rows), at], usem.at[index, quarter]))
            downs[-1].append(
                copy_of(down, dbuf.at[pl.ds(pl.multiple_of(index * wide + place, rows), rows), :], dsem.at[index, quarter])
            )
    return ups, downs


def ffn_fwd_call(scalars, inputs, pieces, partial, final):
    rows, depth = inputs.shape
    number = 2 * len(pieces)
    last, has_partial = final is not None, partial is not None

    def kernel(*refs):
        it = iter(refs)
        sc, x_ref = next(it), next(it)
        if last:
            gain_old, bias_old, gain_ref, bias_ref = (next(it) for _ in range(4))
            late_in = [next(it), next(it)]
        part_in = next(it) if has_partial else None
        w_refs = [[next(it) for _ in piece] for piece in pieces]
        if last:
            out_ref, low_ref, scaled_ref, gsum_ref, bsum_ref = (next(it) for _ in range(5))
        else:
            sum_ref = next(it)
        act_ref, slope_ref = next(it), next(it)
        ubuf, dbuf, abuf, sbuf, pbuf, psem = (next(it) for _ in range(6))
        if last:
            acc, hat, cot, lsem = (next(it) for _ in range(4))
        wsem, gsem = next(it), next(it)
        target = acc if last else sum_ref

        up_copies, down_copies = ffn_copies(w_refs, sc[1], ubuf, dbuf, wsem.at[0], wsem.at[1])
        for copies in up_copies + down_copies:
            for copy in copies:
                copy.start()
        if has_partial:
            part_copy = copy_of(part_in, target, psem)
            part_copy.start()
        if last:
            late = [copy_of(late_in[0], hat, lsem.at[0]), copy_of(late_in[1], cot, lsem.at[1])]
            for copy in late:
                copy.start()
        saves = []

        def gate(pre, index):
            activated, slope = gelu_and_slope(pre)
            abuf[:, index * FFN_UNIT : (index + 1) * FFN_UNIT] = activated.astype(BF16)
            sbuf[:, index * FFN_UNIT : (index + 1) * FFN_UNIT] = slope.astype(BF16)

        for index in range(number):
            if index % 2 == 0:
                for copy in up_copies[index // 2]:
                    copy.wait()
            if index:
                gate(pbuf[(index - 1) % 2], index - 1)
            pbuf[index % 2] = dot(x_ref[...], ubuf[:, index * FFN_UNIT : (index + 1) * FFN_UNIT])
        gate(pbuf[(number - 1) % 2], number - 1)
        for index in range(number):
            at = slice(index * FFN_UNIT, (index + 1) * FFN_UNIT)
            saves += [
                copy_of(abuf.at[:, at], act_ref.at[index], gsem.at[0, index]),
                copy_of(sbuf.at[:, at], slope_ref.at[index], gsem.at[1, index]),
            ]
        for copy in saves:
            copy.start()
        for copies in down_copies:
            for copy in copies:
                copy.wait()
        if has_partial:
            part_copy.wait()
            target[...] += dot(abuf[...], dbuf[...])
        else:
            target[...] = dot(abuf[...], dbuf[...])
        if last:
            for copy in late:
                copy.wait()
            gsum_ref[...] = jnp.zeros_like(gsum_ref)
            bsum_ref[...] = jnp.zeros_like(bsum_ref)

            def chunk(at):
                old = hat[at, :] * gain_old[...] + bias_old[...]
                normed, xhat, inverse = norm_chunk(RESIDUAL_ALPHA * old + acc[at, :], gain_ref[...], bias_ref[...])
                out_ref[at, :] = normed.astype(BF16)
                gradient = cot[at, :].astype(F32)
                grad_in = norm_back_chunk(gradient, xhat, inverse, gain_ref[...])
                low_ref[at, :] = grad_in.astype(BF16)
                scaled_ref[at, :] = RESIDUAL_ALPHA * grad_in
                gsum_ref[...] += fold_rows(gradient * xhat)
                bsum_ref[...] += fold_rows(gradient)

            each_chunk(rows, chunk)
        for copy in saves:
            copy.wait()

    big, low = sds((rows, depth), F32), sds((rows, depth), BF16)
    if last:
        shapes = [low, low, big, sds((8, depth), F32), sds((8, depth), F32)]
    else:
        shapes = [big]
    specs_out = [VMEM] * len(shapes) + [ANY, ANY]
    shapes += [sds((number, rows, FFN_UNIT), BF16)] * 2
    args = [scalars, inputs]
    if last:
        args += [final[1], final[2], final[4], final[5]]
    specs = [SMEM] + [VMEM] * (len(args) - 1)
    tail = ([final[0], final[3]] if last else []) + ([partial] if has_partial else []) + [array for piece in pieces for array in piece]
    scratch = [
        pltpu.VMEM((depth, number * FFN_UNIT), BF16),
        pltpu.VMEM((number * FFN_UNIT, depth), BF16),
        pltpu.VMEM((rows, number * FFN_UNIT), BF16),
        pltpu.VMEM((rows, number * FFN_UNIT), BF16),
        pltpu.VMEM((2, rows, FFN_UNIT), F32),
        pltpu.SemaphoreType.DMA,
    ]
    if last:
        scratch += [
            pltpu.VMEM((rows, depth), F32),
            pltpu.VMEM((rows, depth), F32),
            pltpu.VMEM((rows, depth), BF16),
            pltpu.SemaphoreType.DMA((2,)),
        ]
    scratch += [pltpu.SemaphoreType.DMA((2, len(pieces), 4)), pltpu.SemaphoreType.DMA((2, number))]
    return pl.pallas_call(
        kernel,
        out_shape=shapes,
        in_specs=specs + [ANY] * len(tail),
        out_specs=specs_out,
        scratch_shapes=scratch,
        compiler_params=params(),
        cost_estimate=cost_of(12),
        name="ffn_fwd",
    )(*args, *tail)


def ffn_bwd_call(scalars, grad_low, inputs, pieces, saved, plan, carried, norm):
    rows, depth = inputs.shape
    number = len(plan)
    last = norm is not None

    def kernel(*refs):
        it = iter(refs)
        sc, g_in, x_ref = (next(it) for _ in range(3))
        gain_ref = next(it) if last else None
        late_in = [next(it), next(it)] if last else []
        acc_in = next(it)
        w_refs = [[next(it) for _ in piece] for piece in pieces]
        s_refs = [[next(it) for _ in call] for call in saved]
        if last:
            low_ref, scaled_ref, gsum_ref, bsum_ref = (next(it) for _ in range(4))
        else:
            sum_ref = next(it)
        g_ref = next(it)
        ubuf, dbuf, abuf, sbuf, gbuf, stage, psem = (next(it) for _ in range(7))
        if last:
            acc, hat, inv, lsem = (next(it) for _ in range(4))
        wsem, ssem, gsem = next(it), next(it), next(it)
        order, dp = sc[1], sc[2]
        target = acc if last else sum_ref

        ups, downs = ffn_copies(w_refs, order, ubuf, dbuf, wsem.at[0], wsem.at[1])
        slopes, acts = [], []
        for index, (call, at) in enumerate(plan):
            lanes = slice(index * FFN_UNIT, (index + 1) * FFN_UNIT)
            slopes.append(copy_of(s_refs[call][1].at[at], sbuf.at[index], ssem.at[0, index]))
            acts.append(copy_of(s_refs[call][0].at[at], abuf.at[:, lanes], ssem.at[1, index]))
        for copies in downs + [slopes, acts] + ups:
            for copy in copies:
                copy.start()
        part_copy = copy_of(acc_in, target, psem)
        part_copy.start()
        if last:
            late = [copy_of(late_in[0], hat, lsem.at[0]), copy_of(late_in[1], inv, lsem.at[1])]
            for copy in late:
                copy.start()
        for index in range(number):
            if index % 2 == 0:
                for copy in downs[index // 2]:
                    copy.wait()
            slopes[index].wait()
            grad_act = dot_nt(g_in[...], dbuf[index * FFN_UNIT : (index + 1) * FFN_UNIT, :]) * sbuf[index].astype(F32)
            gbuf[:, index * FFN_UNIT : (index + 1) * FFN_UNIT] = grad_act.astype(BF16)
        for copy in acts:
            copy.wait()

        def keep(rows_in, source, column):
            for half in range(number // 2):
                wide = 2 * FFN_UNIT
                weight = dot_tn(rows_in[...], source[:, half * wide : (half + 1) * wide]).astype(BF16)
                for inner in range(4):
                    part = weight[:, inner * FFN_PART : (inner + 1) * FFN_PART]
                    store_shards(stage.at[2 * inner + column, half], part, dp)

        keep(x_ref, gbuf, 0)
        keep(g_in, abuf, 1)
        g_copies = [copy_of(stage, g_ref, gsem)]
        for copy in g_copies:
            copy.start()
        for copies in ups:
            for copy in copies:
                copy.wait()
        part_copy.wait()
        target[...] += dot_nt(gbuf[...], ubuf[...])
        if last:
            for copy in late:
                copy.wait()
            norm_back_rows(acc, hat, inv, gain_ref, low_ref, scaled_ref, gsum_ref, bsum_ref, rows)
        for copy in g_copies:
            copy.wait()

    big, low = sds((rows, depth), F32), sds((rows, depth), BF16)
    shapes = [low, big, sds((8, depth), F32), sds((8, depth), F32)] if last else [big]
    specs_out = [VMEM] * len(shapes) + [ANY]
    shapes.append(sds((8, number // 2, 8, UNIT, FFN_PART), BF16))
    args = [scalars, grad_low, inputs] + ([norm[2]] if last else [])
    specs = [SMEM] + [VMEM] * (len(args) - 1)
    tail = ([norm[0], norm[1]] if last else []) + [carried] + [array for piece in pieces for array in piece]
    for call in saved:
        tail += call
    scratch = [
        pltpu.VMEM((depth, number * FFN_UNIT), BF16),
        pltpu.VMEM((number * FFN_UNIT, depth), BF16),
        pltpu.VMEM((rows, number * FFN_UNIT), BF16),
        pltpu.VMEM((number, rows, FFN_UNIT), BF16),
        pltpu.VMEM((rows, number * FFN_UNIT), BF16),
        pltpu.VMEM((8, number // 2, 8, UNIT, FFN_PART), BF16),
        pltpu.SemaphoreType.DMA,
    ]
    if last:
        scratch += [
            pltpu.VMEM((rows, depth), F32),
            pltpu.VMEM((rows, depth), F32),
            pltpu.VMEM((rows, 128), F32),
            pltpu.SemaphoreType.DMA((2,)),
        ]
    scratch += [pltpu.SemaphoreType.DMA((2, len(pieces), 4)), pltpu.SemaphoreType.DMA((2, number)), pltpu.SemaphoreType.DMA]
    return pl.pallas_call(
        kernel,
        out_shape=shapes,
        in_specs=specs + [ANY] * len(tail),
        out_specs=specs_out,
        scratch_shapes=scratch,
        compiler_params=params(),
        cost_estimate=cost_of(17),
        name="ffn_bwd",
    )(*args, *tail)


def combine(jobs, shapes):
    arrays = []
    for terms, _, _, _ in jobs:
        for array, _ in terms:
            if not any(array is known for known in arrays):
                arrays.append(array)
    position = {id(array): index for index, array in enumerate(arrays)}

    def part_shape(array, index):
        kept = []
        for extent, at in zip(array.shape, index + (slice(None),) * (array.ndim - len(index))):
            if isinstance(at, slice):
                kept.append(len(range(*at.indices(extent))))
        return tuple(kept)

    part_shapes = [part_shape(*terms[0]) for terms, _, _, _ in jobs]
    count = sum(len(terms) for terms, _, _, _ in jobs)

    def kernel(*refs):
        ins, outs = refs[: len(arrays)], refs[len(arrays) : len(arrays) + len(shapes)]
        rest = refs[len(arrays) + len(shapes) :]
        term_bufs, sum_bufs, isem, osem = rest[:count], rest[count : count + len(jobs)], rest[-2], rest[-1]
        loads, number = [], 0
        for terms, _, _, _ in jobs:
            loads.append([])
            for array, index in terms:
                loads[-1].append(copy_of(ins[position[id(array)]].at[index], term_bufs[number], isem.at[number]))
                number += 1
        for group in loads:
            for copy in group:
                copy.start()
        stores, number = [], 0
        for job, (terms, out, place, kind) in enumerate(jobs):
            for copy in loads[job]:
                copy.wait()
            bufs = term_bufs[number : number + len(terms)]
            number += len(terms)
            lead = part_shapes[job][:-2]
            size = 1
            for extent in lead:
                size *= extent

            def one(flat, carry, bufs=bufs, lead=lead, target=sum_bufs[job]):
                index, left = [], flat
                for extent in reversed(lead):
                    index.append(lax.rem(left, extent))
                    left = lax.div(left, extent)
                index = tuple(reversed(index))
                total = bufs[0][index].astype(F32)
                for buf in bufs[1:]:
                    total = total + buf[index].astype(F32)
                target[index] = total.astype(target.dtype)
                return carry

            if kind == "range":
                lax.fori_loop(0, size, one, 0)
            else:
                total = bufs[0][0].astype(F32)
                for buf in bufs[1:]:
                    total = total + buf[0].astype(F32)
                sum_bufs[job][...] = jnp.transpose(total) if kind == "turned" else total
            stores.append(copy_of(sum_bufs[job], outs[out].at[place], osem.at[job]))
            stores[-1].start()
        for copy in stores:
            copy.wait()

    scratch = [pltpu.VMEM(part_shapes[job], array.dtype) for job, (terms, _, _, _) in enumerate(jobs) for array, _ in terms]
    for job, (_, out, _, kind) in enumerate(jobs):
        shape = part_shapes[job]
        shape = {"range": shape, "plain": shape[1:], "turned": shape[:0:-1]}[kind]
        scratch.append(pltpu.VMEM(shape, shapes[out].dtype))
    scratch += [pltpu.SemaphoreType.DMA((count,)), pltpu.SemaphoreType.DMA((len(jobs),))]
    return pl.pallas_call(
        kernel,
        out_shape=list(shapes),
        in_specs=[ANY] * len(arrays),
        out_specs=[ANY] * len(shapes),
        scratch_shapes=scratch,
        compiler_params=params(),
        cost_estimate=cost_of(3),
        name="combine",
    )(*arrays)


def swap_pairs(count, mask):
    return [(i, i ^ mask) for i in range(count)]


def to_sibling(values):
    return lax.ppermute(values, "tensor", swap_pairs(4, 1))


def over_y(values):
    return lax.ppermute(values, "tensor", swap_pairs(4, 2))


def over_dp(values, mask):
    return lax.ppermute(values, "dp", swap_pairs(8, mask))


def over_x(values):
    return over_dp(values, 1)


def over_z_near(values):
    return over_dp(values, 2)


def over_z_far(values):
    return over_dp(values, 4)


def after(values, *earlier):
    return lax.optimization_barrier((values, *earlier))[0]


MOVES = {"y": over_y, "x": over_x, "z": over_z_near}


class Reduction:
    def __init__(self, sent, portions, finish):
        self.other, self.finish = to_sibling(sent), finish
        self.portions, self.stage, self.sends, self.total = portions, 0, None, None

    def begin(self, kept, *earlier):
        other = after(self.other, *earlier)
        split = (kept.shape[0], 2, 2, 2, 2, *kept.shape[3:])
        arrays = (kept.reshape(split), other.reshape(split))
        self.blocks, self.tail = kept.shape[0], kept.shape[3:]
        self.terms = [[(array, ("b", "y", "x", "z", "w"), low, {}) for array in arrays] for low, _, _ in self.portions]

    def receive(self, *earlier):
        if self.stage == 4:
            moved = after(over_z_far(self.sends[0]), *earlier)
            for (low, _, _), terms in zip(self.portions, self.terms):
                terms.append((moved, ("b",), low, {}))
        elif self.stage:
            for send, (_, _, orders), terms in zip(self.sends, self.portions, self.terms):
                left = tuple(a for a in ("b", "y", "x", "z", "w") if a not in orders[: self.stage])
                terms.append((after(MOVES[orders[self.stage - 1]](send), *earlier), left, 0, {}))

    def jobs(self, first_out):
        jobs, shapes = [], []
        stage = self.stage
        for number, ((low, high, orders), terms) in enumerate(zip(self.portions, self.terms)):
            axis = (*orders, "w", None)[stage]
            picked = []
            for array, axes, start, fixed in terms:
                index = [slice(start, start + high - low)]
                for name in axes[1:]:
                    index.append(1 if name == axis else fixed.get(name, 0 if name in orders[:stage] or (stage > 3 and name == "w") else slice(None)))
                picked.append((array, tuple(index)))
            if stage < 3:
                shapes.append(sds((high - low, *(2,) * (3 - stage), *self.tail), BF16))
                jobs.append((picked, first_out + number, slice(0, high - low), "range"))
            elif stage == 3:
                if not number:
                    shapes.append(sds((self.blocks, *self.tail), BF16))
                jobs.append((picked, first_out, slice(low, high), "range"))
            else:
                if not number:
                    shapes += self.finish[0]
                for block in range(low, high):
                    shift = block - low
                    one = [(a, (slice(index[0].start + shift, index[0].start + shift + 1), *index[1:])) for a, index in picked]
                    out, place, kind = self.finish[1](block)
                    jobs.append((one, first_out + out, place, kind))
        self.stage += 1
        return jobs, shapes


def attention_finish(counts):
    stacks = [sds((count, UNIT, 2 * UNIT) if count > 1 else (UNIT, 2 * UNIT), F32) for count in counts]

    def place_of(block):
        half, matrix = block // 4, block % 4
        lanes = slice(half * UNIT, (half + 1) * UNIT)
        if matrix == 3:
            return len(counts), (lanes, slice(None)), "turned"
        stack = 0 if matrix < counts[0] else 1
        if counts[stack] == 1:
            return stack, (slice(None), lanes), "plain"
        return stack, (matrix - sum(counts[:stack]), slice(None), lanes), "plain"

    return [*stacks, sds((2 * UNIT, UNIT), F32)], place_of


def ffn_finish():
    def place_of(block):
        lanes = slice(block // 2 * FFN_PART, (block // 2 + 1) * FFN_PART)
        if block % 2:
            return 1, (lanes, slice(None)), "turned"
        return 0, (slice(None), lanes), "plain"

    return [sds((UNIT, 4 * FFN_PART), F32), sds((4 * FFN_PART, UNIT), F32)], place_of


def advance(reductions, *earlier):
    jobs, shapes, bounds = [], [], []
    for reduction in reductions:
        reduction.receive(*earlier)
        more, made = reduction.jobs(len(shapes))
        bounds.append((len(shapes), len(shapes) + len(made)))
        jobs, shapes = jobs + more, shapes + made
    results = combine(jobs, shapes)
    for reduction, (low, high) in zip(reductions, bounds):
        reduction.sends = list(results[low:high])
        if reduction.stage == 5:
            reduction.total = results[low:high]
    return list(results)


def sentence_body(
    tokens,
    memory,
    dec_lengths,
    mem_lengths,
    self_qkv,
    self_out,
    cross_q,
    cross_kv,
    cross_out,
    ffn_in,
    ffn_out,
    norm_gains,
    norm_biases,
    cotangent,
):
    dp = lax.axis_index("dp")
    mine = lax.axis_index("tensor")
    order = dp & 3
    inner = (dp >> 1) & 1
    self_scalars = jnp.stack([dec_lengths[0, mine], order, dp, inner]).astype(jnp.int32)
    cross_scalars = jnp.stack([mem_lengths[0, mine], order, dp, inner]).astype(jnp.int32)
    gains = [norm_gains[i : i + 1] for i in range(3)]
    biases = [norm_biases[i : i + 1] for i in range(3)]

    def part_rows(values, parts):
        rows = values.shape[-2] // parts
        place = order if parts == 4 else inner
        return lax.dynamic_slice_in_dim(values, place * rows, rows, values.ndim - 2)

    def folded(values):
        blocks = values.reshape(values.shape[0], 4, 2 * UNIT)
        return blocks.transpose(1, 0, 2).reshape(1, 4 * values.shape[0], 2 * UNIT)

    self_near = over_y(jnp.concatenate([part_rows(self_qkv, 4), folded(part_rows(self_out, 4))]))
    cross_near = over_y(
        jnp.concatenate([part_rows(cross_q, 2)[None], part_rows(cross_kv, 2), folded(part_rows(cross_out, 2))])
    )
    ffn_near = over_y(jnp.stack([part_rows(ffn_in, 4), part_rows(ffn_out, 4)]))
    self_own = (self_qkv, self_out)
    self_sib = tuple(to_sibling(w) for w in self_own)
    self_a = attention_fwd_call(self_scalars, [], [tokens], [self_own, self_sib], None, None)
    self_near = after(self_near, self_a[4])
    self_side, self_up = over_x(self_near), over_z_near(self_near)
    self_corner = over_x(self_up)
    self_rest = jnp.stack([after(self_near, cross_near), self_side, self_up, self_corner])
    cross_up = over_z_near(cross_near)
    self_far = to_sibling(self_rest)
    self_pieces = [self_own, self_sib, (self_rest,), (self_far,)]
    cross_own, ffn_own = (cross_q, cross_kv, cross_out), (ffn_in, ffn_out)
    cross_sib = tuple(to_sibling(after(w, self_near)) for w in cross_own)
    self_b = attention_fwd_call(
        after(self_scalars, *cross_sib), [tokens], [tokens], self_pieces[2:], self_a[5], (gains[0], biases[0])
    )
    first_low, first_hat, first_inv = self_b[5:]
    cross_in = [first_low, memory]
    cross_rest = jnp.stack([cross_near, after(cross_up, self_b[4])])
    cross_far = to_sibling(cross_rest)
    cross_a = attention_fwd_call(after(cross_scalars, ffn_near), [], cross_in, [cross_own, cross_sib], None, None)
    ffn_sib = tuple(to_sibling(after(w, ffn_near)) for w in ffn_own)
    ffn_side, ffn_up = over_x(ffn_near), over_z_near(ffn_near)
    cross_pieces = [cross_own, cross_sib, (cross_rest,), (after(cross_far, cross_a[4]),)]
    cross_b = attention_fwd_call(
        cross_scalars, [first_hat, gains[0], biases[0]], cross_in, cross_pieces[2:], cross_a[5], (gains[1], biases[1])
    )
    second_low, second_hat, second_inv = cross_b[5:]
    ffn_side, ffn_up = after(ffn_side, cross_b[4]), after(ffn_up, cross_b[4])
    up_corner, down_corner = over_x(ffn_up[:1]), over_z_near(ffn_side[1:])
    ffn_pieces = [ffn_own, ffn_sib]
    ffn_a = ffn_fwd_call(cross_scalars, second_low, ffn_pieces, None, None)
    up_corner, down_corner = after(up_corner, ffn_a[0]), after(down_corner, ffn_a[0])
    ffn_rest = (ffn_near, ffn_side, ffn_up, up_corner, down_corner)
    ffn_pieces += [ffn_rest, tuple(to_sibling(w) for w in ffn_rest)]
    ffn_b = ffn_fwd_call(
        cross_scalars, second_low, ffn_pieces[2:], ffn_a[0],
        (second_hat, gains[1], biases[1], cotangent, gains[2], biases[2]),
    )
    out_rows, third_low, third_scaled, third_gain, third_bias = ffn_b[:5]

    def plan_of(pieces):
        return [(piece // 2, 2 * (piece % 2) + half) for piece in pieces for half in (0, 1)]

    ffn_saved = [ffn_a[1:3], ffn_b[5:7]]
    ffn_d = ffn_bwd_call(
        cross_scalars, third_low, second_low, ffn_pieces[1::2], ffn_saved, plan_of((1, 3)), third_scaled, None
    )
    ffn_sum = Reduction(ffn_d[1], [(0, 3, "yzx"), (3, 6, "xyz"), (6, 8, "zxy")], ffn_finish())
    ffn_e = ffn_bwd_call(
        cross_scalars, third_low, second_low, ffn_pieces[::2], ffn_saved, plan_of((0, 2)), ffn_d[0],
        (second_hat, second_inv, gains[1]),
    )
    second_back, second_scaled, second_gain, second_bias = ffn_e[:4]
    ffn_sum.begin(ffn_e[4], second_gain)
    second_back = after(second_back, *advance([ffn_sum]))

    cross_e = attention_bwd_call(
        cross_scalars, second_back, cross_in, cross_pieces[1::2] + cross_pieces[::2],
        [cross_a[:5], cross_b[:5]], plan_of((1, 3, 0, 2)), second_scaled,
        (first_hat, first_inv, gains[0]), 2,
    )
    first_back, first_scaled, first_gain, first_bias, memory_part = cross_e[:5]
    norm_sums = jnp.stack([first_gain, second_gain, third_gain, first_bias, second_bias, third_bias])
    norm_sums = jnp.concatenate([jnp.sum(norm_sums, axis=1), jnp.zeros((2, norm_sums.shape[2]), F32)])
    norm_sums = lax.all_gather(norm_sums, ("dp", "tensor"), axis=0)
    sends = advance([ffn_sum], first_gain)
    cross_sum = Reduction(after(cross_e[5], *sends), [(0, 4, "zyx"), (4, 8, "yxz")], attention_finish((1, 2)))
    first_back = after(first_back, *sends)

    self_saved = [self_a[:5], self_b[:5]]
    self_d = attention_bwd_call(
        self_scalars, first_back, [tokens], self_pieces[1::2], self_saved, plan_of((1, 3)), None, None
    )
    cross_sum.begin(cross_e[6], self_d[0])
    sends = advance([cross_sum, ffn_sum], self_d[0])
    self_sum = Reduction(after(self_d[1], *sends), [(0, 4, "yxz"), (4, 8, "xzy")], attention_finish((3,)))
    first_back = after(first_back, *sends)
    self_e = attention_bwd_call(
        self_scalars, first_back, [tokens], self_pieces[::2], self_saved, plan_of((0, 2)), None, None
    )
    self_sum.begin(self_e[1], self_e[0])
    sends = advance([self_sum])
    grad_tokens, grad_memory = inputs_back_call(
        self_scalars, after(first_scaled, *sends),
        [(self_d[0], self_pieces[1::2]), (self_e[0], self_pieces[::2])],
        (memory_part, cross_pieces[1::2] + cross_pieces[::2]),
    )
    sends = advance([cross_sum, ffn_sum], *sends)
    sends = advance([self_sum], *sends, grad_tokens)
    sends = advance([cross_sum, ffn_sum], *sends)
    sends = advance([self_sum], *sends)
    norm_total = jnp.sum(after(norm_sums, *sends), axis=0)
    sends = advance([cross_sum], *sends, norm_total)
    sends = advance([self_sum], *sends)
    sends = advance([cross_sum], *sends)
    advance([self_sum], *sends)
    self_sum, cross_sum, ffn_sum = self_sum.total, cross_sum.total, ffn_sum.total

    return (
        out_rows,
        grad_tokens,
        grad_memory,
        *self_sum,
        *cross_sum,
        *ffn_sum,
        norm_total[:3],
        norm_total[3:6],
    )


def sentence_fits(mesh, tokens, memory, dec_lengths):
    shape = dict(mesh.shape)
    rows = tokens.shape[0] // mesh.size
    sentences = dec_lengths.shape[1]
    return (
        shape["tensor"] == 4
        and shape["dp"] == 8
        and sentences == 4
        and rows == 512
        and memory.shape[0] // mesh.size == rows
        and tokens.shape[1] == 1024
    )


def smooth_gate(values):
    return jax.nn.gelu(values, approximate=True)


def norm_rows(hidden, norm_gain, norm_bias):
    center = hidden - jnp.mean(hidden, axis=-1, keepdims=True)
    inverse = lax.rsqrt(jnp.mean(center * center, axis=-1, keepdims=True) + NORM_EPSILON)
    normed = center * inverse
    return (normed * norm_gain + norm_bias, normed, inverse)


def norm_back(gradient, normed, inverse, norm_gain):
    scaled = gradient * norm_gain
    grad_in = inverse * (
        scaled
        - jnp.mean(scaled, axis=-1, keepdims=True)
        - normed * jnp.mean(scaled * normed, axis=-1, keepdims=True)
    )
    return (grad_in, jnp.sum(gradient * normed, axis=0), jnp.sum(gradient, axis=0))


def head_view(values, sentences):
    return values.reshape(sentences, -1, values.shape[1] // HEAD_DIM, HEAD_DIM)


def masked_scores(query_heads, key_heads, key_mask):
    scores = jnp.einsum(
        "sqhe,skhe->shqk", query_heads, key_heads, preferred_element_type=jnp.float32
    ) * HEAD_DIM ** (-0.5)
    return jnp.where(key_mask, scores, MASKED_SCORE)


def attention_forward(query_rows, key_rows, value_rows, key_mask, sentences):
    scores = masked_scores(
        head_view(query_rows, sentences), head_view(key_rows, sentences), key_mask
    )
    row_peak = jnp.max(scores, axis=-1, keepdims=True)
    exponent_terms = jnp.exp(scores - row_peak)
    row_sum = jnp.sum(exponent_terms, axis=-1, keepdims=True)
    softmax_probs = exponent_terms / row_sum
    attended = jnp.einsum(
        "shqk,skhe->sqhe",
        softmax_probs.astype(jnp.bfloat16),
        head_view(value_rows, sentences),
        preferred_element_type=jnp.float32,
    ).astype(jnp.bfloat16)
    return (attended.reshape(query_rows.shape), row_peak + jnp.log(row_sum))


def attention_backward(query_rows, key_rows, value_rows, key_mask, log_total, grad_rows, sentences):
    query_heads = head_view(query_rows, sentences)
    key_heads = head_view(key_rows, sentences)
    value_heads = head_view(value_rows, sentences)
    grad_heads = head_view(grad_rows, sentences)
    softmax_probs = jnp.exp(masked_scores(query_heads, key_heads, key_mask) - log_total)
    grad_probs = jnp.einsum(
        "sqhe,skhe->shqk", grad_heads, value_heads, preferred_element_type=jnp.float32
    )
    row_delta = jnp.sum(softmax_probs * grad_probs, axis=-1, keepdims=True)
    grad_scores = (softmax_probs * (grad_probs - row_delta)).astype(jnp.bfloat16)
    score_scale = HEAD_DIM ** (-0.5)
    grad_query = (
        jnp.einsum("shqk,skhe->sqhe", grad_scores, key_heads, preferred_element_type=jnp.float32)
        * score_scale
    ).astype(jnp.bfloat16)
    grad_key = (
        jnp.einsum("shqk,sqhe->skhe", grad_scores, query_heads, preferred_element_type=jnp.float32)
        * score_scale
    ).astype(jnp.bfloat16)
    grad_value = jnp.einsum(
        "shqk,sqhe->skhe",
        softmax_probs.astype(jnp.bfloat16),
        grad_heads,
        preferred_element_type=jnp.float32,
    ).astype(jnp.bfloat16)
    return (
        grad_query.reshape(query_rows.shape),
        grad_key.reshape(key_rows.shape),
        grad_value.reshape(value_rows.shape),
    )


def body(
    tokens,
    memory,
    dec_lengths,
    mem_lengths,
    self_qkv,
    self_out,
    cross_q,
    cross_kv,
    cross_out,
    ffn_in,
    ffn_out,
    norm_gains,
    norm_biases,
    cotangent,
):
    row_share = tokens.shape[0]
    sentences = dec_lengths.shape[1]
    all_tokens, all_memory = (
        lax.all_gather(tokens, "tensor", axis=0, tiled=True),
        lax.all_gather(memory, "tensor", axis=0, tiled=True),
    )
    sentence_len = all_tokens.shape[0] // sentences
    memory_len = all_memory.shape[0] // sentences
    positions = jnp.arange(sentence_len, dtype=jnp.int32)
    self_mask = (
        (positions[None, :] <= positions[:, None])[None]
        & (positions[None, None, :] < dec_lengths[0][:, None, None])
    )[:, None]
    memory_positions = jnp.arange(memory_len, dtype=jnp.int32)
    cross_mask = (memory_positions[None, :] < mem_lengths[0][:, None])[:, None, None, :]

    def branch_rows(attended, weight):
        return lax.psum_scatter(
            jnp.dot(attended, weight, preferred_element_type=jnp.float32).astype(jnp.bfloat16),
            "tensor",
            scatter_dimension=0,
            tiled=True,
        ).astype(jnp.float32)

    def branch_grad(grad_rows, attended, weight):
        grad_low = grad_rows.astype(jnp.bfloat16)
        grad_all = lax.all_gather(grad_low, "tensor", axis=0, tiled=True)
        grad_attended = jnp.dot(grad_all, weight.T, preferred_element_type=jnp.float32).astype(
            jnp.bfloat16
        )
        weight_part = jnp.dot(attended.T, grad_all, preferred_element_type=jnp.float32)
        return (grad_attended, weight_part)

    def gather_normed(values):
        return lax.all_gather(values, "tensor", axis=0, tiled=True)

    def head_input_sum(term):
        return lax.psum_scatter(
            term(jnp.int32(0), row_share * lax.axis_size("tensor")).astype(jnp.bfloat16),
            "tensor",
            scatter_dimension=0,
            tiled=True,
        ).astype(jnp.float32)

    self_proj = jnp.einsum(
        "td,cde->cte", all_tokens, self_qkv, preferred_element_type=jnp.float32
    ).astype(jnp.bfloat16)
    self_att, self_lse = attention_forward(
        self_proj[0], self_proj[1], self_proj[2], self_mask, sentences
    )
    self_branch = branch_rows(self_att, self_out)
    first_norm, first_hat, first_inv = norm_rows(
        RESIDUAL_ALPHA * tokens.astype(jnp.float32) + self_branch, norm_gains[0], norm_biases[0]
    )
    first_all = gather_normed(first_norm.astype(jnp.bfloat16))
    cross_query = jnp.dot(first_all, cross_q, preferred_element_type=jnp.float32).astype(
        jnp.bfloat16
    )
    cross_proj = jnp.einsum(
        "td,cde->cte", all_memory, cross_kv, preferred_element_type=jnp.float32
    ).astype(jnp.bfloat16)
    cross_att, cross_lse = attention_forward(
        cross_query, cross_proj[0], cross_proj[1], cross_mask, sentences
    )
    cross_branch = branch_rows(cross_att, cross_out)
    second_norm, second_hat, second_inv = norm_rows(
        RESIDUAL_ALPHA * first_norm + cross_branch, norm_gains[1], norm_biases[1]
    )
    second_all = gather_normed(second_norm.astype(jnp.bfloat16))
    pre_gate = jnp.dot(second_all, ffn_in, preferred_element_type=jnp.float32)
    activated = smooth_gate(pre_gate).astype(jnp.bfloat16)
    ffn_branch = lax.psum_scatter(
        jnp.dot(activated, ffn_out, preferred_element_type=jnp.float32).astype(jnp.bfloat16),
        "tensor",
        scatter_dimension=0,
        tiled=True,
    ).astype(jnp.float32)
    out_rows, third_hat, third_inv = norm_rows(
        RESIDUAL_ALPHA * second_norm + ffn_branch, norm_gains[2], norm_biases[2]
    )
    grad_third, third_gain, third_bias = norm_back(
        cotangent.astype(jnp.float32), third_hat, third_inv, norm_gains[2]
    )
    grad_ffn_all = lax.all_gather(grad_third.astype(jnp.bfloat16), "tensor", axis=0, tiled=True)
    unused_gate, gate_pull = jax.vjp(smooth_gate, pre_gate)
    grad_act = gate_pull(jnp.dot(grad_ffn_all, ffn_out.T, preferred_element_type=jnp.float32))[
        0
    ].astype(jnp.bfloat16)
    grad_ffn_out = jnp.dot(activated.T, grad_ffn_all, preferred_element_type=jnp.float32)
    grad_ffn_in = jnp.dot(second_all.T, grad_act, preferred_element_type=jnp.float32)
    grad_second = RESIDUAL_ALPHA * grad_third + lax.psum_scatter(
        jnp.dot(grad_act, ffn_in.T, preferred_element_type=jnp.float32).astype(jnp.bfloat16),
        "tensor",
        scatter_dimension=0,
        tiled=True,
    ).astype(jnp.float32)
    grad_second_in, second_gain, second_bias = norm_back(
        grad_second, second_hat, second_inv, norm_gains[1]
    )
    grad_cross_att, cross_out_part = branch_grad(grad_second_in, cross_att, cross_out)
    grad_cq, grad_ck, grad_cv = attention_backward(
        cross_query, cross_proj[0], cross_proj[1], cross_mask, cross_lse, grad_cross_att, sentences
    )
    grad_cross_q = jnp.dot(first_all.T, grad_cq, preferred_element_type=jnp.float32)
    cross_grads = jnp.stack([grad_ck, grad_cv])
    grad_cross_kv = jnp.einsum(
        "td,cte->cde", all_memory, cross_grads, preferred_element_type=jnp.float32
    )
    grad_memory = lax.psum_scatter(
        jnp.einsum("cte,cde->td", cross_grads, cross_kv, preferred_element_type=jnp.float32).astype(
            jnp.bfloat16
        ),
        "tensor",
        scatter_dimension=0,
        tiled=True,
    ).astype(jnp.float32)

    def cross_input_term(first_row, row_total):
        return jnp.dot(grad_cq, cross_q.T, preferred_element_type=jnp.float32)

    cross_input = head_input_sum(cross_input_term)
    grad_first = RESIDUAL_ALPHA * grad_second_in + cross_input
    grad_first_in, first_gain, first_bias = norm_back(
        grad_first, first_hat, first_inv, norm_gains[0]
    )
    grad_self_att, self_out_part = branch_grad(grad_first_in, self_att, self_out)
    grad_sq, grad_sk, grad_sv = attention_backward(
        self_proj[0], self_proj[1], self_proj[2], self_mask, self_lse, grad_self_att, sentences
    )
    self_grads = jnp.stack([grad_sq, grad_sk, grad_sv])
    grad_self_qkv = jnp.einsum(
        "td,cte->cde", all_tokens, self_grads, preferred_element_type=jnp.float32
    )

    def self_input_term(first_row, row_total):
        return jnp.einsum("cte,cde->td", self_grads, self_qkv, preferred_element_type=jnp.float32)

    self_input = head_input_sum(self_input_term)
    grad_tokens = RESIDUAL_ALPHA * grad_first_in + self_input
    summed = (
        lax.psum_scatter(
            grad_self_qkv.astype(jnp.bfloat16), "dp", scatter_dimension=1, tiled=True
        ).astype(jnp.float32),
        lax.psum_scatter(
            self_out_part.astype(jnp.bfloat16), "dp", scatter_dimension=1, tiled=True
        ).astype(jnp.float32),
        lax.psum_scatter(
            grad_cross_q.astype(jnp.bfloat16), "dp", scatter_dimension=0, tiled=True
        ).astype(jnp.float32),
        lax.psum_scatter(
            grad_cross_kv.astype(jnp.bfloat16), "dp", scatter_dimension=1, tiled=True
        ).astype(jnp.float32),
        lax.psum_scatter(
            cross_out_part.astype(jnp.bfloat16), "dp", scatter_dimension=1, tiled=True
        ).astype(jnp.float32),
        lax.psum_scatter(
            grad_ffn_in.astype(jnp.bfloat16), "dp", scatter_dimension=0, tiled=True
        ).astype(jnp.float32),
        lax.psum_scatter(
            grad_ffn_out.astype(jnp.bfloat16), "dp", scatter_dimension=1, tiled=True
        ).astype(jnp.float32),
    )
    gain_total, bias_total = lax.psum(
        (
            jnp.stack([first_gain, second_gain, third_gain]),
            jnp.stack([first_bias, second_bias, third_bias]),
        ),
        ("dp", "tensor"),
    )
    return (
        out_rows.astype(jnp.bfloat16),
        grad_tokens,
        grad_memory,
        summed[0],
        summed[1],
        summed[2],
        summed[3],
        summed[4],
        summed[5],
        summed[6],
        gain_total,
        bias_total,
    )


def solution(mesh):
    in_specs = (
        P(("dp", "tensor"), None),
        P(("dp", "tensor"), None),
        P("dp", None),
        P("dp", None),
        P(None, None, "tensor"),
        P("tensor", None),
        P(None, "tensor"),
        P(None, None, "tensor"),
        P("tensor", None),
        P(None, "tensor"),
        P("tensor", None),
        P(),
        P(),
        P(("dp", "tensor"), None),
    )
    out_specs = (
        P(("dp", "tensor"), None),
        P(("dp", "tensor"), None),
        P(("dp", "tensor"), None),
        P(None, "dp", "tensor"),
        P("tensor", "dp"),
        P("dp", "tensor"),
        P(None, "dp", "tensor"),
        P("tensor", "dp"),
        P("dp", "tensor"),
        P("tensor", "dp"),
        P(),
        P(),
    )

    def step(*args):
        chosen = sentence_body if sentence_fits(mesh, args[0], args[1], args[2]) else body
        return jax.shard_map(
            chosen, mesh=mesh, in_specs=in_specs, out_specs=out_specs, check_vma=False
        )(*args)

    return step
```

```python
import functools
import jax
import jax.numpy as jnp
from jax import lax
from jax.experimental import pallas as pl
from jax.experimental.pallas import tpu as pltpu
from jax.sharding import PartitionSpec as P

HEAD_DIM = 64
RESIDUAL_ALPHA = 4.16
NORM_EPSILON = 1e-05
MASKED_SCORE = -1000000000.0
SCORE_SCALE = HEAD_DIM ** (-0.5)
UNIT = 128
QUERY_BLOCK = 256
FFN_UNIT = 512
ROW_CHUNK = 64
BF16 = jnp.bfloat16
F32 = jnp.float32


def dot(left, right):
    return lax.dot_general(left, right, (((1,), (0,)), ((), ())), preferred_element_type=F32)


def dot_tn(left, right):
    return lax.dot_general(left, right, (((0,), (0,)), ((), ())), preferred_element_type=F32)


def dot_nt(left, right):
    return lax.dot_general(left, right, (((1,), (1,)), ((), ())), preferred_element_type=F32)


def shard_of(position):
    return ((position >> 2) & 1) | (position & 2) | ((position & 1) << 2)


def copy_of(source, target, sem):
    return pltpu.make_async_copy(source, target, sem)


def own_lanes(rows, head):
    lanes = lax.broadcasted_iota(jnp.int32, rows.shape, 1)
    return jnp.where((lanes >= HEAD_DIM) if head else (lanes < HEAD_DIM), rows, 0.0)


def extended_keys(keys, length):
    lanes = lax.broadcasted_iota(jnp.int32, keys.shape, 1)
    rows = lax.broadcasted_iota(jnp.int32, keys.shape, 0)
    mask = jnp.where((lanes == 0) & (rows >= length), MASKED_SCORE, 0.0).astype(BF16)
    keys = keys.astype(F32)
    return [jnp.concatenate([own_lanes(keys, head).astype(BF16), mask], axis=1) for head in (0, 1)]


def extended_query(query):
    lanes = lax.broadcasted_iota(jnp.int32, query.shape, 1)
    return jnp.concatenate([query, jnp.where(lanes == 0, 1.0, 0.0).astype(BF16)], axis=1)


def fill_diagonal(diagonal):
    keys = lax.broadcasted_iota(jnp.int32, diagonal.shape, 0)
    queries = lax.broadcasted_iota(jnp.int32, diagonal.shape, 1)
    diagonal[...] = jnp.where(keys <= queries, 0.0, MASKED_SCORE)


def key_ranges(block, keys, causal):
    if not causal:
        return [(0, keys)]
    return [(low, low + QUERY_BLOCK) for low in range(0, (block + 1) * QUERY_BLOCK, QUERY_BLOCK)]


def attend_unit(query, keys, values, length, causal, diagonal, lse_ref):
    rows, count = query.shape[0], keys.shape[0]
    values_t = jnp.transpose(values.astype(F32)).astype(BF16)
    wide_keys, wide_query = extended_keys(keys, length), extended_query(query)
    items = [(head, block) for block in range(rows // QUERY_BLOCK) for head in (0, 1)]
    scores, probs, totals, mixed = {}, {}, {}, {}
    for head, block in items:
        part = wide_query[block * QUERY_BLOCK : (block + 1) * QUERY_BLOCK]
        ranges = key_ranges(block, count, causal)
        scores[head, block] = [dot_nt(wide_keys[head][a:b], part) for a, b in ranges]
        if causal:
            scores[head, block][-1] = scores[head, block][-1] + diagonal[...]
    for head, block in items:
        pieces = scores[head, block]
        peak = functools.reduce(jnp.maximum, [jnp.max(p, axis=0, keepdims=True) for p in pieces])
        terms = [jnp.exp(p - peak) for p in pieces]
        total = sum(jnp.sum(t, axis=0, keepdims=True) for t in terms)
        at = slice(block * QUERY_BLOCK, (block + 1) * QUERY_BLOCK)
        lse_ref[head : head + 1, at] = peak + jnp.log(total)
        totals[head, block] = total
        probs[head, block] = jnp.concatenate([t.astype(BF16) for t in terms], axis=0)
    for head, block in items:
        own = values_t[head * HEAD_DIM : (head + 1) * HEAD_DIM, : probs[head, block].shape[0]]
        mixed[head, block] = dot(own, probs[head, block]) / totals[head, block]
    out = [
        jnp.transpose(jnp.concatenate([mixed[0, block], mixed[1, block]], axis=0))
        for block in range(rows // QUERY_BLOCK)
    ]
    return jnp.concatenate(out, axis=0).astype(BF16)


def attend_back_unit(query, keys, values, attended, grad, length, causal, diagonal, lse_ref):
    rows, count = query.shape[0], keys.shape[0]
    blocks = range(rows // QUERY_BLOCK)
    query_f, keys_f, grad_f = (a.astype(F32) for a in (query, keys, grad))
    wide_keys, wide_query = extended_keys(keys, length), extended_query(query)
    delta = jnp.transpose(grad_f * attended.astype(F32))
    deltas = [
        jnp.sum(delta[head * HEAD_DIM : (head + 1) * HEAD_DIM], axis=0, keepdims=True)
        for head in (0, 1)
    ]
    keys_t = jnp.transpose(keys_f).astype(BF16)
    query_own = [own_lanes(query_f, head).astype(BF16) for head in (0, 1)]
    grad_own = [own_lanes(grad_f, head).astype(BF16) for head in (0, 1)]
    items = [(head, block) for block in blocks for head in (0, 1)]
    scores, slopes, probs, back, grad_query = {}, {}, {}, {}, {}
    for head, block in items:
        at = slice(block * QUERY_BLOCK, (block + 1) * QUERY_BLOCK)
        for a, b in key_ranges(block, count, causal):
            scores[head, block, a] = dot_nt(wide_keys[head][a:b], wide_query[at])
            slopes[head, block, a] = dot_nt(values[a:b], grad_own[head][at])
    for head, block in items:
        at = slice(block * QUERY_BLOCK, (block + 1) * QUERY_BLOCK)
        ranges = key_ranges(block, count, causal)
        for a, b in ranges:
            score = scores[head, block, a]
            if causal and (a, b) == ranges[-1]:
                score = score + diagonal[...]
            prob = jnp.exp(score - lse_ref[head : head + 1, at])
            probs[head, block, a] = prob.astype(BF16)
            back[head, block, a] = (prob * (slopes[head, block, a] - deltas[head][:, at])).astype(BF16)
    for head, block in items:
        own = keys_t[head * HEAD_DIM : (head + 1) * HEAD_DIM]
        grad_query[head, block] = sum(
            dot(own[:, a:b], back[head, block, a]) for a, b in key_ranges(block, count, causal)
        )
    grad_keys, grad_values = [], []
    for low in sorted({key[2] for key in back}):
        live = [key for key in back if key[2] == low]
        at = [slice(block * QUERY_BLOCK, (block + 1) * QUERY_BLOCK) for _, block, _ in live]
        grad_values.append(
            dot(
                jnp.concatenate([probs[key] for key in live], axis=1),
                jnp.concatenate([grad_own[key[0]][a] for key, a in zip(live, at)], axis=0),
            )
        )
        grad_keys.append(
            dot(
                jnp.concatenate([back[key] for key in live], axis=1),
                jnp.concatenate([query_own[key[0]][a] for key, a in zip(live, at)], axis=0),
            )
        )
    grad_query = [
        jnp.transpose(jnp.concatenate([grad_query[0, block], grad_query[1, block]], axis=0)) * SCORE_SCALE
        for block in blocks
    ]
    return tuple(
        jnp.concatenate(parts, axis=0).astype(BF16) for parts in (grad_query, grad_keys, grad_values)
    )


def norm_chunk(hidden, gain, bias):
    center = hidden - jnp.mean(hidden, axis=-1, keepdims=True)
    inverse = lax.rsqrt(jnp.mean(center * center, axis=-1, keepdims=True) + NORM_EPSILON)
    normed = center * inverse
    return normed * gain + bias, normed, inverse


def norm_back_chunk(gradient, normed, inverse, gain):
    scaled = gradient * gain
    return inverse * (
        scaled
        - jnp.mean(scaled, axis=-1, keepdims=True)
        - normed * jnp.mean(scaled * normed, axis=-1, keepdims=True)
    )


def fold_rows(values):
    return jnp.sum(values.reshape(values.shape[0] // 8, 8, values.shape[1]), axis=0)


def each_chunk(rows, body, results):
    def step(index, carry):
        at = pl.ds(pl.multiple_of(index * ROW_CHUNK, ROW_CHUNK), ROW_CHUNK)
        body(at)
        for buffer, out, sem in results:
            copy_of(buffer.at[at, :], out.at[at, :], sem).start()
        return carry

    lax.fori_loop(0, rows // ROW_CHUNK, step, 0)
    return [copy_of(*result) for result in results]


def store_shards(target, weight, dp):
    for block in range(8):
        target[shard_of(block ^ dp)] = weight[block * UNIT : (block + 1) * UNIT]


SMEM = pl.BlockSpec(memory_space=pltpu.SMEM)
VMEM = pl.BlockSpec(memory_space=pltpu.VMEM)
ANY = pl.BlockSpec(memory_space=pl.ANY)


def params(limit=62):
    return pltpu.CompilerParams(vmem_limit_bytes=limit * 1024 * 1024)


def cost_of(microseconds):
    return pl.CostEstimate(flops=int(microseconds * 1.1e9), bytes_accessed=4 << 20, transcendentals=0)


def sds(shape, dtype):
    return jax.ShapeDtypeStruct(shape, dtype)


def weight_copies(pieces, sc, wbuf, obuf, wsem, osem, columns=(0, 1, 2)):
    groups, outs = [[], [], []], []
    wide = 2 * UNIT
    for index, refs in enumerate(pieces):
        at = slice(index * wide, (index + 1) * wide)
        if len(refs[-1].shape) == 2:
            column = 0
            for ref in refs[:-1]:
                for source in [ref] if len(ref.shape) == 2 else [ref.at[c] for c in range(ref.shape[0])]:
                    if column in columns:
                        low = (columns.index(column) * len(pieces) + index) * wide
                        groups[column].append(copy_of(source, wbuf.at[:, low : low + wide], wsem.at[column, index, 0]))
                    column += 1
            if obuf is not None:
                outs.append(copy_of(refs[-1], obuf.at[at, :], osem.at[index, 0]))
            continue
        parts = [refs[0].at[n] for n in range(refs[0].shape[0])] if len(refs[0].shape) == 4 else refs
        rows = parts[0].shape[1]
        part = wide // len(parts)
        for quarter, ref in enumerate(parts):
            place = quarter ^ (sc[1] if len(parts) == 4 else sc[3])
            for column in columns:
                low = (columns.index(column) * len(pieces) + index) * wide
                groups[column].append(
                    copy_of(
                        ref.at[column],
                        wbuf.at[pl.ds(pl.multiple_of(place * rows, rows), rows), low : low + wide],
                        wsem.at[column, index, quarter],
                    )
                )
            for block in range(4 if obuf is not None else 0):
                outs.append(
                    copy_of(
                        ref.at[3, block * part : (block + 1) * part, :],
                        obuf.at[pl.ds(pl.multiple_of(index * wide + place * part, part), part), block * wide : (block + 1) * wide],
                        osem.at[index, 4 * quarter + block],
                    )
                )
    return groups, outs


def attention_fwd_call(scalars, residual, others, pieces, partial, norm):
    rows, depth = others[0].shape
    causal = len(others) == 1
    number, wide = 2 * len(pieces), 2 * len(pieces) * UNIT
    last, has_partial = norm is not None, partial is not None

    def kernel(*refs):
        it = iter(refs)
        sc = next(it)
        in_refs = [next(it) for _ in others]
        gain_ref, bias_ref = (next(it), next(it)) if last else (None, None)
        old_rows = [next(it) for _ in residual[1:]] if last else []
        res_in = next(it) if last else None
        part_in = next(it) if has_partial else None
        w_refs = [[next(it) for _ in piece] for piece in pieces]
        unit_outs, lse_ref = [next(it) for _ in range(4)], next(it)
        if last:
            norm_outs = [next(it) for _ in range(3)]
        else:
            sum_ref = next(it)
        wbuf, obuf, att_all, diagonal, wsem, osem, lsem, usem = (next(it) for _ in range(8))
        q_ref, k_ref, v_ref, att_ref = (next(it) for _ in range(4))
        if last:
            acc, old, low_ref, hat_ref, inv_ref = (next(it) for _ in range(5))
        length = sc[0] if causal else sc[4]
        groups, outs = weight_copies(w_refs, sc, wbuf, obuf, wsem, osem)
        for copies in groups + [outs]:
            for copy in copies:
                copy.start()
        target = acc if last else sum_ref
        late = []
        if has_partial:
            late.append(copy_of(part_in, target, lsem.at[0]))
        if last:
            late.append(copy_of(res_in, old, lsem.at[1]))
        for copy in late:
            copy.start()
        if causal:
            fill_diagonal(diagonal)
        for c, result in enumerate((q_ref, k_ref, v_ref)):
            for copy in groups[c]:
                copy.wait()
            rows_in = in_refs[0] if causal or c == 0 else in_refs[1]
            proj = dot(rows_in[...], wbuf[:, c * wide : (c + 1) * wide]).astype(BF16)
            if c == 0:
                proj = (proj.astype(F32) * SCORE_SCALE).astype(BF16)
            for index in range(number):
                result[index] = proj[:, index * UNIT : (index + 1) * UNIT]

        flushes = [copy_of(*pair, usem.at[index]) for index, pair in enumerate(zip((q_ref, k_ref, v_ref, att_ref), unit_outs))]
        for copy in flushes[:3]:
            copy.start()

        def step(u, carry):
            attended = attend_unit(q_ref[u], k_ref[u], v_ref[u], length, causal, diagonal, lse_ref.at[u])
            att_ref[u] = attended
            att_all[:, pl.ds(pl.multiple_of(u * UNIT, UNIT), UNIT)] = attended
            return carry

        lax.fori_loop(0, number, step, 0)
        flushes[3].start()
        for copy in outs + late:
            copy.wait()
        if has_partial:
            target[...] += dot(att_all[...], obuf[...])
        else:
            target[...] = dot(att_all[...], obuf[...])
        if last:
            def chunk(at):
                before = old[at, :].astype(F32)
                if old_rows:
                    before = before * old_rows[0][...] + old_rows[1][...]
                normed, hat, inverse = norm_chunk(RESIDUAL_ALPHA * before + acc[at, :], gain_ref[...], bias_ref[...])
                low_ref[at, :] = normed.astype(BF16)
                hat_ref[at, :] = hat
                inv_ref[at, :] = jnp.broadcast_to(inverse, (ROW_CHUNK, 128))

            triples = zip((low_ref, hat_ref, inv_ref), norm_outs)
            flushes += each_chunk(rows, chunk, [(*pair, usem.at[4 + index]) for index, pair in enumerate(triples)])
        for copy in flushes:
            copy.wait()

    unit_rows = sds((number, rows, UNIT), BF16)
    shapes = [unit_rows] * 4 + [sds((number, 2, rows), F32)]
    if last:
        shapes += [sds((rows, depth), BF16), sds((rows, depth), F32), sds((rows, 128), F32)]
    else:
        shapes += [sds((rows, depth), F32)]
    args = [scalars, *others]
    if last:
        args += [*norm, *residual[1:]]
    tail = ([residual[0]] if last else []) + ([partial] if has_partial else [])
    tail += [array for piece in pieces for array in piece]
    scratch = [
        pltpu.VMEM((depth, 3 * wide), BF16),
        pltpu.VMEM((wide, depth), BF16),
        pltpu.VMEM((rows, wide), BF16),
        pltpu.VMEM((QUERY_BLOCK, QUERY_BLOCK), F32),
        pltpu.SemaphoreType.DMA((3, len(pieces), 4)),
        pltpu.SemaphoreType.DMA((len(pieces), 16)),
        pltpu.SemaphoreType.DMA((2,)),
        pltpu.SemaphoreType.DMA((7,)),
    ]
    scratch += [pltpu.VMEM((number, rows, UNIT), BF16)] * 4
    if last:
        scratch += [pltpu.VMEM((rows, depth), F32), pltpu.VMEM((rows, depth), residual[0].dtype)]
        scratch += [pltpu.VMEM((rows, depth), BF16), pltpu.VMEM((rows, depth), F32), pltpu.VMEM((rows, 128), F32)]
    return pl.pallas_call(
        kernel,
        out_shape=shapes,
        in_specs=[SMEM] + [VMEM] * (len(args) - 1) + [ANY] * len(tail),
        out_specs=[ANY] * 4 + [VMEM] + ([ANY] * 3 if last else [VMEM]),
        scratch_shapes=scratch,
        compiler_params=params(),
        cost_estimate=cost_of(0.6 * number),
        name="self_fwd" if causal else "cross_fwd",
    )(*args, *tail)


def attention_bwd_call(scalars, grad_low, others, pieces, saved, plan, carried, norm, results=1):
    rows, depth = grad_low.shape
    causal = len(others) == 1
    number, n_in, wide = len(plan), len(others), len(plan) * UNIT
    last = norm is not None
    skip = 1 if last else 0

    def kernel(*refs):
        it = iter(refs)
        sc = next(it)
        h_ref = next(it)
        in_refs = [next(it) for _ in range(n_in)]
        gain_ref = next(it) if last else None
        late_in = [next(it), next(it)] if last else []
        acc_in = next(it) if last else None
        w_refs = [[next(it) for _ in piece] for piece in pieces]
        s_refs = [[next(it) for _ in call] for call in saved]
        if last:
            low_ref, scaled_ref, gsum_ref, bsum_ref = (next(it) for _ in range(4))
        dall_ref = next(it)
        g_refs = [next(it) for _ in range(results)]
        wbuf, obuf, sbuf, lbuf, att_all, grad_all = (next(it) for _ in range(6))
        stage, diagonal = next(it), next(it)
        if last:
            dquery, acc, hat, inv, low_buf, scaled_buf, nsem = (next(it) for _ in range(7))
        wsem, osem, ssem, gsem, lsem = (next(it) for _ in range(5))
        length, dp = sc[0] if causal else sc[4], sc[2]

        groups, o_copies = weight_copies(w_refs, sc, wbuf, obuf, wsem, osem, (0,) if last else ())
        for copy in o_copies:
            copy.start()
        s_copies = []
        for index, unit in enumerate(plan):
            lanes = slice(index * UNIT, (index + 1) * UNIT)
            call = s_refs[unit[0]]
            for c in range(3):
                s_copies.append(copy_of(call[c].at[unit[1]], sbuf.at[index, c], ssem.at[c, index]))
            s_copies.append(copy_of(call[3].at[unit[1]], att_all.at[:, lanes], ssem.at[3, index]))
            s_copies.append(copy_of(call[4].at[unit[1]], lbuf.at[index], ssem.at[4, index]))
        late = []
        if last:
            late = groups[0] + [
                copy_of(source, target, lsem.at[index])
                for index, (source, target) in enumerate(((acc_in, acc), (late_in[0], hat), (late_in[1], inv)))
            ]
        for copy in s_copies + late:
            copy.start()
        if causal:
            fill_diagonal(diagonal)
        for copy in o_copies:
            copy.wait()
        grad_att = dot_nt(h_ref[...], obuf[...]).astype(BF16)
        for index in range(number):
            grad_all[index] = grad_att[:, index * UNIT : (index + 1) * UNIT]
        for copy in s_copies:
            copy.wait()

        def step(u, carry):
            at = pl.ds(pl.multiple_of(u * UNIT, UNIT), UNIT)
            parts = attend_back_unit(
                sbuf[u, 0], sbuf[u, 1], sbuf[u, 2], att_all[:, at], grad_all[u], length, causal, diagonal, lbuf.at[u]
            )
            if last:
                dquery[:, at] = parts[0]
            for c in range(skip, 3):
                dall_ref[:, pl.ds(pl.multiple_of((c - skip) * wide + u * UNIT, UNIT), UNIT)] = parts[c]
            return carry

        lax.fori_loop(0, number, step, 0)

        share = number // 2 // results

        def keep(rows_in, source, column):
            weight = dot_tn(rows_in[...], source).astype(BF16)
            for index in range(number):
                piece = index // 2
                target = stage.at[piece // share, (index % 2) * 4 + column, piece % share]
                store_shards(target, weight[:, index * UNIT : (index + 1) * UNIT], dp)

        if last:
            keep(in_refs[0], dquery[...], 0)
        for c in range(skip, 3):
            keep(in_refs[-1], dall_ref[:, (c - skip) * wide : (c - skip + 1) * wide], c)
        keep(h_ref, att_all[...], 3)
        g_copies = [copy_of(stage.at[index], ref, gsem.at[index]) for index, ref in enumerate(g_refs)]
        for copy in g_copies:
            copy.start()
        for copy in late:
            copy.wait()
        if last:
            acc[...] += dot_nt(dquery[...], wbuf[...])
            g_copies += norm_back_rows(
                acc, hat, inv, gain_ref, low_buf, scaled_buf, (low_ref, scaled_ref), nsem, gsum_ref, bsum_ref, rows
            )
        for copy in g_copies:
            copy.wait()

    big = sds((rows, depth), F32)
    shapes = []
    if last:
        shapes += [sds((rows, depth), BF16), big, sds((8, depth), F32), sds((8, depth), F32)]
    shapes.append(sds((rows, (3 - skip) * wide), BF16))
    specs_out = ([ANY] * 2 + [VMEM] * 3 if last else [VMEM]) + [ANY] * results
    shapes += [sds((8, number // 2 // results, 8, UNIT, UNIT), BF16)] * results
    args = [scalars, grad_low, *others] + ([norm[2]] if last else [])
    tail = [norm[0], norm[1], carried] if last else []
    tail += [array for piece in pieces for array in piece]
    for call in saved:
        tail += call
    scratch = [
        pltpu.VMEM((depth, wide) if last else (16, 128), BF16),
        pltpu.VMEM((wide, depth), BF16),
        pltpu.VMEM((number, 3, rows, UNIT), BF16),
        pltpu.VMEM((number, 2, rows), F32),
        pltpu.VMEM((rows, wide), BF16),
        pltpu.VMEM((number, rows, UNIT), BF16),
        pltpu.VMEM((results, 8, number // 2 // results, 8, UNIT, UNIT), BF16),
        pltpu.VMEM((QUERY_BLOCK, QUERY_BLOCK), F32),
    ]
    if last:
        scratch += [pltpu.VMEM((rows, wide), BF16), pltpu.VMEM((rows, depth), F32), pltpu.VMEM((rows, depth), F32), pltpu.VMEM((rows, 128), F32)]
        scratch += [pltpu.VMEM((rows, depth), BF16), pltpu.VMEM((rows, depth), F32), pltpu.SemaphoreType.DMA((2,))]
    scratch += [
        pltpu.SemaphoreType.DMA((3, len(pieces), 4)),
        pltpu.SemaphoreType.DMA((len(pieces), 16)),
        pltpu.SemaphoreType.DMA((5, number)),
        pltpu.SemaphoreType.DMA((results,)),
        pltpu.SemaphoreType.DMA((4,)),
    ]
    return pl.pallas_call(
        kernel,
        out_shape=shapes,
        in_specs=[SMEM] + [VMEM] * (len(args) - 1) + [ANY] * len(tail),
        out_specs=specs_out,
        scratch_shapes=scratch,
        compiler_params=params(),
        cost_estimate=cost_of(4.2 * number),
        name="self_bwd" if causal else "cross_bwd",
    )(*args, *tail)


def inputs_back_call(scalars, base, parts, memory_part):
    rows, depth = base.shape
    jobs = [(0, grad, pieces, (0, 1, 2)) for grad, pieces in parts] + [(1, *memory_part, (1, 2))]

    def kernel(*refs):
        it = iter(refs)
        sc, base_ref = next(it), next(it)
        grads = [next(it) for _ in jobs]
        w_refs = [[[next(it) for _ in piece] for piece in pieces] for _, _, pieces, _ in jobs]
        outs = [next(it), next(it)]
        bufs, sems = [next(it) for _ in jobs], [next(it) for _ in jobs]
        copies = []
        for index, (_, _, _, columns) in enumerate(jobs):
            groups, _ = weight_copies(w_refs[index], sc, bufs[index], None, sems[index], None, columns)
            copies.append([copy for group in groups for copy in group])
            for copy in copies[-1]:
                copy.start()
        outs[0][...] = base_ref[...]
        for index, (out, _, _, _) in enumerate(jobs):
            for copy in copies[index]:
                copy.wait()
            if out:
                outs[1][...] = dot_nt(grads[index][...], bufs[index][...])
            else:
                outs[0][...] += dot_nt(grads[index][...], bufs[index][...])

    args = [scalars, base] + [grad for _, grad, _, _ in jobs]
    tail = [array for _, _, pieces, _ in jobs for piece in pieces for array in piece]
    return pl.pallas_call(
        kernel,
        out_shape=[sds((rows, depth), F32)] * 2,
        in_specs=[SMEM] + [VMEM] * (len(args) - 1) + [ANY] * len(tail),
        out_specs=[VMEM] * 2,
        scratch_shapes=[pltpu.VMEM((depth, grad.shape[1]), BF16) for _, grad, _, _ in jobs]
        + [pltpu.SemaphoreType.DMA((3, len(pieces), 4)) for _, _, pieces, _ in jobs],
        compiler_params=params(),
        cost_estimate=cost_of(12),
        name="inputs_back",
    )(*args, *tail)


def norm_back_rows(acc, hat, inv, gain_ref, low_buf, scaled_buf, outs, sems, gsum_ref, bsum_ref, rows):
    gsum_ref[...] = jnp.zeros_like(gsum_ref)
    bsum_ref[...] = jnp.zeros_like(bsum_ref)

    def chunk(at):
        gradient, normed = acc[at, :], hat[at, :]
        grad_in = norm_back_chunk(gradient, normed, inv[at, :1], gain_ref[...])
        low_buf[at, :] = grad_in.astype(BF16)
        scaled_buf[at, :] = RESIDUAL_ALPHA * grad_in
        gsum_ref[...] += fold_rows(gradient * normed)
        bsum_ref[...] += fold_rows(gradient)

    pairs = zip((low_buf, scaled_buf), outs)
    return each_chunk(rows, chunk, [(*pair, sems.at[index]) for index, pair in enumerate(pairs)])


GELU_SCALE = 0.7978845608028654
GELU_CUBE = 0.044715


def gelu_and_slope(pre):
    square = pre * pre
    inner = pre * (GELU_SCALE + (GELU_SCALE * GELU_CUBE) * square)
    curve = jnp.tanh(inner)
    half = 0.5 + 0.5 * curve
    slope = half * (1.0 + pre * (1.0 - curve) * (GELU_SCALE + (3.0 * GELU_SCALE * GELU_CUBE) * square))
    return pre * half, slope


FFN_PART = FFN_UNIT // 2


def ffn_copies(pieces, order, ubuf, dbuf, usem, dsem):
    ups, downs = [], []
    for index, refs in enumerate(pieces):
        wide = 2 * FFN_UNIT
        at = slice(index * wide, (index + 1) * wide)
        if len(refs) == 2:
            ups.append([copy_of(refs[0], ubuf.at[:, at], usem.at[index, 0])])
            downs.append([copy_of(refs[1], dbuf.at[at, :], dsem.at[index, 0])])
            continue
        ups.append([])
        downs.append([])
        rows = refs[0].shape[1]
        for quarter in range(4):
            up = refs[quarter].at[0]
            down = refs[quarter].at[1] if quarter < 3 else refs[4].at[0]
            place = (quarter ^ order) * rows
            ups[-1].append(copy_of(up, ubuf.at[pl.ds(pl.multiple_of(place, rows), rows), at], usem.at[index, quarter]))
            downs[-1].append(
                copy_of(down, dbuf.at[pl.ds(pl.multiple_of(index * wide + place, rows), rows), :], dsem.at[index, quarter])
            )
    return ups, downs


def ffn_fwd_call(scalars, inputs, pieces, partial, final):
    rows, depth = inputs.shape
    number = 2 * len(pieces)
    last, has_partial = final is not None, partial is not None

    def kernel(*refs):
        it = iter(refs)
        sc, x_ref = next(it), next(it)
        if last:
            gain_old, bias_old, gain_ref, bias_ref = (next(it) for _ in range(4))
            late_in = [next(it), next(it)]
        part_in = next(it) if has_partial else None
        w_refs = [[next(it) for _ in piece] for piece in pieces]
        if last:
            norm_outs = [next(it) for _ in range(3)]
            gsum_ref, bsum_ref = next(it), next(it)
        else:
            sum_ref = next(it)
        act_ref, slope_ref = next(it), next(it)
        ubuf, dbuf, abuf, sbuf, pbuf, psem = (next(it) for _ in range(6))
        if last:
            acc, hat, cot, lsem, out_ref, low_ref, scaled_ref, nsem = (next(it) for _ in range(8))
        wsem, gsem = next(it), next(it)
        target = acc if last else sum_ref

        up_copies, down_copies = ffn_copies(w_refs, sc[1], ubuf, dbuf, wsem.at[0], wsem.at[1])
        for copies in up_copies + down_copies:
            for copy in copies:
                copy.start()
        if has_partial:
            part_copy = copy_of(part_in, target, psem)
            part_copy.start()
        if last:
            late = [copy_of(late_in[0], hat, lsem.at[0]), copy_of(late_in[1], cot, lsem.at[1])]
            for copy in late:
                copy.start()
        saves = []

        def gate(pre, index):
            activated, slope = gelu_and_slope(pre)
            abuf[:, index * FFN_UNIT : (index + 1) * FFN_UNIT] = activated.astype(BF16)
            sbuf[:, index * FFN_UNIT : (index + 1) * FFN_UNIT] = slope.astype(BF16)

        for index in range(number):
            if index % 2 == 0:
                for copy in up_copies[index // 2]:
                    copy.wait()
            if index:
                gate(pbuf[(index - 1) % 2], index - 1)
            pbuf[index % 2] = dot(x_ref[...], ubuf[:, index * FFN_UNIT : (index + 1) * FFN_UNIT])
        gate(pbuf[(number - 1) % 2], number - 1)
        for index in range(number):
            at = slice(index * FFN_UNIT, (index + 1) * FFN_UNIT)
            saves += [
                copy_of(abuf.at[:, at], act_ref.at[index], gsem.at[0, index]),
                copy_of(sbuf.at[:, at], slope_ref.at[index], gsem.at[1, index]),
            ]
        for copy in saves:
            copy.start()
        for copies in down_copies:
            for copy in copies:
                copy.wait()
        if has_partial:
            part_copy.wait()
            target[...] += dot(abuf[...], dbuf[...])
        else:
            target[...] = dot(abuf[...], dbuf[...])
        if last:
            for copy in late:
                copy.wait()
            gsum_ref[...] = jnp.zeros_like(gsum_ref)
            bsum_ref[...] = jnp.zeros_like(bsum_ref)

            def chunk(at):
                old = hat[at, :] * gain_old[...] + bias_old[...]
                normed, xhat, inverse = norm_chunk(RESIDUAL_ALPHA * old + acc[at, :], gain_ref[...], bias_ref[...])
                out_ref[at, :] = normed.astype(BF16)
                gradient = cot[at, :].astype(F32)
                grad_in = norm_back_chunk(gradient, xhat, inverse, gain_ref[...])
                low_ref[at, :] = grad_in.astype(BF16)
                scaled_ref[at, :] = RESIDUAL_ALPHA * grad_in
                gsum_ref[...] += fold_rows(gradient * xhat)
                bsum_ref[...] += fold_rows(gradient)

            triples = zip((out_ref, low_ref, scaled_ref), norm_outs)
            saves += each_chunk(rows, chunk, [(*pair, nsem.at[index]) for index, pair in enumerate(triples)])
        for copy in saves:
            copy.wait()

    big, low = sds((rows, depth), F32), sds((rows, depth), BF16)
    if last:
        shapes = [low, low, big, sds((8, depth), F32), sds((8, depth), F32)]
    else:
        shapes = [big]
    specs_out = ([ANY] * 3 + [VMEM] * 2 if last else [VMEM]) + [ANY, ANY]
    shapes += [sds((number, rows, FFN_UNIT), BF16)] * 2
    args = [scalars, inputs]
    if last:
        args += [final[1], final[2], final[4], final[5]]
    specs = [SMEM] + [VMEM] * (len(args) - 1)
    tail = ([final[0], final[3]] if last else []) + ([partial] if has_partial else []) + [array for piece in pieces for array in piece]
    scratch = [
        pltpu.VMEM((depth, number * FFN_UNIT), BF16),
        pltpu.VMEM((number * FFN_UNIT, depth), BF16),
        pltpu.VMEM((rows, number * FFN_UNIT), BF16),
        pltpu.VMEM((rows, number * FFN_UNIT), BF16),
        pltpu.VMEM((2, rows, FFN_UNIT), F32),
        pltpu.SemaphoreType.DMA,
    ]
    if last:
        scratch += [
            pltpu.VMEM((rows, depth), F32),
            pltpu.VMEM((rows, depth), F32),
            pltpu.VMEM((rows, depth), BF16),
            pltpu.SemaphoreType.DMA((2,)),
            pltpu.VMEM((rows, depth), BF16),
            pltpu.VMEM((rows, depth), BF16),
            pltpu.VMEM((rows, depth), F32),
            pltpu.SemaphoreType.DMA((3,)),
        ]
    scratch += [pltpu.SemaphoreType.DMA((2, len(pieces), 4)), pltpu.SemaphoreType.DMA((2, number))]
    return pl.pallas_call(
        kernel,
        out_shape=shapes,
        in_specs=specs + [ANY] * len(tail),
        out_specs=specs_out,
        scratch_shapes=scratch,
        compiler_params=params(),
        cost_estimate=cost_of(12),
        name="ffn_fwd",
    )(*args, *tail)


def ffn_bwd_call(scalars, grad_low, inputs, pieces, saved, plan, carried, norm):
    rows, depth = inputs.shape
    number = len(plan)
    last = norm is not None

    def kernel(*refs):
        it = iter(refs)
        sc, g_in, x_ref = (next(it) for _ in range(3))
        gain_ref = next(it) if last else None
        late_in = [next(it), next(it)] if last else []
        acc_in = next(it)
        w_refs = [[next(it) for _ in piece] for piece in pieces]
        s_refs = [[next(it) for _ in call] for call in saved]
        if last:
            low_ref, scaled_ref, gsum_ref, bsum_ref = (next(it) for _ in range(4))
        else:
            sum_ref = next(it)
        g_ref = next(it)
        ubuf, dbuf, abuf, sbuf, gbuf, stage, psem = (next(it) for _ in range(7))
        if last:
            acc, hat, inv, lsem, low_buf, scaled_buf, nsem = (next(it) for _ in range(7))
        wsem, ssem, gsem = next(it), next(it), next(it)
        order, dp = sc[1], sc[2]
        target = acc if last else sum_ref

        ups, downs = ffn_copies(w_refs, order, ubuf, dbuf, wsem.at[0], wsem.at[1])
        slopes, acts = [], []
        for index, (call, at) in enumerate(plan):
            lanes = slice(index * FFN_UNIT, (index + 1) * FFN_UNIT)
            slopes.append(copy_of(s_refs[call][1].at[at], sbuf.at[index], ssem.at[0, index]))
            acts.append(copy_of(s_refs[call][0].at[at], abuf.at[:, lanes], ssem.at[1, index]))
        for copies in downs + [slopes, acts] + ups:
            for copy in copies:
                copy.start()
        part_copy = copy_of(acc_in, target, psem)
        part_copy.start()
        if last:
            late = [copy_of(late_in[0], hat, lsem.at[0]), copy_of(late_in[1], inv, lsem.at[1])]
            for copy in late:
                copy.start()
        for index in range(number):
            if index % 2 == 0:
                for copy in downs[index // 2]:
                    copy.wait()
            slopes[index].wait()
            grad_act = dot_nt(g_in[...], dbuf[index * FFN_UNIT : (index + 1) * FFN_UNIT, :]) * sbuf[index].astype(F32)
            gbuf[:, index * FFN_UNIT : (index + 1) * FFN_UNIT] = grad_act.astype(BF16)
        for copy in acts:
            copy.wait()

        def keep(rows_in, source, column):
            for half in range(number // 2):
                wide = 2 * FFN_UNIT
                weight = dot_tn(rows_in[...], source[:, half * wide : (half + 1) * wide]).astype(BF16)
                for inner in range(4):
                    part = weight[:, inner * FFN_PART : (inner + 1) * FFN_PART]
                    store_shards(stage.at[2 * inner + column, half], part, dp)

        keep(x_ref, gbuf, 0)
        keep(g_in, abuf, 1)
        g_copies = [copy_of(stage, g_ref, gsem)]
        for copy in g_copies:
            copy.start()
        for copies in ups:
            for copy in copies:
                copy.wait()
        part_copy.wait()
        target[...] += dot_nt(gbuf[...], ubuf[...])
        if last:
            for copy in late:
                copy.wait()
            g_copies += norm_back_rows(
                acc, hat, inv, gain_ref, low_buf, scaled_buf, (low_ref, scaled_ref), nsem, gsum_ref, bsum_ref, rows
            )
        for copy in g_copies:
            copy.wait()

    big, low = sds((rows, depth), F32), sds((rows, depth), BF16)
    shapes = [low, big, sds((8, depth), F32), sds((8, depth), F32)] if last else [big]
    specs_out = ([ANY] * 2 + [VMEM] * 2 if last else [VMEM]) + [ANY]
    shapes.append(sds((8, number // 2, 8, UNIT, FFN_PART), BF16))
    args = [scalars, grad_low, inputs] + ([norm[2]] if last else [])
    specs = [SMEM] + [VMEM] * (len(args) - 1)
    tail = ([norm[0], norm[1]] if last else []) + [carried] + [array for piece in pieces for array in piece]
    for call in saved:
        tail += call
    scratch = [
        pltpu.VMEM((depth, number * FFN_UNIT), BF16),
        pltpu.VMEM((number * FFN_UNIT, depth), BF16),
        pltpu.VMEM((rows, number * FFN_UNIT), BF16),
        pltpu.VMEM((number, rows, FFN_UNIT), BF16),
        pltpu.VMEM((rows, number * FFN_UNIT), BF16),
        pltpu.VMEM((8, number // 2, 8, UNIT, FFN_PART), BF16),
        pltpu.SemaphoreType.DMA,
    ]
    if last:
        scratch += [
            pltpu.VMEM((rows, depth), F32),
            pltpu.VMEM((rows, depth), F32),
            pltpu.VMEM((rows, 128), F32),
            pltpu.SemaphoreType.DMA((2,)),
            pltpu.VMEM((rows, depth), BF16),
            pltpu.VMEM((rows, depth), F32),
            pltpu.SemaphoreType.DMA((2,)),
        ]
    scratch += [pltpu.SemaphoreType.DMA((2, len(pieces), 4)), pltpu.SemaphoreType.DMA((2, number)), pltpu.SemaphoreType.DMA]
    return pl.pallas_call(
        kernel,
        out_shape=shapes,
        in_specs=specs + [ANY] * len(tail),
        out_specs=specs_out,
        scratch_shapes=scratch,
        compiler_params=params(),
        cost_estimate=cost_of(17),
        name="ffn_bwd",
    )(*args, *tail)


def combine(jobs, shapes):
    arrays = []
    for terms, _, _, _ in jobs:
        for array, _ in terms:
            if not any(array is known for known in arrays):
                arrays.append(array)
    position = {id(array): index for index, array in enumerate(arrays)}

    def part_shape(array, index):
        kept = []
        for extent, at in zip(array.shape, index + (slice(None),) * (array.ndim - len(index))):
            if isinstance(at, slice):
                kept.append(len(range(*at.indices(extent))))
        return tuple(kept)

    part_shapes = [part_shape(*terms[0]) for terms, _, _, _ in jobs]
    count = sum(len(terms) for terms, _, _, _ in jobs)

    def kernel(*refs):
        ins, outs = refs[: len(arrays)], refs[len(arrays) : len(arrays) + len(shapes)]
        rest = refs[len(arrays) + len(shapes) :]
        term_bufs, sum_bufs, isem, osem = rest[:count], rest[count : count + len(jobs)], rest[-2], rest[-1]
        loads, number = [], 0
        for terms, _, _, _ in jobs:
            loads.append([])
            for array, index in terms:
                loads[-1].append(copy_of(ins[position[id(array)]].at[index], term_bufs[number], isem.at[number]))
                number += 1
        for group in loads:
            for copy in group:
                copy.start()
        stores, number = [], 0
        for job, (terms, out, place, kind) in enumerate(jobs):
            for copy in loads[job]:
                copy.wait()
            bufs = term_bufs[number : number + len(terms)]
            number += len(terms)
            lead = part_shapes[job][:-2]
            size = 1
            for extent in lead:
                size *= extent

            def one(flat, carry, bufs=bufs, lead=lead, target=sum_bufs[job]):
                index, left = [], flat
                for extent in reversed(lead):
                    index.append(lax.rem(left, extent))
                    left = lax.div(left, extent)
                index = tuple(reversed(index))
                total = bufs[0][index].astype(F32)
                for buf in bufs[1:]:
                    total = total + buf[index].astype(F32)
                target[index] = total.astype(target.dtype)
                return carry

            if kind == "range":
                lax.fori_loop(0, size, one, 0)
            else:
                total = bufs[0][0].astype(F32)
                for buf in bufs[1:]:
                    total = total + buf[0].astype(F32)
                sum_bufs[job][...] = jnp.transpose(total) if kind == "turned" else total
            stores.append(copy_of(sum_bufs[job], outs[out].at[place], osem.at[job]))
            stores[-1].start()
        for copy in stores:
            copy.wait()

    scratch = [pltpu.VMEM(part_shapes[job], array.dtype) for job, (terms, _, _, _) in enumerate(jobs) for array, _ in terms]
    for job, (_, out, _, kind) in enumerate(jobs):
        shape = part_shapes[job]
        shape = {"range": shape, "plain": shape[1:], "turned": shape[:0:-1]}[kind]
        scratch.append(pltpu.VMEM(shape, shapes[out].dtype))
    scratch += [pltpu.SemaphoreType.DMA((count,)), pltpu.SemaphoreType.DMA((len(jobs),))]
    return pl.pallas_call(
        kernel,
        out_shape=list(shapes),
        in_specs=[ANY] * len(arrays),
        out_specs=[ANY] * len(shapes),
        scratch_shapes=scratch,
        compiler_params=params(),
        cost_estimate=cost_of(3),
        name="combine",
    )(*arrays)


def swap_pairs(count, mask):
    return [(i, i ^ mask) for i in range(count)]


def to_sibling(values):
    return lax.ppermute(values, "tensor", swap_pairs(4, 1))


def over_y(values):
    return lax.ppermute(values, "tensor", swap_pairs(4, 2))


def over_dp(values, mask):
    return lax.ppermute(values, "dp", swap_pairs(8, mask))


def over_x(values):
    return over_dp(values, 1)


def over_z_near(values):
    return over_dp(values, 2)


def over_z_far(values):
    return over_dp(values, 4)


def after(values, *earlier):
    return lax.optimization_barrier((values, *earlier))[0]


MOVES = {"y": over_y, "x": over_x, "z": over_z_near}


class Reduction:
    def __init__(self, sent, portions, finish):
        self.other, self.finish = to_sibling(sent), finish
        self.portions, self.stage, self.sends, self.total = portions, 0, None, None

    def begin(self, kept, *earlier):
        other = after(self.other, *earlier)
        split = (kept.shape[0], 2, 2, 2, 2, *kept.shape[3:])
        arrays = (kept.reshape(split), other.reshape(split))
        self.blocks, self.tail = kept.shape[0], kept.shape[3:]
        self.terms = [[(array, ("b", "y", "x", "z", "w"), low, {}) for array in arrays] for low, _, _ in self.portions]

    def receive(self, *earlier):
        if self.stage == 4:
            moved = after(over_z_far(self.sends[0]), *earlier)
            for (low, _, _), terms in zip(self.portions, self.terms):
                terms.append((moved, ("b",), low, {}))
        elif self.stage:
            for send, (_, _, orders), terms in zip(self.sends, self.portions, self.terms):
                left = tuple(a for a in ("b", "y", "x", "z", "w") if a not in orders[: self.stage])
                terms.append((after(MOVES[orders[self.stage - 1]](send), *earlier), left, 0, {}))

    def jobs(self, first_out):
        jobs, shapes = [], []
        stage = self.stage
        for number, ((low, high, orders), terms) in enumerate(zip(self.portions, self.terms)):
            axis = (*orders, "w", None)[stage]
            picked = []
            for array, axes, start, fixed in terms:
                index = [slice(start, start + high - low)]
                for name in axes[1:]:
                    index.append(1 if name == axis else fixed.get(name, 0 if name in orders[:stage] or (stage > 3 and name == "w") else slice(None)))
                picked.append((array, tuple(index)))
            if stage < 3:
                shapes.append(sds((high - low, *(2,) * (3 - stage), *self.tail), BF16))
                jobs.append((picked, first_out + number, slice(0, high - low), "range"))
            elif stage == 3:
                if not number:
                    shapes.append(sds((self.blocks, *self.tail), BF16))
                jobs.append((picked, first_out, slice(low, high), "range"))
            else:
                if not number:
                    shapes += self.finish[0]
                for block in range(low, high):
                    shift = block - low
                    one = [(a, (slice(index[0].start + shift, index[0].start + shift + 1), *index[1:])) for a, index in picked]
                    out, place, kind = self.finish[1](block)
                    jobs.append((one, first_out + out, place, kind))
        self.stage += 1
        return jobs, shapes


def attention_finish(counts):
    stacks = [sds((count, UNIT, 2 * UNIT) if count > 1 else (UNIT, 2 * UNIT), F32) for count in counts]

    def place_of(block):
        half, matrix = block // 4, block % 4
        lanes = slice(half * UNIT, (half + 1) * UNIT)
        if matrix == 3:
            return len(counts), (lanes, slice(None)), "turned"
        stack = 0 if matrix < counts[0] else 1
        if counts[stack] == 1:
            return stack, (slice(None), lanes), "plain"
        return stack, (matrix - sum(counts[:stack]), slice(None), lanes), "plain"

    return [*stacks, sds((2 * UNIT, UNIT), F32)], place_of


def ffn_finish():
    def place_of(block):
        lanes = slice(block // 2 * FFN_PART, (block // 2 + 1) * FFN_PART)
        if block % 2:
            return 1, (lanes, slice(None)), "turned"
        return 0, (slice(None), lanes), "plain"

    return [sds((UNIT, 4 * FFN_PART), F32), sds((4 * FFN_PART, UNIT), F32)], place_of


def advance(reductions, *earlier):
    jobs, shapes, bounds = [], [], []
    for reduction in reductions:
        reduction.receive(*earlier)
        more, made = reduction.jobs(len(shapes))
        bounds.append((len(shapes), len(shapes) + len(made)))
        jobs, shapes = jobs + more, shapes + made
    results = combine(jobs, shapes)
    for reduction, (low, high) in zip(reductions, bounds):
        reduction.sends = list(results[low:high])
        if reduction.stage == 5:
            reduction.total = results[low:high]
    return list(results)


def sentence_body(
    tokens,
    memory,
    dec_lengths,
    mem_lengths,
    self_qkv,
    self_out,
    cross_q,
    cross_kv,
    cross_out,
    ffn_in,
    ffn_out,
    norm_gains,
    norm_biases,
    cotangent,
):
    dp = lax.axis_index("dp")
    mine = lax.axis_index("tensor")
    order = dp & 3
    inner = (dp >> 1) & 1
    scalars = jnp.stack([dec_lengths[0, mine], order, dp, inner, mem_lengths[0, mine]]).astype(jnp.int32)
    gains = [norm_gains[i : i + 1] for i in range(3)]
    biases = [norm_biases[i : i + 1] for i in range(3)]

    def part_rows(values, parts):
        rows = values.shape[-2] // parts
        place = order if parts == 4 else inner
        return lax.dynamic_slice_in_dim(values, place * rows, rows, values.ndim - 2)

    def folded(values):
        blocks = values.reshape(values.shape[0], 4, 2 * UNIT)
        return blocks.transpose(1, 0, 2).reshape(1, 4 * values.shape[0], 2 * UNIT)

    self_near = over_y(jnp.concatenate([part_rows(self_qkv, 4), folded(part_rows(self_out, 4))]))
    cross_near = over_y(
        jnp.concatenate([part_rows(cross_q, 2)[None], part_rows(cross_kv, 2), folded(part_rows(cross_out, 2))])
    )
    ffn_near = over_y(jnp.stack([part_rows(ffn_in, 4), part_rows(ffn_out, 4)]))
    self_own = (self_qkv, self_out)
    self_sib = tuple(to_sibling(w) for w in self_own)
    self_a = attention_fwd_call(scalars, [], [tokens], [self_own, self_sib], None, None)
    self_near = after(self_near, self_a[4])
    self_side, self_up = over_x(self_near), over_z_near(self_near)
    self_corner = over_x(self_up)
    cross_own, ffn_own = (cross_q, cross_kv, cross_out), (ffn_in, ffn_out)
    cross_sib = tuple(to_sibling(w) for w in cross_own)
    cross_up = over_z_near(cross_near)
    self_rest = (self_near, self_side, self_up, after(self_corner, cross_near, *cross_sib))
    self_far = tuple(to_sibling(w) for w in self_rest)
    self_pieces = [self_own, self_sib, self_rest, self_far]
    self_b = attention_fwd_call(
        scalars, [tokens], [tokens], self_pieces[2:], self_a[5], (gains[0], biases[0])
    )
    first_low, first_hat, first_inv = self_b[5:]
    cross_in = [first_low, memory]
    cross_rest = jnp.stack([cross_near, after(cross_up, self_b[4])])
    cross_far = to_sibling(cross_rest)
    cross_a = attention_fwd_call(after(scalars, ffn_near), [], cross_in, [cross_own, cross_sib], None, None)
    ffn_sib = tuple(to_sibling(after(w, ffn_near)) for w in ffn_own)
    ffn_side, ffn_up = over_x(ffn_near), over_z_near(ffn_near)
    cross_pieces = [cross_own, cross_sib, (cross_rest,), (after(cross_far, cross_a[4]),)]
    cross_b = attention_fwd_call(
        scalars, [first_hat, gains[0], biases[0]], cross_in, cross_pieces[2:], cross_a[5], (gains[1], biases[1])
    )
    second_low, second_hat, second_inv = cross_b[5:]
    ffn_side, ffn_up = after(ffn_side, cross_b[4]), after(ffn_up, cross_b[4])
    up_corner, down_corner = over_x(ffn_up[:1]), over_z_near(ffn_side[1:])
    ffn_pieces = [ffn_own, ffn_sib]
    ffn_a = ffn_fwd_call(scalars, second_low, ffn_pieces, None, None)
    up_corner, down_corner = after(up_corner, ffn_a[0]), after(down_corner, ffn_a[0])
    ffn_rest = (ffn_near, ffn_side, ffn_up, up_corner, down_corner)
    ffn_pieces += [ffn_rest, tuple(to_sibling(w) for w in ffn_rest)]
    ffn_b = ffn_fwd_call(
        scalars, second_low, ffn_pieces[2:], ffn_a[0],
        (second_hat, gains[1], biases[1], cotangent, gains[2], biases[2]),
    )
    out_rows, third_low, third_scaled, third_gain, third_bias = ffn_b[:5]

    def plan_of(pieces):
        return [(piece // 2, 2 * (piece % 2) + half) for piece in pieces for half in (0, 1)]

    ffn_saved = [ffn_a[1:3], ffn_b[5:7]]
    ffn_d = ffn_bwd_call(
        scalars, third_low, second_low, ffn_pieces[1::2], ffn_saved, plan_of((1, 3)), third_scaled, None
    )
    ffn_sum = Reduction(ffn_d[1], [(0, 3, "yzx"), (3, 6, "xyz"), (6, 8, "zxy")], ffn_finish())
    ffn_e = ffn_bwd_call(
        scalars, third_low, second_low, ffn_pieces[::2], ffn_saved, plan_of((0, 2)), ffn_d[0],
        (second_hat, second_inv, gains[1]),
    )
    second_back, second_scaled, second_gain, second_bias = ffn_e[:4]
    ffn_sum.begin(ffn_e[4], second_gain)
    second_back = after(second_back, *advance([ffn_sum]))

    cross_e = attention_bwd_call(
        scalars, second_back, cross_in, cross_pieces[1::2] + cross_pieces[::2],
        [cross_a[:5], cross_b[:5]], plan_of((1, 3, 0, 2)), second_scaled,
        (first_hat, first_inv, gains[0]), 2,
    )
    first_back, first_scaled, first_gain, first_bias, memory_part = cross_e[:5]
    norm_sums = jnp.stack([first_gain, second_gain, third_gain, first_bias, second_bias, third_bias])
    norm_sums = jnp.concatenate([jnp.sum(norm_sums, axis=1), jnp.zeros((2, norm_sums.shape[2]), F32)])
    norm_sums = lax.all_gather(norm_sums, ("dp", "tensor"), axis=0)
    sends = advance([ffn_sum], first_gain)
    cross_sum = Reduction(after(cross_e[5], *sends), [(0, 4, "zyx"), (4, 8, "yxz")], attention_finish((1, 2)))
    first_back = after(first_back, *sends)

    self_saved = [self_a[:5], self_b[:5]]
    self_d = attention_bwd_call(
        scalars, first_back, [tokens], self_pieces[1::2], self_saved, plan_of((1, 3)), None, None
    )
    cross_sum.begin(cross_e[6], self_d[0])
    sends = advance([cross_sum, ffn_sum], self_d[0])
    self_sum = Reduction(after(self_d[1], *sends), [(0, 4, "yxz"), (4, 8, "xzy")], attention_finish((3,)))
    first_back = after(first_back, *sends)
    self_e = attention_bwd_call(
        scalars, first_back, [tokens], self_pieces[::2], self_saved, plan_of((0, 2)), None, None
    )
    self_sum.begin(self_e[1], self_e[0])
    sends = advance([self_sum])
    grad_tokens, grad_memory = inputs_back_call(
        scalars, after(first_scaled, *sends),
        [(self_d[0], self_pieces[1::2]), (self_e[0], self_pieces[::2])],
        (memory_part, cross_pieces[1::2] + cross_pieces[::2]),
    )
    sends = advance([cross_sum, ffn_sum], *sends)
    sends = advance([self_sum], *sends, grad_tokens)
    sends = advance([cross_sum, ffn_sum], *sends)
    sends = advance([self_sum], *sends)
    norm_total = jnp.sum(after(norm_sums, *sends), axis=0)
    sends = advance([cross_sum], *sends, norm_total)
    sends = advance([self_sum], *sends)
    sends = advance([cross_sum], *sends)
    advance([self_sum], *sends)
    self_sum, cross_sum, ffn_sum = self_sum.total, cross_sum.total, ffn_sum.total

    return (
        out_rows,
        grad_tokens,
        grad_memory,
        *self_sum,
        *cross_sum,
        *ffn_sum,
        norm_total[:3],
        norm_total[3:6],
    )


def sentence_fits(mesh, tokens, memory, dec_lengths):
    shape = dict(mesh.shape)
    rows = tokens.shape[0] // mesh.size
    sentences = dec_lengths.shape[1]
    return (
        shape["tensor"] == 4
        and shape["dp"] == 8
        and sentences == 4
        and rows == 512
        and memory.shape[0] // mesh.size == rows
        and tokens.shape[1] == 1024
    )


def smooth_gate(values):
    return jax.nn.gelu(values, approximate=True)


def norm_rows(hidden, norm_gain, norm_bias):
    center = hidden - jnp.mean(hidden, axis=-1, keepdims=True)
    inverse = lax.rsqrt(jnp.mean(center * center, axis=-1, keepdims=True) + NORM_EPSILON)
    normed = center * inverse
    return (normed * norm_gain + norm_bias, normed, inverse)


def norm_back(gradient, normed, inverse, norm_gain):
    scaled = gradient * norm_gain
    grad_in = inverse * (
        scaled
        - jnp.mean(scaled, axis=-1, keepdims=True)
        - normed * jnp.mean(scaled * normed, axis=-1, keepdims=True)
    )
    return (grad_in, jnp.sum(gradient * normed, axis=0), jnp.sum(gradient, axis=0))


def head_view(values, sentences):
    return values.reshape(sentences, -1, values.shape[1] // HEAD_DIM, HEAD_DIM)


def masked_scores(query_heads, key_heads, key_mask):
    scores = jnp.einsum(
        "sqhe,skhe->shqk", query_heads, key_heads, preferred_element_type=jnp.float32
    ) * HEAD_DIM ** (-0.5)
    return jnp.where(key_mask, scores, MASKED_SCORE)


def attention_forward(query_rows, key_rows, value_rows, key_mask, sentences):
    scores = masked_scores(
        head_view(query_rows, sentences), head_view(key_rows, sentences), key_mask
    )
    row_peak = jnp.max(scores, axis=-1, keepdims=True)
    exponent_terms = jnp.exp(scores - row_peak)
    row_sum = jnp.sum(exponent_terms, axis=-1, keepdims=True)
    softmax_probs = exponent_terms / row_sum
    attended = jnp.einsum(
        "shqk,skhe->sqhe",
        softmax_probs.astype(jnp.bfloat16),
        head_view(value_rows, sentences),
        preferred_element_type=jnp.float32,
    ).astype(jnp.bfloat16)
    return (attended.reshape(query_rows.shape), row_peak + jnp.log(row_sum))


def attention_backward(query_rows, key_rows, value_rows, key_mask, log_total, grad_rows, sentences):
    query_heads = head_view(query_rows, sentences)
    key_heads = head_view(key_rows, sentences)
    value_heads = head_view(value_rows, sentences)
    grad_heads = head_view(grad_rows, sentences)
    softmax_probs = jnp.exp(masked_scores(query_heads, key_heads, key_mask) - log_total)
    grad_probs = jnp.einsum(
        "sqhe,skhe->shqk", grad_heads, value_heads, preferred_element_type=jnp.float32
    )
    row_delta = jnp.sum(softmax_probs * grad_probs, axis=-1, keepdims=True)
    grad_scores = (softmax_probs * (grad_probs - row_delta)).astype(jnp.bfloat16)
    score_scale = HEAD_DIM ** (-0.5)
    grad_query = (
        jnp.einsum("shqk,skhe->sqhe", grad_scores, key_heads, preferred_element_type=jnp.float32)
        * score_scale
    ).astype(jnp.bfloat16)
    grad_key = (
        jnp.einsum("shqk,sqhe->skhe", grad_scores, query_heads, preferred_element_type=jnp.float32)
        * score_scale
    ).astype(jnp.bfloat16)
    grad_value = jnp.einsum(
        "shqk,sqhe->skhe",
        softmax_probs.astype(jnp.bfloat16),
        grad_heads,
        preferred_element_type=jnp.float32,
    ).astype(jnp.bfloat16)
    return (
        grad_query.reshape(query_rows.shape),
        grad_key.reshape(key_rows.shape),
        grad_value.reshape(value_rows.shape),
    )


def body(
    tokens,
    memory,
    dec_lengths,
    mem_lengths,
    self_qkv,
    self_out,
    cross_q,
    cross_kv,
    cross_out,
    ffn_in,
    ffn_out,
    norm_gains,
    norm_biases,
    cotangent,
):
    row_share = tokens.shape[0]
    sentences = dec_lengths.shape[1]
    all_tokens, all_memory = (
        lax.all_gather(tokens, "tensor", axis=0, tiled=True),
        lax.all_gather(memory, "tensor", axis=0, tiled=True),
    )
    sentence_len = all_tokens.shape[0] // sentences
    memory_len = all_memory.shape[0] // sentences
    positions = jnp.arange(sentence_len, dtype=jnp.int32)
    self_mask = (
        (positions[None, :] <= positions[:, None])[None]
        & (positions[None, None, :] < dec_lengths[0][:, None, None])
    )[:, None]
    memory_positions = jnp.arange(memory_len, dtype=jnp.int32)
    cross_mask = (memory_positions[None, :] < mem_lengths[0][:, None])[:, None, None, :]

    def branch_rows(attended, weight):
        return lax.psum_scatter(
            jnp.dot(attended, weight, preferred_element_type=jnp.float32).astype(jnp.bfloat16),
            "tensor",
            scatter_dimension=0,
            tiled=True,
        ).astype(jnp.float32)

    def branch_grad(grad_rows, attended, weight):
        grad_low = grad_rows.astype(jnp.bfloat16)
        grad_all = lax.all_gather(grad_low, "tensor", axis=0, tiled=True)
        grad_attended = jnp.dot(grad_all, weight.T, preferred_element_type=jnp.float32).astype(
            jnp.bfloat16
        )
        weight_part = jnp.dot(attended.T, grad_all, preferred_element_type=jnp.float32)
        return (grad_attended, weight_part)

    def gather_normed(values):
        return lax.all_gather(values, "tensor", axis=0, tiled=True)

    def head_input_sum(term):
        return lax.psum_scatter(
            term(jnp.int32(0), row_share * lax.axis_size("tensor")).astype(jnp.bfloat16),
            "tensor",
            scatter_dimension=0,
            tiled=True,
        ).astype(jnp.float32)

    self_proj = jnp.einsum(
        "td,cde->cte", all_tokens, self_qkv, preferred_element_type=jnp.float32
    ).astype(jnp.bfloat16)
    self_att, self_lse = attention_forward(
        self_proj[0], self_proj[1], self_proj[2], self_mask, sentences
    )
    self_branch = branch_rows(self_att, self_out)
    first_norm, first_hat, first_inv = norm_rows(
        RESIDUAL_ALPHA * tokens.astype(jnp.float32) + self_branch, norm_gains[0], norm_biases[0]
    )
    first_all = gather_normed(first_norm.astype(jnp.bfloat16))
    cross_query = jnp.dot(first_all, cross_q, preferred_element_type=jnp.float32).astype(
        jnp.bfloat16
    )
    cross_proj = jnp.einsum(
        "td,cde->cte", all_memory, cross_kv, preferred_element_type=jnp.float32
    ).astype(jnp.bfloat16)
    cross_att, cross_lse = attention_forward(
        cross_query, cross_proj[0], cross_proj[1], cross_mask, sentences
    )
    cross_branch = branch_rows(cross_att, cross_out)
    second_norm, second_hat, second_inv = norm_rows(
        RESIDUAL_ALPHA * first_norm + cross_branch, norm_gains[1], norm_biases[1]
    )
    second_all = gather_normed(second_norm.astype(jnp.bfloat16))
    pre_gate = jnp.dot(second_all, ffn_in, preferred_element_type=jnp.float32)
    activated = smooth_gate(pre_gate).astype(jnp.bfloat16)
    ffn_branch = lax.psum_scatter(
        jnp.dot(activated, ffn_out, preferred_element_type=jnp.float32).astype(jnp.bfloat16),
        "tensor",
        scatter_dimension=0,
        tiled=True,
    ).astype(jnp.float32)
    out_rows, third_hat, third_inv = norm_rows(
        RESIDUAL_ALPHA * second_norm + ffn_branch, norm_gains[2], norm_biases[2]
    )
    grad_third, third_gain, third_bias = norm_back(
        cotangent.astype(jnp.float32), third_hat, third_inv, norm_gains[2]
    )
    grad_ffn_all = lax.all_gather(grad_third.astype(jnp.bfloat16), "tensor", axis=0, tiled=True)
    unused_gate, gate_pull = jax.vjp(smooth_gate, pre_gate)
    grad_act = gate_pull(jnp.dot(grad_ffn_all, ffn_out.T, preferred_element_type=jnp.float32))[
        0
    ].astype(jnp.bfloat16)
    grad_ffn_out = jnp.dot(activated.T, grad_ffn_all, preferred_element_type=jnp.float32)
    grad_ffn_in = jnp.dot(second_all.T, grad_act, preferred_element_type=jnp.float32)
    grad_second = RESIDUAL_ALPHA * grad_third + lax.psum_scatter(
        jnp.dot(grad_act, ffn_in.T, preferred_element_type=jnp.float32).astype(jnp.bfloat16),
        "tensor",
        scatter_dimension=0,
        tiled=True,
    ).astype(jnp.float32)
    grad_second_in, second_gain, second_bias = norm_back(
        grad_second, second_hat, second_inv, norm_gains[1]
    )
    grad_cross_att, cross_out_part = branch_grad(grad_second_in, cross_att, cross_out)
    grad_cq, grad_ck, grad_cv = attention_backward(
        cross_query, cross_proj[0], cross_proj[1], cross_mask, cross_lse, grad_cross_att, sentences
    )
    grad_cross_q = jnp.dot(first_all.T, grad_cq, preferred_element_type=jnp.float32)
    cross_grads = jnp.stack([grad_ck, grad_cv])
    grad_cross_kv = jnp.einsum(
        "td,cte->cde", all_memory, cross_grads, preferred_element_type=jnp.float32
    )
    grad_memory = lax.psum_scatter(
        jnp.einsum("cte,cde->td", cross_grads, cross_kv, preferred_element_type=jnp.float32).astype(
            jnp.bfloat16
        ),
        "tensor",
        scatter_dimension=0,
        tiled=True,
    ).astype(jnp.float32)

    def cross_input_term(first_row, row_total):
        return jnp.dot(grad_cq, cross_q.T, preferred_element_type=jnp.float32)

    cross_input = head_input_sum(cross_input_term)
    grad_first = RESIDUAL_ALPHA * grad_second_in + cross_input
    grad_first_in, first_gain, first_bias = norm_back(
        grad_first, first_hat, first_inv, norm_gains[0]
    )
    grad_self_att, self_out_part = branch_grad(grad_first_in, self_att, self_out)
    grad_sq, grad_sk, grad_sv = attention_backward(
        self_proj[0], self_proj[1], self_proj[2], self_mask, self_lse, grad_self_att, sentences
    )
    self_grads = jnp.stack([grad_sq, grad_sk, grad_sv])
    grad_self_qkv = jnp.einsum(
        "td,cte->cde", all_tokens, self_grads, preferred_element_type=jnp.float32
    )

    def self_input_term(first_row, row_total):
        return jnp.einsum("cte,cde->td", self_grads, self_qkv, preferred_element_type=jnp.float32)

    self_input = head_input_sum(self_input_term)
    grad_tokens = RESIDUAL_ALPHA * grad_first_in + self_input
    summed = (
        lax.psum_scatter(
            grad_self_qkv.astype(jnp.bfloat16), "dp", scatter_dimension=1, tiled=True
        ).astype(jnp.float32),
        lax.psum_scatter(
            self_out_part.astype(jnp.bfloat16), "dp", scatter_dimension=1, tiled=True
        ).astype(jnp.float32),
        lax.psum_scatter(
            grad_cross_q.astype(jnp.bfloat16), "dp", scatter_dimension=0, tiled=True
        ).astype(jnp.float32),
        lax.psum_scatter(
            grad_cross_kv.astype(jnp.bfloat16), "dp", scatter_dimension=1, tiled=True
        ).astype(jnp.float32),
        lax.psum_scatter(
            cross_out_part.astype(jnp.bfloat16), "dp", scatter_dimension=1, tiled=True
        ).astype(jnp.float32),
        lax.psum_scatter(
            grad_ffn_in.astype(jnp.bfloat16), "dp", scatter_dimension=0, tiled=True
        ).astype(jnp.float32),
        lax.psum_scatter(
            grad_ffn_out.astype(jnp.bfloat16), "dp", scatter_dimension=1, tiled=True
        ).astype(jnp.float32),
    )
    gain_total, bias_total = lax.psum(
        (
            jnp.stack([first_gain, second_gain, third_gain]),
            jnp.stack([first_bias, second_bias, third_bias]),
        ),
        ("dp", "tensor"),
    )
    return (
        out_rows.astype(jnp.bfloat16),
        grad_tokens,
        grad_memory,
        summed[0],
        summed[1],
        summed[2],
        summed[3],
        summed[4],
        summed[5],
        summed[6],
        gain_total,
        bias_total,
    )


def solution(mesh):
    in_specs = (
        P(("dp", "tensor"), None),
        P(("dp", "tensor"), None),
        P("dp", None),
        P("dp", None),
        P(None, None, "tensor"),
        P("tensor", None),
        P(None, "tensor"),
        P(None, None, "tensor"),
        P("tensor", None),
        P(None, "tensor"),
        P("tensor", None),
        P(),
        P(),
        P(("dp", "tensor"), None),
    )
    out_specs = (
        P(("dp", "tensor"), None),
        P(("dp", "tensor"), None),
        P(("dp", "tensor"), None),
        P(None, "dp", "tensor"),
        P("tensor", "dp"),
        P("dp", "tensor"),
        P(None, "dp", "tensor"),
        P("tensor", "dp"),
        P("dp", "tensor"),
        P("tensor", "dp"),
        P(),
        P(),
    )

    def step(*args):
        chosen = sentence_body if sentence_fits(mesh, args[0], args[1], args[2]) else body
        return jax.shard_map(
            chosen, mesh=mesh, in_specs=in_specs, out_specs=out_specs, check_vma=False
        )(*args)

    return step
```

```python
import functools
import jax
import jax.numpy as jnp
from jax import lax
from jax.experimental import pallas as pl
from jax.experimental.pallas import tpu as pltpu
from jax.sharding import PartitionSpec as P

HEAD_DIM = 64
RESIDUAL_ALPHA = 4.16
NORM_EPSILON = 1e-05
MASKED_SCORE = -1000000000.0
SCORE_SCALE = HEAD_DIM ** (-0.5)
UNIT = 128
QUERY_BLOCK = 256
FFN_UNIT = 512
ROW_CHUNK = 64
BF16 = jnp.bfloat16
F32 = jnp.float32


def dot(left, right):
    return lax.dot_general(left, right, (((1,), (0,)), ((), ())), preferred_element_type=F32)


def dot_tn(left, right):
    return lax.dot_general(left, right, (((0,), (0,)), ((), ())), preferred_element_type=F32)


def dot_nt(left, right):
    return lax.dot_general(left, right, (((1,), (1,)), ((), ())), preferred_element_type=F32)


def shard_of(position):
    return ((position >> 2) & 1) | (position & 2) | ((position & 1) << 2)


def copy_of(source, target, sem):
    return pltpu.make_async_copy(source, target, sem)


def own_lanes(rows, head):
    lanes = lax.broadcasted_iota(jnp.int32, rows.shape, 1)
    return jnp.where((lanes >= HEAD_DIM) if head else (lanes < HEAD_DIM), rows, 0.0)


def extended_keys(keys, length):
    lanes = lax.broadcasted_iota(jnp.int32, keys.shape, 1)
    rows = lax.broadcasted_iota(jnp.int32, keys.shape, 0)
    mask = jnp.where((lanes == 0) & (rows >= length), MASKED_SCORE, 0.0).astype(BF16)
    keys = keys.astype(F32)
    return [jnp.concatenate([own_lanes(keys, head).astype(BF16), mask], axis=1) for head in (0, 1)]


def extended_query(query):
    lanes = lax.broadcasted_iota(jnp.int32, query.shape, 1)
    return jnp.concatenate([query, jnp.where(lanes == 0, 1.0, 0.0).astype(BF16)], axis=1)


def fill_diagonal(diagonal):
    keys = lax.broadcasted_iota(jnp.int32, diagonal.shape, 0)
    queries = lax.broadcasted_iota(jnp.int32, diagonal.shape, 1)
    diagonal[...] = jnp.where(keys <= queries, 0.0, MASKED_SCORE)


def key_ranges(block, keys, causal):
    if not causal:
        return [(0, keys)]
    return [(low, low + QUERY_BLOCK) for low in range(0, (block + 1) * QUERY_BLOCK, QUERY_BLOCK)]


def attend_unit(query, keys, values, length, causal, diagonal, lse_ref):
    rows, count = query.shape[0], keys.shape[0]
    values_t = jnp.transpose(values.astype(F32)).astype(BF16)
    wide_keys, wide_query = extended_keys(keys, length), extended_query(query)
    items = [(head, block) for block in range(rows // QUERY_BLOCK) for head in (0, 1)]
    scores, probs, totals, mixed = {}, {}, {}, {}
    for head, block in items:
        part = wide_query[block * QUERY_BLOCK : (block + 1) * QUERY_BLOCK]
        ranges = key_ranges(block, count, causal)
        scores[head, block] = [dot_nt(wide_keys[head][a:b], part) for a, b in ranges]
        if causal:
            scores[head, block][-1] = scores[head, block][-1] + diagonal[...]
    for head, block in items:
        pieces = scores[head, block]
        peak = functools.reduce(jnp.maximum, [jnp.max(p, axis=0, keepdims=True) for p in pieces])
        terms = [jnp.exp(p - peak) for p in pieces]
        total = sum(jnp.sum(t, axis=0, keepdims=True) for t in terms)
        at = slice(block * QUERY_BLOCK, (block + 1) * QUERY_BLOCK)
        lse_ref[head : head + 1, at] = peak + jnp.log(total)
        totals[head, block] = total
        probs[head, block] = jnp.concatenate([t.astype(BF16) for t in terms], axis=0)
    for head, block in items:
        own = values_t[head * HEAD_DIM : (head + 1) * HEAD_DIM, : probs[head, block].shape[0]]
        mixed[head, block] = dot(own, probs[head, block]) / totals[head, block]
    out = [
        jnp.transpose(jnp.concatenate([mixed[0, block], mixed[1, block]], axis=0))
        for block in range(rows // QUERY_BLOCK)
    ]
    return jnp.concatenate(out, axis=0).astype(BF16)


def attend_back_unit(query, keys, values, attended, grad, length, causal, diagonal, lse_ref):
    rows, count = query.shape[0], keys.shape[0]
    blocks = range(rows // QUERY_BLOCK)
    query_f, keys_f, grad_f = (a.astype(F32) for a in (query, keys, grad))
    wide_keys, wide_query = extended_keys(keys, length), extended_query(query)
    delta = jnp.transpose(grad_f * attended.astype(F32))
    deltas = [
        jnp.sum(delta[head * HEAD_DIM : (head + 1) * HEAD_DIM], axis=0, keepdims=True)
        for head in (0, 1)
    ]
    keys_t = jnp.transpose(keys_f).astype(BF16)
    query_own = [own_lanes(query_f, head).astype(BF16) for head in (0, 1)]
    grad_own = [own_lanes(grad_f, head).astype(BF16) for head in (0, 1)]
    items = [(head, block) for block in blocks for head in (0, 1)]
    scores, slopes, probs, back, grad_query = {}, {}, {}, {}, {}
    for head, block in items:
        at = slice(block * QUERY_BLOCK, (block + 1) * QUERY_BLOCK)
        for a, b in key_ranges(block, count, causal):
            scores[head, block, a] = dot_nt(wide_keys[head][a:b], wide_query[at])
            slopes[head, block, a] = dot_nt(values[a:b], grad_own[head][at])
    for head, block in items:
        at = slice(block * QUERY_BLOCK, (block + 1) * QUERY_BLOCK)
        ranges = key_ranges(block, count, causal)
        for a, b in ranges:
            score = scores[head, block, a]
            if causal and (a, b) == ranges[-1]:
                score = score + diagonal[...]
            prob = jnp.exp(score - lse_ref[head : head + 1, at])
            probs[head, block, a] = prob.astype(BF16)
            back[head, block, a] = (prob * (slopes[head, block, a] - deltas[head][:, at])).astype(BF16)
    for head, block in items:
        own = keys_t[head * HEAD_DIM : (head + 1) * HEAD_DIM]
        grad_query[head, block] = sum(
            dot(own[:, a:b], back[head, block, a]) for a, b in key_ranges(block, count, causal)
        )
    grad_keys, grad_values = [], []
    for low in sorted({key[2] for key in back}):
        live = [key for key in back if key[2] == low]
        at = [slice(block * QUERY_BLOCK, (block + 1) * QUERY_BLOCK) for _, block, _ in live]
        grad_values.append(
            dot(
                jnp.concatenate([probs[key] for key in live], axis=1),
                jnp.concatenate([grad_own[key[0]][a] for key, a in zip(live, at)], axis=0),
            )
        )
        grad_keys.append(
            dot(
                jnp.concatenate([back[key] for key in live], axis=1),
                jnp.concatenate([query_own[key[0]][a] for key, a in zip(live, at)], axis=0),
            )
        )
    grad_query = [
        jnp.transpose(jnp.concatenate([grad_query[0, block], grad_query[1, block]], axis=0)) * SCORE_SCALE
        for block in blocks
    ]
    return tuple(
        jnp.concatenate(parts, axis=0).astype(BF16) for parts in (grad_query, grad_keys, grad_values)
    )


def norm_chunk(hidden, gain, bias):
    center = hidden - jnp.mean(hidden, axis=-1, keepdims=True)
    inverse = lax.rsqrt(jnp.mean(center * center, axis=-1, keepdims=True) + NORM_EPSILON)
    normed = center * inverse
    return normed * gain + bias, normed, inverse


def norm_back_chunk(gradient, normed, inverse, gain):
    scaled = gradient * gain
    return inverse * (
        scaled
        - jnp.mean(scaled, axis=-1, keepdims=True)
        - normed * jnp.mean(scaled * normed, axis=-1, keepdims=True)
    )


def fold_rows(values):
    return jnp.sum(values.reshape(values.shape[0] // 8, 8, values.shape[1]), axis=0)


def each_chunk(rows, body, results):
    def step(index, carry):
        at = pl.ds(pl.multiple_of(index * ROW_CHUNK, ROW_CHUNK), ROW_CHUNK)
        body(at)
        for buffer, out, sem in results:
            copy_of(buffer.at[at, :], out.at[at, :], sem).start()
        return carry

    lax.fori_loop(0, rows // ROW_CHUNK, step, 0)
    return [copy_of(*result) for result in results]


def store_shards(target, weight, dp):
    for block in range(8):
        target[shard_of(block ^ dp)] = weight[block * UNIT : (block + 1) * UNIT]


SMEM = pl.BlockSpec(memory_space=pltpu.SMEM)
VMEM = pl.BlockSpec(memory_space=pltpu.VMEM)
ANY = pl.BlockSpec(memory_space=pl.ANY)


def params(limit=62):
    return pltpu.CompilerParams(vmem_limit_bytes=limit * 1024 * 1024)


def cost_of(microseconds):
    return pl.CostEstimate(flops=int(microseconds * 1.1e9), bytes_accessed=4 << 20, transcendentals=0)


def sds(shape, dtype):
    return jax.ShapeDtypeStruct(shape, dtype)


def position():
    dp = lax.axis_index("dp")
    return dp & 3, dp, (dp >> 1) & 1


def weight_copies(pieces, wbuf, obuf, wsem, osem, columns=(0, 1, 2)):
    groups, outs = [[], [], []], []
    wide = 2 * UNIT
    order, _, inner = position()
    for index, refs in enumerate(pieces):
        at = slice(index * wide, (index + 1) * wide)
        if len(refs[-1].shape) == 2:
            column = 0
            for ref in refs[:-1]:
                for source in [ref] if len(ref.shape) == 2 else [ref.at[c] for c in range(ref.shape[0])]:
                    if column in columns:
                        low = (columns.index(column) * len(pieces) + index) * wide
                        groups[column].append(copy_of(source, wbuf.at[:, low : low + wide], wsem.at[column, index, 0]))
                    column += 1
            if obuf is not None:
                outs.append(copy_of(refs[-1], obuf.at[at, :], osem.at[index, 0]))
            continue
        parts = [refs[0].at[n] for n in range(refs[0].shape[0])] if len(refs[0].shape) == 4 else refs
        rows = parts[0].shape[1]
        part = wide // len(parts)
        for quarter, ref in enumerate(parts):
            place = quarter ^ (order if len(parts) == 4 else inner)
            for column in columns:
                low = (columns.index(column) * len(pieces) + index) * wide
                groups[column].append(
                    copy_of(
                        ref.at[column],
                        wbuf.at[pl.ds(pl.multiple_of(place * rows, rows), rows), low : low + wide],
                        wsem.at[column, index, quarter],
                    )
                )
            for block in range(4 if obuf is not None else 0):
                outs.append(
                    copy_of(
                        ref.at[3, block * part : (block + 1) * part, :],
                        obuf.at[pl.ds(pl.multiple_of(index * wide + place * part, part), part), block * wide : (block + 1) * wide],
                        osem.at[index, 4 * quarter + block],
                    )
                )
    return groups, outs


def attention_fwd_call(lengths, residual, others, pieces, partial, norm):
    rows, depth = others[0].shape
    causal = len(others) == 1
    number, wide = 2 * len(pieces), 2 * len(pieces) * UNIT
    last, has_partial = norm is not None, partial is not None

    def kernel(*refs):
        it = iter(refs)
        len_ref = next(it)
        in_refs = [next(it) for _ in others]
        gain_ref, bias_ref = (next(it), next(it)) if last else (None, None)
        old_rows = [next(it) for _ in residual[1:]] if last else []
        res_in = next(it) if last else None
        part_in = next(it) if has_partial else None
        w_refs = [[next(it) for _ in piece] for piece in pieces]
        unit_outs, lse_ref = [next(it) for _ in range(4)], next(it)
        if last:
            norm_outs = [next(it) for _ in range(3)]
        else:
            sum_ref = next(it)
        wbuf, obuf, att_all, diagonal, wsem, osem, lsem, usem = (next(it) for _ in range(8))
        q_ref, k_ref, v_ref, att_ref = (next(it) for _ in range(4))
        if last:
            acc, old, low_ref, hat_ref, inv_ref = (next(it) for _ in range(5))
        length = len_ref[0, lax.axis_index("tensor")]
        groups, outs = weight_copies(w_refs, wbuf, obuf, wsem, osem)
        for copies in groups + [outs]:
            for copy in copies:
                copy.start()
        target = acc if last else sum_ref
        late = []
        if has_partial:
            late.append(copy_of(part_in, target, lsem.at[0]))
        if last:
            late.append(copy_of(res_in, old, lsem.at[1]))
        for copy in late:
            copy.start()
        if causal:
            fill_diagonal(diagonal)
        for c, result in enumerate((q_ref, k_ref, v_ref)):
            for copy in groups[c]:
                copy.wait()
            rows_in = in_refs[0] if causal or c == 0 else in_refs[1]
            proj = dot(rows_in[...], wbuf[:, c * wide : (c + 1) * wide]).astype(BF16)
            if c == 0:
                proj = (proj.astype(F32) * SCORE_SCALE).astype(BF16)
            for index in range(number):
                result[index] = proj[:, index * UNIT : (index + 1) * UNIT]

        flushes = [copy_of(*pair, usem.at[index]) for index, pair in enumerate(zip((q_ref, k_ref, v_ref, att_ref), unit_outs))]
        for copy in flushes[:3]:
            copy.start()

        def step(first, carry):
            for u in [first * 4 + inner for inner in range(4)]:
                attended = attend_unit(q_ref[u], k_ref[u], v_ref[u], length, causal, diagonal, lse_ref.at[u])
                att_ref[u] = attended
                att_all[:, pl.ds(pl.multiple_of(u * UNIT, UNIT), UNIT)] = attended
            return carry

        lax.fori_loop(0, number // 4, step, 0)
        flushes[3].start()
        for copy in outs + late:
            copy.wait()
        if has_partial:
            target[...] += dot(att_all[...], obuf[...])
        else:
            target[...] = dot(att_all[...], obuf[...])
        if last:
            def chunk(at):
                before = old[at, :].astype(F32)
                if old_rows:
                    before = before * old_rows[0][...] + old_rows[1][...]
                normed, hat, inverse = norm_chunk(RESIDUAL_ALPHA * before + acc[at, :], gain_ref[...], bias_ref[...])
                low_ref[at, :] = normed.astype(BF16)
                hat_ref[at, :] = hat
                inv_ref[at, :] = jnp.broadcast_to(inverse, (ROW_CHUNK, 128))

            triples = zip((low_ref, hat_ref, inv_ref), norm_outs)
            flushes += each_chunk(rows, chunk, [(*pair, usem.at[4 + index]) for index, pair in enumerate(triples)])
        for copy in flushes:
            copy.wait()

    unit_rows = sds((number, rows, UNIT), BF16)
    shapes = [unit_rows] * 4 + [sds((number, 2, rows), F32)]
    if last:
        shapes += [sds((rows, depth), BF16), sds((rows, depth), F32), sds((rows, 128), F32)]
    else:
        shapes += [sds((rows, depth), F32)]
    args = [lengths, *others]
    if last:
        args += [*norm, *residual[1:]]
    tail = ([residual[0]] if last else []) + ([partial] if has_partial else [])
    tail += [array for piece in pieces for array in piece]
    scratch = [
        pltpu.VMEM((depth, 3 * wide), BF16),
        pltpu.VMEM((wide, depth), BF16),
        pltpu.VMEM((rows, wide), BF16),
        pltpu.VMEM((QUERY_BLOCK, QUERY_BLOCK), F32),
        pltpu.SemaphoreType.DMA((3, len(pieces), 4)),
        pltpu.SemaphoreType.DMA((len(pieces), 16)),
        pltpu.SemaphoreType.DMA((2,)),
        pltpu.SemaphoreType.DMA((7,)),
    ]
    scratch += [pltpu.VMEM((number, rows, UNIT), BF16)] * 4
    if last:
        scratch += [pltpu.VMEM((rows, depth), F32), pltpu.VMEM((rows, depth), residual[0].dtype)]
        scratch += [pltpu.VMEM((rows, depth), BF16), pltpu.VMEM((rows, depth), F32), pltpu.VMEM((rows, 128), F32)]
    return pl.pallas_call(
        kernel,
        out_shape=shapes,
        in_specs=[SMEM] + [VMEM] * (len(args) - 1) + [ANY] * len(tail),
        out_specs=[ANY] * 4 + [VMEM] + ([ANY] * 3 if last else [VMEM]),
        scratch_shapes=scratch,
        compiler_params=params(),
        cost_estimate=cost_of(0.6 * number),
        name="self_fwd" if causal else "cross_fwd",
    )(*args, *tail)


def attention_bwd_call(lengths, grad_low, others, pieces, saved, plan, carried, norm, results=1):
    rows, depth = grad_low.shape
    causal = len(others) == 1
    number, n_in, wide = len(plan), len(others), len(plan) * UNIT
    last = norm is not None
    skip = 1 if last else 0

    def kernel(*refs):
        it = iter(refs)
        len_ref = next(it)
        h_ref = next(it)
        in_refs = [next(it) for _ in range(n_in)]
        gain_ref = next(it) if last else None
        late_in = [next(it), next(it)] if last else []
        acc_in = next(it) if last else None
        w_refs = [[next(it) for _ in piece] for piece in pieces]
        s_refs = [[next(it) for _ in call] for call in saved]
        if last:
            low_ref, scaled_ref, gsum_ref, bsum_ref = (next(it) for _ in range(4))
        dall_ref = next(it)
        g_refs = [next(it) for _ in range(results)]
        wbuf, obuf, sbuf, lbuf, att_all, grad_all = (next(it) for _ in range(6))
        stage, diagonal = next(it), next(it)
        if last:
            dquery, acc, hat, inv, low_buf, scaled_buf, nsem = (next(it) for _ in range(7))
        wsem, osem, ssem, gsem, lsem = (next(it) for _ in range(5))
        length, dp = len_ref[0, lax.axis_index("tensor")], lax.axis_index("dp")

        groups, o_copies = weight_copies(w_refs, wbuf, obuf, wsem, osem, (0,) if last else ())
        for copy in o_copies:
            copy.start()
        s_copies = []
        for index, unit in enumerate(plan):
            lanes = slice(index * UNIT, (index + 1) * UNIT)
            call = s_refs[unit[0]]
            for c in range(3):
                s_copies.append(copy_of(call[c].at[unit[1]], sbuf.at[index, c], ssem.at[c, index]))
            s_copies.append(copy_of(call[3].at[unit[1]], att_all.at[:, lanes], ssem.at[3, index]))
            s_copies.append(copy_of(call[4].at[unit[1]], lbuf.at[index], ssem.at[4, index]))
        late = []
        if last:
            late = groups[0] + [
                copy_of(source, target, lsem.at[index])
                for index, (source, target) in enumerate(((acc_in, acc), (late_in[0], hat), (late_in[1], inv)))
            ]
        for copy in s_copies + late:
            copy.start()
        if causal:
            fill_diagonal(diagonal)
        for copy in o_copies:
            copy.wait()
        grad_att = dot_nt(h_ref[...], obuf[...]).astype(BF16)
        for index in range(number):
            grad_all[index] = grad_att[:, index * UNIT : (index + 1) * UNIT]
        for copy in s_copies:
            copy.wait()

        def step(first, carry):
            units = [first * 2, first * 2 + 1]
            ats = [pl.ds(pl.multiple_of(u * UNIT, UNIT), UNIT) for u in units]
            parts = [
                attend_back_unit(
                    sbuf[u, 0], sbuf[u, 1], sbuf[u, 2], att_all[:, at], grad_all[u], length, causal, diagonal, lbuf.at[u]
                )
                for u, at in zip(units, ats)
            ]
            for u, at, part in zip(units, ats, parts):
                if last:
                    dquery[:, at] = part[0]
                for c in range(skip, 3):
                    dall_ref[:, pl.ds(pl.multiple_of((c - skip) * wide + u * UNIT, UNIT), UNIT)] = part[c]
            return carry

        lax.fori_loop(0, number // 2, step, 0)
        share = number // 2 // results

        def keep(rows_in, source, column):
            weight = dot_tn(rows_in[...], source).astype(BF16)
            for index in range(number):
                piece = index // 2
                target = stage.at[piece // share, (index % 2) * 4 + column, piece % share]
                store_shards(target, weight[:, index * UNIT : (index + 1) * UNIT], dp)

        if last:
            keep(in_refs[0], dquery[...], 0)
        for c in range(skip, 3):
            keep(in_refs[-1], dall_ref[:, (c - skip) * wide : (c - skip + 1) * wide], c)
        keep(h_ref, att_all[...], 3)
        g_copies = [copy_of(stage.at[index], ref, gsem.at[index]) for index, ref in enumerate(g_refs)]
        for copy in g_copies:
            copy.start()
        for copy in late:
            copy.wait()
        if last:
            acc[...] += dot_nt(dquery[...], wbuf[...])
            g_copies += norm_back_rows(
                acc, hat, inv, gain_ref, low_buf, scaled_buf, (low_ref, scaled_ref), nsem, gsum_ref, bsum_ref, rows
            )
        for copy in g_copies:
            copy.wait()

    big = sds((rows, depth), F32)
    shapes = []
    if last:
        shapes += [sds((rows, depth), BF16), big, sds((8, depth), F32), sds((8, depth), F32)]
    shapes.append(sds((rows, (3 - skip) * wide), BF16))
    specs_out = ([ANY] * 2 + [VMEM] * 3 if last else [VMEM]) + [ANY] * results
    shapes += [sds((8, number // 2 // results, 8, UNIT, UNIT), BF16)] * results
    args = [lengths, grad_low, *others] + ([norm[2]] if last else [])
    tail = [norm[0], norm[1], carried] if last else []
    tail += [array for piece in pieces for array in piece]
    for call in saved:
        tail += call
    scratch = [
        pltpu.VMEM((depth, wide) if last else (16, 128), BF16),
        pltpu.VMEM((wide, depth), BF16),
        pltpu.VMEM((number, 3, rows, UNIT), BF16),
        pltpu.VMEM((number, 2, rows), F32),
        pltpu.VMEM((rows, wide), BF16),
        pltpu.VMEM((number, rows, UNIT), BF16),
        pltpu.VMEM((results, 8, number // 2 // results, 8, UNIT, UNIT), BF16),
        pltpu.VMEM((QUERY_BLOCK, QUERY_BLOCK), F32),
    ]
    if last:
        scratch += [pltpu.VMEM((rows, wide), BF16), pltpu.VMEM((rows, depth), F32), pltpu.VMEM((rows, depth), F32), pltpu.VMEM((rows, 128), F32)]
        scratch += [pltpu.VMEM((rows, depth), BF16), pltpu.VMEM((rows, depth), F32), pltpu.SemaphoreType.DMA((2,))]
    scratch += [
        pltpu.SemaphoreType.DMA((3, len(pieces), 4)),
        pltpu.SemaphoreType.DMA((len(pieces), 16)),
        pltpu.SemaphoreType.DMA((5, number)),
        pltpu.SemaphoreType.DMA((results,)),
        pltpu.SemaphoreType.DMA((4,)),
    ]
    return pl.pallas_call(
        kernel,
        out_shape=shapes,
        in_specs=[SMEM] + [VMEM] * (len(args) - 1) + [ANY] * len(tail),
        out_specs=specs_out,
        scratch_shapes=scratch,
        compiler_params=params(),
        cost_estimate=cost_of(4.2 * number),
        name="self_bwd" if causal else "cross_bwd",
    )(*args, *tail)


def inputs_back_call(base, parts, columns):
    rows, depth = parts[0][0].shape[0], parts[0][1][0][0].shape[-2]

    def kernel(*refs):
        it = iter(refs)
        base_ref = next(it) if base is not None else None
        grads = [next(it) for _ in parts]
        w_refs = [[[next(it) for _ in piece] for piece in pieces] for _, pieces in parts]
        out = next(it)
        bufs, sems = [next(it) for _ in parts], [next(it) for _ in parts]
        copies = []
        for index in range(len(parts)):
            groups, _ = weight_copies(w_refs[index], bufs[index], None, sems[index], None, columns)
            copies.append([copy for group in groups for copy in group])
            for copy in copies[-1]:
                copy.start()
        if base is not None:
            out[...] = base_ref[...]
        for index in range(len(parts)):
            for copy in copies[index]:
                copy.wait()
            if index or base is not None:
                out[...] += dot_nt(grads[index][...], bufs[index][...])
            else:
                out[...] = dot_nt(grads[index][...], bufs[index][...])

    args = ([base] if base is not None else []) + [grad for grad, _ in parts]
    tail = [array for _, pieces in parts for piece in pieces for array in piece]
    return pl.pallas_call(
        kernel,
        out_shape=sds((rows, depth), F32),
        in_specs=[VMEM] * len(args) + [ANY] * len(tail),
        out_specs=VMEM,
        scratch_shapes=[pltpu.VMEM((depth, grad.shape[1]), BF16) for grad, _ in parts]
        + [pltpu.SemaphoreType.DMA((3, len(pieces), 4)) for _, pieces in parts],
        compiler_params=params(),
        cost_estimate=cost_of(7),
        name="inputs_back",
    )(*args, *tail)


def norm_back_rows(acc, hat, inv, gain_ref, low_buf, scaled_buf, outs, sems, gsum_ref, bsum_ref, rows):
    gsum_ref[...] = jnp.zeros_like(gsum_ref)
    bsum_ref[...] = jnp.zeros_like(bsum_ref)

    def chunk(at):
        gradient, normed = acc[at, :], hat[at, :]
        grad_in = norm_back_chunk(gradient, normed, inv[at, :1], gain_ref[...])
        low_buf[at, :] = grad_in.astype(BF16)
        scaled_buf[at, :] = RESIDUAL_ALPHA * grad_in
        gsum_ref[...] += fold_rows(gradient * normed)
        bsum_ref[...] += fold_rows(gradient)

    pairs = zip((low_buf, scaled_buf), outs)
    return each_chunk(rows, chunk, [(*pair, sems.at[index]) for index, pair in enumerate(pairs)])


GELU_SCALE = 0.7978845608028654
GELU_CUBE = 0.044715


def gelu_and_slope(pre):
    square = pre * pre
    inner = pre * (GELU_SCALE + (GELU_SCALE * GELU_CUBE) * square)
    curve = jnp.tanh(inner)
    half = 0.5 + 0.5 * curve
    slope = half * (1.0 + pre * (1.0 - curve) * (GELU_SCALE + (3.0 * GELU_SCALE * GELU_CUBE) * square))
    return pre * half, slope


FFN_PART = FFN_UNIT // 2


def ffn_copies(pieces, ubuf, dbuf, usem, dsem):
    ups, downs = [], []
    order, _, _ = position()
    for index, refs in enumerate(pieces):
        wide = 2 * FFN_UNIT
        at = slice(index * wide, (index + 1) * wide)
        if len(refs) == 2:
            ups.append([copy_of(refs[0], ubuf.at[:, at], usem.at[index, 0])])
            downs.append([copy_of(refs[1], dbuf.at[at, :], dsem.at[index, 0])])
            continue
        ups.append([])
        downs.append([])
        rows = refs[0].shape[1]
        for quarter in range(4):
            up = refs[quarter].at[0]
            down = refs[quarter].at[1] if quarter < 3 else refs[4].at[0]
            place = (quarter ^ order) * rows
            ups[-1].append(copy_of(up, ubuf.at[pl.ds(pl.multiple_of(place, rows), rows), at], usem.at[index, quarter]))
            downs[-1].append(
                copy_of(down, dbuf.at[pl.ds(pl.multiple_of(index * wide + place, rows), rows), :], dsem.at[index, quarter])
            )
    return ups, downs


def ffn_fwd_call(inputs, pieces, partial, final):
    rows, depth = inputs.shape
    number = 2 * len(pieces)
    last, has_partial = final is not None, partial is not None

    def kernel(*refs):
        it = iter(refs)
        x_ref = next(it)
        if last:
            gain_old, bias_old, gain_ref, bias_ref = (next(it) for _ in range(4))
            late_in = [next(it), next(it)]
        part_in = next(it) if has_partial else None
        w_refs = [[next(it) for _ in piece] for piece in pieces]
        if last:
            norm_outs = [next(it) for _ in range(3)]
            gsum_ref, bsum_ref = next(it), next(it)
        else:
            sum_ref = next(it)
        act_ref, slope_ref = next(it), next(it)
        ubuf, dbuf, abuf, sbuf, pbuf, psem = (next(it) for _ in range(6))
        if last:
            acc, hat, cot, lsem, out_ref, low_ref, scaled_ref, nsem = (next(it) for _ in range(8))
        wsem, gsem = next(it), next(it)
        target = acc if last else sum_ref

        up_copies, down_copies = ffn_copies(w_refs, ubuf, dbuf, wsem.at[0], wsem.at[1])
        for copies in up_copies + down_copies:
            for copy in copies:
                copy.start()
        if has_partial:
            part_copy = copy_of(part_in, target, psem)
            part_copy.start()
        if last:
            late = [copy_of(late_in[0], hat, lsem.at[0]), copy_of(late_in[1], cot, lsem.at[1])]
            for copy in late:
                copy.start()
        saves = []

        def gate(pre, index):
            activated, slope = gelu_and_slope(pre)
            abuf[:, index * FFN_UNIT : (index + 1) * FFN_UNIT] = activated.astype(BF16)
            sbuf[:, index * FFN_UNIT : (index + 1) * FFN_UNIT] = slope.astype(BF16)

        for index in range(number):
            if index % 2 == 0:
                for copy in up_copies[index // 2]:
                    copy.wait()
            if index:
                gate(pbuf[(index - 1) % 2], index - 1)
            pbuf[index % 2] = dot(x_ref[...], ubuf[:, index * FFN_UNIT : (index + 1) * FFN_UNIT])
        gate(pbuf[(number - 1) % 2], number - 1)
        for index in range(number):
            at = slice(index * FFN_UNIT, (index + 1) * FFN_UNIT)
            saves += [
                copy_of(abuf.at[:, at], act_ref.at[index], gsem.at[0, index]),
                copy_of(sbuf.at[:, at], slope_ref.at[index], gsem.at[1, index]),
            ]
        for copy in saves:
            copy.start()
        for copies in down_copies:
            for copy in copies:
                copy.wait()
        if has_partial:
            part_copy.wait()
            target[...] += dot(abuf[...], dbuf[...])
        else:
            target[...] = dot(abuf[...], dbuf[...])
        if last:
            for copy in late:
                copy.wait()
            gsum_ref[...] = jnp.zeros_like(gsum_ref)
            bsum_ref[...] = jnp.zeros_like(bsum_ref)

            def chunk(at):
                old = hat[at, :] * gain_old[...] + bias_old[...]
                normed, xhat, inverse = norm_chunk(RESIDUAL_ALPHA * old + acc[at, :], gain_ref[...], bias_ref[...])
                out_ref[at, :] = normed.astype(BF16)
                gradient = cot[at, :].astype(F32)
                grad_in = norm_back_chunk(gradient, xhat, inverse, gain_ref[...])
                low_ref[at, :] = grad_in.astype(BF16)
                scaled_ref[at, :] = RESIDUAL_ALPHA * grad_in
                gsum_ref[...] += fold_rows(gradient * xhat)
                bsum_ref[...] += fold_rows(gradient)

            triples = zip((out_ref, low_ref, scaled_ref), norm_outs)
            saves += each_chunk(rows, chunk, [(*pair, nsem.at[index]) for index, pair in enumerate(triples)])
        for copy in saves:
            copy.wait()

    big, low = sds((rows, depth), F32), sds((rows, depth), BF16)
    if last:
        shapes = [low, low, big, sds((8, depth), F32), sds((8, depth), F32)]
    else:
        shapes = [big]
    specs_out = ([ANY] * 3 + [VMEM] * 2 if last else [VMEM]) + [ANY, ANY]
    shapes += [sds((number, rows, FFN_UNIT), BF16)] * 2
    args = [inputs]
    if last:
        args += [final[1], final[2], final[4], final[5]]
    specs = [VMEM] * len(args)
    tail = ([final[0], final[3]] if last else []) + ([partial] if has_partial else []) + [array for piece in pieces for array in piece]
    scratch = [
        pltpu.VMEM((depth, number * FFN_UNIT), BF16),
        pltpu.VMEM((number * FFN_UNIT, depth), BF16),
        pltpu.VMEM((rows, number * FFN_UNIT), BF16),
        pltpu.VMEM((rows, number * FFN_UNIT), BF16),
        pltpu.VMEM((2, rows, FFN_UNIT), F32),
        pltpu.SemaphoreType.DMA,
    ]
    if last:
        scratch += [
            pltpu.VMEM((rows, depth), F32),
            pltpu.VMEM((rows, depth), F32),
            pltpu.VMEM((rows, depth), BF16),
            pltpu.SemaphoreType.DMA((2,)),
            pltpu.VMEM((rows, depth), BF16),
            pltpu.VMEM((rows, depth), BF16),
            pltpu.VMEM((rows, depth), F32),
            pltpu.SemaphoreType.DMA((3,)),
        ]
    scratch += [pltpu.SemaphoreType.DMA((2, len(pieces), 4)), pltpu.SemaphoreType.DMA((2, number))]
    return pl.pallas_call(
        kernel,
        out_shape=shapes,
        in_specs=specs + [ANY] * len(tail),
        out_specs=specs_out,
        scratch_shapes=scratch,
        compiler_params=params(),
        cost_estimate=cost_of(12),
        name="ffn_fwd",
    )(*args, *tail)


def ffn_bwd_call(grad_low, inputs, pieces, saved, plan, carried, norm):
    rows, depth = inputs.shape
    number = len(plan)
    last = norm is not None

    def kernel(*refs):
        it = iter(refs)
        g_in, x_ref = next(it), next(it)
        gain_ref = next(it) if last else None
        late_in = [next(it), next(it)] if last else []
        acc_in = next(it)
        w_refs = [[next(it) for _ in piece] for piece in pieces]
        s_refs = [[next(it) for _ in call] for call in saved]
        if last:
            low_ref, scaled_ref, gsum_ref, bsum_ref = (next(it) for _ in range(4))
        else:
            sum_ref = next(it)
        g_ref = next(it)
        ubuf, dbuf, abuf, sbuf, gbuf, stage, psem = (next(it) for _ in range(7))
        if last:
            acc, hat, inv, lsem, low_buf, scaled_buf, nsem = (next(it) for _ in range(7))
        wsem, ssem, gsem = next(it), next(it), next(it)
        dp = lax.axis_index("dp")
        target = acc if last else sum_ref

        ups, downs = ffn_copies(w_refs, ubuf, dbuf, wsem.at[0], wsem.at[1])
        slopes, acts = [], []
        for index, (call, at) in enumerate(plan):
            lanes = slice(index * FFN_UNIT, (index + 1) * FFN_UNIT)
            slopes.append(copy_of(s_refs[call][1].at[at], sbuf.at[index], ssem.at[0, index]))
            acts.append(copy_of(s_refs[call][0].at[at], abuf.at[:, lanes], ssem.at[1, index]))
        for copies in downs + [slopes, acts] + ups:
            for copy in copies:
                copy.start()
        part_copy = copy_of(acc_in, target, psem)
        part_copy.start()
        if last:
            late = [copy_of(late_in[0], hat, lsem.at[0]), copy_of(late_in[1], inv, lsem.at[1])]
            for copy in late:
                copy.start()
        for index in range(number):
            if index % 2 == 0:
                for copy in downs[index // 2]:
                    copy.wait()
            slopes[index].wait()
            grad_act = dot_nt(g_in[...], dbuf[index * FFN_UNIT : (index + 1) * FFN_UNIT, :]) * sbuf[index].astype(F32)
            gbuf[:, index * FFN_UNIT : (index + 1) * FFN_UNIT] = grad_act.astype(BF16)
        for copy in acts:
            copy.wait()

        def keep(rows_in, source, column):
            for half in range(number // 2):
                wide = 2 * FFN_UNIT
                weight = dot_tn(rows_in[...], source[:, half * wide : (half + 1) * wide]).astype(BF16)
                for inner in range(4):
                    part = weight[:, inner * FFN_PART : (inner + 1) * FFN_PART]
                    store_shards(stage.at[2 * inner + column, half], part, dp)

        keep(x_ref, gbuf, 0)
        keep(g_in, abuf, 1)
        g_copies = [copy_of(stage, g_ref, gsem)]
        for copy in g_copies:
            copy.start()
        for copies in ups:
            for copy in copies:
                copy.wait()
        part_copy.wait()
        target[...] += dot_nt(gbuf[...], ubuf[...])
        if last:
            for copy in late:
                copy.wait()
            g_copies += norm_back_rows(
                acc, hat, inv, gain_ref, low_buf, scaled_buf, (low_ref, scaled_ref), nsem, gsum_ref, bsum_ref, rows
            )
        for copy in g_copies:
            copy.wait()

    big, low = sds((rows, depth), F32), sds((rows, depth), BF16)
    shapes = [low, big, sds((8, depth), F32), sds((8, depth), F32)] if last else [big]
    specs_out = ([ANY] * 2 + [VMEM] * 2 if last else [VMEM]) + [ANY]
    shapes.append(sds((8, number // 2, 8, UNIT, FFN_PART), BF16))
    args = [grad_low, inputs] + ([norm[2]] if last else [])
    specs = [VMEM] * len(args)
    tail = ([norm[0], norm[1]] if last else []) + [carried] + [array for piece in pieces for array in piece]
    for call in saved:
        tail += call
    scratch = [
        pltpu.VMEM((depth, number * FFN_UNIT), BF16),
        pltpu.VMEM((number * FFN_UNIT, depth), BF16),
        pltpu.VMEM((rows, number * FFN_UNIT), BF16),
        pltpu.VMEM((number, rows, FFN_UNIT), BF16),
        pltpu.VMEM((rows, number * FFN_UNIT), BF16),
        pltpu.VMEM((8, number // 2, 8, UNIT, FFN_PART), BF16),
        pltpu.SemaphoreType.DMA,
    ]
    if last:
        scratch += [
            pltpu.VMEM((rows, depth), F32),
            pltpu.VMEM((rows, depth), F32),
            pltpu.VMEM((rows, 128), F32),
            pltpu.SemaphoreType.DMA((2,)),
            pltpu.VMEM((rows, depth), BF16),
            pltpu.VMEM((rows, depth), F32),
            pltpu.SemaphoreType.DMA((2,)),
        ]
    scratch += [pltpu.SemaphoreType.DMA((2, len(pieces), 4)), pltpu.SemaphoreType.DMA((2, number)), pltpu.SemaphoreType.DMA]
    return pl.pallas_call(
        kernel,
        out_shape=shapes,
        in_specs=specs + [ANY] * len(tail),
        out_specs=specs_out,
        scratch_shapes=scratch,
        compiler_params=params(),
        cost_estimate=cost_of(17),
        name="ffn_bwd",
    )(*args, *tail)


def combine(jobs, shapes):
    arrays = []
    for terms, _, _, _ in jobs:
        for array, _ in terms:
            if not any(array is known for known in arrays):
                arrays.append(array)
    position = {id(array): index for index, array in enumerate(arrays)}

    def part_shape(array, index):
        kept = []
        for extent, at in zip(array.shape, index + (slice(None),) * (array.ndim - len(index))):
            if isinstance(at, slice):
                kept.append(len(range(*at.indices(extent))))
        return tuple(kept)

    part_shapes = [part_shape(*terms[0]) for terms, _, _, _ in jobs]
    count = sum(len(terms) for terms, _, _, _ in jobs)

    def kernel(*refs):
        ins, outs = refs[: len(arrays)], refs[len(arrays) : len(arrays) + len(shapes)]
        rest = refs[len(arrays) + len(shapes) :]
        term_bufs, sum_bufs, isem, osem = rest[:count], rest[count : count + len(jobs)], rest[-2], rest[-1]
        loads, number = [], 0
        for terms, _, _, _ in jobs:
            loads.append([])
            for array, index in terms:
                loads[-1].append(copy_of(ins[position[id(array)]].at[index], term_bufs[number], isem.at[number]))
                number += 1
        for group in loads:
            for copy in group:
                copy.start()
        stores, number = [], 0
        for job, (terms, out, place, kind) in enumerate(jobs):
            for copy in loads[job]:
                copy.wait()
            bufs = term_bufs[number : number + len(terms)]
            number += len(terms)
            lead = part_shapes[job][:-2]
            size = 1
            for extent in lead:
                size *= extent

            def one(flat, carry, bufs=bufs, lead=lead, target=sum_bufs[job]):
                index, left = [], flat
                for extent in reversed(lead):
                    index.append(lax.rem(left, extent))
                    left = lax.div(left, extent)
                index = tuple(reversed(index))
                total = bufs[0][index].astype(F32)
                for buf in bufs[1:]:
                    total = total + buf[index].astype(F32)
                target[index] = total.astype(target.dtype)
                return carry

            if kind == "range":
                lax.fori_loop(0, size, one, 0)
            else:
                total = bufs[0][0].astype(F32)
                for buf in bufs[1:]:
                    total = total + buf[0].astype(F32)
                sum_bufs[job][...] = jnp.transpose(total) if kind == "turned" else total
            stores.append(copy_of(sum_bufs[job], outs[out].at[place], osem.at[job]))
            stores[-1].start()
        for copy in stores:
            copy.wait()

    scratch = [pltpu.VMEM(part_shapes[job], array.dtype) for job, (terms, _, _, _) in enumerate(jobs) for array, _ in terms]
    for job, (_, out, _, kind) in enumerate(jobs):
        shape = part_shapes[job]
        shape = {"range": shape, "plain": shape[1:], "turned": shape[:0:-1]}[kind]
        scratch.append(pltpu.VMEM(shape, shapes[out].dtype))
    scratch += [pltpu.SemaphoreType.DMA((count,)), pltpu.SemaphoreType.DMA((len(jobs),))]
    return pl.pallas_call(
        kernel,
        out_shape=list(shapes),
        in_specs=[ANY] * len(arrays),
        out_specs=[ANY] * len(shapes),
        scratch_shapes=scratch,
        compiler_params=params(),
        cost_estimate=cost_of(3),
        name="combine",
    )(*arrays)


def swap_pairs(count, mask):
    return [(i, i ^ mask) for i in range(count)]


def to_sibling(values):
    return lax.ppermute(values, "tensor", swap_pairs(4, 1))


def over_y(values):
    return lax.ppermute(values, "tensor", swap_pairs(4, 2))


def over_dp(values, mask):
    return lax.ppermute(values, "dp", swap_pairs(8, mask))


def over_x(values):
    return over_dp(values, 1)


def over_z_near(values):
    return over_dp(values, 2)


def over_z_far(values):
    return over_dp(values, 4)


def after(values, *earlier):
    return lax.optimization_barrier((values, *earlier))[0]


MOVES = {"y": over_y, "x": over_x, "z": over_z_near}


class Reduction:
    def __init__(self, sent, portions, finish):
        self.other, self.finish = to_sibling(sent), finish
        self.portions, self.stage, self.sends, self.total = portions, 0, None, None

    def begin(self, kept, *earlier):
        other = after(self.other, *earlier)
        split = (kept.shape[0], 2, 2, 2, 2, *kept.shape[3:])
        arrays = (kept.reshape(split), other.reshape(split))
        self.blocks, self.tail = kept.shape[0], kept.shape[3:]
        self.terms = [[(array, ("b", "y", "x", "z", "w"), low, {}) for array in arrays] for low, _, _ in self.portions]

    def receive(self, *earlier):
        if self.stage == 4:
            moved = after(over_z_far(self.sends[0]), *earlier)
            for (low, _, _), terms in zip(self.portions, self.terms):
                terms.append((moved, ("b",), low, {}))
        elif self.stage:
            for send, (_, _, orders), terms in zip(self.sends, self.portions, self.terms):
                left = tuple(a for a in ("b", "y", "x", "z", "w") if a not in orders[: self.stage])
                terms.append((after(MOVES[orders[self.stage - 1]](send), *earlier), left, 0, {}))

    def jobs(self, first_out):
        jobs, shapes = [], []
        stage = self.stage
        for number, ((low, high, orders), terms) in enumerate(zip(self.portions, self.terms)):
            axis = (*orders, "w", None)[stage]
            picked = []
            for array, axes, start, fixed in terms:
                index = [slice(start, start + high - low)]
                for name in axes[1:]:
                    index.append(1 if name == axis else fixed.get(name, 0 if name in orders[:stage] or (stage > 3 and name == "w") else slice(None)))
                picked.append((array, tuple(index)))
            if stage < 3:
                shapes.append(sds((high - low, *(2,) * (3 - stage), *self.tail), BF16))
                jobs.append((picked, first_out + number, slice(0, high - low), "range"))
            elif stage == 3:
                if not number:
                    shapes.append(sds((self.blocks, *self.tail), BF16))
                jobs.append((picked, first_out, slice(low, high), "range"))
            else:
                if not number:
                    shapes += self.finish[0]
                for block in range(low, high):
                    shift = block - low
                    one = [(a, (slice(index[0].start + shift, index[0].start + shift + 1), *index[1:])) for a, index in picked]
                    out, place, kind = self.finish[1](block)
                    jobs.append((one, first_out + out, place, kind))
        self.stage += 1
        return jobs, shapes


def attention_finish(counts):
    stacks = [sds((count, UNIT, 2 * UNIT) if count > 1 else (UNIT, 2 * UNIT), F32) for count in counts]

    def place_of(block):
        half, matrix = block // 4, block % 4
        lanes = slice(half * UNIT, (half + 1) * UNIT)
        if matrix == 3:
            return len(counts), (lanes, slice(None)), "turned"
        stack = 0 if matrix < counts[0] else 1
        if counts[stack] == 1:
            return stack, (slice(None), lanes), "plain"
        return stack, (matrix - sum(counts[:stack]), slice(None), lanes), "plain"

    return [*stacks, sds((2 * UNIT, UNIT), F32)], place_of


def ffn_finish():
    def place_of(block):
        lanes = slice(block // 2 * FFN_PART, (block // 2 + 1) * FFN_PART)
        if block % 2:
            return 1, (lanes, slice(None)), "turned"
        return 0, (slice(None), lanes), "plain"

    return [sds((UNIT, 4 * FFN_PART), F32), sds((4 * FFN_PART, UNIT), F32)], place_of


def advance(reductions, *earlier):
    jobs, shapes, bounds = [], [], []
    for reduction in reductions:
        reduction.receive(*earlier)
        more, made = reduction.jobs(len(shapes))
        bounds.append((len(shapes), len(shapes) + len(made)))
        jobs, shapes = jobs + more, shapes + made
    results = combine(jobs, shapes)
    for reduction, (low, high) in zip(reductions, bounds):
        reduction.sends = list(results[low:high])
        if reduction.stage == 5:
            reduction.total = results[low:high]
    return list(results)


def sentence_body(
    tokens,
    memory,
    dec_lengths,
    mem_lengths,
    self_qkv,
    self_out,
    cross_q,
    cross_kv,
    cross_out,
    ffn_in,
    ffn_out,
    norm_gains,
    norm_biases,
    cotangent,
):
    dp = lax.axis_index("dp")
    order = dp & 3
    inner = (dp >> 1) & 1
    gains = [norm_gains[i : i + 1] for i in range(3)]
    biases = [norm_biases[i : i + 1] for i in range(3)]

    def part_rows(values, parts):
        rows = values.shape[-2] // parts
        place = order if parts == 4 else inner
        return lax.dynamic_slice_in_dim(values, place * rows, rows, values.ndim - 2)

    def folded(values):
        blocks = values.reshape(values.shape[0], 4, 2 * UNIT)
        return blocks.transpose(1, 0, 2).reshape(1, 4 * values.shape[0], 2 * UNIT)

    self_near = over_y(jnp.concatenate([part_rows(self_qkv, 4), folded(part_rows(self_out, 4))]))
    cross_near = over_y(
        jnp.concatenate([part_rows(cross_q, 2)[None], part_rows(cross_kv, 2), folded(part_rows(cross_out, 2))])
    )
    ffn_near = over_y(jnp.stack([part_rows(ffn_in, 4), part_rows(ffn_out, 4)]))
    self_own = (self_qkv, self_out)
    self_sib = tuple(to_sibling(w) for w in self_own)
    self_a = attention_fwd_call(dec_lengths, [], [tokens], [self_own, self_sib], None, None)
    self_near = after(self_near, self_a[4])
    self_side, self_up = over_x(self_near), over_z_near(self_near)
    self_corner = over_x(self_up)
    cross_own, ffn_own = (cross_q, cross_kv, cross_out), (ffn_in, ffn_out)
    cross_sib = tuple(to_sibling(w) for w in cross_own)
    cross_up = over_z_near(cross_near)
    self_rest = (self_near, self_side, self_up, after(self_corner, cross_near, *cross_sib))
    self_far = tuple(to_sibling(w) for w in self_rest)
    self_pieces = [self_own, self_sib, self_rest, self_far]
    self_b = attention_fwd_call(
        dec_lengths, [tokens], [tokens], self_pieces[2:], self_a[5], (gains[0], biases[0])
    )
    first_low, first_hat, first_inv = self_b[5:]
    cross_in = [first_low, memory]
    cross_rest = jnp.stack([cross_near, after(cross_up, self_b[4])])
    cross_far = to_sibling(cross_rest)
    ffn_sib = tuple(to_sibling(after(w, ffn_near)) for w in ffn_own)
    ffn_side, ffn_up = over_x(ffn_near), over_z_near(ffn_near)
    cross_pieces = [cross_own, cross_sib, (cross_rest,), (cross_far,)]
    cross_b = attention_fwd_call(
        mem_lengths, [first_hat, gains[0], biases[0]], [after(first_low, ffn_near), memory], cross_pieces, None,
        (gains[1], biases[1]),
    )
    second_low, second_hat, second_inv = cross_b[5:]
    ffn_side, ffn_up = after(ffn_side, cross_b[4]), after(ffn_up, cross_b[4])
    up_corner, down_corner = over_x(ffn_up[:1]), over_z_near(ffn_side[1:])
    ffn_pieces = [ffn_own, ffn_sib]
    ffn_a = ffn_fwd_call(second_low, ffn_pieces, None, None)
    up_corner, down_corner = after(up_corner, ffn_a[0]), after(down_corner, ffn_a[0])
    ffn_rest = (ffn_near, ffn_side, ffn_up, up_corner, down_corner)
    ffn_pieces += [ffn_rest, tuple(to_sibling(w) for w in ffn_rest)]
    ffn_b = ffn_fwd_call(
        second_low, ffn_pieces[2:], ffn_a[0],
        (second_hat, gains[1], biases[1], cotangent, gains[2], biases[2]),
    )
    out_rows, third_low, third_scaled, third_gain, third_bias = ffn_b[:5]

    def plan_of(pieces):
        return [(piece // 2, 2 * (piece % 2) + half) for piece in pieces for half in (0, 1)]

    ffn_saved = [ffn_a[1:3], ffn_b[5:7]]
    ffn_d = ffn_bwd_call(
        third_low, second_low, ffn_pieces[1::2], ffn_saved, plan_of((1, 3)), third_scaled, None
    )
    ffn_sum = Reduction(ffn_d[1], [(0, 3, "yzx"), (3, 6, "xyz"), (6, 8, "zxy")], ffn_finish())
    ffn_e = ffn_bwd_call(
        third_low, second_low, ffn_pieces[::2], ffn_saved, plan_of((0, 2)), ffn_d[0],
        (second_hat, second_inv, gains[1]),
    )
    second_back, second_scaled, second_gain, second_bias = ffn_e[:4]
    ffn_sum.begin(ffn_e[4], second_gain)
    second_back = after(second_back, *advance([ffn_sum]))

    cross_e = attention_bwd_call(
        mem_lengths, second_back, cross_in, cross_pieces[1::2] + cross_pieces[::2],
        [cross_b[:5]], [(0, 2 * p + half) for p in (1, 3, 0, 2) for half in (0, 1)], second_scaled,
        (first_hat, first_inv, gains[0]), 2,
    )
    first_back, first_scaled, first_gain, first_bias, memory_part = cross_e[:5]
    norm_sums = jnp.stack([first_gain, second_gain, third_gain, first_bias, second_bias, third_bias])
    norm_sums = jnp.concatenate([jnp.sum(norm_sums, axis=1), jnp.zeros((2, norm_sums.shape[2]), F32)])
    norm_sums = lax.all_gather(norm_sums, ("dp", "tensor"), axis=0)
    sends = advance([ffn_sum], first_gain)
    cross_sum = Reduction(after(cross_e[5], *sends), [(0, 4, "zyx"), (4, 8, "yxz")], attention_finish((1, 2)))
    first_back = after(first_back, *sends)

    self_saved = [self_a[:5], self_b[:5]]
    self_d = attention_bwd_call(
        dec_lengths, first_back, [tokens], self_pieces[1::2], self_saved, plan_of((1, 3)), None, None
    )
    cross_sum.begin(cross_e[6], self_d[0])
    sends = advance([cross_sum, ffn_sum], self_d[0])
    self_sum = Reduction(after(self_d[1], *sends), [(0, 4, "yxz"), (4, 8, "xzy")], attention_finish((3,)))
    first_back = after(first_back, *sends)
    self_e = attention_bwd_call(
        dec_lengths, first_back, [tokens], self_pieces[::2], self_saved, plan_of((0, 2)), None, None
    )
    self_sum.begin(self_e[1], self_e[0])
    sends = advance([self_sum])
    grad_tokens = inputs_back_call(
        after(first_scaled, *sends), [(self_d[0], self_pieces[1::2]), (self_e[0], self_pieces[::2])], (0, 1, 2)
    )
    sends = advance([cross_sum, ffn_sum], *sends)
    sends = advance([self_sum], *sends, grad_tokens)
    sends = advance([cross_sum, ffn_sum], *sends)
    sends = advance([self_sum], *sends)
    norm_total = jnp.sum(after(norm_sums, *sends), axis=0)
    sends = advance([cross_sum], *sends, norm_total)
    sends = advance([self_sum], *sends)
    grad_memory = inputs_back_call(
        None, [(after(memory_part, *sends), cross_pieces[1::2] + cross_pieces[::2])], (1, 2)
    )
    advance([cross_sum], *sends, grad_memory)
    advance([self_sum], grad_memory)
    self_sum, cross_sum, ffn_sum = self_sum.total, cross_sum.total, ffn_sum.total

    return (
        out_rows,
        grad_tokens,
        grad_memory,
        *self_sum,
        *cross_sum,
        *ffn_sum,
        norm_total[:3],
        norm_total[3:6],
    )


def sentence_fits(mesh, tokens, memory, dec_lengths):
    shape = dict(mesh.shape)
    rows = tokens.shape[0] // mesh.size
    sentences = dec_lengths.shape[1]
    return (
        shape["tensor"] == 4
        and shape["dp"] == 8
        and sentences == 4
        and rows == 512
        and memory.shape[0] // mesh.size == rows
        and tokens.shape[1] == 1024
    )


def smooth_gate(values):
    return jax.nn.gelu(values, approximate=True)


def norm_rows(hidden, norm_gain, norm_bias):
    center = hidden - jnp.mean(hidden, axis=-1, keepdims=True)
    inverse = lax.rsqrt(jnp.mean(center * center, axis=-1, keepdims=True) + NORM_EPSILON)
    normed = center * inverse
    return (normed * norm_gain + norm_bias, normed, inverse)


def norm_back(gradient, normed, inverse, norm_gain):
    scaled = gradient * norm_gain
    grad_in = inverse * (
        scaled
        - jnp.mean(scaled, axis=-1, keepdims=True)
        - normed * jnp.mean(scaled * normed, axis=-1, keepdims=True)
    )
    return (grad_in, jnp.sum(gradient * normed, axis=0), jnp.sum(gradient, axis=0))


def head_view(values, sentences):
    return values.reshape(sentences, -1, values.shape[1] // HEAD_DIM, HEAD_DIM)


def masked_scores(query_heads, key_heads, key_mask):
    scores = jnp.einsum(
        "sqhe,skhe->shqk", query_heads, key_heads, preferred_element_type=jnp.float32
    ) * HEAD_DIM ** (-0.5)
    return jnp.where(key_mask, scores, MASKED_SCORE)


def attention_forward(query_rows, key_rows, value_rows, key_mask, sentences):
    scores = masked_scores(
        head_view(query_rows, sentences), head_view(key_rows, sentences), key_mask
    )
    row_peak = jnp.max(scores, axis=-1, keepdims=True)
    exponent_terms = jnp.exp(scores - row_peak)
    row_sum = jnp.sum(exponent_terms, axis=-1, keepdims=True)
    softmax_probs = exponent_terms / row_sum
    attended = jnp.einsum(
        "shqk,skhe->sqhe",
        softmax_probs.astype(jnp.bfloat16),
        head_view(value_rows, sentences),
        preferred_element_type=jnp.float32,
    ).astype(jnp.bfloat16)
    return (attended.reshape(query_rows.shape), row_peak + jnp.log(row_sum))


def attention_backward(query_rows, key_rows, value_rows, key_mask, log_total, grad_rows, sentences):
    query_heads = head_view(query_rows, sentences)
    key_heads = head_view(key_rows, sentences)
    value_heads = head_view(value_rows, sentences)
    grad_heads = head_view(grad_rows, sentences)
    softmax_probs = jnp.exp(masked_scores(query_heads, key_heads, key_mask) - log_total)
    grad_probs = jnp.einsum(
        "sqhe,skhe->shqk", grad_heads, value_heads, preferred_element_type=jnp.float32
    )
    row_delta = jnp.sum(softmax_probs * grad_probs, axis=-1, keepdims=True)
    grad_scores = (softmax_probs * (grad_probs - row_delta)).astype(jnp.bfloat16)
    score_scale = HEAD_DIM ** (-0.5)
    grad_query = (
        jnp.einsum("shqk,skhe->sqhe", grad_scores, key_heads, preferred_element_type=jnp.float32)
        * score_scale
    ).astype(jnp.bfloat16)
    grad_key = (
        jnp.einsum("shqk,sqhe->skhe", grad_scores, query_heads, preferred_element_type=jnp.float32)
        * score_scale
    ).astype(jnp.bfloat16)
    grad_value = jnp.einsum(
        "shqk,sqhe->skhe",
        softmax_probs.astype(jnp.bfloat16),
        grad_heads,
        preferred_element_type=jnp.float32,
    ).astype(jnp.bfloat16)
    return (
        grad_query.reshape(query_rows.shape),
        grad_key.reshape(key_rows.shape),
        grad_value.reshape(value_rows.shape),
    )


def body(
    tokens,
    memory,
    dec_lengths,
    mem_lengths,
    self_qkv,
    self_out,
    cross_q,
    cross_kv,
    cross_out,
    ffn_in,
    ffn_out,
    norm_gains,
    norm_biases,
    cotangent,
):
    row_share = tokens.shape[0]
    sentences = dec_lengths.shape[1]
    all_tokens, all_memory = (
        lax.all_gather(tokens, "tensor", axis=0, tiled=True),
        lax.all_gather(memory, "tensor", axis=0, tiled=True),
    )
    sentence_len = all_tokens.shape[0] // sentences
    memory_len = all_memory.shape[0] // sentences
    positions = jnp.arange(sentence_len, dtype=jnp.int32)
    self_mask = (
        (positions[None, :] <= positions[:, None])[None]
        & (positions[None, None, :] < dec_lengths[0][:, None, None])
    )[:, None]
    memory_positions = jnp.arange(memory_len, dtype=jnp.int32)
    cross_mask = (memory_positions[None, :] < mem_lengths[0][:, None])[:, None, None, :]

    def branch_rows(attended, weight):
        return lax.psum_scatter(
            jnp.dot(attended, weight, preferred_element_type=jnp.float32).astype(jnp.bfloat16),
            "tensor",
            scatter_dimension=0,
            tiled=True,
        ).astype(jnp.float32)

    def branch_grad(grad_rows, attended, weight):
        grad_low = grad_rows.astype(jnp.bfloat16)
        grad_all = lax.all_gather(grad_low, "tensor", axis=0, tiled=True)
        grad_attended = jnp.dot(grad_all, weight.T, preferred_element_type=jnp.float32).astype(
            jnp.bfloat16
        )
        weight_part = jnp.dot(attended.T, grad_all, preferred_element_type=jnp.float32)
        return (grad_attended, weight_part)

    def gather_normed(values):
        return lax.all_gather(values, "tensor", axis=0, tiled=True)

    def head_input_sum(term):
        return lax.psum_scatter(
            term(jnp.int32(0), row_share * lax.axis_size("tensor")).astype(jnp.bfloat16),
            "tensor",
            scatter_dimension=0,
            tiled=True,
        ).astype(jnp.float32)

    self_proj = jnp.einsum(
        "td,cde->cte", all_tokens, self_qkv, preferred_element_type=jnp.float32
    ).astype(jnp.bfloat16)
    self_att, self_lse = attention_forward(
        self_proj[0], self_proj[1], self_proj[2], self_mask, sentences
    )
    self_branch = branch_rows(self_att, self_out)
    first_norm, first_hat, first_inv = norm_rows(
        RESIDUAL_ALPHA * tokens.astype(jnp.float32) + self_branch, norm_gains[0], norm_biases[0]
    )
    first_all = gather_normed(first_norm.astype(jnp.bfloat16))
    cross_query = jnp.dot(first_all, cross_q, preferred_element_type=jnp.float32).astype(
        jnp.bfloat16
    )
    cross_proj = jnp.einsum(
        "td,cde->cte", all_memory, cross_kv, preferred_element_type=jnp.float32
    ).astype(jnp.bfloat16)
    cross_att, cross_lse = attention_forward(
        cross_query, cross_proj[0], cross_proj[1], cross_mask, sentences
    )
    cross_branch = branch_rows(cross_att, cross_out)
    second_norm, second_hat, second_inv = norm_rows(
        RESIDUAL_ALPHA * first_norm + cross_branch, norm_gains[1], norm_biases[1]
    )
    second_all = gather_normed(second_norm.astype(jnp.bfloat16))
    pre_gate = jnp.dot(second_all, ffn_in, preferred_element_type=jnp.float32)
    activated = smooth_gate(pre_gate).astype(jnp.bfloat16)
    ffn_branch = lax.psum_scatter(
        jnp.dot(activated, ffn_out, preferred_element_type=jnp.float32).astype(jnp.bfloat16),
        "tensor",
        scatter_dimension=0,
        tiled=True,
    ).astype(jnp.float32)
    out_rows, third_hat, third_inv = norm_rows(
        RESIDUAL_ALPHA * second_norm + ffn_branch, norm_gains[2], norm_biases[2]
    )
    grad_third, third_gain, third_bias = norm_back(
        cotangent.astype(jnp.float32), third_hat, third_inv, norm_gains[2]
    )
    grad_ffn_all = lax.all_gather(grad_third.astype(jnp.bfloat16), "tensor", axis=0, tiled=True)
    unused_gate, gate_pull = jax.vjp(smooth_gate, pre_gate)
    grad_act = gate_pull(jnp.dot(grad_ffn_all, ffn_out.T, preferred_element_type=jnp.float32))[
        0
    ].astype(jnp.bfloat16)
    grad_ffn_out = jnp.dot(activated.T, grad_ffn_all, preferred_element_type=jnp.float32)
    grad_ffn_in = jnp.dot(second_all.T, grad_act, preferred_element_type=jnp.float32)
    grad_second = RESIDUAL_ALPHA * grad_third + lax.psum_scatter(
        jnp.dot(grad_act, ffn_in.T, preferred_element_type=jnp.float32).astype(jnp.bfloat16),
        "tensor",
        scatter_dimension=0,
        tiled=True,
    ).astype(jnp.float32)
    grad_second_in, second_gain, second_bias = norm_back(
        grad_second, second_hat, second_inv, norm_gains[1]
    )
    grad_cross_att, cross_out_part = branch_grad(grad_second_in, cross_att, cross_out)
    grad_cq, grad_ck, grad_cv = attention_backward(
        cross_query, cross_proj[0], cross_proj[1], cross_mask, cross_lse, grad_cross_att, sentences
    )
    grad_cross_q = jnp.dot(first_all.T, grad_cq, preferred_element_type=jnp.float32)
    cross_grads = jnp.stack([grad_ck, grad_cv])
    grad_cross_kv = jnp.einsum(
        "td,cte->cde", all_memory, cross_grads, preferred_element_type=jnp.float32
    )
    grad_memory = lax.psum_scatter(
        jnp.einsum("cte,cde->td", cross_grads, cross_kv, preferred_element_type=jnp.float32).astype(
            jnp.bfloat16
        ),
        "tensor",
        scatter_dimension=0,
        tiled=True,
    ).astype(jnp.float32)

    def cross_input_term(first_row, row_total):
        return jnp.dot(grad_cq, cross_q.T, preferred_element_type=jnp.float32)

    cross_input = head_input_sum(cross_input_term)
    grad_first = RESIDUAL_ALPHA * grad_second_in + cross_input
    grad_first_in, first_gain, first_bias = norm_back(
        grad_first, first_hat, first_inv, norm_gains[0]
    )
    grad_self_att, self_out_part = branch_grad(grad_first_in, self_att, self_out)
    grad_sq, grad_sk, grad_sv = attention_backward(
        self_proj[0], self_proj[1], self_proj[2], self_mask, self_lse, grad_self_att, sentences
    )
    self_grads = jnp.stack([grad_sq, grad_sk, grad_sv])
    grad_self_qkv = jnp.einsum(
        "td,cte->cde", all_tokens, self_grads, preferred_element_type=jnp.float32
    )

    def self_input_term(first_row, row_total):
        return jnp.einsum("cte,cde->td", self_grads, self_qkv, preferred_element_type=jnp.float32)

    self_input = head_input_sum(self_input_term)
    grad_tokens = RESIDUAL_ALPHA * grad_first_in + self_input
    summed = (
        lax.psum_scatter(
            grad_self_qkv.astype(jnp.bfloat16), "dp", scatter_dimension=1, tiled=True
        ).astype(jnp.float32),
        lax.psum_scatter(
            self_out_part.astype(jnp.bfloat16), "dp", scatter_dimension=1, tiled=True
        ).astype(jnp.float32),
        lax.psum_scatter(
            grad_cross_q.astype(jnp.bfloat16), "dp", scatter_dimension=0, tiled=True
        ).astype(jnp.float32),
        lax.psum_scatter(
            grad_cross_kv.astype(jnp.bfloat16), "dp", scatter_dimension=1, tiled=True
        ).astype(jnp.float32),
        lax.psum_scatter(
            cross_out_part.astype(jnp.bfloat16), "dp", scatter_dimension=1, tiled=True
        ).astype(jnp.float32),
        lax.psum_scatter(
            grad_ffn_in.astype(jnp.bfloat16), "dp", scatter_dimension=0, tiled=True
        ).astype(jnp.float32),
        lax.psum_scatter(
            grad_ffn_out.astype(jnp.bfloat16), "dp", scatter_dimension=1, tiled=True
        ).astype(jnp.float32),
    )
    gain_total, bias_total = lax.psum(
        (
            jnp.stack([first_gain, second_gain, third_gain]),
            jnp.stack([first_bias, second_bias, third_bias]),
        ),
        ("dp", "tensor"),
    )
    return (
        out_rows.astype(jnp.bfloat16),
        grad_tokens,
        grad_memory,
        summed[0],
        summed[1],
        summed[2],
        summed[3],
        summed[4],
        summed[5],
        summed[6],
        gain_total,
        bias_total,
    )


def solution(mesh):
    in_specs = (
        P(("dp", "tensor"), None),
        P(("dp", "tensor"), None),
        P("dp", None),
        P("dp", None),
        P(None, None, "tensor"),
        P("tensor", None),
        P(None, "tensor"),
        P(None, None, "tensor"),
        P("tensor", None),
        P(None, "tensor"),
        P("tensor", None),
        P(),
        P(),
        P(("dp", "tensor"), None),
    )
    out_specs = (
        P(("dp", "tensor"), None),
        P(("dp", "tensor"), None),
        P(("dp", "tensor"), None),
        P(None, "dp", "tensor"),
        P("tensor", "dp"),
        P("dp", "tensor"),
        P(None, "dp", "tensor"),
        P("tensor", "dp"),
        P("dp", "tensor"),
        P("tensor", "dp"),
        P(),
        P(),
    )

    def step(*args):
        chosen = sentence_body if sentence_fits(mesh, args[0], args[1], args[2]) else body
        return jax.shard_map(
            chosen, mesh=mesh, in_specs=in_specs, out_specs=out_specs, check_vma=False
        )(*args)

    return step
```

```python
import functools
import jax
import jax.numpy as jnp
from jax import lax
from jax.experimental import pallas as pl
from jax.experimental.pallas import tpu as pltpu
from jax.sharding import PartitionSpec as P

HEAD_DIM = 64
RESIDUAL_ALPHA = 4.16
NORM_EPSILON = 1e-05
MASKED_SCORE = -1000000000.0
SCORE_SCALE = HEAD_DIM ** (-0.5)
UNIT = 128
QUERY_BLOCK = 256
FFN_UNIT = 512
ROW_CHUNK = 64
BF16 = jnp.bfloat16
F32 = jnp.float32


def dot(left, right):
    return lax.dot_general(left, right, (((1,), (0,)), ((), ())), preferred_element_type=F32)


def dot_tn(left, right):
    return lax.dot_general(left, right, (((0,), (0,)), ((), ())), preferred_element_type=F32)


def dot_nt(left, right):
    return lax.dot_general(left, right, (((1,), (1,)), ((), ())), preferred_element_type=F32)


def shard_of(position):
    return ((position >> 2) & 1) | (position & 2) | ((position & 1) << 2)


def copy_of(source, target, sem):
    return pltpu.make_async_copy(source, target, sem)


def own_lanes(rows, head):
    lanes = lax.broadcasted_iota(jnp.int32, rows.shape, 1)
    return jnp.where((lanes >= HEAD_DIM) if head else (lanes < HEAD_DIM), rows, 0.0)


def extended_keys(keys, length):
    lanes = lax.broadcasted_iota(jnp.int32, keys.shape, 1)
    rows = lax.broadcasted_iota(jnp.int32, keys.shape, 0)
    mask = jnp.where((lanes == 0) & (rows >= length), MASKED_SCORE, 0.0).astype(BF16)
    keys = keys.astype(F32)
    return [jnp.concatenate([own_lanes(keys, head).astype(BF16), mask], axis=1) for head in (0, 1)]


def extended_query(query):
    lanes = lax.broadcasted_iota(jnp.int32, query.shape, 1)
    return jnp.concatenate([query, jnp.where(lanes == 0, 1.0, 0.0).astype(BF16)], axis=1)


def fill_diagonal(diagonal):
    keys = lax.broadcasted_iota(jnp.int32, diagonal.shape, 0)
    queries = lax.broadcasted_iota(jnp.int32, diagonal.shape, 1)
    diagonal[...] = jnp.where(keys <= queries, 0.0, MASKED_SCORE)


def key_ranges(block, keys, causal):
    if not causal:
        return [(0, keys)]
    return [(low, low + QUERY_BLOCK) for low in range(0, (block + 1) * QUERY_BLOCK, QUERY_BLOCK)]


def attend_unit(query, keys, values, length, causal, diagonal, lse_ref):
    rows, count = query.shape[0], keys.shape[0]
    values_t = jnp.transpose(values.astype(F32)).astype(BF16)
    wide_keys, wide_query = extended_keys(keys, length), extended_query(query)
    items = [(head, block) for block in range(rows // QUERY_BLOCK) for head in (0, 1)]
    scores, probs, totals, mixed = {}, {}, {}, {}
    for head, block in items:
        part = wide_query[block * QUERY_BLOCK : (block + 1) * QUERY_BLOCK]
        ranges = key_ranges(block, count, causal)
        scores[head, block] = [dot_nt(wide_keys[head][a:b], part) for a, b in ranges]
        if causal:
            scores[head, block][-1] = scores[head, block][-1] + diagonal[...]
    for head, block in items:
        pieces = scores[head, block]
        peak = functools.reduce(jnp.maximum, [jnp.max(p, axis=0, keepdims=True) for p in pieces])
        terms = [jnp.exp(p - peak) for p in pieces]
        total = sum(jnp.sum(t, axis=0, keepdims=True) for t in terms)
        at = slice(block * QUERY_BLOCK, (block + 1) * QUERY_BLOCK)
        lse_ref[head : head + 1, at] = peak + jnp.log(total)
        totals[head, block] = total
        probs[head, block] = jnp.concatenate([t.astype(BF16) for t in terms], axis=0)
    for head, block in items:
        own = values_t[head * HEAD_DIM : (head + 1) * HEAD_DIM, : probs[head, block].shape[0]]
        mixed[head, block] = dot(own, probs[head, block]) / totals[head, block]
    out = [
        jnp.transpose(jnp.concatenate([mixed[0, block], mixed[1, block]], axis=0))
        for block in range(rows // QUERY_BLOCK)
    ]
    return jnp.concatenate(out, axis=0).astype(BF16)


def attend_back_unit(query, keys, values, attended, grad, length, causal, diagonal, lse_ref):
    rows, count = query.shape[0], keys.shape[0]
    blocks = range(rows // QUERY_BLOCK)
    query_f, keys_f, grad_f = (a.astype(F32) for a in (query, keys, grad))
    wide_keys, wide_query = extended_keys(keys, length), extended_query(query)
    delta = jnp.transpose(grad_f * attended.astype(F32))
    deltas = [
        jnp.sum(delta[head * HEAD_DIM : (head + 1) * HEAD_DIM], axis=0, keepdims=True)
        for head in (0, 1)
    ]
    keys_t = jnp.transpose(keys_f).astype(BF16)
    query_own = [own_lanes(query_f, head).astype(BF16) for head in (0, 1)]
    grad_own = [own_lanes(grad_f, head).astype(BF16) for head in (0, 1)]
    items = [(head, block) for block in blocks for head in (0, 1)]
    scores, slopes, probs, back, grad_query = {}, {}, {}, {}, {}
    for head, block in items:
        at = slice(block * QUERY_BLOCK, (block + 1) * QUERY_BLOCK)
        for a, b in key_ranges(block, count, causal):
            scores[head, block, a] = dot_nt(wide_keys[head][a:b], wide_query[at])
            slopes[head, block, a] = dot_nt(values[a:b], grad_own[head][at])
    for head, block in items:
        at = slice(block * QUERY_BLOCK, (block + 1) * QUERY_BLOCK)
        ranges = key_ranges(block, count, causal)
        for a, b in ranges:
            score = scores[head, block, a]
            if causal and (a, b) == ranges[-1]:
                score = score + diagonal[...]
            prob = jnp.exp(score - lse_ref[head : head + 1, at])
            probs[head, block, a] = prob.astype(BF16)
            back[head, block, a] = (prob * (slopes[head, block, a] - deltas[head][:, at])).astype(BF16)
    for head, block in items:
        own = keys_t[head * HEAD_DIM : (head + 1) * HEAD_DIM]
        grad_query[head, block] = sum(
            dot(own[:, a:b], back[head, block, a]) for a, b in key_ranges(block, count, causal)
        )
    grad_keys, grad_values = [], []
    for low in sorted({key[2] for key in back}):
        live = [key for key in back if key[2] == low]
        at = [slice(block * QUERY_BLOCK, (block + 1) * QUERY_BLOCK) for _, block, _ in live]
        grad_values.append(
            dot(
                jnp.concatenate([probs[key] for key in live], axis=1),
                jnp.concatenate([grad_own[key[0]][a] for key, a in zip(live, at)], axis=0),
            )
        )
        grad_keys.append(
            dot(
                jnp.concatenate([back[key] for key in live], axis=1),
                jnp.concatenate([query_own[key[0]][a] for key, a in zip(live, at)], axis=0),
            )
        )
    grad_query = [
        jnp.transpose(jnp.concatenate([grad_query[0, block], grad_query[1, block]], axis=0)) * SCORE_SCALE
        for block in blocks
    ]
    return tuple(
        jnp.concatenate(parts, axis=0).astype(BF16) for parts in (grad_query, grad_keys, grad_values)
    )


def norm_chunk(hidden, gain, bias):
    center = hidden - jnp.mean(hidden, axis=-1, keepdims=True)
    inverse = lax.rsqrt(jnp.mean(center * center, axis=-1, keepdims=True) + NORM_EPSILON)
    normed = center * inverse
    return normed * gain + bias, normed, inverse


def norm_back_chunk(gradient, normed, inverse, gain):
    scaled = gradient * gain
    return inverse * (
        scaled
        - jnp.mean(scaled, axis=-1, keepdims=True)
        - normed * jnp.mean(scaled * normed, axis=-1, keepdims=True)
    )


def fold_rows(values):
    return jnp.sum(values.reshape(values.shape[0] // 8, 8, values.shape[1]), axis=0)


def each_chunk(rows, body, results):
    def step(index, carry):
        at = pl.ds(pl.multiple_of(index * ROW_CHUNK, ROW_CHUNK), ROW_CHUNK)
        body(at)
        for buffer, out, sem in results:
            copy_of(buffer.at[at, :], out.at[at, :], sem).start()
        return carry

    lax.fori_loop(0, rows // ROW_CHUNK, step, 0)
    return [copy_of(*result) for result in results]


def store_shards(target, weight, dp):
    for block in range(8):
        target[shard_of(block ^ dp)] = weight[block * UNIT : (block + 1) * UNIT]


SMEM = pl.BlockSpec(memory_space=pltpu.SMEM)
VMEM = pl.BlockSpec(memory_space=pltpu.VMEM)
ANY = pl.BlockSpec(memory_space=pl.ANY)


def params(limit=62):
    return pltpu.CompilerParams(vmem_limit_bytes=limit * 1024 * 1024)


def cost_of(microseconds):
    return pl.CostEstimate(flops=int(microseconds * 1.1e9), bytes_accessed=4 << 20, transcendentals=0)


def sds(shape, dtype):
    return jax.ShapeDtypeStruct(shape, dtype)


def position():
    dp = lax.axis_index("dp")
    return dp & 3, dp, (dp >> 1) & 1


def weight_copies(pieces, wbuf, obuf, wsem, osem, columns=(0, 1, 2)):
    groups, outs = [[], [], []], []
    wide = 2 * UNIT
    order, _, inner = position()
    for index, refs in enumerate(pieces):
        at = slice(index * wide, (index + 1) * wide)
        if len(refs[-1].shape) == 2:
            column = 0
            for ref in refs[:-1]:
                for source in [ref] if len(ref.shape) == 2 else [ref.at[c] for c in range(ref.shape[0])]:
                    if column in columns:
                        low = (columns.index(column) * len(pieces) + index) * wide
                        groups[column].append(copy_of(source, wbuf.at[:, low : low + wide], wsem.at[column, index, 0]))
                    column += 1
            if obuf is not None:
                outs.append(copy_of(refs[-1], obuf.at[at, :], osem.at[index, 0]))
            continue
        parts = [refs[0].at[n] for n in range(refs[0].shape[0])] if len(refs[0].shape) == 4 else refs
        rows = parts[0].shape[1]
        part = wide // len(parts)
        for quarter, ref in enumerate(parts):
            place = quarter ^ (order if len(parts) == 4 else inner)
            for column in columns:
                low = (columns.index(column) * len(pieces) + index) * wide
                groups[column].append(
                    copy_of(
                        ref.at[column],
                        wbuf.at[pl.ds(pl.multiple_of(place * rows, rows), rows), low : low + wide],
                        wsem.at[column, index, quarter],
                    )
                )
            for block in range(4 if obuf is not None else 0):
                outs.append(
                    copy_of(
                        ref.at[3, block * part : (block + 1) * part, :],
                        obuf.at[pl.ds(pl.multiple_of(index * wide + place * part, part), part), block * wide : (block + 1) * wide],
                        osem.at[index, 4 * quarter + block],
                    )
                )
    return groups, outs


def attention_fwd_call(lengths, residual, others, pieces, partial, norm):
    rows, depth = others[0].shape
    causal = len(others) == 1
    number, wide = 2 * len(pieces), 2 * len(pieces) * UNIT
    last, has_partial = norm is not None, partial is not None

    def kernel(*refs):
        it = iter(refs)
        len_ref = next(it)
        in_refs = [next(it) for _ in others]
        gain_ref, bias_ref = (next(it), next(it)) if last else (None, None)
        old_rows = [next(it) for _ in residual[1:]] if last else []
        res_in = next(it) if last else None
        part_in = next(it) if has_partial else None
        w_refs = [[next(it) for _ in piece] for piece in pieces]
        unit_outs, lse_ref = [next(it) for _ in range(4)], next(it)
        if last:
            norm_outs = [next(it) for _ in range(3)]
        else:
            sum_ref = next(it)
        wbuf, obuf, att_all, diagonal, wsem, osem, lsem, usem = (next(it) for _ in range(8))
        q_ref, k_ref, v_ref, att_ref = (next(it) for _ in range(4))
        if last:
            acc, old, low_ref, hat_ref, inv_ref = (next(it) for _ in range(5))
        length = len_ref[0, lax.axis_index("tensor")]
        groups, outs = weight_copies(w_refs, wbuf, obuf, wsem, osem)
        for copies in groups + [outs]:
            for copy in copies:
                copy.start()
        target = acc if last else sum_ref
        late = []
        if has_partial:
            late.append(copy_of(part_in, target, lsem.at[0]))
        if last:
            late.append(copy_of(res_in, old, lsem.at[1]))
        for copy in late:
            copy.start()
        if causal:
            fill_diagonal(diagonal)
        for c, result in enumerate((q_ref, k_ref, v_ref)):
            for copy in groups[c]:
                copy.wait()
            rows_in = in_refs[0] if causal or c == 0 else in_refs[1]
            proj = dot(rows_in[...], wbuf[:, c * wide : (c + 1) * wide]).astype(BF16)
            if c == 0:
                proj = (proj.astype(F32) * SCORE_SCALE).astype(BF16)
            for index in range(number):
                result[index] = proj[:, index * UNIT : (index + 1) * UNIT]

        flushes = [copy_of(*pair, usem.at[index]) for index, pair in enumerate(zip((q_ref, k_ref, v_ref, att_ref), unit_outs))]
        for copy in flushes[:3]:
            copy.start()

        def step(first, carry):
            for u in [first * 4 + inner for inner in range(4)]:
                attended = attend_unit(q_ref[u], k_ref[u], v_ref[u], length, causal, diagonal, lse_ref.at[u])
                att_ref[u] = attended
                att_all[:, pl.ds(pl.multiple_of(u * UNIT, UNIT), UNIT)] = attended
            return carry

        lax.fori_loop(0, number // 4, step, 0)
        flushes[3].start()
        for copy in outs + late:
            copy.wait()
        if has_partial:
            target[...] += dot(att_all[...], obuf[...])
        else:
            target[...] = dot(att_all[...], obuf[...])
        if last:
            def chunk(at):
                before = old[at, :].astype(F32)
                if old_rows:
                    before = before * old_rows[0][...] + old_rows[1][...]
                normed, hat, inverse = norm_chunk(RESIDUAL_ALPHA * before + acc[at, :], gain_ref[...], bias_ref[...])
                low_ref[at, :] = normed.astype(BF16)
                hat_ref[at, :] = hat
                inv_ref[at, :] = jnp.broadcast_to(inverse, (ROW_CHUNK, 128))

            triples = zip((low_ref, hat_ref, inv_ref), norm_outs)
            flushes += each_chunk(rows, chunk, [(*pair, usem.at[4 + index]) for index, pair in enumerate(triples)])
        for copy in flushes:
            copy.wait()

    unit_rows = sds((number, rows, UNIT), BF16)
    shapes = [unit_rows] * 4 + [sds((number, 2, rows), F32)]
    if last:
        shapes += [sds((rows, depth), BF16), sds((rows, depth), F32), sds((rows, 128), F32)]
    else:
        shapes += [sds((rows, depth), F32)]
    args = [lengths, *others]
    if last:
        args += [*norm, *residual[1:]]
    tail = ([residual[0]] if last else []) + ([partial] if has_partial else [])
    tail += [array for piece in pieces for array in piece]
    scratch = [
        pltpu.VMEM((depth, 3 * wide), BF16),
        pltpu.VMEM((wide, depth), BF16),
        pltpu.VMEM((rows, wide), BF16),
        pltpu.VMEM((QUERY_BLOCK, QUERY_BLOCK), F32),
        pltpu.SemaphoreType.DMA((3, len(pieces), 4)),
        pltpu.SemaphoreType.DMA((len(pieces), 16)),
        pltpu.SemaphoreType.DMA((2,)),
        pltpu.SemaphoreType.DMA((7,)),
    ]
    scratch += [pltpu.VMEM((number, rows, UNIT), BF16)] * 4
    if last:
        scratch += [pltpu.VMEM((rows, depth), F32), pltpu.VMEM((rows, depth), residual[0].dtype)]
        scratch += [pltpu.VMEM((rows, depth), BF16), pltpu.VMEM((rows, depth), F32), pltpu.VMEM((rows, 128), F32)]
    return pl.pallas_call(
        kernel,
        out_shape=shapes,
        in_specs=[SMEM] + [VMEM] * (len(args) - 1) + [ANY] * len(tail),
        out_specs=[ANY] * 4 + [VMEM] + ([ANY] * 3 if last else [VMEM]),
        scratch_shapes=scratch,
        compiler_params=params(),
        cost_estimate=cost_of(0.6 * number),
        name="self_fwd" if causal else "cross_fwd",
    )(*args, *tail)


def attention_bwd_call(lengths, grad_low, others, pieces, saved, plan, carried, norm, results=1):
    rows, depth = grad_low.shape
    causal = len(others) == 1
    number, n_in, wide = len(plan), len(others), len(plan) * UNIT
    last = norm is not None
    skip = 1 if last else 0

    def kernel(*refs):
        it = iter(refs)
        len_ref = next(it)
        h_ref = next(it)
        in_refs = [next(it) for _ in range(n_in)]
        gain_ref = next(it) if last else None
        late_in = [next(it), next(it)] if last else []
        acc_in = next(it) if last else None
        w_refs = [[next(it) for _ in piece] for piece in pieces]
        s_refs = [[next(it) for _ in call] for call in saved]
        if last:
            low_ref, scaled_ref, gsum_ref, bsum_ref = (next(it) for _ in range(4))
        dall_ref = next(it)
        g_refs = [next(it) for _ in range(results)]
        wbuf, obuf, sbuf, lbuf, att_all, grad_all = (next(it) for _ in range(6))
        stage, diagonal = next(it), next(it)
        if last:
            dquery, acc, hat, inv, low_buf, scaled_buf, nsem = (next(it) for _ in range(7))
        wsem, osem, ssem, gsem, lsem = (next(it) for _ in range(5))
        length, dp = len_ref[0, lax.axis_index("tensor")], lax.axis_index("dp")

        groups, o_copies = weight_copies(w_refs, wbuf, obuf, wsem, osem, (0,) if last else ())
        for copy in o_copies:
            copy.start()
        s_copies = []
        for index, unit in enumerate(plan):
            lanes = slice(index * UNIT, (index + 1) * UNIT)
            call = s_refs[unit[0]]
            for c in range(3):
                s_copies.append(copy_of(call[c].at[unit[1]], sbuf.at[index, c], ssem.at[c, index]))
            s_copies.append(copy_of(call[3].at[unit[1]], att_all.at[:, lanes], ssem.at[3, index]))
            s_copies.append(copy_of(call[4].at[unit[1]], lbuf.at[index], ssem.at[4, index]))
        late = []
        if last:
            late = groups[0] + [
                copy_of(source, target, lsem.at[index])
                for index, (source, target) in enumerate(((acc_in, acc), (late_in[0], hat), (late_in[1], inv)))
            ]
        for copy in s_copies + late:
            copy.start()
        if causal:
            fill_diagonal(diagonal)
        for copy in o_copies:
            copy.wait()
        grad_att = dot_nt(h_ref[...], obuf[...]).astype(BF16)
        for index in range(number):
            grad_all[index] = grad_att[:, index * UNIT : (index + 1) * UNIT]
        for copy in s_copies:
            copy.wait()

        def step(first, carry):
            units = [first * 2, first * 2 + 1]
            ats = [pl.ds(pl.multiple_of(u * UNIT, UNIT), UNIT) for u in units]
            parts = [
                attend_back_unit(
                    sbuf[u, 0], sbuf[u, 1], sbuf[u, 2], att_all[:, at], grad_all[u], length, causal, diagonal, lbuf.at[u]
                )
                for u, at in zip(units, ats)
            ]
            for u, at, part in zip(units, ats, parts):
                if last:
                    dquery[:, at] = part[0]
                for c in range(skip, 3):
                    dall_ref[:, pl.ds(pl.multiple_of((c - skip) * wide + u * UNIT, UNIT), UNIT)] = part[c]
            return carry

        lax.fori_loop(0, number // 2, step, 0)
        share = number // 2 // results

        def keep(rows_in, source, column):
            weight = dot_tn(rows_in[...], source).astype(BF16)
            for index in range(number):
                piece = index // 2
                target = stage.at[piece // share, (index % 2) * 4 + column, piece % share]
                store_shards(target, weight[:, index * UNIT : (index + 1) * UNIT], dp)

        if last:
            keep(in_refs[0], dquery[...], 0)
        for c in range(skip, 3):
            keep(in_refs[-1], dall_ref[:, (c - skip) * wide : (c - skip + 1) * wide], c)
        keep(h_ref, att_all[...], 3)
        g_copies = [copy_of(stage.at[index], ref, gsem.at[index]) for index, ref in enumerate(g_refs)]
        for copy in g_copies:
            copy.start()
        for copy in late:
            copy.wait()
        if last:
            acc[...] += dot_nt(dquery[...], wbuf[...])
            g_copies += norm_back_rows(
                acc, hat, inv, gain_ref, low_buf, scaled_buf, (low_ref, scaled_ref), nsem, gsum_ref, bsum_ref, rows
            )
        for copy in g_copies:
            copy.wait()

    big = sds((rows, depth), F32)
    shapes = []
    if last:
        shapes += [sds((rows, depth), BF16), big, sds((8, depth), F32), sds((8, depth), F32)]
    shapes.append(sds((rows, (3 - skip) * wide), BF16))
    specs_out = ([ANY] * 2 + [VMEM] * 3 if last else [VMEM]) + [ANY] * results
    shapes += [sds((8, number // 2 // results, 8, UNIT, UNIT), BF16)] * results
    args = [lengths, grad_low, *others] + ([norm[2]] if last else [])
    tail = [norm[0], norm[1], carried] if last else []
    tail += [array for piece in pieces for array in piece]
    for call in saved:
        tail += call
    scratch = [
        pltpu.VMEM((depth, wide) if last else (16, 128), BF16),
        pltpu.VMEM((wide, depth), BF16),
        pltpu.VMEM((number, 3, rows, UNIT), BF16),
        pltpu.VMEM((number, 2, rows), F32),
        pltpu.VMEM((rows, wide), BF16),
        pltpu.VMEM((number, rows, UNIT), BF16),
        pltpu.VMEM((results, 8, number // 2 // results, 8, UNIT, UNIT), BF16),
        pltpu.VMEM((QUERY_BLOCK, QUERY_BLOCK), F32),
    ]
    if last:
        scratch += [pltpu.VMEM((rows, wide), BF16), pltpu.VMEM((rows, depth), F32), pltpu.VMEM((rows, depth), F32), pltpu.VMEM((rows, 128), F32)]
        scratch += [pltpu.VMEM((rows, depth), BF16), pltpu.VMEM((rows, depth), F32), pltpu.SemaphoreType.DMA((2,))]
    scratch += [
        pltpu.SemaphoreType.DMA((3, len(pieces), 4)),
        pltpu.SemaphoreType.DMA((len(pieces), 16)),
        pltpu.SemaphoreType.DMA((5, number)),
        pltpu.SemaphoreType.DMA((results,)),
        pltpu.SemaphoreType.DMA((4,)),
    ]
    return pl.pallas_call(
        kernel,
        out_shape=shapes,
        in_specs=[SMEM] + [VMEM] * (len(args) - 1) + [ANY] * len(tail),
        out_specs=specs_out,
        scratch_shapes=scratch,
        compiler_params=params(),
        cost_estimate=cost_of(4.2 * number),
        name="self_bwd" if causal else "cross_bwd",
    )(*args, *tail)


def inputs_back_call(base, parts, columns):
    rows, depth = parts[0][0].shape[0], parts[0][1][0][0].shape[-2]

    def kernel(*refs):
        it = iter(refs)
        base_ref = next(it) if base is not None else None
        grads = [next(it) for _ in parts]
        w_refs = [[[next(it) for _ in piece] for piece in pieces] for _, pieces in parts]
        out = next(it)
        bufs, sems = [next(it) for _ in parts], [next(it) for _ in parts]
        copies = []
        for index in range(len(parts)):
            groups, _ = weight_copies(w_refs[index], bufs[index], None, sems[index], None, columns)
            copies.append([copy for group in groups for copy in group])
            for copy in copies[-1]:
                copy.start()
        if base is not None:
            out[...] = base_ref[...]
        for index in range(len(parts)):
            for copy in copies[index]:
                copy.wait()
            if index or base is not None:
                out[...] += dot_nt(grads[index][...], bufs[index][...])
            else:
                out[...] = dot_nt(grads[index][...], bufs[index][...])

    args = ([base] if base is not None else []) + [grad for grad, _ in parts]
    tail = [array for _, pieces in parts for piece in pieces for array in piece]
    return pl.pallas_call(
        kernel,
        out_shape=sds((rows, depth), F32),
        in_specs=[VMEM] * len(args) + [ANY] * len(tail),
        out_specs=VMEM,
        scratch_shapes=[pltpu.VMEM((depth, grad.shape[1]), BF16) for grad, _ in parts]
        + [pltpu.SemaphoreType.DMA((3, len(pieces), 4)) for _, pieces in parts],
        compiler_params=params(),
        cost_estimate=cost_of(7),
        name="inputs_back",
    )(*args, *tail)


def norm_back_rows(acc, hat, inv, gain_ref, low_buf, scaled_buf, outs, sems, gsum_ref, bsum_ref, rows):
    gsum_ref[...] = jnp.zeros_like(gsum_ref)
    bsum_ref[...] = jnp.zeros_like(bsum_ref)

    def chunk(at):
        gradient, normed = acc[at, :], hat[at, :]
        grad_in = norm_back_chunk(gradient, normed, inv[at, :1], gain_ref[...])
        low_buf[at, :] = grad_in.astype(BF16)
        scaled_buf[at, :] = RESIDUAL_ALPHA * grad_in
        gsum_ref[...] += fold_rows(gradient * normed)
        bsum_ref[...] += fold_rows(gradient)

    pairs = zip((low_buf, scaled_buf), outs)
    return each_chunk(rows, chunk, [(*pair, sems.at[index]) for index, pair in enumerate(pairs)])


GELU_SCALE = 0.7978845608028654
GELU_CUBE = 0.044715


def gelu_and_slope(pre):
    square = pre * pre
    inner = pre * (GELU_SCALE + (GELU_SCALE * GELU_CUBE) * square)
    curve = jnp.tanh(inner)
    half = 0.5 + 0.5 * curve
    slope = half * (1.0 + pre * (1.0 - curve) * (GELU_SCALE + (3.0 * GELU_SCALE * GELU_CUBE) * square))
    return pre * half, slope


FFN_PART = FFN_UNIT // 2


def ffn_copies(pieces, ubuf, dbuf, usem, dsem):
    ups, downs = [], []
    order, _, _ = position()
    for index, refs in enumerate(pieces):
        wide = 2 * FFN_UNIT
        at = slice(index * wide, (index + 1) * wide)
        if len(refs) == 2:
            ups.append([copy_of(refs[0], ubuf.at[:, at], usem.at[index, 0])])
            downs.append([copy_of(refs[1], dbuf.at[at, :], dsem.at[index, 0])])
            continue
        ups.append([])
        downs.append([])
        rows = refs[0].shape[1]
        for quarter in range(4):
            up = refs[quarter].at[0]
            down = refs[quarter].at[1] if quarter < 3 else refs[4].at[0]
            place = (quarter ^ order) * rows
            ups[-1].append(copy_of(up, ubuf.at[pl.ds(pl.multiple_of(place, rows), rows), at], usem.at[index, quarter]))
            downs[-1].append(
                copy_of(down, dbuf.at[pl.ds(pl.multiple_of(index * wide + place, rows), rows), :], dsem.at[index, quarter])
            )
    return ups, downs


def ffn_fwd_call(inputs, pieces, partial, final):
    rows, depth = inputs.shape
    number = 2 * len(pieces)
    last, has_partial = final is not None, partial is not None

    def kernel(*refs):
        it = iter(refs)
        x_ref = next(it)
        if last:
            gain_old, bias_old, gain_ref, bias_ref = (next(it) for _ in range(4))
            late_in = [next(it), next(it)]
        part_in = next(it) if has_partial else None
        w_refs = [[next(it) for _ in piece] for piece in pieces]
        if last:
            norm_outs = [next(it) for _ in range(3)]
            gsum_ref, bsum_ref = next(it), next(it)
        else:
            sum_ref = next(it)
        act_ref, slope_ref = next(it), next(it)
        ubuf, dbuf, abuf, sbuf, pbuf, psem = (next(it) for _ in range(6))
        if last:
            acc, hat, cot, lsem, out_ref, low_ref, scaled_ref, nsem = (next(it) for _ in range(8))
        wsem, gsem = next(it), next(it)
        target = acc if last else sum_ref

        up_copies, down_copies = ffn_copies(w_refs, ubuf, dbuf, wsem.at[0], wsem.at[1])
        for copies in up_copies + down_copies:
            for copy in copies:
                copy.start()
        if has_partial:
            part_copy = copy_of(part_in, target, psem)
            part_copy.start()
        if last:
            late = [copy_of(late_in[0], hat, lsem.at[0]), copy_of(late_in[1], cot, lsem.at[1])]
            for copy in late:
                copy.start()
        saves = []

        def gate(pre, index):
            activated, slope = gelu_and_slope(pre)
            abuf[:, index * FFN_UNIT : (index + 1) * FFN_UNIT] = activated.astype(BF16)
            sbuf[:, index * FFN_UNIT : (index + 1) * FFN_UNIT] = slope.astype(BF16)

        for index in range(number):
            if index % 2 == 0:
                for copy in up_copies[index // 2]:
                    copy.wait()
            if index:
                gate(pbuf[(index - 1) % 2], index - 1)
            pbuf[index % 2] = dot(x_ref[...], ubuf[:, index * FFN_UNIT : (index + 1) * FFN_UNIT])
        gate(pbuf[(number - 1) % 2], number - 1)
        for index in range(number):
            at = slice(index * FFN_UNIT, (index + 1) * FFN_UNIT)
            saves += [
                copy_of(abuf.at[:, at], act_ref.at[index], gsem.at[0, index]),
                copy_of(sbuf.at[:, at], slope_ref.at[index], gsem.at[1, index]),
            ]
        for copy in saves:
            copy.start()
        for copies in down_copies:
            for copy in copies:
                copy.wait()
        if has_partial:
            part_copy.wait()
            target[...] += dot(abuf[...], dbuf[...])
        else:
            target[...] = dot(abuf[...], dbuf[...])
        if last:
            for copy in late:
                copy.wait()
            gsum_ref[...] = jnp.zeros_like(gsum_ref)
            bsum_ref[...] = jnp.zeros_like(bsum_ref)

            def chunk(at):
                old = hat[at, :] * gain_old[...] + bias_old[...]
                normed, xhat, inverse = norm_chunk(RESIDUAL_ALPHA * old + acc[at, :], gain_ref[...], bias_ref[...])
                out_ref[at, :] = normed.astype(BF16)
                gradient = cot[at, :].astype(F32)
                grad_in = norm_back_chunk(gradient, xhat, inverse, gain_ref[...])
                low_ref[at, :] = grad_in.astype(BF16)
                scaled_ref[at, :] = RESIDUAL_ALPHA * grad_in
                gsum_ref[...] += fold_rows(gradient * xhat)
                bsum_ref[...] += fold_rows(gradient)

            triples = zip((out_ref, low_ref, scaled_ref), norm_outs)
            saves += each_chunk(rows, chunk, [(*pair, nsem.at[index]) for index, pair in enumerate(triples)])
        for copy in saves:
            copy.wait()

    big, low = sds((rows, depth), F32), sds((rows, depth), BF16)
    if last:
        shapes = [low, low, big, sds((8, depth), F32), sds((8, depth), F32)]
    else:
        shapes = [big]
    specs_out = ([ANY] * 3 + [VMEM] * 2 if last else [VMEM]) + [ANY, ANY]
    shapes += [sds((number, rows, FFN_UNIT), BF16)] * 2
    args = [inputs]
    if last:
        args += [final[1], final[2], final[4], final[5]]
    specs = [VMEM] * len(args)
    tail = ([final[0], final[3]] if last else []) + ([partial] if has_partial else []) + [array for piece in pieces for array in piece]
    scratch = [
        pltpu.VMEM((depth, number * FFN_UNIT), BF16),
        pltpu.VMEM((number * FFN_UNIT, depth), BF16),
        pltpu.VMEM((rows, number * FFN_UNIT), BF16),
        pltpu.VMEM((rows, number * FFN_UNIT), BF16),
        pltpu.VMEM((2, rows, FFN_UNIT), F32),
        pltpu.SemaphoreType.DMA,
    ]
    if last:
        scratch += [
            pltpu.VMEM((rows, depth), F32),
            pltpu.VMEM((rows, depth), F32),
            pltpu.VMEM((rows, depth), BF16),
            pltpu.SemaphoreType.DMA((2,)),
            pltpu.VMEM((rows, depth), BF16),
            pltpu.VMEM((rows, depth), BF16),
            pltpu.VMEM((rows, depth), F32),
            pltpu.SemaphoreType.DMA((3,)),
        ]
    scratch += [pltpu.SemaphoreType.DMA((2, len(pieces), 4)), pltpu.SemaphoreType.DMA((2, number))]
    return pl.pallas_call(
        kernel,
        out_shape=shapes,
        in_specs=specs + [ANY] * len(tail),
        out_specs=specs_out,
        scratch_shapes=scratch,
        compiler_params=params(),
        cost_estimate=cost_of(12),
        name="ffn_fwd",
    )(*args, *tail)


def ffn_bwd_call(grad_low, inputs, pieces, saved, plan, carried, norm):
    rows, depth = inputs.shape
    number = len(plan)
    last = norm is not None

    def kernel(*refs):
        it = iter(refs)
        g_in, x_ref = next(it), next(it)
        gain_ref = next(it) if last else None
        late_in = [next(it), next(it)] if last else []
        acc_in = next(it)
        w_refs = [[next(it) for _ in piece] for piece in pieces]
        s_refs = [[next(it) for _ in call] for call in saved]
        if last:
            low_ref, scaled_ref, gsum_ref, bsum_ref = (next(it) for _ in range(4))
        else:
            sum_ref = next(it)
        g_ref = next(it)
        ubuf, dbuf, abuf, sbuf, gbuf, stage, psem = (next(it) for _ in range(7))
        if last:
            acc, hat, inv, lsem, low_buf, scaled_buf, nsem = (next(it) for _ in range(7))
        wsem, ssem, gsem = next(it), next(it), next(it)
        dp = lax.axis_index("dp")
        target = acc if last else sum_ref

        ups, downs = ffn_copies(w_refs, ubuf, dbuf, wsem.at[0], wsem.at[1])
        slopes, acts = [], []
        for index, (call, at) in enumerate(plan):
            lanes = slice(index * FFN_UNIT, (index + 1) * FFN_UNIT)
            slopes.append(copy_of(s_refs[call][1].at[at], sbuf.at[index], ssem.at[0, index]))
            acts.append(copy_of(s_refs[call][0].at[at], abuf.at[:, lanes], ssem.at[1, index]))
        for copies in downs + [slopes, acts] + ups:
            for copy in copies:
                copy.start()
        part_copy = copy_of(acc_in, target, psem)
        part_copy.start()
        if last:
            late = [copy_of(late_in[0], hat, lsem.at[0]), copy_of(late_in[1], inv, lsem.at[1])]
            for copy in late:
                copy.start()
        for index in range(number):
            if index % 2 == 0:
                for copy in downs[index // 2]:
                    copy.wait()
            slopes[index].wait()
            grad_act = dot_nt(g_in[...], dbuf[index * FFN_UNIT : (index + 1) * FFN_UNIT, :]) * sbuf[index].astype(F32)
            gbuf[:, index * FFN_UNIT : (index + 1) * FFN_UNIT] = grad_act.astype(BF16)
        for copy in acts:
            copy.wait()

        def keep(rows_in, source, column):
            for half in range(number // 2):
                wide = 2 * FFN_UNIT
                weight = dot_tn(rows_in[...], source[:, half * wide : (half + 1) * wide]).astype(BF16)
                for inner in range(4):
                    part = weight[:, inner * FFN_PART : (inner + 1) * FFN_PART]
                    store_shards(stage.at[2 * inner + column, half], part, dp)

        keep(x_ref, gbuf, 0)
        keep(g_in, abuf, 1)
        g_copies = [copy_of(stage, g_ref, gsem)]
        for copy in g_copies:
            copy.start()
        for copies in ups:
            for copy in copies:
                copy.wait()
        part_copy.wait()
        target[...] += dot_nt(gbuf[...], ubuf[...])
        if last:
            for copy in late:
                copy.wait()
            g_copies += norm_back_rows(
                acc, hat, inv, gain_ref, low_buf, scaled_buf, (low_ref, scaled_ref), nsem, gsum_ref, bsum_ref, rows
            )
        for copy in g_copies:
            copy.wait()

    big, low = sds((rows, depth), F32), sds((rows, depth), BF16)
    shapes = [low, big, sds((8, depth), F32), sds((8, depth), F32)] if last else [big]
    specs_out = ([ANY] * 2 + [VMEM] * 2 if last else [VMEM]) + [ANY]
    shapes.append(sds((8, number // 2, 8, UNIT, FFN_PART), BF16))
    args = [grad_low, inputs] + ([norm[2]] if last else [])
    specs = [VMEM] * len(args)
    tail = ([norm[0], norm[1]] if last else []) + [carried] + [array for piece in pieces for array in piece]
    for call in saved:
        tail += call
    scratch = [
        pltpu.VMEM((depth, number * FFN_UNIT), BF16),
        pltpu.VMEM((number * FFN_UNIT, depth), BF16),
        pltpu.VMEM((rows, number * FFN_UNIT), BF16),
        pltpu.VMEM((number, rows, FFN_UNIT), BF16),
        pltpu.VMEM((rows, number * FFN_UNIT), BF16),
        pltpu.VMEM((8, number // 2, 8, UNIT, FFN_PART), BF16),
        pltpu.SemaphoreType.DMA,
    ]
    if last:
        scratch += [
            pltpu.VMEM((rows, depth), F32),
            pltpu.VMEM((rows, depth), F32),
            pltpu.VMEM((rows, 128), F32),
            pltpu.SemaphoreType.DMA((2,)),
            pltpu.VMEM((rows, depth), BF16),
            pltpu.VMEM((rows, depth), F32),
            pltpu.SemaphoreType.DMA((2,)),
        ]
    scratch += [pltpu.SemaphoreType.DMA((2, len(pieces), 4)), pltpu.SemaphoreType.DMA((2, number)), pltpu.SemaphoreType.DMA]
    return pl.pallas_call(
        kernel,
        out_shape=shapes,
        in_specs=specs + [ANY] * len(tail),
        out_specs=specs_out,
        scratch_shapes=scratch,
        compiler_params=params(),
        cost_estimate=cost_of(17),
        name="ffn_bwd",
    )(*args, *tail)


def combine(jobs, shapes):
    arrays = []
    for terms, _, _, _ in jobs:
        for array, _ in terms:
            if not any(array is known for known in arrays):
                arrays.append(array)
    position = {id(array): index for index, array in enumerate(arrays)}

    def part_shape(array, index):
        kept = []
        for extent, at in zip(array.shape, index + (slice(None),) * (array.ndim - len(index))):
            if isinstance(at, slice):
                kept.append(len(range(*at.indices(extent))))
        return tuple(kept)

    part_shapes = [part_shape(*terms[0]) for terms, _, _, _ in jobs]
    count = sum(len(terms) for terms, _, _, _ in jobs)

    def kernel(*refs):
        ins, outs = refs[: len(arrays)], refs[len(arrays) : len(arrays) + len(shapes)]
        rest = refs[len(arrays) + len(shapes) :]
        term_bufs, sum_bufs, isem, osem = rest[:count], rest[count : count + len(jobs)], rest[-2], rest[-1]
        loads, number = [], 0
        for terms, _, _, _ in jobs:
            loads.append([])
            for array, index in terms:
                loads[-1].append(copy_of(ins[position[id(array)]].at[index], term_bufs[number], isem.at[number]))
                number += 1
        for group in loads:
            for copy in group:
                copy.start()
        stores, number = [], 0
        for job, (terms, out, place, kind) in enumerate(jobs):
            for copy in loads[job]:
                copy.wait()
            bufs = term_bufs[number : number + len(terms)]
            number += len(terms)
            lead = part_shapes[job][:-2]
            size = 1
            for extent in lead:
                size *= extent

            def one(flat, carry, bufs=bufs, lead=lead, target=sum_bufs[job]):
                index, left = [], flat
                for extent in reversed(lead):
                    index.append(lax.rem(left, extent))
                    left = lax.div(left, extent)
                index = tuple(reversed(index))
                total = bufs[0][index].astype(F32)
                for buf in bufs[1:]:
                    total = total + buf[index].astype(F32)
                target[index] = total.astype(target.dtype)
                return carry

            if kind == "range":
                lax.fori_loop(0, size, one, 0)
            else:
                total = bufs[0][0].astype(F32)
                for buf in bufs[1:]:
                    total = total + buf[0].astype(F32)
                sum_bufs[job][...] = jnp.transpose(total) if kind == "turned" else total
            stores.append(copy_of(sum_bufs[job], outs[out].at[place], osem.at[job]))
            stores[-1].start()
        for copy in stores:
            copy.wait()

    scratch = [pltpu.VMEM(part_shapes[job], array.dtype) for job, (terms, _, _, _) in enumerate(jobs) for array, _ in terms]
    for job, (_, out, _, kind) in enumerate(jobs):
        shape = part_shapes[job]
        shape = {"range": shape, "plain": shape[1:], "turned": shape[:0:-1]}[kind]
        scratch.append(pltpu.VMEM(shape, shapes[out].dtype))
    scratch += [pltpu.SemaphoreType.DMA((count,)), pltpu.SemaphoreType.DMA((len(jobs),))]
    return pl.pallas_call(
        kernel,
        out_shape=list(shapes),
        in_specs=[ANY] * len(arrays),
        out_specs=[ANY] * len(shapes),
        scratch_shapes=scratch,
        compiler_params=params(),
        cost_estimate=cost_of(3),
        name="combine",
    )(*arrays)


def swap_pairs(count, mask):
    return [(i, i ^ mask) for i in range(count)]


def to_sibling(values):
    return lax.ppermute(values, "tensor", swap_pairs(4, 1))


def over_y(values):
    return lax.ppermute(values, "tensor", swap_pairs(4, 2))


def over_dp(values, mask):
    return lax.ppermute(values, "dp", swap_pairs(8, mask))


def over_x(values):
    return over_dp(values, 1)


def over_z_near(values):
    return over_dp(values, 2)


def over_z_far(values):
    return over_dp(values, 4)


def after(values, *earlier):
    return lax.optimization_barrier((values, *earlier))[0]


MOVES = {"y": over_y, "x": over_x, "z": over_z_near}


class Reduction:
    def __init__(self, sent, portions, finish):
        self.other, self.finish = to_sibling(sent), finish
        self.portions, self.stage, self.sends, self.total = portions, 0, None, None

    def begin(self, kept, *earlier):
        other = after(self.other, *earlier)
        split = (kept.shape[0], 2, 2, 2, 2, *kept.shape[3:])
        arrays = (kept.reshape(split), other.reshape(split))
        self.blocks, self.tail = kept.shape[0], kept.shape[3:]
        self.terms = [[(array, ("b", "y", "x", "z", "w"), low, {}) for array in arrays] for low, _, _ in self.portions]

    def receive(self, *earlier):
        if self.stage == 4:
            moved = after(over_z_far(self.sends[0]), *earlier)
            for (low, _, _), terms in zip(self.portions, self.terms):
                terms.append((moved, ("b",), low, {}))
        elif self.stage:
            for send, (_, _, orders), terms in zip(self.sends, self.portions, self.terms):
                left = tuple(a for a in ("b", "y", "x", "z", "w") if a not in orders[: self.stage])
                terms.append((after(MOVES[orders[self.stage - 1]](send), *earlier), left, 0, {}))

    def jobs(self, first_out):
        jobs, shapes = [], []
        stage = self.stage
        for number, ((low, high, orders), terms) in enumerate(zip(self.portions, self.terms)):
            axis = (*orders, "w", None)[stage]
            picked = []
            for array, axes, start, fixed in terms:
                index = [slice(start, start + high - low)]
                for name in axes[1:]:
                    index.append(1 if name == axis else fixed.get(name, 0 if name in orders[:stage] or (stage > 3 and name == "w") else slice(None)))
                picked.append((array, tuple(index)))
            if stage < 3:
                shapes.append(sds((high - low, *(2,) * (3 - stage), *self.tail), BF16))
                jobs.append((picked, first_out + number, slice(0, high - low), "range"))
            elif stage == 3:
                if not number:
                    shapes.append(sds((self.blocks, *self.tail), BF16))
                jobs.append((picked, first_out, slice(low, high), "range"))
            else:
                if not number:
                    shapes += self.finish[0]
                for block in range(low, high):
                    shift = block - low
                    one = [(a, (slice(index[0].start + shift, index[0].start + shift + 1), *index[1:])) for a, index in picked]
                    out, place, kind = self.finish[1](block)
                    jobs.append((one, first_out + out, place, kind))
        self.stage += 1
        return jobs, shapes


def attention_finish(counts):
    stacks = [sds((count, UNIT, 2 * UNIT) if count > 1 else (UNIT, 2 * UNIT), F32) for count in counts]

    def place_of(block):
        half, matrix = block // 4, block % 4
        lanes = slice(half * UNIT, (half + 1) * UNIT)
        if matrix == 3:
            return len(counts), (lanes, slice(None)), "turned"
        stack = 0 if matrix < counts[0] else 1
        if counts[stack] == 1:
            return stack, (slice(None), lanes), "plain"
        return stack, (matrix - sum(counts[:stack]), slice(None), lanes), "plain"

    return [*stacks, sds((2 * UNIT, UNIT), F32)], place_of


def ffn_finish():
    def place_of(block):
        lanes = slice(block // 2 * FFN_PART, (block // 2 + 1) * FFN_PART)
        if block % 2:
            return 1, (lanes, slice(None)), "turned"
        return 0, (slice(None), lanes), "plain"

    return [sds((UNIT, 4 * FFN_PART), F32), sds((4 * FFN_PART, UNIT), F32)], place_of


def advance(reductions, *earlier):
    jobs, shapes, bounds = [], [], []
    for reduction in reductions:
        reduction.receive(*earlier)
        more, made = reduction.jobs(len(shapes))
        bounds.append((len(shapes), len(shapes) + len(made)))
        jobs, shapes = jobs + more, shapes + made
    results = combine(jobs, shapes)
    for reduction, (low, high) in zip(reductions, bounds):
        reduction.sends = list(results[low:high])
        if reduction.stage == 5:
            reduction.total = results[low:high]
    return list(results)


def sentence_body(
    tokens,
    memory,
    dec_lengths,
    mem_lengths,
    self_qkv,
    self_out,
    cross_q,
    cross_kv,
    cross_out,
    ffn_in,
    ffn_out,
    norm_gains,
    norm_biases,
    cotangent,
):
    dp = lax.axis_index("dp")
    order = dp & 3
    inner = (dp >> 1) & 1
    gains = [norm_gains[i : i + 1] for i in range(3)]
    biases = [norm_biases[i : i + 1] for i in range(3)]

    def part_rows(values, parts):
        rows = values.shape[-2] // parts
        place = order if parts == 4 else inner
        return lax.dynamic_slice_in_dim(values, place * rows, rows, values.ndim - 2)

    def folded(values):
        blocks = values.reshape(values.shape[0], 4, 2 * UNIT)
        return blocks.transpose(1, 0, 2).reshape(1, 4 * values.shape[0], 2 * UNIT)

    self_near = over_y(jnp.concatenate([part_rows(self_qkv, 4), folded(part_rows(self_out, 4))]))
    cross_near = over_y(
        jnp.concatenate([part_rows(cross_q, 2)[None], part_rows(cross_kv, 2), folded(part_rows(cross_out, 2))])
    )
    ffn_near = over_y(jnp.stack([part_rows(ffn_in, 4), part_rows(ffn_out, 4)]))
    self_own = (self_qkv, self_out)
    self_sib = tuple(to_sibling(w) for w in self_own)
    self_a = attention_fwd_call(dec_lengths, [], [tokens], [self_own, self_sib], None, None)
    self_near = after(self_near, self_a[4])
    self_side, self_up = over_x(self_near), over_z_near(self_near)
    self_corner = over_x(self_up)
    cross_own, ffn_own = (cross_q, cross_kv, cross_out), (ffn_in, ffn_out)
    cross_sib = tuple(to_sibling(w) for w in cross_own)
    cross_up = over_z_near(cross_near)
    self_rest = (self_near, self_side, self_up, after(self_corner, cross_near, *cross_sib))
    self_far = tuple(to_sibling(w) for w in self_rest)
    self_pieces = [self_own, self_sib, self_rest, self_far]
    self_b = attention_fwd_call(
        dec_lengths, [tokens], [tokens], self_pieces[2:], self_a[5], (gains[0], biases[0])
    )
    first_low, first_hat, first_inv = self_b[5:]
    cross_in = [first_low, memory]
    cross_rest = jnp.stack([cross_near, after(cross_up, self_b[4])])
    cross_far = to_sibling(cross_rest)
    ffn_sib = tuple(to_sibling(after(w, ffn_near)) for w in ffn_own)
    ffn_side, ffn_up = over_x(ffn_near), over_z_near(ffn_near)
    cross_pieces = [cross_own, cross_sib, (cross_rest,), (cross_far,)]
    cross_b = attention_fwd_call(
        mem_lengths, [first_hat, gains[0], biases[0]], [after(first_low, ffn_near), memory], cross_pieces, None,
        (gains[1], biases[1]),
    )
    second_low, second_hat, second_inv = cross_b[5:]
    ffn_side, ffn_up = after(ffn_side, cross_b[4]), after(ffn_up, cross_b[4])
    up_corner, down_corner = over_x(ffn_up[:1]), over_z_near(ffn_side[1:])
    ffn_pieces = [ffn_own, ffn_sib]
    ffn_a = ffn_fwd_call(second_low, ffn_pieces, None, None)
    up_corner, down_corner = after(up_corner, ffn_a[0]), after(down_corner, ffn_a[0])
    ffn_rest = (ffn_near, ffn_side, ffn_up, up_corner, down_corner)
    ffn_pieces += [ffn_rest, tuple(to_sibling(w) for w in ffn_rest)]
    ffn_b = ffn_fwd_call(
        second_low, ffn_pieces[2:], ffn_a[0],
        (second_hat, gains[1], biases[1], cotangent, gains[2], biases[2]),
    )
    out_rows, third_low, third_scaled, third_gain, third_bias = ffn_b[:5]

    def plan_of(pieces):
        return [(piece // 2, 2 * (piece % 2) + half) for piece in pieces for half in (0, 1)]

    ffn_saved = [ffn_a[1:3], ffn_b[5:7]]
    ffn_d = ffn_bwd_call(
        third_low, second_low, ffn_pieces[1::2], ffn_saved, plan_of((1, 3)), third_scaled, None
    )
    ffn_sum = Reduction(ffn_d[1], [(0, 3, "yzx"), (3, 6, "xyz"), (6, 8, "zxy")], ffn_finish())
    ffn_e = ffn_bwd_call(
        third_low, second_low, ffn_pieces[::2], ffn_saved, plan_of((0, 2)), ffn_d[0],
        (second_hat, second_inv, gains[1]),
    )
    second_back, second_scaled, second_gain, second_bias = ffn_e[:4]
    ffn_sum.begin(ffn_e[4], second_gain)
    second_back = after(second_back, *advance([ffn_sum]))

    cross_e = attention_bwd_call(
        mem_lengths, second_back, cross_in, cross_pieces[1::2] + cross_pieces[::2],
        [cross_b[:5]], [(0, 2 * p + half) for p in (1, 3, 0, 2) for half in (0, 1)], second_scaled,
        (first_hat, first_inv, gains[0]), 2,
    )
    first_back, first_scaled, first_gain, first_bias, memory_part = cross_e[:5]
    norm_sums = jnp.stack([first_gain, second_gain, third_gain, first_bias, second_bias, third_bias])
    norm_sums = jnp.concatenate([jnp.sum(norm_sums, axis=1), jnp.zeros((2, norm_sums.shape[2]), F32)])
    norm_sums = lax.all_gather(norm_sums, ("dp", "tensor"), axis=0)
    sends = advance([ffn_sum], first_gain)
    cross_sum = Reduction(after(cross_e[5], *sends), [(0, 4, "zyx"), (4, 8, "yxz")], attention_finish((1, 2)))
    first_back = after(first_back, *sends)

    self_saved = [self_a[:5], self_b[:5]]
    self_d = attention_bwd_call(
        dec_lengths, first_back, [tokens], self_pieces[1::2], self_saved, plan_of((1, 3)), None, None
    )
    cross_sum.begin(cross_e[6], self_d[0])
    sends = advance([cross_sum, ffn_sum], self_d[0])
    self_sum = Reduction(after(self_d[1], *sends), [(0, 4, "yxz"), (4, 8, "xzy")], attention_finish((3,)))
    first_back = after(first_back, *sends)
    self_e = attention_bwd_call(
        dec_lengths, first_back, [tokens], self_pieces[::2], self_saved, plan_of((0, 2)), None, None
    )
    self_sum.begin(self_e[1], self_e[0])
    sends = advance([self_sum])
    grad_tokens = inputs_back_call(
        after(first_scaled, *sends), [(self_d[0], self_pieces[1::2]), (self_e[0], self_pieces[::2])], (0, 1, 2)
    )
    sends = advance([cross_sum, ffn_sum], *sends)
    sends = advance([self_sum], *sends, grad_tokens)
    sends = advance([cross_sum, ffn_sum], *sends)
    sends = advance([self_sum], *sends)
    sends = advance([cross_sum], *sends)
    sends = advance([self_sum], *sends)
    grad_memory = inputs_back_call(
        None, [(after(memory_part, *sends), cross_pieces[1::2] + cross_pieces[::2])], (1, 2)
    )
    advance([cross_sum], *sends, grad_memory)
    norm_total = jnp.sum(after(norm_sums, grad_memory), axis=0)
    advance([self_sum], grad_memory)
    self_sum, cross_sum, ffn_sum = self_sum.total, cross_sum.total, ffn_sum.total

    return (
        out_rows,
        grad_tokens,
        grad_memory,
        *self_sum,
        *cross_sum,
        *ffn_sum,
        norm_total[:3],
        norm_total[3:6],
    )


def sentence_fits(mesh, tokens, memory, dec_lengths):
    shape = dict(mesh.shape)
    rows = tokens.shape[0] // mesh.size
    sentences = dec_lengths.shape[1]
    return (
        shape["tensor"] == 4
        and shape["dp"] == 8
        and sentences == 4
        and rows == 512
        and memory.shape[0] // mesh.size == rows
        and tokens.shape[1] == 1024
    )


def smooth_gate(values):
    return jax.nn.gelu(values, approximate=True)


def norm_rows(hidden, norm_gain, norm_bias):
    center = hidden - jnp.mean(hidden, axis=-1, keepdims=True)
    inverse = lax.rsqrt(jnp.mean(center * center, axis=-1, keepdims=True) + NORM_EPSILON)
    normed = center * inverse
    return (normed * norm_gain + norm_bias, normed, inverse)


def norm_back(gradient, normed, inverse, norm_gain):
    scaled = gradient * norm_gain
    grad_in = inverse * (
        scaled
        - jnp.mean(scaled, axis=-1, keepdims=True)
        - normed * jnp.mean(scaled * normed, axis=-1, keepdims=True)
    )
    return (grad_in, jnp.sum(gradient * normed, axis=0), jnp.sum(gradient, axis=0))


def head_view(values, sentences):
    return values.reshape(sentences, -1, values.shape[1] // HEAD_DIM, HEAD_DIM)


def masked_scores(query_heads, key_heads, key_mask):
    scores = jnp.einsum(
        "sqhe,skhe->shqk", query_heads, key_heads, preferred_element_type=jnp.float32
    ) * HEAD_DIM ** (-0.5)
    return jnp.where(key_mask, scores, MASKED_SCORE)


def attention_forward(query_rows, key_rows, value_rows, key_mask, sentences):
    scores = masked_scores(
        head_view(query_rows, sentences), head_view(key_rows, sentences), key_mask
    )
    row_peak = jnp.max(scores, axis=-1, keepdims=True)
    exponent_terms = jnp.exp(scores - row_peak)
    row_sum = jnp.sum(exponent_terms, axis=-1, keepdims=True)
    softmax_probs = exponent_terms / row_sum
    attended = jnp.einsum(
        "shqk,skhe->sqhe",
        softmax_probs.astype(jnp.bfloat16),
        head_view(value_rows, sentences),
        preferred_element_type=jnp.float32,
    ).astype(jnp.bfloat16)
    return (attended.reshape(query_rows.shape), row_peak + jnp.log(row_sum))


def attention_backward(query_rows, key_rows, value_rows, key_mask, log_total, grad_rows, sentences):
    query_heads = head_view(query_rows, sentences)
    key_heads = head_view(key_rows, sentences)
    value_heads = head_view(value_rows, sentences)
    grad_heads = head_view(grad_rows, sentences)
    softmax_probs = jnp.exp(masked_scores(query_heads, key_heads, key_mask) - log_total)
    grad_probs = jnp.einsum(
        "sqhe,skhe->shqk", grad_heads, value_heads, preferred_element_type=jnp.float32
    )
    row_delta = jnp.sum(softmax_probs * grad_probs, axis=-1, keepdims=True)
    grad_scores = (softmax_probs * (grad_probs - row_delta)).astype(jnp.bfloat16)
    score_scale = HEAD_DIM ** (-0.5)
    grad_query = (
        jnp.einsum("shqk,skhe->sqhe", grad_scores, key_heads, preferred_element_type=jnp.float32)
        * score_scale
    ).astype(jnp.bfloat16)
    grad_key = (
        jnp.einsum("shqk,sqhe->skhe", grad_scores, query_heads, preferred_element_type=jnp.float32)
        * score_scale
    ).astype(jnp.bfloat16)
    grad_value = jnp.einsum(
        "shqk,sqhe->skhe",
        softmax_probs.astype(jnp.bfloat16),
        grad_heads,
        preferred_element_type=jnp.float32,
    ).astype(jnp.bfloat16)
    return (
        grad_query.reshape(query_rows.shape),
        grad_key.reshape(key_rows.shape),
        grad_value.reshape(value_rows.shape),
    )


def body(
    tokens,
    memory,
    dec_lengths,
    mem_lengths,
    self_qkv,
    self_out,
    cross_q,
    cross_kv,
    cross_out,
    ffn_in,
    ffn_out,
    norm_gains,
    norm_biases,
    cotangent,
):
    row_share = tokens.shape[0]
    sentences = dec_lengths.shape[1]
    all_tokens, all_memory = (
        lax.all_gather(tokens, "tensor", axis=0, tiled=True),
        lax.all_gather(memory, "tensor", axis=0, tiled=True),
    )
    sentence_len = all_tokens.shape[0] // sentences
    memory_len = all_memory.shape[0] // sentences
    positions = jnp.arange(sentence_len, dtype=jnp.int32)
    self_mask = (
        (positions[None, :] <= positions[:, None])[None]
        & (positions[None, None, :] < dec_lengths[0][:, None, None])
    )[:, None]
    memory_positions = jnp.arange(memory_len, dtype=jnp.int32)
    cross_mask = (memory_positions[None, :] < mem_lengths[0][:, None])[:, None, None, :]

    def branch_rows(attended, weight):
        return lax.psum_scatter(
            jnp.dot(attended, weight, preferred_element_type=jnp.float32).astype(jnp.bfloat16),
            "tensor",
            scatter_dimension=0,
            tiled=True,
        ).astype(jnp.float32)

    def branch_grad(grad_rows, attended, weight):
        grad_low = grad_rows.astype(jnp.bfloat16)
        grad_all = lax.all_gather(grad_low, "tensor", axis=0, tiled=True)
        grad_attended = jnp.dot(grad_all, weight.T, preferred_element_type=jnp.float32).astype(
            jnp.bfloat16
        )
        weight_part = jnp.dot(attended.T, grad_all, preferred_element_type=jnp.float32)
        return (grad_attended, weight_part)

    def gather_normed(values):
        return lax.all_gather(values, "tensor", axis=0, tiled=True)

    def head_input_sum(term):
        return lax.psum_scatter(
            term(jnp.int32(0), row_share * lax.axis_size("tensor")).astype(jnp.bfloat16),
            "tensor",
            scatter_dimension=0,
            tiled=True,
        ).astype(jnp.float32)

    self_proj = jnp.einsum(
        "td,cde->cte", all_tokens, self_qkv, preferred_element_type=jnp.float32
    ).astype(jnp.bfloat16)
    self_att, self_lse = attention_forward(
        self_proj[0], self_proj[1], self_proj[2], self_mask, sentences
    )
    self_branch = branch_rows(self_att, self_out)
    first_norm, first_hat, first_inv = norm_rows(
        RESIDUAL_ALPHA * tokens.astype(jnp.float32) + self_branch, norm_gains[0], norm_biases[0]
    )
    first_all = gather_normed(first_norm.astype(jnp.bfloat16))
    cross_query = jnp.dot(first_all, cross_q, preferred_element_type=jnp.float32).astype(
        jnp.bfloat16
    )
    cross_proj = jnp.einsum(
        "td,cde->cte", all_memory, cross_kv, preferred_element_type=jnp.float32
    ).astype(jnp.bfloat16)
    cross_att, cross_lse = attention_forward(
        cross_query, cross_proj[0], cross_proj[1], cross_mask, sentences
    )
    cross_branch = branch_rows(cross_att, cross_out)
    second_norm, second_hat, second_inv = norm_rows(
        RESIDUAL_ALPHA * first_norm + cross_branch, norm_gains[1], norm_biases[1]
    )
    second_all = gather_normed(second_norm.astype(jnp.bfloat16))
    pre_gate = jnp.dot(second_all, ffn_in, preferred_element_type=jnp.float32)
    activated = smooth_gate(pre_gate).astype(jnp.bfloat16)
    ffn_branch = lax.psum_scatter(
        jnp.dot(activated, ffn_out, preferred_element_type=jnp.float32).astype(jnp.bfloat16),
        "tensor",
        scatter_dimension=0,
        tiled=True,
    ).astype(jnp.float32)
    out_rows, third_hat, third_inv = norm_rows(
        RESIDUAL_ALPHA * second_norm + ffn_branch, norm_gains[2], norm_biases[2]
    )
    grad_third, third_gain, third_bias = norm_back(
        cotangent.astype(jnp.float32), third_hat, third_inv, norm_gains[2]
    )
    grad_ffn_all = lax.all_gather(grad_third.astype(jnp.bfloat16), "tensor", axis=0, tiled=True)
    unused_gate, gate_pull = jax.vjp(smooth_gate, pre_gate)
    grad_act = gate_pull(jnp.dot(grad_ffn_all, ffn_out.T, preferred_element_type=jnp.float32))[
        0
    ].astype(jnp.bfloat16)
    grad_ffn_out = jnp.dot(activated.T, grad_ffn_all, preferred_element_type=jnp.float32)
    grad_ffn_in = jnp.dot(second_all.T, grad_act, preferred_element_type=jnp.float32)
    grad_second = RESIDUAL_ALPHA * grad_third + lax.psum_scatter(
        jnp.dot(grad_act, ffn_in.T, preferred_element_type=jnp.float32).astype(jnp.bfloat16),
        "tensor",
        scatter_dimension=0,
        tiled=True,
    ).astype(jnp.float32)
    grad_second_in, second_gain, second_bias = norm_back(
        grad_second, second_hat, second_inv, norm_gains[1]
    )
    grad_cross_att, cross_out_part = branch_grad(grad_second_in, cross_att, cross_out)
    grad_cq, grad_ck, grad_cv = attention_backward(
        cross_query, cross_proj[0], cross_proj[1], cross_mask, cross_lse, grad_cross_att, sentences
    )
    grad_cross_q = jnp.dot(first_all.T, grad_cq, preferred_element_type=jnp.float32)
    cross_grads = jnp.stack([grad_ck, grad_cv])
    grad_cross_kv = jnp.einsum(
        "td,cte->cde", all_memory, cross_grads, preferred_element_type=jnp.float32
    )
    grad_memory = lax.psum_scatter(
        jnp.einsum("cte,cde->td", cross_grads, cross_kv, preferred_element_type=jnp.float32).astype(
            jnp.bfloat16
        ),
        "tensor",
        scatter_dimension=0,
        tiled=True,
    ).astype(jnp.float32)

    def cross_input_term(first_row, row_total):
        return jnp.dot(grad_cq, cross_q.T, preferred_element_type=jnp.float32)

    cross_input = head_input_sum(cross_input_term)
    grad_first = RESIDUAL_ALPHA * grad_second_in + cross_input
    grad_first_in, first_gain, first_bias = norm_back(
        grad_first, first_hat, first_inv, norm_gains[0]
    )
    grad_self_att, self_out_part = branch_grad(grad_first_in, self_att, self_out)
    grad_sq, grad_sk, grad_sv = attention_backward(
        self_proj[0], self_proj[1], self_proj[2], self_mask, self_lse, grad_self_att, sentences
    )
    self_grads = jnp.stack([grad_sq, grad_sk, grad_sv])
    grad_self_qkv = jnp.einsum(
        "td,cte->cde", all_tokens, self_grads, preferred_element_type=jnp.float32
    )

    def self_input_term(first_row, row_total):
        return jnp.einsum("cte,cde->td", self_grads, self_qkv, preferred_element_type=jnp.float32)

    self_input = head_input_sum(self_input_term)
    grad_tokens = RESIDUAL_ALPHA * grad_first_in + self_input
    summed = (
        lax.psum_scatter(
            grad_self_qkv.astype(jnp.bfloat16), "dp", scatter_dimension=1, tiled=True
        ).astype(jnp.float32),
        lax.psum_scatter(
            self_out_part.astype(jnp.bfloat16), "dp", scatter_dimension=1, tiled=True
        ).astype(jnp.float32),
        lax.psum_scatter(
            grad_cross_q.astype(jnp.bfloat16), "dp", scatter_dimension=0, tiled=True
        ).astype(jnp.float32),
        lax.psum_scatter(
            grad_cross_kv.astype(jnp.bfloat16), "dp", scatter_dimension=1, tiled=True
        ).astype(jnp.float32),
        lax.psum_scatter(
            cross_out_part.astype(jnp.bfloat16), "dp", scatter_dimension=1, tiled=True
        ).astype(jnp.float32),
        lax.psum_scatter(
            grad_ffn_in.astype(jnp.bfloat16), "dp", scatter_dimension=0, tiled=True
        ).astype(jnp.float32),
        lax.psum_scatter(
            grad_ffn_out.astype(jnp.bfloat16), "dp", scatter_dimension=1, tiled=True
        ).astype(jnp.float32),
    )
    gain_total, bias_total = lax.psum(
        (
            jnp.stack([first_gain, second_gain, third_gain]),
            jnp.stack([first_bias, second_bias, third_bias]),
        ),
        ("dp", "tensor"),
    )
    return (
        out_rows.astype(jnp.bfloat16),
        grad_tokens,
        grad_memory,
        summed[0],
        summed[1],
        summed[2],
        summed[3],
        summed[4],
        summed[5],
        summed[6],
        gain_total,
        bias_total,
    )


def solution(mesh):
    in_specs = (
        P(("dp", "tensor"), None),
        P(("dp", "tensor"), None),
        P("dp", None),
        P("dp", None),
        P(None, None, "tensor"),
        P("tensor", None),
        P(None, "tensor"),
        P(None, None, "tensor"),
        P("tensor", None),
        P(None, "tensor"),
        P("tensor", None),
        P(),
        P(),
        P(("dp", "tensor"), None),
    )
    out_specs = (
        P(("dp", "tensor"), None),
        P(("dp", "tensor"), None),
        P(("dp", "tensor"), None),
        P(None, "dp", "tensor"),
        P("tensor", "dp"),
        P("dp", "tensor"),
        P(None, "dp", "tensor"),
        P("tensor", "dp"),
        P("dp", "tensor"),
        P("tensor", "dp"),
        P(),
        P(),
    )

    def step(*args):
        chosen = sentence_body if sentence_fits(mesh, args[0], args[1], args[2]) else body
        return jax.shard_map(
            chosen, mesh=mesh, in_specs=in_specs, out_specs=out_specs, check_vma=False
        )(*args)

    return step
```

```python
import functools
import jax
import jax.numpy as jnp
from jax import lax
from jax.experimental import pallas as pl
from jax.experimental.pallas import tpu as pltpu
from jax.sharding import PartitionSpec as P

HEAD_DIM = 64
RESIDUAL_ALPHA = 4.16
NORM_EPSILON = 1e-05
MASKED_SCORE = -1000000000.0
SCORE_SCALE = HEAD_DIM ** (-0.5)
UNIT = 128
QUERY_BLOCK = 256
FFN_UNIT = 512
ROW_CHUNK = 64
BF16 = jnp.bfloat16
F32 = jnp.float32


def dot(left, right):
    return lax.dot_general(left, right, (((1,), (0,)), ((), ())), preferred_element_type=F32)


def dot_tn(left, right):
    return lax.dot_general(left, right, (((0,), (0,)), ((), ())), preferred_element_type=F32)


def dot_nt(left, right):
    return lax.dot_general(left, right, (((1,), (1,)), ((), ())), preferred_element_type=F32)


def shard_of(position):
    return ((position >> 2) & 1) | (position & 2) | ((position & 1) << 2)


def copy_of(source, target, sem):
    return pltpu.make_async_copy(source, target, sem)


def own_lanes(rows, head):
    lanes = lax.broadcasted_iota(jnp.int32, rows.shape, 1)
    return jnp.where((lanes >= HEAD_DIM) if head else (lanes < HEAD_DIM), rows, 0.0)


def extended_keys(keys, length):
    lanes = lax.broadcasted_iota(jnp.int32, keys.shape, 1)
    rows = lax.broadcasted_iota(jnp.int32, keys.shape, 0)
    mask = jnp.where((lanes == 0) & (rows >= length), MASKED_SCORE, 0.0).astype(BF16)
    keys = keys.astype(F32)
    return [jnp.concatenate([own_lanes(keys, head).astype(BF16), mask], axis=1) for head in (0, 1)]


def extended_query(query):
    lanes = lax.broadcasted_iota(jnp.int32, query.shape, 1)
    return jnp.concatenate([query, jnp.where(lanes == 0, 1.0, 0.0).astype(BF16)], axis=1)


def fill_diagonal(diagonal):
    keys = lax.broadcasted_iota(jnp.int32, diagonal.shape, 0)
    queries = lax.broadcasted_iota(jnp.int32, diagonal.shape, 1)
    diagonal[...] = jnp.where(keys <= queries, 0.0, MASKED_SCORE)


def key_ranges(block, keys, causal):
    if not causal:
        return [(0, keys)]
    return [(low, low + QUERY_BLOCK) for low in range(0, (block + 1) * QUERY_BLOCK, QUERY_BLOCK)]


def attend_unit(query, keys, values, length, causal, diagonal, lse_ref):
    rows, count = query.shape[0], keys.shape[0]
    values_t = jnp.transpose(values.astype(F32)).astype(BF16)
    wide_keys, wide_query = extended_keys(keys, length), extended_query(query)
    items = [(head, block) for block in range(rows // QUERY_BLOCK) for head in (0, 1)]
    scores, probs, totals, mixed = {}, {}, {}, {}
    for head, block in items:
        part = wide_query[block * QUERY_BLOCK : (block + 1) * QUERY_BLOCK]
        ranges = key_ranges(block, count, causal)
        scores[head, block] = [dot_nt(wide_keys[head][a:b], part) for a, b in ranges]
        if causal:
            scores[head, block][-1] = scores[head, block][-1] + diagonal[...]
    for head, block in items:
        pieces = scores[head, block]
        peak = functools.reduce(jnp.maximum, [jnp.max(p, axis=0, keepdims=True) for p in pieces])
        terms = [jnp.exp(p - peak) for p in pieces]
        total = sum(jnp.sum(t, axis=0, keepdims=True) for t in terms)
        at = slice(block * QUERY_BLOCK, (block + 1) * QUERY_BLOCK)
        lse_ref[head : head + 1, at] = peak + jnp.log(total)
        totals[head, block] = total
        probs[head, block] = jnp.concatenate([t.astype(BF16) for t in terms], axis=0)
    for head, block in items:
        own = values_t[head * HEAD_DIM : (head + 1) * HEAD_DIM, : probs[head, block].shape[0]]
        mixed[head, block] = dot(own, probs[head, block]) / totals[head, block]
    out = [
        jnp.transpose(jnp.concatenate([mixed[0, block], mixed[1, block]], axis=0))
        for block in range(rows // QUERY_BLOCK)
    ]
    return jnp.concatenate(out, axis=0).astype(BF16)


def attend_back_unit(query, keys, values, attended, grad, length, causal, diagonal, lse_ref):
    rows, count = query.shape[0], keys.shape[0]
    blocks = range(rows // QUERY_BLOCK)
    query_f, keys_f, grad_f = (a.astype(F32) for a in (query, keys, grad))
    wide_keys, wide_query = extended_keys(keys, length), extended_query(query)
    delta = jnp.transpose(grad_f * attended.astype(F32))
    deltas = [
        jnp.sum(delta[head * HEAD_DIM : (head + 1) * HEAD_DIM], axis=0, keepdims=True)
        for head in (0, 1)
    ]
    keys_t = jnp.transpose(keys_f).astype(BF16)
    query_own = [own_lanes(query_f, head).astype(BF16) for head in (0, 1)]
    grad_own = [own_lanes(grad_f, head).astype(BF16) for head in (0, 1)]
    items = [(head, block) for block in blocks for head in (0, 1)]
    scores, slopes, probs, back, grad_query = {}, {}, {}, {}, {}
    for head, block in items:
        at = slice(block * QUERY_BLOCK, (block + 1) * QUERY_BLOCK)
        for a, b in key_ranges(block, count, causal):
            scores[head, block, a] = dot_nt(wide_keys[head][a:b], wide_query[at])
            slopes[head, block, a] = dot_nt(values[a:b], grad_own[head][at])
    for head, block in items:
        at = slice(block * QUERY_BLOCK, (block + 1) * QUERY_BLOCK)
        ranges = key_ranges(block, count, causal)
        for a, b in ranges:
            score = scores[head, block, a]
            if causal and (a, b) == ranges[-1]:
                score = score + diagonal[...]
            prob = jnp.exp(score - lse_ref[head : head + 1, at])
            probs[head, block, a] = prob.astype(BF16)
            back[head, block, a] = (prob * (slopes[head, block, a] - deltas[head][:, at])).astype(BF16)
    for head, block in items:
        own = keys_t[head * HEAD_DIM : (head + 1) * HEAD_DIM]
        grad_query[head, block] = sum(
            dot(own[:, a:b], back[head, block, a]) for a, b in key_ranges(block, count, causal)
        )
    grad_keys, grad_values = [], []
    for low in sorted({key[2] for key in back}):
        live = [key for key in back if key[2] == low]
        at = [slice(block * QUERY_BLOCK, (block + 1) * QUERY_BLOCK) for _, block, _ in live]
        grad_values.append(
            dot(
                jnp.concatenate([probs[key] for key in live], axis=1),
                jnp.concatenate([grad_own[key[0]][a] for key, a in zip(live, at)], axis=0),
            )
        )
        grad_keys.append(
            dot(
                jnp.concatenate([back[key] for key in live], axis=1),
                jnp.concatenate([query_own[key[0]][a] for key, a in zip(live, at)], axis=0),
            )
        )
    grad_query = [
        jnp.transpose(jnp.concatenate([grad_query[0, block], grad_query[1, block]], axis=0)) * SCORE_SCALE
        for block in blocks
    ]
    return tuple(
        jnp.concatenate(parts, axis=0).astype(BF16) for parts in (grad_query, grad_keys, grad_values)
    )


def norm_chunk(hidden, gain, bias):
    center = hidden - jnp.mean(hidden, axis=-1, keepdims=True)
    inverse = lax.rsqrt(jnp.mean(center * center, axis=-1, keepdims=True) + NORM_EPSILON)
    normed = center * inverse
    return normed * gain + bias, normed, inverse


def norm_back_chunk(gradient, normed, inverse, gain):
    scaled = gradient * gain
    return inverse * (
        scaled
        - jnp.mean(scaled, axis=-1, keepdims=True)
        - normed * jnp.mean(scaled * normed, axis=-1, keepdims=True)
    )


def fold_rows(values):
    return jnp.sum(values.reshape(values.shape[0] // 8, 8, values.shape[1]), axis=0)


def each_chunk(rows, body, results):
    def step(index, carry):
        at = pl.ds(pl.multiple_of(index * ROW_CHUNK, ROW_CHUNK), ROW_CHUNK)
        body(at)
        for buffer, out, sem in results:
            copy_of(buffer.at[at, :], out.at[at, :], sem).start()
        return carry

    lax.fori_loop(0, rows // ROW_CHUNK, step, 0)
    return [copy_of(*result) for result in results]


def store_shards(target, weight, dp):
    for block in range(8):
        target[shard_of(block ^ dp)] = weight[block * UNIT : (block + 1) * UNIT]


SMEM = pl.BlockSpec(memory_space=pltpu.SMEM)
VMEM = pl.BlockSpec(memory_space=pltpu.VMEM)
ANY = pl.BlockSpec(memory_space=pl.ANY)


def params(limit=62):
    return pltpu.CompilerParams(vmem_limit_bytes=limit * 1024 * 1024)


def cost_of(microseconds):
    return pl.CostEstimate(flops=int(microseconds * 1.1e9), bytes_accessed=4 << 20, transcendentals=0)


def sds(shape, dtype):
    return jax.ShapeDtypeStruct(shape, dtype)


def position():
    dp = lax.axis_index("dp")
    return dp & 3, dp, (dp >> 1) & 1


def weight_copies(pieces, wbuf, obuf, wsem, osem, columns=(0, 1, 2)):
    groups, outs = [[], [], []], []
    wide = 2 * UNIT
    order, _, inner = position()
    for index, refs in enumerate(pieces):
        at = slice(index * wide, (index + 1) * wide)
        if len(refs[-1].shape) == 2:
            column = 0
            for ref in refs[:-1]:
                for source in [ref] if len(ref.shape) == 2 else [ref.at[c] for c in range(ref.shape[0])]:
                    if column in columns:
                        low = (columns.index(column) * len(pieces) + index) * wide
                        groups[column].append(copy_of(source, wbuf.at[:, low : low + wide], wsem.at[column, index, 0]))
                    column += 1
            if obuf is not None:
                outs.append(copy_of(refs[-1], obuf.at[at, :], osem.at[index, 0]))
            continue
        parts = [refs[0].at[n] for n in range(refs[0].shape[0])] if len(refs[0].shape) == 4 else refs
        rows = parts[0].shape[1]
        part = wide // len(parts)
        for quarter, ref in enumerate(parts):
            place = quarter ^ (order if len(parts) == 4 else inner)
            for column in columns:
                low = (columns.index(column) * len(pieces) + index) * wide
                groups[column].append(
                    copy_of(
                        ref.at[column],
                        wbuf.at[pl.ds(pl.multiple_of(place * rows, rows), rows), low : low + wide],
                        wsem.at[column, index, quarter],
                    )
                )
            for block in range(4 if obuf is not None else 0):
                outs.append(
                    copy_of(
                        ref.at[3, block * part : (block + 1) * part, :],
                        obuf.at[pl.ds(pl.multiple_of(index * wide + place * part, part), part), block * wide : (block + 1) * wide],
                        osem.at[index, 4 * quarter + block],
                    )
                )
    return groups, outs


def attention_fwd_call(lengths, residual, others, pieces, partial, norm):
    rows, depth = others[0].shape
    causal = len(others) == 1
    number, wide = 2 * len(pieces), 2 * len(pieces) * UNIT
    last, has_partial = norm is not None, partial is not None

    def kernel(*refs):
        it = iter(refs)
        len_ref = next(it)
        in_refs = [next(it) for _ in others]
        gain_ref, bias_ref = (next(it), next(it)) if last else (None, None)
        old_rows = [next(it) for _ in residual[1:]] if last else []
        res_in = next(it) if last else None
        part_in = next(it) if has_partial else None
        w_refs = [[next(it) for _ in piece] for piece in pieces]
        unit_outs, lse_ref = [next(it) for _ in range(4)], next(it)
        if last:
            norm_outs = [next(it) for _ in range(3)]
        else:
            sum_ref = next(it)
        wbuf, obuf, att_all, diagonal, wsem, osem, lsem, usem = (next(it) for _ in range(8))
        q_ref, k_ref, v_ref, att_ref = (next(it) for _ in range(4))
        if last:
            acc, old, low_ref, hat_ref, inv_ref = (next(it) for _ in range(5))
        length = len_ref[0, lax.axis_index("tensor")]
        groups, outs = weight_copies(w_refs, wbuf, obuf, wsem, osem)
        for copies in groups + [outs]:
            for copy in copies:
                copy.start()
        target = acc if last else sum_ref
        late = []
        if has_partial:
            late.append(copy_of(part_in, target, lsem.at[0]))
        if last:
            late.append(copy_of(res_in, old, lsem.at[1]))
        for copy in late:
            copy.start()
        if causal:
            fill_diagonal(diagonal)
        for c, result in enumerate((q_ref, k_ref, v_ref)):
            for copy in groups[c]:
                copy.wait()
            rows_in = in_refs[0] if causal or c == 0 else in_refs[1]
            proj = dot(rows_in[...], wbuf[:, c * wide : (c + 1) * wide]).astype(BF16)
            if c == 0:
                proj = (proj.astype(F32) * SCORE_SCALE).astype(BF16)
            for index in range(number):
                result[index] = proj[:, index * UNIT : (index + 1) * UNIT]

        flushes = [copy_of(*pair, usem.at[index]) for index, pair in enumerate(zip((q_ref, k_ref, v_ref, att_ref), unit_outs))]
        for copy in flushes[:3]:
            copy.start()

        def step(first, carry):
            for u in [first * 4 + inner for inner in range(4)]:
                attended = attend_unit(q_ref[u], k_ref[u], v_ref[u], length, causal, diagonal, lse_ref.at[u])
                att_ref[u] = attended
                att_all[:, pl.ds(pl.multiple_of(u * UNIT, UNIT), UNIT)] = attended
            return carry

        lax.fori_loop(0, number // 4, step, 0)
        flushes[3].start()
        for copy in outs + late:
            copy.wait()
        if has_partial:
            target[...] += dot(att_all[...], obuf[...])
        else:
            target[...] = dot(att_all[...], obuf[...])
        if last:
            def chunk(at):
                before = old[at, :].astype(F32)
                if old_rows:
                    before = before * old_rows[0][...] + old_rows[1][...]
                normed, hat, inverse = norm_chunk(RESIDUAL_ALPHA * before + acc[at, :], gain_ref[...], bias_ref[...])
                low_ref[at, :] = normed.astype(BF16)
                hat_ref[at, :] = hat
                inv_ref[at, :] = jnp.broadcast_to(inverse, (ROW_CHUNK, 128))

            triples = zip((low_ref, hat_ref, inv_ref), norm_outs)
            flushes += each_chunk(rows, chunk, [(*pair, usem.at[4 + index]) for index, pair in enumerate(triples)])
        for copy in flushes:
            copy.wait()

    unit_rows = sds((number, rows, UNIT), BF16)
    shapes = [unit_rows] * 4 + [sds((number, 2, rows), F32)]
    if last:
        shapes += [sds((rows, depth), BF16), sds((rows, depth), F32), sds((rows, 128), F32)]
    else:
        shapes += [sds((rows, depth), F32)]
    args = [lengths, *others]
    if last:
        args += [*norm, *residual[1:]]
    tail = ([residual[0]] if last else []) + ([partial] if has_partial else [])
    tail += [array for piece in pieces for array in piece]
    scratch = [
        pltpu.VMEM((depth, 3 * wide), BF16),
        pltpu.VMEM((wide, depth), BF16),
        pltpu.VMEM((rows, wide), BF16),
        pltpu.VMEM((QUERY_BLOCK, QUERY_BLOCK), F32),
        pltpu.SemaphoreType.DMA((3, len(pieces), 4)),
        pltpu.SemaphoreType.DMA((len(pieces), 16)),
        pltpu.SemaphoreType.DMA((2,)),
        pltpu.SemaphoreType.DMA((7,)),
    ]
    scratch += [pltpu.VMEM((number, rows, UNIT), BF16)] * 4
    if last:
        scratch += [pltpu.VMEM((rows, depth), F32), pltpu.VMEM((rows, depth), residual[0].dtype)]
        scratch += [pltpu.VMEM((rows, depth), BF16), pltpu.VMEM((rows, depth), F32), pltpu.VMEM((rows, 128), F32)]
    return pl.pallas_call(
        kernel,
        out_shape=shapes,
        in_specs=[SMEM] + [VMEM] * (len(args) - 1) + [ANY] * len(tail),
        out_specs=[ANY] * 4 + [VMEM] + ([ANY] * 3 if last else [VMEM]),
        scratch_shapes=scratch,
        compiler_params=params(),
        cost_estimate=cost_of(0.6 * number),
        name="self_fwd" if causal else "cross_fwd",
    )(*args, *tail)


def attention_bwd_call(lengths, grad_low, others, pieces, saved, plan, carried, norm, results=1):
    rows, depth = grad_low.shape
    causal = len(others) == 1
    number, n_in, wide = len(plan), len(others), len(plan) * UNIT
    last = norm is not None
    skip = 1 if last else 0

    def kernel(*refs):
        it = iter(refs)
        len_ref = next(it)
        h_ref = next(it)
        in_refs = [next(it) for _ in range(n_in)]
        gain_ref = next(it) if last else None
        late_in = [next(it), next(it)] if last else []
        acc_in = next(it) if last else None
        w_refs = [[next(it) for _ in piece] for piece in pieces]
        s_refs = [[next(it) for _ in call] for call in saved]
        if last:
            low_ref, scaled_ref, gsum_ref, bsum_ref = (next(it) for _ in range(4))
        dall_ref = next(it)
        g_refs = [next(it) for _ in range(results)]
        wbuf, obuf, sbuf, lbuf, att_all, grad_all = (next(it) for _ in range(6))
        stage, diagonal = next(it), next(it)
        if last:
            dquery, acc, hat, inv, low_buf, scaled_buf, nsem = (next(it) for _ in range(7))
        wsem, osem, ssem, gsem, lsem = (next(it) for _ in range(5))
        length, dp = len_ref[0, lax.axis_index("tensor")], lax.axis_index("dp")

        groups, o_copies = weight_copies(w_refs, wbuf, obuf, wsem, osem, (0,) if last else ())
        for copy in o_copies:
            copy.start()
        s_copies = []
        for index, unit in enumerate(plan):
            lanes = slice(index * UNIT, (index + 1) * UNIT)
            call = s_refs[unit[0]]
            for c in range(3):
                s_copies.append(copy_of(call[c].at[unit[1]], sbuf.at[index, c], ssem.at[c, index]))
            s_copies.append(copy_of(call[3].at[unit[1]], att_all.at[:, lanes], ssem.at[3, index]))
            s_copies.append(copy_of(call[4].at[unit[1]], lbuf.at[index], ssem.at[4, index]))
        late = []
        if last:
            late = groups[0] + [
                copy_of(source, target, lsem.at[index])
                for index, (source, target) in enumerate(((acc_in, acc), (late_in[0], hat), (late_in[1], inv)))
            ]
        for copy in s_copies + late:
            copy.start()
        if causal:
            fill_diagonal(diagonal)
        for copy in o_copies:
            copy.wait()
        grad_att = dot_nt(h_ref[...], obuf[...]).astype(BF16)
        for index in range(number):
            grad_all[index] = grad_att[:, index * UNIT : (index + 1) * UNIT]
        for copy in s_copies:
            copy.wait()

        def step(first, carry):
            units = [first * 2, first * 2 + 1]
            ats = [pl.ds(pl.multiple_of(u * UNIT, UNIT), UNIT) for u in units]
            parts = [
                attend_back_unit(
                    sbuf[u, 0], sbuf[u, 1], sbuf[u, 2], att_all[:, at], grad_all[u], length, causal, diagonal, lbuf.at[u]
                )
                for u, at in zip(units, ats)
            ]
            for u, at, part in zip(units, ats, parts):
                if last:
                    dquery[:, at] = part[0]
                for c in range(skip, 3):
                    dall_ref[:, pl.ds(pl.multiple_of((c - skip) * wide + u * UNIT, UNIT), UNIT)] = part[c]
            return carry

        lax.fori_loop(0, number // 2, step, 0)
        share = number // 2 // results

        def keep(rows_in, source, column):
            weight = dot_tn(rows_in[...], source).astype(BF16)
            for index in range(number):
                piece = index // 2
                target = stage.at[piece // share, (index % 2) * 4 + column, piece % share]
                store_shards(target, weight[:, index * UNIT : (index + 1) * UNIT], dp)

        if last:
            keep(in_refs[0], dquery[...], 0)
        for c in range(skip, 3):
            keep(in_refs[-1], dall_ref[:, (c - skip) * wide : (c - skip + 1) * wide], c)
        keep(h_ref, att_all[...], 3)
        g_copies = [copy_of(stage.at[index], ref, gsem.at[index]) for index, ref in enumerate(g_refs)]
        for copy in g_copies:
            copy.start()
        for copy in late:
            copy.wait()
        if last:
            acc[...] += dot_nt(dquery[...], wbuf[...])
            g_copies += norm_back_rows(
                acc, hat, inv, gain_ref, low_buf, scaled_buf, (low_ref, scaled_ref), nsem, gsum_ref, bsum_ref, rows
            )
        for copy in g_copies:
            copy.wait()

    big = sds((rows, depth), F32)
    shapes = []
    if last:
        shapes += [sds((rows, depth), BF16), big, sds((8, depth), F32), sds((8, depth), F32)]
    shapes.append(sds((rows, (3 - skip) * wide), BF16))
    specs_out = ([ANY] * 2 + [VMEM] * 3 if last else [VMEM]) + [ANY] * results
    shapes += [sds((8, number // 2 // results, 8, UNIT, UNIT), BF16)] * results
    args = [lengths, grad_low, *others] + ([norm[2]] if last else [])
    tail = [norm[0], norm[1], carried] if last else []
    tail += [array for piece in pieces for array in piece]
    for call in saved:
        tail += call
    scratch = [
        pltpu.VMEM((depth, wide) if last else (16, 128), BF16),
        pltpu.VMEM((wide, depth), BF16),
        pltpu.VMEM((number, 3, rows, UNIT), BF16),
        pltpu.VMEM((number, 2, rows), F32),
        pltpu.VMEM((rows, wide), BF16),
        pltpu.VMEM((number, rows, UNIT), BF16),
        pltpu.VMEM((results, 8, number // 2 // results, 8, UNIT, UNIT), BF16),
        pltpu.VMEM((QUERY_BLOCK, QUERY_BLOCK), F32),
    ]
    if last:
        scratch += [pltpu.VMEM((rows, wide), BF16), pltpu.VMEM((rows, depth), F32), pltpu.VMEM((rows, depth), F32), pltpu.VMEM((rows, 128), F32)]
        scratch += [pltpu.VMEM((rows, depth), BF16), pltpu.VMEM((rows, depth), F32), pltpu.SemaphoreType.DMA((2,))]
    scratch += [
        pltpu.SemaphoreType.DMA((3, len(pieces), 4)),
        pltpu.SemaphoreType.DMA((len(pieces), 16)),
        pltpu.SemaphoreType.DMA((5, number)),
        pltpu.SemaphoreType.DMA((results,)),
        pltpu.SemaphoreType.DMA((4,)),
    ]
    return pl.pallas_call(
        kernel,
        out_shape=shapes,
        in_specs=[SMEM] + [VMEM] * (len(args) - 1) + [ANY] * len(tail),
        out_specs=specs_out,
        scratch_shapes=scratch,
        compiler_params=params(),
        cost_estimate=cost_of(4.2 * number),
        name="self_bwd" if causal else "cross_bwd",
    )(*args, *tail)


def inputs_back_call(base, parts, columns):
    rows, depth = parts[0][0].shape[0], parts[0][1][0][0].shape[-2]

    def kernel(*refs):
        it = iter(refs)
        base_ref = next(it) if base is not None else None
        grads = [next(it) for _ in parts]
        w_refs = [[[next(it) for _ in piece] for piece in pieces] for _, pieces in parts]
        out = next(it)
        bufs, sems = [next(it) for _ in parts], [next(it) for _ in parts]
        copies = []
        for index in range(len(parts)):
            groups, _ = weight_copies(w_refs[index], bufs[index], None, sems[index], None, columns)
            copies.append([copy for group in groups for copy in group])
            for copy in copies[-1]:
                copy.start()
        if base is not None:
            out[...] = base_ref[...]
        for index in range(len(parts)):
            for copy in copies[index]:
                copy.wait()
            if index or base is not None:
                out[...] += dot_nt(grads[index][...], bufs[index][...])
            else:
                out[...] = dot_nt(grads[index][...], bufs[index][...])

    args = ([base] if base is not None else []) + [grad for grad, _ in parts]
    tail = [array for _, pieces in parts for piece in pieces for array in piece]
    return pl.pallas_call(
        kernel,
        out_shape=sds((rows, depth), F32),
        in_specs=[VMEM] * len(args) + [ANY] * len(tail),
        out_specs=VMEM,
        scratch_shapes=[pltpu.VMEM((depth, grad.shape[1]), BF16) for grad, _ in parts]
        + [pltpu.SemaphoreType.DMA((3, len(pieces), 4)) for _, pieces in parts],
        compiler_params=params(),
        cost_estimate=cost_of(7),
        name="inputs_back",
    )(*args, *tail)


def norm_back_rows(acc, hat, inv, gain_ref, low_buf, scaled_buf, outs, sems, gsum_ref, bsum_ref, rows):
    gsum_ref[...] = jnp.zeros_like(gsum_ref)
    bsum_ref[...] = jnp.zeros_like(bsum_ref)

    def chunk(at):
        gradient, normed = acc[at, :], hat[at, :]
        grad_in = norm_back_chunk(gradient, normed, inv[at, :1], gain_ref[...])
        low_buf[at, :] = grad_in.astype(BF16)
        scaled_buf[at, :] = RESIDUAL_ALPHA * grad_in
        gsum_ref[...] += fold_rows(gradient * normed)
        bsum_ref[...] += fold_rows(gradient)

    pairs = zip((low_buf, scaled_buf), outs)
    return each_chunk(rows, chunk, [(*pair, sems.at[index]) for index, pair in enumerate(pairs)])


GELU_SCALE = 0.7978845608028654
GELU_CUBE = 0.044715


def gelu_and_slope(pre):
    square = pre * pre
    inner = pre * (GELU_SCALE + (GELU_SCALE * GELU_CUBE) * square)
    curve = jnp.tanh(inner)
    half = 0.5 + 0.5 * curve
    slope = half * (1.0 + pre * (1.0 - curve) * (GELU_SCALE + (3.0 * GELU_SCALE * GELU_CUBE) * square))
    return pre * half, slope


FFN_PART = FFN_UNIT // 2


def ffn_copies(pieces, ubuf, dbuf, usem, dsem):
    ups, downs = [], []
    order, _, _ = position()
    for index, refs in enumerate(pieces):
        wide = 2 * FFN_UNIT
        at = slice(index * wide, (index + 1) * wide)
        if len(refs) == 2:
            ups.append([copy_of(refs[0], ubuf.at[:, at], usem.at[index, 0])])
            downs.append([copy_of(refs[1], dbuf.at[at, :], dsem.at[index, 0])])
            continue
        ups.append([])
        downs.append([])
        rows = refs[0].shape[1]
        for quarter in range(4):
            up = refs[quarter].at[0]
            down = refs[quarter].at[1] if quarter < 3 else refs[4].at[0]
            place = (quarter ^ order) * rows
            ups[-1].append(copy_of(up, ubuf.at[pl.ds(pl.multiple_of(place, rows), rows), at], usem.at[index, quarter]))
            downs[-1].append(
                copy_of(down, dbuf.at[pl.ds(pl.multiple_of(index * wide + place, rows), rows), :], dsem.at[index, quarter])
            )
    return ups, downs


def ffn_fwd_call(inputs, pieces, partial, final):
    rows, depth = inputs.shape
    number = 2 * len(pieces)
    last, has_partial = final is not None, partial is not None

    def kernel(*refs):
        it = iter(refs)
        x_ref = next(it)
        if last:
            gain_old, bias_old, gain_ref, bias_ref = (next(it) for _ in range(4))
            late_in = [next(it), next(it)]
        part_in = next(it) if has_partial else None
        w_refs = [[next(it) for _ in piece] for piece in pieces]
        if last:
            norm_outs = [next(it) for _ in range(3)]
            gsum_ref, bsum_ref = next(it), next(it)
        else:
            sum_ref = next(it)
        act_ref, slope_ref = next(it), next(it)
        ubuf, dbuf, abuf, sbuf, pbuf, psem = (next(it) for _ in range(6))
        if last:
            acc, hat, cot, lsem, out_ref, low_ref, scaled_ref, nsem = (next(it) for _ in range(8))
        wsem, gsem = next(it), next(it)
        target = acc if last else sum_ref

        up_copies, down_copies = ffn_copies(w_refs, ubuf, dbuf, wsem.at[0], wsem.at[1])
        for copies in up_copies + down_copies:
            for copy in copies:
                copy.start()
        if has_partial:
            part_copy = copy_of(part_in, target, psem)
            part_copy.start()
        if last:
            late = [copy_of(late_in[0], hat, lsem.at[0]), copy_of(late_in[1], cot, lsem.at[1])]
            for copy in late:
                copy.start()
        saves = []

        def gate(pre, index):
            activated, slope = gelu_and_slope(pre)
            abuf[:, index * FFN_UNIT : (index + 1) * FFN_UNIT] = activated.astype(BF16)
            sbuf[:, index * FFN_UNIT : (index + 1) * FFN_UNIT] = slope.astype(BF16)

        for index in range(number):
            if index % 2 == 0:
                for copy in up_copies[index // 2]:
                    copy.wait()
            if index:
                gate(pbuf[(index - 1) % 2], index - 1)
            pbuf[index % 2] = dot(x_ref[...], ubuf[:, index * FFN_UNIT : (index + 1) * FFN_UNIT])
        gate(pbuf[(number - 1) % 2], number - 1)
        for index in range(number):
            at = slice(index * FFN_UNIT, (index + 1) * FFN_UNIT)
            saves += [
                copy_of(abuf.at[:, at], act_ref.at[index], gsem.at[0, index]),
                copy_of(sbuf.at[:, at], slope_ref.at[index], gsem.at[1, index]),
            ]
        for copy in saves:
            copy.start()
        for copies in down_copies:
            for copy in copies:
                copy.wait()
        if has_partial:
            part_copy.wait()
            target[...] += dot(abuf[...], dbuf[...])
        else:
            target[...] = dot(abuf[...], dbuf[...])
        if last:
            for copy in late:
                copy.wait()
            gsum_ref[...] = jnp.zeros_like(gsum_ref)
            bsum_ref[...] = jnp.zeros_like(bsum_ref)

            def chunk(at):
                old = hat[at, :] * gain_old[...] + bias_old[...]
                normed, xhat, inverse = norm_chunk(RESIDUAL_ALPHA * old + acc[at, :], gain_ref[...], bias_ref[...])
                out_ref[at, :] = normed.astype(BF16)
                gradient = cot[at, :].astype(F32)
                grad_in = norm_back_chunk(gradient, xhat, inverse, gain_ref[...])
                low_ref[at, :] = grad_in.astype(BF16)
                scaled_ref[at, :] = RESIDUAL_ALPHA * grad_in
                gsum_ref[...] += fold_rows(gradient * xhat)
                bsum_ref[...] += fold_rows(gradient)

            triples = zip((out_ref, low_ref, scaled_ref), norm_outs)
            saves += each_chunk(rows, chunk, [(*pair, nsem.at[index]) for index, pair in enumerate(triples)])
        for copy in saves:
            copy.wait()

    big, low = sds((rows, depth), F32), sds((rows, depth), BF16)
    if last:
        shapes = [low, low, big, sds((8, depth), F32), sds((8, depth), F32)]
    else:
        shapes = [big]
    specs_out = ([ANY] * 3 + [VMEM] * 2 if last else [VMEM]) + [ANY, ANY]
    shapes += [sds((number, rows, FFN_UNIT), BF16)] * 2
    args = [inputs]
    if last:
        args += [final[1], final[2], final[4], final[5]]
    specs = [VMEM] * len(args)
    tail = ([final[0], final[3]] if last else []) + ([partial] if has_partial else []) + [array for piece in pieces for array in piece]
    scratch = [
        pltpu.VMEM((depth, number * FFN_UNIT), BF16),
        pltpu.VMEM((number * FFN_UNIT, depth), BF16),
        pltpu.VMEM((rows, number * FFN_UNIT), BF16),
        pltpu.VMEM((rows, number * FFN_UNIT), BF16),
        pltpu.VMEM((2, rows, FFN_UNIT), F32),
        pltpu.SemaphoreType.DMA,
    ]
    if last:
        scratch += [
            pltpu.VMEM((rows, depth), F32),
            pltpu.VMEM((rows, depth), F32),
            pltpu.VMEM((rows, depth), BF16),
            pltpu.SemaphoreType.DMA((2,)),
            pltpu.VMEM((rows, depth), BF16),
            pltpu.VMEM((rows, depth), BF16),
            pltpu.VMEM((rows, depth), F32),
            pltpu.SemaphoreType.DMA((3,)),
        ]
    scratch += [pltpu.SemaphoreType.DMA((2, len(pieces), 4)), pltpu.SemaphoreType.DMA((2, number))]
    return pl.pallas_call(
        kernel,
        out_shape=shapes,
        in_specs=specs + [ANY] * len(tail),
        out_specs=specs_out,
        scratch_shapes=scratch,
        compiler_params=params(),
        cost_estimate=cost_of(12),
        name="ffn_fwd",
    )(*args, *tail)


def ffn_bwd_call(grad_low, inputs, pieces, saved, plan, carried, norm):
    rows, depth = inputs.shape
    number = len(plan)
    last = norm is not None

    def kernel(*refs):
        it = iter(refs)
        g_in, x_ref = next(it), next(it)
        gain_ref = next(it) if last else None
        late_in = [next(it), next(it)] if last else []
        acc_in = next(it)
        w_refs = [[next(it) for _ in piece] for piece in pieces]
        s_refs = [[next(it) for _ in call] for call in saved]
        if last:
            low_ref, scaled_ref, gsum_ref, bsum_ref = (next(it) for _ in range(4))
        else:
            sum_ref = next(it)
        g_ref = next(it)
        ubuf, dbuf, abuf, sbuf, gbuf, stage, psem = (next(it) for _ in range(7))
        if last:
            acc, hat, inv, lsem, low_buf, scaled_buf, nsem = (next(it) for _ in range(7))
        wsem, ssem, gsem = next(it), next(it), next(it)
        dp = lax.axis_index("dp")
        target = acc if last else sum_ref

        ups, downs = ffn_copies(w_refs, ubuf, dbuf, wsem.at[0], wsem.at[1])
        slopes, acts = [], []
        for index, (call, at) in enumerate(plan):
            lanes = slice(index * FFN_UNIT, (index + 1) * FFN_UNIT)
            slopes.append(copy_of(s_refs[call][1].at[at], sbuf.at[index], ssem.at[0, index]))
            acts.append(copy_of(s_refs[call][0].at[at], abuf.at[:, lanes], ssem.at[1, index]))
        for copies in downs + [slopes, acts] + ups:
            for copy in copies:
                copy.start()
        part_copy = copy_of(acc_in, target, psem)
        part_copy.start()
        if last:
            late = [copy_of(late_in[0], hat, lsem.at[0]), copy_of(late_in[1], inv, lsem.at[1])]
            for copy in late:
                copy.start()
        for index in range(number):
            if index % 2 == 0:
                for copy in downs[index // 2]:
                    copy.wait()
            slopes[index].wait()
            grad_act = dot_nt(g_in[...], dbuf[index * FFN_UNIT : (index + 1) * FFN_UNIT, :]) * sbuf[index].astype(F32)
            gbuf[:, index * FFN_UNIT : (index + 1) * FFN_UNIT] = grad_act.astype(BF16)
        for copy in acts:
            copy.wait()

        def keep(rows_in, source, column):
            for half in range(number // 2):
                wide = 2 * FFN_UNIT
                weight = dot_tn(rows_in[...], source[:, half * wide : (half + 1) * wide]).astype(BF16)
                for inner in range(4):
                    part = weight[:, inner * FFN_PART : (inner + 1) * FFN_PART]
                    store_shards(stage.at[2 * inner + column, half], part, dp)

        keep(x_ref, gbuf, 0)
        keep(g_in, abuf, 1)
        g_copies = [copy_of(stage, g_ref, gsem)]
        for copy in g_copies:
            copy.start()
        for copies in ups:
            for copy in copies:
                copy.wait()
        part_copy.wait()
        target[...] += dot_nt(gbuf[...], ubuf[...])
        if last:
            for copy in late:
                copy.wait()
            g_copies += norm_back_rows(
                acc, hat, inv, gain_ref, low_buf, scaled_buf, (low_ref, scaled_ref), nsem, gsum_ref, bsum_ref, rows
            )
        for copy in g_copies:
            copy.wait()

    big, low = sds((rows, depth), F32), sds((rows, depth), BF16)
    shapes = [low, big, sds((8, depth), F32), sds((8, depth), F32)] if last else [big]
    specs_out = ([ANY] * 2 + [VMEM] * 2 if last else [VMEM]) + [ANY]
    shapes.append(sds((8, number // 2, 8, UNIT, FFN_PART), BF16))
    args = [grad_low, inputs] + ([norm[2]] if last else [])
    specs = [VMEM] * len(args)
    tail = ([norm[0], norm[1]] if last else []) + [carried] + [array for piece in pieces for array in piece]
    for call in saved:
        tail += call
    scratch = [
        pltpu.VMEM((depth, number * FFN_UNIT), BF16),
        pltpu.VMEM((number * FFN_UNIT, depth), BF16),
        pltpu.VMEM((rows, number * FFN_UNIT), BF16),
        pltpu.VMEM((number, rows, FFN_UNIT), BF16),
        pltpu.VMEM((rows, number * FFN_UNIT), BF16),
        pltpu.VMEM((8, number // 2, 8, UNIT, FFN_PART), BF16),
        pltpu.SemaphoreType.DMA,
    ]
    if last:
        scratch += [
            pltpu.VMEM((rows, depth), F32),
            pltpu.VMEM((rows, depth), F32),
            pltpu.VMEM((rows, 128), F32),
            pltpu.SemaphoreType.DMA((2,)),
            pltpu.VMEM((rows, depth), BF16),
            pltpu.VMEM((rows, depth), F32),
            pltpu.SemaphoreType.DMA((2,)),
        ]
    scratch += [pltpu.SemaphoreType.DMA((2, len(pieces), 4)), pltpu.SemaphoreType.DMA((2, number)), pltpu.SemaphoreType.DMA]
    return pl.pallas_call(
        kernel,
        out_shape=shapes,
        in_specs=specs + [ANY] * len(tail),
        out_specs=specs_out,
        scratch_shapes=scratch,
        compiler_params=params(),
        cost_estimate=cost_of(17),
        name="ffn_bwd",
    )(*args, *tail)


def combine(jobs, shapes):
    arrays = []
    for terms, _, _, _ in jobs:
        for array, _ in terms:
            if not any(array is known for known in arrays):
                arrays.append(array)
    position = {id(array): index for index, array in enumerate(arrays)}

    def part_shape(array, index):
        kept = []
        for extent, at in zip(array.shape, index + (slice(None),) * (array.ndim - len(index))):
            if isinstance(at, slice):
                kept.append(len(range(*at.indices(extent))))
        return tuple(kept)

    part_shapes = [part_shape(*terms[0]) for terms, _, _, _ in jobs]
    count = sum(len(terms) for terms, _, _, _ in jobs)

    def kernel(*refs):
        ins, outs = refs[: len(arrays)], refs[len(arrays) : len(arrays) + len(shapes)]
        rest = refs[len(arrays) + len(shapes) :]
        term_bufs, sum_bufs, isem, osem = rest[:count], rest[count : count + len(jobs)], rest[-2], rest[-1]
        loads, number = [], 0
        for terms, _, _, _ in jobs:
            loads.append([])
            for array, index in terms:
                loads[-1].append(copy_of(ins[position[id(array)]].at[index], term_bufs[number], isem.at[number]))
                number += 1
        for group in loads:
            for copy in group:
                copy.start()
        stores, number = [], 0
        for job, (terms, out, place, kind) in enumerate(jobs):
            for copy in loads[job]:
                copy.wait()
            bufs = term_bufs[number : number + len(terms)]
            number += len(terms)
            lead = part_shapes[job][:-2]
            size = 1
            for extent in lead:
                size *= extent

            def one(flat, carry, bufs=bufs, lead=lead, target=sum_bufs[job]):
                index, left = [], flat
                for extent in reversed(lead):
                    index.append(lax.rem(left, extent))
                    left = lax.div(left, extent)
                index = tuple(reversed(index))
                total = bufs[0][index].astype(F32)
                for buf in bufs[1:]:
                    total = total + buf[index].astype(F32)
                target[index] = total.astype(target.dtype)
                return carry

            if kind == "range":
                lax.fori_loop(0, size, one, 0)
            else:
                total = bufs[0][0].astype(F32)
                for buf in bufs[1:]:
                    total = total + buf[0].astype(F32)
                sum_bufs[job][...] = jnp.transpose(total) if kind == "turned" else total
            stores.append(copy_of(sum_bufs[job], outs[out].at[place], osem.at[job]))
            stores[-1].start()
        for copy in stores:
            copy.wait()

    scratch = [pltpu.VMEM(part_shapes[job], array.dtype) for job, (terms, _, _, _) in enumerate(jobs) for array, _ in terms]
    for job, (_, out, _, kind) in enumerate(jobs):
        shape = part_shapes[job]
        shape = {"range": shape, "plain": shape[1:], "turned": shape[:0:-1]}[kind]
        scratch.append(pltpu.VMEM(shape, shapes[out].dtype))
    scratch += [pltpu.SemaphoreType.DMA((count,)), pltpu.SemaphoreType.DMA((len(jobs),))]
    return pl.pallas_call(
        kernel,
        out_shape=list(shapes),
        in_specs=[ANY] * len(arrays),
        out_specs=[ANY] * len(shapes),
        scratch_shapes=scratch,
        compiler_params=params(),
        cost_estimate=cost_of(3),
        name="combine",
    )(*arrays)


def swap_pairs(count, mask):
    return [(i, i ^ mask) for i in range(count)]


def to_sibling(values):
    return lax.ppermute(values, "tensor", swap_pairs(4, 1))


def over_y(values):
    return lax.ppermute(values, "tensor", swap_pairs(4, 2))


def over_dp(values, mask):
    return lax.ppermute(values, "dp", swap_pairs(8, mask))


def over_x(values):
    return over_dp(values, 1)


def over_z_near(values):
    return over_dp(values, 2)


def over_z_far(values):
    return over_dp(values, 4)


def after(values, *earlier):
    return lax.optimization_barrier((values, *earlier))[0]


MOVES = {"y": over_y, "x": over_x, "z": over_z_near}


class Reduction:
    def __init__(self, sent, portions, finish):
        self.other, self.finish = to_sibling(sent), finish
        self.portions, self.stage, self.sends, self.total = portions, 0, None, None

    def begin(self, kept, *earlier):
        other = after(self.other, *earlier)
        split = (kept.shape[0], 2, 2, 2, 2, *kept.shape[3:])
        arrays = (kept.reshape(split), other.reshape(split))
        self.blocks, self.tail = kept.shape[0], kept.shape[3:]
        self.terms = [[(array, ("b", "y", "x", "z", "w"), low, {}) for array in arrays] for low, _, _ in self.portions]

    def receive(self, *earlier):
        if self.stage == 4:
            moved = after(over_z_far(self.sends[0]), *earlier)
            for (low, _, _), terms in zip(self.portions, self.terms):
                terms.append((moved, ("b",), low, {}))
        elif self.stage:
            for send, (_, _, orders), terms in zip(self.sends, self.portions, self.terms):
                left = tuple(a for a in ("b", "y", "x", "z", "w") if a not in orders[: self.stage])
                terms.append((after(MOVES[orders[self.stage - 1]](send), *earlier), left, 0, {}))

    def jobs(self, first_out):
        jobs, shapes = [], []
        stage = self.stage
        for number, ((low, high, orders), terms) in enumerate(zip(self.portions, self.terms)):
            axis = (*orders, "w", None)[stage]
            picked = []
            for array, axes, start, fixed in terms:
                index = [slice(start, start + high - low)]
                for name in axes[1:]:
                    index.append(1 if name == axis else fixed.get(name, 0 if name in orders[:stage] or (stage > 3 and name == "w") else slice(None)))
                picked.append((array, tuple(index)))
            if stage < 3:
                shapes.append(sds((high - low, *(2,) * (3 - stage), *self.tail), BF16))
                jobs.append((picked, first_out + number, slice(0, high - low), "range"))
            elif stage == 3:
                if not number:
                    shapes.append(sds((self.blocks, *self.tail), BF16))
                jobs.append((picked, first_out, slice(low, high), "range"))
            else:
                if not number:
                    shapes += self.finish[0]
                for block in range(low, high):
                    shift = block - low
                    one = [(a, (slice(index[0].start + shift, index[0].start + shift + 1), *index[1:])) for a, index in picked]
                    out, place, kind = self.finish[1](block)
                    jobs.append((one, first_out + out, place, kind))
        self.stage += 1
        return jobs, shapes


def attention_finish(counts):
    stacks = [sds((count, UNIT, 2 * UNIT) if count > 1 else (UNIT, 2 * UNIT), F32) for count in counts]

    def place_of(block):
        half, matrix = block // 4, block % 4
        lanes = slice(half * UNIT, (half + 1) * UNIT)
        if matrix == 3:
            return len(counts), (lanes, slice(None)), "turned"
        stack = 0 if matrix < counts[0] else 1
        if counts[stack] == 1:
            return stack, (slice(None), lanes), "plain"
        return stack, (matrix - sum(counts[:stack]), slice(None), lanes), "plain"

    return [*stacks, sds((2 * UNIT, UNIT), F32)], place_of


def ffn_finish():
    def place_of(block):
        lanes = slice(block // 2 * FFN_PART, (block // 2 + 1) * FFN_PART)
        if block % 2:
            return 1, (lanes, slice(None)), "turned"
        return 0, (slice(None), lanes), "plain"

    return [sds((UNIT, 4 * FFN_PART), F32), sds((4 * FFN_PART, UNIT), F32)], place_of


def advance(reductions, *earlier):
    jobs, shapes, bounds = [], [], []
    for reduction in reductions:
        reduction.receive(*earlier)
        more, made = reduction.jobs(len(shapes))
        bounds.append((len(shapes), len(shapes) + len(made)))
        jobs, shapes = jobs + more, shapes + made
    results = combine(jobs, shapes)
    for reduction, (low, high) in zip(reductions, bounds):
        reduction.sends = list(results[low:high])
        if reduction.stage == 5:
            reduction.total = results[low:high]
    return list(results)


def sentence_body(
    tokens,
    memory,
    dec_lengths,
    mem_lengths,
    self_qkv,
    self_out,
    cross_q,
    cross_kv,
    cross_out,
    ffn_in,
    ffn_out,
    norm_gains,
    norm_biases,
    cotangent,
):
    dp = lax.axis_index("dp")
    order = dp & 3
    inner = (dp >> 1) & 1
    gains = [norm_gains[i : i + 1] for i in range(3)]
    biases = [norm_biases[i : i + 1] for i in range(3)]

    def part_rows(values, parts):
        rows = values.shape[-2] // parts
        place = order if parts == 4 else inner
        return lax.dynamic_slice_in_dim(values, place * rows, rows, values.ndim - 2)

    def folded(values):
        blocks = values.reshape(values.shape[0], 4, 2 * UNIT)
        return blocks.transpose(1, 0, 2).reshape(1, 4 * values.shape[0], 2 * UNIT)

    self_near = over_y(jnp.concatenate([part_rows(self_qkv, 4), folded(part_rows(self_out, 4))]))
    cross_near = over_y(
        jnp.concatenate([part_rows(cross_q, 2)[None], part_rows(cross_kv, 2), folded(part_rows(cross_out, 2))])
    )
    ffn_near = over_y(jnp.stack([part_rows(ffn_in, 4), part_rows(ffn_out, 4)]))
    self_own = (self_qkv, self_out)
    self_sib = tuple(to_sibling(w) for w in self_own)
    self_a = attention_fwd_call(dec_lengths, [], [tokens], [self_own, self_sib], None, None)
    self_near = after(self_near, self_a[4])
    self_side, self_up = over_x(self_near), over_z_near(self_near)
    self_corner = over_x(self_up)
    cross_own, ffn_own = (cross_q, cross_kv, cross_out), (ffn_in, ffn_out)
    cross_sib = tuple(to_sibling(w) for w in cross_own)
    cross_up = over_z_near(cross_near)
    self_rest = (self_near, self_side, self_up, after(self_corner, cross_near, *cross_sib))
    self_far = tuple(to_sibling(w) for w in self_rest)
    self_pieces = [self_own, self_sib, self_rest, self_far]
    self_b = attention_fwd_call(
        dec_lengths, [tokens], [tokens], self_pieces[2:], self_a[5], (gains[0], biases[0])
    )
    first_low, first_hat, first_inv = self_b[5:]
    cross_in = [first_low, memory]
    cross_rest = jnp.stack([cross_near, after(cross_up, self_b[4])])
    cross_far = to_sibling(cross_rest)
    ffn_sib = tuple(to_sibling(after(w, ffn_near)) for w in ffn_own)
    ffn_side, ffn_up = over_x(ffn_near), over_z_near(ffn_near)
    cross_pieces = [cross_own, cross_sib, (cross_rest,), (cross_far,)]
    cross_b = attention_fwd_call(
        mem_lengths, [first_hat, gains[0], biases[0]], [after(first_low, ffn_near), memory], cross_pieces, None,
        (gains[1], biases[1]),
    )
    second_low, second_hat, second_inv = cross_b[5:]
    ffn_side, ffn_up = after(ffn_side, cross_b[4]), after(ffn_up, cross_b[4])
    up_corner, down_corner = over_x(ffn_up[:1]), over_z_near(ffn_side[1:])
    ffn_pieces = [ffn_own, ffn_sib]
    ffn_a = ffn_fwd_call(second_low, ffn_pieces, None, None)
    up_corner, down_corner = after(up_corner, ffn_a[0]), after(down_corner, ffn_a[0])
    ffn_rest = (ffn_near, ffn_side, ffn_up, up_corner, down_corner)
    ffn_pieces += [ffn_rest, tuple(to_sibling(w) for w in ffn_rest)]
    ffn_b = ffn_fwd_call(
        second_low, ffn_pieces[2:], ffn_a[0],
        (second_hat, gains[1], biases[1], cotangent, gains[2], biases[2]),
    )
    out_rows, third_low, third_scaled, third_gain, third_bias = ffn_b[:5]

    def plan_of(pieces):
        return [(piece // 2, 2 * (piece % 2) + half) for piece in pieces for half in (0, 1)]

    ffn_saved = [ffn_a[1:3], ffn_b[5:7]]
    ffn_d = ffn_bwd_call(
        third_low, second_low, ffn_pieces[1::2], ffn_saved, plan_of((1, 3)), third_scaled, None
    )
    ffn_sum = Reduction(ffn_d[1], [(0, 3, "yzx"), (3, 6, "xyz"), (6, 8, "zxy")], ffn_finish())
    ffn_e = ffn_bwd_call(
        third_low, second_low, ffn_pieces[::2], ffn_saved, plan_of((0, 2)), ffn_d[0],
        (second_hat, second_inv, gains[1]),
    )
    second_back, second_scaled, second_gain, second_bias = ffn_e[:4]
    ffn_sum.begin(ffn_e[4], second_gain)
    second_back = after(second_back, *advance([ffn_sum]))

    cross_e = attention_bwd_call(
        mem_lengths, second_back, cross_in, cross_pieces[1::2] + cross_pieces[::2],
        [cross_b[:5]], [(0, 2 * p + half) for p in (1, 3, 0, 2) for half in (0, 1)], second_scaled,
        (first_hat, first_inv, gains[0]), 2,
    )
    first_back, first_scaled, first_gain, first_bias, memory_part = cross_e[:5]
    norm_sums = jnp.stack([first_gain, second_gain, third_gain, first_bias, second_bias, third_bias])
    norm_sums = jnp.concatenate([jnp.sum(norm_sums, axis=1), jnp.zeros((2, norm_sums.shape[2]), F32)])
    norm_sums = lax.all_gather(norm_sums, ("dp", "tensor"), axis=0)
    sends = advance([ffn_sum], first_gain)
    cross_sum = Reduction(after(cross_e[5], *sends), [(0, 4, "zyx"), (4, 8, "yxz")], attention_finish((1, 2)))
    first_back = after(first_back, *sends)

    self_saved = [self_a[:5], self_b[:5]]
    self_d = attention_bwd_call(
        dec_lengths, first_back, [tokens], self_pieces[1::2], self_saved, plan_of((1, 3)), None, None
    )
    cross_sum.begin(cross_e[6], self_d[0])
    sends = advance([cross_sum, ffn_sum], self_d[0])
    self_sum = Reduction(after(self_d[1], *sends), [(0, 4, "yxz"), (4, 8, "xzy")], attention_finish((3,)))
    first_back = after(first_back, *sends)
    self_e = attention_bwd_call(
        dec_lengths, first_back, [tokens], self_pieces[::2], self_saved, plan_of((0, 2)), None, None
    )
    self_sum.begin(self_e[1], self_e[0])
    sends = advance([self_sum])
    grad_tokens = inputs_back_call(
        after(first_scaled, *sends), [(self_d[0], self_pieces[1::2]), (self_e[0], self_pieces[::2])], (0, 1, 2)
    )
    sends = advance([cross_sum, ffn_sum], *sends)
    sends = advance([self_sum], *sends, grad_tokens)
    norm_total = jnp.sum(after(norm_sums, *sends), axis=0)
    sends = advance([cross_sum, ffn_sum], *sends, norm_total)
    sends = advance([self_sum], *sends)
    sends = advance([cross_sum], *sends)
    sends = advance([self_sum], *sends)
    grad_memory = inputs_back_call(
        None, [(after(memory_part, *sends), cross_pieces[1::2] + cross_pieces[::2])], (1, 2)
    )
    advance([cross_sum], *sends, grad_memory)
    advance([self_sum], grad_memory)
    self_sum, cross_sum, ffn_sum = self_sum.total, cross_sum.total, ffn_sum.total

    return (
        out_rows,
        grad_tokens,
        grad_memory,
        *self_sum,
        *cross_sum,
        *ffn_sum,
        norm_total[:3],
        norm_total[3:6],
    )


def sentence_fits(mesh, tokens, memory, dec_lengths):
    shape = dict(mesh.shape)
    rows = tokens.shape[0] // mesh.size
    sentences = dec_lengths.shape[1]
    return (
        shape["tensor"] == 4
        and shape["dp"] == 8
        and sentences == 4
        and rows == 512
        and memory.shape[0] // mesh.size == rows
        and tokens.shape[1] == 1024
    )


def smooth_gate(values):
    return jax.nn.gelu(values, approximate=True)


def norm_rows(hidden, norm_gain, norm_bias):
    center = hidden - jnp.mean(hidden, axis=-1, keepdims=True)
    inverse = lax.rsqrt(jnp.mean(center * center, axis=-1, keepdims=True) + NORM_EPSILON)
    normed = center * inverse
    return (normed * norm_gain + norm_bias, normed, inverse)


def norm_back(gradient, normed, inverse, norm_gain):
    scaled = gradient * norm_gain
    grad_in = inverse * (
        scaled
        - jnp.mean(scaled, axis=-1, keepdims=True)
        - normed * jnp.mean(scaled * normed, axis=-1, keepdims=True)
    )
    return (grad_in, jnp.sum(gradient * normed, axis=0), jnp.sum(gradient, axis=0))


def head_view(values, sentences):
    return values.reshape(sentences, -1, values.shape[1] // HEAD_DIM, HEAD_DIM)


def masked_scores(query_heads, key_heads, key_mask):
    scores = jnp.einsum(
        "sqhe,skhe->shqk", query_heads, key_heads, preferred_element_type=jnp.float32
    ) * HEAD_DIM ** (-0.5)
    return jnp.where(key_mask, scores, MASKED_SCORE)


def attention_forward(query_rows, key_rows, value_rows, key_mask, sentences):
    scores = masked_scores(
        head_view(query_rows, sentences), head_view(key_rows, sentences), key_mask
    )
    row_peak = jnp.max(scores, axis=-1, keepdims=True)
    exponent_terms = jnp.exp(scores - row_peak)
    row_sum = jnp.sum(exponent_terms, axis=-1, keepdims=True)
    softmax_probs = exponent_terms / row_sum
    attended = jnp.einsum(
        "shqk,skhe->sqhe",
        softmax_probs.astype(jnp.bfloat16),
        head_view(value_rows, sentences),
        preferred_element_type=jnp.float32,
    ).astype(jnp.bfloat16)
    return (attended.reshape(query_rows.shape), row_peak + jnp.log(row_sum))


def attention_backward(query_rows, key_rows, value_rows, key_mask, log_total, grad_rows, sentences):
    query_heads = head_view(query_rows, sentences)
    key_heads = head_view(key_rows, sentences)
    value_heads = head_view(value_rows, sentences)
    grad_heads = head_view(grad_rows, sentences)
    softmax_probs = jnp.exp(masked_scores(query_heads, key_heads, key_mask) - log_total)
    grad_probs = jnp.einsum(
        "sqhe,skhe->shqk", grad_heads, value_heads, preferred_element_type=jnp.float32
    )
    row_delta = jnp.sum(softmax_probs * grad_probs, axis=-1, keepdims=True)
    grad_scores = (softmax_probs * (grad_probs - row_delta)).astype(jnp.bfloat16)
    score_scale = HEAD_DIM ** (-0.5)
    grad_query = (
        jnp.einsum("shqk,skhe->sqhe", grad_scores, key_heads, preferred_element_type=jnp.float32)
        * score_scale
    ).astype(jnp.bfloat16)
    grad_key = (
        jnp.einsum("shqk,sqhe->skhe", grad_scores, query_heads, preferred_element_type=jnp.float32)
        * score_scale
    ).astype(jnp.bfloat16)
    grad_value = jnp.einsum(
        "shqk,sqhe->skhe",
        softmax_probs.astype(jnp.bfloat16),
        grad_heads,
        preferred_element_type=jnp.float32,
    ).astype(jnp.bfloat16)
    return (
        grad_query.reshape(query_rows.shape),
        grad_key.reshape(key_rows.shape),
        grad_value.reshape(value_rows.shape),
    )


def body(
    tokens,
    memory,
    dec_lengths,
    mem_lengths,
    self_qkv,
    self_out,
    cross_q,
    cross_kv,
    cross_out,
    ffn_in,
    ffn_out,
    norm_gains,
    norm_biases,
    cotangent,
):
    row_share = tokens.shape[0]
    sentences = dec_lengths.shape[1]
    all_tokens, all_memory = (
        lax.all_gather(tokens, "tensor", axis=0, tiled=True),
        lax.all_gather(memory, "tensor", axis=0, tiled=True),
    )
    sentence_len = all_tokens.shape[0] // sentences
    memory_len = all_memory.shape[0] // sentences
    positions = jnp.arange(sentence_len, dtype=jnp.int32)
    self_mask = (
        (positions[None, :] <= positions[:, None])[None]
        & (positions[None, None, :] < dec_lengths[0][:, None, None])
    )[:, None]
    memory_positions = jnp.arange(memory_len, dtype=jnp.int32)
    cross_mask = (memory_positions[None, :] < mem_lengths[0][:, None])[:, None, None, :]

    def branch_rows(attended, weight):
        return lax.psum_scatter(
            jnp.dot(attended, weight, preferred_element_type=jnp.float32).astype(jnp.bfloat16),
            "tensor",
            scatter_dimension=0,
            tiled=True,
        ).astype(jnp.float32)

    def branch_grad(grad_rows, attended, weight):
        grad_low = grad_rows.astype(jnp.bfloat16)
        grad_all = lax.all_gather(grad_low, "tensor", axis=0, tiled=True)
        grad_attended = jnp.dot(grad_all, weight.T, preferred_element_type=jnp.float32).astype(
            jnp.bfloat16
        )
        weight_part = jnp.dot(attended.T, grad_all, preferred_element_type=jnp.float32)
        return (grad_attended, weight_part)

    def gather_normed(values):
        return lax.all_gather(values, "tensor", axis=0, tiled=True)

    def head_input_sum(term):
        return lax.psum_scatter(
            term(jnp.int32(0), row_share * lax.axis_size("tensor")).astype(jnp.bfloat16),
            "tensor",
            scatter_dimension=0,
            tiled=True,
        ).astype(jnp.float32)

    self_proj = jnp.einsum(
        "td,cde->cte", all_tokens, self_qkv, preferred_element_type=jnp.float32
    ).astype(jnp.bfloat16)
    self_att, self_lse = attention_forward(
        self_proj[0], self_proj[1], self_proj[2], self_mask, sentences
    )
    self_branch = branch_rows(self_att, self_out)
    first_norm, first_hat, first_inv = norm_rows(
        RESIDUAL_ALPHA * tokens.astype(jnp.float32) + self_branch, norm_gains[0], norm_biases[0]
    )
    first_all = gather_normed(first_norm.astype(jnp.bfloat16))
    cross_query = jnp.dot(first_all, cross_q, preferred_element_type=jnp.float32).astype(
        jnp.bfloat16
    )
    cross_proj = jnp.einsum(
        "td,cde->cte", all_memory, cross_kv, preferred_element_type=jnp.float32
    ).astype(jnp.bfloat16)
    cross_att, cross_lse = attention_forward(
        cross_query, cross_proj[0], cross_proj[1], cross_mask, sentences
    )
    cross_branch = branch_rows(cross_att, cross_out)
    second_norm, second_hat, second_inv = norm_rows(
        RESIDUAL_ALPHA * first_norm + cross_branch, norm_gains[1], norm_biases[1]
    )
    second_all = gather_normed(second_norm.astype(jnp.bfloat16))
    pre_gate = jnp.dot(second_all, ffn_in, preferred_element_type=jnp.float32)
    activated = smooth_gate(pre_gate).astype(jnp.bfloat16)
    ffn_branch = lax.psum_scatter(
        jnp.dot(activated, ffn_out, preferred_element_type=jnp.float32).astype(jnp.bfloat16),
        "tensor",
        scatter_dimension=0,
        tiled=True,
    ).astype(jnp.float32)
    out_rows, third_hat, third_inv = norm_rows(
        RESIDUAL_ALPHA * second_norm + ffn_branch, norm_gains[2], norm_biases[2]
    )
    grad_third, third_gain, third_bias = norm_back(
        cotangent.astype(jnp.float32), third_hat, third_inv, norm_gains[2]
    )
    grad_ffn_all = lax.all_gather(grad_third.astype(jnp.bfloat16), "tensor", axis=0, tiled=True)
    unused_gate, gate_pull = jax.vjp(smooth_gate, pre_gate)
    grad_act = gate_pull(jnp.dot(grad_ffn_all, ffn_out.T, preferred_element_type=jnp.float32))[
        0
    ].astype(jnp.bfloat16)
    grad_ffn_out = jnp.dot(activated.T, grad_ffn_all, preferred_element_type=jnp.float32)
    grad_ffn_in = jnp.dot(second_all.T, grad_act, preferred_element_type=jnp.float32)
    grad_second = RESIDUAL_ALPHA * grad_third + lax.psum_scatter(
        jnp.dot(grad_act, ffn_in.T, preferred_element_type=jnp.float32).astype(jnp.bfloat16),
        "tensor",
        scatter_dimension=0,
        tiled=True,
    ).astype(jnp.float32)
    grad_second_in, second_gain, second_bias = norm_back(
        grad_second, second_hat, second_inv, norm_gains[1]
    )
    grad_cross_att, cross_out_part = branch_grad(grad_second_in, cross_att, cross_out)
    grad_cq, grad_ck, grad_cv = attention_backward(
        cross_query, cross_proj[0], cross_proj[1], cross_mask, cross_lse, grad_cross_att, sentences
    )
    grad_cross_q = jnp.dot(first_all.T, grad_cq, preferred_element_type=jnp.float32)
    cross_grads = jnp.stack([grad_ck, grad_cv])
    grad_cross_kv = jnp.einsum(
        "td,cte->cde", all_memory, cross_grads, preferred_element_type=jnp.float32
    )
    grad_memory = lax.psum_scatter(
        jnp.einsum("cte,cde->td", cross_grads, cross_kv, preferred_element_type=jnp.float32).astype(
            jnp.bfloat16
        ),
        "tensor",
        scatter_dimension=0,
        tiled=True,
    ).astype(jnp.float32)

    def cross_input_term(first_row, row_total):
        return jnp.dot(grad_cq, cross_q.T, preferred_element_type=jnp.float32)

    cross_input = head_input_sum(cross_input_term)
    grad_first = RESIDUAL_ALPHA * grad_second_in + cross_input
    grad_first_in, first_gain, first_bias = norm_back(
        grad_first, first_hat, first_inv, norm_gains[0]
    )
    grad_self_att, self_out_part = branch_grad(grad_first_in, self_att, self_out)
    grad_sq, grad_sk, grad_sv = attention_backward(
        self_proj[0], self_proj[1], self_proj[2], self_mask, self_lse, grad_self_att, sentences
    )
    self_grads = jnp.stack([grad_sq, grad_sk, grad_sv])
    grad_self_qkv = jnp.einsum(
        "td,cte->cde", all_tokens, self_grads, preferred_element_type=jnp.float32
    )

    def self_input_term(first_row, row_total):
        return jnp.einsum("cte,cde->td", self_grads, self_qkv, preferred_element_type=jnp.float32)

    self_input = head_input_sum(self_input_term)
    grad_tokens = RESIDUAL_ALPHA * grad_first_in + self_input
    summed = (
        lax.psum_scatter(
            grad_self_qkv.astype(jnp.bfloat16), "dp", scatter_dimension=1, tiled=True
        ).astype(jnp.float32),
        lax.psum_scatter(
            self_out_part.astype(jnp.bfloat16), "dp", scatter_dimension=1, tiled=True
        ).astype(jnp.float32),
        lax.psum_scatter(
            grad_cross_q.astype(jnp.bfloat16), "dp", scatter_dimension=0, tiled=True
        ).astype(jnp.float32),
        lax.psum_scatter(
            grad_cross_kv.astype(jnp.bfloat16), "dp", scatter_dimension=1, tiled=True
        ).astype(jnp.float32),
        lax.psum_scatter(
            cross_out_part.astype(jnp.bfloat16), "dp", scatter_dimension=1, tiled=True
        ).astype(jnp.float32),
        lax.psum_scatter(
            grad_ffn_in.astype(jnp.bfloat16), "dp", scatter_dimension=0, tiled=True
        ).astype(jnp.float32),
        lax.psum_scatter(
            grad_ffn_out.astype(jnp.bfloat16), "dp", scatter_dimension=1, tiled=True
        ).astype(jnp.float32),
    )
    gain_total, bias_total = lax.psum(
        (
            jnp.stack([first_gain, second_gain, third_gain]),
            jnp.stack([first_bias, second_bias, third_bias]),
        ),
        ("dp", "tensor"),
    )
    return (
        out_rows.astype(jnp.bfloat16),
        grad_tokens,
        grad_memory,
        summed[0],
        summed[1],
        summed[2],
        summed[3],
        summed[4],
        summed[5],
        summed[6],
        gain_total,
        bias_total,
    )


def solution(mesh):
    in_specs = (
        P(("dp", "tensor"), None),
        P(("dp", "tensor"), None),
        P("dp", None),
        P("dp", None),
        P(None, None, "tensor"),
        P("tensor", None),
        P(None, "tensor"),
        P(None, None, "tensor"),
        P("tensor", None),
        P(None, "tensor"),
        P("tensor", None),
        P(),
        P(),
        P(("dp", "tensor"), None),
    )
    out_specs = (
        P(("dp", "tensor"), None),
        P(("dp", "tensor"), None),
        P(("dp", "tensor"), None),
        P(None, "dp", "tensor"),
        P("tensor", "dp"),
        P("dp", "tensor"),
        P(None, "dp", "tensor"),
        P("tensor", "dp"),
        P("dp", "tensor"),
        P("tensor", "dp"),
        P(),
        P(),
    )

    def step(*args):
        chosen = sentence_body if sentence_fits(mesh, args[0], args[1], args[2]) else body
        return jax.shard_map(
            chosen, mesh=mesh, in_specs=in_specs, out_specs=out_specs, check_vma=False
        )(*args)

    return step
```

```python
import functools
import jax
import jax.numpy as jnp
from jax import lax
from jax.experimental import pallas as pl
from jax.experimental.pallas import tpu as pltpu
from jax.sharding import PartitionSpec as P

HEAD_DIM = 64
RESIDUAL_ALPHA = 4.16
NORM_EPSILON = 1e-05
MASKED_SCORE = -1000000000.0
SCORE_SCALE = HEAD_DIM ** (-0.5)
UNIT = 128
QUERY_BLOCK = 256
FFN_UNIT = 512
ROW_CHUNK = 64
BF16 = jnp.bfloat16
F32 = jnp.float32


def dot(left, right):
    return lax.dot_general(left, right, (((1,), (0,)), ((), ())), preferred_element_type=F32)


def dot_tn(left, right):
    return lax.dot_general(left, right, (((0,), (0,)), ((), ())), preferred_element_type=F32)


def dot_nt(left, right):
    return lax.dot_general(left, right, (((1,), (1,)), ((), ())), preferred_element_type=F32)


def shard_of(position):
    return ((position >> 2) & 1) | (position & 2) | ((position & 1) << 2)


def copy_of(source, target, sem):
    return pltpu.make_async_copy(source, target, sem)


def own_lanes(rows, head):
    lanes = lax.broadcasted_iota(jnp.int32, rows.shape, 1)
    return jnp.where((lanes >= HEAD_DIM) if head else (lanes < HEAD_DIM), rows, 0.0)


def extended_keys(keys, length):
    lanes = lax.broadcasted_iota(jnp.int32, keys.shape, 1)
    rows = lax.broadcasted_iota(jnp.int32, keys.shape, 0)
    mask = jnp.where((lanes == 0) & (rows >= length), MASKED_SCORE, 0.0).astype(BF16)
    keys = keys.astype(F32)
    return [jnp.concatenate([own_lanes(keys, head).astype(BF16), mask], axis=1) for head in (0, 1)]


def extended_query(query):
    lanes = lax.broadcasted_iota(jnp.int32, query.shape, 1)
    return jnp.concatenate([query, jnp.where(lanes == 0, 1.0, 0.0).astype(BF16)], axis=1)


def fill_diagonal(diagonal):
    keys = lax.broadcasted_iota(jnp.int32, diagonal.shape, 0)
    queries = lax.broadcasted_iota(jnp.int32, diagonal.shape, 1)
    diagonal[...] = jnp.where(keys <= queries, 0.0, MASKED_SCORE)


def key_ranges(block, keys, causal):
    if not causal:
        return [(0, keys)]
    return [(low, low + QUERY_BLOCK) for low in range(0, (block + 1) * QUERY_BLOCK, QUERY_BLOCK)]


def attend_unit(query, keys, values, length, causal, diagonal, lse_ref):
    rows, count = query.shape[0], keys.shape[0]
    values_t = jnp.transpose(values.astype(F32)).astype(BF16)
    wide_keys, wide_query = extended_keys(keys, length), extended_query(query)
    items = [(head, block) for block in range(rows // QUERY_BLOCK) for head in (0, 1)]
    scores, probs, totals, mixed = {}, {}, {}, {}
    for head, block in items:
        part = wide_query[block * QUERY_BLOCK : (block + 1) * QUERY_BLOCK]
        ranges = key_ranges(block, count, causal)
        scores[head, block] = [dot_nt(wide_keys[head][a:b], part) for a, b in ranges]
        if causal:
            scores[head, block][-1] = scores[head, block][-1] + diagonal[...]
    for head, block in items:
        pieces = scores[head, block]
        peak = functools.reduce(jnp.maximum, [jnp.max(p, axis=0, keepdims=True) for p in pieces])
        terms = [jnp.exp(p - peak) for p in pieces]
        total = sum(jnp.sum(t, axis=0, keepdims=True) for t in terms)
        at = slice(block * QUERY_BLOCK, (block + 1) * QUERY_BLOCK)
        lse_ref[head : head + 1, at] = peak + jnp.log(total)
        totals[head, block] = total
        probs[head, block] = jnp.concatenate([t.astype(BF16) for t in terms], axis=0)
    for head, block in items:
        own = values_t[head * HEAD_DIM : (head + 1) * HEAD_DIM, : probs[head, block].shape[0]]
        mixed[head, block] = dot(own, probs[head, block]) / totals[head, block]
    out = [
        jnp.transpose(jnp.concatenate([mixed[0, block], mixed[1, block]], axis=0))
        for block in range(rows // QUERY_BLOCK)
    ]
    return jnp.concatenate(out, axis=0).astype(BF16)


def attend_back_unit(query, keys, values, attended, grad, length, causal, diagonal, lse_ref):
    rows, count = query.shape[0], keys.shape[0]
    blocks = range(rows // QUERY_BLOCK)
    query_f, keys_f, grad_f = (a.astype(F32) for a in (query, keys, grad))
    wide_keys, wide_query = extended_keys(keys, length), extended_query(query)
    delta = jnp.transpose(grad_f * attended.astype(F32))
    deltas = [
        jnp.sum(delta[head * HEAD_DIM : (head + 1) * HEAD_DIM], axis=0, keepdims=True)
        for head in (0, 1)
    ]
    keys_t = jnp.transpose(keys_f).astype(BF16)
    query_own = [own_lanes(query_f, head).astype(BF16) for head in (0, 1)]
    grad_own = [own_lanes(grad_f, head).astype(BF16) for head in (0, 1)]
    items = [(head, block) for block in blocks for head in (0, 1)]
    scores, slopes, probs, back, grad_query = {}, {}, {}, {}, {}
    for head, block in items:
        at = slice(block * QUERY_BLOCK, (block + 1) * QUERY_BLOCK)
        for a, b in key_ranges(block, count, causal):
            scores[head, block, a] = dot_nt(wide_keys[head][a:b], wide_query[at])
            slopes[head, block, a] = dot_nt(values[a:b], grad_own[head][at])
    for head, block in items:
        at = slice(block * QUERY_BLOCK, (block + 1) * QUERY_BLOCK)
        ranges = key_ranges(block, count, causal)
        for a, b in ranges:
            score = scores[head, block, a]
            if causal and (a, b) == ranges[-1]:
                score = score + diagonal[...]
            prob = jnp.exp(score - lse_ref[head : head + 1, at])
            probs[head, block, a] = prob.astype(BF16)
            back[head, block, a] = (prob * (slopes[head, block, a] - deltas[head][:, at])).astype(BF16)
    for head, block in items:
        own = keys_t[head * HEAD_DIM : (head + 1) * HEAD_DIM]
        grad_query[head, block] = sum(
            dot(own[:, a:b], back[head, block, a]) for a, b in key_ranges(block, count, causal)
        )
    grad_keys, grad_values = [], []
    for low in sorted({key[2] for key in back}):
        live = [key for key in back if key[2] == low]
        at = [slice(block * QUERY_BLOCK, (block + 1) * QUERY_BLOCK) for _, block, _ in live]
        grad_values.append(
            dot(
                jnp.concatenate([probs[key] for key in live], axis=1),
                jnp.concatenate([grad_own[key[0]][a] for key, a in zip(live, at)], axis=0),
            )
        )
        grad_keys.append(
            dot(
                jnp.concatenate([back[key] for key in live], axis=1),
                jnp.concatenate([query_own[key[0]][a] for key, a in zip(live, at)], axis=0),
            )
        )
    grad_query = [
        jnp.transpose(jnp.concatenate([grad_query[0, block], grad_query[1, block]], axis=0)) * SCORE_SCALE
        for block in blocks
    ]
    return tuple(
        jnp.concatenate(parts, axis=0).astype(BF16) for parts in (grad_query, grad_keys, grad_values)
    )


def norm_chunk(hidden, gain, bias):
    center = hidden - jnp.mean(hidden, axis=-1, keepdims=True)
    inverse = lax.rsqrt(jnp.mean(center * center, axis=-1, keepdims=True) + NORM_EPSILON)
    normed = center * inverse
    return normed * gain + bias, normed, inverse


def norm_back_chunk(gradient, normed, inverse, gain):
    scaled = gradient * gain
    return inverse * (
        scaled
        - jnp.mean(scaled, axis=-1, keepdims=True)
        - normed * jnp.mean(scaled * normed, axis=-1, keepdims=True)
    )


def fold_rows(values):
    return jnp.sum(values.reshape(values.shape[0] // 8, 8, values.shape[1]), axis=0)


def each_chunk(rows, body, results):
    def step(index, carry):
        at = pl.ds(pl.multiple_of(index * ROW_CHUNK, ROW_CHUNK), ROW_CHUNK)
        body(at)
        for buffer, out, sem in results:
            copy_of(buffer.at[at, :], out.at[at, :], sem).start()
        return carry

    lax.fori_loop(0, rows // ROW_CHUNK, step, 0)
    return [copy_of(*result) for result in results]


def store_shards(target, weight, dp):
    for block in range(8):
        target[shard_of(block ^ dp)] = weight[block * UNIT : (block + 1) * UNIT]


SMEM = pl.BlockSpec(memory_space=pltpu.SMEM)
VMEM = pl.BlockSpec(memory_space=pltpu.VMEM)
ANY = pl.BlockSpec(memory_space=pl.ANY)


def params(limit=62):
    return pltpu.CompilerParams(vmem_limit_bytes=limit * 1024 * 1024)


def cost_of(microseconds):
    return pl.CostEstimate(flops=int(microseconds * 1.1e9), bytes_accessed=4 << 20, transcendentals=0)


def sds(shape, dtype):
    return jax.ShapeDtypeStruct(shape, dtype)


def position():
    dp = lax.axis_index("dp")
    return dp & 3, dp, (dp >> 1) & 1


def weight_copies(pieces, wbuf, obuf, wsem, osem, columns=(0, 1, 2)):
    groups, outs = [[], [], []], []
    wide = 2 * UNIT
    order, _, inner = position()
    for index, refs in enumerate(pieces):
        at = slice(index * wide, (index + 1) * wide)
        if len(refs[-1].shape) == 2:
            column = 0
            for ref in refs[:-1]:
                for source in [ref] if len(ref.shape) == 2 else [ref.at[c] for c in range(ref.shape[0])]:
                    if column in columns:
                        low = (columns.index(column) * len(pieces) + index) * wide
                        groups[column].append(copy_of(source, wbuf.at[:, low : low + wide], wsem.at[column, index, 0]))
                    column += 1
            if obuf is not None:
                outs.append(copy_of(refs[-1], obuf.at[at, :], osem.at[index, 0]))
            continue
        parts = [refs[0].at[n] for n in range(refs[0].shape[0])] if len(refs[0].shape) == 4 else refs
        rows = parts[0].shape[1]
        part = wide // len(parts)
        for quarter, ref in enumerate(parts):
            place = quarter ^ (order if len(parts) == 4 else inner)
            for column in columns:
                low = (columns.index(column) * len(pieces) + index) * wide
                groups[column].append(
                    copy_of(
                        ref.at[column],
                        wbuf.at[pl.ds(pl.multiple_of(place * rows, rows), rows), low : low + wide],
                        wsem.at[column, index, quarter],
                    )
                )
            for block in range(4 if obuf is not None else 0):
                outs.append(
                    copy_of(
                        ref.at[3, block * part : (block + 1) * part, :],
                        obuf.at[pl.ds(pl.multiple_of(index * wide + place * part, part), part), block * wide : (block + 1) * wide],
                        osem.at[index, 4 * quarter + block],
                    )
                )
    return groups, outs


def attention_fwd_call(lengths, residual, others, pieces, partial, norm):
    rows, depth = others[0].shape
    causal = len(others) == 1
    number, wide = 2 * len(pieces), 2 * len(pieces) * UNIT
    last, has_partial = norm is not None, partial is not None

    def kernel(*refs):
        it = iter(refs)
        len_ref = next(it)
        in_refs = [next(it) for _ in others]
        gain_ref, bias_ref = (next(it), next(it)) if last else (None, None)
        old_rows = [next(it) for _ in residual[1:]] if last else []
        res_in = next(it) if last else None
        part_in = next(it) if has_partial else None
        w_refs = [[next(it) for _ in piece] for piece in pieces]
        unit_outs, lse_ref = [next(it) for _ in range(4)], next(it)
        if last:
            norm_outs = [next(it) for _ in range(3)]
        else:
            sum_ref = next(it)
        wbuf, obuf, att_all, diagonal, wsem, osem, lsem, usem = (next(it) for _ in range(8))
        q_ref, k_ref, v_ref, att_ref = (next(it) for _ in range(4))
        if last:
            acc, old, low_ref, hat_ref, inv_ref = (next(it) for _ in range(5))
        length = len_ref[0, lax.axis_index("tensor")]
        groups, outs = weight_copies(w_refs, wbuf, obuf, wsem, osem)
        for copies in groups + [outs]:
            for copy in copies:
                copy.start()
        target = acc if last else sum_ref
        late = []
        if has_partial:
            late.append(copy_of(part_in, target, lsem.at[0]))
        if last:
            late.append(copy_of(res_in, old, lsem.at[1]))
        for copy in late:
            copy.start()
        if causal:
            fill_diagonal(diagonal)
        for c, result in enumerate((q_ref, k_ref, v_ref)):
            for copy in groups[c]:
                copy.wait()
            rows_in = in_refs[0] if causal or c == 0 else in_refs[1]
            proj = dot(rows_in[...], wbuf[:, c * wide : (c + 1) * wide]).astype(BF16)
            if c == 0:
                proj = (proj.astype(F32) * SCORE_SCALE).astype(BF16)
            for index in range(number):
                result[index] = proj[:, index * UNIT : (index + 1) * UNIT]

        flushes = [copy_of(*pair, usem.at[index]) for index, pair in enumerate(zip((q_ref, k_ref, v_ref, att_ref), unit_outs))]
        for copy in flushes[:3]:
            copy.start()

        def step(first, carry):
            for u in [first * 4 + inner for inner in range(4)]:
                attended = attend_unit(q_ref[u], k_ref[u], v_ref[u], length, causal, diagonal, lse_ref.at[u])
                att_ref[u] = attended
                att_all[:, pl.ds(pl.multiple_of(u * UNIT, UNIT), UNIT)] = attended
            return carry

        lax.fori_loop(0, number // 4, step, 0)
        flushes[3].start()
        for copy in outs + late:
            copy.wait()
        if has_partial:
            target[...] += dot(att_all[...], obuf[...])
        else:
            target[...] = dot(att_all[...], obuf[...])
        if last:
            def chunk(at):
                before = old[at, :].astype(F32)
                if old_rows:
                    before = before * old_rows[0][...] + old_rows[1][...]
                normed, hat, inverse = norm_chunk(RESIDUAL_ALPHA * before + acc[at, :], gain_ref[...], bias_ref[...])
                low_ref[at, :] = normed.astype(BF16)
                hat_ref[at, :] = hat
                inv_ref[at, :] = jnp.broadcast_to(inverse, (ROW_CHUNK, 128))

            triples = zip((low_ref, hat_ref, inv_ref), norm_outs)
            flushes += each_chunk(rows, chunk, [(*pair, usem.at[4 + index]) for index, pair in enumerate(triples)])
        for copy in flushes:
            copy.wait()

    unit_rows = sds((number, rows, UNIT), BF16)
    shapes = [unit_rows] * 4 + [sds((number, 2, rows), F32)]
    if last:
        shapes += [sds((rows, depth), BF16), sds((rows, depth), F32), sds((rows, 128), F32)]
    else:
        shapes += [sds((rows, depth), F32)]
    args = [lengths, *others]
    if last:
        args += [*norm, *residual[1:]]
    tail = ([residual[0]] if last else []) + ([partial] if has_partial else [])
    tail += [array for piece in pieces for array in piece]
    scratch = [
        pltpu.VMEM((depth, 3 * wide), BF16),
        pltpu.VMEM((wide, depth), BF16),
        pltpu.VMEM((rows, wide), BF16),
        pltpu.VMEM((QUERY_BLOCK, QUERY_BLOCK), F32),
        pltpu.SemaphoreType.DMA((3, len(pieces), 4)),
        pltpu.SemaphoreType.DMA((len(pieces), 16)),
        pltpu.SemaphoreType.DMA((2,)),
        pltpu.SemaphoreType.DMA((7,)),
    ]
    scratch += [pltpu.VMEM((number, rows, UNIT), BF16)] * 4
    if last:
        scratch += [pltpu.VMEM((rows, depth), F32), pltpu.VMEM((rows, depth), residual[0].dtype)]
        scratch += [pltpu.VMEM((rows, depth), BF16), pltpu.VMEM((rows, depth), F32), pltpu.VMEM((rows, 128), F32)]
    return pl.pallas_call(
        kernel,
        out_shape=shapes,
        in_specs=[SMEM] + [VMEM] * (len(args) - 1) + [ANY] * len(tail),
        out_specs=[ANY] * 4 + [VMEM] + ([ANY] * 3 if last else [VMEM]),
        scratch_shapes=scratch,
        compiler_params=params(),
        cost_estimate=cost_of(0.6 * number),
        name="self_fwd" if causal else "cross_fwd",
    )(*args, *tail)


def attention_bwd_call(lengths, grad_low, others, pieces, saved, plan, carried, norm, results=1):
    rows, depth = grad_low.shape
    causal = len(others) == 1
    number, n_in, wide = len(plan), len(others), len(plan) * UNIT
    last = norm is not None
    skip = 1 if last else 0

    def kernel(*refs):
        it = iter(refs)
        len_ref = next(it)
        h_ref = next(it)
        in_refs = [next(it) for _ in range(n_in)]
        gain_ref = next(it) if last else None
        late_in = [next(it), next(it)] if last else []
        acc_in = next(it) if last else None
        w_refs = [[next(it) for _ in piece] for piece in pieces]
        s_refs = [[next(it) for _ in call] for call in saved]
        if last:
            low_ref, scaled_ref, gsum_ref, bsum_ref = (next(it) for _ in range(4))
        dall_ref = next(it)
        g_refs = [next(it) for _ in range(results)]
        wbuf, obuf, sbuf, lbuf, att_all, grad_all = (next(it) for _ in range(6))
        stage, diagonal = next(it), next(it)
        if last:
            dquery, acc, hat, inv, low_buf, scaled_buf, nsem = (next(it) for _ in range(7))
        wsem, osem, ssem, gsem, lsem = (next(it) for _ in range(5))
        length, dp = len_ref[0, lax.axis_index("tensor")], lax.axis_index("dp")

        groups, o_copies = weight_copies(w_refs, wbuf, obuf, wsem, osem, (0,) if last else ())
        for copy in o_copies:
            copy.start()
        s_copies = []
        for index, unit in enumerate(plan):
            lanes = slice(index * UNIT, (index + 1) * UNIT)
            call = s_refs[unit[0]]
            for c in range(3):
                s_copies.append(copy_of(call[c].at[unit[1]], sbuf.at[index, c], ssem.at[c, index]))
            s_copies.append(copy_of(call[3].at[unit[1]], att_all.at[:, lanes], ssem.at[3, index]))
            s_copies.append(copy_of(call[4].at[unit[1]], lbuf.at[index], ssem.at[4, index]))
        late = []
        if last:
            late = groups[0] + [
                copy_of(source, target, lsem.at[index])
                for index, (source, target) in enumerate(((acc_in, acc), (late_in[0], hat), (late_in[1], inv)))
            ]
        for copy in s_copies + late:
            copy.start()
        if causal:
            fill_diagonal(diagonal)
        for copy in o_copies:
            copy.wait()
        grad_att = dot_nt(h_ref[...], obuf[...]).astype(BF16)
        for index in range(number):
            grad_all[index] = grad_att[:, index * UNIT : (index + 1) * UNIT]
        for copy in s_copies:
            copy.wait()

        def step(first, carry):
            units = [first * 2, first * 2 + 1]
            ats = [pl.ds(pl.multiple_of(u * UNIT, UNIT), UNIT) for u in units]
            parts = [
                attend_back_unit(
                    sbuf[u, 0], sbuf[u, 1], sbuf[u, 2], att_all[:, at], grad_all[u], length, causal, diagonal, lbuf.at[u]
                )
                for u, at in zip(units, ats)
            ]
            for u, at, part in zip(units, ats, parts):
                if last:
                    dquery[:, at] = part[0]
                for c in range(skip, 3):
                    dall_ref[:, pl.ds(pl.multiple_of((c - skip) * wide + u * UNIT, UNIT), UNIT)] = part[c]
            return carry

        lax.fori_loop(0, number // 2, step, 0)
        share = number // 2 // results

        def keep(rows_in, source, column):
            weight = dot_tn(rows_in[...], source).astype(BF16)
            for index in range(number):
                piece = index // 2
                target = stage.at[piece // share, (index % 2) * 4 + column, piece % share]
                store_shards(target, weight[:, index * UNIT : (index + 1) * UNIT], dp)

        if last:
            keep(in_refs[0], dquery[...], 0)
        for c in range(skip, 3):
            keep(in_refs[-1], dall_ref[:, (c - skip) * wide : (c - skip + 1) * wide], c)
        keep(h_ref, att_all[...], 3)
        g_copies = [copy_of(stage.at[index], ref, gsem.at[index]) for index, ref in enumerate(g_refs)]
        for copy in g_copies:
            copy.start()
        for copy in late:
            copy.wait()
        if last:
            acc[...] += dot_nt(dquery[...], wbuf[...])
            g_copies += norm_back_rows(
                acc, hat, inv, gain_ref, low_buf, scaled_buf, (low_ref, scaled_ref), nsem, gsum_ref, bsum_ref, rows
            )
        for copy in g_copies:
            copy.wait()

    big = sds((rows, depth), F32)
    shapes = []
    if last:
        shapes += [sds((rows, depth), BF16), big, sds((8, depth), F32), sds((8, depth), F32)]
    shapes.append(sds((rows, (3 - skip) * wide), BF16))
    specs_out = ([ANY] * 2 + [VMEM] * 3 if last else [VMEM]) + [ANY] * results
    shapes += [sds((8, number // 2 // results, 8, UNIT, UNIT), BF16)] * results
    args = [lengths, grad_low, *others] + ([norm[2]] if last else [])
    tail = [norm[0], norm[1], carried] if last else []
    tail += [array for piece in pieces for array in piece]
    for call in saved:
        tail += call
    scratch = [
        pltpu.VMEM((depth, wide) if last else (16, 128), BF16),
        pltpu.VMEM((wide, depth), BF16),
        pltpu.VMEM((number, 3, rows, UNIT), BF16),
        pltpu.VMEM((number, 2, rows), F32),
        pltpu.VMEM((rows, wide), BF16),
        pltpu.VMEM((number, rows, UNIT), BF16),
        pltpu.VMEM((results, 8, number // 2 // results, 8, UNIT, UNIT), BF16),
        pltpu.VMEM((QUERY_BLOCK, QUERY_BLOCK), F32),
    ]
    if last:
        scratch += [pltpu.VMEM((rows, wide), BF16), pltpu.VMEM((rows, depth), F32), pltpu.VMEM((rows, depth), F32), pltpu.VMEM((rows, 128), F32)]
        scratch += [pltpu.VMEM((rows, depth), BF16), pltpu.VMEM((rows, depth), F32), pltpu.SemaphoreType.DMA((2,))]
    scratch += [
        pltpu.SemaphoreType.DMA((3, len(pieces), 4)),
        pltpu.SemaphoreType.DMA((len(pieces), 16)),
        pltpu.SemaphoreType.DMA((5, number)),
        pltpu.SemaphoreType.DMA((results,)),
        pltpu.SemaphoreType.DMA((4,)),
    ]
    return pl.pallas_call(
        kernel,
        out_shape=shapes,
        in_specs=[SMEM] + [VMEM] * (len(args) - 1) + [ANY] * len(tail),
        out_specs=specs_out,
        scratch_shapes=scratch,
        compiler_params=params(),
        cost_estimate=cost_of(4.2 * number),
        name="self_bwd" if causal else "cross_bwd",
    )(*args, *tail)


def inputs_back_call(base, parts, columns):
    rows, depth = parts[0][0].shape[0], parts[0][1][0][0].shape[-2]

    def kernel(*refs):
        it = iter(refs)
        base_ref = next(it) if base is not None else None
        grads = [next(it) for _ in parts]
        w_refs = [[[next(it) for _ in piece] for piece in pieces] for _, pieces in parts]
        out = next(it)
        bufs, sems = [next(it) for _ in parts], [next(it) for _ in parts]
        copies = []
        for index in range(len(parts)):
            groups, _ = weight_copies(w_refs[index], bufs[index], None, sems[index], None, columns)
            copies.append([copy for group in groups for copy in group])
            for copy in copies[-1]:
                copy.start()
        if base is not None:
            out[...] = base_ref[...]
        for index in range(len(parts)):
            for copy in copies[index]:
                copy.wait()
            if index or base is not None:
                out[...] += dot_nt(grads[index][...], bufs[index][...])
            else:
                out[...] = dot_nt(grads[index][...], bufs[index][...])

    args = ([base] if base is not None else []) + [grad for grad, _ in parts]
    tail = [array for _, pieces in parts for piece in pieces for array in piece]
    return pl.pallas_call(
        kernel,
        out_shape=sds((rows, depth), F32),
        in_specs=[VMEM] * len(args) + [ANY] * len(tail),
        out_specs=VMEM,
        scratch_shapes=[pltpu.VMEM((depth, grad.shape[1]), BF16) for grad, _ in parts]
        + [pltpu.SemaphoreType.DMA((3, len(pieces), 4)) for _, pieces in parts],
        compiler_params=params(),
        cost_estimate=cost_of(7),
        name="inputs_back",
    )(*args, *tail)


def norm_back_rows(acc, hat, inv, gain_ref, low_buf, scaled_buf, outs, sems, gsum_ref, bsum_ref, rows):
    gsum_ref[...] = jnp.zeros_like(gsum_ref)
    bsum_ref[...] = jnp.zeros_like(bsum_ref)

    def chunk(at):
        gradient, normed = acc[at, :], hat[at, :]
        grad_in = norm_back_chunk(gradient, normed, inv[at, :1], gain_ref[...])
        low_buf[at, :] = grad_in.astype(BF16)
        scaled_buf[at, :] = RESIDUAL_ALPHA * grad_in
        gsum_ref[...] += fold_rows(gradient * normed)
        bsum_ref[...] += fold_rows(gradient)

    pairs = zip((low_buf, scaled_buf), outs)
    return each_chunk(rows, chunk, [(*pair, sems.at[index]) for index, pair in enumerate(pairs)])


GELU_SCALE = 0.7978845608028654
GELU_CUBE = 0.044715


def gelu_and_slope(pre):
    square = pre * pre
    inner = pre * (GELU_SCALE + (GELU_SCALE * GELU_CUBE) * square)
    curve = jnp.tanh(inner)
    half = 0.5 + 0.5 * curve
    slope = half * (1.0 + pre * (1.0 - curve) * (GELU_SCALE + (3.0 * GELU_SCALE * GELU_CUBE) * square))
    return pre * half, slope


FFN_PART = FFN_UNIT // 2


def ffn_copies(pieces, ubuf, dbuf, usem, dsem):
    ups, downs = [], []
    order, _, _ = position()
    for index, refs in enumerate(pieces):
        wide = 2 * FFN_UNIT
        at = slice(index * wide, (index + 1) * wide)
        if len(refs) == 2:
            ups.append([copy_of(refs[0], ubuf.at[:, at], usem.at[index, 0])])
            downs.append([copy_of(refs[1], dbuf.at[at, :], dsem.at[index, 0])])
            continue
        ups.append([])
        downs.append([])
        rows = refs[0].shape[1]
        for quarter in range(4):
            up = refs[quarter].at[0]
            down = refs[quarter].at[1] if quarter < 3 else refs[4].at[0]
            place = (quarter ^ order) * rows
            ups[-1].append(copy_of(up, ubuf.at[pl.ds(pl.multiple_of(place, rows), rows), at], usem.at[index, quarter]))
            downs[-1].append(
                copy_of(down, dbuf.at[pl.ds(pl.multiple_of(index * wide + place, rows), rows), :], dsem.at[index, quarter])
            )
    return ups, downs


def ffn_fwd_call(inputs, pieces, partial, final):
    rows, depth = inputs.shape
    number = 2 * len(pieces)
    last, has_partial = final is not None, partial is not None

    def kernel(*refs):
        it = iter(refs)
        x_ref = next(it)
        if last:
            gain_old, bias_old, gain_ref, bias_ref = (next(it) for _ in range(4))
            late_in = [next(it), next(it)]
        part_in = next(it) if has_partial else None
        w_refs = [[next(it) for _ in piece] for piece in pieces]
        if last:
            norm_outs = [next(it) for _ in range(3)]
            gsum_ref, bsum_ref = next(it), next(it)
        else:
            sum_ref = next(it)
        act_ref, slope_ref = next(it), next(it)
        ubuf, dbuf, abuf, sbuf, pbuf, psem = (next(it) for _ in range(6))
        if last:
            acc, hat, cot, lsem, out_ref, low_ref, scaled_ref, nsem = (next(it) for _ in range(8))
        wsem, gsem = next(it), next(it)
        target = acc if last else sum_ref

        up_copies, down_copies = ffn_copies(w_refs, ubuf, dbuf, wsem.at[0], wsem.at[1])
        for copies in up_copies + down_copies:
            for copy in copies:
                copy.start()
        if has_partial:
            part_copy = copy_of(part_in, target, psem)
            part_copy.start()
        if last:
            late = [copy_of(late_in[0], hat, lsem.at[0]), copy_of(late_in[1], cot, lsem.at[1])]
            for copy in late:
                copy.start()
        saves = []

        def gate(pre, index):
            activated, slope = gelu_and_slope(pre)
            abuf[:, index * FFN_UNIT : (index + 1) * FFN_UNIT] = activated.astype(BF16)
            sbuf[:, index * FFN_UNIT : (index + 1) * FFN_UNIT] = slope.astype(BF16)

        for index in range(number):
            if index % 2 == 0:
                for copy in up_copies[index // 2]:
                    copy.wait()
            if index:
                gate(pbuf[(index - 1) % 2], index - 1)
            pbuf[index % 2] = dot(x_ref[...], ubuf[:, index * FFN_UNIT : (index + 1) * FFN_UNIT])
        gate(pbuf[(number - 1) % 2], number - 1)
        for index in range(number):
            at = slice(index * FFN_UNIT, (index + 1) * FFN_UNIT)
            saves += [
                copy_of(abuf.at[:, at], act_ref.at[index], gsem.at[0, index]),
                copy_of(sbuf.at[:, at], slope_ref.at[index], gsem.at[1, index]),
            ]
        for copy in saves:
            copy.start()
        for copies in down_copies:
            for copy in copies:
                copy.wait()
        if has_partial:
            part_copy.wait()
            target[...] += dot(abuf[...], dbuf[...])
        else:
            target[...] = dot(abuf[...], dbuf[...])
        if last:
            for copy in late:
                copy.wait()
            gsum_ref[...] = jnp.zeros_like(gsum_ref)
            bsum_ref[...] = jnp.zeros_like(bsum_ref)

            def chunk(at):
                old = hat[at, :] * gain_old[...] + bias_old[...]
                normed, xhat, inverse = norm_chunk(RESIDUAL_ALPHA * old + acc[at, :], gain_ref[...], bias_ref[...])
                out_ref[at, :] = normed.astype(BF16)
                gradient = cot[at, :].astype(F32)
                grad_in = norm_back_chunk(gradient, xhat, inverse, gain_ref[...])
                low_ref[at, :] = grad_in.astype(BF16)
                scaled_ref[at, :] = RESIDUAL_ALPHA * grad_in
                gsum_ref[...] += fold_rows(gradient * xhat)
                bsum_ref[...] += fold_rows(gradient)

            triples = zip((out_ref, low_ref, scaled_ref), norm_outs)
            saves += each_chunk(rows, chunk, [(*pair, nsem.at[index]) for index, pair in enumerate(triples)])
        for copy in saves:
            copy.wait()

    big, low = sds((rows, depth), F32), sds((rows, depth), BF16)
    if last:
        shapes = [low, low, big, sds((8, depth), F32), sds((8, depth), F32)]
    else:
        shapes = [big]
    specs_out = ([ANY] * 3 + [VMEM] * 2 if last else [VMEM]) + [ANY, ANY]
    shapes += [sds((number, rows, FFN_UNIT), BF16)] * 2
    args = [inputs]
    if last:
        args += [final[1], final[2], final[4], final[5]]
    specs = [VMEM] * len(args)
    tail = ([final[0], final[3]] if last else []) + ([partial] if has_partial else []) + [array for piece in pieces for array in piece]
    scratch = [
        pltpu.VMEM((depth, number * FFN_UNIT), BF16),
        pltpu.VMEM((number * FFN_UNIT, depth), BF16),
        pltpu.VMEM((rows, number * FFN_UNIT), BF16),
        pltpu.VMEM((rows, number * FFN_UNIT), BF16),
        pltpu.VMEM((2, rows, FFN_UNIT), F32),
        pltpu.SemaphoreType.DMA,
    ]
    if last:
        scratch += [
            pltpu.VMEM((rows, depth), F32),
            pltpu.VMEM((rows, depth), F32),
            pltpu.VMEM((rows, depth), BF16),
            pltpu.SemaphoreType.DMA((2,)),
            pltpu.VMEM((rows, depth), BF16),
            pltpu.VMEM((rows, depth), BF16),
            pltpu.VMEM((rows, depth), F32),
            pltpu.SemaphoreType.DMA((3,)),
        ]
    scratch += [pltpu.SemaphoreType.DMA((2, len(pieces), 4)), pltpu.SemaphoreType.DMA((2, number))]
    return pl.pallas_call(
        kernel,
        out_shape=shapes,
        in_specs=specs + [ANY] * len(tail),
        out_specs=specs_out,
        scratch_shapes=scratch,
        compiler_params=params(),
        cost_estimate=cost_of(12),
        name="ffn_fwd",
    )(*args, *tail)


def ffn_bwd_call(grad_low, inputs, pieces, saved, plan, carried, norm):
    rows, depth = inputs.shape
    number = len(plan)
    last = norm is not None

    def kernel(*refs):
        it = iter(refs)
        g_in, x_ref = next(it), next(it)
        gain_ref = next(it) if last else None
        late_in = [next(it), next(it)] if last else []
        acc_in = next(it)
        w_refs = [[next(it) for _ in piece] for piece in pieces]
        s_refs = [[next(it) for _ in call] for call in saved]
        if last:
            low_ref, scaled_ref, gsum_ref, bsum_ref = (next(it) for _ in range(4))
        else:
            sum_ref = next(it)
        g_ref = next(it)
        ubuf, dbuf, abuf, sbuf, gbuf, stage, psem = (next(it) for _ in range(7))
        if last:
            acc, hat, inv, lsem, low_buf, scaled_buf, nsem = (next(it) for _ in range(7))
        wsem, ssem, gsem = next(it), next(it), next(it)
        dp = lax.axis_index("dp")
        target = acc if last else sum_ref

        ups, downs = ffn_copies(w_refs, ubuf, dbuf, wsem.at[0], wsem.at[1])
        slopes, acts = [], []
        for index, (call, at) in enumerate(plan):
            lanes = slice(index * FFN_UNIT, (index + 1) * FFN_UNIT)
            slopes.append(copy_of(s_refs[call][1].at[at], sbuf.at[index], ssem.at[0, index]))
            acts.append(copy_of(s_refs[call][0].at[at], abuf.at[:, lanes], ssem.at[1, index]))
        for copies in downs + [slopes, acts] + ups:
            for copy in copies:
                copy.start()
        part_copy = copy_of(acc_in, target, psem)
        part_copy.start()
        if last:
            late = [copy_of(late_in[0], hat, lsem.at[0]), copy_of(late_in[1], inv, lsem.at[1])]
            for copy in late:
                copy.start()
        for index in range(number):
            if index % 2 == 0:
                for copy in downs[index // 2]:
                    copy.wait()
            slopes[index].wait()
            grad_act = dot_nt(g_in[...], dbuf[index * FFN_UNIT : (index + 1) * FFN_UNIT, :]) * sbuf[index].astype(F32)
            gbuf[:, index * FFN_UNIT : (index + 1) * FFN_UNIT] = grad_act.astype(BF16)
        for copy in acts:
            copy.wait()

        def keep(rows_in, source, column):
            for half in range(number // 2):
                wide = 2 * FFN_UNIT
                weight = dot_tn(rows_in[...], source[:, half * wide : (half + 1) * wide]).astype(BF16)
                for inner in range(4):
                    part = weight[:, inner * FFN_PART : (inner + 1) * FFN_PART]
                    store_shards(stage.at[2 * inner + column, half], part, dp)

        keep(x_ref, gbuf, 0)
        keep(g_in, abuf, 1)
        g_copies = [copy_of(stage, g_ref, gsem)]
        for copy in g_copies:
            copy.start()
        for copies in ups:
            for copy in copies:
                copy.wait()
        part_copy.wait()
        target[...] += dot_nt(gbuf[...], ubuf[...])
        if last:
            for copy in late:
                copy.wait()
            g_copies += norm_back_rows(
                acc, hat, inv, gain_ref, low_buf, scaled_buf, (low_ref, scaled_ref), nsem, gsum_ref, bsum_ref, rows
            )
        for copy in g_copies:
            copy.wait()

    big, low = sds((rows, depth), F32), sds((rows, depth), BF16)
    shapes = [low, big, sds((8, depth), F32), sds((8, depth), F32)] if last else [big]
    specs_out = ([ANY] * 2 + [VMEM] * 2 if last else [VMEM]) + [ANY]
    shapes.append(sds((8, number // 2, 8, UNIT, FFN_PART), BF16))
    args = [grad_low, inputs] + ([norm[2]] if last else [])
    specs = [VMEM] * len(args)
    tail = ([norm[0], norm[1]] if last else []) + [carried] + [array for piece in pieces for array in piece]
    for call in saved:
        tail += call
    scratch = [
        pltpu.VMEM((depth, number * FFN_UNIT), BF16),
        pltpu.VMEM((number * FFN_UNIT, depth), BF16),
        pltpu.VMEM((rows, number * FFN_UNIT), BF16),
        pltpu.VMEM((number, rows, FFN_UNIT), BF16),
        pltpu.VMEM((rows, number * FFN_UNIT), BF16),
        pltpu.VMEM((8, number // 2, 8, UNIT, FFN_PART), BF16),
        pltpu.SemaphoreType.DMA,
    ]
    if last:
        scratch += [
            pltpu.VMEM((rows, depth), F32),
            pltpu.VMEM((rows, depth), F32),
            pltpu.VMEM((rows, 128), F32),
            pltpu.SemaphoreType.DMA((2,)),
            pltpu.VMEM((rows, depth), BF16),
            pltpu.VMEM((rows, depth), F32),
            pltpu.SemaphoreType.DMA((2,)),
        ]
    scratch += [pltpu.SemaphoreType.DMA((2, len(pieces), 4)), pltpu.SemaphoreType.DMA((2, number)), pltpu.SemaphoreType.DMA]
    return pl.pallas_call(
        kernel,
        out_shape=shapes,
        in_specs=specs + [ANY] * len(tail),
        out_specs=specs_out,
        scratch_shapes=scratch,
        compiler_params=params(),
        cost_estimate=cost_of(17),
        name="ffn_bwd",
    )(*args, *tail)


def combine(jobs, shapes):
    arrays = []
    for terms, _, _, _ in jobs:
        for array, _ in terms:
            if not any(array is known for known in arrays):
                arrays.append(array)
    position = {id(array): index for index, array in enumerate(arrays)}

    def part_shape(array, index):
        kept = []
        for extent, at in zip(array.shape, index + (slice(None),) * (array.ndim - len(index))):
            if isinstance(at, slice):
                kept.append(len(range(*at.indices(extent))))
        return tuple(kept)

    part_shapes = [part_shape(*terms[0]) for terms, _, _, _ in jobs]
    count = sum(len(terms) for terms, _, _, _ in jobs)

    def kernel(*refs):
        ins, outs = refs[: len(arrays)], refs[len(arrays) : len(arrays) + len(shapes)]
        rest = refs[len(arrays) + len(shapes) :]
        term_bufs, sum_bufs, isem, osem = rest[:count], rest[count : count + len(jobs)], rest[-2], rest[-1]
        loads, number = [], 0
        for terms, _, _, _ in jobs:
            loads.append([])
            for array, index in terms:
                loads[-1].append(copy_of(ins[position[id(array)]].at[index], term_bufs[number], isem.at[number]))
                number += 1
        for group in loads:
            for copy in group:
                copy.start()
        stores, number = [], 0
        for job, (terms, out, place, kind) in enumerate(jobs):
            for copy in loads[job]:
                copy.wait()
            bufs = term_bufs[number : number + len(terms)]
            number += len(terms)
            lead = part_shapes[job][:-2]
            size = 1
            for extent in lead:
                size *= extent

            def one(flat, carry, bufs=bufs, lead=lead, target=sum_bufs[job]):
                index, left = [], flat
                for extent in reversed(lead):
                    index.append(lax.rem(left, extent))
                    left = lax.div(left, extent)
                index = tuple(reversed(index))
                total = bufs[0][index].astype(F32)
                for buf in bufs[1:]:
                    total = total + buf[index].astype(F32)
                target[index] = total.astype(target.dtype)
                return carry

            if kind == "range":
                lax.fori_loop(0, size, one, 0)
            else:
                total = bufs[0][0].astype(F32)
                for buf in bufs[1:]:
                    total = total + buf[0].astype(F32)
                sum_bufs[job][...] = jnp.transpose(total) if kind == "turned" else total
            stores.append(copy_of(sum_bufs[job], outs[out].at[place], osem.at[job]))
            stores[-1].start()
        for copy in stores:
            copy.wait()

    scratch = [pltpu.VMEM(part_shapes[job], array.dtype) for job, (terms, _, _, _) in enumerate(jobs) for array, _ in terms]
    for job, (_, out, _, kind) in enumerate(jobs):
        shape = part_shapes[job]
        shape = {"range": shape, "plain": shape[1:], "turned": shape[:0:-1]}[kind]
        scratch.append(pltpu.VMEM(shape, shapes[out].dtype))
    scratch += [pltpu.SemaphoreType.DMA((count,)), pltpu.SemaphoreType.DMA((len(jobs),))]
    return pl.pallas_call(
        kernel,
        out_shape=list(shapes),
        in_specs=[ANY] * len(arrays),
        out_specs=[ANY] * len(shapes),
        scratch_shapes=scratch,
        compiler_params=params(),
        cost_estimate=cost_of(3),
        name="combine",
    )(*arrays)


def swap_pairs(count, mask):
    return [(i, i ^ mask) for i in range(count)]


def to_sibling(values):
    return lax.ppermute(values, "tensor", swap_pairs(4, 1))


def over_y(values):
    return lax.ppermute(values, "tensor", swap_pairs(4, 2))


def over_dp(values, mask):
    return lax.ppermute(values, "dp", swap_pairs(8, mask))


def over_x(values):
    return over_dp(values, 1)


def over_z_near(values):
    return over_dp(values, 2)


def over_z_far(values):
    return over_dp(values, 4)


def after(values, *earlier):
    return lax.optimization_barrier((values, *earlier))[0]


MOVES = {"y": over_y, "x": over_x, "z": over_z_near}


class Reduction:
    def __init__(self, sent, portions, finish):
        self.other, self.finish = to_sibling(sent), finish
        self.portions, self.stage, self.sends, self.total = portions, 0, None, None

    def begin(self, kept, *earlier):
        other = after(self.other, *earlier)
        split = (kept.shape[0], 2, 2, 2, 2, *kept.shape[3:])
        arrays = (kept.reshape(split), other.reshape(split))
        self.blocks, self.tail = kept.shape[0], kept.shape[3:]
        self.terms = [[(array, ("b", "y", "x", "z", "w"), low, {}) for array in arrays] for low, _, _ in self.portions]

    def receive(self, *earlier):
        if self.stage == 4:
            moved = after(over_z_far(self.sends[0]), *earlier)
            for (low, _, _), terms in zip(self.portions, self.terms):
                terms.append((moved, ("b",), low, {}))
        elif self.stage:
            for send, (_, _, orders), terms in zip(self.sends, self.portions, self.terms):
                left = tuple(a for a in ("b", "y", "x", "z", "w") if a not in orders[: self.stage])
                terms.append((after(MOVES[orders[self.stage - 1]](send), *earlier), left, 0, {}))

    def jobs(self, first_out):
        jobs, shapes = [], []
        stage = self.stage
        for number, ((low, high, orders), terms) in enumerate(zip(self.portions, self.terms)):
            axis = (*orders, "w", None)[stage]
            picked = []
            for array, axes, start, fixed in terms:
                index = [slice(start, start + high - low)]
                for name in axes[1:]:
                    index.append(1 if name == axis else fixed.get(name, 0 if name in orders[:stage] or (stage > 3 and name == "w") else slice(None)))
                picked.append((array, tuple(index)))
            if stage < 3:
                shapes.append(sds((high - low, *(2,) * (3 - stage), *self.tail), BF16))
                jobs.append((picked, first_out + number, slice(0, high - low), "range"))
            elif stage == 3:
                if not number:
                    shapes.append(sds((self.blocks, *self.tail), BF16))
                jobs.append((picked, first_out, slice(low, high), "range"))
            else:
                if not number:
                    shapes += self.finish[0]
                for block in range(low, high):
                    shift = block - low
                    one = [(a, (slice(index[0].start + shift, index[0].start + shift + 1), *index[1:])) for a, index in picked]
                    out, place, kind = self.finish[1](block)
                    jobs.append((one, first_out + out, place, kind))
        self.stage += 1
        return jobs, shapes

    def keep(self, results):
        self.sends = results
        if self.stage == 5:
            self.total = results


def attention_finish(counts):
    stacks = [sds((count, UNIT, 2 * UNIT) if count > 1 else (UNIT, 2 * UNIT), F32) for count in counts]

    def place_of(block):
        half, matrix = block // 4, block % 4
        lanes = slice(half * UNIT, (half + 1) * UNIT)
        if matrix == 3:
            return len(counts), (lanes, slice(None)), "turned"
        stack = 0 if matrix < counts[0] else 1
        if counts[stack] == 1:
            return stack, (slice(None), lanes), "plain"
        return stack, (matrix - sum(counts[:stack]), slice(None), lanes), "plain"

    return [*stacks, sds((2 * UNIT, UNIT), F32)], place_of


def ffn_finish():
    def place_of(block):
        lanes = slice(block // 2 * FFN_PART, (block // 2 + 1) * FFN_PART)
        if block % 2:
            return 1, (lanes, slice(None)), "turned"
        return 0, (slice(None), lanes), "plain"

    return [sds((UNIT, 4 * FFN_PART), F32), sds((4 * FFN_PART, UNIT), F32)], place_of


class Shared:
    def __init__(self, values):
        self.values, self.moves = values, [to_sibling, over_x, over_z_near, over_y, over_z_far]

    def receive(self, *earlier):
        self.moved = after(self.moves.pop(0)(self.values), *earlier)

    def jobs(self, first_out):
        terms = [(array, (slice(0, 1),)) for array in (self.values, self.moved)]
        return [(terms, first_out, slice(0, 1), "range")], [sds(self.values.shape, F32)]

    def keep(self, results):
        self.values, = results


def advance(reductions, *earlier):
    jobs, shapes, bounds = [], [], []
    for reduction in reductions:
        reduction.receive(*earlier)
        more, made = reduction.jobs(len(shapes))
        bounds.append((len(shapes), len(shapes) + len(made)))
        jobs, shapes = jobs + more, shapes + made
    results = combine(jobs, shapes)
    for reduction, (low, high) in zip(reductions, bounds):
        reduction.keep(list(results[low:high]))
    return list(results)


def sentence_body(
    tokens,
    memory,
    dec_lengths,
    mem_lengths,
    self_qkv,
    self_out,
    cross_q,
    cross_kv,
    cross_out,
    ffn_in,
    ffn_out,
    norm_gains,
    norm_biases,
    cotangent,
):
    dp = lax.axis_index("dp")
    order = dp & 3
    inner = (dp >> 1) & 1
    gains = [norm_gains[i : i + 1] for i in range(3)]
    biases = [norm_biases[i : i + 1] for i in range(3)]

    def part_rows(values, parts):
        rows = values.shape[-2] // parts
        place = order if parts == 4 else inner
        return lax.dynamic_slice_in_dim(values, place * rows, rows, values.ndim - 2)

    def folded(values):
        blocks = values.reshape(values.shape[0], 4, 2 * UNIT)
        return blocks.transpose(1, 0, 2).reshape(1, 4 * values.shape[0], 2 * UNIT)

    self_near = over_y(jnp.concatenate([part_rows(self_qkv, 4), folded(part_rows(self_out, 4))]))
    cross_near = over_y(
        jnp.concatenate([part_rows(cross_q, 2)[None], part_rows(cross_kv, 2), folded(part_rows(cross_out, 2))])
    )
    ffn_near = over_y(jnp.stack([part_rows(ffn_in, 4), part_rows(ffn_out, 4)]))
    self_own = (self_qkv, self_out)
    self_sib = tuple(to_sibling(w) for w in self_own)
    self_a = attention_fwd_call(dec_lengths, [], [tokens], [self_own, self_sib], None, None)
    self_near = after(self_near, self_a[4])
    self_side, self_up = over_x(self_near), over_z_near(self_near)
    self_corner = over_x(self_up)
    cross_own, ffn_own = (cross_q, cross_kv, cross_out), (ffn_in, ffn_out)
    cross_sib = tuple(to_sibling(w) for w in cross_own)
    cross_up = over_z_near(cross_near)
    self_rest = (self_near, self_side, self_up, after(self_corner, cross_near, *cross_sib))
    self_far = tuple(to_sibling(w) for w in self_rest)
    self_pieces = [self_own, self_sib, self_rest, self_far]
    self_b = attention_fwd_call(
        dec_lengths, [tokens], [tokens], self_pieces[2:], self_a[5], (gains[0], biases[0])
    )
    first_low, first_hat, first_inv = self_b[5:]
    cross_in = [first_low, memory]
    cross_rest = jnp.stack([cross_near, after(cross_up, self_b[4])])
    cross_far = to_sibling(cross_rest)
    ffn_sib = tuple(to_sibling(after(w, ffn_near)) for w in ffn_own)
    ffn_side, ffn_up = over_x(ffn_near), over_z_near(ffn_near)
    cross_pieces = [cross_own, cross_sib, (cross_rest,), (cross_far,)]
    cross_b = attention_fwd_call(
        mem_lengths, [first_hat, gains[0], biases[0]], [after(first_low, ffn_near), memory], cross_pieces, None,
        (gains[1], biases[1]),
    )
    second_low, second_hat, second_inv = cross_b[5:]
    ffn_side, ffn_up = after(ffn_side, cross_b[4]), after(ffn_up, cross_b[4])
    up_corner, down_corner = over_x(ffn_up[:1]), over_z_near(ffn_side[1:])
    ffn_pieces = [ffn_own, ffn_sib]
    ffn_a = ffn_fwd_call(second_low, ffn_pieces, None, None)
    up_corner, down_corner = after(up_corner, ffn_a[0]), after(down_corner, ffn_a[0])
    ffn_rest = (ffn_near, ffn_side, ffn_up, up_corner, down_corner)
    ffn_pieces += [ffn_rest, tuple(to_sibling(w) for w in ffn_rest)]
    ffn_b = ffn_fwd_call(
        second_low, ffn_pieces[2:], ffn_a[0],
        (second_hat, gains[1], biases[1], cotangent, gains[2], biases[2]),
    )
    out_rows, third_low, third_scaled, third_gain, third_bias = ffn_b[:5]

    def plan_of(pieces):
        return [(piece // 2, 2 * (piece % 2) + half) for piece in pieces for half in (0, 1)]

    ffn_saved = [ffn_a[1:3], ffn_b[5:7]]
    ffn_d = ffn_bwd_call(
        third_low, second_low, ffn_pieces[1::2], ffn_saved, plan_of((1, 3)), third_scaled, None
    )
    ffn_sum = Reduction(ffn_d[1], [(0, 3, "yzx"), (3, 6, "xyz"), (6, 8, "zxy")], ffn_finish())
    ffn_e = ffn_bwd_call(
        third_low, second_low, ffn_pieces[::2], ffn_saved, plan_of((0, 2)), ffn_d[0],
        (second_hat, second_inv, gains[1]),
    )
    second_back, second_scaled, second_gain, second_bias = ffn_e[:4]
    ffn_sum.begin(ffn_e[4], second_gain)
    second_back = after(second_back, *advance([ffn_sum]))

    cross_e = attention_bwd_call(
        mem_lengths, second_back, cross_in, cross_pieces[1::2] + cross_pieces[::2],
        [cross_b[:5]], [(0, 2 * p + half) for p in (1, 3, 0, 2) for half in (0, 1)], second_scaled,
        (first_hat, first_inv, gains[0]), 2,
    )
    first_back, first_scaled, first_gain, first_bias, memory_part = cross_e[:5]
    norm_sums = jnp.stack([first_gain, second_gain, third_gain, first_bias, second_bias, third_bias])
    norm_sums = jnp.concatenate([jnp.sum(norm_sums, axis=1), jnp.zeros((2, norm_sums.shape[2]), F32)])
    norms = Shared(norm_sums[None])
    sends = advance([ffn_sum], first_gain)
    cross_sum = Reduction(after(cross_e[5], *sends), [(0, 4, "zyx"), (4, 8, "yxz")], attention_finish((1, 2)))
    first_back = after(first_back, *sends)

    self_saved = [self_a[:5], self_b[:5]]
    self_d = attention_bwd_call(
        dec_lengths, first_back, [tokens], self_pieces[1::2], self_saved, plan_of((1, 3)), None, None
    )
    cross_sum.begin(cross_e[6], self_d[0])
    sends = advance([cross_sum, ffn_sum, norms], self_d[0])
    self_sum = Reduction(after(self_d[1], *sends), [(0, 4, "yxz"), (4, 8, "xzy")], attention_finish((3,)))
    first_back = after(first_back, *sends)
    self_e = attention_bwd_call(
        dec_lengths, first_back, [tokens], self_pieces[::2], self_saved, plan_of((0, 2)), None, None
    )
    self_sum.begin(self_e[1], self_e[0])
    sends = advance([self_sum, norms], self_e[0])
    grad_tokens = inputs_back_call(
        after(first_scaled, *sends), [(self_d[0], self_pieces[1::2]), (self_e[0], self_pieces[::2])], (0, 1, 2)
    )
    sends = advance([cross_sum, ffn_sum], *sends)
    sends = advance([self_sum, norms], *sends, grad_tokens)
    sends = advance([cross_sum, ffn_sum], *sends)
    sends = advance([self_sum, norms], *sends)
    sends = advance([cross_sum], *sends)
    sends = advance([self_sum], *sends)
    grad_memory = inputs_back_call(
        None, [(after(memory_part, *sends), cross_pieces[1::2] + cross_pieces[::2])], (1, 2)
    )
    advance([cross_sum, norms], *sends, grad_memory)
    norm_total = norms.values[0]
    advance([self_sum], grad_memory)
    self_sum, cross_sum, ffn_sum = self_sum.total, cross_sum.total, ffn_sum.total

    return (
        out_rows,
        grad_tokens,
        grad_memory,
        *self_sum,
        *cross_sum,
        *ffn_sum,
        norm_total[:3],
        norm_total[3:6],
    )


def sentence_fits(mesh, tokens, memory, dec_lengths):
    shape = dict(mesh.shape)
    rows = tokens.shape[0] // mesh.size
    sentences = dec_lengths.shape[1]
    return (
        shape["tensor"] == 4
        and shape["dp"] == 8
        and sentences == 4
        and rows == 512
        and memory.shape[0] // mesh.size == rows
        and tokens.shape[1] == 1024
    )


def smooth_gate(values):
    return jax.nn.gelu(values, approximate=True)


def norm_rows(hidden, norm_gain, norm_bias):
    center = hidden - jnp.mean(hidden, axis=-1, keepdims=True)
    inverse = lax.rsqrt(jnp.mean(center * center, axis=-1, keepdims=True) + NORM_EPSILON)
    normed = center * inverse
    return (normed * norm_gain + norm_bias, normed, inverse)


def norm_back(gradient, normed, inverse, norm_gain):
    scaled = gradient * norm_gain
    grad_in = inverse * (
        scaled
        - jnp.mean(scaled, axis=-1, keepdims=True)
        - normed * jnp.mean(scaled * normed, axis=-1, keepdims=True)
    )
    return (grad_in, jnp.sum(gradient * normed, axis=0), jnp.sum(gradient, axis=0))


def head_view(values, sentences):
    return values.reshape(sentences, -1, values.shape[1] // HEAD_DIM, HEAD_DIM)


def masked_scores(query_heads, key_heads, key_mask):
    scores = jnp.einsum(
        "sqhe,skhe->shqk", query_heads, key_heads, preferred_element_type=jnp.float32
    ) * HEAD_DIM ** (-0.5)
    return jnp.where(key_mask, scores, MASKED_SCORE)


def attention_forward(query_rows, key_rows, value_rows, key_mask, sentences):
    scores = masked_scores(
        head_view(query_rows, sentences), head_view(key_rows, sentences), key_mask
    )
    row_peak = jnp.max(scores, axis=-1, keepdims=True)
    exponent_terms = jnp.exp(scores - row_peak)
    row_sum = jnp.sum(exponent_terms, axis=-1, keepdims=True)
    softmax_probs = exponent_terms / row_sum
    attended = jnp.einsum(
        "shqk,skhe->sqhe",
        softmax_probs.astype(jnp.bfloat16),
        head_view(value_rows, sentences),
        preferred_element_type=jnp.float32,
    ).astype(jnp.bfloat16)
    return (attended.reshape(query_rows.shape), row_peak + jnp.log(row_sum))


def attention_backward(query_rows, key_rows, value_rows, key_mask, log_total, grad_rows, sentences):
    query_heads = head_view(query_rows, sentences)
    key_heads = head_view(key_rows, sentences)
    value_heads = head_view(value_rows, sentences)
    grad_heads = head_view(grad_rows, sentences)
    softmax_probs = jnp.exp(masked_scores(query_heads, key_heads, key_mask) - log_total)
    grad_probs = jnp.einsum(
        "sqhe,skhe->shqk", grad_heads, value_heads, preferred_element_type=jnp.float32
    )
    row_delta = jnp.sum(softmax_probs * grad_probs, axis=-1, keepdims=True)
    grad_scores = (softmax_probs * (grad_probs - row_delta)).astype(jnp.bfloat16)
    score_scale = HEAD_DIM ** (-0.5)
    grad_query = (
        jnp.einsum("shqk,skhe->sqhe", grad_scores, key_heads, preferred_element_type=jnp.float32)
        * score_scale
    ).astype(jnp.bfloat16)
    grad_key = (
        jnp.einsum("shqk,sqhe->skhe", grad_scores, query_heads, preferred_element_type=jnp.float32)
        * score_scale
    ).astype(jnp.bfloat16)
    grad_value = jnp.einsum(
        "shqk,sqhe->skhe",
        softmax_probs.astype(jnp.bfloat16),
        grad_heads,
        preferred_element_type=jnp.float32,
    ).astype(jnp.bfloat16)
    return (
        grad_query.reshape(query_rows.shape),
        grad_key.reshape(key_rows.shape),
        grad_value.reshape(value_rows.shape),
    )


def body(
    tokens,
    memory,
    dec_lengths,
    mem_lengths,
    self_qkv,
    self_out,
    cross_q,
    cross_kv,
    cross_out,
    ffn_in,
    ffn_out,
    norm_gains,
    norm_biases,
    cotangent,
):
    row_share = tokens.shape[0]
    sentences = dec_lengths.shape[1]
    all_tokens, all_memory = (
        lax.all_gather(tokens, "tensor", axis=0, tiled=True),
        lax.all_gather(memory, "tensor", axis=0, tiled=True),
    )
    sentence_len = all_tokens.shape[0] // sentences
    memory_len = all_memory.shape[0] // sentences
    positions = jnp.arange(sentence_len, dtype=jnp.int32)
    self_mask = (
        (positions[None, :] <= positions[:, None])[None]
        & (positions[None, None, :] < dec_lengths[0][:, None, None])
    )[:, None]
    memory_positions = jnp.arange(memory_len, dtype=jnp.int32)
    cross_mask = (memory_positions[None, :] < mem_lengths[0][:, None])[:, None, None, :]

    def branch_rows(attended, weight):
        return lax.psum_scatter(
            jnp.dot(attended, weight, preferred_element_type=jnp.float32).astype(jnp.bfloat16),
            "tensor",
            scatter_dimension=0,
            tiled=True,
        ).astype(jnp.float32)

    def branch_grad(grad_rows, attended, weight):
        grad_low = grad_rows.astype(jnp.bfloat16)
        grad_all = lax.all_gather(grad_low, "tensor", axis=0, tiled=True)
        grad_attended = jnp.dot(grad_all, weight.T, preferred_element_type=jnp.float32).astype(
            jnp.bfloat16
        )
        weight_part = jnp.dot(attended.T, grad_all, preferred_element_type=jnp.float32)
        return (grad_attended, weight_part)

    def gather_normed(values):
        return lax.all_gather(values, "tensor", axis=0, tiled=True)

    def head_input_sum(term):
        return lax.psum_scatter(
            term(jnp.int32(0), row_share * lax.axis_size("tensor")).astype(jnp.bfloat16),
            "tensor",
            scatter_dimension=0,
            tiled=True,
        ).astype(jnp.float32)

    self_proj = jnp.einsum(
        "td,cde->cte", all_tokens, self_qkv, preferred_element_type=jnp.float32
    ).astype(jnp.bfloat16)
    self_att, self_lse = attention_forward(
        self_proj[0], self_proj[1], self_proj[2], self_mask, sentences
    )
    self_branch = branch_rows(self_att, self_out)
    first_norm, first_hat, first_inv = norm_rows(
        RESIDUAL_ALPHA * tokens.astype(jnp.float32) + self_branch, norm_gains[0], norm_biases[0]
    )
    first_all = gather_normed(first_norm.astype(jnp.bfloat16))
    cross_query = jnp.dot(first_all, cross_q, preferred_element_type=jnp.float32).astype(
        jnp.bfloat16
    )
    cross_proj = jnp.einsum(
        "td,cde->cte", all_memory, cross_kv, preferred_element_type=jnp.float32
    ).astype(jnp.bfloat16)
    cross_att, cross_lse = attention_forward(
        cross_query, cross_proj[0], cross_proj[1], cross_mask, sentences
    )
    cross_branch = branch_rows(cross_att, cross_out)
    second_norm, second_hat, second_inv = norm_rows(
        RESIDUAL_ALPHA * first_norm + cross_branch, norm_gains[1], norm_biases[1]
    )
    second_all = gather_normed(second_norm.astype(jnp.bfloat16))
    pre_gate = jnp.dot(second_all, ffn_in, preferred_element_type=jnp.float32)
    activated = smooth_gate(pre_gate).astype(jnp.bfloat16)
    ffn_branch = lax.psum_scatter(
        jnp.dot(activated, ffn_out, preferred_element_type=jnp.float32).astype(jnp.bfloat16),
        "tensor",
        scatter_dimension=0,
        tiled=True,
    ).astype(jnp.float32)
    out_rows, third_hat, third_inv = norm_rows(
        RESIDUAL_ALPHA * second_norm + ffn_branch, norm_gains[2], norm_biases[2]
    )
    grad_third, third_gain, third_bias = norm_back(
        cotangent.astype(jnp.float32), third_hat, third_inv, norm_gains[2]
    )
    grad_ffn_all = lax.all_gather(grad_third.astype(jnp.bfloat16), "tensor", axis=0, tiled=True)
    unused_gate, gate_pull = jax.vjp(smooth_gate, pre_gate)
    grad_act = gate_pull(jnp.dot(grad_ffn_all, ffn_out.T, preferred_element_type=jnp.float32))[
        0
    ].astype(jnp.bfloat16)
    grad_ffn_out = jnp.dot(activated.T, grad_ffn_all, preferred_element_type=jnp.float32)
    grad_ffn_in = jnp.dot(second_all.T, grad_act, preferred_element_type=jnp.float32)
    grad_second = RESIDUAL_ALPHA * grad_third + lax.psum_scatter(
        jnp.dot(grad_act, ffn_in.T, preferred_element_type=jnp.float32).astype(jnp.bfloat16),
        "tensor",
        scatter_dimension=0,
        tiled=True,
    ).astype(jnp.float32)
    grad_second_in, second_gain, second_bias = norm_back(
        grad_second, second_hat, second_inv, norm_gains[1]
    )
    grad_cross_att, cross_out_part = branch_grad(grad_second_in, cross_att, cross_out)
    grad_cq, grad_ck, grad_cv = attention_backward(
        cross_query, cross_proj[0], cross_proj[1], cross_mask, cross_lse, grad_cross_att, sentences
    )
    grad_cross_q = jnp.dot(first_all.T, grad_cq, preferred_element_type=jnp.float32)
    cross_grads = jnp.stack([grad_ck, grad_cv])
    grad_cross_kv = jnp.einsum(
        "td,cte->cde", all_memory, cross_grads, preferred_element_type=jnp.float32
    )
    grad_memory = lax.psum_scatter(
        jnp.einsum("cte,cde->td", cross_grads, cross_kv, preferred_element_type=jnp.float32).astype(
            jnp.bfloat16
        ),
        "tensor",
        scatter_dimension=0,
        tiled=True,
    ).astype(jnp.float32)

    def cross_input_term(first_row, row_total):
        return jnp.dot(grad_cq, cross_q.T, preferred_element_type=jnp.float32)

    cross_input = head_input_sum(cross_input_term)
    grad_first = RESIDUAL_ALPHA * grad_second_in + cross_input
    grad_first_in, first_gain, first_bias = norm_back(
        grad_first, first_hat, first_inv, norm_gains[0]
    )
    grad_self_att, self_out_part = branch_grad(grad_first_in, self_att, self_out)
    grad_sq, grad_sk, grad_sv = attention_backward(
        self_proj[0], self_proj[1], self_proj[2], self_mask, self_lse, grad_self_att, sentences
    )
    self_grads = jnp.stack([grad_sq, grad_sk, grad_sv])
    grad_self_qkv = jnp.einsum(
        "td,cte->cde", all_tokens, self_grads, preferred_element_type=jnp.float32
    )

    def self_input_term(first_row, row_total):
        return jnp.einsum("cte,cde->td", self_grads, self_qkv, preferred_element_type=jnp.float32)

    self_input = head_input_sum(self_input_term)
    grad_tokens = RESIDUAL_ALPHA * grad_first_in + self_input
    summed = (
        lax.psum_scatter(
            grad_self_qkv.astype(jnp.bfloat16), "dp", scatter_dimension=1, tiled=True
        ).astype(jnp.float32),
        lax.psum_scatter(
            self_out_part.astype(jnp.bfloat16), "dp", scatter_dimension=1, tiled=True
        ).astype(jnp.float32),
        lax.psum_scatter(
            grad_cross_q.astype(jnp.bfloat16), "dp", scatter_dimension=0, tiled=True
        ).astype(jnp.float32),
        lax.psum_scatter(
            grad_cross_kv.astype(jnp.bfloat16), "dp", scatter_dimension=1, tiled=True
        ).astype(jnp.float32),
        lax.psum_scatter(
            cross_out_part.astype(jnp.bfloat16), "dp", scatter_dimension=1, tiled=True
        ).astype(jnp.float32),
        lax.psum_scatter(
            grad_ffn_in.astype(jnp.bfloat16), "dp", scatter_dimension=0, tiled=True
        ).astype(jnp.float32),
        lax.psum_scatter(
            grad_ffn_out.astype(jnp.bfloat16), "dp", scatter_dimension=1, tiled=True
        ).astype(jnp.float32),
    )
    gain_total, bias_total = lax.psum(
        (
            jnp.stack([first_gain, second_gain, third_gain]),
            jnp.stack([first_bias, second_bias, third_bias]),
        ),
        ("dp", "tensor"),
    )
    return (
        out_rows.astype(jnp.bfloat16),
        grad_tokens,
        grad_memory,
        summed[0],
        summed[1],
        summed[2],
        summed[3],
        summed[4],
        summed[5],
        summed[6],
        gain_total,
        bias_total,
    )


def solution(mesh):
    in_specs = (
        P(("dp", "tensor"), None),
        P(("dp", "tensor"), None),
        P("dp", None),
        P("dp", None),
        P(None, None, "tensor"),
        P("tensor", None),
        P(None, "tensor"),
        P(None, None, "tensor"),
        P("tensor", None),
        P(None, "tensor"),
        P("tensor", None),
        P(),
        P(),
        P(("dp", "tensor"), None),
    )
    out_specs = (
        P(("dp", "tensor"), None),
        P(("dp", "tensor"), None),
        P(("dp", "tensor"), None),
        P(None, "dp", "tensor"),
        P("tensor", "dp"),
        P("dp", "tensor"),
        P(None, "dp", "tensor"),
        P("tensor", "dp"),
        P("dp", "tensor"),
        P("tensor", "dp"),
        P(),
        P(),
    )

    def step(*args):
        chosen = sentence_body if sentence_fits(mesh, args[0], args[1], args[2]) else body
        return jax.shard_map(
            chosen, mesh=mesh, in_specs=in_specs, out_specs=out_specs, check_vma=False
        )(*args)

    return step
```

```python
import functools
import jax
import jax.numpy as jnp
from jax import lax
from jax.experimental import pallas as pl
from jax.experimental.pallas import tpu as pltpu
from jax.sharding import PartitionSpec as P

HEAD_DIM = 64
RESIDUAL_ALPHA = 4.16
NORM_EPSILON = 1e-05
MASKED_SCORE = -1000000000.0
SCORE_SCALE = HEAD_DIM ** (-0.5)
UNIT = 128
QUERY_BLOCK = 256
FFN_UNIT = 512
ROW_CHUNK = 128
BF16 = jnp.bfloat16
F32 = jnp.float32


def dot(left, right):
    return lax.dot_general(left, right, (((1,), (0,)), ((), ())), preferred_element_type=F32)


def dot_tn(left, right):
    return lax.dot_general(left, right, (((0,), (0,)), ((), ())), preferred_element_type=F32)


def dot_nt(left, right):
    return lax.dot_general(left, right, (((1,), (1,)), ((), ())), preferred_element_type=F32)


def shard_of(position):
    return ((position >> 2) & 1) | (position & 2) | ((position & 1) << 2)


def copy_of(source, target, sem):
    return pltpu.make_async_copy(source, target, sem)


def own_lanes(rows, head):
    lanes = lax.broadcasted_iota(jnp.int32, rows.shape, 1)
    return jnp.where((lanes >= HEAD_DIM) if head else (lanes < HEAD_DIM), rows, 0.0)


def extended_keys(keys, length):
    lanes = lax.broadcasted_iota(jnp.int32, keys.shape, 1)
    rows = lax.broadcasted_iota(jnp.int32, keys.shape, 0)
    mask = jnp.where((lanes == 0) & (rows >= length), MASKED_SCORE, 0.0).astype(BF16)
    keys = keys.astype(F32)
    return [jnp.concatenate([own_lanes(keys, head).astype(BF16), mask], axis=1) for head in (0, 1)]


def extended_query(query):
    lanes = lax.broadcasted_iota(jnp.int32, query.shape, 1)
    return jnp.concatenate([query, jnp.where(lanes == 0, 1.0, 0.0).astype(BF16)], axis=1)


def fill_diagonal(diagonal):
    keys = lax.broadcasted_iota(jnp.int32, diagonal.shape, 0)
    queries = lax.broadcasted_iota(jnp.int32, diagonal.shape, 1)
    diagonal[...] = jnp.where(keys <= queries, 0.0, MASKED_SCORE)


def key_ranges(block, keys, causal):
    if not causal:
        return [(0, keys)]
    return [(low, low + QUERY_BLOCK) for low in range(0, (block + 1) * QUERY_BLOCK, QUERY_BLOCK)]


def attend_unit(query, keys, values, length, causal, diagonal, lse_ref):
    rows, count = query.shape[0], keys.shape[0]
    values_t = jnp.transpose(values.astype(F32)).astype(BF16)
    wide_keys, wide_query = extended_keys(keys, length), extended_query(query)
    items = [(head, block) for block in range(rows // QUERY_BLOCK) for head in (0, 1)]
    scores, probs, totals, mixed = {}, {}, {}, {}
    for head, block in items:
        part = wide_query[block * QUERY_BLOCK : (block + 1) * QUERY_BLOCK]
        ranges = key_ranges(block, count, causal)
        scores[head, block] = [dot_nt(wide_keys[head][a:b], part) for a, b in ranges]
        if causal:
            scores[head, block][-1] = scores[head, block][-1] + diagonal[...]
    for head, block in items:
        pieces = scores[head, block]
        peak = functools.reduce(jnp.maximum, [jnp.max(p, axis=0, keepdims=True) for p in pieces])
        terms = [jnp.exp(p - peak) for p in pieces]
        total = sum(jnp.sum(t, axis=0, keepdims=True) for t in terms)
        at = slice(block * QUERY_BLOCK, (block + 1) * QUERY_BLOCK)
        lse_ref[head : head + 1, at] = peak + jnp.log(total)
        totals[head, block] = total
        probs[head, block] = jnp.concatenate([t.astype(BF16) for t in terms], axis=0)
    for head, block in items:
        own = values_t[head * HEAD_DIM : (head + 1) * HEAD_DIM, : probs[head, block].shape[0]]
        mixed[head, block] = dot(own, probs[head, block]) / totals[head, block]
    out = [
        jnp.transpose(jnp.concatenate([mixed[0, block], mixed[1, block]], axis=0))
        for block in range(rows // QUERY_BLOCK)
    ]
    return jnp.concatenate(out, axis=0).astype(BF16)


def attend_back_unit(query, keys, values, attended, grad, length, causal, diagonal, lse_ref):
    rows, count = query.shape[0], keys.shape[0]
    blocks = range(rows // QUERY_BLOCK)
    query_f, keys_f, grad_f = (a.astype(F32) for a in (query, keys, grad))
    wide_keys, wide_query = extended_keys(keys, length), extended_query(query)
    delta = jnp.transpose(grad_f * attended.astype(F32))
    deltas = [
        jnp.sum(delta[head * HEAD_DIM : (head + 1) * HEAD_DIM], axis=0, keepdims=True)
        for head in (0, 1)
    ]
    keys_t = jnp.transpose(keys_f).astype(BF16)
    query_own = [own_lanes(query_f, head).astype(BF16) for head in (0, 1)]
    grad_own = [own_lanes(grad_f, head).astype(BF16) for head in (0, 1)]
    items = [(head, block) for block in blocks for head in (0, 1)]
    scores, slopes, probs, back, grad_query = {}, {}, {}, {}, {}
    for head, block in items:
        at = slice(block * QUERY_BLOCK, (block + 1) * QUERY_BLOCK)
        for a, b in key_ranges(block, count, causal):
            scores[head, block, a] = dot_nt(wide_keys[head][a:b], wide_query[at])
            slopes[head, block, a] = dot_nt(values[a:b], grad_own[head][at])
    for head, block in items:
        at = slice(block * QUERY_BLOCK, (block + 1) * QUERY_BLOCK)
        ranges = key_ranges(block, count, causal)
        for a, b in ranges:
            score = scores[head, block, a]
            if causal and (a, b) == ranges[-1]:
                score = score + diagonal[...]
            prob = jnp.exp(score - lse_ref[head : head + 1, at])
            probs[head, block, a] = prob.astype(BF16)
            back[head, block, a] = (prob * (slopes[head, block, a] - deltas[head][:, at])).astype(BF16)
    for head, block in items:
        own = keys_t[head * HEAD_DIM : (head + 1) * HEAD_DIM]
        grad_query[head, block] = sum(
            dot(own[:, a:b], back[head, block, a]) for a, b in key_ranges(block, count, causal)
        )
    grad_keys, grad_values = [], []
    for low in sorted({key[2] for key in back}):
        live = [key for key in back if key[2] == low]
        at = [slice(block * QUERY_BLOCK, (block + 1) * QUERY_BLOCK) for _, block, _ in live]
        grad_values.append(
            dot(
                jnp.concatenate([probs[key] for key in live], axis=1),
                jnp.concatenate([grad_own[key[0]][a] for key, a in zip(live, at)], axis=0),
            )
        )
        grad_keys.append(
            dot(
                jnp.concatenate([back[key] for key in live], axis=1),
                jnp.concatenate([query_own[key[0]][a] for key, a in zip(live, at)], axis=0),
            )
        )
    grad_query = [
        jnp.transpose(jnp.concatenate([grad_query[0, block], grad_query[1, block]], axis=0)) * SCORE_SCALE
        for block in blocks
    ]
    return tuple(
        jnp.concatenate(parts, axis=0).astype(BF16) for parts in (grad_query, grad_keys, grad_values)
    )


def norm_chunk(hidden, gain, bias):
    center = hidden - jnp.mean(hidden, axis=-1, keepdims=True)
    inverse = lax.rsqrt(jnp.mean(center * center, axis=-1, keepdims=True) + NORM_EPSILON)
    normed = center * inverse
    return normed * gain + bias, normed, inverse


def norm_back_chunk(gradient, normed, inverse, gain):
    scaled = gradient * gain
    return inverse * (
        scaled
        - jnp.mean(scaled, axis=-1, keepdims=True)
        - normed * jnp.mean(scaled * normed, axis=-1, keepdims=True)
    )


def fold_rows(values):
    return jnp.sum(values.reshape(values.shape[0] // 8, 8, values.shape[1]), axis=0)


def each_chunk(rows, body, results):
    def step(index, carry):
        at = pl.ds(pl.multiple_of(index * ROW_CHUNK, ROW_CHUNK), ROW_CHUNK)
        body(at)
        for buffer, out, sem in results:
            copy_of(buffer.at[at, :], out.at[at, :], sem).start()
        return carry

    lax.fori_loop(0, rows // ROW_CHUNK, step, 0)
    return [copy_of(*result) for result in results]


def store_shards(target, weight, dp):
    for block in range(8):
        target[shard_of(block ^ dp)] = weight[block * UNIT : (block + 1) * UNIT]


SMEM = pl.BlockSpec(memory_space=pltpu.SMEM)
VMEM = pl.BlockSpec(memory_space=pltpu.VMEM)
ANY = pl.BlockSpec(memory_space=pl.ANY)


def params(limit=62):
    return pltpu.CompilerParams(vmem_limit_bytes=limit * 1024 * 1024)


def cost_of(microseconds):
    return pl.CostEstimate(flops=int(microseconds * 1.1e9), bytes_accessed=4 << 20, transcendentals=0)


def sds(shape, dtype):
    return jax.ShapeDtypeStruct(shape, dtype)


def position():
    dp = lax.axis_index("dp")
    return dp & 3, dp, (dp >> 1) & 1


def weight_copies(pieces, wbuf, obuf, wsem, osem, columns=(0, 1, 2)):
    groups, outs = [[], [], []], []
    wide = 2 * UNIT
    order, _, inner = position()
    for index, refs in enumerate(pieces):
        at = slice(index * wide, (index + 1) * wide)
        if len(refs[-1].shape) == 2:
            column = 0
            for ref in refs[:-1]:
                for source in [ref] if len(ref.shape) == 2 else [ref.at[c] for c in range(ref.shape[0])]:
                    if column in columns:
                        low = (columns.index(column) * len(pieces) + index) * wide
                        groups[column].append(copy_of(source, wbuf.at[:, low : low + wide], wsem.at[column, index, 0]))
                    column += 1
            if obuf is not None:
                outs.append(copy_of(refs[-1], obuf.at[at, :], osem.at[index, 0]))
            continue
        parts = [refs[0].at[n] for n in range(refs[0].shape[0])] if len(refs[0].shape) == 4 else refs
        rows = parts[0].shape[1]
        part = wide // len(parts)
        for quarter, ref in enumerate(parts):
            place = quarter ^ (order if len(parts) == 4 else inner)
            for column in columns:
                low = (columns.index(column) * len(pieces) + index) * wide
                groups[column].append(
                    copy_of(
                        ref.at[column],
                        wbuf.at[pl.ds(pl.multiple_of(place * rows, rows), rows), low : low + wide],
                        wsem.at[column, index, quarter],
                    )
                )
            for block in range(4 if obuf is not None else 0):
                outs.append(
                    copy_of(
                        ref.at[3, block * part : (block + 1) * part, :],
                        obuf.at[pl.ds(pl.multiple_of(index * wide + place * part, part), part), block * wide : (block + 1) * wide],
                        osem.at[index, 4 * quarter + block],
                    )
                )
    return groups, outs


def attention_fwd_call(lengths, residual, others, pieces, partial, norm):
    rows, depth = others[0].shape
    causal = len(others) == 1
    number, wide = 2 * len(pieces), 2 * len(pieces) * UNIT
    last, has_partial = norm is not None, partial is not None

    def kernel(*refs):
        it = iter(refs)
        len_ref = next(it)
        in_refs = [next(it) for _ in others]
        gain_ref, bias_ref = (next(it), next(it)) if last else (None, None)
        old_rows = [next(it) for _ in residual[1:]] if last else []
        res_in = next(it) if last else None
        part_in = next(it) if has_partial else None
        w_refs = [[next(it) for _ in piece] for piece in pieces]
        unit_outs, lse_ref = [next(it) for _ in range(4)], next(it)
        if last:
            norm_outs = [next(it) for _ in range(3)]
        else:
            sum_ref = next(it)
        wbuf, obuf, att_all, diagonal, wsem, osem, lsem, usem = (next(it) for _ in range(8))
        q_ref, k_ref, v_ref, att_ref = (next(it) for _ in range(4))
        if last:
            acc, old, low_ref, hat_ref, inv_ref = (next(it) for _ in range(5))
        length = len_ref[0, lax.axis_index("tensor")]
        groups, outs = weight_copies(w_refs, wbuf, obuf, wsem, osem)
        for copies in groups + [outs]:
            for copy in copies:
                copy.start()
        target = acc if last else sum_ref
        late = []
        if has_partial:
            late.append(copy_of(part_in, target, lsem.at[0]))
        if last:
            late.append(copy_of(res_in, old, lsem.at[1]))
        for copy in late:
            copy.start()
        if causal:
            fill_diagonal(diagonal)
        for c, result in enumerate((q_ref, k_ref, v_ref)):
            for copy in groups[c]:
                copy.wait()
            rows_in = in_refs[0] if causal or c == 0 else in_refs[1]
            proj = dot(rows_in[...], wbuf[:, c * wide : (c + 1) * wide]).astype(BF16)
            if c == 0:
                proj = (proj.astype(F32) * SCORE_SCALE).astype(BF16)
            for index in range(number):
                result[index] = proj[:, index * UNIT : (index + 1) * UNIT]

        flushes = [copy_of(*pair, usem.at[index]) for index, pair in enumerate(zip((q_ref, k_ref, v_ref, att_ref), unit_outs))]
        for copy in flushes[:3]:
            copy.start()

        def step(first, carry):
            for u in [first * 4 + inner for inner in range(4)]:
                attended = attend_unit(q_ref[u], k_ref[u], v_ref[u], length, causal, diagonal, lse_ref.at[u])
                att_ref[u] = attended
                att_all[:, pl.ds(pl.multiple_of(u * UNIT, UNIT), UNIT)] = attended
            return carry

        lax.fori_loop(0, number // 4, step, 0)
        flushes[3].start()
        for copy in outs + late:
            copy.wait()
        if has_partial:
            target[...] += dot(att_all[...], obuf[...])
        else:
            target[...] = dot(att_all[...], obuf[...])
        if last:
            def chunk(at):
                before = old[at, :].astype(F32)
                if old_rows:
                    before = before * old_rows[0][...] + old_rows[1][...]
                normed, hat, inverse = norm_chunk(RESIDUAL_ALPHA * before + acc[at, :], gain_ref[...], bias_ref[...])
                low_ref[at, :] = normed.astype(BF16)
                hat_ref[at, :] = hat
                inv_ref[at, :] = jnp.broadcast_to(inverse, (ROW_CHUNK, 128))

            triples = zip((low_ref, hat_ref, inv_ref), norm_outs)
            flushes += each_chunk(rows, chunk, [(*pair, usem.at[4 + index]) for index, pair in enumerate(triples)])
        for copy in flushes:
            copy.wait()

    unit_rows = sds((number, rows, UNIT), BF16)
    shapes = [unit_rows] * 4 + [sds((number, 2, rows), F32)]
    if last:
        shapes += [sds((rows, depth), BF16), sds((rows, depth), F32), sds((rows, 128), F32)]
    else:
        shapes += [sds((rows, depth), F32)]
    args = [lengths, *others]
    if last:
        args += [*norm, *residual[1:]]
    tail = ([residual[0]] if last else []) + ([partial] if has_partial else [])
    tail += [array for piece in pieces for array in piece]
    scratch = [
        pltpu.VMEM((depth, 3 * wide), BF16),
        pltpu.VMEM((wide, depth), BF16),
        pltpu.VMEM((rows, wide), BF16),
        pltpu.VMEM((QUERY_BLOCK, QUERY_BLOCK), F32),
        pltpu.SemaphoreType.DMA((3, len(pieces), 4)),
        pltpu.SemaphoreType.DMA((len(pieces), 16)),
        pltpu.SemaphoreType.DMA((2,)),
        pltpu.SemaphoreType.DMA((7,)),
    ]
    scratch += [pltpu.VMEM((number, rows, UNIT), BF16)] * 4
    if last:
        scratch += [pltpu.VMEM((rows, depth), F32), pltpu.VMEM((rows, depth), residual[0].dtype)]
        scratch += [pltpu.VMEM((rows, depth), BF16), pltpu.VMEM((rows, depth), F32), pltpu.VMEM((rows, 128), F32)]
    return pl.pallas_call(
        kernel,
        out_shape=shapes,
        in_specs=[SMEM] + [VMEM] * (len(args) - 1) + [ANY] * len(tail),
        out_specs=[ANY] * 4 + [VMEM] + ([ANY] * 3 if last else [VMEM]),
        scratch_shapes=scratch,
        compiler_params=params(),
        cost_estimate=cost_of(0.6 * number),
        name="self_fwd" if causal else "cross_fwd",
    )(*args, *tail)


def attention_bwd_call(lengths, grad_low, others, pieces, saved, plan, carried, norm, results=1):
    rows, depth = grad_low.shape
    causal = len(others) == 1
    number, n_in, wide = len(plan), len(others), len(plan) * UNIT
    last = norm is not None
    skip = 1 if last else 0

    def kernel(*refs):
        it = iter(refs)
        len_ref = next(it)
        h_ref = next(it)
        in_refs = [next(it) for _ in range(n_in)]
        gain_ref = next(it) if last else None
        late_in = [next(it), next(it)] if last else []
        acc_in = next(it) if last else None
        w_refs = [[next(it) for _ in piece] for piece in pieces]
        s_refs = [[next(it) for _ in call] for call in saved]
        if last:
            low_ref, scaled_ref, gsum_ref, bsum_ref = (next(it) for _ in range(4))
        dall_ref = next(it)
        g_refs = [next(it) for _ in range(results)]
        wbuf, obuf, sbuf, lbuf, att_all, grad_all = (next(it) for _ in range(6))
        stage, diagonal = next(it), next(it)
        if last:
            dquery, acc, hat, inv, low_buf, scaled_buf, nsem = (next(it) for _ in range(7))
        wsem, osem, ssem, gsem, lsem = (next(it) for _ in range(5))
        length, dp = len_ref[0, lax.axis_index("tensor")], lax.axis_index("dp")

        groups, o_copies = weight_copies(w_refs, wbuf, obuf, wsem, osem, (0,) if last else ())
        for copy in o_copies:
            copy.start()
        s_copies = []
        for index, unit in enumerate(plan):
            lanes = slice(index * UNIT, (index + 1) * UNIT)
            call = s_refs[unit[0]]
            for c in range(3):
                s_copies.append(copy_of(call[c].at[unit[1]], sbuf.at[index, c], ssem.at[c, index]))
            s_copies.append(copy_of(call[3].at[unit[1]], att_all.at[:, lanes], ssem.at[3, index]))
            s_copies.append(copy_of(call[4].at[unit[1]], lbuf.at[index], ssem.at[4, index]))
        late = []
        if last:
            late = groups[0] + [
                copy_of(source, target, lsem.at[index])
                for index, (source, target) in enumerate(((acc_in, acc), (late_in[0], hat), (late_in[1], inv)))
            ]
        for copy in s_copies + late:
            copy.start()
        if causal:
            fill_diagonal(diagonal)
        for copy in o_copies:
            copy.wait()
        grad_att = dot_nt(h_ref[...], obuf[...]).astype(BF16)
        for index in range(number):
            grad_all[index] = grad_att[:, index * UNIT : (index + 1) * UNIT]
        for copy in s_copies:
            copy.wait()

        def step(first, carry):
            units = [first * 2, first * 2 + 1]
            ats = [pl.ds(pl.multiple_of(u * UNIT, UNIT), UNIT) for u in units]
            parts = [
                attend_back_unit(
                    sbuf[u, 0], sbuf[u, 1], sbuf[u, 2], att_all[:, at], grad_all[u], length, causal, diagonal, lbuf.at[u]
                )
                for u, at in zip(units, ats)
            ]
            for u, at, part in zip(units, ats, parts):
                if last:
                    dquery[:, at] = part[0]
                for c in range(skip, 3):
                    dall_ref[:, pl.ds(pl.multiple_of((c - skip) * wide + u * UNIT, UNIT), UNIT)] = part[c]
            return carry

        lax.fori_loop(0, number // 2, step, 0)
        share = number // 2 // results

        def keep(rows_in, source, column):
            weight = dot_tn(rows_in[...], source).astype(BF16)
            for index in range(number):
                piece = index // 2
                target = stage.at[piece // share, (index % 2) * 4 + column, piece % share]
                store_shards(target, weight[:, index * UNIT : (index + 1) * UNIT], dp)

        if last:
            keep(in_refs[0], dquery[...], 0)
        for c in range(skip, 3):
            keep(in_refs[-1], dall_ref[:, (c - skip) * wide : (c - skip + 1) * wide], c)
        keep(h_ref, att_all[...], 3)
        g_copies = [copy_of(stage.at[index], ref, gsem.at[index]) for index, ref in enumerate(g_refs)]
        for copy in g_copies:
            copy.start()
        for copy in late:
            copy.wait()
        if last:
            acc[...] += dot_nt(dquery[...], wbuf[...])
            g_copies += norm_back_rows(
                acc, hat, inv, gain_ref, low_buf, scaled_buf, (low_ref, scaled_ref), nsem, gsum_ref, bsum_ref, rows
            )
        for copy in g_copies:
            copy.wait()

    big = sds((rows, depth), F32)
    shapes = []
    if last:
        shapes += [sds((rows, depth), BF16), big, sds((8, depth), F32), sds((8, depth), F32)]
    shapes.append(sds((rows, (3 - skip) * wide), BF16))
    specs_out = ([ANY] * 2 + [VMEM] * 3 if last else [VMEM]) + [ANY] * results
    shapes += [sds((8, number // 2 // results, 8, UNIT, UNIT), BF16)] * results
    args = [lengths, grad_low, *others] + ([norm[2]] if last else [])
    tail = [norm[0], norm[1], carried] if last else []
    tail += [array for piece in pieces for array in piece]
    for call in saved:
        tail += call
    scratch = [
        pltpu.VMEM((depth, wide) if last else (16, 128), BF16),
        pltpu.VMEM((wide, depth), BF16),
        pltpu.VMEM((number, 3, rows, UNIT), BF16),
        pltpu.VMEM((number, 2, rows), F32),
        pltpu.VMEM((rows, wide), BF16),
        pltpu.VMEM((number, rows, UNIT), BF16),
        pltpu.VMEM((results, 8, number // 2 // results, 8, UNIT, UNIT), BF16),
        pltpu.VMEM((QUERY_BLOCK, QUERY_BLOCK), F32),
    ]
    if last:
        scratch += [pltpu.VMEM((rows, wide), BF16), pltpu.VMEM((rows, depth), F32), pltpu.VMEM((rows, depth), F32), pltpu.VMEM((rows, 128), F32)]
        scratch += [pltpu.VMEM((rows, depth), BF16), pltpu.VMEM((rows, depth), F32), pltpu.SemaphoreType.DMA((2,))]
    scratch += [
        pltpu.SemaphoreType.DMA((3, len(pieces), 4)),
        pltpu.SemaphoreType.DMA((len(pieces), 16)),
        pltpu.SemaphoreType.DMA((5, number)),
        pltpu.SemaphoreType.DMA((results,)),
        pltpu.SemaphoreType.DMA((4,)),
    ]
    return pl.pallas_call(
        kernel,
        out_shape=shapes,
        in_specs=[SMEM] + [VMEM] * (len(args) - 1) + [ANY] * len(tail),
        out_specs=specs_out,
        scratch_shapes=scratch,
        compiler_params=params(),
        cost_estimate=cost_of(4.2 * number),
        name="self_bwd" if causal else "cross_bwd",
    )(*args, *tail)


def inputs_back_call(base, parts, columns):
    rows, depth = parts[0][0].shape[0], parts[0][1][0][0].shape[-2]

    def kernel(*refs):
        it = iter(refs)
        base_ref = next(it) if base is not None else None
        grads = [next(it) for _ in parts]
        w_refs = [[[next(it) for _ in piece] for piece in pieces] for _, pieces in parts]
        out = next(it)
        bufs, sems = [next(it) for _ in parts], [next(it) for _ in parts]
        copies = []
        for index in range(len(parts)):
            groups, _ = weight_copies(w_refs[index], bufs[index], None, sems[index], None, columns)
            copies.append([copy for group in groups for copy in group])
            for copy in copies[-1]:
                copy.start()
        if base is not None:
            out[...] = base_ref[...]
        for index in range(len(parts)):
            for copy in copies[index]:
                copy.wait()
            if index or base is not None:
                out[...] += dot_nt(grads[index][...], bufs[index][...])
            else:
                out[...] = dot_nt(grads[index][...], bufs[index][...])

    args = ([base] if base is not None else []) + [grad for grad, _ in parts]
    tail = [array for _, pieces in parts for piece in pieces for array in piece]
    return pl.pallas_call(
        kernel,
        out_shape=sds((rows, depth), F32),
        in_specs=[VMEM] * len(args) + [ANY] * len(tail),
        out_specs=VMEM,
        scratch_shapes=[pltpu.VMEM((depth, grad.shape[1]), BF16) for grad, _ in parts]
        + [pltpu.SemaphoreType.DMA((3, len(pieces), 4)) for _, pieces in parts],
        compiler_params=params(),
        cost_estimate=cost_of(7),
        name="inputs_back",
    )(*args, *tail)


def norm_back_rows(acc, hat, inv, gain_ref, low_buf, scaled_buf, outs, sems, gsum_ref, bsum_ref, rows):
    gsum_ref[...] = jnp.zeros_like(gsum_ref)
    bsum_ref[...] = jnp.zeros_like(bsum_ref)

    def chunk(at):
        gradient, normed = acc[at, :], hat[at, :]
        grad_in = norm_back_chunk(gradient, normed, inv[at, :1], gain_ref[...])
        low_buf[at, :] = grad_in.astype(BF16)
        scaled_buf[at, :] = RESIDUAL_ALPHA * grad_in
        gsum_ref[...] += fold_rows(gradient * normed)
        bsum_ref[...] += fold_rows(gradient)

    pairs = zip((low_buf, scaled_buf), outs)
    return each_chunk(rows, chunk, [(*pair, sems.at[index]) for index, pair in enumerate(pairs)])


GELU_SCALE = 0.7978845608028654
GELU_CUBE = 0.044715


def gelu_and_slope(pre):
    square = pre * pre
    inner = pre * (GELU_SCALE + (GELU_SCALE * GELU_CUBE) * square)
    curve = jnp.tanh(inner)
    half = 0.5 + 0.5 * curve
    slope = half * (1.0 + pre * (1.0 - curve) * (GELU_SCALE + (3.0 * GELU_SCALE * GELU_CUBE) * square))
    return pre * half, slope


FFN_PART = FFN_UNIT // 2


def ffn_copies(pieces, ubuf, dbuf, usem, dsem):
    ups, downs = [], []
    order, _, _ = position()
    for index, refs in enumerate(pieces):
        wide = 2 * FFN_UNIT
        at = slice(index * wide, (index + 1) * wide)
        if len(refs) == 2:
            ups.append([copy_of(refs[0], ubuf.at[:, at], usem.at[index, 0])])
            downs.append([copy_of(refs[1], dbuf.at[at, :], dsem.at[index, 0])])
            continue
        ups.append([])
        downs.append([])
        rows = refs[0].shape[1]
        for quarter in range(4):
            up = refs[quarter].at[0]
            down = refs[quarter].at[1] if quarter < 3 else refs[4].at[0]
            place = (quarter ^ order) * rows
            ups[-1].append(copy_of(up, ubuf.at[pl.ds(pl.multiple_of(place, rows), rows), at], usem.at[index, quarter]))
            downs[-1].append(
                copy_of(down, dbuf.at[pl.ds(pl.multiple_of(index * wide + place, rows), rows), :], dsem.at[index, quarter])
            )
    return ups, downs


def ffn_fwd_call(inputs, pieces, partial, final):
    rows, depth = inputs.shape
    number = 2 * len(pieces)
    last, has_partial = final is not None, partial is not None

    def kernel(*refs):
        it = iter(refs)
        x_ref = next(it)
        if last:
            gain_old, bias_old, gain_ref, bias_ref = (next(it) for _ in range(4))
            late_in = [next(it), next(it)]
        part_in = next(it) if has_partial else None
        w_refs = [[next(it) for _ in piece] for piece in pieces]
        if last:
            norm_outs = [next(it) for _ in range(3)]
            gsum_ref, bsum_ref = next(it), next(it)
        else:
            sum_ref = next(it)
        act_ref, slope_ref = next(it), next(it)
        ubuf, dbuf, abuf, sbuf, pbuf, psem = (next(it) for _ in range(6))
        if last:
            acc, hat, cot, lsem, out_ref, low_ref, scaled_ref, nsem = (next(it) for _ in range(8))
        wsem, gsem = next(it), next(it)
        target = acc if last else sum_ref

        up_copies, down_copies = ffn_copies(w_refs, ubuf, dbuf, wsem.at[0], wsem.at[1])
        for copies in up_copies + down_copies:
            for copy in copies:
                copy.start()
        if has_partial:
            part_copy = copy_of(part_in, target, psem)
            part_copy.start()
        if last:
            late = [copy_of(late_in[0], hat, lsem.at[0]), copy_of(late_in[1], cot, lsem.at[1])]
            for copy in late:
                copy.start()
        saves = []

        def gate(pre, index):
            activated, slope = gelu_and_slope(pre)
            abuf[:, index * FFN_UNIT : (index + 1) * FFN_UNIT] = activated.astype(BF16)
            sbuf[:, index * FFN_UNIT : (index + 1) * FFN_UNIT] = slope.astype(BF16)

        for index in range(number):
            if index % 2 == 0:
                for copy in up_copies[index // 2]:
                    copy.wait()
            if index:
                gate(pbuf[(index - 1) % 2], index - 1)
            pbuf[index % 2] = dot(x_ref[...], ubuf[:, index * FFN_UNIT : (index + 1) * FFN_UNIT])
        gate(pbuf[(number - 1) % 2], number - 1)
        for index in range(number):
            at = slice(index * FFN_UNIT, (index + 1) * FFN_UNIT)
            saves += [
                copy_of(abuf.at[:, at], act_ref.at[index], gsem.at[0, index]),
                copy_of(sbuf.at[:, at], slope_ref.at[index], gsem.at[1, index]),
            ]
        for copy in saves:
            copy.start()
        for copies in down_copies:
            for copy in copies:
                copy.wait()
        if has_partial:
            part_copy.wait()
            target[...] += dot(abuf[...], dbuf[...])
        else:
            target[...] = dot(abuf[...], dbuf[...])
        if last:
            for copy in late:
                copy.wait()
            gsum_ref[...] = jnp.zeros_like(gsum_ref)
            bsum_ref[...] = jnp.zeros_like(bsum_ref)

            def chunk(at):
                old = hat[at, :] * gain_old[...] + bias_old[...]
                normed, xhat, inverse = norm_chunk(RESIDUAL_ALPHA * old + acc[at, :], gain_ref[...], bias_ref[...])
                out_ref[at, :] = normed.astype(BF16)
                gradient = cot[at, :].astype(F32)
                grad_in = norm_back_chunk(gradient, xhat, inverse, gain_ref[...])
                low_ref[at, :] = grad_in.astype(BF16)
                scaled_ref[at, :] = RESIDUAL_ALPHA * grad_in
                gsum_ref[...] += fold_rows(gradient * xhat)
                bsum_ref[...] += fold_rows(gradient)

            triples = zip((out_ref, low_ref, scaled_ref), norm_outs)
            saves += each_chunk(rows, chunk, [(*pair, nsem.at[index]) for index, pair in enumerate(triples)])
        for copy in saves:
            copy.wait()

    big, low = sds((rows, depth), F32), sds((rows, depth), BF16)
    if last:
        shapes = [low, low, big, sds((8, depth), F32), sds((8, depth), F32)]
    else:
        shapes = [big]
    specs_out = ([ANY] * 3 + [VMEM] * 2 if last else [VMEM]) + [ANY, ANY]
    shapes += [sds((number, rows, FFN_UNIT), BF16)] * 2
    args = [inputs]
    if last:
        args += [final[1], final[2], final[4], final[5]]
    specs = [VMEM] * len(args)
    tail = ([final[0], final[3]] if last else []) + ([partial] if has_partial else []) + [array for piece in pieces for array in piece]
    scratch = [
        pltpu.VMEM((depth, number * FFN_UNIT), BF16),
        pltpu.VMEM((number * FFN_UNIT, depth), BF16),
        pltpu.VMEM((rows, number * FFN_UNIT), BF16),
        pltpu.VMEM((rows, number * FFN_UNIT), BF16),
        pltpu.VMEM((2, rows, FFN_UNIT), F32),
        pltpu.SemaphoreType.DMA,
    ]
    if last:
        scratch += [
            pltpu.VMEM((rows, depth), F32),
            pltpu.VMEM((rows, depth), F32),
            pltpu.VMEM((rows, depth), BF16),
            pltpu.SemaphoreType.DMA((2,)),
            pltpu.VMEM((rows, depth), BF16),
            pltpu.VMEM((rows, depth), BF16),
            pltpu.VMEM((rows, depth), F32),
            pltpu.SemaphoreType.DMA((3,)),
        ]
    scratch += [pltpu.SemaphoreType.DMA((2, len(pieces), 4)), pltpu.SemaphoreType.DMA((2, number))]
    return pl.pallas_call(
        kernel,
        out_shape=shapes,
        in_specs=specs + [ANY] * len(tail),
        out_specs=specs_out,
        scratch_shapes=scratch,
        compiler_params=params(),
        cost_estimate=cost_of(12),
        name="ffn_fwd",
    )(*args, *tail)


def ffn_bwd_call(grad_low, inputs, pieces, saved, plan, carried, norm):
    rows, depth = inputs.shape
    number = len(plan)
    last = norm is not None

    def kernel(*refs):
        it = iter(refs)
        g_in, x_ref = next(it), next(it)
        gain_ref = next(it) if last else None
        late_in = [next(it), next(it)] if last else []
        acc_in = next(it)
        w_refs = [[next(it) for _ in piece] for piece in pieces]
        s_refs = [[next(it) for _ in call] for call in saved]
        if last:
            low_ref, scaled_ref, gsum_ref, bsum_ref = (next(it) for _ in range(4))
        else:
            sum_ref = next(it)
        g_ref = next(it)
        ubuf, dbuf, abuf, sbuf, gbuf, stage, psem = (next(it) for _ in range(7))
        if last:
            acc, hat, inv, lsem, low_buf, scaled_buf, nsem = (next(it) for _ in range(7))
        wsem, ssem, gsem = next(it), next(it), next(it)
        dp = lax.axis_index("dp")
        target = acc if last else sum_ref

        ups, downs = ffn_copies(w_refs, ubuf, dbuf, wsem.at[0], wsem.at[1])
        slopes, acts = [], []
        for index, (call, at) in enumerate(plan):
            lanes = slice(index * FFN_UNIT, (index + 1) * FFN_UNIT)
            slopes.append(copy_of(s_refs[call][1].at[at], sbuf.at[index], ssem.at[0, index]))
            acts.append(copy_of(s_refs[call][0].at[at], abuf.at[:, lanes], ssem.at[1, index]))
        for copies in downs + [slopes, acts] + ups:
            for copy in copies:
                copy.start()
        part_copy = copy_of(acc_in, target, psem)
        part_copy.start()
        if last:
            late = [copy_of(late_in[0], hat, lsem.at[0]), copy_of(late_in[1], inv, lsem.at[1])]
            for copy in late:
                copy.start()
        for index in range(number):
            if index % 2 == 0:
                for copy in downs[index // 2]:
                    copy.wait()
            slopes[index].wait()
            grad_act = dot_nt(g_in[...], dbuf[index * FFN_UNIT : (index + 1) * FFN_UNIT, :]) * sbuf[index].astype(F32)
            gbuf[:, index * FFN_UNIT : (index + 1) * FFN_UNIT] = grad_act.astype(BF16)
        for copy in acts:
            copy.wait()

        def keep(rows_in, source, column):
            for half in range(number // 2):
                wide = 2 * FFN_UNIT
                weight = dot_tn(rows_in[...], source[:, half * wide : (half + 1) * wide]).astype(BF16)
                for inner in range(4):
                    part = weight[:, inner * FFN_PART : (inner + 1) * FFN_PART]
                    store_shards(stage.at[2 * inner + column, half], part, dp)

        keep(x_ref, gbuf, 0)
        keep(g_in, abuf, 1)
        g_copies = [copy_of(stage, g_ref, gsem)]
        for copy in g_copies:
            copy.start()
        for copies in ups:
            for copy in copies:
                copy.wait()
        part_copy.wait()
        target[...] += dot_nt(gbuf[...], ubuf[...])
        if last:
            for copy in late:
                copy.wait()
            g_copies += norm_back_rows(
                acc, hat, inv, gain_ref, low_buf, scaled_buf, (low_ref, scaled_ref), nsem, gsum_ref, bsum_ref, rows
            )
        for copy in g_copies:
            copy.wait()

    big, low = sds((rows, depth), F32), sds((rows, depth), BF16)
    shapes = [low, big, sds((8, depth), F32), sds((8, depth), F32)] if last else [big]
    specs_out = ([ANY] * 2 + [VMEM] * 2 if last else [VMEM]) + [ANY]
    shapes.append(sds((8, number // 2, 8, UNIT, FFN_PART), BF16))
    args = [grad_low, inputs] + ([norm[2]] if last else [])
    specs = [VMEM] * len(args)
    tail = ([norm[0], norm[1]] if last else []) + [carried] + [array for piece in pieces for array in piece]
    for call in saved:
        tail += call
    scratch = [
        pltpu.VMEM((depth, number * FFN_UNIT), BF16),
        pltpu.VMEM((number * FFN_UNIT, depth), BF16),
        pltpu.VMEM((rows, number * FFN_UNIT), BF16),
        pltpu.VMEM((number, rows, FFN_UNIT), BF16),
        pltpu.VMEM((rows, number * FFN_UNIT), BF16),
        pltpu.VMEM((8, number // 2, 8, UNIT, FFN_PART), BF16),
        pltpu.SemaphoreType.DMA,
    ]
    if last:
        scratch += [
            pltpu.VMEM((rows, depth), F32),
            pltpu.VMEM((rows, depth), F32),
            pltpu.VMEM((rows, 128), F32),
            pltpu.SemaphoreType.DMA((2,)),
            pltpu.VMEM((rows, depth), BF16),
            pltpu.VMEM((rows, depth), F32),
            pltpu.SemaphoreType.DMA((2,)),
        ]
    scratch += [pltpu.SemaphoreType.DMA((2, len(pieces), 4)), pltpu.SemaphoreType.DMA((2, number)), pltpu.SemaphoreType.DMA]
    return pl.pallas_call(
        kernel,
        out_shape=shapes,
        in_specs=specs + [ANY] * len(tail),
        out_specs=specs_out,
        scratch_shapes=scratch,
        compiler_params=params(),
        cost_estimate=cost_of(17),
        name="ffn_bwd",
    )(*args, *tail)


def combine(jobs, shapes):
    arrays = []
    for terms, _, _, _ in jobs:
        for array, _ in terms:
            if not any(array is known for known in arrays):
                arrays.append(array)
    position = {id(array): index for index, array in enumerate(arrays)}

    def part_shape(array, index):
        kept = []
        for extent, at in zip(array.shape, index + (slice(None),) * (array.ndim - len(index))):
            if isinstance(at, slice):
                kept.append(len(range(*at.indices(extent))))
        return tuple(kept)

    part_shapes = [part_shape(*terms[0]) for terms, _, _, _ in jobs]
    count = sum(len(terms) for terms, _, _, _ in jobs)

    def kernel(*refs):
        ins, outs = refs[: len(arrays)], refs[len(arrays) : len(arrays) + len(shapes)]
        rest = refs[len(arrays) + len(shapes) :]
        term_bufs, sum_bufs, isem, osem = rest[:count], rest[count : count + len(jobs)], rest[-2], rest[-1]
        loads, number = [], 0
        for terms, _, _, _ in jobs:
            loads.append([])
            for array, index in terms:
                loads[-1].append(copy_of(ins[position[id(array)]].at[index], term_bufs[number], isem.at[number]))
                number += 1
        for group in loads:
            for copy in group:
                copy.start()
        stores, number = [], 0
        for job, (terms, out, place, kind) in enumerate(jobs):
            for copy in loads[job]:
                copy.wait()
            bufs = term_bufs[number : number + len(terms)]
            number += len(terms)
            lead = part_shapes[job][:-2]
            size = 1
            for extent in lead:
                size *= extent

            def one(flat, carry, bufs=bufs, lead=lead, target=sum_bufs[job]):
                index, left = [], flat
                for extent in reversed(lead):
                    index.append(lax.rem(left, extent))
                    left = lax.div(left, extent)
                index = tuple(reversed(index))
                total = bufs[0][index].astype(F32)
                for buf in bufs[1:]:
                    total = total + buf[index].astype(F32)
                target[index] = total.astype(target.dtype)
                return carry

            if kind == "range":
                lax.fori_loop(0, size, one, 0)
            else:
                total = bufs[0][0].astype(F32)
                for buf in bufs[1:]:
                    total = total + buf[0].astype(F32)
                sum_bufs[job][...] = jnp.transpose(total) if kind == "turned" else total
            stores.append(copy_of(sum_bufs[job], outs[out].at[place], osem.at[job]))
            stores[-1].start()
        for copy in stores:
            copy.wait()

    scratch = [pltpu.VMEM(part_shapes[job], array.dtype) for job, (terms, _, _, _) in enumerate(jobs) for array, _ in terms]
    for job, (_, out, _, kind) in enumerate(jobs):
        shape = part_shapes[job]
        shape = {"range": shape, "plain": shape[1:], "turned": shape[:0:-1]}[kind]
        scratch.append(pltpu.VMEM(shape, shapes[out].dtype))
    scratch += [pltpu.SemaphoreType.DMA((count,)), pltpu.SemaphoreType.DMA((len(jobs),))]
    return pl.pallas_call(
        kernel,
        out_shape=list(shapes),
        in_specs=[ANY] * len(arrays),
        out_specs=[ANY] * len(shapes),
        scratch_shapes=scratch,
        compiler_params=params(),
        cost_estimate=cost_of(3),
        name="combine",
    )(*arrays)


def swap_pairs(count, mask):
    return [(i, i ^ mask) for i in range(count)]


def to_sibling(values):
    return lax.ppermute(values, "tensor", swap_pairs(4, 1))


def over_y(values):
    return lax.ppermute(values, "tensor", swap_pairs(4, 2))


def over_dp(values, mask):
    return lax.ppermute(values, "dp", swap_pairs(8, mask))


def over_x(values):
    return over_dp(values, 1)


def over_z_near(values):
    return over_dp(values, 2)


def over_z_far(values):
    return over_dp(values, 4)


def after(values, *earlier):
    return lax.optimization_barrier((values, *earlier))[0]


MOVES = {"y": over_y, "x": over_x, "z": over_z_near}


class Reduction:
    def __init__(self, sent, portions, finish):
        self.other, self.finish = to_sibling(sent), finish
        self.portions, self.stage, self.sends, self.total = portions, 0, None, None

    def begin(self, kept, *earlier):
        other = after(self.other, *earlier)
        split = (kept.shape[0], 2, 2, 2, 2, *kept.shape[3:])
        arrays = (kept.reshape(split), other.reshape(split))
        self.blocks, self.tail = kept.shape[0], kept.shape[3:]
        self.terms = [[(array, ("b", "y", "x", "z", "w"), low, {}) for array in arrays] for low, _, _ in self.portions]

    def receive(self, *earlier):
        if self.stage == 4:
            moved = after(over_z_far(self.sends[0]), *earlier)
            for (low, _, _), terms in zip(self.portions, self.terms):
                terms.append((moved, ("b",), low, {}))
        elif self.stage:
            for send, (_, _, orders), terms in zip(self.sends, self.portions, self.terms):
                left = tuple(a for a in ("b", "y", "x", "z", "w") if a not in orders[: self.stage])
                terms.append((after(MOVES[orders[self.stage - 1]](send), *earlier), left, 0, {}))

    def jobs(self, first_out):
        jobs, shapes = [], []
        stage = self.stage
        for number, ((low, high, orders), terms) in enumerate(zip(self.portions, self.terms)):
            axis = (*orders, "w", None)[stage]
            picked = []
            for array, axes, start, fixed in terms:
                index = [slice(start, start + high - low)]
                for name in axes[1:]:
                    index.append(1 if name == axis else fixed.get(name, 0 if name in orders[:stage] or (stage > 3 and name == "w") else slice(None)))
                picked.append((array, tuple(index)))
            if stage < 3:
                shapes.append(sds((high - low, *(2,) * (3 - stage), *self.tail), BF16))
                jobs.append((picked, first_out + number, slice(0, high - low), "range"))
            elif stage == 3:
                if not number:
                    shapes.append(sds((self.blocks, *self.tail), BF16))
                jobs.append((picked, first_out, slice(low, high), "range"))
            else:
                if not number:
                    shapes += self.finish[0]
                for block in range(low, high):
                    shift = block - low
                    one = [(a, (slice(index[0].start + shift, index[0].start + shift + 1), *index[1:])) for a, index in picked]
                    out, place, kind = self.finish[1](block)
                    jobs.append((one, first_out + out, place, kind))
        self.stage += 1
        return jobs, shapes

    def keep(self, results):
        self.sends = results
        if self.stage == 5:
            self.total = results


def attention_finish(counts):
    stacks = [sds((count, UNIT, 2 * UNIT) if count > 1 else (UNIT, 2 * UNIT), F32) for count in counts]

    def place_of(block):
        half, matrix = block // 4, block % 4
        lanes = slice(half * UNIT, (half + 1) * UNIT)
        if matrix == 3:
            return len(counts), (lanes, slice(None)), "turned"
        stack = 0 if matrix < counts[0] else 1
        if counts[stack] == 1:
            return stack, (slice(None), lanes), "plain"
        return stack, (matrix - sum(counts[:stack]), slice(None), lanes), "plain"

    return [*stacks, sds((2 * UNIT, UNIT), F32)], place_of


def ffn_finish():
    def place_of(block):
        lanes = slice(block // 2 * FFN_PART, (block // 2 + 1) * FFN_PART)
        if block % 2:
            return 1, (lanes, slice(None)), "turned"
        return 0, (slice(None), lanes), "plain"

    return [sds((UNIT, 4 * FFN_PART), F32), sds((4 * FFN_PART, UNIT), F32)], place_of


class Shared:
    def __init__(self, values):
        self.values, self.moves = values, [to_sibling, over_x, over_z_near, over_y, over_z_far]

    def receive(self, *earlier):
        self.moved = after(self.moves.pop(0)(self.values), *earlier)

    def jobs(self, first_out):
        terms = [(array, (slice(0, 1),)) for array in (self.values, self.moved)]
        return [(terms, first_out, slice(0, 1), "range")], [sds(self.values.shape, F32)]

    def keep(self, results):
        self.values, = results


def advance(reductions, *earlier):
    jobs, shapes, bounds = [], [], []
    for reduction in reductions:
        reduction.receive(*earlier)
        more, made = reduction.jobs(len(shapes))
        bounds.append((len(shapes), len(shapes) + len(made)))
        jobs, shapes = jobs + more, shapes + made
    results = combine(jobs, shapes)
    for reduction, (low, high) in zip(reductions, bounds):
        reduction.keep(list(results[low:high]))
    return list(results)


def sentence_body(
    tokens,
    memory,
    dec_lengths,
    mem_lengths,
    self_qkv,
    self_out,
    cross_q,
    cross_kv,
    cross_out,
    ffn_in,
    ffn_out,
    norm_gains,
    norm_biases,
    cotangent,
):
    dp = lax.axis_index("dp")
    order = dp & 3
    inner = (dp >> 1) & 1
    gains = [norm_gains[i : i + 1] for i in range(3)]
    biases = [norm_biases[i : i + 1] for i in range(3)]

    def part_rows(values, parts):
        rows = values.shape[-2] // parts
        place = order if parts == 4 else inner
        return lax.dynamic_slice_in_dim(values, place * rows, rows, values.ndim - 2)

    def folded(values):
        blocks = values.reshape(values.shape[0], 4, 2 * UNIT)
        return blocks.transpose(1, 0, 2).reshape(1, 4 * values.shape[0], 2 * UNIT)

    self_near = over_y(jnp.concatenate([part_rows(self_qkv, 4), folded(part_rows(self_out, 4))]))
    cross_near = over_y(
        jnp.concatenate([part_rows(cross_q, 2)[None], part_rows(cross_kv, 2), folded(part_rows(cross_out, 2))])
    )
    ffn_near = over_y(jnp.stack([part_rows(ffn_in, 4), part_rows(ffn_out, 4)]))
    self_own = (self_qkv, self_out)
    self_sib = tuple(to_sibling(w) for w in self_own)
    self_a = attention_fwd_call(dec_lengths, [], [tokens], [self_own, self_sib], None, None)
    self_near = after(self_near, self_a[4])
    self_side, self_up = over_x(self_near), over_z_near(self_near)
    self_corner = over_x(self_up)
    cross_own, ffn_own = (cross_q, cross_kv, cross_out), (ffn_in, ffn_out)
    cross_sib = tuple(to_sibling(w) for w in cross_own)
    cross_up = over_z_near(cross_near)
    self_rest = (self_near, self_side, self_up, after(self_corner, cross_near, *cross_sib))
    self_far = tuple(to_sibling(w) for w in self_rest)
    self_pieces = [self_own, self_sib, self_rest, self_far]
    self_b = attention_fwd_call(
        dec_lengths, [tokens], [tokens], self_pieces[2:], self_a[5], (gains[0], biases[0])
    )
    first_low, first_hat, first_inv = self_b[5:]
    cross_in = [first_low, memory]
    cross_rest = jnp.stack([cross_near, after(cross_up, self_b[4])])
    cross_far = to_sibling(cross_rest)
    ffn_sib = tuple(to_sibling(after(w, ffn_near)) for w in ffn_own)
    ffn_side, ffn_up = over_x(ffn_near), over_z_near(ffn_near)
    cross_pieces = [cross_own, cross_sib, (cross_rest,), (cross_far,)]
    cross_b = attention_fwd_call(
        mem_lengths, [first_hat, gains[0], biases[0]], [after(first_low, ffn_near), memory], cross_pieces, None,
        (gains[1], biases[1]),
    )
    second_low, second_hat, second_inv = cross_b[5:]
    ffn_side, ffn_up = after(ffn_side, cross_b[4]), after(ffn_up, cross_b[4])
    up_corner, down_corner = over_x(ffn_up[:1]), over_z_near(ffn_side[1:])
    ffn_pieces = [ffn_own, ffn_sib]
    ffn_a = ffn_fwd_call(second_low, ffn_pieces, None, None)
    up_corner, down_corner = after(up_corner, ffn_a[0]), after(down_corner, ffn_a[0])
    ffn_rest = (ffn_near, ffn_side, ffn_up, up_corner, down_corner)
    ffn_pieces += [ffn_rest, tuple(to_sibling(w) for w in ffn_rest)]
    ffn_b = ffn_fwd_call(
        second_low, ffn_pieces[2:], ffn_a[0],
        (second_hat, gains[1], biases[1], cotangent, gains[2], biases[2]),
    )
    out_rows, third_low, third_scaled, third_gain, third_bias = ffn_b[:5]

    def plan_of(pieces):
        return [(piece // 2, 2 * (piece % 2) + half) for piece in pieces for half in (0, 1)]

    ffn_saved = [ffn_a[1:3], ffn_b[5:7]]
    ffn_d = ffn_bwd_call(
        third_low, second_low, ffn_pieces[1::2], ffn_saved, plan_of((1, 3)), third_scaled, None
    )
    ffn_sum = Reduction(ffn_d[1], [(0, 3, "yzx"), (3, 6, "xyz"), (6, 8, "zxy")], ffn_finish())
    ffn_e = ffn_bwd_call(
        third_low, second_low, ffn_pieces[::2], ffn_saved, plan_of((0, 2)), ffn_d[0],
        (second_hat, second_inv, gains[1]),
    )
    second_back, second_scaled, second_gain, second_bias = ffn_e[:4]
    ffn_sum.begin(ffn_e[4], second_gain)
    second_back = after(second_back, *advance([ffn_sum]))

    cross_e = attention_bwd_call(
        mem_lengths, second_back, cross_in, cross_pieces[1::2] + cross_pieces[::2],
        [cross_b[:5]], [(0, 2 * p + half) for p in (1, 3, 0, 2) for half in (0, 1)], second_scaled,
        (first_hat, first_inv, gains[0]), 2,
    )
    first_back, first_scaled, first_gain, first_bias, memory_part = cross_e[:5]
    norm_sums = jnp.stack([first_gain, second_gain, third_gain, first_bias, second_bias, third_bias])
    norm_sums = jnp.concatenate([jnp.sum(norm_sums, axis=1), jnp.zeros((2, norm_sums.shape[2]), F32)])
    norms = Shared(norm_sums[None])
    sends = advance([ffn_sum], first_gain)
    cross_sum = Reduction(after(cross_e[5], *sends), [(0, 4, "zyx"), (4, 8, "yxz")], attention_finish((1, 2)))
    first_back = after(first_back, *sends)

    self_saved = [self_a[:5], self_b[:5]]
    self_d = attention_bwd_call(
        dec_lengths, first_back, [tokens], self_pieces[1::2], self_saved, plan_of((1, 3)), None, None
    )
    cross_sum.begin(cross_e[6], self_d[0])
    sends = advance([cross_sum, ffn_sum, norms], self_d[0])
    self_sum = Reduction(after(self_d[1], *sends), [(0, 4, "yxz"), (4, 8, "xzy")], attention_finish((3,)))
    first_back = after(first_back, *sends)
    self_e = attention_bwd_call(
        dec_lengths, first_back, [tokens], self_pieces[::2], self_saved, plan_of((0, 2)), None, None
    )
    self_sum.begin(self_e[1], self_e[0])
    sends = advance([self_sum, norms], self_e[0])
    grad_tokens = inputs_back_call(
        after(first_scaled, *sends), [(self_d[0], self_pieces[1::2]), (self_e[0], self_pieces[::2])], (0, 1, 2)
    )
    sends = advance([cross_sum, ffn_sum], *sends)
    sends = advance([self_sum, norms], *sends, grad_tokens)
    sends = advance([cross_sum, ffn_sum], *sends)
    sends = advance([self_sum, norms], *sends)
    sends = advance([cross_sum], *sends)
    sends = advance([self_sum], *sends)
    grad_memory = inputs_back_call(
        None, [(after(memory_part, *sends), cross_pieces[1::2] + cross_pieces[::2])], (1, 2)
    )
    advance([self_sum, cross_sum, norms], grad_memory)
    norm_total = norms.values[0]
    self_sum, cross_sum, ffn_sum = self_sum.total, cross_sum.total, ffn_sum.total

    return (
        out_rows,
        grad_tokens,
        grad_memory,
        *self_sum,
        *cross_sum,
        *ffn_sum,
        norm_total[:3],
        norm_total[3:6],
    )


def sentence_fits(mesh, tokens, memory, dec_lengths):
    shape = dict(mesh.shape)
    rows = tokens.shape[0] // mesh.size
    sentences = dec_lengths.shape[1]
    return (
        shape["tensor"] == 4
        and shape["dp"] == 8
        and sentences == 4
        and rows == 512
        and memory.shape[0] // mesh.size == rows
        and tokens.shape[1] == 1024
    )


def smooth_gate(values):
    return jax.nn.gelu(values, approximate=True)


def norm_rows(hidden, norm_gain, norm_bias):
    center = hidden - jnp.mean(hidden, axis=-1, keepdims=True)
    inverse = lax.rsqrt(jnp.mean(center * center, axis=-1, keepdims=True) + NORM_EPSILON)
    normed = center * inverse
    return (normed * norm_gain + norm_bias, normed, inverse)


def norm_back(gradient, normed, inverse, norm_gain):
    scaled = gradient * norm_gain
    grad_in = inverse * (
        scaled
        - jnp.mean(scaled, axis=-1, keepdims=True)
        - normed * jnp.mean(scaled * normed, axis=-1, keepdims=True)
    )
    return (grad_in, jnp.sum(gradient * normed, axis=0), jnp.sum(gradient, axis=0))


def head_view(values, sentences):
    return values.reshape(sentences, -1, values.shape[1] // HEAD_DIM, HEAD_DIM)


def masked_scores(query_heads, key_heads, key_mask):
    scores = jnp.einsum(
        "sqhe,skhe->shqk", query_heads, key_heads, preferred_element_type=jnp.float32
    ) * HEAD_DIM ** (-0.5)
    return jnp.where(key_mask, scores, MASKED_SCORE)


def attention_forward(query_rows, key_rows, value_rows, key_mask, sentences):
    scores = masked_scores(
        head_view(query_rows, sentences), head_view(key_rows, sentences), key_mask
    )
    row_peak = jnp.max(scores, axis=-1, keepdims=True)
    exponent_terms = jnp.exp(scores - row_peak)
    row_sum = jnp.sum(exponent_terms, axis=-1, keepdims=True)
    softmax_probs = exponent_terms / row_sum
    attended = jnp.einsum(
        "shqk,skhe->sqhe",
        softmax_probs.astype(jnp.bfloat16),
        head_view(value_rows, sentences),
        preferred_element_type=jnp.float32,
    ).astype(jnp.bfloat16)
    return (attended.reshape(query_rows.shape), row_peak + jnp.log(row_sum))


def attention_backward(query_rows, key_rows, value_rows, key_mask, log_total, grad_rows, sentences):
    query_heads = head_view(query_rows, sentences)
    key_heads = head_view(key_rows, sentences)
    value_heads = head_view(value_rows, sentences)
    grad_heads = head_view(grad_rows, sentences)
    softmax_probs = jnp.exp(masked_scores(query_heads, key_heads, key_mask) - log_total)
    grad_probs = jnp.einsum(
        "sqhe,skhe->shqk", grad_heads, value_heads, preferred_element_type=jnp.float32
    )
    row_delta = jnp.sum(softmax_probs * grad_probs, axis=-1, keepdims=True)
    grad_scores = (softmax_probs * (grad_probs - row_delta)).astype(jnp.bfloat16)
    score_scale = HEAD_DIM ** (-0.5)
    grad_query = (
        jnp.einsum("shqk,skhe->sqhe", grad_scores, key_heads, preferred_element_type=jnp.float32)
        * score_scale
    ).astype(jnp.bfloat16)
    grad_key = (
        jnp.einsum("shqk,sqhe->skhe", grad_scores, query_heads, preferred_element_type=jnp.float32)
        * score_scale
    ).astype(jnp.bfloat16)
    grad_value = jnp.einsum(
        "shqk,sqhe->skhe",
        softmax_probs.astype(jnp.bfloat16),
        grad_heads,
        preferred_element_type=jnp.float32,
    ).astype(jnp.bfloat16)
    return (
        grad_query.reshape(query_rows.shape),
        grad_key.reshape(key_rows.shape),
        grad_value.reshape(value_rows.shape),
    )


def body(
    tokens,
    memory,
    dec_lengths,
    mem_lengths,
    self_qkv,
    self_out,
    cross_q,
    cross_kv,
    cross_out,
    ffn_in,
    ffn_out,
    norm_gains,
    norm_biases,
    cotangent,
):
    row_share = tokens.shape[0]
    sentences = dec_lengths.shape[1]
    all_tokens, all_memory = (
        lax.all_gather(tokens, "tensor", axis=0, tiled=True),
        lax.all_gather(memory, "tensor", axis=0, tiled=True),
    )
    sentence_len = all_tokens.shape[0] // sentences
    memory_len = all_memory.shape[0] // sentences
    positions = jnp.arange(sentence_len, dtype=jnp.int32)
    self_mask = (
        (positions[None, :] <= positions[:, None])[None]
        & (positions[None, None, :] < dec_lengths[0][:, None, None])
    )[:, None]
    memory_positions = jnp.arange(memory_len, dtype=jnp.int32)
    cross_mask = (memory_positions[None, :] < mem_lengths[0][:, None])[:, None, None, :]

    def branch_rows(attended, weight):
        return lax.psum_scatter(
            jnp.dot(attended, weight, preferred_element_type=jnp.float32).astype(jnp.bfloat16),
            "tensor",
            scatter_dimension=0,
            tiled=True,
        ).astype(jnp.float32)

    def branch_grad(grad_rows, attended, weight):
        grad_low = grad_rows.astype(jnp.bfloat16)
        grad_all = lax.all_gather(grad_low, "tensor", axis=0, tiled=True)
        grad_attended = jnp.dot(grad_all, weight.T, preferred_element_type=jnp.float32).astype(
            jnp.bfloat16
        )
        weight_part = jnp.dot(attended.T, grad_all, preferred_element_type=jnp.float32)
        return (grad_attended, weight_part)

    def gather_normed(values):
        return lax.all_gather(values, "tensor", axis=0, tiled=True)

    def head_input_sum(term):
        return lax.psum_scatter(
            term(jnp.int32(0), row_share * lax.axis_size("tensor")).astype(jnp.bfloat16),
            "tensor",
            scatter_dimension=0,
            tiled=True,
        ).astype(jnp.float32)

    self_proj = jnp.einsum(
        "td,cde->cte", all_tokens, self_qkv, preferred_element_type=jnp.float32
    ).astype(jnp.bfloat16)
    self_att, self_lse = attention_forward(
        self_proj[0], self_proj[1], self_proj[2], self_mask, sentences
    )
    self_branch = branch_rows(self_att, self_out)
    first_norm, first_hat, first_inv = norm_rows(
        RESIDUAL_ALPHA * tokens.astype(jnp.float32) + self_branch, norm_gains[0], norm_biases[0]
    )
    first_all = gather_normed(first_norm.astype(jnp.bfloat16))
    cross_query = jnp.dot(first_all, cross_q, preferred_element_type=jnp.float32).astype(
        jnp.bfloat16
    )
    cross_proj = jnp.einsum(
        "td,cde->cte", all_memory, cross_kv, preferred_element_type=jnp.float32
    ).astype(jnp.bfloat16)
    cross_att, cross_lse = attention_forward(
        cross_query, cross_proj[0], cross_proj[1], cross_mask, sentences
    )
    cross_branch = branch_rows(cross_att, cross_out)
    second_norm, second_hat, second_inv = norm_rows(
        RESIDUAL_ALPHA * first_norm + cross_branch, norm_gains[1], norm_biases[1]
    )
    second_all = gather_normed(second_norm.astype(jnp.bfloat16))
    pre_gate = jnp.dot(second_all, ffn_in, preferred_element_type=jnp.float32)
    activated = smooth_gate(pre_gate).astype(jnp.bfloat16)
    ffn_branch = lax.psum_scatter(
        jnp.dot(activated, ffn_out, preferred_element_type=jnp.float32).astype(jnp.bfloat16),
        "tensor",
        scatter_dimension=0,
        tiled=True,
    ).astype(jnp.float32)
    out_rows, third_hat, third_inv = norm_rows(
        RESIDUAL_ALPHA * second_norm + ffn_branch, norm_gains[2], norm_biases[2]
    )
    grad_third, third_gain, third_bias = norm_back(
        cotangent.astype(jnp.float32), third_hat, third_inv, norm_gains[2]
    )
    grad_ffn_all = lax.all_gather(grad_third.astype(jnp.bfloat16), "tensor", axis=0, tiled=True)
    unused_gate, gate_pull = jax.vjp(smooth_gate, pre_gate)
    grad_act = gate_pull(jnp.dot(grad_ffn_all, ffn_out.T, preferred_element_type=jnp.float32))[
        0
    ].astype(jnp.bfloat16)
    grad_ffn_out = jnp.dot(activated.T, grad_ffn_all, preferred_element_type=jnp.float32)
    grad_ffn_in = jnp.dot(second_all.T, grad_act, preferred_element_type=jnp.float32)
    grad_second = RESIDUAL_ALPHA * grad_third + lax.psum_scatter(
        jnp.dot(grad_act, ffn_in.T, preferred_element_type=jnp.float32).astype(jnp.bfloat16),
        "tensor",
        scatter_dimension=0,
        tiled=True,
    ).astype(jnp.float32)
    grad_second_in, second_gain, second_bias = norm_back(
        grad_second, second_hat, second_inv, norm_gains[1]
    )
    grad_cross_att, cross_out_part = branch_grad(grad_second_in, cross_att, cross_out)
    grad_cq, grad_ck, grad_cv = attention_backward(
        cross_query, cross_proj[0], cross_proj[1], cross_mask, cross_lse, grad_cross_att, sentences
    )
    grad_cross_q = jnp.dot(first_all.T, grad_cq, preferred_element_type=jnp.float32)
    cross_grads = jnp.stack([grad_ck, grad_cv])
    grad_cross_kv = jnp.einsum(
        "td,cte->cde", all_memory, cross_grads, preferred_element_type=jnp.float32
    )
    grad_memory = lax.psum_scatter(
        jnp.einsum("cte,cde->td", cross_grads, cross_kv, preferred_element_type=jnp.float32).astype(
            jnp.bfloat16
        ),
        "tensor",
        scatter_dimension=0,
        tiled=True,
    ).astype(jnp.float32)

    def cross_input_term(first_row, row_total):
        return jnp.dot(grad_cq, cross_q.T, preferred_element_type=jnp.float32)

    cross_input = head_input_sum(cross_input_term)
    grad_first = RESIDUAL_ALPHA * grad_second_in + cross_input
    grad_first_in, first_gain, first_bias = norm_back(
        grad_first, first_hat, first_inv, norm_gains[0]
    )
    grad_self_att, self_out_part = branch_grad(grad_first_in, self_att, self_out)
    grad_sq, grad_sk, grad_sv = attention_backward(
        self_proj[0], self_proj[1], self_proj[2], self_mask, self_lse, grad_self_att, sentences
    )
    self_grads = jnp.stack([grad_sq, grad_sk, grad_sv])
    grad_self_qkv = jnp.einsum(
        "td,cte->cde", all_tokens, self_grads, preferred_element_type=jnp.float32
    )

    def self_input_term(first_row, row_total):
        return jnp.einsum("cte,cde->td", self_grads, self_qkv, preferred_element_type=jnp.float32)

    self_input = head_input_sum(self_input_term)
    grad_tokens = RESIDUAL_ALPHA * grad_first_in + self_input
    summed = (
        lax.psum_scatter(
            grad_self_qkv.astype(jnp.bfloat16), "dp", scatter_dimension=1, tiled=True
        ).astype(jnp.float32),
        lax.psum_scatter(
            self_out_part.astype(jnp.bfloat16), "dp", scatter_dimension=1, tiled=True
        ).astype(jnp.float32),
        lax.psum_scatter(
            grad_cross_q.astype(jnp.bfloat16), "dp", scatter_dimension=0, tiled=True
        ).astype(jnp.float32),
        lax.psum_scatter(
            grad_cross_kv.astype(jnp.bfloat16), "dp", scatter_dimension=1, tiled=True
        ).astype(jnp.float32),
        lax.psum_scatter(
            cross_out_part.astype(jnp.bfloat16), "dp", scatter_dimension=1, tiled=True
        ).astype(jnp.float32),
        lax.psum_scatter(
            grad_ffn_in.astype(jnp.bfloat16), "dp", scatter_dimension=0, tiled=True
        ).astype(jnp.float32),
        lax.psum_scatter(
            grad_ffn_out.astype(jnp.bfloat16), "dp", scatter_dimension=1, tiled=True
        ).astype(jnp.float32),
    )
    gain_total, bias_total = lax.psum(
        (
            jnp.stack([first_gain, second_gain, third_gain]),
            jnp.stack([first_bias, second_bias, third_bias]),
        ),
        ("dp", "tensor"),
    )
    return (
        out_rows.astype(jnp.bfloat16),
        grad_tokens,
        grad_memory,
        summed[0],
        summed[1],
        summed[2],
        summed[3],
        summed[4],
        summed[5],
        summed[6],
        gain_total,
        bias_total,
    )


def solution(mesh):
    in_specs = (
        P(("dp", "tensor"), None),
        P(("dp", "tensor"), None),
        P("dp", None),
        P("dp", None),
        P(None, None, "tensor"),
        P("tensor", None),
        P(None, "tensor"),
        P(None, None, "tensor"),
        P("tensor", None),
        P(None, "tensor"),
        P("tensor", None),
        P(),
        P(),
        P(("dp", "tensor"), None),
    )
    out_specs = (
        P(("dp", "tensor"), None),
        P(("dp", "tensor"), None),
        P(("dp", "tensor"), None),
        P(None, "dp", "tensor"),
        P("tensor", "dp"),
        P("dp", "tensor"),
        P(None, "dp", "tensor"),
        P("tensor", "dp"),
        P("dp", "tensor"),
        P("tensor", "dp"),
        P(),
        P(),
    )

    def step(*args):
        chosen = sentence_body if sentence_fits(mesh, args[0], args[1], args[2]) else body
        return jax.shard_map(
            chosen, mesh=mesh, in_specs=in_specs, out_specs=out_specs, check_vma=False
        )(*args)

    return step
```
